32 devices in a mesh: expert: 8 (over z, x), hidden: 4 (over y, core).
Axes of the slice: x: 2, y: 2, z: 4, core: 2. Of those that a mesh axis runs over, the one named last changes fastest.
Arguments:
- tokens: bfloat16 [16384, 768], P(('expert', 'hidden')), may hold values from -6 to 6
- doc_lengths: int32 [8, 3], P('expert'), may hold values from 1 to 1024, 2048 in all within a row
- expert_ids: int32 [16384, 2], P(('expert', 'hidden')), may hold values from 0 to 7, all different within a row; in each aligned block of 512 rows (0 to 511, 512 to 1023, ...) at most 160 rows name the same one
- gain_one: float32 [768], replicated, may hold values from 0.5 to 1.5
- shift_one: float32 [768], replicated, may hold values from -1.25 to 1.25
- w_query: bfloat16 [768, 768], replicated, may hold values from -0.21875 to 0.21875
- w_key: bfloat16 [768, 768], replicated, may hold values from -0.21875 to 0.21875
- w_value: bfloat16 [768, 768], replicated, may hold values from -0.21875 to 0.21875
- w_out: bfloat16 [768, 768], replicated, may hold values from -3.5 to 3.5
- gain_two: float32 [768], replicated, may hold values from 0.5 to 1.5
- shift_two: float32 [768], replicated, may hold values from -1.25 to 1.25
- w_router: bfloat16 [768, 8], replicated, may hold values from -0.21875 to 0.21875
- w_up: bfloat16 [8, 768, 3072], P('expert', None, 'hidden'), may hold values from -0.21875 to 0.21875
- w_down: bfloat16 [8, 3072, 768], P('expert', 'hidden'), may hold values from -0.109375 to 0.109375
- out_grad: bfloat16 [16384, 768], P(('expert', 'hidden')), may hold values from -6 to 6
Outputs:
- output: bfloat16 [16384, 768], P(('expert', 'hidden'))
- input_grad: bfloat16 [16384, 768], P(('expert', 'hidden'))
- gain_one_grad: float32 [768], replicated
- shift_one_grad: float32 [768], replicated
- w_query_grad: float32 [768, 768], replicated
- w_key_grad: float32 [768, 768], replicated
- w_value_grad: float32 [768, 768], replicated
- w_out_grad: float32 [768, 768], replicated
- gain_two_grad: float32 [768], replicated
- shift_two_grad: float32 [768], replicated
- w_router_grad: float32 [768, 8], replicated
- w_up_grad: float32 [8, 768, 3072], P('expert', None, 'hidden')
- w_down_grad: float32 [8, 3072, 768], P('expert', 'hidden')
- load: float32 [8], replicated
The draws below stay inside these ranges and needn't reach their ends.
Inputs may be any that keep to these rules, and one draw needn't show every extreme that they name: `doc_lengths`: the lengths of a group's documents, in order; they sum to 2048 and the longest in every group is 1024. `expert_ids`: each token names 2 different experts; among the 512 tokens of one device no expert is named more than 160 times, and in every draw some expert is named exactly 160 times by one device.
All inputs are finite; a program needn't handle non-finite values.
Results may differ from the reference program's by a relative error of at most 0.019.
Values may be sent and summed in bfloat16 or wider, within the bound.
A program may use at most 192 MiB of HBM per device.

```python
import math
import jax
import jax.numpy as jnp
import numpy as np
from jax import lax

D = 768
HEADS = 12
HEAD_DIM = 64
FF = 3072
TOP = 2
DOCS = 3
TOK_DEV = 512
EXPERTS = 8
OLD = 4
SOURCES = 32
TOKENS = 16384
GROUP = 2048
LONGEST = 1024
CAP = 160
N_EXPERT = 8


def block_scale(stream_key, extent, shards, smallest, top_value):
    level, own = 1.0, jax.random.fold_in(stream_key, 6)
    for axis_at, blocks in shards:
        draws = jnp.exp(jax.random.uniform(jax.random.fold_in(own, axis_at), (blocks,), jnp.float32, smallest / len(shards), top_value / len(shards)))
        level = level * jnp.repeat(draws, extent[axis_at] // blocks).reshape([-1 if axis == axis_at else 1 for axis in range(len(extent))])
    return level


def split_up(amount, total, limit, slope):
    portions = [(1 << 20) // math.isqrt(standing ** slope) + 1 for standing in range(2, amount + 1)]
    rest, holding = total - limit - (amount - 1), [1] * (amount - 1)
    while rest > 0:
        movable = [i for i in range(amount - 1) if holding[i] < limit]
        mass, left = sum([portions[i] for i in movable]), rest
        for i in movable:
            addition = min(limit - holding[i], max(1, left * portions[i] // mass), rest)
            holding[i] = holding[i] + addition
            rest = rest - addition
    return np.array([limit] + holding)


def uneven(key, amount, total, most, slope):
    if amount == 2:
        one = jax.random.randint(key, (), max(1, total - most), min(most, total - 1) + 1)
        return jnp.stack([one, total - one])
    sizes = jnp.asarray(split_up(amount, total, most, slope), jnp.int32)
    twos = (amount - 1) // 2
    donor, sink = sizes[1:1 + 2 * twos:2], sizes[2:2 + 2 * twos:2]
    slack = jnp.minimum(donor - 1, most - sink)
    passed = jax.random.randint(jax.random.fold_in(key, 1), (twos,), 0, 1 << 20) % (slack + 1)
    sizes = sizes.at[1:1 + 2 * twos:2].set(donor - passed).at[2:2 + 2 * twos:2].set(sink + passed)
    return sizes[jax.random.permutation(jax.random.fold_in(key, 2), amount)]


def deal_out(stream_key, own, number, rows, number_of, top, limit, skew):
    ranking = jax.random.permutation(stream_key, number_of)
    crowded, common = portions_of(number_of, rows * top, limit, skew, True), portions_of(number_of, rows * top, limit, skew, False)
    places = jnp.arange(number_of)

    def named(tallies, turn):
        used = int((tallies > 0).sum())
        fixed = max(1, used // 4)
        shifted = fixed + (places - fixed + turn * (used - fixed)) % max(1, number_of - fixed)
        return jnp.zeros((number_of,), jnp.int32).at[ranking[jnp.where(places < fixed, places, shifted)]].set(jnp.asarray(tallies, jnp.int32))

    tallies = jnp.where(number % 4 == 0, named(crowded, number // 4), named(common, number - number // 4 - 1))
    mixed = jax.random.permutation(jax.random.fold_in(own, 3), number_of)
    donor, receiver = mixed[0:number_of // 2 * 2:2], mixed[1:number_of // 2 * 2:2]
    slack = jnp.minimum(tallies[donor] - 1, limit - tallies[receiver]) // 2
    slack = jnp.where((donor == ranking[0]) | (receiver == ranking[0]) | (tallies[receiver] == 0), 0, jnp.maximum(slack, 0))
    shifted = jax.random.randint(jax.random.fold_in(own, 4), (number_of // 2,), 0, 1 << 20) % (slack + 1)
    tallies = tallies.at[donor].add(-shifted).at[receiver].add(shifted)
    labels = jnp.searchsorted(jnp.cumsum(tallies), jnp.arange(rows * top), side="right").astype(jnp.int32)
    table = labels.reshape(top, rows).T
    table = table[jax.random.permutation(jax.random.fold_in(own, 1), rows)]
    turn = jax.random.randint(jax.random.fold_in(own, 2), (rows, 1), 0, top)
    return jnp.take_along_axis(table, (jnp.arange(top)[None, :] + turn) % top, axis=1)


def portions_of(count, total, limit, lean, full):
    loads = [(1 << 20) // math.isqrt(grade ** lean) + 1 for grade in range(1, count + 1)]
    largest = limit if full else min(limit, max(-(-total // count), total * loads[0] // sum(loads)))
    least = 1 if total - largest >= count - 1 else 0
    given, surplus = [largest] + [least] * (count - 1), total - largest - least * (count - 1)
    while surplus > 0:
        movable = [i for i in range(1, count) if given[i] < largest] or [i for i in range(1, count) if given[i] < limit]
        pool, budget = sum([loads[i] for i in movable]), surplus
        for i in movable:
            more = min(limit - given[i], max(1, budget * loads[i] // pool), surplus)
            given[i] = given[i] + more
            surplus = surplus - more
    return np.array(given)


def gaussian(stream_key, extent, scale, reach, cuts=(), kind=jnp.bfloat16):
    factor_of = block_scale(stream_key, extent, cuts, -0.22, 0.18) if cuts else 1.0
    entries = jax.random.normal(stream_key, extent, jnp.float32) * scale * factor_of
    return jnp.minimum(jnp.maximum(entries, -reach), reach).astype(kind)


def setup_inputs(seed: int = 0) -> dict:
    arg_keys = jax.random.split(jax.random.key(seed), 16)
    tokens = gaussian(arg_keys[0], (TOKENS, D), 1.0, 6.0, ((0, 32),))
    doc_lengths = jax.vmap(lambda own: uneven(own, DOCS, GROUP, LONGEST, 2))(jax.random.split(arg_keys[1], N_EXPERT)).reshape((N_EXPERT, DOCS)).astype(jnp.int32)
    expert_ids_keys = jax.random.split(jax.random.fold_in(arg_keys[2], 1), TOKENS // TOK_DEV)
    expert_ids_turns = jax.random.permutation(jax.random.fold_in(arg_keys[2], 3), TOKENS // TOK_DEV)
    expert_ids = jax.vmap(lambda own, number: deal_out(jax.random.fold_in(arg_keys[2], 2), own, number, TOK_DEV, EXPERTS, TOP, CAP, 1))(expert_ids_keys, expert_ids_turns).reshape((TOKENS, TOP))
    gain_one = jnp.clip(1.0 + 0.1 * jax.random.normal(arg_keys[3], (D,), jnp.float32), 0.5, 1.5)
    shift_one = gaussian(arg_keys[4], (D,), 0.2, 1.25, (), jnp.float32)
    w_query = gaussian(arg_keys[5], (D, D), D ** -0.5, 0.21875)
    w_key = gaussian(arg_keys[6], (D, D), D ** -0.5, 0.21875)
    w_value = gaussian(arg_keys[7], (D, D), D ** -0.5, 0.21875)
    w_out = gaussian(arg_keys[8], (D, D), (max(1, D // 256)) ** -0.5, 3.5)
    gain_two = jnp.clip(1.0 + 0.1 * jax.random.normal(arg_keys[9], (D,), jnp.float32), 0.5, 1.5)
    shift_two = gaussian(arg_keys[10], (D,), 0.2, 1.25, (), jnp.float32)
    w_router = gaussian(arg_keys[11], (D, EXPERTS), D ** -0.5, 0.21875)
    w_up = gaussian(arg_keys[12], (EXPERTS, D, FF), D ** -0.5, 0.21875, ((0, 8), (2, 4)))
    w_down = gaussian(arg_keys[13], (EXPERTS, FF, D), FF ** -0.5, 0.109375, ((0, 8), (1, 4)))
    out_grad = gaussian(arg_keys[14], (TOKENS, D), 1.0, 6.0, ((0, 32),))
    return {"tokens": tokens, "doc_lengths": doc_lengths, "expert_ids": expert_ids, "gain_one": gain_one, "shift_one": shift_one, "w_query": w_query, "w_key": w_key, "w_value": w_value, "w_out": w_out, "gain_two": gain_two, "shift_two": shift_two, "w_router": w_router, "w_up": w_up, "w_down": w_down, "out_grad": out_grad}


EPSILON = 1e-05
SCALE = 0.125
MASKED = -1e+30
EXACT = lax.Precision.HIGHEST

@jax.custom_vjp
def low(v):
    return lax.optimization_barrier(v.astype(jnp.bfloat16)).astype(jnp.float32)

@jax.custom_vjp
def low_back(v):
    return v

def low_keep(v):
    return (low(v), None)

def low_pass(kept, grad):
    return (grad,)

def back_keep(v):
    return (v, None)

def back_low(kept, grad):
    return (low(grad),)
low.defvjp(low_keep, low_pass)
low_back.defvjp(back_keep, back_low)

def rounded(value):
    return low_back(low(value))

def exact_dot(left, right):
    return jnp.dot(left, right, precision=EXACT)

def layer_norm(values, gain, shift):
    row_mean = lax.optimization_barrier(jnp.mean(values, axis=-1, keepdims=True))
    centred = values - row_mean
    variance = lax.optimization_barrier(jnp.mean(centred * centred, axis=-1, keepdims=True))
    return centred * lax.rsqrt(variance + EPSILON) * gain + shift

def split_heads(array):
    return array.reshape(array.shape[0], HEADS, HEAD_DIM).transpose(1, 0, 2)

def attend_group(pieces):
    queries, key_proj, value_proj, lengths = pieces
    position = jnp.arange(GROUP, dtype=jnp.int32)
    doc_ends = jnp.cumsum(lengths)
    document = lax.optimization_barrier(jnp.sum((position[:, None] >= doc_ends[None, :]).astype(jnp.int32), axis=1))
    allowed = (document[:, None] == document[None, :]) & (position[None, :] <= position[:, None])

    def one_head(head_pieces):
        q_head, k_head, v_head = head_pieces
        scores = low_back(exact_dot(q_head, k_head.T) * SCALE)
        scores = jnp.where(allowed, scores, MASKED)
        weights = jax.nn.softmax(scores, axis=-1)
        return exact_dot(low(weights), v_head)
    mixture = lax.map(jax.checkpoint(one_head), (split_heads(queries), split_heads(key_proj), split_heads(value_proj)))
    return mixture.transpose(1, 0, 2).reshape(GROUP, D)

def run_expert(pieces):
    slot_rows, up_weight, down_weight = pieces
    pre_act = low_back(exact_dot(slot_rows, up_weight))
    hidden_act = low(jax.nn.gelu(pre_act, approximate=True))
    return exact_dot(hidden_act, down_weight)

def routing(expert_ids):
    flat_ids = expert_ids.reshape(SOURCES, TOK_DEV * TOP)
    onehot = (flat_ids[:, :, None] == jnp.arange(EXPERTS, dtype=jnp.int32)[None, None, :]).astype(jnp.int32)
    before = jnp.cumsum(onehot, axis=1) - onehot
    slot_index = lax.optimization_barrier(jnp.sum(before * onehot, axis=2)).astype(jnp.int32)
    source = jnp.arange(SOURCES, dtype=jnp.int32)[:, None]
    position = flat_ids * (SOURCES * CAP) + source * CAP + slot_index
    counts = lax.optimization_barrier(jnp.sum(onehot, axis=(0, 1)))
    return (position.reshape(-1).astype(jnp.int32), counts)

def reference(tokens, doc_lengths, expert_ids, gain_one, shift_one, w_query, w_key, w_value, w_out, gain_two, shift_two, w_router, w_up, w_down, out_grad):
    position, counts = routing(expert_ids)

    def to_groups(array):
        return array.reshape(N_EXPERT, GROUP, D)

    def forward(input_float, first_gain, first_shift, query_weight, key_weight, value_weight, out_weight, second_gain, second_shift, router_weight, up_weight, down_weight):
        first = low(layer_norm(input_float, first_gain, first_shift))
        queries = rounded(exact_dot(first, query_weight))
        key_proj = rounded(exact_dot(first, key_weight))
        value_proj = rounded(exact_dot(first, value_weight))
        attended = lax.map(jax.checkpoint(attend_group), (to_groups(queries), to_groups(key_proj), to_groups(value_proj), doc_lengths))
        attended = rounded(attended.reshape(TOKENS, D))
        residual = input_float + low_back(exact_dot(attended, out_weight))
        second = low(layer_norm(residual, second_gain, second_shift))
        logits = exact_dot(second, router_weight)
        chosen = jnp.take_along_axis(logits, expert_ids, axis=1)
        gate_weights = jax.nn.softmax(chosen, axis=-1)
        expert_in = low_back(jnp.repeat(second, TOP, axis=0))
        slot_rows = jnp.zeros((EXPERTS * SOURCES * CAP, D), jnp.float32).at[position].set(expert_in)
        produced = lax.map(jax.checkpoint(run_expert), (slot_rows.reshape(EXPERTS, SOURCES * CAP, D), up_weight, down_weight))
        returned = rounded(produced.reshape(EXPERTS * SOURCES * CAP, D)[position])
        expert_mix = lax.optimization_barrier(jnp.sum(gate_weights[:, :, None] * returned.reshape(TOKENS, TOP, D), axis=1))
        return residual + expert_mix
    floats = (tokens.astype(jnp.float32), gain_one.astype(jnp.float32), shift_one.astype(jnp.float32), w_query.astype(jnp.float32), w_key.astype(jnp.float32), w_value.astype(jnp.float32), w_out.astype(jnp.float32), gain_two.astype(jnp.float32), shift_two.astype(jnp.float32), w_router.astype(jnp.float32), w_up.astype(jnp.float32), w_down.astype(jnp.float32))
    output, pull = jax.vjp(forward, *floats)
    grads = pull(out_grad.astype(jnp.float32))
    trainable = (jnp.arange(EXPERTS) >= OLD).astype(jnp.float32)[:, None, None]
    load = counts.astype(jnp.float32) * EXPERTS / (TOKENS * TOP)
    return (output.astype(jnp.bfloat16), grads[0].astype(jnp.bfloat16), grads[1], grads[2], grads[3], grads[4], grads[5], grads[6], grads[7], grads[8], grads[9], grads[10] * trainable, grads[11] * trainable, load)
```

```python
from functools import partial

import jax
import jax.numpy as jnp
from jax import lax
from jax.experimental import pallas as pl
from jax.experimental.pallas import tpu as pltpu
from jax.sharding import PartitionSpec as P

HEAD_DIM = 64
HEADS = 12
EPSILON = 1e-05
SCALE = 0.125
MASKED = -1e30
BLOCK = 256
LANES = 128
BF = jnp.bfloat16
F32 = jnp.float32
I32 = jnp.int32
MESH = pl.DeviceIdType.MESH
ANY = pl.BlockSpec(memory_space=pl.ANY)
SMEM = pl.BlockSpec(memory_space=pltpu.SMEM)
VMEM = pl.BlockSpec(memory_space=pltpu.VMEM)
DMA = pltpu.SemaphoreType.DMA
GELU_A = 0.7978845608028654
GELU_B = 0.044715


def mm(left, right):
    return jnp.dot(left, right, preferred_element_type=F32)


def mm_nt(left, right):
    return lax.dot_general(left, right, (((1,), (1,)), ((), ())), preferred_element_type=F32)


def mm_tn(left, right):
    return lax.dot_general(left, right, (((0,), (0,)), ((), ())), preferred_element_type=F32)


def iota(shape, axis):
    return lax.broadcasted_iota(I32, shape, axis)


def norm_parts(values):
    centred = values - jnp.mean(values, axis=-1, keepdims=True)
    inverse = lax.rsqrt(jnp.mean(centred * centred, axis=-1, keepdims=True) + EPSILON)
    return centred * inverse, inverse


def norm_back(grad_out, normed, inverse, gain):
    grad_normed = grad_out * gain
    first = jnp.mean(grad_normed, axis=-1, keepdims=True)
    second = jnp.mean(grad_normed * normed, axis=-1, keepdims=True)
    return inverse * (grad_normed - first - normed * second)


def split_two(value):
    high = value.astype(BF)
    return high, (value - high.astype(F32)).astype(BF)


def shape_of(shape, dtype):
    return jax.ShapeDtypeStruct(shape, dtype)


def local_call(body, name, outs, *args, specs=None, scratch=(), flops=0, vmem=60):
    nbytes = sum(a.size * a.dtype.itemsize for a in args)
    return pl.pallas_call(
        body,
        name=name,
        out_shape=outs,
        in_specs=specs or [VMEM] * len(args),
        out_specs=jax.tree.map(lambda _: VMEM, outs),
        scratch_shapes=list(scratch),
        compiler_params=pltpu.CompilerParams(vmem_limit_bytes=vmem << 20),
        cost_estimate=pl.CostEstimate(flops=flops, bytes_accessed=nbytes, transcendentals=0),
    )(*args)


def greet(peers):
    barrier = pltpu.get_barrier_semaphore()
    for peer in peers:
        pl.semaphore_signal(barrier, inc=1, device_id=peer, device_id_type=MESH)
    pl.semaphore_wait(barrier, len(peers))


def remote(src, dst, send, recv, peer):
    return pltpu.make_async_remote_copy(
        src_ref=src, dst_ref=dst, send_sem=send, recv_sem=recv, device_id=peer, device_id_type=MESH
    )


def exchange_body(axis, size, count, *refs):
    ins, outs = refs[:count], refs[count : 2 * count]
    local_sem, send_sem, recv_sem = refs[2 * count :]
    me = lax.axis_index(axis)
    peers = [lax.rem(me + step, size) for step in range(1, size)]
    greet([{axis: peer} for peer in peers])
    copies = []
    for at, peer in enumerate(peers):
        for which in range(count):
            copy = remote(
                ins[which].at[peer],
                outs[which].at[me],
                send_sem.at[which, at],
                recv_sem.at[which, at],
                {axis: peer},
            )
            copy.start()
            copies.append(copy)
    own = [
        pltpu.make_async_copy(ins[which].at[me], outs[which].at[me], local_sem.at[which])
        for which in range(count)
    ]
    for copy in own:
        copy.start()
    for copy in own:
        copy.wait()
    for copy in copies:
        copy.wait()


def exchange(axis, arrays, name, cid):
    size = lax.axis_size(axis)
    count = len(arrays)
    return pl.pallas_call(
        partial(exchange_body, axis, size, count),
        name=name,
        out_shape=[shape_of(a.shape, a.dtype) for a in arrays],
        in_specs=[ANY] * count,
        out_specs=[ANY] * count,
        scratch_shapes=[DMA((count,)), DMA((count, size - 1)), DMA((count, size - 1))],
        compiler_params=pltpu.CompilerParams(collective_id=cid, has_side_effects=True),
    )(*arrays)


def gather_body(size, chunks, x, o, local_sem, s1, r1, s2, r2, s3, r3):
    me = lax.axis_index("hidden")
    core = lax.rem(me, 2)
    far = size // 2
    pair = me // 2
    mate = pair * 2 + 1 - core
    others = [lax.rem(pair + step, far) * 2 + core for step in range(1, far)]
    greet([{"hidden": p} for p in others] + [{"hidden": mate}])
    own = pltpu.make_async_copy(x, o.at[me], local_sem)
    own.start()
    rows = x.shape[0] // chunks
    across, beside, onward = [], [], []
    for k in range(chunks):
        part = pl.ds(k * rows, rows)
        for n, peer in enumerate(others):
            copy = remote(x.at[part], o.at[me, part], s1.at[n, k], r1.at[n, k], {"hidden": peer})
            copy.start()
            across.append((n, k, copy))
        copy = remote(x.at[part], o.at[me, part], s2.at[k], r2.at[k], {"hidden": mate})
        copy.start()
        beside.append(copy)
    for n, k, copy in across:
        part = pl.ds(k * rows, rows)
        source = lax.rem(pair + far - (n + 1), far) * 2 + core
        copy.wait_recv()
        slot = o.at[source, part]
        onto = remote(slot, slot, s3.at[n, k], r3.at[n, k], {"hidden": mate})
        onto.start()
        onward.append(onto)
    own.wait()
    for _, _, copy in across:
        copy.wait_send()
    for copy in beside + onward:
        copy.wait()


def gather_hidden(x, name, cid, chunks=8):
    size = lax.axis_size("hidden")
    far = size // 2
    return pl.pallas_call(
        partial(gather_body, size, chunks),
        name=name,
        out_shape=shape_of((size, *x.shape), x.dtype),
        in_specs=[ANY],
        out_specs=ANY,
        scratch_shapes=[DMA]
        + [DMA((far - 1, chunks))] * 2
        + [DMA((chunks,))] * 2
        + [DMA((far - 1, chunks))] * 2,
        compiler_params=pltpu.CompilerParams(collective_id=cid, has_side_effects=True),
    )(x)


def total_body(sizes, x, o, first, second, s1, r1, s2, r2):
    along = ("hidden", "expert")
    me = [lax.axis_index(axis) for axis in along]
    peers = [
        [{axis: lax.rem(me[n] + step, sizes[n])} for step in range(1, sizes[n])]
        for n, axis in enumerate(along)
    ]
    greet(peers[0] + peers[1])
    held = x
    for n, (box, send, recv) in enumerate(((first, s1, r1), (second, s2, r2))):
        copies = []
        for at, peer in enumerate(peers[n]):
            copy = remote(held, box.at[at], send.at[at], recv.at[at], peer)
            copy.start()
            copies.append(copy)
        for copy in copies:
            copy.wait()
        summed = held[...]
        for at in range(sizes[n] - 1):
            summed = summed + box[at]
        o[...] = summed
        held = o


def total_all(x, name, cid):
    sizes = (lax.axis_size("hidden"), lax.axis_size("expert"))
    return pl.pallas_call(
        partial(total_body, sizes),
        name=name,
        out_shape=shape_of(x.shape, x.dtype),
        in_specs=[VMEM],
        out_specs=VMEM,
        scratch_shapes=[
            pltpu.VMEM((sizes[0] - 1, *x.shape), x.dtype),
            pltpu.VMEM((sizes[1] - 1, *x.shape), x.dtype),
            DMA((sizes[0] - 1,)),
            DMA((sizes[0] - 1,)),
            DMA((sizes[1] - 1,)),
            DMA((sizes[1] - 1,)),
        ],
        compiler_params=pltpu.CompilerParams(collective_id=cid, has_side_effects=True),
    )(x)


def sum_scatter_body(axis, size, x, o, box, send, recv):
    me = lax.axis_index(axis)
    peers = [lax.rem(me + step, size) for step in range(1, size)]
    greet([{axis: peer} for peer in peers])
    copies = []
    for at, peer in enumerate(peers):
        copy = remote(x.at[peer], box.at[at], send.at[at], recv.at[at], {axis: peer})
        copy.start()
        copies.append(copy)
    total = x[me].astype(F32)
    for at, copy in enumerate(copies):
        copy.wait_recv()
        total = total + box[at].astype(F32)
    o[...] = total.astype(o.dtype)
    for copy in copies:
        copy.wait_send()


def sum_scatter(axis, x, name, cid, dtype):
    size = lax.axis_size(axis)
    return pl.pallas_call(
        partial(sum_scatter_body, axis, size),
        name=name,
        out_shape=shape_of(x.shape[1:], dtype),
        in_specs=[VMEM],
        out_specs=VMEM,
        scratch_shapes=[
            pltpu.VMEM((size - 1, *x.shape[1:]), x.dtype),
            DMA((size - 1,)),
            DMA((size - 1,)),
        ],
        compiler_params=pltpu.CompilerParams(
            collective_id=cid, has_side_effects=True, vmem_limit_bytes=40 << 20
        ),
    )(x)


def route_body(experts, capacity, ids, ids_t, grad, pos, pos_t, slot, count, out):
    rows = ids.shape[0]
    col = [ids[:, j : j + 1] for j in range(2)]
    row = [ids_t[j : j + 1, :] for j in range(2)]
    lane = iota((rows, LANES), 1)
    hot = [(lane == c).astype(BF) for c in col]
    either = hot[0] + hot[1]
    below = (iota((rows, rows), 0) > iota((rows, rows), 1)).astype(BF)
    before = mm(below, either)
    wide = max(experts, 16)
    deep = iota((wide, rows), 0)
    hot_t = [(deep == r).astype(BF) for r in row]
    either_t = hot_t[0] + hot_t[1]
    above = (iota((rows, rows), 0) < iota((rows, rows), 1)).astype(BF)
    before_t = mm(either_t, above)
    count[...] = jnp.sum(either.astype(F32), axis=0, keepdims=True)
    slots_t = []
    for j in range(2):
        at = jnp.sum(hot[j].astype(F32) * before, axis=1, keepdims=True).astype(I32)
        pos[:, j : j + 1] = col[j] * capacity + at
        slot[:, j : j + 1] = at
        at_t = jnp.sum(hot_t[j].astype(F32) * before_t, axis=0, keepdims=True).astype(I32)
        at_t = row[j] * capacity + at_t
        pos_t[j : j + 1, :] = at_t
        slots_t.append(at_t)
    total = experts * capacity
    half = total // 2
    for n in range(2):
        place = iota((half, rows), 0) + n * half
        pick = ((place == slots_t[0]) | (place == slots_t[1])).astype(BF)
        out[pl.ds(n * half, half), :] = mm(pick, grad[...]).astype(BF)


def doc_bounds(docs, count):
    ends, at = [], 0
    for n in range(count - 1):
        at = at + docs[0, n]
        ends.append(at)
    return ends


def start_of(place, ends):
    begin = jnp.zeros_like(place)
    for end in ends:
        begin = jnp.where(place >= end, end, begin)
    return begin


def end_of(place, ends, last):
    finish = last
    for end in reversed(ends):
        finish = jnp.where(place < end, end, finish)
    return finish


def forward_body(heads, docs, tokens, gain, shift, w_t, h_one, qkv_t, out_t, lse, keys):
    count = tokens.shape[0]
    width = heads * HEAD_DIM
    blocks = count // BLOCK
    ends = doc_bounds(docs, docs.shape[1])

    def project(i, _):
        rows = pl.ds(pl.multiple_of(i * BLOCK, BLOCK), BLOCK)
        normed, _unused = norm_parts(tokens[rows, :].astype(F32))
        hidden = (normed * gain[...] + shift[...]).astype(BF)
        h_one[rows, :] = hidden
        block = mm_nt(w_t[...], hidden)
        qkv_t[0:width, rows] = block[0:width].astype(BF)
        qkv_t[width:, rows] = block[width:].astype(BF)
        for n in range(heads):
            part = block[width + n * HEAD_DIM : width + (n + 1) * HEAD_DIM]
            keys[n, rows, :] = part.T.astype(BF)
        return 0

    lax.fori_loop(0, blocks, project, 0)
    lse[...] = jnp.zeros_like(lse)

    def attend(i, _):
        base = i * BLOCK
        rows = pl.ds(pl.multiple_of(base, BLOCK), BLOCK)
        q_pos = base + iota((1, BLOCK), 1)
        begin = start_of(q_pos, ends)
        first = start_of(base, ends) // BLOCK
        queries = [
            qkv_t[n * HEAD_DIM : (n + 1) * HEAD_DIM, rows] * jnp.asarray(SCALE, BF)
            for n in range(heads)
        ]

        def step(j, carry):
            at = pl.multiple_of(j * BLOCK, BLOCK)
            part = pl.ds(at, BLOCK)
            k_pos = at + iota((BLOCK, BLOCK), 0)
            allowed = (k_pos <= q_pos) & (k_pos >= begin)
            result = []
            for n in range(heads):
                top, total, acc = carry[n]
                score = mm(keys[n, part, :], queries[n])
                score = jnp.where(allowed, score, MASKED)
                new_top = jnp.maximum(top, jnp.max(score, axis=0, keepdims=True))
                fade = jnp.exp(top - new_top)
                weight = jnp.exp(score - new_top)
                total = total * fade + jnp.sum(weight, axis=0, keepdims=True)
                lo = 2 * width + n * HEAD_DIM
                value = qkv_t[lo : lo + HEAD_DIM, part]
                acc = acc * fade + mm(value, weight.astype(BF))
                result.append((new_top, total, acc))
            return tuple(result)

        empty = (
            jnp.full((1, BLOCK), MASKED, F32),
            jnp.zeros((1, BLOCK), F32),
            jnp.zeros((HEAD_DIM, BLOCK), F32),
        )
        final = lax.fori_loop(first, i + 1, step, (empty,) * heads)
        for n in range(heads):
            top, total, acc = final[n]
            out_t[n * HEAD_DIM : (n + 1) * HEAD_DIM, rows] = (acc / total).astype(BF)
            lse[n : n + 1, rows] = top + jnp.log(total)
        return 0

    lax.fori_loop(0, blocks, attend, 0)


def middle_body(
    experts,
    capacity,
    padded,
    tokens,
    att_t,
    w_out,
    gain,
    shift,
    w_router,
    ids,
    slot,
    pos_t,
    residual,
    gates,
    slots,
    gate_rows,
):
    rows = tokens.shape[0]
    res = tokens[...].astype(F32) + mm_tn(att_t[...], w_out[...])
    residual[...] = res
    normed, _unused = norm_parts(res)
    hidden = (normed * gain[...] + shift[...]).astype(BF)
    logits = mm(hidden, w_router[...])
    lane = iota((rows, experts), 1)
    chosen = [
        jnp.sum(jnp.where(lane == ids[:, j : j + 1], logits, 0.0), axis=1, keepdims=True)
        for j in range(2)
    ]
    top = jnp.maximum(chosen[0], chosen[1])
    raised = [jnp.exp(c - top) for c in chosen]
    both = raised[0] + raised[1]
    gate = [r / both for r in raised]
    for j in range(2):
        gates[:, j : j + 1] = gate[j]
    total = experts * capacity
    half = total // 2
    for n in range(2):
        place = iota((half, rows), 0) + n * half
        pick = ((place == pos_t[0:1, :]) | (place == pos_t[1:2, :])).astype(BF)
        slots[pl.ds(n * half, half), :] = mm(pick, hidden).astype(BF)
    column = iota((rows, padded), 1)
    for e in range(experts):
        mix = jnp.zeros((rows, padded), F32)
        for j in range(2):
            here = (ids[:, j : j + 1] == e) & (slot[:, j : j + 1] == column)
            mix = jnp.where(here, gate[j], mix)
        line = jnp.sum(mix, axis=0, keepdims=True)
        gate_rows[e] = jnp.broadcast_to(line, (8, padded))


def experts_body(
    sources, capacity, padded, xs, gs, gate_rows, ups, downs, y, dx, dg, xg, dy, act, dz
):
    rows = xs.shape[0]
    shards = ups.shape[0]
    width = ups.shape[2]
    x, g = xs[...], gs[...]
    y_acc = jnp.zeros((rows, x.shape[1]), F32)
    dx_acc = jnp.zeros((rows, x.shape[1]), F32)
    for c in range(shards):
        z = mm(x, ups[c])
        du = mm_nt(g, downs[c])
        square = z * z
        t = jnp.tanh(z * (GELU_A + GELU_A * GELU_B * square))
        plus = 0.5 + 0.5 * t
        hidden = (z * plus).astype(BF)
        slope = plus + 0.5 * z * (1.0 - t * t) * (GELU_A + 3.0 * GELU_A * GELU_B * square)
        back = (slope * du).astype(BF)
        act[:, c * width : (c + 1) * width] = hidden
        dz[:, c * width : (c + 1) * width] = back
        y_acc = y_acc + mm(hidden, downs[c])
        dx_acc = dx_acc + mm_nt(back, ups[c])
    y_low = y_acc.astype(BF)
    y[...] = y_low
    dx[...] = dx_acc.astype(BF)
    dots = jnp.sum(y_low.astype(F32) * g.astype(F32), axis=1, keepdims=True)
    for s in range(sources):
        part = slice(s * capacity, (s + 1) * capacity)
        gate = gate_rows[s].T[0:capacity, 0:1]
        xg[part, :] = (x[part].astype(F32) * gate).astype(BF)
        dy[part, :] = (g[part].astype(F32) * gate).astype(BF)
        tall = jnp.broadcast_to(dots[part], (capacity, LANES))
        if padded > capacity:
            tall = jnp.concatenate([tall, jnp.zeros((padded - capacity, LANES), F32)], axis=0)
        dg[s] = tall.T[0:8]


def second_body(
    experts,
    capacity,
    padded,
    residual,
    grad,
    dx,
    dg_rows,
    gates,
    ids,
    slot,
    pos,
    att_t,
    w_out,
    gain,
    shift,
    w_router,
    d_res,
    d_att_t,
    w_out_grad,
    sums,
    router_grad,
):
    rows = residual.shape[0]
    normed, inverse = norm_parts(residual[...])
    hidden = (normed * gain[...] + shift[...]).astype(BF)
    gate = [gates[:, j : j + 1] for j in range(2)]
    column = iota((rows, padded), 1)
    dots = []
    for j in range(2):
        mix = jnp.zeros((rows, padded), F32)
        for e in range(experts):
            here = (ids[:, j : j + 1] == e) & (slot[:, j : j + 1] == column)
            mix = jnp.where(here, dg_rows[e, 0:1, :], mix)
        dots.append(jnp.sum(mix, axis=1, keepdims=True))
    mean = gate[0] * dots[0] + gate[1] * dots[1]
    lane = iota((rows, experts), 1)
    d_logits = jnp.zeros((rows, experts), F32)
    for j in range(2):
        d_logits = jnp.where(lane == ids[:, j : j + 1], gate[j] * (dots[j] - mean), d_logits)
    high, low = split_two(d_logits)
    d_hidden = mm_nt(high, w_router[...]) + mm_nt(low, w_router[...])
    router_grad[...] = mm_tn(high, hidden) + mm_tn(low, hidden)
    total = experts * capacity
    place = iota((rows, total), 1)
    for j in range(2):
        pick = (place == pos[:, j : j + 1]).astype(BF)
        d_hidden = d_hidden + gate[j] * mm(pick, dx[...])
    sums[0:1, :] = jnp.sum(d_hidden * normed, axis=0, keepdims=True)
    sums[1:2, :] = jnp.sum(d_hidden, axis=0, keepdims=True)
    d_resid = grad[...].astype(F32) + norm_back(d_hidden, normed, inverse, gain[...])
    d_res[...] = d_resid
    branch = d_resid.astype(BF)
    d_att_t[...] = mm_nt(w_out[...], branch).astype(BF)
    w_out_grad[...] = mm(att_t[...], branch).astype(BF)


def output_body(residual, gates, pos, y, out):
    rows, total = residual.shape[0], y.shape[0]
    place = iota((rows, total), 1)
    result = residual[...]
    for j in range(2):
        pick = (place == pos[:, j : j + 1]).astype(BF)
        result = result + gates[:, j : j + 1] * mm(pick, y[...])
    out[...] = result.astype(BF)


def backward_body(
    heads,
    docs,
    tokens,
    gain,
    h_one,
    qkv_t,
    out_t,
    lse,
    d_att_t,
    w_t,
    d_hidden,
    w_grad,
    sums,
    keys,
    values,
    dots,
    dq_acc,
    dk_acc,
    dv_acc,
    d_qkv,
    w_acc,
):
    count = tokens.shape[0]
    width = heads * HEAD_DIM
    blocks = count // BLOCK
    ends = doc_bounds(docs, docs.shape[1])
    dq_acc[...] = jnp.zeros_like(dq_acc)

    def prepare(i, _):
        rows = pl.ds(pl.multiple_of(i * BLOCK, BLOCK), BLOCK)
        for n in range(heads):
            lo = n * HEAD_DIM
            here = slice(lo, lo + HEAD_DIM)
            keys[n, rows, :] = (
                qkv_t[width + lo : width + lo + HEAD_DIM, rows].astype(F32).T.astype(BF)
            )
            values[n, rows, :] = (
                qkv_t[2 * width + lo : 2 * width + lo + HEAD_DIM, rows].astype(F32).T.astype(BF)
            )
            product = out_t[here, rows].astype(F32) * d_att_t[here, rows].astype(F32)
            dots[n : n + 1, rows] = jnp.sum(product, axis=0, keepdims=True)
        return 0

    lax.fori_loop(0, blocks, prepare, 0)

    def over_keys(j, _):
        at = pl.multiple_of(j * BLOCK, BLOCK)
        part = pl.ds(at, BLOCK)
        k_pos = at + iota((BLOCK, BLOCK), 0)
        last = (end_of(at + BLOCK - 1, ends, count) - 1) // BLOCK
        dk_acc[...] = jnp.zeros_like(dk_acc)
        dv_acc[...] = jnp.zeros_like(dv_acc)

        def over_queries(i, _):
            base = pl.multiple_of(i * BLOCK, BLOCK)
            rows = pl.ds(base, BLOCK)
            q_pos = base + iota((1, BLOCK), 1)
            begin = start_of(q_pos, ends)
            allowed = (k_pos <= q_pos) & (k_pos >= begin)
            for n in range(heads):
                here = slice(n * HEAD_DIM, (n + 1) * HEAD_DIM)
                query = qkv_t[here, rows] * jnp.asarray(SCALE, BF)
                d_att = d_att_t[here, rows]
                score = mm(keys[n, part, :], query) - lse[n : n + 1, rows]
                weight = jnp.exp(jnp.where(allowed, score, MASKED))
                d_weight = mm(values[n, part, :], d_att)
                d_score = (weight * (d_weight - dots[n : n + 1, rows])).astype(BF)
                dv_acc[here, :] += mm_nt(d_att, weight.astype(BF))
                dk_acc[here, :] += mm_nt(query, d_score)
                lo = width + n * HEAD_DIM
                dq_acc[here, rows] += mm(qkv_t[lo : lo + HEAD_DIM, part], d_score)
            return 0

        lax.fori_loop(j, last + 1, over_queries, 0)
        d_qkv[width : 2 * width, part] = dk_acc[...].astype(BF)
        d_qkv[2 * width :, part] = dv_acc[...].astype(BF)
        return 0

    lax.fori_loop(0, blocks, over_keys, 0)
    w_acc[...] = jnp.zeros_like(w_acc)
    sums[...] = jnp.zeros_like(sums)

    def finish(i, _):
        rows = pl.ds(pl.multiple_of(i * BLOCK, BLOCK), BLOCK)
        d_qkv[0:width, rows] = (dq_acc[:, rows] * SCALE).astype(BF)
        block = d_qkv[:, rows]
        grad = mm_tn(block, w_t[...])
        normed, _unused = norm_parts(tokens[rows, :].astype(F32))
        d_hidden[rows, :] = grad.astype(BF)
        sums[0:1, :] += jnp.sum(grad * normed, axis=0, keepdims=True)
        sums[1:2, :] += jnp.sum(grad, axis=0, keepdims=True)
        w_acc[...] += mm(block, h_one[rows, :])
        return 0

    lax.fori_loop(0, blocks, finish, 0)
    w_grad[...] = w_acc[...].astype(BF)


def input_body(tokens, gain, d_res, d_hidden, out):
    normed, inverse = norm_parts(tokens[...].astype(F32))
    grad = d_hidden[...].astype(F32)
    out[...] = (d_res[...] + norm_back(grad, normed, inverse, gain[...])).astype(BF)


def shards(
    tokens,
    doc_lengths,
    expert_ids,
    gain_one,
    shift_one,
    w_query,
    w_key,
    w_value,
    w_out,
    gain_two,
    shift_two,
    w_router,
    w_up,
    w_down,
    out_grad,
):
    rows, model = tokens.shape
    n_expert, n_hidden = lax.axis_size("expert"), lax.axis_size("hidden")
    experts = n_expert * w_up.shape[0]
    capacity = max(2, rows * 2 * 5 // (4 * experts))
    padded = -(-capacity // LANES) * LANES
    total = experts * capacity
    group = rows * n_hidden
    heads = HEADS // n_hidden
    width = heads * HEAD_DIM
    mine = lax.axis_index("hidden") * width
    g1, s1 = gain_one.reshape(1, model), shift_one.reshape(1, model)
    g2, s2 = gain_two.reshape(1, model), shift_two.reshape(1, model)

    pos, pos_t, slot, count, g_slots = local_call(
        partial(route_body, experts, capacity),
        "route",
        [
            shape_of((rows, 2), I32),
            shape_of((2, rows), I32),
            shape_of((rows, 2), I32),
            shape_of((1, LANES), F32),
            shape_of((total, model), BF),
        ],
        expert_ids,
        expert_ids.T,
        out_grad,
    )
    g_in = lax.all_to_all(
        g_slots.reshape(experts, capacity, model), "expert", split_axis=0, concat_axis=0, tiled=True
    ).reshape(total, model)

    all_tokens = gather_hidden(tokens, "gather_tokens", 1).reshape(group, model)
    up_src, down_src, all_tokens = lax.optimization_barrier((w_up, w_down, all_tokens))
    ups = lax.all_gather(up_src, "hidden", axis=0, tiled=True)
    downs = lax.all_gather(down_src, "hidden", axis=0, tiled=True)

    w_t = jnp.concatenate(
        [lax.dynamic_slice(w, (0, mine), (model, width)).T for w in (w_query, w_key, w_value)],
        axis=0,
    )
    h_one, qkv_t, att_own, lse = local_call(
        partial(forward_body, heads),
        "attend",
        [
            shape_of((group, model), BF),
            shape_of((3 * width, group), BF),
            shape_of((width, group), BF),
            shape_of((8, group), F32),
        ],
        doc_lengths,
        all_tokens,
        g1,
        s1,
        w_t,
        specs=[SMEM, VMEM, VMEM, VMEM, VMEM],
        scratch=[pltpu.VMEM((heads, group, HEAD_DIM), BF)],
    )
    att_split = att_own.reshape(width, n_hidden, rows).transpose(1, 0, 2)
    (att_t,) = exchange("hidden", [att_split], "swap_att", 2)
    att_t = att_t.reshape(model, rows)

    residual, gates, x_slots, gate_rows = local_call(
        partial(middle_body, experts, capacity, padded),
        "middle",
        [
            shape_of((rows, model), F32),
            shape_of((rows, 2), F32),
            shape_of((total, model), BF),
            shape_of((experts, 8, padded), F32),
        ],
        tokens,
        att_t,
        w_out,
        g2,
        s2,
        w_router,
        expert_ids,
        slot,
        pos_t,
    )
    x_in, gate_in = exchange(
        "expert", [x_slots.reshape(experts, capacity, model), gate_rows], "dispatch", 3
    )
    x_in = x_in.reshape(total, model)

    per = max(1, 320 // capacity)
    steps = experts // per
    tall = per * capacity
    hidden_units = n_hidden * w_up.shape[2]

    def by_rows(width_of):
        return pl.BlockSpec((tall, width_of), lambda i: (i, 0))

    whole_w = pl.BlockSpec((n_hidden, *w_up.shape[1:]), lambda i: (0, 0, 0))
    by_source = pl.BlockSpec((per, 8, padded), lambda i: (i, 0, 0))
    y_out, dx_out, dg_rows, xg, dy, act, dz = pl.pallas_call(
        partial(experts_body, per, capacity, padded),
        name="experts",
        grid=(steps,),
        out_shape=[
            shape_of((total, model), BF),
            shape_of((total, model), BF),
            shape_of((experts, 8, padded), F32),
            shape_of((total, model), BF),
            shape_of((total, model), BF),
            shape_of((total, hidden_units), BF),
            shape_of((total, hidden_units), BF),
        ],
        in_specs=[by_rows(model), by_rows(model), by_source, whole_w, whole_w],
        out_specs=[
            by_rows(model),
            by_rows(model),
            by_source,
            by_rows(model),
            by_rows(model),
            by_rows(hidden_units),
            by_rows(hidden_units),
        ],
        compiler_params=pltpu.CompilerParams(
            dimension_semantics=("arbitrary",), vmem_limit_bytes=60 << 20
        ),
        cost_estimate=pl.CostEstimate(
            flops=8 * total * model * hidden_units, bytes_accessed=40 << 20, transcendentals=0
        ),
    )(x_in, g_in, gate_in, ups, downs)

    dx_back, dg_back = exchange(
        "expert", [dx_out.reshape(experts, capacity, model), dg_rows], "collect", 4
    )
    dx_back, y_out, act, dz = lax.optimization_barrier((dx_back, y_out, act, dz))
    y_back = lax.all_to_all(
        y_out.reshape(experts, capacity, model), "expert", split_axis=0, concat_axis=0, tiled=True
    ).reshape(total, model)

    trainable = (lax.axis_index("expert") >= experts // 2).astype(F32)
    up_part = lax.dot_general(xg, dz, (((0,), (0,)), ((), ())), preferred_element_type=F32)
    down_part = lax.dot_general(act, dy, (((0,), (0,)), ((), ())), preferred_element_type=F32)
    up_part = up_part.astype(BF).reshape(model, n_hidden, -1).transpose(1, 0, 2)
    down_part = down_part.astype(BF).reshape(n_hidden, -1, model)
    up_grad = lax.psum_scatter(up_part, "hidden", scatter_dimension=0, tiled=True)
    down_grad = lax.psum_scatter(down_part, "hidden", scatter_dimension=0, tiled=True)
    up_grad = up_grad.astype(F32) * trainable
    down_grad = down_grad.astype(F32) * trainable

    d_res, d_att_t, w_out_part, sums_two, router_part = local_call(
        partial(second_body, experts, capacity, padded),
        "second",
        [
            shape_of((rows, model), F32),
            shape_of((model, rows), BF),
            shape_of((model, model), BF),
            shape_of((2, model), F32),
            shape_of((experts, model), F32),
        ],
        residual,
        out_grad,
        dx_back.reshape(total, model),
        dg_back,
        gates,
        expert_ids,
        slot,
        pos,
        att_t,
        w_out,
        g2,
        s2,
        w_router,
    )
    (d_att_in,) = exchange("hidden", [d_att_t.reshape(n_hidden, width, rows)], "swap_datt", 5)
    d_att_own = d_att_in.transpose(1, 0, 2).reshape(width, group)

    d_hidden, w_part, sums_one = local_call(
        partial(backward_body, heads),
        "attend_back",
        [
            shape_of((group, model), BF),
            shape_of((3 * width, model), BF),
            shape_of((2, model), F32),
        ],
        doc_lengths,
        all_tokens,
        g1,
        h_one,
        qkv_t,
        att_own,
        lse,
        d_att_own,
        w_t,
        specs=[SMEM] + [VMEM] * 8,
        scratch=[
            pltpu.VMEM((heads, group, HEAD_DIM), BF),
            pltpu.VMEM((heads, group, HEAD_DIM), BF),
            pltpu.VMEM((8, group), F32),
            pltpu.VMEM((width, group), F32),
            pltpu.VMEM((width, BLOCK), F32),
            pltpu.VMEM((width, BLOCK), F32),
            pltpu.VMEM((3 * width, group), BF),
            pltpu.VMEM((3 * width, model), F32),
        ],
    )
    output = local_call(
        output_body, "output", shape_of((rows, model), BF), residual, gates, pos, y_back
    )
    d_hidden_own = sum_scatter(
        "hidden", d_hidden.reshape(n_hidden, rows, model), "sum_dh", 6, F32
    )
    input_grad = local_call(
        input_body, "input_grad", shape_of((rows, model), BF), tokens, g1, d_res, d_hidden_own
    )

    w_out_own = sum_scatter(
        "hidden", w_out_part.reshape(n_hidden, width, model), "sum_wout", 7, BF
    )
    w_all = jnp.concatenate([w_part, w_out_own], axis=0)
    piece = sum_scatter(
        "expert", w_all.reshape(n_expert, 4 * width // n_expert, model), "sum_w", 8, BF
    )
    pieces = exchange_all(piece, "spread_expert", 9).reshape(4 * width, model)
    full = gather_hidden(pieces, "spread_hidden", 10).reshape(n_hidden, 4, width, model)
    w_grads = [full[:, n].reshape(model, model).T.astype(F32) for n in range(3)]
    w_out_grad = full[:, 3].reshape(model, model).astype(F32)
    counts = jnp.zeros((1, model), F32).at[:, :experts].set(count[:, :experts])
    small = jnp.concatenate([sums_one, sums_two, counts, router_part], axis=0)
    short = small.shape[0]
    small = jnp.pad(small, ((0, -short % 8), (0, 0)))
    small = total_all(small, "total", 11)
    load = small[4, :experts] * experts / (rows * n_expert * n_hidden * 2)
    return (
        output,
        input_grad,
        small[0],
        small[1],
        *w_grads,
        w_out_grad,
        small[2],
        small[3],
        small[5 : 5 + experts].T,
        up_grad,
        down_grad,
        load,
    )


def spread_body(axis, size, x, o, local_sem, send_sem, recv_sem):
    me = lax.axis_index(axis)
    peers = [lax.rem(me + step, size) for step in range(1, size)]
    greet([{axis: peer} for peer in peers])
    copies = []
    for at, peer in enumerate(peers):
        copy = remote(x, o.at[me], send_sem.at[at], recv_sem.at[at], {axis: peer})
        copy.start()
        copies.append(copy)
    own = pltpu.make_async_copy(x, o.at[me], local_sem)
    own.start()
    own.wait()
    for copy in copies:
        copy.wait()


def exchange_all(x, name, cid):
    size = lax.axis_size("expert")
    return pl.pallas_call(
        partial(spread_body, "expert", size),
        name=name,
        out_shape=shape_of((size, *x.shape), x.dtype),
        in_specs=[ANY],
        out_specs=ANY,
        scratch_shapes=[DMA, DMA((size - 1,)), DMA((size - 1,))],
        compiler_params=pltpu.CompilerParams(collective_id=cid, has_side_effects=True),
    )(x)


def solution(mesh):
    in_specs = (
        P(("expert", "hidden"), None),
        P("expert", None),
        P(("expert", "hidden"), None),
        P(),
        P(),
        P(),
        P(),
        P(),
        P(),
        P(),
        P(),
        P(),
        P("expert", None, "hidden"),
        P("expert", "hidden", None),
        P(("expert", "hidden"), None),
    )
    out_specs = (
        P(("expert", "hidden"), None),
        P(("expert", "hidden"), None),
        P(),
        P(),
        P(),
        P(),
        P(),
        P(),
        P(),
        P(),
        P(),
        P("expert", None, "hidden"),
        P("expert", "hidden", None),
        P(),
    )
    return jax.shard_map(shards, mesh=mesh, in_specs=in_specs, out_specs=out_specs, check_vma=False)
```

```python
from functools import partial

import jax
import jax.numpy as jnp
from jax import lax
from jax.experimental import pallas as pl
from jax.experimental.pallas import tpu as pltpu
from jax.sharding import PartitionSpec as P

HEAD_DIM = 64
HEADS = 12
EPSILON = 1e-05
SCALE = 0.125
MASKED = -1e30
BLOCK = 256
LANES = 128
BF = jnp.bfloat16
F32 = jnp.float32
I32 = jnp.int32
MESH = pl.DeviceIdType.MESH
ANY = pl.BlockSpec(memory_space=pl.ANY)
SMEM = pl.BlockSpec(memory_space=pltpu.SMEM)
VMEM = pl.BlockSpec(memory_space=pltpu.VMEM)
DMA = pltpu.SemaphoreType.DMA
GELU_A = 0.7978845608028654
GELU_B = 0.044715


def mm(left, right):
    return jnp.dot(left, right, preferred_element_type=F32)


def mm_nt(left, right):
    return lax.dot_general(left, right, (((1,), (1,)), ((), ())), preferred_element_type=F32)


def mm_tn(left, right):
    return lax.dot_general(left, right, (((0,), (0,)), ((), ())), preferred_element_type=F32)


def iota(shape, axis):
    return lax.broadcasted_iota(I32, shape, axis)


def norm_parts(values):
    centred = values - jnp.mean(values, axis=-1, keepdims=True)
    inverse = lax.rsqrt(jnp.mean(centred * centred, axis=-1, keepdims=True) + EPSILON)
    return centred * inverse, inverse


def norm_back(grad_out, normed, inverse, gain):
    grad_normed = grad_out * gain
    first = jnp.mean(grad_normed, axis=-1, keepdims=True)
    second = jnp.mean(grad_normed * normed, axis=-1, keepdims=True)
    return inverse * (grad_normed - first - normed * second)


def split_two(value):
    high = value.astype(BF)
    return high, (value - high.astype(F32)).astype(BF)


def shape_of(shape, dtype):
    return jax.ShapeDtypeStruct(shape, dtype)


def local_call(body, name, outs, *args, specs=None, scratch=(), flops=0, vmem=60):
    nbytes = sum(a.size * a.dtype.itemsize for a in args)
    return pl.pallas_call(
        body,
        name=name,
        out_shape=outs,
        in_specs=specs or [VMEM] * len(args),
        out_specs=jax.tree.map(lambda _: VMEM, outs),
        scratch_shapes=list(scratch),
        compiler_params=pltpu.CompilerParams(vmem_limit_bytes=vmem << 20),
        cost_estimate=pl.CostEstimate(flops=flops, bytes_accessed=nbytes, transcendentals=0),
    )(*args)


def greet(peers):
    barrier = pltpu.get_barrier_semaphore()
    for peer in peers:
        pl.semaphore_signal(barrier, inc=1, device_id=peer, device_id_type=MESH)
    pl.semaphore_wait(barrier, len(peers))


def remote(src, dst, send, recv, peer):
    return pltpu.make_async_remote_copy(
        src_ref=src, dst_ref=dst, send_sem=send, recv_sem=recv, device_id=peer, device_id_type=MESH
    )


def exchange_body(axis, size, count, *refs):
    ins, outs = refs[:count], refs[count : 2 * count]
    local_sem, send_sem, recv_sem = refs[2 * count :]
    me = lax.axis_index(axis)
    peers = [lax.rem(me + step, size) for step in range(1, size)]
    greet([{axis: peer} for peer in peers])
    copies = []
    for at, peer in enumerate(peers):
        for which in range(count):
            copy = remote(
                ins[which].at[peer],
                outs[which].at[me],
                send_sem.at[which, at],
                recv_sem.at[which, at],
                {axis: peer},
            )
            copy.start()
            copies.append(copy)
    own = [
        pltpu.make_async_copy(ins[which].at[me], outs[which].at[me], local_sem.at[which])
        for which in range(count)
    ]
    for copy in own:
        copy.start()
    for copy in own:
        copy.wait()
    for copy in copies:
        copy.wait()


def exchange(axis, arrays, name, cid):
    size = lax.axis_size(axis)
    count = len(arrays)
    return pl.pallas_call(
        partial(exchange_body, axis, size, count),
        name=name,
        out_shape=[shape_of(a.shape, a.dtype) for a in arrays],
        in_specs=[ANY] * count,
        out_specs=[ANY] * count,
        scratch_shapes=[DMA((count,)), DMA((count, size - 1)), DMA((count, size - 1))],
        compiler_params=pltpu.CompilerParams(collective_id=cid, has_side_effects=True),
    )(*arrays)


def gather_body(size, chunks, x, o, local_sem, s1, r1, s2, r2, s3, r3):
    me = lax.axis_index("hidden")
    core = lax.rem(me, 2)
    far = size // 2
    pair = me // 2
    mate = pair * 2 + 1 - core
    others = [lax.rem(pair + step, far) * 2 + core for step in range(1, far)]
    greet([{"hidden": p} for p in others] + [{"hidden": mate}])
    own = pltpu.make_async_copy(x, o.at[me], local_sem)
    own.start()
    rows = x.shape[0] // chunks
    across, beside, onward = [], [], []
    for k in range(chunks):
        part = pl.ds(k * rows, rows)
        for n, peer in enumerate(others):
            copy = remote(x.at[part], o.at[me, part], s1.at[n, k], r1.at[n, k], {"hidden": peer})
            copy.start()
            across.append((n, k, copy))
        copy = remote(x.at[part], o.at[me, part], s2.at[k], r2.at[k], {"hidden": mate})
        copy.start()
        beside.append(copy)
    for n, k, copy in across:
        part = pl.ds(k * rows, rows)
        source = lax.rem(pair + far - (n + 1), far) * 2 + core
        copy.wait_recv()
        slot = o.at[source, part]
        onto = remote(slot, slot, s3.at[n, k], r3.at[n, k], {"hidden": mate})
        onto.start()
        onward.append(onto)
    own.wait()
    for _, _, copy in across:
        copy.wait_send()
    for copy in beside + onward:
        copy.wait()


def gather_hidden(x, name, cid, chunks=8):
    size = lax.axis_size("hidden")
    far = size // 2
    return pl.pallas_call(
        partial(gather_body, size, chunks),
        name=name,
        out_shape=shape_of((size, *x.shape), x.dtype),
        in_specs=[ANY],
        out_specs=ANY,
        scratch_shapes=[DMA]
        + [DMA((far - 1, chunks))] * 2
        + [DMA((chunks,))] * 2
        + [DMA((far - 1, chunks))] * 2,
        compiler_params=pltpu.CompilerParams(collective_id=cid, has_side_effects=True),
    )(x)


def sum_scatter_body(axis, size, x, o, box, send, recv):
    me = lax.axis_index(axis)
    peers = [lax.rem(me + step, size) for step in range(1, size)]
    greet([{axis: peer} for peer in peers])
    copies = []
    for at, peer in enumerate(peers):
        copy = remote(x.at[peer], box.at[at], send.at[at], recv.at[at], {axis: peer})
        copy.start()
        copies.append(copy)
    total = x[me].astype(F32)
    for at, copy in enumerate(copies):
        copy.wait_recv()
        total = total + box[at].astype(F32)
    o[...] = total.astype(o.dtype)
    for copy in copies:
        copy.wait_send()


def sum_scatter(axis, x, name, cid, dtype):
    size = lax.axis_size(axis)
    return pl.pallas_call(
        partial(sum_scatter_body, axis, size),
        name=name,
        out_shape=shape_of(x.shape[1:], dtype),
        in_specs=[VMEM],
        out_specs=VMEM,
        scratch_shapes=[
            pltpu.VMEM((size - 1, *x.shape[1:]), x.dtype),
            DMA((size - 1,)),
            DMA((size - 1,)),
        ],
        compiler_params=pltpu.CompilerParams(
            collective_id=cid, has_side_effects=True, vmem_limit_bytes=40 << 20
        ),
    )(x)


def moe_body(
    size,
    capacity,
    padded,
    per,
    x_slots,
    gate_rows,
    g_in,
    ups,
    downs,
    dx_back,
    dg_back,
    y_out,
    up_part,
    down_part,
    xv,
    gv,
    gates_v,
    up_v,
    down_v,
    act,
    dz,
    xg,
    dy,
    xg_t,
    dy_t,
    dxv,
    yv,
    dgv,
    y_acc,
    dx_acc,
    load_sem,
    g_sem,
    own_sem,
    xs_sem,
    xr_sem,
    gs_sem,
    gr_sem,
    ds_sem,
    dr_sem,
    ts_sem,
    tr_sem,
    out_sem,
):
    me = lax.axis_index("expert")
    shards_n = ups.shape[0]
    tall = per * capacity
    steps = size // per

    def to_peer(p):
        return lax.rem(me + 3 * p, size)

    def from_peer(p):
        return lax.rem(me + 3 * (size - p), size)

    def rows_of(p):
        return pl.ds(pl.multiple_of(p * capacity, capacity), capacity)

    def send_x(p):
        peer = to_peer(p)
        return remote(
            x_slots.at[peer], xv.at[rows_of(p)], xs_sem.at[p], xr_sem.at[p], {"expert": peer}
        )

    def send_gate(p):
        peer = to_peer(p)
        return remote(
            gate_rows.at[peer], gates_v.at[p], gs_sem.at[p], gr_sem.at[p], {"expert": peer}
        )

    def send_dx(p):
        peer = from_peer(p)
        return remote(
            dxv.at[rows_of(p)], dx_back.at[me], ds_sem.at[p], dr_sem.at[p], {"expert": peer}
        )

    def send_dg(p):
        peer = from_peer(p)
        return remote(dgv.at[p], dg_back.at[me], ts_sem.at[p], tr_sem.at[p], {"expert": peer})

    def load_g(p):
        return pltpu.make_async_copy(g_in.at[from_peer(p)], gv.at[rows_of(p)], g_sem.at[p])

    def save_y(p):
        return pltpu.make_async_copy(yv.at[rows_of(p)], y_out.at[from_peer(p)], out_sem.at[p])

    own_x = pltpu.make_async_copy(x_slots.at[me], xv.at[rows_of(0)], own_sem.at[0])
    own_gate = pltpu.make_async_copy(gate_rows.at[me], gates_v.at[0], own_sem.at[1])
    own_dx = pltpu.make_async_copy(dxv.at[rows_of(0)], dx_back.at[me], own_sem.at[2])
    own_dg = pltpu.make_async_copy(dgv.at[0], dg_back.at[me], own_sem.at[3])
    loads = [pltpu.make_async_copy(ups, up_v, load_sem.at[0])]
    loads += [pltpu.make_async_copy(downs, down_v, load_sem.at[1])]
    own_x.start()
    own_gate.start()
    for p in range(size):
        load_g(p).start()
    for load in loads:
        load.start()
    greet([{"expert": lax.rem(me + step, size)} for step in range(1, size)])
    for p in range(1, size):
        send_x(p).start()
        send_gate(p).start()
    own_x.wait()
    own_gate.wait()
    for load in loads:
        load.wait()

    def step_body(step, _):
        base = step * per
        for s in range(per):

            @pl.when(base + s > 0)
            def _arrive(s=s):
                send_x(base + s).wait_recv()
                send_gate(base + s).wait_recv()

            load_g(base + s).wait()
        rows = pl.ds(pl.multiple_of(step * tall, tall), tall)
        x, g = xv[rows, :], gv[rows, :]
        y_acc[...] = jnp.zeros_like(y_acc)
        dx_acc[...] = jnp.zeros_like(dx_acc)

        def shard_body(c, _):
            z = mm(x, up_v[c])
            du = mm_nt(g, down_v[c])
            square = z * z
            t = jnp.tanh(z * (GELU_A + GELU_A * GELU_B * square))
            plus = 0.5 + 0.5 * t
            hidden = (z * plus).astype(BF)
            slope = plus + 0.5 * z * (1.0 - t * t) * (GELU_A + 3.0 * GELU_A * GELU_B * square)
            back = (slope * du).astype(BF)
            act[c, rows, :] = hidden
            dz[c, rows, :] = back
            y_acc[...] += mm(hidden, down_v[c])
            dx_acc[...] += mm_nt(back, up_v[c])
            return 0

        lax.fori_loop(0, shards_n, shard_body, 0)
        dxv[rows, :] = dx_acc[...].astype(BF)
        y_low = y_acc[...].astype(BF)
        yv[rows, :] = y_low
        dots = jnp.sum(y_low.astype(F32) * g.astype(F32), axis=1, keepdims=True)
        for s in range(per):
            p = base + s
            part = slice(s * capacity, (s + 1) * capacity)
            tall_dots = jnp.broadcast_to(dots[part], (capacity, LANES))
            if padded > capacity:
                blank = jnp.zeros((padded - capacity, LANES), F32)
                tall_dots = jnp.concatenate([tall_dots, blank], axis=0)
            dgv[p] = tall_dots.T[0:8]

            @pl.when(p > 0)
            def _give(p=p):
                send_dx(p).start()
                send_dg(p).start()

            @pl.when(p == 0)
            def _keep():
                own_dx.start()
                own_dg.start()

            save_y(p).start()
        for s in range(per):
            p = base + s
            part = slice(s * capacity, (s + 1) * capacity)
            gate = gates_v[p].T[0:capacity, 0:1]
            xg[rows_of(p), :] = (x[part].astype(F32) * gate).astype(BF)
            dy[rows_of(p), :] = (g[part].astype(F32) * gate).astype(BF)
        return 0

    lax.fori_loop(0, steps, step_body, 0)

    total = size * capacity
    turn = 256
    for k in range(total // turn):
        rows = slice(k * turn, (k + 1) * turn)
        xg_t[:, rows] = xg[rows, :].astype(F32).T.astype(BF)
        dy_t[:, rows] = dy[rows, :].astype(F32).T.astype(BF)
    model = xg_t.shape[0]
    bands = model // turn

    def weight_body(n, _):
        c, band = n // bands, lax.rem(n, bands)
        lines = pl.ds(pl.multiple_of(band * turn, turn), turn)
        up_v[c, lines, :] = mm(xg_t[lines, :], dz[c]).astype(BF)
        down_v[c, lines, :] = mm(dy_t[lines, :], act[c]).astype(BF)
        return 0

    lax.fori_loop(0, shards_n * bands, weight_body, 0)
    keep_up = pltpu.make_async_copy(up_v, up_part, load_sem.at[0])
    keep_down = pltpu.make_async_copy(down_v, down_part, load_sem.at[1])
    keep_up.start()
    keep_down.start()
    for p in range(1, size):
        send_x(p).wait_send()
        send_gate(p).wait_send()
        send_dx(p).wait()
        send_dg(p).wait()
    for p in range(size):
        save_y(p).wait()
    own_dx.wait()
    own_dg.wait()
    keep_up.wait()
    keep_down.wait()


def run_experts(x_slots, gate_rows, g_in, ups, downs, cid):
    size = lax.axis_size("expert")
    experts, capacity, model = x_slots.shape
    padded = gate_rows.shape[2]
    shards_n, _unused, width = ups.shape
    total = experts * capacity
    per = 1
    while per * 2 * capacity <= 320 and size % (per * 2) == 0:
        per *= 2
    tall = per * capacity
    rows2 = (total, model)
    return pl.pallas_call(
        partial(moe_body, size, capacity, padded, per),
        name="experts",
        out_shape=[
            shape_of(x_slots.shape, BF),
            shape_of(gate_rows.shape, F32),
            shape_of(x_slots.shape, BF),
            shape_of((shards_n, model, width), BF),
            shape_of((shards_n, model, width), BF),
        ],
        in_specs=[ANY] * 5,
        out_specs=[ANY] * 5,
        scratch_shapes=[
            pltpu.VMEM(rows2, BF),
            pltpu.VMEM(rows2, BF),
            pltpu.VMEM(gate_rows.shape, F32),
            pltpu.VMEM((shards_n, model, width), BF),
            pltpu.VMEM((shards_n, width, model), BF),
            pltpu.VMEM((shards_n, total, width), BF),
            pltpu.VMEM((shards_n, total, width), BF),
            pltpu.VMEM(rows2, BF),
            pltpu.VMEM(rows2, BF),
            pltpu.VMEM((model, total), BF),
            pltpu.VMEM((model, total), BF),
            pltpu.VMEM(rows2, BF),
            pltpu.VMEM(rows2, BF),
            pltpu.VMEM(gate_rows.shape, F32),
            pltpu.VMEM((tall, model), F32),
            pltpu.VMEM((tall, model), F32),
            DMA((2,)),
            DMA((size,)),
            DMA((4,)),
        ]
        + [DMA((size,))] * 9,
        compiler_params=pltpu.CompilerParams(
            collective_id=cid, has_side_effects=True, vmem_limit_bytes=60 << 20
        ),
        cost_estimate=pl.CostEstimate(
            flops=12 * total * model * width * shards_n, bytes_accessed=40 << 20, transcendentals=0
        ),
    )(x_slots, gate_rows, g_in, ups, downs)


def tail_body(
    n_e,
    n_h,
    chunks,
    dh,
    w_all,
    small,
    tokens,
    gain,
    d_res,
    residual,
    gates,
    pos,
    y_back,
    input_grad,
    output,
    full,
    total,
    mine,
    beside,
    across,
    passing,
    w_box,
    piece,
    small_mid,
    small_h,
    small_e,
    mine_sem,
    cs_sem,
    cr_sem,
    as_sem,
    ar_sem,
    ws_sem,
    wr_sem,
    hs_sem,
    hr_sem,
    es_sem,
    er_sem,
    keep_sem,
    zs_sem,
    zr_sem,
    xs_sem,
    xr_sem,
    ys_sem,
    yr_sem,
    ms_sem,
    mr_sem,
):
    e, h = lax.axis_index("expert"), lax.axis_index("hidden")
    far, high = n_h // 2, n_e // 2
    pair, core = h // 2, lax.rem(h, 2)
    eh, el = e // 2, lax.rem(e, 2)
    mate = pair * 2 + 1 - core
    greet(
        [{"expert": lax.rem(e + step, n_e)} for step in range(1, n_e)]
        + [{"hidden": lax.rem(h + step, n_h)} for step in range(1, n_h)]
    )
    w_sends = []
    for at in range(n_e - 1):
        peer = lax.rem(e + 1 + at, n_e)
        copy = remote(
            w_all.at[peer], w_box.at[at], ws_sem.at[at], wr_sem.at[at], {"expert": peer}
        )
        copy.start()
        w_sends.append(copy)
    rows = dh.shape[1] // chunks
    core_sends = {}
    for step in list(range(1, far)) + [0]:
        there = lax.rem(pair + step, far)
        for k in range(chunks):
            part = pl.ds(k * rows, rows)
            copy = remote(
                dh.at[there * 2 + 1 - core, part],
                beside.at[step, part],
                cs_sem.at[step, k],
                cr_sem.at[step, k],
                {"hidden": mate},
            )
            copy.start()
            core_sends[step, k] = copy
    loads = []
    for step in range(far):
        there = lax.rem(pair + step, far)
        load = pltpu.make_async_copy(dh.at[there * 2 + core], mine.at[step], mine_sem.at[step])
        load.start()
        loads.append(load)
    small_sends = []
    for at in range(n_h - 1):
        peer = lax.rem(h + 1 + at, n_h)
        copy = remote(small, small_h.at[at], hs_sem.at[at], hr_sem.at[at], {"hidden": peer})
        copy.start()
        small_sends.append(copy)
    for load in loads:
        load.wait()
    far_sends = []
    for step in range(1, far):
        there = lax.rem(pair + step, far)
        for k in range(chunks):
            part = pl.ds(k * rows, rows)
            core_sends[step, k].wait_recv()
            both = mine[step, part, :].astype(F32) + beside[step, part, :].astype(F32)
            passing[step - 1, part, :] = both.astype(BF)
            copy = remote(
                passing.at[step - 1, part],
                across.at[step - 1, part],
                as_sem.at[step - 1, k],
                ar_sem.at[step - 1, k],
                {"hidden": there * 2 + core},
            )
            copy.start()
            far_sends.append(copy)
    for copy in small_sends:
        copy.wait_recv()
    summed = small[...]
    for at in range(n_h - 1):
        summed = summed + small_h[at]
    small_mid[...] = summed
    small_out = []
    for at in range(n_e - 1):
        peer = lax.rem(e + 1 + at, n_e)
        copy = remote(small_mid, small_e.at[at], es_sem.at[at], er_sem.at[at], {"expert": peer})
        copy.start()
        small_out.append(copy)
    for copy in w_sends:
        copy.wait_recv()
    acc = w_all[e].astype(F32)
    for at in range(n_e - 1):
        acc = acc + w_box[at].astype(F32)
    piece[...] = acc.astype(BF)
    keep = pltpu.make_async_copy(piece, full.at[h, e], keep_sem)
    keep.start()
    started = []

    def slot(eh_of, el_of, pair_of, core_of):
        return full.at[pair_of * 2 + core_of, eh_of * 2 + el_of]

    def back(step, size, place):
        return lax.rem(place + size - step, size)

    def give_z(source):
        for s in range(1, high):
            there = lax.rem(eh + s, high) * 2 + el
            copy = remote(
                source, slot(eh, el, pair, core), zs_sem.at[s], zr_sem.at[s], {"expert": there}
            )
            copy.start()
            started.append(copy)

    def z_arrival(s):
        place = slot(back(s, high, eh), el, pair, core)
        return place, remote(place, place, zs_sem.at[s], zr_sem.at[s], {"expert": e})

    def give_x(source, s):
        target = slot(back(s, high, eh), el, pair, core)
        copy = remote(
            source, target, xs_sem.at[s], xr_sem.at[s], {"expert": eh * 2 + 1 - el}
        )
        copy.start()
        started.append(copy)

    def x_arrival(s):
        place = slot(back(s, high, eh), 1 - el, pair, core)
        return place, remote(place, place, xs_sem.at[s], xr_sem.at[s], {"expert": e})

    def give_y(source, s, flag):
        target = slot(back(s, high, eh), el if flag == 0 else 1 - el, pair, core)
        for t in range(1, far):
            there = lax.rem(pair + t, far) * 2 + core
            at = 2 * s + flag
            copy = remote(
                source, target, ys_sem.at[t, at], yr_sem.at[t, at], {"hidden": there}
            )
            copy.start()
            started.append(copy)

    def y_arrival(t, s, flag):
        other = el if flag == 0 else 1 - el
        place = slot(back(s, high, eh), other, back(t, far, pair), core)
        at = 2 * s + flag
        return place, remote(place, place, ys_sem.at[t, at], yr_sem.at[t, at], {"hidden": h})

    def give_mate(source, t, s, flag):
        other = el if flag == 0 else 1 - el
        target = slot(back(s, high, eh), other, back(t, far, pair), core)
        at = 2 * s + flag
        copy = remote(source, target, ms_sem.at[t, at], mr_sem.at[t, at], {"hidden": mate})
        copy.start()
        started.append(copy)

    def mate_arrival(t, s, flag):
        other = el if flag == 0 else 1 - el
        place = slot(back(s, high, eh), other, back(t, far, pair), 1 - core)
        at = 2 * s + flag
        return place, remote(place, place, ms_sem.at[t, at], mr_sem.at[t, at], {"hidden": h})

    give_z(piece)
    give_x(piece, 0)
    give_y(piece, 0, 0)
    give_mate(piece, 0, 0, 0)
    for s in range(1, high):
        place, arrival = z_arrival(s)
        arrival.wait_recv()
        give_x(place, s)
        give_y(place, s, 0)
        give_mate(place, 0, s, 0)
    for s in range(high):
        place, arrival = x_arrival(s)
        arrival.wait_recv()
        give_y(place, s, 1)
        give_mate(place, 0, s, 1)
    place_of = iota((residual.shape[0], y_back.shape[0]), 1)
    result = residual[...]
    for j in range(2):
        pick = (place_of == pos[:, j : j + 1]).astype(BF)
        result = result + gates[:, j : j + 1] * mm(pick, y_back[...])
    output[...] = result.astype(BF)
    for copy in small_out:
        copy.wait_recv()
    summed = small_mid[...]
    for at in range(n_e - 1):
        summed = summed + small_e[at]
    total[...] = summed
    for k in range(chunks):
        part = pl.ds(k * rows, rows)
        core_sends[0, k].wait_recv()
    for copy in far_sends:
        copy.wait_recv()
    grad = mine[0].astype(F32) + beside[0].astype(F32)
    for step in range(far - 1):
        grad = grad + across[step].astype(F32)
    normed, inverse = norm_parts(tokens[...].astype(F32))
    input_grad[...] = (d_res[...] + norm_back(grad, normed, inverse, gain[...])).astype(BF)
    for t in range(1, far):
        for s in range(high):
            for flag in range(2):
                place, arrival = y_arrival(t, s, flag)
                arrival.wait_recv()
                give_mate(place, t, s, flag)
    for t in range(far):
        for s in range(high):
            for flag in range(2):
                _place, arrival = mate_arrival(t, s, flag)
                arrival.wait_recv()
    keep.wait()
    for copy in started + w_sends + small_sends + small_out + far_sends:
        copy.wait_send()
    for copy in core_sends.values():
        copy.wait_send()


def run_tail(dh, w_all, small, tokens, gain, d_res, residual, gates, pos, y_back, cid):
    n_e, n_h = lax.axis_size("expert"), lax.axis_size("hidden")
    far, high = n_h // 2, n_e // 2
    chunks = 4
    _unused, rows, model = dh.shape
    piece = w_all.shape[1:]
    return pl.pallas_call(
        partial(tail_body, n_e, n_h, chunks),
        name="tail",
        out_shape=[
            shape_of((rows, model), BF),
            shape_of((rows, model), BF),
            shape_of((n_h, n_e, *piece), BF),
            shape_of(small.shape, F32),
        ],
        in_specs=[ANY] + [VMEM] * 9,
        out_specs=[VMEM, VMEM, ANY, VMEM],
        scratch_shapes=[
            pltpu.VMEM((far, rows, model), BF),
            pltpu.VMEM((far, rows, model), BF),
            pltpu.VMEM((far - 1, rows, model), BF),
            pltpu.VMEM((far - 1, rows, model), BF),
            pltpu.VMEM((n_e - 1, *piece), BF),
            pltpu.VMEM(piece, BF),
            pltpu.VMEM(small.shape, F32),
            pltpu.VMEM((n_h - 1, *small.shape), F32),
            pltpu.VMEM((n_e - 1, *small.shape), F32),
            DMA((far,)),
            DMA((far, chunks)),
            DMA((far, chunks)),
            DMA((far - 1, chunks)),
            DMA((far - 1, chunks)),
            DMA((n_e - 1,)),
            DMA((n_e - 1,)),
            DMA((n_h - 1,)),
            DMA((n_h - 1,)),
            DMA((n_e - 1,)),
            DMA((n_e - 1,)),
            DMA,
            DMA((high,)),
            DMA((high,)),
            DMA((high,)),
            DMA((high,)),
            DMA((far, n_e)),
            DMA((far, n_e)),
            DMA((far, n_e)),
            DMA((far, n_e)),
        ],
        compiler_params=pltpu.CompilerParams(
            collective_id=cid, has_side_effects=True, vmem_limit_bytes=56 << 20
        ),
    )(dh, w_all, small, tokens, gain, d_res, residual, gates, pos, y_back)


def turn_body(width, full, q_out, k_out, v_out, o_out):
    for n, out in enumerate((q_out, k_out, v_out)):
        part = full[:, n * width : (n + 1) * width, :].astype(F32)
        out[...] = part.reshape(-1, part.shape[2]).T
    part = full[:, 3 * width :, :].astype(F32)
    o_out[...] = part.reshape(-1, part.shape[2])


def turn_weights(full, width):
    n_h, deep, model = full.shape
    cols = 256
    across = pl.BlockSpec((cols, model), lambda i: (i, 0))
    down = pl.BlockSpec((model, cols), lambda i: (0, i))
    square = shape_of((model, model), F32)
    return pl.pallas_call(
        partial(turn_body, width),
        name="turn_weights",
        grid=(model // cols,),
        out_shape=[square] * 4,
        in_specs=[pl.BlockSpec((n_h, deep, cols), lambda i: (0, 0, i))],
        out_specs=[across, across, across, down],
        compiler_params=pltpu.CompilerParams(
            dimension_semantics=("arbitrary",), vmem_limit_bytes=40 << 20
        ),
        cost_estimate=pl.CostEstimate(flops=0, bytes_accessed=14 << 20, transcendentals=0),
    )(full)


def route_body(experts, capacity, ids, ids_t, grad, pos, pos_t, slot, count, out):
    rows = ids.shape[0]
    col = [ids[:, j : j + 1] for j in range(2)]
    row = [ids_t[j : j + 1, :] for j in range(2)]
    lane = iota((rows, LANES), 1)
    hot = [(lane == c).astype(BF) for c in col]
    either = hot[0] + hot[1]
    below = (iota((rows, rows), 0) > iota((rows, rows), 1)).astype(BF)
    before = mm(below, either)
    wide = max(experts, 16)
    deep = iota((wide, rows), 0)
    hot_t = [(deep == r).astype(BF) for r in row]
    either_t = hot_t[0] + hot_t[1]
    above = (iota((rows, rows), 0) < iota((rows, rows), 1)).astype(BF)
    before_t = mm(either_t, above)
    count[...] = jnp.sum(either.astype(F32), axis=0, keepdims=True)
    slots_t = []
    for j in range(2):
        at = jnp.sum(hot[j].astype(F32) * before, axis=1, keepdims=True).astype(I32)
        pos[:, j : j + 1] = col[j] * capacity + at
        slot[:, j : j + 1] = at
        at_t = jnp.sum(hot_t[j].astype(F32) * before_t, axis=0, keepdims=True).astype(I32)
        at_t = row[j] * capacity + at_t
        pos_t[j : j + 1, :] = at_t
        slots_t.append(at_t)
    total = experts * capacity
    half = total // 2
    for n in range(2):
        place = iota((half, rows), 0) + n * half
        pick = ((place == slots_t[0]) | (place == slots_t[1])).astype(BF)
        out[pl.ds(n * half, half), :] = mm(pick, grad[...]).astype(BF)


def doc_bounds(docs, count):
    ends, at = [], 0
    for n in range(count - 1):
        at = at + docs[0, n]
        ends.append(at)
    return ends


def start_of(place, ends):
    begin = jnp.zeros_like(place)
    for end in ends:
        begin = jnp.where(place >= end, end, begin)
    return begin


def end_of(place, ends, last):
    finish = last
    for end in reversed(ends):
        finish = jnp.where(place < end, end, finish)
    return finish


def forward_body(heads, docs, tokens, gain, shift, w_t, h_one, qkv_t, out_t, lse, keys):
    count = tokens.shape[0]
    width = heads * HEAD_DIM
    blocks = count // BLOCK
    ends = doc_bounds(docs, docs.shape[1])

    def project(i, _):
        rows = pl.ds(pl.multiple_of(i * BLOCK, BLOCK), BLOCK)
        normed, _unused = norm_parts(tokens[rows, :].astype(F32))
        hidden = (normed * gain[...] + shift[...]).astype(BF)
        h_one[rows, :] = hidden
        block = mm_nt(w_t[...], hidden)
        qkv_t[0:width, rows] = block[0:width].astype(BF)
        qkv_t[width:, rows] = block[width:].astype(BF)
        for n in range(heads):
            part = block[width + n * HEAD_DIM : width + (n + 1) * HEAD_DIM]
            keys[n, rows, :] = part.T.astype(BF)
        return 0

    lax.fori_loop(0, blocks, project, 0)
    lse[...] = jnp.zeros_like(lse)
    per_device = out_t.shape[2] // BLOCK

    def attend(i, _):
        base = i * BLOCK
        rows = pl.ds(pl.multiple_of(base, BLOCK), BLOCK)
        q_pos = base + iota((1, BLOCK), 1)
        begin = start_of(q_pos, ends)
        first = start_of(base, ends) // BLOCK
        queries = [
            qkv_t[n * HEAD_DIM : (n + 1) * HEAD_DIM, rows] * jnp.asarray(SCALE, BF)
            for n in range(heads)
        ]

        def step(j, carry):
            at = pl.multiple_of(j * BLOCK, BLOCK)
            part = pl.ds(at, BLOCK)
            k_pos = at + iota((BLOCK, BLOCK), 0)
            allowed = (k_pos <= q_pos) & (k_pos >= begin)
            result = []
            for n in range(heads):
                top, total, acc = carry[n]
                score = mm(keys[n, part, :], queries[n])
                score = jnp.where(allowed, score, MASKED)
                new_top = jnp.maximum(top, jnp.max(score, axis=0, keepdims=True))
                fade = jnp.exp(top - new_top)
                weight = jnp.exp(score - new_top)
                total = total * fade + jnp.sum(weight, axis=0, keepdims=True)
                lo = 2 * width + n * HEAD_DIM
                value = qkv_t[lo : lo + HEAD_DIM, part]
                acc = acc * fade + mm(value, weight.astype(BF))
                result.append((new_top, total, acc))
            return tuple(result)

        empty = (
            jnp.full((1, BLOCK), MASKED, F32),
            jnp.zeros((1, BLOCK), F32),
            jnp.zeros((HEAD_DIM, BLOCK), F32),
        )
        final = lax.fori_loop(first, i + 1, step, (empty,) * heads)
        cols = pl.ds(pl.multiple_of(lax.rem(i, per_device) * BLOCK, BLOCK), BLOCK)
        for n in range(heads):
            top, total, acc = final[n]
            out_t[i // per_device, n * HEAD_DIM : (n + 1) * HEAD_DIM, cols] = (acc / total).astype(BF)
            lse[n : n + 1, rows] = top + jnp.log(total)
        return 0

    lax.fori_loop(0, blocks, attend, 0)


def middle_body(
    experts,
    capacity,
    padded,
    tokens,
    att_t,
    w_out,
    gain,
    shift,
    w_router,
    ids,
    slot,
    pos_t,
    residual,
    gates,
    slots,
    gate_rows,
):
    rows = tokens.shape[0]
    res = tokens[...].astype(F32) + mm_tn(att_t[...], w_out[...])
    residual[...] = res
    normed, _unused = norm_parts(res)
    hidden = (normed * gain[...] + shift[...]).astype(BF)
    logits = mm(hidden, w_router[...])
    lane = iota((rows, experts), 1)
    chosen = [
        jnp.sum(jnp.where(lane == ids[:, j : j + 1], logits, 0.0), axis=1, keepdims=True)
        for j in range(2)
    ]
    top = jnp.maximum(chosen[0], chosen[1])
    raised = [jnp.exp(c - top) for c in chosen]
    both = raised[0] + raised[1]
    gate = [r / both for r in raised]
    for j in range(2):
        gates[:, j : j + 1] = gate[j]
    total = experts * capacity
    half = total // 2
    for n in range(2):
        place = iota((half, rows), 0) + n * half
        pick = ((place == pos_t[0:1, :]) | (place == pos_t[1:2, :])).astype(BF)
        slots[pl.ds(n * half, half), :] = mm(pick, hidden).astype(BF)
    column = iota((rows, padded), 1)
    for e in range(experts):
        mix = jnp.zeros((rows, padded), F32)
        for j in range(2):
            here = (ids[:, j : j + 1] == e) & (slot[:, j : j + 1] == column)
            mix = jnp.where(here, gate[j], mix)
        line = jnp.sum(mix, axis=0, keepdims=True)
        gate_rows[e] = jnp.broadcast_to(line, (8, padded))


def second_body(
    experts,
    capacity,
    padded,
    residual,
    grad,
    dx,
    dg_rows,
    gates,
    ids,
    slot,
    pos,
    att_t,
    w_out,
    gain,
    shift,
    w_router,
    d_res,
    d_att_t,
    w_out_grad,
    sums,
    router_grad,
):
    rows = residual.shape[0]
    normed, inverse = norm_parts(residual[...])
    hidden = (normed * gain[...] + shift[...]).astype(BF)
    gate = [gates[:, j : j + 1] for j in range(2)]
    column = iota((rows, padded), 1)
    dots = []
    for j in range(2):
        mix = jnp.zeros((rows, padded), F32)
        for e in range(experts):
            here = (ids[:, j : j + 1] == e) & (slot[:, j : j + 1] == column)
            mix = jnp.where(here, dg_rows[e, 0:1, :], mix)
        dots.append(jnp.sum(mix, axis=1, keepdims=True))
    mean = gate[0] * dots[0] + gate[1] * dots[1]
    lane = iota((rows, experts), 1)
    d_logits = jnp.zeros((rows, experts), F32)
    for j in range(2):
        d_logits = jnp.where(lane == ids[:, j : j + 1], gate[j] * (dots[j] - mean), d_logits)
    high, low = split_two(d_logits)
    d_hidden = mm_nt(high, w_router[...]) + mm_nt(low, w_router[...])
    router_grad[...] = mm_tn(high, hidden) + mm_tn(low, hidden)
    total = experts * capacity
    place = iota((rows, total), 1)
    for j in range(2):
        pick = (place == pos[:, j : j + 1]).astype(BF)
        d_hidden = d_hidden + gate[j] * mm(pick, dx[...])
    sums[0:1, :] = jnp.sum(d_hidden * normed, axis=0, keepdims=True)
    sums[1:2, :] = jnp.sum(d_hidden, axis=0, keepdims=True)
    d_resid = grad[...].astype(F32) + norm_back(d_hidden, normed, inverse, gain[...])
    d_res[...] = d_resid
    branch = d_resid.astype(BF)
    d_att_t[...] = mm_nt(w_out[...], branch).astype(BF)
    w_out_grad[...] = mm(att_t[...], branch).astype(BF)


def backward_body(
    heads,
    docs,
    tokens,
    gain,
    h_one,
    qkv_t,
    out_t,
    lse,
    d_att_t,
    w_t,
    d_hidden,
    w_grad,
    sums,
    keys,
    values,
    dots,
    dq_acc,
    dk_acc,
    dv_acc,
    d_qkv,
    w_acc,
):
    count = tokens.shape[0]
    width = heads * HEAD_DIM
    blocks = count // BLOCK
    ends = doc_bounds(docs, docs.shape[1])
    dq_acc[...] = jnp.zeros_like(dq_acc)
    per_device = out_t.shape[2] // BLOCK

    def cols_of(i):
        return pl.ds(pl.multiple_of(lax.rem(i, per_device) * BLOCK, BLOCK), BLOCK)

    def prepare(i, _):
        rows = pl.ds(pl.multiple_of(i * BLOCK, BLOCK), BLOCK)
        cols = cols_of(i)
        for n in range(heads):
            lo = n * HEAD_DIM
            here = slice(lo, lo + HEAD_DIM)
            keys[n, rows, :] = (
                qkv_t[width + lo : width + lo + HEAD_DIM, rows].astype(F32).T.astype(BF)
            )
            values[n, rows, :] = (
                qkv_t[2 * width + lo : 2 * width + lo + HEAD_DIM, rows].astype(F32).T.astype(BF)
            )
            product = out_t[i // per_device, here, cols].astype(F32)
            product = product * d_att_t[i // per_device, here, cols].astype(F32)
            dots[n : n + 1, rows] = jnp.sum(product, axis=0, keepdims=True)
        return 0

    lax.fori_loop(0, blocks, prepare, 0)

    def over_keys(j, _):
        at = pl.multiple_of(j * BLOCK, BLOCK)
        part = pl.ds(at, BLOCK)
        k_pos = at + iota((BLOCK, BLOCK), 0)
        last = (end_of(at + BLOCK - 1, ends, count) - 1) // BLOCK
        dk_acc[...] = jnp.zeros_like(dk_acc)
        dv_acc[...] = jnp.zeros_like(dv_acc)

        def over_queries(i, _):
            base = pl.multiple_of(i * BLOCK, BLOCK)
            rows = pl.ds(base, BLOCK)
            q_pos = base + iota((1, BLOCK), 1)
            begin = start_of(q_pos, ends)
            allowed = (k_pos <= q_pos) & (k_pos >= begin)
            for n in range(heads):
                here = slice(n * HEAD_DIM, (n + 1) * HEAD_DIM)
                query = qkv_t[here, rows] * jnp.asarray(SCALE, BF)
                d_att = d_att_t[i // per_device, here, cols_of(i)]
                score = mm(keys[n, part, :], query) - lse[n : n + 1, rows]
                weight = jnp.exp(jnp.where(allowed, score, MASKED))
                d_weight = mm(values[n, part, :], d_att)
                d_score = (weight * (d_weight - dots[n : n + 1, rows])).astype(BF)
                dv_acc[here, :] += mm_nt(d_att, weight.astype(BF))
                dk_acc[here, :] += mm_nt(query, d_score)
                lo = width + n * HEAD_DIM
                dq_acc[here, rows] += mm(qkv_t[lo : lo + HEAD_DIM, part], d_score)
            return 0

        lax.fori_loop(j, last + 1, over_queries, 0)
        d_qkv[width : 2 * width, part] = dk_acc[...].astype(BF)
        d_qkv[2 * width :, part] = dv_acc[...].astype(BF)
        return 0

    lax.fori_loop(0, blocks, over_keys, 0)
    w_acc[...] = jnp.zeros_like(w_acc)
    sums[...] = jnp.zeros_like(sums)

    def finish(i, _):
        rows = pl.ds(pl.multiple_of(i * BLOCK, BLOCK), BLOCK)
        d_qkv[0:width, rows] = (dq_acc[:, rows] * SCALE).astype(BF)
        block = d_qkv[:, rows]
        grad = mm_tn(block, w_t[...])
        normed, _unused = norm_parts(tokens[rows, :].astype(F32))
        d_hidden[rows, :] = grad.astype(BF)
        sums[0:1, :] += jnp.sum(grad * normed, axis=0, keepdims=True)
        sums[1:2, :] += jnp.sum(grad, axis=0, keepdims=True)
        w_acc[...] += mm(block, h_one[rows, :])
        return 0

    lax.fori_loop(0, blocks, finish, 0)
    w_grad[...] = w_acc[...].astype(BF)


def shards(
    tokens,
    doc_lengths,
    expert_ids,
    gain_one,
    shift_one,
    w_query,
    w_key,
    w_value,
    w_out,
    gain_two,
    shift_two,
    w_router,
    w_up,
    w_down,
    out_grad,
):
    rows, model = tokens.shape
    n_expert, n_hidden = lax.axis_size("expert"), lax.axis_size("hidden")
    experts = n_expert * w_up.shape[0]
    capacity = max(2, rows * 2 * 5 // (4 * experts))
    capacity = -(-capacity // 16) * 16
    padded = -(-capacity // LANES) * LANES
    total = experts * capacity
    group = rows * n_hidden
    heads = HEADS // n_hidden
    width = heads * HEAD_DIM
    mine = lax.axis_index("hidden") * width
    g1, s1 = gain_one.reshape(1, model), shift_one.reshape(1, model)
    g2, s2 = gain_two.reshape(1, model), shift_two.reshape(1, model)

    pos, pos_t, slot, count, g_slots = local_call(
        partial(route_body, experts, capacity),
        "route",
        [
            shape_of((rows, 2), I32),
            shape_of((2, rows), I32),
            shape_of((rows, 2), I32),
            shape_of((1, LANES), F32),
            shape_of((total, model), BF),
        ],
        expert_ids,
        expert_ids.T,
        out_grad,
    )
    g_in = lax.all_to_all(
        g_slots.reshape(experts, capacity, model), "expert", split_axis=0, concat_axis=0, tiled=True
    )

    all_tokens = gather_hidden(tokens, "gather_tokens", 1).reshape(group, model)
    up_src, down_src, all_tokens = lax.optimization_barrier((w_up, w_down, all_tokens))
    ups = lax.all_gather(up_src, "hidden", axis=0, tiled=True)
    downs = lax.all_gather(down_src, "hidden", axis=0, tiled=True)

    w_t = jnp.concatenate(
        [lax.dynamic_slice(w, (0, mine), (model, width)).T for w in (w_query, w_key, w_value)],
        axis=0,
    )
    h_one, qkv_t, att_own, lse = local_call(
        partial(forward_body, heads),
        "attend",
        [
            shape_of((group, model), BF),
            shape_of((3 * width, group), BF),
            shape_of((n_hidden, width, rows), BF),
            shape_of((8, group), F32),
        ],
        doc_lengths,
        all_tokens,
        g1,
        s1,
        w_t,
        specs=[SMEM, VMEM, VMEM, VMEM, VMEM],
        scratch=[pltpu.VMEM((heads, group, HEAD_DIM), BF)],
    )
    (att_t,) = exchange("hidden", [att_own], "swap_att", 2)
    att_t = att_t.reshape(model, rows)

    residual, gates, x_slots, gate_rows = local_call(
        partial(middle_body, experts, capacity, padded),
        "middle",
        [
            shape_of((rows, model), F32),
            shape_of((rows, 2), F32),
            shape_of((total, model), BF),
            shape_of((experts, 8, padded), F32),
        ],
        tokens,
        att_t,
        w_out,
        g2,
        s2,
        w_router,
        expert_ids,
        slot,
        pos_t,
    )
    dx_back, dg_back, y_out, up_part, down_part = run_experts(
        x_slots.reshape(experts, capacity, model), gate_rows, g_in, ups, downs, 3
    )
    y_back = lax.all_to_all(y_out, "expert", split_axis=0, concat_axis=0, tiled=True)
    y_back = y_back.reshape(total, model)

    trainable = (lax.axis_index("expert") >= experts // 2).astype(F32)
    up_grad = lax.psum_scatter(up_part, "hidden", scatter_dimension=0, tiled=True)
    down_grad = lax.psum_scatter(down_part, "hidden", scatter_dimension=0, tiled=True)
    up_grad = up_grad.astype(F32) * trainable
    down_grad = down_grad.astype(F32).transpose(0, 2, 1) * trainable

    d_res, d_att_t, w_out_part, sums_two, router_part = local_call(
        partial(second_body, experts, capacity, padded),
        "second",
        [
            shape_of((rows, model), F32),
            shape_of((model, rows), BF),
            shape_of((model, model), BF),
            shape_of((2, model), F32),
            shape_of((experts, model), F32),
        ],
        residual,
        out_grad,
        dx_back.reshape(total, model),
        dg_back,
        gates,
        expert_ids,
        slot,
        pos,
        att_t,
        w_out,
        g2,
        s2,
        w_router,
    )
    (d_att_in,) = exchange("hidden", [d_att_t.reshape(n_hidden, width, rows)], "swap_datt", 5)

    d_hidden, w_part, sums_one = local_call(
        partial(backward_body, heads),
        "attend_back",
        [
            shape_of((group, model), BF),
            shape_of((3 * width, model), BF),
            shape_of((2, model), F32),
        ],
        doc_lengths,
        all_tokens,
        g1,
        h_one,
        qkv_t,
        att_own,
        lse,
        d_att_in,
        w_t,
        specs=[SMEM] + [VMEM] * 8,
        scratch=[
            pltpu.VMEM((heads, group, HEAD_DIM), BF),
            pltpu.VMEM((heads, group, HEAD_DIM), BF),
            pltpu.VMEM((8, group), F32),
            pltpu.VMEM((width, group), F32),
            pltpu.VMEM((width, BLOCK), F32),
            pltpu.VMEM((width, BLOCK), F32),
            pltpu.VMEM((3 * width, group), BF),
            pltpu.VMEM((3 * width, model), F32),
        ],
    )
    w_out_own = sum_scatter(
        "hidden", w_out_part.reshape(n_hidden, width, model), "sum_wout", 7, BF
    )

    w_all = jnp.concatenate([w_part, w_out_own], axis=0)
    counts = jnp.zeros((1, model), F32).at[:, :experts].set(count[:, :experts])
    small = jnp.concatenate([sums_one, sums_two, counts, router_part], axis=0)
    small = jnp.pad(small, ((0, -small.shape[0] % 8), (0, 0)))
    input_grad, output, full, small = run_tail(
        d_hidden.reshape(n_hidden, rows, model),
        w_all.reshape(n_expert, 4 * width // n_expert, model),
        small,
        tokens,
        g1,
        d_res,
        residual,
        gates,
        pos,
        y_back,
        8,
    )
    w_grads = turn_weights(full.reshape(n_hidden, 4 * width, model), width)
    load = small[4, :experts] * experts / (rows * n_expert * n_hidden * 2)
    return (
        output,
        input_grad,
        small[0],
        small[1],
        *w_grads,
        small[2],
        small[3],
        small[5 : 5 + experts].T,
        up_grad,
        down_grad,
        load,
    )


def solution(mesh):
    in_specs = (
        P(("expert", "hidden"), None),
        P("expert", None),
        P(("expert", "hidden"), None),
        P(),
        P(),
        P(),
        P(),
        P(),
        P(),
        P(),
        P(),
        P(),
        P("expert", None, "hidden"),
        P("expert", "hidden", None),
        P(("expert", "hidden"), None),
    )
    out_specs = (
        P(("expert", "hidden"), None),
        P(("expert", "hidden"), None),
        P(),
        P(),
        P(),
        P(),
        P(),
        P(),
        P(),
        P(),
        P(),
        P("expert", None, "hidden"),
        P("expert", "hidden", None),
        P(),
    )
    return jax.shard_map(shards, mesh=mesh, in_specs=in_specs, out_specs=out_specs, check_vma=False)
```

```python
from functools import partial

import jax
import jax.numpy as jnp
from jax import lax
from jax.experimental import pallas as pl
from jax.experimental.pallas import tpu as pltpu
from jax.sharding import PartitionSpec as P

HEAD_DIM = 64
HEADS = 12
EPSILON = 1e-05
SCALE = 0.125
MASKED = -1e30
BLOCK = 256
LONGEST = 1024
REACH = LONGEST // BLOCK + 1
LANES = 128
BF = jnp.bfloat16
F32 = jnp.float32
I32 = jnp.int32
MESH = pl.DeviceIdType.MESH
ANY = pl.BlockSpec(memory_space=pl.ANY)
SMEM = pl.BlockSpec(memory_space=pltpu.SMEM)
VMEM = pl.BlockSpec(memory_space=pltpu.VMEM)
DMA = pltpu.SemaphoreType.DMA
GELU_A = 0.7978845608028654
GELU_B = 0.044715


def mm(left, right):
    return jnp.dot(left, right, preferred_element_type=F32)


def mm_nt(left, right):
    return lax.dot_general(left, right, (((1,), (1,)), ((), ())), preferred_element_type=F32)


def mm_tn(left, right):
    return lax.dot_general(left, right, (((0,), (0,)), ((), ())), preferred_element_type=F32)


def iota(shape, axis):
    return lax.broadcasted_iota(I32, shape, axis)


def norm_parts(values):
    centred = values - jnp.mean(values, axis=-1, keepdims=True)
    inverse = lax.rsqrt(jnp.mean(centred * centred, axis=-1, keepdims=True) + EPSILON)
    return centred * inverse, inverse


def norm_back(grad_out, normed, inverse, gain):
    grad_normed = grad_out * gain
    first = jnp.mean(grad_normed, axis=-1, keepdims=True)
    second = jnp.mean(grad_normed * normed, axis=-1, keepdims=True)
    return inverse * (grad_normed - first - normed * second)


def split_two(value):
    high = value.astype(BF)
    return high, (value - high.astype(F32)).astype(BF)


def shape_of(shape, dtype):
    return jax.ShapeDtypeStruct(shape, dtype)


def greet(peers):
    barrier = pltpu.get_barrier_semaphore()
    for peer in peers:
        pl.semaphore_signal(barrier, inc=1, device_id=peer, device_id_type=MESH)
    pl.semaphore_wait(barrier, len(peers))


def remote(src, dst, send, recv, peer):
    return pltpu.make_async_remote_copy(
        src_ref=src, dst_ref=dst, send_sem=send, recv_sem=recv, device_id=peer, device_id_type=MESH
    )


def doc_bounds(docs):
    ends, at = [], 0
    for n in range(docs.shape[1] - 1):
        at = at + docs[0, n]
        ends.append(at)
    return ends


def start_of(place, ends):
    begin = jnp.zeros_like(place)
    for end in ends:
        begin = jnp.where(place >= end, end, begin)
    return begin


def aligned(at, size):
    return pl.ds(pl.multiple_of(at, size), size)


def find_slots(experts, capacity, ids, ids_t, pos, slot, count):
    rows = ids.shape[0]
    col = [ids[:, j : j + 1] for j in range(2)]
    row = [ids_t[j : j + 1, :] for j in range(2)]
    lane = iota((rows, LANES), 1)
    hot = [(lane == c).astype(BF) for c in col]
    either = hot[0] + hot[1]
    below = (iota((rows, rows), 0) > iota((rows, rows), 1)).astype(BF)
    before = mm(below, either)
    wide = max(experts, 16)
    deep = iota((wide, rows), 0)
    hot_t = [(deep == r).astype(BF) for r in row]
    above = (iota((rows, rows), 0) < iota((rows, rows), 1)).astype(BF)
    before_t = mm(hot_t[0] + hot_t[1], above)
    count[...] = jnp.sum(either.astype(F32), axis=0, keepdims=True)
    flat_t = []
    for j in range(2):
        at = jnp.sum(hot[j].astype(F32) * before, axis=1, keepdims=True).astype(I32)
        pos[:, j : j + 1] = col[j] * capacity + at
        slot[:, j : j + 1] = at
        at_t = jnp.sum(hot_t[j].astype(F32) * before_t, axis=0, keepdims=True).astype(I32)
        flat_t.append(row[j] * capacity + at_t)
    return flat_t


def fill_slots(flat_t, source, out):
    total, rows = out.shape[0], source.shape[0]
    half = total // 2
    for n in range(2):
        place = iota((half, rows), 0) + n * half
        pick = ((place == flat_t[0]) | (place == flat_t[1])).astype(BF)
        out[pl.ds(n * half, half), :] = mm(pick, source).astype(BF)


def attend_block(heads, ends, i, qkv, keys, scores, lse):
    width = heads * HEAD_DIM
    base = i * BLOCK
    rows = aligned(base, BLOCK)
    q_pos = base + iota((1, BLOCK), 1)
    begin = start_of(q_pos, ends)
    first = (i - (REACH - 1)) * (i // (REACH - 1))
    queries = [
        qkv[n * HEAD_DIM : (n + 1) * HEAD_DIM, rows] * jnp.asarray(SCALE, BF) for n in range(heads)
    ]
    tops = [jnp.full((1, BLOCK), MASKED, F32)] * heads
    for k in range(REACH):
        part = aligned((first + k) * BLOCK, BLOCK)
        k_pos = (first + k) * BLOCK + iota((BLOCK, BLOCK), 0)
        allowed = (k_pos <= q_pos) & (k_pos >= begin)
        for n in range(heads):
            score = jnp.where(allowed, mm(keys[n, part, :], queries[n]), MASKED)
            scores[n, k] = score
            tops[n] = jnp.maximum(tops[n], jnp.max(score, axis=0, keepdims=True))
    result = []
    for n in range(heads):
        total = jnp.zeros((1, BLOCK), F32)
        acc = jnp.zeros((HEAD_DIM, BLOCK), F32)
        lo = 2 * width + n * HEAD_DIM
        for k in range(REACH):
            weight = jnp.exp(scores[n, k] - tops[n])
            total = total + jnp.sum(weight, axis=0, keepdims=True)
            value = qkv[lo : lo + HEAD_DIM, aligned((first + k) * BLOCK, BLOCK)]
            acc = acc + mm(value, weight.astype(BF))
        lse[n : n + 1, rows] = tops[n] + jnp.log(total)
        result.append((acc / total).astype(BF))
    return result


def front_body(
    n_e,
    n_h,
    experts,
    capacity,
    padded,
    heads,
    chunks,
    docs,
    ids,
    ids_t,
    g1,
    s1,
    g2,
    s2,
    w_router,
    tokens,
    out_grad,
    w_query,
    w_key,
    w_value,
    w_out,
    w_up,
    w_down,
    all_tokens,
    qkv_out,
    att_out,
    att_t_out,
    w_t_out,
    g_in,
    x_slots,
    ups,
    downs,
    pos,
    slot,
    count,
    lse,
    residual,
    gates,
    gate_rows,
    tv,
    gv,
    wv,
    wo,
    w_t,
    qkv,
    keys,
    scores,
    att_v,
    att_in,
    g_slots,
    xs_v,
    own_sem,
    w_sem,
    save_sem,
    ty_s,
    ty_r,
    tc_s,
    tc_r,
    tf_s,
    tf_r,
    gs_s,
    gs_r,
    at_s,
    at_r,
    wy_s,
    wy_r,
    wc_s,
    wc_r,
    wf_s,
    wf_r,
):
    e, h = lax.axis_index("expert"), lax.axis_index("hidden")
    far = n_h // 2
    pair, core = h // 2, lax.rem(h, 2)
    mate = pair * 2 + 1 - core
    rows, model = tokens.shape
    width = heads * HEAD_DIM
    per_device = rows // BLOCK
    ends = doc_bounds(docs)

    def across(t):
        return lax.rem(pair + t, far) * 2 + core

    def origin(t):
        return lax.rem(pair + far - t, far) * 2 + core

    own_tokens = pltpu.make_async_copy(tokens, tv.at[h], own_sem.at[0])
    own_grad = pltpu.make_async_copy(out_grad, gv, own_sem.at[1])
    own_grad.start()
    own_tokens.start()
    w_loads = [
        pltpu.make_async_copy(w, wv.at[n], w_sem.at[n])
        for n, w in enumerate((w_query, w_key, w_value))
    ]
    w_loads.append(pltpu.make_async_copy(w_out, wo, w_sem.at[3]))
    for load in w_loads:
        load.start()
    greet(
        [{"hidden": lax.rem(h + step, n_h)} for step in range(1, n_h)]
        + [{"expert": lax.rem(e + step, n_e)} for step in range(1, n_e)]
    )

    piece = rows // chunks
    sends = []
    for k in range(chunks):
        part = pl.ds(k * piece, piece)
        for t in range(1, far):
            copy = remote(
                tokens.at[part],
                tv.at[h, part],
                ty_s.at[t, k],
                ty_r.at[t, k],
                {"hidden": across(t)},
            )
            copy.start()
            sends.append(copy)
    beside = remote(tokens, tv.at[h], tc_s, tc_r, {"hidden": mate})
    beside.start()
    sends.append(beside)

    flat_t = find_slots(experts, capacity, ids, ids_t, pos, slot, count)
    own_grad.wait()
    fill_slots(flat_t, gv[...], g_slots)
    for step in range(1, n_e):
        peer = lax.rem(e + step, n_e)
        copy = remote(
            g_slots.at[aligned(peer * capacity, capacity)],
            g_in.at[e],
            gs_s.at[step],
            gs_r.at[step],
            {"expert": peer},
        )
        copy.start()
        sends.append(copy)
    own_slots = pltpu.make_async_copy(
        g_slots.at[aligned(e * capacity, capacity)], g_in.at[e], own_sem.at[1]
    )
    own_slots.start()

    def pass_on(t, k):
        part = pl.ds(k * piece, piece)
        place = tv.at[origin(t), part]
        remote(place, place, ty_s.at[t, k], ty_r.at[t, k], {"hidden": across(t)}).wait_recv()
        copy = remote(place, place, tf_s.at[t, k], tf_r.at[t, k], {"hidden": mate})
        copy.start()
        sends.append(copy)

    todo = [(t, k) for k in range(chunks) for t in range(1, far)]
    third = -(-len(todo) // 4)

    def pass_some():
        for _ in range(min(third, len(todo))):
            pass_on(*todo.pop(0))

    pick = (iota((width, model), 1) == iota((width, model), 0) + h * width).astype(BF)
    for n in range(3):
        w_loads[n].wait()
        w_t[n * width : (n + 1) * width, :] = mm_nt(pick, wv[n]).astype(BF)
        if n == 1:
            pass_some()
    save_w = pltpu.make_async_copy(w_t, w_t_out, save_sem.at[0])
    save_w.start()

    def project(source):
        def one(b, _):
            normed, _unused = norm_parts(tv[source, aligned(b * BLOCK, BLOCK), :].astype(F32))
            hidden = (normed * g1[...] + s1[...]).astype(BF)
            block = mm_nt(w_t[...], hidden)
            cols = aligned(source * rows + b * BLOCK, BLOCK)
            qkv[:, cols] = block.astype(BF)
            for n in range(heads):
                lo = width + n * HEAD_DIM
                keys[n, cols, :] = block[lo : lo + HEAD_DIM].T.astype(BF)
            return 0

        lax.fori_loop(0, per_device, one, 0)

    pass_some()
    own_tokens.wait()
    project(h)
    pass_some()
    remote(tokens, tv.at[mate], tc_s, tc_r, {"hidden": mate}).wait_recv()
    project(mate)
    while todo:
        pass_some()

    def weight_part(which, k):
        deep = (w_up, w_down)[which].shape[1] // 2
        return pl.ds(k * deep, deep)

    for which, (source, target) in enumerate(((w_up, ups), (w_down, downs))):
        keep = pltpu.make_async_copy(source.at[0], target.at[h], own_sem.at[2 + which])
        keep.start()
        copy = remote(
            source.at[0], target.at[h], wc_s.at[which], wc_r.at[which], {"hidden": mate}
        )
        copy.start()
        sends.append(copy)
        for k in range(2):
            part = weight_part(which, k)
            for t in range(1, far):
                copy = remote(
                    source.at[0, part],
                    target.at[h, part],
                    wy_s.at[which, t, k],
                    wy_r.at[which, t, k],
                    {"hidden": across(t)},
                )
                copy.start()
                sends.append(copy)
    for t in range(1, far):
        project(origin(t))
    for t in range(1, far):
        there = lax.rem(pair + far - t, far) * 2 + 1 - core
        for k in range(chunks):
            place = tv.at[there, pl.ds(k * piece, piece)]
            remote(place, place, tf_s.at[t, k], tf_r.at[t, k], {"hidden": mate}).wait_recv()
        project(there)
    save_tokens = pltpu.make_async_copy(tv, all_tokens, save_sem.at[1])
    save_qkv = pltpu.make_async_copy(qkv, qkv_out, save_sem.at[2])
    save_tokens.start()
    save_qkv.start()

    lse[...] = jnp.zeros_like(lse)
    owners = []
    for t in range(1, far):
        owners.append(lax.rem(pair + t, far) * 2 + core)
        owners.append(lax.rem(pair + t, far) * 2 + 1 - core)
    owners += [mate, h]
    for at, owner in enumerate(owners):

        def one(b, _, owner=owner):
            done = attend_block(heads, ends, owner * per_device + b, qkv, keys, scores, lse)
            for n in range(heads):
                lo = n * HEAD_DIM
                att_v[owner, lo : lo + HEAD_DIM, aligned(b * BLOCK, BLOCK)] = done[n]
            return 0

        lax.fori_loop(0, per_device, one, 0)
        if at < len(owners) - 1:
            copy = remote(
                att_v.at[owner], att_in.at[h], at_s.at[at], at_r.at[at], {"hidden": owner}
            )
            copy.start()
            sends.append(copy)
    att_in[h] = att_v[h]
    save_att = pltpu.make_async_copy(att_v, att_out, save_sem.at[3])
    save_att.start()
    at = 0
    for t in range(1, far):
        for other in (core, 1 - core):
            place = att_in.at[lax.rem(pair + far - t, far) * 2 + other]
            remote(place, place, at_s.at[at], at_r.at[at], {"hidden": mate}).wait_recv()
            at += 1
    place = att_in.at[mate]
    remote(place, place, at_s.at[at], at_r.at[at], {"hidden": mate}).wait_recv()
    save_att_t = pltpu.make_async_copy(att_in, att_t_out, save_sem.at[4])
    save_att_t.start()

    w_loads[3].wait()
    res = tv[h].astype(F32) + mm_tn(att_in[...].reshape(model, rows), wo[...])
    residual[...] = res
    normed, _unused = norm_parts(res)
    hidden = (normed * g2[...] + s2[...]).astype(BF)
    fill_slots(flat_t, hidden, xs_v)
    save_x = [
        pltpu.make_async_copy(
            xs_v.at[pl.ds(n * capacity, capacity)], x_slots.at[n], save_sem.at[5 + n]
        )
        for n in range(experts)
    ]
    for save in save_x:
        save.start()
    logits = mm(hidden, w_router[...])
    lane = iota((rows, experts), 1)
    chosen = [
        jnp.sum(jnp.where(lane == ids[:, j : j + 1], logits, 0.0), axis=1, keepdims=True)
        for j in range(2)
    ]
    top = jnp.maximum(chosen[0], chosen[1])
    raised = [jnp.exp(c - top) for c in chosen]
    both = raised[0] + raised[1]
    gate = [r / both for r in raised]
    for j in range(2):
        gates[:, j : j + 1] = gate[j]
    column = iota((rows, padded), 1)
    for n in range(experts):
        mix = jnp.zeros((rows, padded), F32)
        for j in range(2):
            here = jnp.where(ids[:, j : j + 1] == n, slot[:, j : j + 1], -1) == column
            mix = jnp.where(here, gate[j], mix)
        line = jnp.sum(mix, axis=0, keepdims=True)
        gate_rows[n] = jnp.broadcast_to(line, (8, padded))

    for which, target in enumerate((ups, downs)):
        for k in range(2):
            part = weight_part(which, k)
            for t in range(1, far):
                place = target.at[origin(t), part]
                remote(
                    place, place, wy_s.at[which, t, k], wy_r.at[which, t, k], {"hidden": mate}
                ).wait_recv()
                copy = remote(
                    place, place, wf_s.at[which, t, k], wf_r.at[which, t, k], {"hidden": mate}
                )
                copy.start()
                sends.append(copy)
    for which, target in enumerate((ups, downs)):
        place = target.at[mate]
        remote(place, place, wc_s.at[which], wc_r.at[which], {"hidden": mate}).wait_recv()
        for k in range(2):
            part = weight_part(which, k)
            for t in range(1, far):
                there = lax.rem(pair + far - t, far) * 2 + 1 - core
                place = target.at[there, part]
                remote(
                    place, place, wf_s.at[which, t, k], wf_r.at[which, t, k], {"hidden": mate}
                ).wait_recv()
        pltpu.make_async_copy(target.at[h], target.at[h], own_sem.at[2 + which]).wait()
    for step in range(1, n_e):
        source = lax.rem(e + n_e - step, n_e)
        place = g_in.at[source]
        remote(place, place, gs_s.at[step], gs_r.at[step], {"expert": e}).wait_recv()
    own_slots.wait()
    for copy in sends:
        copy.wait_send()
    for save in [save_w, save_tokens, save_qkv, save_att, save_att_t, *save_x]:
        save.wait()


def run_front(
    docs, ids, g1, s1, g2, s2, w_router, tokens, out_grad, ws, w_up, w_down, capacity, heads, cid
):
    n_e, n_h = lax.axis_size("expert"), lax.axis_size("hidden")
    experts = n_e * w_up.shape[0]
    rows, model = tokens.shape
    padded = -(-capacity // LANES) * LANES
    width, group, total = heads * HEAD_DIM, rows * n_h, experts * capacity
    far, chunks = n_h // 2, 8

    def pairs(*shape):
        return [DMA(shape), DMA(shape)]

    return pl.pallas_call(
        partial(front_body, n_e, n_h, experts, capacity, padded, heads, chunks),
        name="front",
        out_shape=[
            shape_of((n_h, rows, model), BF),
            shape_of((3 * width, group), BF),
            shape_of((n_h, width, rows), BF),
            shape_of((n_h, width, rows), BF),
            shape_of((3 * width, model), BF),
            shape_of((experts, capacity, model), BF),
            shape_of((experts, capacity, model), BF),
            shape_of((n_h, *w_up.shape[1:]), BF),
            shape_of((n_h, *w_down.shape[1:]), BF),
            shape_of((rows, 2), I32),
            shape_of((rows, 2), I32),
            shape_of((1, LANES), F32),
            shape_of((8, group), F32),
            shape_of((rows, model), F32),
            shape_of((rows, 2), F32),
            shape_of((experts, 8, padded), F32),
        ],
        in_specs=[SMEM] + [VMEM] * 7 + [ANY] * 8,
        out_specs=[ANY] * 9 + [VMEM] * 7,
        scratch_shapes=[
            pltpu.VMEM((n_h, rows, model), BF),
            pltpu.VMEM((rows, model), BF),
            pltpu.VMEM((3, model, model), BF),
            pltpu.VMEM((model, model), BF),
            pltpu.VMEM((3 * width, model), BF),
            pltpu.VMEM((3 * width, group), BF),
            pltpu.VMEM((heads, group, HEAD_DIM), BF),
            pltpu.VMEM((heads, REACH, BLOCK, BLOCK), F32),
            pltpu.VMEM((n_h, width, rows), BF),
            pltpu.VMEM((n_h, width, rows), BF),
            pltpu.VMEM((total, model), BF),
            pltpu.VMEM((total, model), BF),
            DMA((4,)),
            DMA((4,)),
            DMA((5 + experts,)),
            *pairs(far, chunks),
            DMA,
            DMA,
            *pairs(far, chunks),
            *pairs(n_e),
            *pairs(n_h),
            *pairs(2, far, 2),
            *pairs(2),
            *pairs(2, far, 2),
        ],
        compiler_params=pltpu.CompilerParams(
            collective_id=cid, has_side_effects=True, vmem_limit_bytes=58 << 20
        ),
    )(docs, ids, ids.T, g1, s1, g2, s2, w_router, tokens, out_grad, *ws, w_up, w_down)


def moe_body(
    size,
    capacity,
    padded,
    per,
    x_slots,
    gate_rows,
    g_in,
    ups,
    downs,
    dx_back,
    dg_back,
    y_out,
    up_part,
    down_part,
    xv,
    gv,
    gates_v,
    up_v,
    down_v,
    act,
    dz,
    xg,
    dy,
    xg_t,
    dy_t,
    dxv,
    yv,
    dgv,
    y_acc,
    dx_acc,
    load_sem,
    g_sem,
    own_sem,
    xs_sem,
    xr_sem,
    gs_sem,
    gr_sem,
    ds_sem,
    dr_sem,
    ts_sem,
    tr_sem,
    out_sem,
):
    me = lax.axis_index("expert")
    shards_n = ups.shape[0]
    tall = per * capacity
    steps = size // per

    def to_peer(p):
        return lax.rem(me + 3 * p, size)

    def from_peer(p):
        return lax.rem(me + 3 * (size - p), size)

    def rows_of(p):
        return pl.ds(pl.multiple_of(p * capacity, capacity), capacity)

    def send_x(p):
        peer = to_peer(p)
        return remote(
            x_slots.at[peer], xv.at[rows_of(p)], xs_sem.at[p], xr_sem.at[p], {"expert": peer}
        )

    def send_gate(p):
        peer = to_peer(p)
        return remote(
            gate_rows.at[peer], gates_v.at[p], gs_sem.at[p], gr_sem.at[p], {"expert": peer}
        )

    def send_dx(p):
        peer = from_peer(p)
        return remote(
            dxv.at[rows_of(p)], dx_back.at[me], ds_sem.at[p], dr_sem.at[p], {"expert": peer}
        )

    def send_dg(p):
        peer = from_peer(p)
        return remote(dgv.at[p], dg_back.at[me], ts_sem.at[p], tr_sem.at[p], {"expert": peer})

    def load_g(p):
        return pltpu.make_async_copy(g_in.at[from_peer(p)], gv.at[rows_of(p)], g_sem.at[p])

    def save_y(p):
        return pltpu.make_async_copy(yv.at[rows_of(p)], y_out.at[from_peer(p)], out_sem.at[p])

    own_x = pltpu.make_async_copy(x_slots.at[me], xv.at[rows_of(0)], own_sem.at[0])
    own_gate = pltpu.make_async_copy(gate_rows.at[me], gates_v.at[0], own_sem.at[1])
    own_dx = pltpu.make_async_copy(dxv.at[rows_of(0)], dx_back.at[me], own_sem.at[2])
    own_dg = pltpu.make_async_copy(dgv.at[0], dg_back.at[me], own_sem.at[3])
    loads = [pltpu.make_async_copy(ups, up_v, load_sem.at[0])]
    loads += [pltpu.make_async_copy(downs, down_v, load_sem.at[1])]
    own_x.start()
    own_gate.start()
    for p in range(size):
        load_g(p).start()
    for load in loads:
        load.start()
    greet([{"expert": lax.rem(me + step, size)} for step in range(1, size)])
    for p in range(1, size):
        send_x(p).start()
        send_gate(p).start()
    own_x.wait()
    own_gate.wait()
    for load in loads:
        load.wait()

    def step_body(step, _):
        base = step * per
        for s in range(per):

            @pl.when(base + s > 0)
            def _arrive(s=s):
                send_x(base + s).wait_recv()
                send_gate(base + s).wait_recv()

            load_g(base + s).wait()
        rows = pl.ds(pl.multiple_of(step * tall, tall), tall)
        x, g = xv[rows, :], gv[rows, :]
        y_acc[...] = jnp.zeros_like(y_acc)
        dx_acc[...] = jnp.zeros_like(dx_acc)

        def shard_body(c, _):
            z = mm(x, up_v[c])
            du = mm_nt(g, down_v[c])
            square = z * z
            t = jnp.tanh(z * (GELU_A + GELU_A * GELU_B * square))
            plus = 0.5 + 0.5 * t
            hidden = (z * plus).astype(BF)
            slope = plus + 0.5 * z * (1.0 - t * t) * (GELU_A + 3.0 * GELU_A * GELU_B * square)
            back = (slope * du).astype(BF)
            act[c, rows, :] = hidden
            dz[c, rows, :] = back
            y_acc[...] += mm(hidden, down_v[c])
            dx_acc[...] += mm_nt(back, up_v[c])
            return 0

        lax.fori_loop(0, shards_n, shard_body, 0)
        dxv[rows, :] = dx_acc[...].astype(BF)
        y_low = y_acc[...].astype(BF)
        yv[rows, :] = y_low
        dots = jnp.sum(y_low.astype(F32) * g.astype(F32), axis=1, keepdims=True)
        for s in range(per):
            p = base + s
            part = slice(s * capacity, (s + 1) * capacity)
            tall_dots = jnp.broadcast_to(dots[part], (capacity, LANES))
            if padded > capacity:
                blank = jnp.zeros((padded - capacity, LANES), F32)
                tall_dots = jnp.concatenate([tall_dots, blank], axis=0)
            dgv[p] = tall_dots.T[0:8]

            @pl.when(p > 0)
            def _give(p=p):
                send_dx(p).start()
                send_dg(p).start()

            @pl.when(p == 0)
            def _keep():
                own_dx.start()
                own_dg.start()

            save_y(p).start()
        for s in range(per):
            p = base + s
            part = slice(s * capacity, (s + 1) * capacity)
            gate = gates_v[p].T[0:capacity, 0:1]
            xg[rows_of(p), :] = (x[part].astype(F32) * gate).astype(BF)
            dy[rows_of(p), :] = (g[part].astype(F32) * gate).astype(BF)
        return 0

    lax.fori_loop(0, steps, step_body, 0)

    total = size * capacity
    turn = 256
    for k in range(total // turn):
        rows = slice(k * turn, (k + 1) * turn)
        xg_t[:, rows] = xg[rows, :].astype(F32).T.astype(BF)
        dy_t[:, rows] = dy[rows, :].astype(F32).T.astype(BF)
    model = xg_t.shape[0]
    bands = model // turn

    def weight_body(n, _):
        c, band = n // bands, lax.rem(n, bands)
        lines = pl.ds(pl.multiple_of(band * turn, turn), turn)
        up_v[c, lines, :] = mm(xg_t[lines, :], dz[c]).astype(BF)
        down_v[c, lines, :] = mm(dy_t[lines, :], act[c]).astype(BF)
        return 0

    lax.fori_loop(0, shards_n * bands, weight_body, 0)
    keep_up = pltpu.make_async_copy(up_v, up_part, load_sem.at[0])
    keep_down = pltpu.make_async_copy(down_v, down_part, load_sem.at[1])
    keep_up.start()
    keep_down.start()
    for p in range(1, size):
        send_x(p).wait_send()
        send_gate(p).wait_send()
        send_dx(p).wait()
        send_dg(p).wait()
    for p in range(size):
        save_y(p).wait()
    own_dx.wait()
    own_dg.wait()
    keep_up.wait()
    keep_down.wait()


def run_experts(x_slots, gate_rows, g_in, ups, downs, cid):
    size = lax.axis_size("expert")
    experts, capacity, model = x_slots.shape
    padded = gate_rows.shape[2]
    shards_n, _unused, width = ups.shape
    total = experts * capacity
    per = 1
    while per * 2 * capacity <= 320 and size % (per * 2) == 0:
        per *= 2
    tall = per * capacity
    rows2 = (total, model)
    return pl.pallas_call(
        partial(moe_body, size, capacity, padded, per),
        name="experts",
        out_shape=[
            shape_of(x_slots.shape, BF),
            shape_of(gate_rows.shape, F32),
            shape_of(x_slots.shape, BF),
            shape_of((shards_n, model, width), BF),
            shape_of((shards_n, model, width), BF),
        ],
        in_specs=[ANY] * 5,
        out_specs=[ANY] * 5,
        scratch_shapes=[
            pltpu.VMEM(rows2, BF),
            pltpu.VMEM(rows2, BF),
            pltpu.VMEM(gate_rows.shape, F32),
            pltpu.VMEM((shards_n, model, width), BF),
            pltpu.VMEM((shards_n, width, model), BF),
            pltpu.VMEM((shards_n, total, width), BF),
            pltpu.VMEM((shards_n, total, width), BF),
            pltpu.VMEM(rows2, BF),
            pltpu.VMEM(rows2, BF),
            pltpu.VMEM((model, total), BF),
            pltpu.VMEM((model, total), BF),
            pltpu.VMEM(rows2, BF),
            pltpu.VMEM(rows2, BF),
            pltpu.VMEM(gate_rows.shape, F32),
            pltpu.VMEM((tall, model), F32),
            pltpu.VMEM((tall, model), F32),
            DMA((2,)),
            DMA((size,)),
            DMA((4,)),
        ]
        + [DMA((size,))] * 9,
        compiler_params=pltpu.CompilerParams(
            collective_id=cid, has_side_effects=True, vmem_limit_bytes=60 << 20
        ),
        cost_estimate=pl.CostEstimate(
            flops=12 * total * model * width * shards_n, bytes_accessed=40 << 20, transcendentals=0
        ),
    )(x_slots, gate_rows, g_in, ups, downs)


def tail_body(
    n_e,
    n_h,
    chunks,
    dh,
    w_all,
    small,
    tokens,
    gain,
    d_res,
    residual,
    gates,
    pos,
    y_back,
    input_grad,
    output,
    full,
    total,
    mine,
    beside,
    across,
    passing,
    w_box,
    piece,
    small_mid,
    small_h,
    small_e,
    mine_sem,
    cs_sem,
    cr_sem,
    as_sem,
    ar_sem,
    ws_sem,
    wr_sem,
    hs_sem,
    hr_sem,
    es_sem,
    er_sem,
    keep_sem,
    zs_sem,
    zr_sem,
    xs_sem,
    xr_sem,
    ys_sem,
    yr_sem,
    ms_sem,
    mr_sem,
):
    e, h = lax.axis_index("expert"), lax.axis_index("hidden")
    far, high = n_h // 2, n_e // 2
    pair, core = h // 2, lax.rem(h, 2)
    eh, el = e // 2, lax.rem(e, 2)
    mate = pair * 2 + 1 - core
    greet(
        [{"expert": lax.rem(e + step, n_e)} for step in range(1, n_e)]
        + [{"hidden": lax.rem(h + step, n_h)} for step in range(1, n_h)]
    )
    w_sends = []
    for at in range(n_e - 1):
        peer = lax.rem(e + 1 + at, n_e)
        copy = remote(
            w_all.at[peer], w_box.at[at], ws_sem.at[at], wr_sem.at[at], {"expert": peer}
        )
        copy.start()
        w_sends.append(copy)
    rows = dh.shape[1] // chunks
    core_sends = {}
    for step in list(range(1, far)) + [0]:
        there = lax.rem(pair + step, far)
        for k in range(chunks):
            part = pl.ds(k * rows, rows)
            copy = remote(
                dh.at[there * 2 + 1 - core, part],
                beside.at[step, part],
                cs_sem.at[step, k],
                cr_sem.at[step, k],
                {"hidden": mate},
            )
            copy.start()
            core_sends[step, k] = copy
    loads = []
    for step in range(far):
        there = lax.rem(pair + step, far)
        load = pltpu.make_async_copy(dh.at[there * 2 + core], mine.at[step], mine_sem.at[step])
        load.start()
        loads.append(load)
    small_sends = []
    for at in range(n_h - 1):
        peer = lax.rem(h + 1 + at, n_h)
        copy = remote(small, small_h.at[at], hs_sem.at[at], hr_sem.at[at], {"hidden": peer})
        copy.start()
        small_sends.append(copy)
    for load in loads:
        load.wait()
    far_sends = []
    for step in range(1, far):
        there = lax.rem(pair + step, far)
        for k in range(chunks):
            part = pl.ds(k * rows, rows)
            core_sends[step, k].wait_recv()
            both = mine[step, part, :].astype(F32) + beside[step, part, :].astype(F32)
            passing[step - 1, part, :] = both.astype(BF)
            copy = remote(
                passing.at[step - 1, part],
                across.at[step - 1, part],
                as_sem.at[step - 1, k],
                ar_sem.at[step - 1, k],
                {"hidden": there * 2 + core},
            )
            copy.start()
            far_sends.append(copy)
    for copy in small_sends:
        copy.wait_recv()
    summed = small[...]
    for at in range(n_h - 1):
        summed = summed + small_h[at]
    small_mid[...] = summed
    small_out = []
    for at in range(n_e - 1):
        peer = lax.rem(e + 1 + at, n_e)
        copy = remote(small_mid, small_e.at[at], es_sem.at[at], er_sem.at[at], {"expert": peer})
        copy.start()
        small_out.append(copy)
    for copy in w_sends:
        copy.wait_recv()
    acc = w_all[e].astype(F32)
    for at in range(n_e - 1):
        acc = acc + w_box[at].astype(F32)
    piece[...] = acc.astype(BF)
    keep = pltpu.make_async_copy(piece, full.at[h, e], keep_sem)
    keep.start()
    started = []

    def slot(eh_of, el_of, pair_of, core_of):
        return full.at[pair_of * 2 + core_of, eh_of * 2 + el_of]

    def back(step, size, place):
        return lax.rem(place + size - step, size)

    def give_z(source):
        for s in range(1, high):
            there = lax.rem(eh + s, high) * 2 + el
            copy = remote(
                source, slot(eh, el, pair, core), zs_sem.at[s], zr_sem.at[s], {"expert": there}
            )
            copy.start()
            started.append(copy)

    def z_arrival(s):
        place = slot(back(s, high, eh), el, pair, core)
        return place, remote(place, place, zs_sem.at[s], zr_sem.at[s], {"expert": e})

    def give_x(source, s):
        target = slot(back(s, high, eh), el, pair, core)
        copy = remote(
            source, target, xs_sem.at[s], xr_sem.at[s], {"expert": eh * 2 + 1 - el}
        )
        copy.start()
        started.append(copy)

    def x_arrival(s):
        place = slot(back(s, high, eh), 1 - el, pair, core)
        return place, remote(place, place, xs_sem.at[s], xr_sem.at[s], {"expert": e})

    def give_y(source, s, flag):
        target = slot(back(s, high, eh), el if flag == 0 else 1 - el, pair, core)
        for t in range(1, far):
            there = lax.rem(pair + t, far) * 2 + core
            at = 2 * s + flag
            copy = remote(
                source, target, ys_sem.at[t, at], yr_sem.at[t, at], {"hidden": there}
            )
            copy.start()
            started.append(copy)

    def y_arrival(t, s, flag):
        other = el if flag == 0 else 1 - el
        place = slot(back(s, high, eh), other, back(t, far, pair), core)
        at = 2 * s + flag
        return place, remote(place, place, ys_sem.at[t, at], yr_sem.at[t, at], {"hidden": h})

    def give_mate(source, t, s, flag):
        other = el if flag == 0 else 1 - el
        target = slot(back(s, high, eh), other, back(t, far, pair), core)
        at = 2 * s + flag
        copy = remote(source, target, ms_sem.at[t, at], mr_sem.at[t, at], {"hidden": mate})
        copy.start()
        started.append(copy)

    def mate_arrival(t, s, flag):
        other = el if flag == 0 else 1 - el
        place = slot(back(s, high, eh), other, back(t, far, pair), 1 - core)
        at = 2 * s + flag
        return place, remote(place, place, ms_sem.at[t, at], mr_sem.at[t, at], {"hidden": h})

    give_z(piece)
    give_x(piece, 0)
    give_y(piece, 0, 0)
    give_mate(piece, 0, 0, 0)
    for s in range(1, high):
        place, arrival = z_arrival(s)
        arrival.wait_recv()
        give_x(place, s)
        give_y(place, s, 0)
        give_mate(place, 0, s, 0)
    for s in range(high):
        place, arrival = x_arrival(s)
        arrival.wait_recv()
        give_y(place, s, 1)
        give_mate(place, 0, s, 1)
    place_of = iota((residual.shape[0], y_back.shape[0]), 1)
    result = residual[...]
    for j in range(2):
        pick = (place_of == pos[:, j : j + 1]).astype(BF)
        result = result + gates[:, j : j + 1] * mm(pick, y_back[...])
    output[...] = result.astype(BF)
    for copy in small_out:
        copy.wait_recv()
    summed = small_mid[...]
    for at in range(n_e - 1):
        summed = summed + small_e[at]
    total[...] = summed
    for k in range(chunks):
        part = pl.ds(k * rows, rows)
        core_sends[0, k].wait_recv()
    for copy in far_sends:
        copy.wait_recv()
    grad = mine[0].astype(F32) + beside[0].astype(F32)
    for step in range(far - 1):
        grad = grad + across[step].astype(F32)
    normed, inverse = norm_parts(tokens[...].astype(F32))
    input_grad[...] = (d_res[...] + norm_back(grad, normed, inverse, gain[...])).astype(BF)
    for t in range(1, far):
        for s in range(high):
            for flag in range(2):
                place, arrival = y_arrival(t, s, flag)
                arrival.wait_recv()
                give_mate(place, t, s, flag)
    for t in range(far):
        for s in range(high):
            for flag in range(2):
                _place, arrival = mate_arrival(t, s, flag)
                arrival.wait_recv()
    keep.wait()
    for copy in started + w_sends + small_sends + small_out + far_sends:
        copy.wait_send()
    for copy in core_sends.values():
        copy.wait_send()


def run_tail(dh, w_all, small, tokens, gain, d_res, residual, gates, pos, y_back, cid):
    n_e, n_h = lax.axis_size("expert"), lax.axis_size("hidden")
    far, high = n_h // 2, n_e // 2
    chunks = 4
    _unused, rows, model = dh.shape
    piece = w_all.shape[1:]
    return pl.pallas_call(
        partial(tail_body, n_e, n_h, chunks),
        name="tail",
        out_shape=[
            shape_of((rows, model), BF),
            shape_of((rows, model), BF),
            shape_of((n_h, n_e, *piece), BF),
            shape_of(small.shape, F32),
        ],
        in_specs=[ANY] + [VMEM] * 9,
        out_specs=[VMEM, VMEM, ANY, VMEM],
        scratch_shapes=[
            pltpu.VMEM((far, rows, model), BF),
            pltpu.VMEM((far, rows, model), BF),
            pltpu.VMEM((far - 1, rows, model), BF),
            pltpu.VMEM((far - 1, rows, model), BF),
            pltpu.VMEM((n_e - 1, *piece), BF),
            pltpu.VMEM(piece, BF),
            pltpu.VMEM(small.shape, F32),
            pltpu.VMEM((n_h - 1, *small.shape), F32),
            pltpu.VMEM((n_e - 1, *small.shape), F32),
            DMA((far,)),
            DMA((far, chunks)),
            DMA((far, chunks)),
            DMA((far - 1, chunks)),
            DMA((far - 1, chunks)),
            DMA((n_e - 1,)),
            DMA((n_e - 1,)),
            DMA((n_h - 1,)),
            DMA((n_h - 1,)),
            DMA((n_e - 1,)),
            DMA((n_e - 1,)),
            DMA,
            DMA((high,)),
            DMA((high,)),
            DMA((high,)),
            DMA((high,)),
            DMA((far, n_e)),
            DMA((far, n_e)),
            DMA((far, n_e)),
            DMA((far, n_e)),
        ],
        compiler_params=pltpu.CompilerParams(
            collective_id=cid, has_side_effects=True, vmem_limit_bytes=56 << 20
        ),
    )(dh, w_all, small, tokens, gain, d_res, residual, gates, pos, y_back)


def turn_body(width, old, full, dw, q_out, k_out, v_out, o_out, up_out, down_out):
    for n, out in enumerate((q_out, k_out, v_out)):
        part = full[:, n * width : (n + 1) * width, :].astype(F32)
        out[...] = part.reshape(-1, part.shape[2]).T
    part = full[:, 3 * width :, :].astype(F32)
    o_out[...] = part.reshape(-1, part.shape[2])
    trained = jnp.where(lax.axis_index("expert") >= old, 1.0, 0.0)
    up_out[...] = dw[0] * trained
    down_out[...] = dw[1].T * trained


def turn_weights(full, dw, width, old):
    n_h, deep, model = full.shape
    cols = 256
    across = pl.BlockSpec((cols, model), lambda i: (i, 0))
    down = pl.BlockSpec((model, cols), lambda i: (0, i))
    square = shape_of((model, model), F32)
    return pl.pallas_call(
        partial(turn_body, width, old),
        name="turn_weights",
        grid=(model // cols,),
        out_shape=[square] * 6,
        in_specs=[
            pl.BlockSpec((n_h, deep, cols), lambda i: (0, 0, i)),
            pl.BlockSpec((2, model, cols), lambda i: (0, 0, i)),
        ],
        out_specs=[across, across, across, down, down, across],
        compiler_params=pltpu.CompilerParams(
            dimension_semantics=("arbitrary",), vmem_limit_bytes=40 << 20
        ),
        cost_estimate=pl.CostEstimate(flops=0, bytes_accessed=24 << 20, transcendentals=0),
    )(full, dw)


def attend_back(heads, ends, blocks, per_device, qkv, d_att, lse, dots, keys, values, accs, d_qkv):
    width = heads * HEAD_DIM
    dq_acc, dk_acc, dv_acc = accs

    def over_keys(j, _):
        part = aligned(j * BLOCK, BLOCK)
        k_pos = j * BLOCK + iota((BLOCK, BLOCK), 0)
        stop = (j + REACH) - (j - (REACH - 2)) * (j // (REACH - 1))
        dk_acc[...] = jnp.zeros_like(dk_acc)
        dv_acc[...] = jnp.zeros_like(dv_acc)

        def over_queries(i, _):
            rows = aligned(i * BLOCK, BLOCK)
            cols = aligned(lax.rem(i, per_device) * BLOCK, BLOCK)
            q_pos = i * BLOCK + iota((1, BLOCK), 1)
            begin = start_of(q_pos, ends)
            allowed = (k_pos <= q_pos) & (k_pos >= begin)
            for n in range(heads):
                here = slice(n * HEAD_DIM, (n + 1) * HEAD_DIM)
                query = qkv[here, rows] * jnp.asarray(SCALE, BF)
                given = d_att[i // per_device, here, cols]
                score = mm(keys[n, part, :], query) - lse[n : n + 1, rows]
                weight = jnp.exp(jnp.where(allowed, score, MASKED))
                d_weight = mm(values[n, part, :], given)
                d_score = (weight * (d_weight - dots[n : n + 1, rows])).astype(BF)
                dv_acc[here, :] += mm_nt(given, weight.astype(BF))
                dk_acc[here, :] += mm_nt(query, d_score)
                lo = width + n * HEAD_DIM
                dq_acc[here, rows] += mm(qkv[lo : lo + HEAD_DIM, part], d_score)
            return 0

        lax.fori_loop(j, stop, over_queries, 0)
        d_qkv[width : 2 * width, part] = dk_acc[...].astype(BF)
        d_qkv[2 * width :, part] = dv_acc[...].astype(BF)
        return 0

    lax.fori_loop(0, blocks, over_keys, 0)


def back_body(
    n_e,
    n_h,
    experts,
    capacity,
    padded,
    heads,
    docs,
    ids,
    slot,
    pos,
    gates,
    count,
    g1,
    s1,
    g2,
    s2,
    w_router,
    lse,
    dg_rows,
    dx_back,
    y_out,
    up_part,
    down_part,
    out_grad,
    residual,
    all_tokens,
    qkv_in,
    att_in,
    att_t_in,
    w_out,
    w_t_in,
    y_back,
    d_hidden,
    d_res,
    w_all,
    small,
    dw_own,
    dxv,
    gv,
    res_v,
    tv,
    qkv,
    att_v,
    att_t,
    wo,
    w_t,
    d_att_v,
    d_att,
    wo_box,
    keys,
    values,
    dots,
    dq_acc,
    dk_acc,
    dv_acc,
    d_qkv,
    w_acc,
    dw_mine,
    dw_beside,
    dw_across,
    load_sem,
    save_sem,
    dw_sem,
    y_own,
    y_s,
    y_r,
    at_s,
    at_r,
    wo_s,
    wo_r,
    dc_s,
    dc_r,
    da_s,
    da_r,
):
    e, h = lax.axis_index("expert"), lax.axis_index("hidden")
    far = n_h // 2
    pair, core = h // 2, lax.rem(h, 2)
    mate = pair * 2 + 1 - core
    rows, model = out_grad.shape
    width = heads * HEAD_DIM
    group = rows * n_h
    per_device = rows // BLOCK
    blocks = group // BLOCK
    ends = doc_bounds(docs)
    sends = []

    loads = [
        pltpu.make_async_copy(source, target, load_sem.at[n])
        for n, (source, target) in enumerate(
            (
                (residual, res_v),
                (dx_back, dxv),
                (out_grad, gv),
                (w_out, wo),
                (att_t_in, att_t),
                (qkv_in, qkv),
                (att_in, att_v),
                (all_tokens, tv),
                (w_t_in, w_t),
            )
        )
    ]
    for load in loads:
        load.start()
    greet(
        [{"hidden": lax.rem(h + step, n_h)} for step in range(1, n_h)]
        + [{"expert": lax.rem(e + step, n_e)} for step in range(1, n_e)]
    )
    mine = []
    for step in list(range(1, far)) + [0]:
        there = lax.rem(pair + step, far)
        for which, part in enumerate((up_part, down_part)):
            copy = remote(
                part.at[there * 2 + 1 - core],
                dw_beside.at[which, step],
                dc_s.at[which, step],
                dc_r.at[which, step],
                {"hidden": mate},
            )
            copy.start()
            sends.append(copy)
            load = pltpu.make_async_copy(
                part.at[there * 2 + core], dw_mine.at[which, step], dw_sem.at[which, step]
            )
            load.start()
            mine.append(load)
    for step in range(1, n_e):
        peer = lax.rem(e + step, n_e)
        copy = remote(y_out.at[peer], y_back.at[e], y_s.at[step], y_r.at[step], {"expert": peer})
        copy.start()
        sends.append(copy)
    own_y = pltpu.make_async_copy(y_out.at[e], y_back.at[e], y_own)
    own_y.start()

    for load in loads[:3]:
        load.wait()
    normed, inverse = norm_parts(res_v[...])
    hidden = (normed * g2[...] + s2[...]).astype(BF)
    gate = [gates[:, j : j + 1] for j in range(2)]
    column = iota((rows, padded), 1)
    dot_of = []
    for j in range(2):
        mix = jnp.zeros((rows, padded), F32)
        for n in range(experts):
            here = jnp.where(ids[:, j : j + 1] == n, slot[:, j : j + 1], -1) == column
            mix = jnp.where(here, dg_rows[n, 0:1, :], mix)
        dot_of.append(jnp.sum(mix, axis=1, keepdims=True))
    mean = gate[0] * dot_of[0] + gate[1] * dot_of[1]
    lane = iota((rows, experts), 1)
    d_logits = jnp.zeros((rows, experts), F32)
    for j in range(2):
        d_logits = jnp.where(lane == ids[:, j : j + 1], gate[j] * (dot_of[j] - mean), d_logits)
    high, low = split_two(d_logits)
    grad = mm_nt(high, w_router[...]) + mm_nt(low, w_router[...])
    small[...] = jnp.zeros_like(small)
    small[5 : 5 + experts, :] = mm_tn(high, hidden) + mm_tn(low, hidden)
    small[4:5, 0:LANES] = count[...]
    place = iota((rows, experts * capacity), 1)
    for j in range(2):
        pick = (place == pos[:, j : j + 1]).astype(BF)
        grad = grad + gate[j] * mm(pick, dxv[...])
    small[2:3, :] = jnp.sum(grad * normed, axis=0, keepdims=True)
    small[3:4, :] = jnp.sum(grad, axis=0, keepdims=True)
    d_resid = gv[...].astype(F32) + norm_back(grad, normed, inverse, g2[...])
    d_res[...] = d_resid
    branch = d_resid.astype(BF)
    loads[3].wait()
    for t in range(n_h):
        owner = lax.rem(h + t, n_h)
        block = mm_nt(wo[owner], branch).astype(BF)
        if t == 0:
            d_att[h] = block
        else:
            d_att_v[owner] = block
            copy = remote(
                d_att_v.at[owner], d_att.at[h], at_s.at[t], at_r.at[t], {"hidden": owner}
            )
            copy.start()
            sends.append(copy)
    loads[4].wait()
    for t in range(n_h):
        owner = lax.rem(h + t, n_h)
        wo[owner] = mm(att_t[owner], branch).astype(BF)
        if t > 0:
            copy = remote(
                wo.at[owner], wo_box.at[t - 1], wo_s.at[t], wo_r.at[t], {"hidden": owner}
            )
            copy.start()
            sends.append(copy)

    for load in mine:
        load.wait()
    lines_w = dw_mine.shape[2]
    bands = lines_w // 96
    for step in range(1, far):
        for which in range(2):
            there = dw_beside.at[which, step]
            remote(
                there, there, dc_s.at[which, step], dc_r.at[which, step], {"hidden": mate}
            ).wait_recv()

            def add(n, _, which=which, step=step):
                band = aligned(n * 96, 96)
                both = dw_mine[which, step, band, :].astype(F32)
                both = both + dw_beside[which, step, band, :].astype(F32)
                dw_mine[which, step, band, :] = both.astype(BF)
                return 0

            lax.fori_loop(0, bands, add, 0)
            copy = remote(
                dw_mine.at[which, step],
                dw_across.at[which, step - 1],
                da_s.at[which, step],
                da_r.at[which, step],
                {"hidden": lax.rem(pair + step, far) * 2 + core},
            )
            copy.start()
            sends.append(copy)

    for load in loads[5:]:
        load.wait()
    dq_acc[...] = jnp.zeros_like(dq_acc)

    def turn(i, _):
        cols = aligned(i * BLOCK, BLOCK)
        for n in range(heads):
            lo = width + n * HEAD_DIM
            keys[n, cols, :] = qkv[lo : lo + HEAD_DIM, cols].astype(F32).T.astype(BF)
            lo = 2 * width + n * HEAD_DIM
            values[n, cols, :] = qkv[lo : lo + HEAD_DIM, cols].astype(F32).T.astype(BF)
        return 0

    lax.fori_loop(0, blocks, turn, 0)
    for t in range(1, n_h):
        there = d_att.at[lax.rem(h + n_h - t, n_h)]
        remote(there, there, at_s.at[t], at_r.at[t], {"hidden": mate}).wait_recv()

    def weigh(i, _):
        cols = aligned(lax.rem(i, per_device) * BLOCK, BLOCK)
        for n in range(heads):
            here = slice(n * HEAD_DIM, (n + 1) * HEAD_DIM)
            product = att_v[i // per_device, here, cols].astype(F32)
            product = product * d_att[i // per_device, here, cols].astype(F32)
            dots[n : n + 1, aligned(i * BLOCK, BLOCK)] = jnp.sum(product, axis=0, keepdims=True)
        return 0

    lax.fori_loop(0, blocks, weigh, 0)
    accs = (dq_acc, dk_acc, dv_acc)
    attend_back(
        heads, ends, blocks, per_device, qkv, d_att, lse, dots, keys, values, accs, d_qkv
    )
    w_acc[...] = jnp.zeros_like(w_acc)

    def finish(i, _):
        cols = aligned(i * BLOCK, BLOCK)
        d_qkv[0:width, cols] = (dq_acc[:, cols] * SCALE).astype(BF)
        block = d_qkv[:, cols]
        grad = mm_tn(block, w_t[...])
        inner = aligned(lax.rem(i, per_device) * BLOCK, BLOCK)
        normed, _unused = norm_parts(tv[i // per_device, inner, :].astype(F32))
        tv[i // per_device, inner, :] = grad.astype(BF)
        small[0:1, :] += jnp.sum(grad * normed, axis=0, keepdims=True)
        small[1:2, :] += jnp.sum(grad, axis=0, keepdims=True)
        hidden = (normed * g1[...] + s1[...]).astype(BF)
        w_acc[...] += mm(block, hidden)
        return 0

    lax.fori_loop(0, blocks, finish, 0)
    save_dh = pltpu.make_async_copy(tv, d_hidden, save_sem)
    save_dh.start()
    w_all[0 : 3 * width, :] = w_acc[...].astype(BF)
    total = wo[h].astype(F32)
    for t in range(1, n_h):
        there = wo_box.at[t - 1]
        remote(there, there, wo_s.at[t], wo_r.at[t], {"hidden": mate}).wait_recv()
        total = total + wo_box[t - 1].astype(F32)
    w_all[3 * width :, :] = total.astype(BF)
    for which in range(2):
        there = dw_beside.at[which, 0]
        remote(there, there, dc_s.at[which, 0], dc_r.at[which, 0], {"hidden": mate}).wait_recv()
        for step in range(1, far):
            there = dw_across.at[which, step - 1]
            remote(
                there, there, da_s.at[which, step], da_r.at[which, step], {"hidden": mate}
            ).wait_recv()

        def add_all(n, _, which=which):
            band = aligned(n * 96, 96)
            both = dw_mine[which, 0, band, :].astype(F32)
            both = both + dw_beside[which, 0, band, :].astype(F32)
            for step in range(1, far):
                both = both + dw_across[which, step - 1, band, :].astype(F32)
            dw_own[which, band, :] = both
            return 0

        lax.fori_loop(0, bands, add_all, 0)
    for step in range(1, n_e):
        there = y_back.at[lax.rem(e + n_e - step, n_e)]
        remote(there, there, y_s.at[step], y_r.at[step], {"expert": e}).wait_recv()
    own_y.wait()
    save_dh.wait()
    for copy in sends:
        copy.wait_send()


def run_back(
    docs,
    ids,
    slot,
    pos,
    gates,
    count,
    g1,
    s1,
    g2,
    s2,
    w_router,
    lse,
    dg_rows,
    dx_back,
    y_out,
    up_part,
    down_part,
    out_grad,
    residual,
    all_tokens,
    qkv,
    att,
    att_t,
    w_out,
    w_t,
    cid,
):
    n_e, n_h = lax.axis_size("expert"), lax.axis_size("hidden")
    experts, capacity, model = y_out.shape
    padded = dg_rows.shape[2]
    rows = out_grad.shape[0]
    width = w_t.shape[0] // 3
    heads = width // HEAD_DIM
    group, far = rows * n_h, n_h // 2
    shard = up_part.shape[1:]
    tall = -(-(5 + experts) // 8) * 8

    def pairs(*shape):
        return [DMA(shape), DMA(shape)]

    return pl.pallas_call(
        partial(back_body, n_e, n_h, experts, capacity, padded, heads),
        name="back",
        out_shape=[
            shape_of(y_out.shape, BF),
            shape_of((n_h, rows, model), BF),
            shape_of((rows, model), F32),
            shape_of((4 * width, model), BF),
            shape_of((tall, model), F32),
            shape_of((2, *shard), F32),
        ],
        in_specs=[SMEM] + [VMEM] * 12 + [ANY] * 12,
        out_specs=[ANY] * 2 + [VMEM] * 4,
        scratch_shapes=[
            pltpu.VMEM((experts * capacity, model), BF),
            pltpu.VMEM((rows, model), BF),
            pltpu.VMEM((rows, model), F32),
            pltpu.VMEM((n_h, rows, model), BF),
            pltpu.VMEM((3 * width, group), BF),
            pltpu.VMEM((n_h, width, rows), BF),
            pltpu.VMEM((n_h, width, rows), BF),
            pltpu.VMEM((n_h, width, model), BF),
            pltpu.VMEM((3 * width, model), BF),
            pltpu.VMEM((n_h, width, rows), BF),
            pltpu.VMEM((n_h, width, rows), BF),
            pltpu.VMEM((n_h - 1, width, model), BF),
            pltpu.VMEM((heads, group, HEAD_DIM), BF),
            pltpu.VMEM((heads, group, HEAD_DIM), BF),
            pltpu.VMEM((8, group), F32),
            pltpu.VMEM((width, group), F32),
            pltpu.VMEM((width, BLOCK), F32),
            pltpu.VMEM((width, BLOCK), F32),
            pltpu.VMEM((3 * width, group), BF),
            pltpu.VMEM((3 * width, model), F32),
            pltpu.VMEM((2, far, *shard), BF),
            pltpu.VMEM((2, far, *shard), BF),
            pltpu.VMEM((2, far - 1, *shard), BF),
            DMA((9,)),
            DMA,
            DMA((2, far)),
            DMA,
            *pairs(n_e),
            *pairs(n_h),
            *pairs(n_h),
            *pairs(2, far),
            *pairs(2, far),
        ],
        compiler_params=pltpu.CompilerParams(
            collective_id=cid, has_side_effects=True, vmem_limit_bytes=60 << 20
        ),
    )(
        docs,
        ids,
        slot,
        pos,
        gates,
        count,
        g1,
        s1,
        g2,
        s2,
        w_router,
        lse,
        dg_rows,
        dx_back.reshape(experts * capacity, model),
        y_out,
        up_part,
        down_part,
        out_grad,
        residual,
        all_tokens,
        qkv,
        att,
        att_t,
        w_out.reshape(n_h, width, model),
        w_t,
    )


def shards(
    tokens,
    doc_lengths,
    expert_ids,
    gain_one,
    shift_one,
    w_query,
    w_key,
    w_value,
    w_out,
    gain_two,
    shift_two,
    w_router,
    w_up,
    w_down,
    out_grad,
):
    rows, model = tokens.shape
    n_expert, n_hidden = lax.axis_size("expert"), lax.axis_size("hidden")
    experts = n_expert * w_up.shape[0]
    capacity = max(2, rows * 2 * 5 // (4 * experts))
    capacity = -(-capacity // 16) * 16
    total = experts * capacity
    heads = HEADS // n_hidden
    width = heads * HEAD_DIM
    g1, s1 = gain_one.reshape(1, model), shift_one.reshape(1, model)
    g2, s2 = gain_two.reshape(1, model), shift_two.reshape(1, model)

    (
        all_tokens,
        qkv,
        att,
        att_t,
        w_t,
        g_in,
        x_slots,
        ups,
        downs,
        pos,
        slot,
        count,
        lse,
        residual,
        gates,
        gate_rows,
    ) = run_front(
        doc_lengths,
        expert_ids,
        g1,
        s1,
        g2,
        s2,
        w_router,
        tokens,
        out_grad,
        (w_query, w_key, w_value, w_out),
        w_up,
        w_down,
        capacity,
        heads,
        1,
    )
    dx_back, dg_back, y_out, up_part, down_part = run_experts(
        x_slots, gate_rows, g_in, ups, downs, 2
    )
    y_back, d_hidden, d_res, w_all, small, dw_own = run_back(
        doc_lengths,
        expert_ids,
        slot,
        pos,
        gates,
        count,
        g1,
        s1,
        g2,
        s2,
        w_router,
        lse,
        dg_back,
        dx_back,
        y_out,
        up_part,
        down_part,
        out_grad,
        residual,
        all_tokens,
        qkv,
        att,
        att_t,
        w_out,
        w_t,
        3,
    )
    input_grad, output, full, small = run_tail(
        d_hidden,
        w_all.reshape(n_expert, 4 * width // n_expert, model),
        small,
        tokens,
        g1,
        d_res,
        residual,
        gates,
        pos,
        y_back.reshape(total, model),
        4,
    )
    *w_grads, up_grad, down_grad = turn_weights(
        full.reshape(n_hidden, 4 * width, model), dw_own, width, experts // 2
    )
    load = small[4, :experts] * experts / (rows * n_expert * n_hidden * 2)
    return (
        output,
        input_grad,
        small[0],
        small[1],
        *w_grads,
        small[2],
        small[3],
        small[5 : 5 + experts].T,
        up_grad[None],
        down_grad[None],
        load,
    )


def solution(mesh):
    in_specs = (
        P(("expert", "hidden"), None),
        P("expert", None),
        P(("expert", "hidden"), None),
        P(),
        P(),
        P(),
        P(),
        P(),
        P(),
        P(),
        P(),
        P(),
        P("expert", None, "hidden"),
        P("expert", "hidden", None),
        P(("expert", "hidden"), None),
    )
    out_specs = (
        P(("expert", "hidden"), None),
        P(("expert", "hidden"), None),
        P(),
        P(),
        P(),
        P(),
        P(),
        P(),
        P(),
        P(),
        P(),
        P("expert", None, "hidden"),
        P("expert", "hidden", None),
        P(),
    )
    return jax.shard_map(shards, mesh=mesh, in_specs=in_specs, out_specs=out_specs, check_vma=False)
```

```python
from functools import partial

import jax
import jax.numpy as jnp
from jax import lax
from jax.experimental import pallas as pl
from jax.experimental.pallas import tpu as pltpu
from jax.sharding import PartitionSpec as P

HEAD_DIM = 64
HEADS = 12
EPSILON = 1e-05
SCALE = 0.125
MASKED = -1e30
BLOCK = 256
LONGEST = 1024
REACH = LONGEST // BLOCK + 1
LANES = 128
BF = jnp.bfloat16
F32 = jnp.float32
I32 = jnp.int32
MESH = pl.DeviceIdType.MESH
ANY = pl.BlockSpec(memory_space=pl.ANY)
SMEM = pl.BlockSpec(memory_space=pltpu.SMEM)
VMEM = pl.BlockSpec(memory_space=pltpu.VMEM)
DMA = pltpu.SemaphoreType.DMA
GELU_A = 0.7978845608028654
GELU_B = 0.044715


def mm(left, right):
    return jnp.dot(left, right, preferred_element_type=F32)


def mm_nt(left, right):
    return lax.dot_general(left, right, (((1,), (1,)), ((), ())), preferred_element_type=F32)


def mm_tn(left, right):
    return lax.dot_general(left, right, (((0,), (0,)), ((), ())), preferred_element_type=F32)


def iota(shape, axis):
    return lax.broadcasted_iota(I32, shape, axis)


def norm_parts(values):
    centred = values - jnp.mean(values, axis=-1, keepdims=True)
    inverse = lax.rsqrt(jnp.mean(centred * centred, axis=-1, keepdims=True) + EPSILON)
    return centred * inverse, inverse


def norm_back(grad_out, normed, inverse, gain):
    grad_normed = grad_out * gain
    first = jnp.mean(grad_normed, axis=-1, keepdims=True)
    second = jnp.mean(grad_normed * normed, axis=-1, keepdims=True)
    return inverse * (grad_normed - first - normed * second)


def split_two(value):
    high = value.astype(BF)
    return high, (value - high.astype(F32)).astype(BF)


def shape_of(shape, dtype):
    return jax.ShapeDtypeStruct(shape, dtype)


def greet(peers):
    barrier = pltpu.get_barrier_semaphore()
    for peer in peers:
        pl.semaphore_signal(barrier, inc=1, device_id=peer, device_id_type=MESH)
    pl.semaphore_wait(barrier, len(peers))


def remote(src, dst, send, recv, peer):
    return pltpu.make_async_remote_copy(
        src_ref=src, dst_ref=dst, send_sem=send, recv_sem=recv, device_id=peer, device_id_type=MESH
    )


def doc_bounds(docs):
    ends, at = [], 0
    for n in range(docs.shape[1] - 1):
        at = at + docs[0, n]
        ends.append(at)
    return ends


def start_of(place, ends):
    begin = jnp.zeros_like(place)
    for end in ends:
        begin = jnp.where(place >= end, end, begin)
    return begin


def lying(ref):
    return ref[...].reshape(1, ref.shape[0])


def aligned(at, size):
    return pl.ds(pl.multiple_of(at, size), size)


def find_slots(experts, capacity, ids, ids_t, pos, slot, count):
    rows = ids_t.shape[1]
    row = [ids_t[j : j + 1, :] for j in range(2)]
    tall = jnp.concatenate([r.astype(F32) for r in row] + [jnp.zeros((6, rows), F32)], axis=0)
    ids[...] = tall.T[:, 0:2].astype(I32)
    col = [ids[:, j : j + 1] for j in range(2)]
    lane = iota((rows, LANES), 1)
    hot = [(lane == c).astype(BF) for c in col]
    either = hot[0] + hot[1]
    below = (iota((rows, rows), 0) > iota((rows, rows), 1)).astype(BF)
    before = mm(below, either)
    wide = max(experts, 16)
    deep = iota((wide, rows), 0)
    hot_t = [(deep == r).astype(BF) for r in row]
    above = (iota((rows, rows), 0) < iota((rows, rows), 1)).astype(BF)
    before_t = mm(hot_t[0] + hot_t[1], above)
    count[...] = jnp.sum(either.astype(F32), axis=0, keepdims=True)
    flat_t = []
    for j in range(2):
        at = jnp.sum(hot[j].astype(F32) * before, axis=1, keepdims=True).astype(I32)
        pos[:, j : j + 1] = col[j] * capacity + at
        slot[:, j : j + 1] = at
        at_t = jnp.sum(hot_t[j].astype(F32) * before_t, axis=0, keepdims=True).astype(I32)
        flat_t.append(row[j] * capacity + at_t)
    return flat_t


def fill_slots(flat_t, source, out):
    total, rows = out.shape[0], source.shape[0]
    half = total // 2
    for n in range(2):
        place = iota((half, rows), 0) + n * half
        pick = ((place == flat_t[0]) | (place == flat_t[1])).astype(BF)
        out[pl.ds(n * half, half), :] = mm(pick, source).astype(BF)


def attend_block(heads, ends, i, qkv, keys, scores, lse):
    width = heads * HEAD_DIM
    base = i * BLOCK
    rows = aligned(base, BLOCK)
    q_pos = base + iota((1, BLOCK), 1)
    begin = start_of(q_pos, ends)
    first = (i - (REACH - 1)) * (i // (REACH - 1))
    queries = [
        qkv[n * HEAD_DIM : (n + 1) * HEAD_DIM, rows] * jnp.asarray(SCALE, BF) for n in range(heads)
    ]
    tops = [jnp.full((1, BLOCK), MASKED, F32)] * heads
    for k in range(REACH):
        part = aligned((first + k) * BLOCK, BLOCK)
        k_pos = (first + k) * BLOCK + iota((BLOCK, BLOCK), 0)
        allowed = (k_pos <= q_pos) & (k_pos >= begin)
        for n in range(heads):
            score = jnp.where(allowed, mm(keys[n, part, :], queries[n]), MASKED)
            scores[n, k] = score
            tops[n] = jnp.maximum(tops[n], jnp.max(score, axis=0, keepdims=True))
    result = []
    for n in range(heads):
        total = jnp.zeros((1, BLOCK), F32)
        acc = jnp.zeros((HEAD_DIM, BLOCK), F32)
        lo = 2 * width + n * HEAD_DIM
        for k in range(REACH):
            weight = jnp.exp(scores[n, k] - tops[n])
            total = total + jnp.sum(weight, axis=0, keepdims=True)
            value = qkv[lo : lo + HEAD_DIM, aligned((first + k) * BLOCK, BLOCK)]
            acc = acc + mm(value, weight.astype(BF))
        lse[n : n + 1, rows] = tops[n] + jnp.log(total)
        result.append((acc / total).astype(BF))
    return result


def front_body(
    n_e,
    n_h,
    experts,
    capacity,
    padded,
    heads,
    chunks,
    docs,
    ids_t,
    g1,
    s1,
    g2,
    s2,
    w_router,
    tokens,
    out_grad,
    w_query,
    w_key,
    w_value,
    w_out,
    w_up,
    all_tokens,
    qkv_out,
    att_out,
    att_t_out,
    w_t_out,
    g_in,
    x_slots,
    ups,
    ids,
    pos,
    slot,
    count,
    lse,
    residual,
    gates,
    gate_rows,
    tv,
    gv,
    wv,
    wo,
    w_t,
    qkv,
    keys,
    scores,
    att_v,
    att_in,
    g_slots,
    xs_v,
    own_sem,
    w_sem,
    save_sem,
    ty_s,
    ty_r,
    tc_s,
    tc_r,
    tf_s,
    tf_r,
    gs_s,
    gs_r,
    at_s,
    at_r,
    wy_s,
    wy_r,
    wc_s,
    wc_r,
    wf_s,
    wf_r,
):
    e, h = lax.axis_index("expert"), lax.axis_index("hidden")
    far = n_h // 2
    pair, core = h // 2, lax.rem(h, 2)
    mate = pair * 2 + 1 - core
    rows, model = tokens.shape
    width = heads * HEAD_DIM
    per_device = rows // BLOCK
    ends = doc_bounds(docs)

    def across(t):
        return lax.rem(pair + t, far) * 2 + core

    def origin(t):
        return lax.rem(pair + far - t, far) * 2 + core

    own_tokens = pltpu.make_async_copy(tokens, tv.at[h], own_sem.at[0])
    own_grad = pltpu.make_async_copy(out_grad, gv, own_sem.at[1])
    own_grad.start()
    own_tokens.start()
    w_loads = [
        pltpu.make_async_copy(w, wv.at[n], w_sem.at[n])
        for n, w in enumerate((w_query, w_key, w_value))
    ]
    w_loads.append(pltpu.make_async_copy(w_out, wo, w_sem.at[3]))
    for load in w_loads:
        load.start()
    greet(
        [{"hidden": lax.rem(h + step, n_h)} for step in range(1, n_h)]
        + [{"expert": lax.rem(e + step, n_e)} for step in range(1, n_e)]
    )

    piece = rows // chunks
    sends = []
    for k in range(chunks):
        part = pl.ds(k * piece, piece)
        for t in range(1, far):
            copy = remote(
                tokens.at[part],
                tv.at[h, part],
                ty_s.at[t, k],
                ty_r.at[t, k],
                {"hidden": across(t)},
            )
            copy.start()
            sends.append(copy)
    beside = remote(tokens, tv.at[h], tc_s, tc_r, {"hidden": mate})
    beside.start()
    sends.append(beside)

    flat_t = find_slots(experts, capacity, ids, ids_t, pos, slot, count)
    own_grad.wait()
    fill_slots(flat_t, gv[...], g_slots)
    for step in range(1, n_e):
        peer = lax.rem(e + step, n_e)
        copy = remote(
            g_slots.at[aligned(peer * capacity, capacity)],
            g_in.at[e],
            gs_s.at[step],
            gs_r.at[step],
            {"expert": peer},
        )
        copy.start()
        sends.append(copy)
    own_slots = pltpu.make_async_copy(
        g_slots.at[aligned(e * capacity, capacity)], g_in.at[e], own_sem.at[1]
    )
    own_slots.start()

    def pass_on(t, k):
        part = pl.ds(k * piece, piece)
        place = tv.at[origin(t), part]
        remote(place, place, ty_s.at[t, k], ty_r.at[t, k], {"hidden": across(t)}).wait_recv()
        copy = remote(place, place, tf_s.at[t, k], tf_r.at[t, k], {"hidden": mate})
        copy.start()
        sends.append(copy)

    todo = [(t, k) for k in range(chunks) for t in range(1, far)]
    third = -(-len(todo) // 4)

    def pass_some():
        for _ in range(min(third, len(todo))):
            pass_on(*todo.pop(0))

    pick = (iota((width, model), 1) == iota((width, model), 0) + h * width).astype(BF)
    for n in range(3):
        w_loads[n].wait()
        w_t[n * width : (n + 1) * width, :] = mm_nt(pick, wv[n]).astype(BF)
        if n == 1:
            pass_some()
    save_w = pltpu.make_async_copy(w_t, w_t_out, save_sem.at[0])
    save_w.start()

    def project(source):
        def one(b, _):
            normed, _unused = norm_parts(tv[source, aligned(b * BLOCK, BLOCK), :].astype(F32))
            hidden = (normed * lying(g1) + lying(s1)).astype(BF)
            block = mm_nt(w_t[...], hidden)
            cols = aligned(source * rows + b * BLOCK, BLOCK)
            qkv[:, cols] = block.astype(BF)
            for n in range(heads):
                lo = width + n * HEAD_DIM
                keys[n, cols, :] = block[lo : lo + HEAD_DIM].T.astype(BF)
            return 0

        lax.fori_loop(0, per_device, one, 0)

    pass_some()
    own_tokens.wait()
    project(h)
    pass_some()
    remote(tokens, tv.at[mate], tc_s, tc_r, {"hidden": mate}).wait_recv()
    project(mate)
    while todo:
        pass_some()

    deep = w_up.shape[1] // 2

    def up_part(k):
        return pl.ds(k * deep, deep)

    def up_across(k):
        for t in range(1, far):
            copy = remote(
                w_up.at[0, up_part(k)],
                ups.at[h, up_part(k)],
                wy_s.at[t, k],
                wy_r.at[t, k],
                {"hidden": across(t)},
            )
            copy.start()
            sends.append(copy)

    def up_onward(k):
        for t in range(1, far):
            place = ups.at[origin(t), up_part(k)]
            remote(place, place, wy_s.at[t, k], wy_r.at[t, k], {"hidden": mate}).wait_recv()
            copy = remote(place, place, wf_s.at[t, k], wf_r.at[t, k], {"hidden": mate})
            copy.start()
            sends.append(copy)

    own_up = pltpu.make_async_copy(w_up.at[0], ups.at[h], own_sem.at[2])
    own_up.start()
    up_beside = remote(w_up.at[0], ups.at[h], wc_s, wc_r, {"hidden": mate})
    up_beside.start()
    sends.append(up_beside)
    up_across(0)
    for t in range(1, far):
        project(origin(t))
    for t in range(1, far):
        there = lax.rem(pair + far - t, far) * 2 + 1 - core
        for k in range(chunks):
            place = tv.at[there, pl.ds(k * piece, piece)]
            remote(place, place, tf_s.at[t, k], tf_r.at[t, k], {"hidden": mate}).wait_recv()
        project(there)
    save_tokens = pltpu.make_async_copy(tv, all_tokens, save_sem.at[1])
    save_qkv = pltpu.make_async_copy(qkv, qkv_out, save_sem.at[2])
    save_tokens.start()
    save_qkv.start()

    lse[...] = jnp.zeros_like(lse)
    owners = []
    for t in range(1, far):
        owners.append(lax.rem(pair + t, far) * 2 + core)
        owners.append(lax.rem(pair + t, far) * 2 + 1 - core)
    owners += [mate, h]
    for at, owner in enumerate(owners):

        def one(b, _, owner=owner):
            done = attend_block(heads, ends, owner * per_device + b, qkv, keys, scores, lse)
            for n in range(heads):
                lo = n * HEAD_DIM
                att_v[owner, lo : lo + HEAD_DIM, aligned(b * BLOCK, BLOCK)] = done[n]
            return 0

        lax.fori_loop(0, per_device, one, 0)
        if at < len(owners) - 1:
            copy = remote(
                att_v.at[owner], att_in.at[h], at_s.at[at], at_r.at[at], {"hidden": owner}
            )
            copy.start()
            sends.append(copy)
    up_onward(0)
    att_in[h] = att_v[h]
    save_att = pltpu.make_async_copy(att_v, att_out, save_sem.at[3])
    save_att.start()
    at = 0
    for t in range(1, far):
        for other in (core, 1 - core):
            place = att_in.at[lax.rem(pair + far - t, far) * 2 + other]
            remote(place, place, at_s.at[at], at_r.at[at], {"hidden": mate}).wait_recv()
            at += 1
    place = att_in.at[mate]
    remote(place, place, at_s.at[at], at_r.at[at], {"hidden": mate}).wait_recv()
    save_att_t = pltpu.make_async_copy(att_in, att_t_out, save_sem.at[4])
    save_att_t.start()

    up_across(1)

    w_loads[3].wait()
    res = tv[h].astype(F32) + mm_tn(att_in[...].reshape(model, rows), wo[...])
    residual[...] = res
    normed, _unused = norm_parts(res)
    hidden = (normed * lying(g2) + lying(s2)).astype(BF)
    fill_slots(flat_t, hidden, xs_v)
    save_x = [
        pltpu.make_async_copy(
            xs_v.at[pl.ds(n * capacity, capacity)], x_slots.at[n], save_sem.at[5 + n]
        )
        for n in range(experts)
    ]
    for save in save_x:
        save.start()
    logits = mm_nt(hidden, w_router[...])
    lane = iota((rows, experts), 1)
    chosen = [
        jnp.sum(jnp.where(lane == ids[:, j : j + 1], logits, 0.0), axis=1, keepdims=True)
        for j in range(2)
    ]
    top = jnp.maximum(chosen[0], chosen[1])
    raised = [jnp.exp(c - top) for c in chosen]
    both = raised[0] + raised[1]
    gate = [r / both for r in raised]
    for j in range(2):
        gates[:, j : j + 1] = gate[j]
    column = iota((rows, padded), 1)
    for n in range(experts):
        mix = jnp.zeros((rows, padded), F32)
        for j in range(2):
            here = jnp.where(ids[:, j : j + 1] == n, slot[:, j : j + 1], -1) == column
            mix = jnp.where(here, gate[j], mix)
        line = jnp.sum(mix, axis=0, keepdims=True)
        gate_rows[n] = jnp.broadcast_to(line, (8, padded))

    up_onward(1)
    place = ups.at[mate]
    remote(place, place, wc_s, wc_r, {"hidden": mate}).wait_recv()
    for k in range(2):
        for t in range(1, far):
            there = lax.rem(pair + far - t, far) * 2 + 1 - core
            place = ups.at[there, up_part(k)]
            remote(place, place, wf_s.at[t, k], wf_r.at[t, k], {"hidden": mate}).wait_recv()
    own_up.wait()
    for step in range(1, n_e):
        source = lax.rem(e + n_e - step, n_e)
        place = g_in.at[source]
        remote(place, place, gs_s.at[step], gs_r.at[step], {"expert": e}).wait_recv()
    own_slots.wait()
    for copy in sends:
        copy.wait_send()
    for save in [save_w, save_tokens, save_qkv, save_att, save_att_t, *save_x]:
        save.wait()


def run_front(
    docs, ids_t, g1, s1, g2, s2, w_router, tokens, out_grad, ws, w_up, capacity, heads, cid
):
    n_e, n_h = lax.axis_size("expert"), lax.axis_size("hidden")
    experts = n_e * w_up.shape[0]
    rows, model = tokens.shape
    padded = -(-capacity // LANES) * LANES
    width, group, total = heads * HEAD_DIM, rows * n_h, experts * capacity
    far, chunks = n_h // 2, 8

    def pairs(*shape):
        return [DMA(shape), DMA(shape)]

    return pl.pallas_call(
        partial(front_body, n_e, n_h, experts, capacity, padded, heads, chunks),
        name="front",
        out_shape=[
            shape_of((n_h, rows, model), BF),
            shape_of((3 * width, group), BF),
            shape_of((n_h, width, rows), BF),
            shape_of((n_h, width, rows), BF),
            shape_of((3 * width, model), BF),
            shape_of((experts, capacity, model), BF),
            shape_of((experts, capacity, model), BF),
            shape_of((n_h, *w_up.shape[1:]), BF),
            shape_of((rows, 2), I32),
            shape_of((rows, 2), I32),
            shape_of((rows, 2), I32),
            shape_of((1, LANES), F32),
            shape_of((8, group), F32),
            shape_of((rows, model), F32),
            shape_of((rows, 2), F32),
            shape_of((experts, 8, padded), F32),
        ],
        in_specs=[SMEM] + [VMEM] * 6 + [ANY] * 7,
        out_specs=[ANY] * 8 + [VMEM] * 8,
        scratch_shapes=[
            pltpu.VMEM((n_h, rows, model), BF),
            pltpu.VMEM((rows, model), BF),
            pltpu.VMEM((3, model, model), BF),
            pltpu.VMEM((model, model), BF),
            pltpu.VMEM((3 * width, model), BF),
            pltpu.VMEM((3 * width, group), BF),
            pltpu.VMEM((heads, group, HEAD_DIM), BF),
            pltpu.VMEM((heads, REACH, BLOCK, BLOCK), F32),
            pltpu.VMEM((n_h, width, rows), BF),
            pltpu.VMEM((n_h, width, rows), BF),
            pltpu.VMEM((total, model), BF),
            pltpu.VMEM((total, model), BF),
            DMA((4,)),
            DMA((4,)),
            DMA((5 + experts,)),
            *pairs(far, chunks),
            DMA,
            DMA,
            *pairs(far, chunks),
            *pairs(n_e),
            *pairs(n_h),
            *pairs(far, 2),
            DMA,
            DMA,
            *pairs(far, 2),
        ],
        compiler_params=pltpu.CompilerParams(
            collective_id=cid, has_side_effects=True, vmem_limit_bytes=58 << 20
        ),
    )(docs, ids_t, g1, s1, g2, s2, w_router, tokens, out_grad, *ws, w_up)


def moe_body(
    size,
    capacity,
    padded,
    per,
    x_slots,
    gate_rows,
    g_in,
    ups,
    w_down,
    dx_back,
    dg_back,
    y_out,
    dw_sum,
    xv,
    gv,
    gates_v,
    up_v,
    down_v,
    act,
    dz,
    xg,
    dy,
    xg_t,
    dy_t,
    dxv,
    yv,
    dgv,
    y_acc,
    dx_acc,
    dw_box,
    load_sem,
    save_sem,
    wy_s,
    wy_r,
    wc_s,
    wc_r,
    wf_s,
    wf_r,
    dc_s,
    dc_r,
    g_sem,
    own_sem,
    xs_sem,
    xr_sem,
    gs_sem,
    gr_sem,
    ds_sem,
    dr_sem,
    ts_sem,
    tr_sem,
    out_sem,
):
    me, h = lax.axis_index("expert"), lax.axis_index("hidden")
    shards_n = ups.shape[0]
    far = shards_n // 2
    pair, core = h // 2, lax.rem(h, 2)
    mate = pair * 2 + 1 - core
    deep = w_down.shape[1] // 2
    tall = per * capacity
    steps = size // per

    def to_peer(p):
        return lax.rem(me + 3 * p, size)

    def from_peer(p):
        return lax.rem(me + 3 * (size - p), size)

    def rows_of(p):
        return pl.ds(pl.multiple_of(p * capacity, capacity), capacity)

    def send_x(p):
        peer = to_peer(p)
        return remote(
            x_slots.at[peer], xv.at[rows_of(p)], xs_sem.at[p], xr_sem.at[p], {"expert": peer}
        )

    def send_gate(p):
        peer = to_peer(p)
        return remote(
            gate_rows.at[peer], gates_v.at[p], gs_sem.at[p], gr_sem.at[p], {"expert": peer}
        )

    def send_dx(p):
        peer = from_peer(p)
        return remote(
            dxv.at[rows_of(p)], dx_back.at[me], ds_sem.at[p], dr_sem.at[p], {"expert": peer}
        )

    def send_dg(p):
        peer = from_peer(p)
        return remote(dgv.at[p], dg_back.at[me], ts_sem.at[p], tr_sem.at[p], {"expert": peer})

    def load_g(p):
        return pltpu.make_async_copy(g_in.at[from_peer(p)], gv.at[rows_of(p)], g_sem.at[p])

    def save_y(p):
        return pltpu.make_async_copy(yv.at[rows_of(p)], y_out.at[from_peer(p)], out_sem.at[p])

    own_x = pltpu.make_async_copy(x_slots.at[me], xv.at[rows_of(0)], own_sem.at[0])
    own_gate = pltpu.make_async_copy(gate_rows.at[me], gates_v.at[0], own_sem.at[1])
    own_dx = pltpu.make_async_copy(dxv.at[rows_of(0)], dx_back.at[me], own_sem.at[2])
    own_dg = pltpu.make_async_copy(dgv.at[0], dg_back.at[me], own_sem.at[3])
    load_up = pltpu.make_async_copy(ups, up_v, load_sem.at[0])
    load_down = pltpu.make_async_copy(w_down.at[0], down_v.at[h], load_sem.at[1])

    def half(k):
        return aligned(k * deep, deep)

    def down_across(t, k):
        there = {"hidden": lax.rem(pair + t, far) * 2 + core}
        return remote(
            w_down.at[0, half(k)], down_v.at[h, half(k)], wy_s.at[t, k], wy_r.at[t, k], there
        )

    def down_onward(t, k):
        place = down_v.at[lax.rem(pair + far - t, far) * 2 + core, half(k)]
        return remote(place, place, wf_s.at[t, k], wf_r.at[t, k], {"hidden": mate})

    down_beside = remote(w_down.at[0], down_v.at[h], wc_s, wc_r, {"hidden": mate})
    own_x.start()
    own_gate.start()
    for p in range(size):
        load_g(p).start()
    load_up.start()
    load_down.start()
    greet(
        [{"expert": lax.rem(me + step, size)} for step in range(1, size)]
        + [{"hidden": lax.rem(h + step, shards_n)} for step in range(1, shards_n)]
    )
    for p in range(1, size):
        send_x(p).start()
        send_gate(p).start()
    for k in range(2):
        for t in range(1, far):
            down_across(t, k).start()
    down_beside.start()
    own_x.wait()
    own_gate.wait()
    load_up.wait()
    load_down.wait()

    def step_body(step, _):
        base = step * per
        for s in range(per):

            @pl.when(base + s > 0)
            def _arrive(s=s):
                send_x(base + s).wait_recv()
                send_gate(base + s).wait_recv()

            load_g(base + s).wait()
        rows = pl.ds(pl.multiple_of(step * tall, tall), tall)
        x, g = xv[rows, :], gv[rows, :]
        y_acc[...] = jnp.zeros_like(y_acc)
        dx_acc[...] = jnp.zeros_like(dx_acc)

        def shard_body(n, _):
            t = n // 2
            beside = lax.rem(n, 2)
            c = lax.rem(pair + far - t, far) * 2 + lax.rem(core + beside, 2)

            @pl.when((step == 0) & (n == 1))
            def _beside():
                down_beside.wait_recv()

            @pl.when((step == 0) & (n >= 2) & (beside == 0))
            def _across():
                for k in range(2):
                    down_across(t, k).wait_recv()
                    down_onward(t, k).start()

            @pl.when((step == 0) & (n >= 2) & (beside == 1))
            def _onward():
                for k in range(2):
                    down_onward(t, k).wait_recv()

            z = mm(x, up_v[c])
            du = mm_nt(g, down_v[c])
            square = z * z
            curve = jnp.tanh(z * (GELU_A + GELU_A * GELU_B * square))
            plus = 0.5 + 0.5 * curve
            hidden = (z * plus).astype(BF)
            rise = GELU_A + 3.0 * GELU_A * GELU_B * square
            slope = plus + 0.5 * z * (1.0 - curve * curve) * rise
            back = (slope * du).astype(BF)
            act[c, rows, :] = hidden
            dz[c, rows, :] = back
            y_acc[...] += mm(hidden, down_v[c])
            dx_acc[...] += mm_nt(back, up_v[c])
            return 0

        lax.fori_loop(0, shards_n, shard_body, 0)
        dxv[rows, :] = dx_acc[...].astype(BF)
        y_low = y_acc[...].astype(BF)
        yv[rows, :] = y_low
        dots = jnp.sum(y_low.astype(F32) * g.astype(F32), axis=1, keepdims=True)
        for s in range(per):
            p = base + s
            part = slice(s * capacity, (s + 1) * capacity)
            tall_dots = jnp.broadcast_to(dots[part], (capacity, LANES))
            if padded > capacity:
                blank = jnp.zeros((padded - capacity, LANES), F32)
                tall_dots = jnp.concatenate([tall_dots, blank], axis=0)
            dgv[p] = tall_dots.T[0:8]

            @pl.when(p > 0)
            def _give(p=p):
                send_dx(p).start()
                send_dg(p).start()

            @pl.when(p == 0)
            def _keep():
                own_dx.start()
                own_dg.start()

            save_y(p).start()
        for s in range(per):
            p = base + s
            part = slice(s * capacity, (s + 1) * capacity)
            gate = gates_v[p].T[0:capacity, 0:1]
            xg[rows_of(p), :] = (x[part].astype(F32) * gate).astype(BF)
            dy[rows_of(p), :] = (g[part].astype(F32) * gate).astype(BF)
        return 0

    lax.fori_loop(0, steps, step_body, 0)

    total = size * capacity
    turn = 256
    for k in range(total // turn):
        rows = slice(k * turn, (k + 1) * turn)
        xg_t[:, rows] = xg[rows, :].astype(F32).T.astype(BF)
        dy_t[:, rows] = dy[rows, :].astype(F32).T.astype(BF)
    model = xg_t.shape[0]
    bands = model // turn

    for t in range(1, far):
        for k in range(2):
            down_across(t, k).wait_send()
            down_onward(t, k).wait_send()
    down_beside.wait_send()

    def give(which, step):
        source = (up_v, down_v)[which].at[lax.rem(pair + step, far) * 2 + 1 - core]
        return remote(
            source,
            dw_box.at[which, step],
            dc_s.at[which, step],
            dc_r.at[which, step],
            {"hidden": mate},
        )

    def keep(which, step):
        source = (up_v, down_v)[which].at[lax.rem(pair + step, far) * 2 + core]
        return pltpu.make_async_copy(source, dw_sum.at[which, step], save_sem.at[which, step])

    order = list(range(1, far)) + [0]
    for step in order:
        c = lax.rem(pair + step, far) * 2 + 1 - core

        def other_body(band, _, c=c):
            lines = aligned(band * turn, turn)
            up_v[c, lines, :] = mm(xg_t[lines, :], dz[c]).astype(BF)
            down_v[c, lines, :] = mm(dy_t[lines, :], act[c]).astype(BF)
            return 0

        lax.fori_loop(0, bands, other_body, 0)
        for which in range(2):
            give(which, step).start()
    for step in order:
        c = lax.rem(pair + step, far) * 2 + core
        for which in range(2):
            give(which, step).wait_recv()

        def own_body(band, _, c=c, step=step):
            lines = aligned(band * turn, turn)
            up = mm(xg_t[lines, :], dz[c]) + dw_box[0, step, lines, :].astype(F32)
            down = mm(dy_t[lines, :], act[c]) + dw_box[1, step, lines, :].astype(F32)
            up_v[c, lines, :] = up.astype(BF)
            down_v[c, lines, :] = down.astype(BF)
            return 0

        lax.fori_loop(0, bands, own_body, 0)
        for which in range(2):
            keep(which, step).start()
    for p in range(1, size):
        send_x(p).wait_send()
        send_gate(p).wait_send()
        send_dx(p).wait()
        send_dg(p).wait()
    for p in range(size):
        save_y(p).wait()
    own_dx.wait()
    own_dg.wait()
    for step in order:
        for which in range(2):
            give(which, step).wait_send()
            keep(which, step).wait()


def run_experts(x_slots, gate_rows, g_in, ups, w_down, cid):
    size = lax.axis_size("expert")
    experts, capacity, model = x_slots.shape
    padded = gate_rows.shape[2]
    shards_n, _unused, width = ups.shape
    total = experts * capacity
    per = 1
    while per * 2 * capacity <= 320 and size % (per * 2) == 0:
        per *= 2
    tall = per * capacity
    rows2 = (total, model)
    return pl.pallas_call(
        partial(moe_body, size, capacity, padded, per),
        name="experts",
        out_shape=[
            shape_of(x_slots.shape, BF),
            shape_of(gate_rows.shape, F32),
            shape_of(x_slots.shape, BF),
            shape_of((2, shards_n // 2, model, width), BF),
        ],
        in_specs=[ANY] * 5,
        out_specs=[ANY] * 4,
        scratch_shapes=[
            pltpu.VMEM(rows2, BF),
            pltpu.VMEM(rows2, BF),
            pltpu.VMEM(gate_rows.shape, F32),
            pltpu.VMEM((shards_n, model, width), BF),
            pltpu.VMEM((shards_n, width, model), BF),
            pltpu.VMEM((shards_n, total, width), BF),
            pltpu.VMEM((shards_n, total, width), BF),
            pltpu.VMEM(rows2, BF),
            pltpu.VMEM(rows2, BF),
            pltpu.VMEM((model, total), BF),
            pltpu.VMEM((model, total), BF),
            pltpu.VMEM(rows2, BF),
            pltpu.VMEM(rows2, BF),
            pltpu.VMEM(gate_rows.shape, F32),
            pltpu.VMEM((tall, model), F32),
            pltpu.VMEM((tall, model), F32),
            pltpu.VMEM((2, shards_n // 2, model, width), BF),
            DMA((2,)),
            DMA((2, shards_n // 2)),
            DMA((shards_n // 2, 2)),
            DMA((shards_n // 2, 2)),
            DMA,
            DMA,
            DMA((shards_n // 2, 2)),
            DMA((shards_n // 2, 2)),
            DMA((2, shards_n // 2)),
            DMA((2, shards_n // 2)),
            DMA((size,)),
            DMA((4,)),
        ]
        + [DMA((size,))] * 9,
        compiler_params=pltpu.CompilerParams(
            collective_id=cid, has_side_effects=True, vmem_limit_bytes=60 << 20
        ),
        cost_estimate=pl.CostEstimate(
            flops=12 * total * model * width * shards_n, bytes_accessed=40 << 20, transcendentals=0
        ),
    )(x_slots, gate_rows, g_in, ups, w_down)


def tail_body(
    n_e,
    n_h,
    chunks,
    dh,
    w_all,
    small,
    tokens,
    gain,
    d_res,
    residual,
    gates,
    pos,
    y_back,
    input_grad,
    output,
    full,
    total,
    mine,
    beside,
    across,
    passing,
    x_box,
    z_box,
    w_mid,
    piece,
    small_mid,
    small_h,
    small_e,
    mine_sem,
    cs_sem,
    cr_sem,
    as_sem,
    ar_sem,
    ws_sem,
    wr_sem,
    vs_sem,
    vr_sem,
    hs_sem,
    hr_sem,
    es_sem,
    er_sem,
    keep_sem,
    zs_sem,
    zr_sem,
    xs_sem,
    xr_sem,
    ys_sem,
    yr_sem,
    ms_sem,
    mr_sem,
):
    e, h = lax.axis_index("expert"), lax.axis_index("hidden")
    far, high = n_h // 2, n_e // 2
    pair, core = h // 2, lax.rem(h, 2)
    eh, el = e // 2, lax.rem(e, 2)
    mate = pair * 2 + 1 - core
    greet(
        [{"expert": lax.rem(e + step, n_e)} for step in range(1, n_e)]
        + [{"hidden": lax.rem(h + step, n_h)} for step in range(1, n_h)]
    )
    w_sends, w_order = [], list(range(1, high)) + [0]
    for step in w_order:
        there = lax.rem(eh + step, high)
        copy = remote(
            w_all.at[there * 2 + 1 - el],
            x_box.at[step],
            ws_sem.at[step],
            wr_sem.at[step],
            {"expert": eh * 2 + 1 - el},
        )
        copy.start()
        w_sends.append(copy)
    rows = dh.shape[1] // chunks
    core_sends = {}
    for step in list(range(1, far)) + [0]:
        there = lax.rem(pair + step, far)
        for k in range(chunks):
            part = pl.ds(k * rows, rows)
            copy = remote(
                dh.at[there * 2 + 1 - core, part],
                beside.at[step, part],
                cs_sem.at[step, k],
                cr_sem.at[step, k],
                {"hidden": mate},
            )
            copy.start()
            core_sends[step, k] = copy
    loads = []
    for step in range(far):
        there = lax.rem(pair + step, far)
        load = pltpu.make_async_copy(dh.at[there * 2 + core], mine.at[step], mine_sem.at[step])
        load.start()
        loads.append(load)
    small_sends = []
    for at in range(n_h - 1):
        peer = lax.rem(h + 1 + at, n_h)
        copy = remote(small, small_h.at[at], hs_sem.at[at], hr_sem.at[at], {"hidden": peer})
        copy.start()
        small_sends.append(copy)
    v_sends = []
    for at, step in enumerate(w_order[:-1]):
        there = lax.rem(eh + step, high) * 2 + el
        w_sends[at].wait_recv()
        w_mid[step - 1] = (w_all[there].astype(F32) + x_box[step].astype(F32)).astype(BF)
        copy = remote(
            w_mid.at[step - 1],
            z_box.at[step - 1],
            vs_sem.at[step],
            vr_sem.at[step],
            {"expert": there},
        )
        copy.start()
        v_sends.append(copy)
    for load in loads:
        load.wait()
    far_sends = []
    for step in range(1, far):
        there = lax.rem(pair + step, far)
        for k in range(chunks):
            part = pl.ds(k * rows, rows)
            core_sends[step, k].wait_recv()
            both = mine[step, part, :].astype(F32) + beside[step, part, :].astype(F32)
            passing[step - 1, part, :] = both.astype(BF)
            copy = remote(
                passing.at[step - 1, part],
                across.at[step - 1, part],
                as_sem.at[step - 1, k],
                ar_sem.at[step - 1, k],
                {"hidden": there * 2 + core},
            )
            copy.start()
            far_sends.append(copy)
    for copy in small_sends:
        copy.wait_recv()
    summed = small[...]
    for at in range(n_h - 1):
        summed = summed + small_h[at]
    small_mid[...] = summed
    small_out = []
    for at in range(n_e - 1):
        peer = lax.rem(e + 1 + at, n_e)
        copy = remote(small_mid, small_e.at[at], es_sem.at[at], er_sem.at[at], {"expert": peer})
        copy.start()
        small_out.append(copy)
    w_sends[-1].wait_recv()
    acc = w_all[e].astype(F32) + x_box[0].astype(F32)
    for at, copy in enumerate(v_sends):
        copy.wait_recv()
        acc = acc + z_box[at].astype(F32)
    piece[...] = acc.astype(BF)
    keep = pltpu.make_async_copy(piece, full.at[h, e], keep_sem)
    keep.start()
    started = []

    def slot(eh_of, el_of, pair_of, core_of):
        return full.at[pair_of * 2 + core_of, eh_of * 2 + el_of]

    def back(step, size, place):
        return lax.rem(place + size - step, size)

    def give_z(source):
        for s in range(1, high):
            there = lax.rem(eh + s, high) * 2 + el
            copy = remote(
                source, slot(eh, el, pair, core), zs_sem.at[s], zr_sem.at[s], {"expert": there}
            )
            copy.start()
            started.append(copy)

    def z_arrival(s):
        place = slot(back(s, high, eh), el, pair, core)
        return place, remote(place, place, zs_sem.at[s], zr_sem.at[s], {"expert": e})

    def give_x(source, s):
        target = slot(back(s, high, eh), el, pair, core)
        copy = remote(
            source, target, xs_sem.at[s], xr_sem.at[s], {"expert": eh * 2 + 1 - el}
        )
        copy.start()
        started.append(copy)

    def x_arrival(s):
        place = slot(back(s, high, eh), 1 - el, pair, core)
        return place, remote(place, place, xs_sem.at[s], xr_sem.at[s], {"expert": e})

    def give_y(source, s, flag):
        target = slot(back(s, high, eh), el if flag == 0 else 1 - el, pair, core)
        for t in range(1, far):
            there = lax.rem(pair + t, far) * 2 + core
            at = 2 * s + flag
            copy = remote(
                source, target, ys_sem.at[t, at], yr_sem.at[t, at], {"hidden": there}
            )
            copy.start()
            started.append(copy)

    def y_arrival(t, s, flag):
        other = el if flag == 0 else 1 - el
        place = slot(back(s, high, eh), other, back(t, far, pair), core)
        at = 2 * s + flag
        return place, remote(place, place, ys_sem.at[t, at], yr_sem.at[t, at], {"hidden": h})

    def give_mate(source, t, s, flag):
        other = el if flag == 0 else 1 - el
        target = slot(back(s, high, eh), other, back(t, far, pair), core)
        at = 2 * s + flag
        copy = remote(source, target, ms_sem.at[t, at], mr_sem.at[t, at], {"hidden": mate})
        copy.start()
        started.append(copy)

    def mate_arrival(t, s, flag):
        other = el if flag == 0 else 1 - el
        place = slot(back(s, high, eh), other, back(t, far, pair), 1 - core)
        at = 2 * s + flag
        return place, remote(place, place, ms_sem.at[t, at], mr_sem.at[t, at], {"hidden": h})

    give_z(piece)
    give_x(piece, 0)
    give_y(piece, 0, 0)
    give_mate(piece, 0, 0, 0)
    for s in range(1, high):
        place, arrival = z_arrival(s)
        arrival.wait_recv()
        give_x(place, s)
        give_y(place, s, 0)
        give_mate(place, 0, s, 0)
    for s in range(high):
        place, arrival = x_arrival(s)
        arrival.wait_recv()
        give_y(place, s, 1)
        give_mate(place, 0, s, 1)
    place_of = iota((residual.shape[0], y_back.shape[0]), 1)
    result = residual[...]
    for j in range(2):
        pick = (place_of == pos[:, j : j + 1]).astype(BF)
        result = result + gates[:, j : j + 1] * mm(pick, y_back[...])
    output[...] = result.astype(BF)
    for copy in small_out:
        copy.wait_recv()
    summed = small_mid[...]
    for at in range(n_e - 1):
        summed = summed + small_e[at]
    total[...] = summed
    for k in range(chunks):
        part = pl.ds(k * rows, rows)
        core_sends[0, k].wait_recv()
    for copy in far_sends:
        copy.wait_recv()
    grad = mine[0].astype(F32) + beside[0].astype(F32)
    for step in range(far - 1):
        grad = grad + across[step].astype(F32)
    normed, inverse = norm_parts(tokens[...].astype(F32))
    input_grad[...] = (d_res[...] + norm_back(grad, normed, inverse, lying(gain))).astype(BF)
    for t in range(1, far):
        for s in range(high):
            for flag in range(2):
                place, arrival = y_arrival(t, s, flag)
                arrival.wait_recv()
                give_mate(place, t, s, flag)
    for t in range(far):
        for s in range(high):
            for flag in range(2):
                _place, arrival = mate_arrival(t, s, flag)
                arrival.wait_recv()
    keep.wait()
    for copy in started + w_sends + v_sends + small_sends + small_out + far_sends:
        copy.wait_send()
    for copy in core_sends.values():
        copy.wait_send()


def run_tail(dh, w_all, small, tokens, gain, d_res, residual, gates, pos, y_back, cid):
    n_e, n_h = lax.axis_size("expert"), lax.axis_size("hidden")
    far, high = n_h // 2, n_e // 2
    chunks = 4
    _unused, rows, model = dh.shape
    piece = w_all.shape[1:]
    return pl.pallas_call(
        partial(tail_body, n_e, n_h, chunks),
        name="tail",
        out_shape=[
            shape_of((rows, model), BF),
            shape_of((rows, model), BF),
            shape_of((n_h, n_e, *piece), BF),
            shape_of(small.shape, F32),
        ],
        in_specs=[ANY] + [VMEM] * 9,
        out_specs=[VMEM, VMEM, ANY, VMEM],
        scratch_shapes=[
            pltpu.VMEM((far, rows, model), BF),
            pltpu.VMEM((far, rows, model), BF),
            pltpu.VMEM((far - 1, rows, model), BF),
            pltpu.VMEM((far - 1, rows, model), BF),
            pltpu.VMEM((high, *piece), BF),
            pltpu.VMEM((high - 1, *piece), BF),
            pltpu.VMEM((high - 1, *piece), BF),
            pltpu.VMEM(piece, BF),
            pltpu.VMEM(small.shape, F32),
            pltpu.VMEM((n_h - 1, *small.shape), F32),
            pltpu.VMEM((n_e - 1, *small.shape), F32),
            DMA((far,)),
            DMA((far, chunks)),
            DMA((far, chunks)),
            DMA((far - 1, chunks)),
            DMA((far - 1, chunks)),
            DMA((high,)),
            DMA((high,)),
            DMA((high,)),
            DMA((high,)),
            DMA((n_h - 1,)),
            DMA((n_h - 1,)),
            DMA((n_e - 1,)),
            DMA((n_e - 1,)),
            DMA,
            DMA((high,)),
            DMA((high,)),
            DMA((high,)),
            DMA((high,)),
            DMA((far, n_e)),
            DMA((far, n_e)),
            DMA((far, n_e)),
            DMA((far, n_e)),
        ],
        compiler_params=pltpu.CompilerParams(
            collective_id=cid, has_side_effects=True, vmem_limit_bytes=56 << 20
        ),
    )(dh, w_all, small, tokens, gain, d_res, residual, gates, pos, y_back)


def turn_body(
    width,
    experts,
    full,
    dw,
    small,
    input_grad,
    output,
    q_out,
    k_out,
    v_out,
    o_out,
    up_out,
    down_out,
    g1_out,
    s1_out,
    g2_out,
    s2_out,
    router_out,
    input_out,
    output_out,
    sem,
):
    step = pl.program_id(0)
    moves = [
        pltpu.make_async_copy(input_grad, input_out, sem.at[0]),
        pltpu.make_async_copy(output, output_out, sem.at[1]),
    ]

    @pl.when(step == 0)
    def _begin():
        for move in moves:
            move.start()
        for n, out in enumerate((g1_out, s1_out, g2_out, s2_out)):
            out[...] = small[n : n + 1, :].reshape(out.shape)
        router_out[...] = small[8 : 8 + experts, :]

    for n, out in enumerate((q_out, k_out, v_out)):
        part = full[:, n * width : (n + 1) * width, :].astype(F32)
        out[...] = part.reshape(-1, part.shape[2]).T
    part = full[:, 3 * width :, :].astype(F32)
    o_out[...] = part.reshape(-1, part.shape[2])
    trained = jnp.where(lax.axis_index("expert") >= experts // 2, 1.0, 0.0)
    up_out[...] = dw[0] * trained
    down_out[...] = dw[1].T * trained

    @pl.when(step == pl.num_programs(0) - 1)
    def _end():
        for move in moves:
            move.wait()


def turn_weights(full, dw, small, input_grad, output, width, experts):
    n_h, deep, model = full.shape
    cols = 256
    across = pl.BlockSpec((cols, model), lambda i: (i, 0))
    down = pl.BlockSpec((model, cols), lambda i: (0, i))
    flat = pl.BlockSpec((model,), lambda i: (0,))
    square = shape_of((model, model), F32)
    return pl.pallas_call(
        partial(turn_body, width, experts),
        name="turn_weights",
        grid=(model // cols,),
        out_shape=[square] * 6
        + [shape_of((model,), F32)] * 4
        + [
            shape_of((experts, model), F32),
            shape_of(input_grad.shape, BF),
            shape_of(output.shape, BF),
        ],
        in_specs=[
            pl.BlockSpec((n_h, deep, cols), lambda i: (0, 0, i)),
            pl.BlockSpec((2, model, cols), lambda i: (0, 0, i)),
            pl.BlockSpec(small.shape, lambda i: (0, 0)),
            ANY,
            ANY,
        ],
        out_specs=[across, across, across, down, down, across]
        + [flat] * 4
        + [pl.BlockSpec((experts, model), lambda i: (0, 0)), ANY, ANY],
        scratch_shapes=[DMA((2,))],
        compiler_params=pltpu.CompilerParams(
            dimension_semantics=("arbitrary",), vmem_limit_bytes=60 << 20
        ),
        cost_estimate=pl.CostEstimate(flops=0, bytes_accessed=24 << 20, transcendentals=0),
    )(full, dw, small, input_grad, output)


def attend_back(heads, ends, blocks, per_device, qkv, d_att, lse, dots, keys, values, accs, d_qkv):
    width = heads * HEAD_DIM
    dq_acc, dk_acc, dv_acc = accs

    def over_keys(j, _):
        part = aligned(j * BLOCK, BLOCK)
        k_pos = j * BLOCK + iota((BLOCK, BLOCK), 0)
        stop = (j + REACH) - (j - (REACH - 2)) * (j // (REACH - 1))
        dk_acc[...] = jnp.zeros_like(dk_acc)
        dv_acc[...] = jnp.zeros_like(dv_acc)

        def over_queries(i, _):
            rows = aligned(i * BLOCK, BLOCK)
            cols = aligned(lax.rem(i, per_device) * BLOCK, BLOCK)
            q_pos = i * BLOCK + iota((1, BLOCK), 1)
            begin = start_of(q_pos, ends)
            allowed = (k_pos <= q_pos) & (k_pos >= begin)
            for n in range(heads):
                here = slice(n * HEAD_DIM, (n + 1) * HEAD_DIM)
                query = qkv[here, rows] * jnp.asarray(SCALE, BF)
                given = d_att[i // per_device, here, cols]
                score = mm(keys[n, part, :], query) - lse[n : n + 1, rows]
                weight = jnp.exp(jnp.where(allowed, score, MASKED))
                d_weight = mm(values[n, part, :], given)
                d_score = (weight * (d_weight - dots[n : n + 1, rows])).astype(BF)
                dv_acc[here, :] += mm_nt(given, weight.astype(BF))
                dk_acc[here, :] += mm_nt(query, d_score)
                lo = width + n * HEAD_DIM
                dq_acc[here, rows] += mm(qkv[lo : lo + HEAD_DIM, part], d_score)
            return 0

        lax.fori_loop(j, stop, over_queries, 0)
        d_qkv[width : 2 * width, part] = dk_acc[...].astype(BF)
        d_qkv[2 * width :, part] = dv_acc[...].astype(BF)
        return 0

    lax.fori_loop(0, blocks, over_keys, 0)


def back_body(
    n_e,
    n_h,
    experts,
    capacity,
    padded,
    heads,
    docs,
    ids,
    slot,
    pos,
    gates,
    count,
    g1,
    s1,
    g2,
    s2,
    w_router,
    lse,
    dg_rows,
    dx_back,
    y_out,
    dw_sum,
    out_grad,
    residual,
    all_tokens,
    qkv_in,
    att_in,
    att_t_in,
    w_out,
    w_t_in,
    y_back,
    d_hidden,
    d_res,
    w_all,
    small,
    dw_own,
    dxv,
    gv,
    res_v,
    tv,
    qkv,
    att_v,
    att_t,
    wo,
    w_t,
    d_att_v,
    d_att,
    wo_box,
    wo_far,
    keys,
    values,
    dots,
    dq_acc,
    dk_acc,
    dv_acc,
    d_qkv,
    w_acc,
    dw_mine,
    dw_across,
    load_sem,
    save_sem,
    dw_sem,
    y_own,
    y_s,
    y_r,
    at_s,
    at_r,
    wo_s,
    wo_r,
    wf_s,
    wf_r,
    da_s,
    da_r,
):
    e, h = lax.axis_index("expert"), lax.axis_index("hidden")
    far = n_h // 2
    pair, core = h // 2, lax.rem(h, 2)
    mate = pair * 2 + 1 - core
    rows, model = out_grad.shape
    width = heads * HEAD_DIM
    group = rows * n_h
    per_device = rows // BLOCK
    blocks = group // BLOCK
    ends = doc_bounds(docs)
    sends = []

    loads = [
        pltpu.make_async_copy(source, target, load_sem.at[n])
        for n, (source, target) in enumerate(
            (
                (residual, res_v),
                (dx_back, dxv),
                (out_grad, gv),
                (w_out, wo),
                (att_t_in, att_t),
                (qkv_in, qkv),
                (att_in, att_v),
                (all_tokens, tv),
                (w_t_in, w_t),
            )
        )
    ]
    for load in loads:
        load.start()
    greet(
        [{"hidden": lax.rem(h + step, n_h)} for step in range(1, n_h)]
        + [{"expert": lax.rem(e + step, n_e)} for step in range(1, n_e)]
    )
    load_dw = pltpu.make_async_copy(dw_sum.at[:, 0], dw_mine, dw_sem)
    load_dw.start()
    deep = dw_mine.shape[1] // 2

    def dw_across_copy(which, step, k):
        part = pl.ds(k * deep, deep)
        return remote(
            dw_sum.at[which, step, part],
            dw_across.at[which, step - 1, part],
            da_s.at[which, step, k],
            da_r.at[which, step, k],
            {"hidden": lax.rem(pair + step, far) * 2 + core},
        )

    def dw_send(which, k):
        for step in range(1, far):
            copy = dw_across_copy(which, step, k)
            copy.start()
            sends.append(copy)

    dw_send(0, 0)
    for step in range(1, n_e):
        peer = lax.rem(e + step, n_e)
        copy = remote(y_out.at[peer], y_back.at[e], y_s.at[step], y_r.at[step], {"expert": peer})
        copy.start()
        sends.append(copy)
    own_y = pltpu.make_async_copy(y_out.at[e], y_back.at[e], y_own)
    own_y.start()

    for load in loads[:3]:
        load.wait()
    normed, inverse = norm_parts(res_v[...])
    hidden = (normed * lying(g2) + lying(s2)).astype(BF)
    gate = [gates[:, j : j + 1] for j in range(2)]
    column = iota((rows, padded), 1)
    dot_of = []
    for j in range(2):
        mix = jnp.zeros((rows, padded), F32)
        for n in range(experts):
            here = jnp.where(ids[:, j : j + 1] == n, slot[:, j : j + 1], -1) == column
            mix = jnp.where(here, dg_rows[n, 0:1, :], mix)
        dot_of.append(jnp.sum(mix, axis=1, keepdims=True))
    mean = gate[0] * dot_of[0] + gate[1] * dot_of[1]
    lane = iota((rows, experts), 1)
    d_logits = jnp.zeros((rows, experts), F32)
    for j in range(2):
        d_logits = jnp.where(lane == ids[:, j : j + 1], gate[j] * (dot_of[j] - mean), d_logits)
    high, low = split_two(d_logits)
    grad = mm(high, w_router[...]) + mm(low, w_router[...])
    small[...] = jnp.zeros_like(small)
    small[8 : 8 + experts, :] = mm_tn(high, hidden) + mm_tn(low, hidden)
    small[4:5, 0:LANES] = count[...]
    place = iota((rows, experts * capacity), 1)
    for j in range(2):
        pick = (place == pos[:, j : j + 1]).astype(BF)
        grad = grad + gate[j] * mm(pick, dxv[...])
    small[2:3, :] = jnp.sum(grad * normed, axis=0, keepdims=True)
    small[3:4, :] = jnp.sum(grad, axis=0, keepdims=True)
    d_resid = gv[...].astype(F32) + norm_back(grad, normed, inverse, lying(g2))
    d_res[...] = d_resid
    branch = d_resid.astype(BF)
    loads[3].wait()
    for t in range(n_h):
        owner = lax.rem(h + t, n_h)
        block = mm_nt(wo[owner], branch).astype(BF)
        if t == 0:
            d_att[h] = block
        else:
            d_att_v[owner] = block
            copy = remote(
                d_att_v.at[owner], d_att.at[h], at_s.at[t], at_r.at[t], {"hidden": owner}
            )
            copy.start()
            sends.append(copy)
    loads[4].wait()
    for t in range(n_h):
        owner = lax.rem(h + t, n_h)
        wo[owner] = mm(att_t[owner], branch).astype(BF)
    for step in list(range(1, far)) + [0]:
        copy = remote(
            wo.at[lax.rem(pair + step, far) * 2 + 1 - core],
            wo_box.at[step],
            wo_s.at[step],
            wo_r.at[step],
            {"hidden": mate},
        )
        copy.start()
        sends.append(copy)
    for load in loads[5:]:
        load.wait()
    dq_acc[...] = jnp.zeros_like(dq_acc)

    def turn(i, _):
        cols = aligned(i * BLOCK, BLOCK)
        for n in range(heads):
            lo = width + n * HEAD_DIM
            keys[n, cols, :] = qkv[lo : lo + HEAD_DIM, cols].astype(F32).T.astype(BF)
            lo = 2 * width + n * HEAD_DIM
            values[n, cols, :] = qkv[lo : lo + HEAD_DIM, cols].astype(F32).T.astype(BF)
        return 0

    lax.fori_loop(0, blocks, turn, 0)
    for t in range(1, n_h):
        there = d_att.at[lax.rem(h + n_h - t, n_h)]
        remote(there, there, at_s.at[t], at_r.at[t], {"hidden": mate}).wait_recv()
    for step in range(1, far):
        owner = lax.rem(pair + step, far) * 2 + core
        there = wo_box.at[step]
        remote(there, there, wo_s.at[step], wo_r.at[step], {"hidden": mate}).wait_recv()
        wo[owner] = (wo[owner].astype(F32) + wo_box[step].astype(F32)).astype(BF)
        copy = remote(
            wo.at[owner], wo_far.at[step - 1], wf_s.at[step], wf_r.at[step], {"hidden": owner}
        )
        copy.start()
        sends.append(copy)
    dw_send(0, 1)
    dw_send(1, 0)
    dw_send(1, 1)

    def weigh(i, _):
        cols = aligned(lax.rem(i, per_device) * BLOCK, BLOCK)
        for n in range(heads):
            here = slice(n * HEAD_DIM, (n + 1) * HEAD_DIM)
            product = att_v[i // per_device, here, cols].astype(F32)
            product = product * d_att[i // per_device, here, cols].astype(F32)
            dots[n : n + 1, aligned(i * BLOCK, BLOCK)] = jnp.sum(product, axis=0, keepdims=True)
        return 0

    lax.fori_loop(0, blocks, weigh, 0)
    accs = (dq_acc, dk_acc, dv_acc)
    attend_back(
        heads, ends, blocks, per_device, qkv, d_att, lse, dots, keys, values, accs, d_qkv
    )
    w_acc[...] = jnp.zeros_like(w_acc)

    def finish(i, _):
        cols = aligned(i * BLOCK, BLOCK)
        d_qkv[0:width, cols] = (dq_acc[:, cols] * SCALE).astype(BF)
        block = d_qkv[:, cols]
        grad = mm_tn(block, w_t[...])
        inner = aligned(lax.rem(i, per_device) * BLOCK, BLOCK)
        normed, _unused = norm_parts(tv[i // per_device, inner, :].astype(F32))
        tv[i // per_device, inner, :] = grad.astype(BF)
        small[0:1, :] += jnp.sum(grad * normed, axis=0, keepdims=True)
        small[1:2, :] += jnp.sum(grad, axis=0, keepdims=True)
        hidden = (normed * lying(g1) + lying(s1)).astype(BF)
        w_acc[...] += mm(block, hidden)
        return 0

    lax.fori_loop(0, blocks, finish, 0)
    save_dh = pltpu.make_async_copy(tv, d_hidden, save_sem)
    save_dh.start()
    w_all[0 : 3 * width, :] = w_acc[...].astype(BF)
    there = wo_box.at[0]
    remote(there, there, wo_s.at[0], wo_r.at[0], {"hidden": mate}).wait_recv()
    total = wo[h].astype(F32) + wo_box[0].astype(F32)
    for step in range(1, far):
        there = wo_far.at[step - 1]
        remote(there, there, wf_s.at[step], wf_r.at[step], {"hidden": mate}).wait_recv()
        total = total + wo_far[step - 1].astype(F32)
    w_all[3 * width :, :] = total.astype(BF)
    load_dw.wait()
    for which in range(2):
        for step in range(1, far):
            for k in range(2):
                dw_across_copy(which, step, k).wait_recv()

        def add_all(n, _, which=which):
            band = aligned(n * 96, 96)
            both = dw_mine[which, band, :].astype(F32)
            for step in range(1, far):
                both = both + dw_across[which, step - 1, band, :].astype(F32)
            dw_own[which, band, :] = both
            return 0

        lax.fori_loop(0, dw_mine.shape[1] // 96, add_all, 0)
    for step in range(1, n_e):
        there = y_back.at[lax.rem(e + n_e - step, n_e)]
        remote(there, there, y_s.at[step], y_r.at[step], {"expert": e}).wait_recv()
    own_y.wait()
    save_dh.wait()
    for copy in sends:
        copy.wait_send()


def run_back(
    docs,
    ids,
    slot,
    pos,
    gates,
    count,
    g1,
    s1,
    g2,
    s2,
    w_router,
    lse,
    dg_rows,
    dx_back,
    y_out,
    dw_sum,
    out_grad,
    residual,
    all_tokens,
    qkv,
    att,
    att_t,
    w_out,
    w_t,
    cid,
):
    n_e, n_h = lax.axis_size("expert"), lax.axis_size("hidden")
    experts, capacity, model = y_out.shape
    padded = dg_rows.shape[2]
    rows = out_grad.shape[0]
    width = w_t.shape[0] // 3
    heads = width // HEAD_DIM
    group, far = rows * n_h, n_h // 2
    shard = dw_sum.shape[2:]
    tall = 8 + experts

    def pairs(*shape):
        return [DMA(shape), DMA(shape)]

    return pl.pallas_call(
        partial(back_body, n_e, n_h, experts, capacity, padded, heads),
        name="back",
        out_shape=[
            shape_of(y_out.shape, BF),
            shape_of((n_h, rows, model), BF),
            shape_of((rows, model), F32),
            shape_of((4 * width, model), BF),
            shape_of((tall, model), F32),
            shape_of((2, *shard), F32),
        ],
        in_specs=[SMEM] + [VMEM] * 12 + [ANY] * 11,
        out_specs=[ANY] * 2 + [VMEM] * 4,
        scratch_shapes=[
            pltpu.VMEM((experts * capacity, model), BF),
            pltpu.VMEM((rows, model), BF),
            pltpu.VMEM((rows, model), F32),
            pltpu.VMEM((n_h, rows, model), BF),
            pltpu.VMEM((3 * width, group), BF),
            pltpu.VMEM((n_h, width, rows), BF),
            pltpu.VMEM((n_h, width, rows), BF),
            pltpu.VMEM((n_h, width, model), BF),
            pltpu.VMEM((3 * width, model), BF),
            pltpu.VMEM((n_h, width, rows), BF),
            pltpu.VMEM((n_h, width, rows), BF),
            pltpu.VMEM((far, width, model), BF),
            pltpu.VMEM((far - 1, width, model), BF),
            pltpu.VMEM((heads, group, HEAD_DIM), BF),
            pltpu.VMEM((heads, group, HEAD_DIM), BF),
            pltpu.VMEM((8, group), F32),
            pltpu.VMEM((width, group), F32),
            pltpu.VMEM((width, BLOCK), F32),
            pltpu.VMEM((width, BLOCK), F32),
            pltpu.VMEM((3 * width, group), BF),
            pltpu.VMEM((3 * width, model), F32),
            pltpu.VMEM((2, *shard), BF),
            pltpu.VMEM((2, far - 1, *shard), BF),
            DMA((9,)),
            DMA,
            DMA,
            DMA,
            *pairs(n_e),
            *pairs(n_h),
            *pairs(far),
            *pairs(far),
            *pairs(2, far, 2),
        ],
        compiler_params=pltpu.CompilerParams(
            collective_id=cid, has_side_effects=True, vmem_limit_bytes=60 << 20
        ),
    )(
        docs,
        ids,
        slot,
        pos,
        gates,
        count,
        g1,
        s1,
        g2,
        s2,
        w_router,
        lse,
        dg_rows,
        dx_back.reshape(experts * capacity, model),
        y_out,
        dw_sum,
        out_grad,
        residual,
        all_tokens,
        qkv,
        att,
        att_t,
        w_out.reshape(n_h, width, model),
        w_t,
    )


def shards(
    tokens,
    doc_lengths,
    expert_ids,
    gain_one,
    shift_one,
    w_query,
    w_key,
    w_value,
    w_out,
    gain_two,
    shift_two,
    w_router,
    w_up,
    w_down,
    out_grad,
):
    rows, model = tokens.shape
    n_expert, n_hidden = lax.axis_size("expert"), lax.axis_size("hidden")
    experts = n_expert * w_up.shape[0]
    capacity = max(2, rows * 2 * 5 // (4 * experts))
    capacity = -(-capacity // 16) * 16
    total = experts * capacity
    heads = HEADS // n_hidden
    width = heads * HEAD_DIM
    g1, s1, g2, s2 = gain_one, shift_one, gain_two, shift_two
    router_t = w_router.T

    (
        all_tokens,
        qkv,
        att,
        att_t,
        w_t,
        g_in,
        x_slots,
        ups,
        ids,
        pos,
        slot,
        count,
        lse,
        residual,
        gates,
        gate_rows,
    ) = run_front(
        doc_lengths,
        expert_ids.T,
        g1,
        s1,
        g2,
        s2,
        router_t,
        tokens,
        out_grad,
        (w_query, w_key, w_value, w_out),
        w_up,
        capacity,
        heads,
        1,
    )
    dx_back, dg_back, y_out, dw_sum = run_experts(x_slots, gate_rows, g_in, ups, w_down, 2)
    y_back, d_hidden, d_res, w_all, small, dw_own = run_back(
        doc_lengths,
        ids,
        slot,
        pos,
        gates,
        count,
        g1,
        s1,
        g2,
        s2,
        router_t,
        lse,
        dg_back,
        dx_back,
        y_out,
        dw_sum,
        out_grad,
        residual,
        all_tokens,
        qkv,
        att,
        att_t,
        w_out,
        w_t,
        3,
    )
    input_grad, output, full, small = run_tail(
        d_hidden,
        w_all.reshape(n_expert, 4 * width // n_expert, model),
        small,
        tokens,
        g1,
        d_res,
        residual,
        gates,
        pos,
        y_back.reshape(total, model),
        4,
    )
    scale = experts / (rows * n_expert * n_hidden * 2)
    turned = turn_weights(
        full.reshape(n_hidden, 4 * width, model),
        dw_own,
        small,
        input_grad,
        output,
        width,
        experts,
    )
    w_grads, (up_grad, down_grad) = turned[:4], turned[4:6]
    gain_one_grad, shift_one_grad, gain_two_grad, shift_two_grad = turned[6:10]
    router_grad, input_grad, output = turned[10:]
    return (
        output,
        input_grad,
        gain_one_grad,
        shift_one_grad,
        *w_grads,
        gain_two_grad,
        shift_two_grad,
        router_grad.T,
        up_grad[None],
        down_grad[None],
        small[4, :experts] * scale,
    )


def solution(mesh):
    in_specs = (
        P(("expert", "hidden"), None),
        P("expert", None),
        P(("expert", "hidden"), None),
        P(),
        P(),
        P(),
        P(),
        P(),
        P(),
        P(),
        P(),
        P(),
        P("expert", None, "hidden"),
        P("expert", "hidden", None),
        P(("expert", "hidden"), None),
    )
    out_specs = (
        P(("expert", "hidden"), None),
        P(("expert", "hidden"), None),
        P(),
        P(),
        P(),
        P(),
        P(),
        P(),
        P(),
        P(),
        P(),
        P("expert", None, "hidden"),
        P("expert", "hidden", None),
        P(),
    )
    return jax.shard_map(shards, mesh=mesh, in_specs=in_specs, out_specs=out_specs, check_vma=False)
```

```python
from functools import partial

import jax
import jax.numpy as jnp
from jax import lax
from jax.experimental import pallas as pl
from jax.experimental.pallas import tpu as pltpu
from jax.sharding import PartitionSpec as P

HEAD_DIM = 64
HEADS = 12
EPSILON = 1e-05
SCALE = 0.125
MASKED = -1e30
BLOCK = 256
LONGEST = 1024
REACH = LONGEST // BLOCK + 1
LANES = 128
BF = jnp.bfloat16
F32 = jnp.float32
I32 = jnp.int32
MESH = pl.DeviceIdType.MESH
ANY = pl.BlockSpec(memory_space=pl.ANY)
SMEM = pl.BlockSpec(memory_space=pltpu.SMEM)
VMEM = pl.BlockSpec(memory_space=pltpu.VMEM)
DMA = pltpu.SemaphoreType.DMA
GELU_A = 0.7978845608028654
GELU_B = 0.044715


def mm(left, right):
    return jnp.dot(left, right, preferred_element_type=F32)


def mm_nt(left, right):
    return lax.dot_general(left, right, (((1,), (1,)), ((), ())), preferred_element_type=F32)


def mm_tn(left, right):
    return lax.dot_general(left, right, (((0,), (0,)), ((), ())), preferred_element_type=F32)


def iota(shape, axis):
    return lax.broadcasted_iota(I32, shape, axis)


def norm_parts(values):
    centred = values - jnp.mean(values, axis=-1, keepdims=True)
    inverse = lax.rsqrt(jnp.mean(centred * centred, axis=-1, keepdims=True) + EPSILON)
    return centred * inverse, inverse


def norm_back(grad_out, normed, inverse, gain):
    grad_normed = grad_out * gain
    first = jnp.mean(grad_normed, axis=-1, keepdims=True)
    second = jnp.mean(grad_normed * normed, axis=-1, keepdims=True)
    return inverse * (grad_normed - first - normed * second)


def split_two(value):
    high = value.astype(BF)
    return high, (value - high.astype(F32)).astype(BF)


def shape_of(shape, dtype):
    return jax.ShapeDtypeStruct(shape, dtype)


def greet(peers):
    barrier = pltpu.get_barrier_semaphore()
    for peer in peers:
        pl.semaphore_signal(barrier, inc=1, device_id=peer, device_id_type=MESH)
    pl.semaphore_wait(barrier, len(peers))


def remote(src, dst, send, recv, peer):
    return pltpu.make_async_remote_copy(
        src_ref=src, dst_ref=dst, send_sem=send, recv_sem=recv, device_id=peer, device_id_type=MESH
    )


def doc_bounds(docs):
    ends, at = [], 0
    for n in range(docs.shape[1] - 1):
        at = at + docs[0, n]
        ends.append(at)
    return ends


def start_of(place, ends):
    begin = jnp.zeros_like(place)
    for end in ends:
        begin = jnp.where(place >= end, end, begin)
    return begin


def lying(ref):
    return ref[...].reshape(1, ref.shape[0])


def aligned(at, size):
    return pl.ds(pl.multiple_of(at, size), size)


def find_slots(experts, capacity, ids, ids_t, pos, slot, count):
    rows = ids_t.shape[1]
    row = [ids_t[j : j + 1, :] for j in range(2)]
    tall = jnp.concatenate([r.astype(F32) for r in row] + [jnp.zeros((6, rows), F32)], axis=0)
    ids[...] = tall.T[:, 0:2].astype(I32)
    col = [ids[:, j : j + 1] for j in range(2)]
    lane = iota((rows, LANES), 1)
    hot = [(lane == c).astype(BF) for c in col]
    either = hot[0] + hot[1]
    below = (iota((rows, rows), 0) > iota((rows, rows), 1)).astype(BF)
    before = mm(below, either)
    wide = max(experts, 16)
    deep = iota((wide, rows), 0)
    hot_t = [(deep == r).astype(BF) for r in row]
    above = (iota((rows, rows), 0) < iota((rows, rows), 1)).astype(BF)
    before_t = mm(hot_t[0] + hot_t[1], above)
    count[...] = jnp.sum(either.astype(F32), axis=0, keepdims=True)
    flat_t = []
    for j in range(2):
        at = jnp.sum(hot[j].astype(F32) * before, axis=1, keepdims=True).astype(I32)
        pos[:, j : j + 1] = col[j] * capacity + at
        slot[:, j : j + 1] = at
        at_t = jnp.sum(hot_t[j].astype(F32) * before_t, axis=0, keepdims=True).astype(I32)
        flat_t.append(row[j] * capacity + at_t)
    return flat_t


def fill_slots(flat_t, source, out):
    total, rows = out.shape[0], source.shape[0]
    half = total // 2
    for n in range(2):
        place = iota((half, rows), 0) + n * half
        pick = ((place == flat_t[0]) | (place == flat_t[1])).astype(BF)
        out[pl.ds(n * half, half), :] = mm(pick, source).astype(BF)


def attend_block(heads, ends, i, span, first, qkv, keys, scores, kept, inverse):
    width = heads * HEAD_DIM
    base = i * BLOCK
    rows = aligned(base, BLOCK)
    q_pos = base + iota((1, BLOCK), 1)
    begin = start_of(q_pos, ends)
    queries = [
        qkv[n * HEAD_DIM : (n + 1) * HEAD_DIM, rows] * jnp.asarray(SCALE, BF) for n in range(heads)
    ]
    tops = [jnp.full((1, BLOCK), MASKED, F32)] * heads
    for k in range(span):
        part = aligned((first + k) * BLOCK, BLOCK)
        k_pos = (first + k) * BLOCK + iota((BLOCK, BLOCK), 0)
        allowed = (k_pos <= q_pos) & (k_pos >= begin)
        for n in range(heads):
            score = jnp.where(allowed, mm(keys[n, part, :], queries[n]), MASKED)
            scores[n, k] = score
            tops[n] = jnp.maximum(tops[n], jnp.max(score, axis=0, keepdims=True))
    result = []
    for n in range(heads):
        total = jnp.zeros((1, BLOCK), F32)
        acc = jnp.zeros((HEAD_DIM, BLOCK), F32)
        lo = 2 * width + n * HEAD_DIM
        for k in range(span):
            weight = jnp.exp(scores[n, k] - tops[n])
            total = total + jnp.sum(weight, axis=0, keepdims=True)
            value = qkv[lo : lo + HEAD_DIM, aligned((first + k) * BLOCK, BLOCK)]
            low = weight.astype(BF)
            kept[n, k] = low
            acc = acc + mm(value, low)
        whole = 1.0 / total
        inverse[n : n + 1, rows] = whole
        result.append((acc * whole).astype(BF))
    return result


def spans(i, body):
    @pl.when(i < 2)
    def _short():
        body(2, 0)

    @pl.when(i >= 2)
    def _long():
        body(REACH, (i - (REACH - 1)) * (i // (REACH - 1)))


def front_body(
    n_e,
    n_h,
    experts,
    capacity,
    padded,
    heads,
    chunks,
    docs,
    ids_t,
    g1,
    s1,
    g2,
    s2,
    w_router,
    tokens,
    out_grad,
    w_query,
    w_key,
    w_value,
    w_out,
    w_up,
    all_tokens,
    qkv_out,
    att_out,
    att_t_out,
    w_t_out,
    g_in,
    x_slots,
    ups,
    weights,
    ids,
    pos,
    slot,
    count,
    inverse,
    residual,
    gates,
    gate_rows,
    tv,
    gv,
    wv,
    wo,
    w_t,
    qkv,
    keys,
    scores,
    kept,
    att_v,
    att_in,
    g_slots,
    xs_v,
    own_sem,
    w_sem,
    save_sem,
    kept_sem,
    ty_s,
    ty_r,
    tc_s,
    tc_r,
    tf_s,
    tf_r,
    gs_s,
    gs_r,
    at_s,
    at_r,
    wy_s,
    wy_r,
    wc_s,
    wc_r,
    wf_s,
    wf_r,
):
    e, h = lax.axis_index("expert"), lax.axis_index("hidden")
    far = n_h // 2
    pair, core = h // 2, lax.rem(h, 2)
    mate = pair * 2 + 1 - core
    rows, model = tokens.shape
    width = heads * HEAD_DIM
    per_device = rows // BLOCK
    ends = doc_bounds(docs)

    def across(t):
        return lax.rem(pair + t, far) * 2 + core

    def origin(t):
        return lax.rem(pair + far - t, far) * 2 + core

    own_tokens = pltpu.make_async_copy(tokens, tv.at[h], own_sem.at[0])
    own_grad = pltpu.make_async_copy(out_grad, gv, own_sem.at[1])
    own_grad.start()
    own_tokens.start()
    w_loads = [
        pltpu.make_async_copy(w, wv.at[n], w_sem.at[n])
        for n, w in enumerate((w_query, w_key, w_value))
    ]
    w_loads.append(pltpu.make_async_copy(w_out, wo, w_sem.at[3]))
    for load in w_loads:
        load.start()
    greet(
        [{"hidden": lax.rem(h + step, n_h)} for step in range(1, n_h)]
        + [{"expert": lax.rem(e + step, n_e)} for step in range(1, n_e)]
    )

    piece = rows // chunks
    sends = []
    for k in range(chunks):
        part = pl.ds(k * piece, piece)
        for t in range(1, far):
            copy = remote(
                tokens.at[part],
                tv.at[h, part],
                ty_s.at[t, k],
                ty_r.at[t, k],
                {"hidden": across(t)},
            )
            copy.start()
            sends.append(copy)
    beside = remote(tokens, tv.at[h], tc_s, tc_r, {"hidden": mate})
    beside.start()
    sends.append(beside)

    flat_t = find_slots(experts, capacity, ids, ids_t, pos, slot, count)
    own_grad.wait()
    fill_slots(flat_t, gv[...], g_slots)
    for step in range(1, n_e):
        peer = lax.rem(e + step, n_e)
        copy = remote(
            g_slots.at[aligned(peer * capacity, capacity)],
            g_in.at[e],
            gs_s.at[step],
            gs_r.at[step],
            {"expert": peer},
        )
        copy.start()
        sends.append(copy)
    own_slots = pltpu.make_async_copy(
        g_slots.at[aligned(e * capacity, capacity)], g_in.at[e], own_sem.at[1]
    )
    own_slots.start()

    def pass_on(t, k):
        part = pl.ds(k * piece, piece)
        place = tv.at[origin(t), part]
        remote(place, place, ty_s.at[t, k], ty_r.at[t, k], {"hidden": across(t)}).wait_recv()
        copy = remote(place, place, tf_s.at[t, k], tf_r.at[t, k], {"hidden": mate})
        copy.start()
        sends.append(copy)

    todo = [(t, k) for k in range(chunks) for t in range(1, far)]
    third = -(-len(todo) // 4)

    def pass_some():
        for _ in range(min(third, len(todo))):
            pass_on(*todo.pop(0))

    pick = (iota((width, model), 1) == iota((width, model), 0) + h * width).astype(BF)
    for n in range(3):
        w_loads[n].wait()
        w_t[n * width : (n + 1) * width, :] = mm_nt(pick, wv[n]).astype(BF)
        if n == 1:
            pass_some()
    save_w = pltpu.make_async_copy(w_t, w_t_out, save_sem.at[0])
    save_w.start()

    def project(source):
        def one(b, _):
            normed, _unused = norm_parts(tv[source, aligned(b * BLOCK, BLOCK), :].astype(F32))
            hidden = (normed * lying(g1) + lying(s1)).astype(BF)
            block = mm_nt(w_t[...], hidden)
            cols = aligned(source * rows + b * BLOCK, BLOCK)
            qkv[:, cols] = block.astype(BF)
            for n in range(heads):
                lo = width + n * HEAD_DIM
                keys[n, cols, :] = block[lo : lo + HEAD_DIM].T.astype(BF)
            return 0

        lax.fori_loop(0, per_device, one, 0)

    pass_some()
    own_tokens.wait()
    project(h)
    pass_some()
    remote(tokens, tv.at[mate], tc_s, tc_r, {"hidden": mate}).wait_recv()
    project(mate)
    while todo:
        pass_some()

    deep = w_up.shape[1] // 2

    def up_part(k):
        return pl.ds(k * deep, deep)

    def up_across(k):
        for t in range(1, far):
            copy = remote(
                w_up.at[0, up_part(k)],
                ups.at[h, up_part(k)],
                wy_s.at[t, k],
                wy_r.at[t, k],
                {"hidden": across(t)},
            )
            copy.start()
            sends.append(copy)

    def up_onward(k):
        for t in range(1, far):
            place = ups.at[origin(t), up_part(k)]
            remote(place, place, wy_s.at[t, k], wy_r.at[t, k], {"hidden": mate}).wait_recv()
            copy = remote(place, place, wf_s.at[t, k], wf_r.at[t, k], {"hidden": mate})
            copy.start()
            sends.append(copy)

    own_up = pltpu.make_async_copy(w_up.at[0], ups.at[h], own_sem.at[2])
    own_up.start()
    up_beside = remote(w_up.at[0], ups.at[h], wc_s, wc_r, {"hidden": mate})
    up_beside.start()
    sends.append(up_beside)
    up_across(0)
    for t in range(1, far):
        project(origin(t))
    for t in range(1, far):
        there = lax.rem(pair + far - t, far) * 2 + 1 - core
        for k in range(chunks):
            place = tv.at[there, pl.ds(k * piece, piece)]
            remote(place, place, tf_s.at[t, k], tf_r.at[t, k], {"hidden": mate}).wait_recv()
        project(there)
    save_tokens = pltpu.make_async_copy(tv, all_tokens, save_sem.at[1])
    save_qkv = pltpu.make_async_copy(qkv, qkv_out, save_sem.at[2])
    save_tokens.start()
    save_qkv.start()

    inverse[...] = jnp.zeros_like(inverse)

    def device_at(n, sign):
        t, other = n // 2, lax.rem(n, 2)
        return lax.rem(pair + far + sign * t, far) * 2 + lax.rem(core + other, 2)

    def give_att(n):
        owner = device_at(n, 1)
        return remote(
            att_v.at[owner], att_in.at[h], at_s.at[n], at_r.at[n], {"hidden": owner}
        )

    def save_kept(i, turn):
        return pltpu.make_async_copy(kept.at[turn], weights.at[i], kept_sem.at[turn])

    def attend(at, _):
        n = n_h - 1 - at // per_device
        b = lax.rem(at, per_device)
        owner = device_at(n, 1)
        i = owner * per_device + b
        turn = lax.rem(at, 2)

        @pl.when(at >= 2)
        def _free():
            save_kept(i, turn).wait()

        def block(span, first):
            done = attend_block(
                heads, ends, i, span, first, qkv, keys, scores, kept.at[turn], inverse
            )
            for m in range(heads):
                lo = m * HEAD_DIM
                att_v[owner, lo : lo + HEAD_DIM, aligned(b * BLOCK, BLOCK)] = done[m]

        spans(i, block)
        save_kept(i, turn).start()

        @pl.when((b == per_device - 1) & (n > 0))
        def _give():
            give_att(n).start()

        return 0

    lax.fori_loop(0, n_h * per_device, attend, 0)
    up_onward(0)
    att_in[h] = att_v[h]
    save_att = pltpu.make_async_copy(att_v, att_out, save_sem.at[3])
    save_att.start()
    for n in range(n_h - 1, 0, -1):
        give_att(n).wait_recv()
    save_att_t = pltpu.make_async_copy(att_in, att_t_out, save_sem.at[4])
    save_att_t.start()

    up_across(1)

    w_loads[3].wait()
    res = tv[h].astype(F32) + mm_tn(att_in[...].reshape(model, rows), wo[...])
    residual[...] = res
    normed, _unused = norm_parts(res)
    hidden = (normed * lying(g2) + lying(s2)).astype(BF)
    fill_slots(flat_t, hidden, xs_v)
    save_x = [
        pltpu.make_async_copy(
            xs_v.at[pl.ds(n * capacity, capacity)], x_slots.at[n], save_sem.at[5 + n]
        )
        for n in range(experts)
    ]
    for save in save_x:
        save.start()
    logits = mm_nt(hidden, w_router[...])
    lane = iota((rows, experts), 1)
    chosen = [
        jnp.sum(jnp.where(lane == ids[:, j : j + 1], logits, 0.0), axis=1, keepdims=True)
        for j in range(2)
    ]
    top = jnp.maximum(chosen[0], chosen[1])
    raised = [jnp.exp(c - top) for c in chosen]
    both = raised[0] + raised[1]
    gate = [r / both for r in raised]
    for j in range(2):
        gates[:, j : j + 1] = gate[j]
    column = iota((rows, padded), 1)
    for n in range(experts):
        mix = jnp.zeros((rows, padded), F32)
        for j in range(2):
            here = jnp.where(ids[:, j : j + 1] == n, slot[:, j : j + 1], -1) == column
            mix = jnp.where(here, gate[j], mix)
        line = jnp.sum(mix, axis=0, keepdims=True)
        gate_rows[n] = jnp.broadcast_to(line, (8, padded))

    up_onward(1)
    place = ups.at[mate]
    remote(place, place, wc_s, wc_r, {"hidden": mate}).wait_recv()
    for k in range(2):
        for t in range(1, far):
            there = lax.rem(pair + far - t, far) * 2 + 1 - core
            place = ups.at[there, up_part(k)]
            remote(place, place, wf_s.at[t, k], wf_r.at[t, k], {"hidden": mate}).wait_recv()
    own_up.wait()
    for step in range(1, n_e):
        source = lax.rem(e + n_e - step, n_e)
        place = g_in.at[source]
        remote(place, place, gs_s.at[step], gs_r.at[step], {"expert": e}).wait_recv()
    own_slots.wait()
    for n in range(1, n_h):
        give_att(n).wait_send()
    for turn in range(2):
        save_kept(0, turn).wait()
    for copy in sends:
        copy.wait_send()
    for save in [save_w, save_tokens, save_qkv, save_att, save_att_t, *save_x]:
        save.wait()


def run_front(
    docs, ids_t, g1, s1, g2, s2, w_router, tokens, out_grad, ws, w_up, capacity, heads, cid
):
    n_e, n_h = lax.axis_size("expert"), lax.axis_size("hidden")
    experts = n_e * w_up.shape[0]
    rows, model = tokens.shape
    padded = -(-capacity // LANES) * LANES
    width, group, total = heads * HEAD_DIM, rows * n_h, experts * capacity
    far, chunks = n_h // 2, 8

    def pairs(*shape):
        return [DMA(shape), DMA(shape)]

    return pl.pallas_call(
        partial(front_body, n_e, n_h, experts, capacity, padded, heads, chunks),
        name="front",
        out_shape=[
            shape_of((n_h, rows, model), BF),
            shape_of((3 * width, group), BF),
            shape_of((n_h, width, rows), BF),
            shape_of((n_h, width, rows), BF),
            shape_of((3 * width, model), BF),
            shape_of((experts, capacity, model), BF),
            shape_of((experts, capacity, model), BF),
            shape_of((n_h, *w_up.shape[1:]), BF),
            shape_of((group // BLOCK, heads, REACH, BLOCK, BLOCK), BF),
            shape_of((rows, 2), I32),
            shape_of((rows, 2), I32),
            shape_of((rows, 2), I32),
            shape_of((1, LANES), F32),
            shape_of((8, group), F32),
            shape_of((rows, model), F32),
            shape_of((rows, 2), F32),
            shape_of((experts, 8, padded), F32),
        ],
        in_specs=[SMEM] + [VMEM] * 6 + [ANY] * 7,
        out_specs=[ANY] * 9 + [VMEM] * 8,
        scratch_shapes=[
            pltpu.VMEM((n_h, rows, model), BF),
            pltpu.VMEM((rows, model), BF),
            pltpu.VMEM((3, model, model), BF),
            pltpu.VMEM((model, model), BF),
            pltpu.VMEM((3 * width, model), BF),
            pltpu.VMEM((3 * width, group), BF),
            pltpu.VMEM((heads, group, HEAD_DIM), BF),
            pltpu.VMEM((heads, REACH, BLOCK, BLOCK), F32),
            pltpu.VMEM((2, heads, REACH, BLOCK, BLOCK), BF),
            pltpu.VMEM((n_h, width, rows), BF),
            pltpu.VMEM((n_h, width, rows), BF),
            pltpu.VMEM((total, model), BF),
            pltpu.VMEM((total, model), BF),
            DMA((4,)),
            DMA((4,)),
            DMA((5 + experts,)),
            DMA((2,)),
            *pairs(far, chunks),
            DMA,
            DMA,
            *pairs(far, chunks),
            *pairs(n_e),
            *pairs(n_h),
            *pairs(far, 2),
            DMA,
            DMA,
            *pairs(far, 2),
        ],
        compiler_params=pltpu.CompilerParams(
            collective_id=cid, has_side_effects=True, vmem_limit_bytes=58 << 20
        ),
    )(docs, ids_t, g1, s1, g2, s2, w_router, tokens, out_grad, *ws, w_up)


def moe_body(
    size,
    capacity,
    padded,
    per,
    x_slots,
    gate_rows,
    g_in,
    ups,
    w_down,
    dx_back,
    dg_back,
    y_out,
    dw_sum,
    dw_far,
    xv,
    gv,
    gates_v,
    up_v,
    down_v,
    act,
    dz,
    xg,
    dy,
    xg_t,
    dy_t,
    dxv,
    yv,
    dgv,
    y_acc,
    dx_acc,
    dw_box,
    load_sem,
    save_sem,
    wy_s,
    wy_r,
    wc_s,
    wc_r,
    wf_s,
    wf_r,
    dc_s,
    dc_r,
    df_s,
    df_r,
    g_sem,
    own_sem,
    xs_sem,
    xr_sem,
    gs_sem,
    gr_sem,
    ds_sem,
    dr_sem,
    ts_sem,
    tr_sem,
    out_sem,
):
    me, h = lax.axis_index("expert"), lax.axis_index("hidden")
    shards_n = ups.shape[0]
    far = shards_n // 2
    pair, core = h // 2, lax.rem(h, 2)
    mate = pair * 2 + 1 - core
    deep = w_down.shape[1] // 2
    tall = per * capacity
    steps = size // per

    def to_peer(p):
        return lax.rem(me + 3 * p, size)

    def from_peer(p):
        return lax.rem(me + 3 * (size - p), size)

    def rows_of(p):
        return pl.ds(pl.multiple_of(p * capacity, capacity), capacity)

    def send_x(p):
        peer = to_peer(p)
        return remote(
            x_slots.at[peer], xv.at[rows_of(p)], xs_sem.at[p], xr_sem.at[p], {"expert": peer}
        )

    def send_gate(p):
        peer = to_peer(p)
        return remote(
            gate_rows.at[peer], gates_v.at[p], gs_sem.at[p], gr_sem.at[p], {"expert": peer}
        )

    def send_dx(p):
        peer = from_peer(p)
        return remote(
            dxv.at[rows_of(p)], dx_back.at[me], ds_sem.at[p], dr_sem.at[p], {"expert": peer}
        )

    def send_dg(p):
        peer = from_peer(p)
        return remote(dgv.at[p], dg_back.at[me], ts_sem.at[p], tr_sem.at[p], {"expert": peer})

    def load_g(p):
        return pltpu.make_async_copy(g_in.at[from_peer(p)], gv.at[rows_of(p)], g_sem.at[p])

    def save_y(p):
        return pltpu.make_async_copy(yv.at[rows_of(p)], y_out.at[from_peer(p)], out_sem.at[p])

    own_x = pltpu.make_async_copy(x_slots.at[me], xv.at[rows_of(0)], own_sem.at[0])
    own_gate = pltpu.make_async_copy(gate_rows.at[me], gates_v.at[0], own_sem.at[1])
    own_dx = pltpu.make_async_copy(dxv.at[rows_of(0)], dx_back.at[me], own_sem.at[2])
    own_dg = pltpu.make_async_copy(dgv.at[0], dg_back.at[me], own_sem.at[3])
    load_up = pltpu.make_async_copy(ups, up_v, load_sem.at[0])
    load_down = pltpu.make_async_copy(w_down.at[0], down_v.at[h], load_sem.at[1])

    def half(k):
        return aligned(k * deep, deep)

    def down_across(t, k):
        there = {"hidden": lax.rem(pair + t, far) * 2 + core}
        return remote(
            w_down.at[0, half(k)], down_v.at[h, half(k)], wy_s.at[t, k], wy_r.at[t, k], there
        )

    def down_onward(t, k):
        place = down_v.at[lax.rem(pair + far - t, far) * 2 + core, half(k)]
        return remote(place, place, wf_s.at[t, k], wf_r.at[t, k], {"hidden": mate})

    down_beside = remote(w_down.at[0], down_v.at[h], wc_s, wc_r, {"hidden": mate})
    own_x.start()
    own_gate.start()
    for p in range(size):
        load_g(p).start()
    load_up.start()
    load_down.start()
    greet(
        [{"expert": lax.rem(me + step, size)} for step in range(1, size)]
        + [{"hidden": lax.rem(h + step, shards_n)} for step in range(1, shards_n)]
    )
    for p in range(1, size):
        send_x(p).start()
        send_gate(p).start()
    for k in range(2):
        for t in range(1, far):
            down_across(t, k).start()
    down_beside.start()
    own_x.wait()
    own_gate.wait()
    load_up.wait()
    load_down.wait()

    def step_body(step, _):
        base = step * per
        for s in range(per):

            @pl.when(base + s > 0)
            def _arrive(s=s):
                send_x(base + s).wait_recv()
                send_gate(base + s).wait_recv()

            load_g(base + s).wait()
        rows = pl.ds(pl.multiple_of(step * tall, tall), tall)
        x, g = xv[rows, :], gv[rows, :]
        y_acc[...] = jnp.zeros_like(y_acc)
        dx_acc[...] = jnp.zeros_like(dx_acc)

        def shard_body(n, _):
            t = n // 2
            beside = lax.rem(n, 2)
            c = lax.rem(pair + far - t, far) * 2 + lax.rem(core + beside, 2)

            @pl.when((step == 0) & (n == 1))
            def _beside():
                down_beside.wait_recv()

            @pl.when((step == 0) & (n >= 2) & (beside == 0))
            def _across():
                for k in range(2):
                    down_across(t, k).wait_recv()
                    down_onward(t, k).start()

            @pl.when((step == 0) & (n >= 2) & (beside == 1))
            def _onward():
                for k in range(2):
                    down_onward(t, k).wait_recv()

            z = mm(x, up_v[c])
            du = mm_nt(g, down_v[c])
            square = z * z
            curve = jnp.tanh(z * (GELU_A + GELU_A * GELU_B * square))
            plus = 0.5 + 0.5 * curve
            hidden = (z * plus).astype(BF)
            rise = GELU_A + 3.0 * GELU_A * GELU_B * square
            slope = plus + 0.5 * z * (1.0 - curve * curve) * rise
            back = (slope * du).astype(BF)
            act[c, rows, :] = hidden
            dz[c, rows, :] = back
            y_acc[...] += mm(hidden, down_v[c])
            dx_acc[...] += mm_nt(back, up_v[c])
            return 0

        lax.fori_loop(0, shards_n, shard_body, 0)
        dxv[rows, :] = dx_acc[...].astype(BF)
        y_low = y_acc[...].astype(BF)
        yv[rows, :] = y_low
        dots = jnp.sum(y_low.astype(F32) * g.astype(F32), axis=1, keepdims=True)
        for s in range(per):
            p = base + s
            part = slice(s * capacity, (s + 1) * capacity)
            tall_dots = jnp.broadcast_to(dots[part], (capacity, LANES))
            if padded > capacity:
                blank = jnp.zeros((padded - capacity, LANES), F32)
                tall_dots = jnp.concatenate([tall_dots, blank], axis=0)
            dgv[p] = tall_dots.T[0:8]

            @pl.when(p > 0)
            def _give(p=p):
                send_dx(p).start()
                send_dg(p).start()

            @pl.when(p == 0)
            def _keep():
                own_dx.start()
                own_dg.start()

            save_y(p).start()
        for s in range(per):
            p = base + s
            part = slice(s * capacity, (s + 1) * capacity)
            gate = gates_v[p].T[0:capacity, 0:1]
            xg[rows_of(p), :] = (x[part].astype(F32) * gate).astype(BF)
            dy[rows_of(p), :] = (g[part].astype(F32) * gate).astype(BF)
        return 0

    lax.fori_loop(0, steps, step_body, 0)

    total = size * capacity
    turn = 256
    for k in range(total // turn):
        rows = slice(k * turn, (k + 1) * turn)
        xg_t[:, rows] = xg[rows, :].astype(F32).T.astype(BF)
        dy_t[:, rows] = dy[rows, :].astype(F32).T.astype(BF)
    model = xg_t.shape[0]
    bands = model // turn

    for t in range(1, far):
        for k in range(2):
            down_across(t, k).wait_send()
            down_onward(t, k).wait_send()
    down_beside.wait_send()

    def give(which, step):
        source = (up_v, down_v)[which].at[lax.rem(pair + step, far) * 2 + 1 - core]
        return remote(
            source,
            dw_box.at[which, step],
            dc_s.at[which, step],
            dc_r.at[which, step],
            {"hidden": mate},
        )

    def keep(which, step):
        source = (up_v, down_v)[which].at[lax.rem(pair + step, far) * 2 + core]
        return pltpu.make_async_copy(source, dw_sum.at[which, step], save_sem.at[which, step])

    def cross(step):
        source = up_v.at[lax.rem(pair + step, far) * 2 + core, half(0)]
        there = {"hidden": lax.rem(pair + step, far) * 2 + core}
        return remote(source, dw_far.at[step - 1], df_s.at[step], df_r.at[step], there)

    def other_body(n, _):
        band, step = lax.rem(n, bands), lax.rem(n // bands + 1, far)
        c = lax.rem(pair + step, far) * 2 + 1 - core
        lines = aligned(band * turn, turn)
        up_v[c, lines, :] = mm(xg_t[lines, :], dz[c]).astype(BF)
        down_v[c, lines, :] = mm(dy_t[lines, :], act[c]).astype(BF)

        @pl.when(band == bands - 1)
        def _give():
            for which in range(2):
                give(which, step).start()

        return 0

    lax.fori_loop(0, far * bands, other_body, 0)

    def own_body(n, _):
        band, step = lax.rem(n, bands), lax.rem(n // bands + 1, far)
        c = lax.rem(pair + step, far) * 2 + core

        @pl.when(band == 0)
        def _take():
            for which in range(2):
                give(which, step).wait_recv()

        lines = aligned(band * turn, turn)
        up = mm(xg_t[lines, :], dz[c]) + dw_box[0, step, lines, :].astype(F32)
        down = mm(dy_t[lines, :], act[c]) + dw_box[1, step, lines, :].astype(F32)
        up_v[c, lines, :] = up.astype(BF)
        down_v[c, lines, :] = down.astype(BF)

        @pl.when(band == bands - 1)
        def _keep():
            for which in range(2):
                keep(which, step).start()

        @pl.when((band == bands - 1) & (step > 0))
        def _cross():
            cross(step).start()

        return 0

    lax.fori_loop(0, far * bands, own_body, 0)
    for p in range(1, size):
        send_x(p).wait_send()
        send_gate(p).wait_send()
        send_dx(p).wait()
        send_dg(p).wait()
    for p in range(size):
        save_y(p).wait()
    own_dx.wait()
    own_dg.wait()
    for step in range(far):
        for which in range(2):
            give(which, step).wait_send()
            keep(which, step).wait()
    for step in range(1, far):
        cross(step).wait()


def run_experts(x_slots, gate_rows, g_in, ups, w_down, cid):
    size = lax.axis_size("expert")
    experts, capacity, model = x_slots.shape
    padded = gate_rows.shape[2]
    shards_n, _unused, width = ups.shape
    total = experts * capacity
    per = 1
    while per * 2 * capacity <= 320 and size % (per * 2) == 0:
        per *= 2
    tall = per * capacity
    rows2 = (total, model)
    return pl.pallas_call(
        partial(moe_body, size, capacity, padded, per),
        name="experts",
        out_shape=[
            shape_of(x_slots.shape, BF),
            shape_of(gate_rows.shape, F32),
            shape_of(x_slots.shape, BF),
            shape_of((2, shards_n // 2, model, width), BF),
            shape_of((shards_n // 2 - 1, model // 2, width), BF),
        ],
        in_specs=[ANY] * 5,
        out_specs=[ANY] * 5,
        scratch_shapes=[
            pltpu.VMEM(rows2, BF),
            pltpu.VMEM(rows2, BF),
            pltpu.VMEM(gate_rows.shape, F32),
            pltpu.VMEM((shards_n, model, width), BF),
            pltpu.VMEM((shards_n, width, model), BF),
            pltpu.VMEM((shards_n, total, width), BF),
            pltpu.VMEM((shards_n, total, width), BF),
            pltpu.VMEM(rows2, BF),
            pltpu.VMEM(rows2, BF),
            pltpu.VMEM((model, total), BF),
            pltpu.VMEM((model, total), BF),
            pltpu.VMEM(rows2, BF),
            pltpu.VMEM(rows2, BF),
            pltpu.VMEM(gate_rows.shape, F32),
            pltpu.VMEM((tall, model), F32),
            pltpu.VMEM((tall, model), F32),
            pltpu.VMEM((2, shards_n // 2, model, width), BF),
            DMA((2,)),
            DMA((2, shards_n // 2)),
            DMA((shards_n // 2, 2)),
            DMA((shards_n // 2, 2)),
            DMA,
            DMA,
            DMA((shards_n // 2, 2)),
            DMA((shards_n // 2, 2)),
            DMA((2, shards_n // 2)),
            DMA((2, shards_n // 2)),
            DMA((shards_n // 2,)),
            DMA((shards_n // 2,)),
            DMA((size,)),
            DMA((4,)),
        ]
        + [DMA((size,))] * 9,
        compiler_params=pltpu.CompilerParams(
            collective_id=cid, has_side_effects=True, vmem_limit_bytes=60 << 20
        ),
        cost_estimate=pl.CostEstimate(
            flops=12 * total * model * width * shards_n, bytes_accessed=40 << 20, transcendentals=0
        ),
    )(x_slots, gate_rows, g_in, ups, w_down)


def tail_body(
    n_e,
    n_h,
    chunks,
    dh,
    w_all,
    small,
    tokens,
    gain,
    d_res,
    residual,
    gates,
    pos,
    y_back,
    input_grad,
    output,
    full,
    total,
    mine,
    beside,
    across,
    passing,
    x_box,
    z_box,
    w_mid,
    piece,
    small_mid,
    small_h,
    small_e,
    mine_sem,
    cs_sem,
    cr_sem,
    as_sem,
    ar_sem,
    ws_sem,
    wr_sem,
    vs_sem,
    vr_sem,
    hs_sem,
    hr_sem,
    es_sem,
    er_sem,
    keep_sem,
    zs_sem,
    zr_sem,
    xs_sem,
    xr_sem,
    ys_sem,
    yr_sem,
    ms_sem,
    mr_sem,
):
    e, h = lax.axis_index("expert"), lax.axis_index("hidden")
    far, high = n_h // 2, n_e // 2
    pair, core = h // 2, lax.rem(h, 2)
    eh, el = e // 2, lax.rem(e, 2)
    mate = pair * 2 + 1 - core
    greet(
        [{"expert": lax.rem(e + step, n_e)} for step in range(1, n_e)]
        + [{"hidden": lax.rem(h + step, n_h)} for step in range(1, n_h)]
    )
    w_sends, w_order = [], list(range(1, high)) + [0]
    for step in w_order:
        there = lax.rem(eh + step, high)
        copy = remote(
            w_all.at[there * 2 + 1 - el],
            x_box.at[step],
            ws_sem.at[step],
            wr_sem.at[step],
            {"expert": eh * 2 + 1 - el},
        )
        copy.start()
        w_sends.append(copy)
    rows = dh.shape[1] // chunks
    core_sends = {}
    for step in list(range(1, far)) + [0]:
        there = lax.rem(pair + step, far)
        for k in range(chunks):
            part = pl.ds(k * rows, rows)
            copy = remote(
                dh.at[there * 2 + 1 - core, part],
                beside.at[step, part],
                cs_sem.at[step, k],
                cr_sem.at[step, k],
                {"hidden": mate},
            )
            copy.start()
            core_sends[step, k] = copy
    loads = []
    for step in range(far):
        there = lax.rem(pair + step, far)
        load = pltpu.make_async_copy(dh.at[there * 2 + core], mine.at[step], mine_sem.at[step])
        load.start()
        loads.append(load)
    small_sends = []
    for at in range(n_h - 1):
        peer = lax.rem(h + 1 + at, n_h)
        copy = remote(small, small_h.at[at], hs_sem.at[at], hr_sem.at[at], {"hidden": peer})
        copy.start()
        small_sends.append(copy)
    v_sends = []
    for at, step in enumerate(w_order[:-1]):
        there = lax.rem(eh + step, high) * 2 + el
        w_sends[at].wait_recv()
        w_mid[step - 1] = (w_all[there].astype(F32) + x_box[step].astype(F32)).astype(BF)
        copy = remote(
            w_mid.at[step - 1],
            z_box.at[step - 1],
            vs_sem.at[step],
            vr_sem.at[step],
            {"expert": there},
        )
        copy.start()
        v_sends.append(copy)
    for load in loads:
        load.wait()
    far_sends = []
    for step in range(1, far):
        there = lax.rem(pair + step, far)
        for k in range(chunks):
            part = pl.ds(k * rows, rows)
            core_sends[step, k].wait_recv()
            both = mine[step, part, :].astype(F32) + beside[step, part, :].astype(F32)
            passing[step - 1, part, :] = both.astype(BF)
            copy = remote(
                passing.at[step - 1, part],
                across.at[step - 1, part],
                as_sem.at[step - 1, k],
                ar_sem.at[step - 1, k],
                {"hidden": there * 2 + core},
            )
            copy.start()
            far_sends.append(copy)
    for copy in small_sends:
        copy.wait_recv()
    summed = small[...]
    for at in range(n_h - 1):
        summed = summed + small_h[at]
    small_mid[...] = summed
    small_out = []
    for at in range(n_e - 1):
        peer = lax.rem(e + 1 + at, n_e)
        copy = remote(small_mid, small_e.at[at], es_sem.at[at], er_sem.at[at], {"expert": peer})
        copy.start()
        small_out.append(copy)
    w_sends[-1].wait_recv()
    acc = w_all[e].astype(F32) + x_box[0].astype(F32)
    for at, copy in enumerate(v_sends):
        copy.wait_recv()
        acc = acc + z_box[at].astype(F32)
    piece[...] = acc.astype(BF)
    keep = pltpu.make_async_copy(piece, full.at[h, e], keep_sem)
    keep.start()
    started = []

    def slot(eh_of, el_of, pair_of, core_of):
        return full.at[pair_of * 2 + core_of, eh_of * 2 + el_of]

    def back(step, size, place):
        return lax.rem(place + size - step, size)

    def give_z(source):
        for s in range(1, high):
            there = lax.rem(eh + s, high) * 2 + el
            copy = remote(
                source, slot(eh, el, pair, core), zs_sem.at[s], zr_sem.at[s], {"expert": there}
            )
            copy.start()
            started.append(copy)

    def z_arrival(s):
        place = slot(back(s, high, eh), el, pair, core)
        return place, remote(place, place, zs_sem.at[s], zr_sem.at[s], {"expert": e})

    def give_x(source, s):
        target = slot(back(s, high, eh), el, pair, core)
        copy = remote(
            source, target, xs_sem.at[s], xr_sem.at[s], {"expert": eh * 2 + 1 - el}
        )
        copy.start()
        started.append(copy)

    def x_arrival(s):
        place = slot(back(s, high, eh), 1 - el, pair, core)
        return place, remote(place, place, xs_sem.at[s], xr_sem.at[s], {"expert": e})

    def give_y(source, s, flag):
        target = slot(back(s, high, eh), el if flag == 0 else 1 - el, pair, core)
        for t in range(1, far):
            there = lax.rem(pair + t, far) * 2 + core
            at = 2 * s + flag
            copy = remote(
                source, target, ys_sem.at[t, at], yr_sem.at[t, at], {"hidden": there}
            )
            copy.start()
            started.append(copy)

    def y_arrival(t, s, flag):
        other = el if flag == 0 else 1 - el
        place = slot(back(s, high, eh), other, back(t, far, pair), core)
        at = 2 * s + flag
        return place, remote(place, place, ys_sem.at[t, at], yr_sem.at[t, at], {"hidden": h})

    def give_mate(source, t, s, flag):
        other = el if flag == 0 else 1 - el
        target = slot(back(s, high, eh), other, back(t, far, pair), core)
        at = 2 * s + flag
        copy = remote(source, target, ms_sem.at[t, at], mr_sem.at[t, at], {"hidden": mate})
        copy.start()
        started.append(copy)

    def mate_arrival(t, s, flag):
        other = el if flag == 0 else 1 - el
        place = slot(back(s, high, eh), other, back(t, far, pair), 1 - core)
        at = 2 * s + flag
        return place, remote(place, place, ms_sem.at[t, at], mr_sem.at[t, at], {"hidden": h})

    give_z(piece)
    give_x(piece, 0)
    give_y(piece, 0, 0)
    give_mate(piece, 0, 0, 0)
    for s in range(1, high):
        place, arrival = z_arrival(s)
        arrival.wait_recv()
        give_x(place, s)
        give_y(place, s, 0)
        give_mate(place, 0, s, 0)
    for s in range(high):
        place, arrival = x_arrival(s)
        arrival.wait_recv()
        give_y(place, s, 1)
        give_mate(place, 0, s, 1)
    place_of = iota((residual.shape[0], y_back.shape[0]), 1)
    result = residual[...]
    for j in range(2):
        pick = (place_of == pos[:, j : j + 1]).astype(BF)
        result = result + gates[:, j : j + 1] * mm(pick, y_back[...])
    output[...] = result.astype(BF)
    for copy in small_out:
        copy.wait_recv()
    summed = small_mid[...]
    for at in range(n_e - 1):
        summed = summed + small_e[at]
    total[...] = summed
    for k in range(chunks):
        part = pl.ds(k * rows, rows)
        core_sends[0, k].wait_recv()
    for copy in far_sends:
        copy.wait_recv()
    grad = mine[0].astype(F32) + beside[0].astype(F32)
    for step in range(far - 1):
        grad = grad + across[step].astype(F32)
    normed, inverse = norm_parts(tokens[...].astype(F32))
    input_grad[...] = (d_res[...] + norm_back(grad, normed, inverse, lying(gain))).astype(BF)
    for t in range(1, far):
        for s in range(high):
            for flag in range(2):
                place, arrival = y_arrival(t, s, flag)
                arrival.wait_recv()
                give_mate(place, t, s, flag)
    for t in range(far):
        for s in range(high):
            for flag in range(2):
                _place, arrival = mate_arrival(t, s, flag)
                arrival.wait_recv()
    keep.wait()
    for copy in started + w_sends + v_sends + small_sends + small_out + far_sends:
        copy.wait_send()
    for copy in core_sends.values():
        copy.wait_send()


def run_tail(dh, w_all, small, tokens, gain, d_res, residual, gates, pos, y_back, cid):
    n_e, n_h = lax.axis_size("expert"), lax.axis_size("hidden")
    far, high = n_h // 2, n_e // 2
    chunks = 4
    _unused, rows, model = dh.shape
    piece = w_all.shape[1:]
    return pl.pallas_call(
        partial(tail_body, n_e, n_h, chunks),
        name="tail",
        out_shape=[
            shape_of((rows, model), BF),
            shape_of((rows, model), BF),
            shape_of((n_h, n_e, *piece), BF),
            shape_of(small.shape, F32),
        ],
        in_specs=[ANY] + [VMEM] * 9,
        out_specs=[VMEM, VMEM, ANY, VMEM],
        scratch_shapes=[
            pltpu.VMEM((far, rows, model), BF),
            pltpu.VMEM((far, rows, model), BF),
            pltpu.VMEM((far - 1, rows, model), BF),
            pltpu.VMEM((far - 1, rows, model), BF),
            pltpu.VMEM((high, *piece), BF),
            pltpu.VMEM((high - 1, *piece), BF),
            pltpu.VMEM((high - 1, *piece), BF),
            pltpu.VMEM(piece, BF),
            pltpu.VMEM(small.shape, F32),
            pltpu.VMEM((n_h - 1, *small.shape), F32),
            pltpu.VMEM((n_e - 1, *small.shape), F32),
            DMA((far,)),
            DMA((far, chunks)),
            DMA((far, chunks)),
            DMA((far - 1, chunks)),
            DMA((far - 1, chunks)),
            DMA((high,)),
            DMA((high,)),
            DMA((high,)),
            DMA((high,)),
            DMA((n_h - 1,)),
            DMA((n_h - 1,)),
            DMA((n_e - 1,)),
            DMA((n_e - 1,)),
            DMA,
            DMA((high,)),
            DMA((high,)),
            DMA((high,)),
            DMA((high,)),
            DMA((far, n_e)),
            DMA((far, n_e)),
            DMA((far, n_e)),
            DMA((far, n_e)),
        ],
        compiler_params=pltpu.CompilerParams(
            collective_id=cid, has_side_effects=True, vmem_limit_bytes=56 << 20
        ),
    )(dh, w_all, small, tokens, gain, d_res, residual, gates, pos, y_back)


def turn_body(
    width,
    experts,
    full,
    dw,
    small,
    input_grad,
    output,
    q_out,
    k_out,
    v_out,
    o_out,
    up_out,
    down_out,
    g1_out,
    s1_out,
    g2_out,
    s2_out,
    router_out,
    input_out,
    output_out,
):
    @pl.when(pl.program_id(0) == 0)
    def _begin():
        input_out[...] = input_grad[...]
        output_out[...] = output[...]
        for n, out in enumerate((g1_out, s1_out, g2_out, s2_out)):
            out[...] = small[n : n + 1, :].reshape(out.shape)
        router_out[...] = small[8 : 8 + experts, :]

    for n, out in enumerate((q_out, k_out, v_out)):
        part = full[:, n * width : (n + 1) * width, :].astype(F32)
        out[...] = part.reshape(-1, part.shape[2]).T
    part = full[:, 3 * width :, :].astype(F32)
    o_out[...] = part.reshape(-1, part.shape[2])
    trained = jnp.where(lax.axis_index("expert") >= experts // 2, 1.0, 0.0)
    up_out[...] = dw[0] * trained
    down_out[...] = dw[1].T * trained


def turn_weights(full, dw, small, input_grad, output, width, experts):
    n_h, deep, model = full.shape
    cols = 256
    across = pl.BlockSpec((cols, model), lambda i: (i, 0))
    down = pl.BlockSpec((model, cols), lambda i: (0, i))
    flat = pl.BlockSpec((model,), lambda i: (0,))
    whole = pl.BlockSpec(output.shape, lambda i: (0, 0))
    square = shape_of((model, model), F32)
    return pl.pallas_call(
        partial(turn_body, width, experts),
        name="turn_weights",
        grid=(model // cols,),
        out_shape=[square] * 6
        + [shape_of((model,), F32)] * 4
        + [
            shape_of((experts, model), F32),
            shape_of(input_grad.shape, BF),
            shape_of(output.shape, BF),
        ],
        in_specs=[
            pl.BlockSpec((n_h, deep, cols), lambda i: (0, 0, i)),
            pl.BlockSpec((2, model, cols), lambda i: (0, 0, i)),
            pl.BlockSpec(small.shape, lambda i: (0, 0)),
            whole,
            whole,
        ],
        out_specs=[across, across, across, down, down, across]
        + [flat] * 4
        + [pl.BlockSpec((experts, model), lambda i: (0, 0)), whole, whole],
        compiler_params=pltpu.CompilerParams(
            dimension_semantics=("arbitrary",), vmem_limit_bytes=60 << 20
        ),
        cost_estimate=pl.CostEstimate(flops=0, bytes_accessed=24 << 20, transcendentals=0),
    )(full, dw, small, input_grad, output)


def attend_back(
    heads, i, span, first, qkv, given, centre, kept, values, dq_acc, dk_acc, dv_acc
):
    width = heads * HEAD_DIM
    rows = aligned(i * BLOCK, BLOCK)
    dq_acc[...] = jnp.zeros_like(dq_acc)
    queries = [
        qkv[n * HEAD_DIM : (n + 1) * HEAD_DIM, rows] * jnp.asarray(SCALE, BF) for n in range(heads)
    ]
    for k in range(span):
        part = aligned((first + k) * BLOCK, BLOCK)
        for n in range(heads):
            here = slice(n * HEAD_DIM, (n + 1) * HEAD_DIM)
            weight = kept[n, k]
            d_weight = mm(values[n, part, :], given[n])
            d_score = (weight.astype(F32) * (d_weight - centre[n])).astype(BF)
            dv_acc[here, part] += mm_nt(given[n], weight)
            dk_acc[here, part] += mm_nt(queries[n], d_score)
            lo = width + n * HEAD_DIM
            dq_acc[here, :] += mm(qkv[lo : lo + HEAD_DIM, part], d_score)


def back_body(
    n_e,
    n_h,
    experts,
    capacity,
    padded,
    heads,
    ids,
    slot,
    pos,
    gates,
    count,
    g1,
    s1,
    g2,
    s2,
    w_router,
    inverse,
    dg_rows,
    dx_back,
    y_out,
    dw_sum,
    dw_far,
    out_grad,
    residual,
    all_tokens,
    qkv_in,
    att_in,
    att_t_in,
    w_out,
    w_t_in,
    weights,
    y_back,
    d_hidden,
    d_res,
    w_all,
    small,
    dw_own,
    dxv,
    gv,
    res_v,
    tv,
    qkv,
    att_v,
    att_t,
    wo,
    w_t,
    d_att_v,
    d_att,
    wo_box,
    wo_far,
    kept,
    values,
    dq_acc,
    dk_acc,
    dv_acc,
    d_qkv,
    w_acc,
    dw_mine,
    dw_across,
    load_sem,
    save_sem,
    dw_sem,
    kept_sem,
    y_own,
    y_s,
    y_r,
    at_s,
    at_r,
    wo_s,
    wo_r,
    wf_s,
    wf_r,
    da_s,
    da_r,
):
    e, h = lax.axis_index("expert"), lax.axis_index("hidden")
    far = n_h // 2
    pair, core = h // 2, lax.rem(h, 2)
    mate = pair * 2 + 1 - core
    rows, model = out_grad.shape
    width = heads * HEAD_DIM
    group = rows * n_h
    per_device = rows // BLOCK
    blocks = group // BLOCK
    sends = []

    loads = [
        pltpu.make_async_copy(source, target, load_sem.at[n])
        for n, (source, target) in enumerate(
            (
                (residual, res_v),
                (dx_back, dxv),
                (out_grad, gv),
                (w_out, wo),
                (att_t_in, att_t),
                (qkv_in, qkv),
                (att_in, att_v),
                (all_tokens, tv),
                (w_t_in, w_t),
            )
        )
    ]
    for load in loads:
        load.start()
    greet(
        [{"hidden": lax.rem(h + step, n_h)} for step in range(1, n_h)]
        + [{"expert": lax.rem(e + step, n_e)} for step in range(1, n_e)]
    )
    load_dw = pltpu.make_async_copy(dw_sum.at[:, 0], dw_mine, dw_sem.at[0])
    load_dw.start()
    deep = dw_mine.shape[1] // 2
    load_far = pltpu.make_async_copy(
        dw_far, dw_across.at[0, :, pl.ds(0, deep)], dw_sem.at[1]
    )
    load_far.start()

    def dw_across_copy(which, step, k):
        part = pl.ds(k * deep, deep)
        return remote(
            dw_sum.at[which, step, part],
            dw_across.at[which, step - 1, part],
            da_s.at[which, step, k],
            da_r.at[which, step, k],
            {"hidden": lax.rem(pair + step, far) * 2 + core},
        )

    def dw_send(which, k):
        for step in range(1, far):
            dw_across_copy(which, step, k).start()

    for step in range(1, n_e):
        peer = lax.rem(e + step, n_e)
        copy = remote(y_out.at[peer], y_back.at[e], y_s.at[step], y_r.at[step], {"expert": peer})
        copy.start()
        sends.append(copy)
    own_y = pltpu.make_async_copy(y_out.at[e], y_back.at[e], y_own)
    own_y.start()

    for load in loads[:3]:
        load.wait()
    normed, spread = norm_parts(res_v[...])
    hidden = (normed * lying(g2) + lying(s2)).astype(BF)
    gate = [gates[:, j : j + 1] for j in range(2)]
    column = iota((rows, padded), 1)
    dot_of = []
    for j in range(2):
        mix = jnp.zeros((rows, padded), F32)
        for n in range(experts):
            here = jnp.where(ids[:, j : j + 1] == n, slot[:, j : j + 1], -1) == column
            mix = jnp.where(here, dg_rows[n, 0:1, :], mix)
        dot_of.append(jnp.sum(mix, axis=1, keepdims=True))
    mean = gate[0] * dot_of[0] + gate[1] * dot_of[1]
    lane = iota((rows, experts), 1)
    d_logits = jnp.zeros((rows, experts), F32)
    for j in range(2):
        d_logits = jnp.where(lane == ids[:, j : j + 1], gate[j] * (dot_of[j] - mean), d_logits)
    high, low = split_two(d_logits)
    grad = mm(high, w_router[...]) + mm(low, w_router[...])
    small[...] = jnp.zeros_like(small)
    small[8 : 8 + experts, :] = mm_tn(high, hidden) + mm_tn(low, hidden)
    small[4:5, 0:LANES] = count[...]
    place = iota((rows, experts * capacity), 1)
    for j in range(2):
        pick = (place == pos[:, j : j + 1]).astype(BF)
        grad = grad + gate[j] * mm(pick, dxv[...])
    small[2:3, :] = jnp.sum(grad * normed, axis=0, keepdims=True)
    small[3:4, :] = jnp.sum(grad, axis=0, keepdims=True)
    d_resid = gv[...].astype(F32) + norm_back(grad, normed, spread, lying(g2))
    d_res[...] = d_resid
    branch = d_resid.astype(BF)
    loads[3].wait()

    def device_at(n, sign):
        t, other = n // 2, lax.rem(n, 2)
        return lax.rem(pair + far + sign * t, far) * 2 + lax.rem(core + other, 2)

    def give_att(n):
        owner = device_at(n, 1)
        return remote(
            d_att_v.at[owner], d_att.at[h], at_s.at[n], at_r.at[n], {"hidden": owner}
        )

    for n in range(n_h - 1, -1, -1):
        owner = device_at(n, 1)
        block = mm_nt(wo[owner], branch).astype(BF)
        if n == 0:
            d_att[h] = block
        else:
            d_att_v[owner] = block
            give_att(n).start()
    loads[4].wait()
    for t in range(n_h):
        owner = lax.rem(h + t, n_h)
        wo[owner] = mm(att_t[owner], branch).astype(BF)
    for step in list(range(1, far)) + [0]:
        copy = remote(
            wo.at[lax.rem(pair + step, far) * 2 + 1 - core],
            wo_box.at[step],
            wo_s.at[step],
            wo_r.at[step],
            {"hidden": mate},
        )
        copy.start()
        sends.append(copy)
    def give_wo(step):
        target = lax.rem(pair + step, far) * 2 + core
        return remote(
            wo.at[target],
            wo_far.at[step - 1],
            wf_s.at[step],
            wf_r.at[step],
            {"hidden": target},
        )

    for load in loads[5:]:
        load.wait()

    def load_kept(i, turn):
        return pltpu.make_async_copy(weights.at[i], kept.at[turn], kept_sem.at[turn])

    def block_at(at):
        owner = device_at(at // per_device, 1)
        return owner, owner * per_device + lax.rem(at, per_device)

    load_kept(block_at(0)[1], 0).start()
    dk_acc[...] = jnp.zeros_like(dk_acc)
    dv_acc[...] = jnp.zeros_like(dv_acc)

    def turn_values(i, _):
        cols = aligned(i * BLOCK, BLOCK)
        for n in range(heads):
            lo = 2 * width + n * HEAD_DIM
            values[n, cols, :] = qkv[lo : lo + HEAD_DIM, cols].astype(F32).T.astype(BF)
        return 0

    lax.fori_loop(0, blocks, turn_values, 0)

    def over_queries(at, _):
        owner, i = block_at(at)
        turn = lax.rem(at, 2)

        @pl.when(at + 1 < blocks)
        def _next():
            load_kept(block_at(at + 1)[1], 1 - turn).start()

        @pl.when((at >= per_device) & (lax.rem(at, per_device) == 0))
        def _arrive():
            n = at // per_device
            source = lax.rem(far - n // 2, far) * 2 + lax.rem(n, 2)
            give_att(source).wait_recv()

        @pl.when(at == per_device)
        def _weights():
            for step in range(1, far):
                there = wo_box.at[step]
                target = lax.rem(pair + step, far) * 2 + core
                remote(there, there, wo_s.at[step], wo_r.at[step], {"hidden": mate}).wait_recv()
                both = wo[target].astype(F32) + wo_box[step].astype(F32)
                wo[target] = both.astype(BF)
                give_wo(step).start()
            dw_send(0, 1)
            dw_send(1, 0)
            dw_send(1, 1)

        load_kept(i, turn).wait()
        cols = aligned(lax.rem(at, per_device) * BLOCK, BLOCK)
        rows_i = aligned(i * BLOCK, BLOCK)
        given, centre = [], []
        for n in range(heads):
            here = slice(n * HEAD_DIM, (n + 1) * HEAD_DIM)
            scaled = d_att[owner, here, cols].astype(F32) * inverse[n : n + 1, rows_i]
            given.append(scaled.astype(BF))
            product = att_v[owner, here, cols].astype(F32) * scaled
            centre.append(jnp.sum(product, axis=0, keepdims=True))

        def block(span, first):
            attend_back(
                heads,
                i,
                span,
                first,
                qkv,
                given,
                centre,
                kept.at[turn],
                values,
                dq_acc,
                dk_acc,
                dv_acc,
            )

        spans(i, block)
        d_qkv[0:width, rows_i] = (dq_acc[...] * SCALE).astype(BF)
        return 0

    lax.fori_loop(0, blocks, over_queries, 0)
    w_acc[...] = jnp.zeros_like(w_acc)

    def finish(i, _):
        cols = aligned(i * BLOCK, BLOCK)
        d_qkv[width : 2 * width, cols] = dk_acc[:, cols].astype(BF)
        d_qkv[2 * width :, cols] = dv_acc[:, cols].astype(BF)
        block = d_qkv[:, cols]
        grad = mm_tn(block, w_t[...])
        inner = aligned(lax.rem(i, per_device) * BLOCK, BLOCK)
        normed, _unused = norm_parts(tv[i // per_device, inner, :].astype(F32))
        tv[i // per_device, inner, :] = grad.astype(BF)
        small[0:1, :] += jnp.sum(grad * normed, axis=0, keepdims=True)
        small[1:2, :] += jnp.sum(grad, axis=0, keepdims=True)
        hidden = (normed * lying(g1) + lying(s1)).astype(BF)
        w_acc[...] += mm(block, hidden)
        return 0

    lax.fori_loop(0, blocks, finish, 0)
    save_dh = pltpu.make_async_copy(tv, d_hidden, save_sem)
    save_dh.start()
    w_all[0 : 3 * width, :] = w_acc[...].astype(BF)
    there = wo_box.at[0]
    remote(there, there, wo_s.at[0], wo_r.at[0], {"hidden": mate}).wait_recv()
    total = wo[h].astype(F32) + wo_box[0].astype(F32)
    for step in range(1, far):
        give_wo(step).wait_recv()
        total = total + wo_far[step - 1].astype(F32)
    w_all[3 * width :, :] = total.astype(BF)
    load_dw.wait()
    load_far.wait()
    for which in range(2):
        for step in range(1, far):
            for k in range(1 - which, 2):
                dw_across_copy(which, step, k).wait()

        def add_all(n, _, which=which):
            band = aligned(n * 96, 96)
            both = dw_mine[which, band, :].astype(F32)
            for step in range(1, far):
                both = both + dw_across[which, step - 1, band, :].astype(F32)
            dw_own[which, band, :] = both
            return 0

        lax.fori_loop(0, dw_mine.shape[1] // 96, add_all, 0)
    for step in range(1, n_e):
        there = y_back.at[lax.rem(e + n_e - step, n_e)]
        remote(there, there, y_s.at[step], y_r.at[step], {"expert": e}).wait_recv()
    own_y.wait()
    save_dh.wait()
    for n in range(1, n_h):
        give_att(n).wait_send()
    for step in range(1, far):
        give_wo(step).wait_send()
    for copy in sends:
        copy.wait_send()


def run_back(
    ids,
    slot,
    pos,
    gates,
    count,
    g1,
    s1,
    g2,
    s2,
    w_router,
    inverse,
    dg_rows,
    dx_back,
    y_out,
    dw_sum,
    dw_far,
    out_grad,
    residual,
    all_tokens,
    qkv,
    att,
    att_t,
    w_out,
    w_t,
    weights,
    cid,
):
    n_e, n_h = lax.axis_size("expert"), lax.axis_size("hidden")
    experts, capacity, model = y_out.shape
    padded = dg_rows.shape[2]
    rows = out_grad.shape[0]
    width = w_t.shape[0] // 3
    heads = width // HEAD_DIM
    group, far = rows * n_h, n_h // 2
    shard = dw_sum.shape[2:]
    tall = 8 + experts

    def pairs(*shape):
        return [DMA(shape), DMA(shape)]

    return pl.pallas_call(
        partial(back_body, n_e, n_h, experts, capacity, padded, heads),
        name="back",
        out_shape=[
            shape_of(y_out.shape, BF),
            shape_of((n_h, rows, model), BF),
            shape_of((rows, model), F32),
            shape_of((4 * width, model), BF),
            shape_of((tall, model), F32),
            shape_of((2, *shard), F32),
        ],
        in_specs=[VMEM] * 12 + [ANY] * 13,
        out_specs=[ANY] * 2 + [VMEM] * 4,
        scratch_shapes=[
            pltpu.VMEM((experts * capacity, model), BF),
            pltpu.VMEM((rows, model), BF),
            pltpu.VMEM((rows, model), F32),
            pltpu.VMEM((n_h, rows, model), BF),
            pltpu.VMEM((3 * width, group), BF),
            pltpu.VMEM((n_h, width, rows), BF),
            pltpu.VMEM((n_h, width, rows), BF),
            pltpu.VMEM((n_h, width, model), BF),
            pltpu.VMEM((3 * width, model), BF),
            pltpu.VMEM((n_h, width, rows), BF),
            pltpu.VMEM((n_h, width, rows), BF),
            pltpu.VMEM((far, width, model), BF),
            pltpu.VMEM((far - 1, width, model), BF),
            pltpu.VMEM((2, heads, REACH, BLOCK, BLOCK), BF),
            pltpu.VMEM((heads, group, HEAD_DIM), BF),
            pltpu.VMEM((width, BLOCK), F32),
            pltpu.VMEM((width, group), F32),
            pltpu.VMEM((width, group), F32),
            pltpu.VMEM((3 * width, group), BF),
            pltpu.VMEM((3 * width, model), F32),
            pltpu.VMEM((2, *shard), BF),
            pltpu.VMEM((2, far - 1, *shard), BF),
            DMA((9,)),
            DMA,
            DMA((2,)),
            DMA((2,)),
            DMA,
            *pairs(n_e),
            *pairs(n_h),
            *pairs(far),
            *pairs(far),
            *pairs(2, far, 2),
        ],
        compiler_params=pltpu.CompilerParams(
            collective_id=cid, has_side_effects=True, vmem_limit_bytes=60 << 20
        ),
    )(
        ids,
        slot,
        pos,
        gates,
        count,
        g1,
        s1,
        g2,
        s2,
        w_router,
        inverse,
        dg_rows,
        dx_back.reshape(experts * capacity, model),
        y_out,
        dw_sum,
        dw_far,
        out_grad,
        residual,
        all_tokens,
        qkv,
        att,
        att_t,
        w_out.reshape(n_h, width, model),
        w_t,
        weights,
    )


def shards(
    tokens,
    doc_lengths,
    expert_ids,
    gain_one,
    shift_one,
    w_query,
    w_key,
    w_value,
    w_out,
    gain_two,
    shift_two,
    w_router,
    w_up,
    w_down,
    out_grad,
):
    rows, model = tokens.shape
    n_expert, n_hidden = lax.axis_size("expert"), lax.axis_size("hidden")
    experts = n_expert * w_up.shape[0]
    capacity = max(2, rows * 2 * 5 // (4 * experts))
    capacity = -(-capacity // 16) * 16
    total = experts * capacity
    heads = HEADS // n_hidden
    width = heads * HEAD_DIM
    g1, s1, g2, s2 = gain_one, shift_one, gain_two, shift_two
    router_t = w_router.T

    (
        all_tokens,
        qkv,
        att,
        att_t,
        w_t,
        g_in,
        x_slots,
        ups,
        weights,
        ids,
        pos,
        slot,
        count,
        inverse,
        residual,
        gates,
        gate_rows,
    ) = run_front(
        doc_lengths,
        expert_ids.T,
        g1,
        s1,
        g2,
        s2,
        router_t,
        tokens,
        out_grad,
        (w_query, w_key, w_value, w_out),
        w_up,
        capacity,
        heads,
        1,
    )
    dx_back, dg_back, y_out, dw_sum, dw_far = run_experts(
        x_slots, gate_rows, g_in, ups, w_down, 2
    )
    y_back, d_hidden, d_res, w_all, small, dw_own = run_back(
        ids,
        slot,
        pos,
        gates,
        count,
        g1,
        s1,
        g2,
        s2,
        router_t,
        inverse,
        dg_back,
        dx_back,
        y_out,
        dw_sum,
        dw_far,
        out_grad,
        residual,
        all_tokens,
        qkv,
        att,
        att_t,
        w_out,
        w_t,
        weights,
        3,
    )
    input_grad, output, full, small = run_tail(
        d_hidden,
        w_all.reshape(n_expert, 4 * width // n_expert, model),
        small,
        tokens,
        g1,
        d_res,
        residual,
        gates,
        pos,
        y_back.reshape(total, model),
        4,
    )
    scale = experts / (rows * n_expert * n_hidden * 2)
    turned = turn_weights(
        full.reshape(n_hidden, 4 * width, model),
        dw_own,
        small,
        input_grad,
        output,
        width,
        experts,
    )
    w_grads, (up_grad, down_grad) = turned[:4], turned[4:6]
    gain_one_grad, shift_one_grad, gain_two_grad, shift_two_grad = turned[6:10]
    router_grad, input_grad, output = turned[10:]
    return (
        output,
        input_grad,
        gain_one_grad,
        shift_one_grad,
        *w_grads,
        gain_two_grad,
        shift_two_grad,
        router_grad.T,
        up_grad[None],
        down_grad[None],
        small[4, :experts] * scale,
    )


def solution(mesh):
    in_specs = (
        P(("expert", "hidden"), None),
        P("expert", None),
        P(("expert", "hidden"), None),
        P(),
        P(),
        P(),
        P(),
        P(),
        P(),
        P(),
        P(),
        P(),
        P("expert", None, "hidden"),
        P("expert", "hidden", None),
        P(("expert", "hidden"), None),
    )
    out_specs = (
        P(("expert", "hidden"), None),
        P(("expert", "hidden"), None),
        P(),
        P(),
        P(),
        P(),
        P(),
        P(),
        P(),
        P(),
        P(),
        P("expert", None, "hidden"),
        P("expert", "hidden", None),
        P(),
    )
    return jax.shard_map(shards, mesh=mesh, in_specs=in_specs, out_specs=out_specs, check_vma=False)
```

```python
from functools import partial

import jax
import jax.numpy as jnp
from jax import lax
from jax.experimental import pallas as pl
from jax.experimental.pallas import tpu as pltpu
from jax.sharding import PartitionSpec as P

HEAD_DIM = 64
HEADS = 12
EPSILON = 1e-05
SCALE = 0.125
MASKED = -1e30
BLOCK = 256
LONGEST = 1024
REACH = LONGEST // BLOCK + 1
LANES = 128
BF = jnp.bfloat16
F32 = jnp.float32
I32 = jnp.int32
MESH = pl.DeviceIdType.MESH
ANY = pl.BlockSpec(memory_space=pl.ANY)
SMEM = pl.BlockSpec(memory_space=pltpu.SMEM)
VMEM = pl.BlockSpec(memory_space=pltpu.VMEM)
DMA = pltpu.SemaphoreType.DMA
GELU_A = 0.7978845608028654
GELU_B = 0.044715


def mm(left, right):
    return jnp.dot(left, right, preferred_element_type=F32)


def mm_nt(left, right):
    return lax.dot_general(left, right, (((1,), (1,)), ((), ())), preferred_element_type=F32)


def mm_tn(left, right):
    return lax.dot_general(left, right, (((0,), (0,)), ((), ())), preferred_element_type=F32)


def iota(shape, axis):
    return lax.broadcasted_iota(I32, shape, axis)


def norm_parts(values):
    centred = values - jnp.mean(values, axis=-1, keepdims=True)
    inverse = lax.rsqrt(jnp.mean(centred * centred, axis=-1, keepdims=True) + EPSILON)
    return centred * inverse, inverse


def norm_back(grad_out, normed, inverse, gain):
    grad_normed = grad_out * gain
    first = jnp.mean(grad_normed, axis=-1, keepdims=True)
    second = jnp.mean(grad_normed * normed, axis=-1, keepdims=True)
    return inverse * (grad_normed - first - normed * second)


def split_two(value):
    high = value.astype(BF)
    return high, (value - high.astype(F32)).astype(BF)


def shape_of(shape, dtype):
    return jax.ShapeDtypeStruct(shape, dtype)


def greet(peers):
    barrier = pltpu.get_barrier_semaphore()
    for peer in peers:
        pl.semaphore_signal(barrier, inc=1, device_id=peer, device_id_type=MESH)
    pl.semaphore_wait(barrier, len(peers))


def remote(src, dst, send, recv, peer):
    return pltpu.make_async_remote_copy(
        src_ref=src, dst_ref=dst, send_sem=send, recv_sem=recv, device_id=peer, device_id_type=MESH
    )


def doc_bounds(docs):
    ends, at = [], 0
    for n in range(docs.shape[1] - 1):
        at = at + docs[0, n]
        ends.append(at)
    return ends


def start_of(place, ends):
    begin = jnp.zeros_like(place)
    for end in ends:
        begin = jnp.where(place >= end, end, begin)
    return begin


def lying(ref):
    return ref[...].reshape(1, ref.shape[0])


def aligned(at, size):
    return pl.ds(pl.multiple_of(at, size), size)


def find_slots(experts, capacity, ids, ids_t, pos, slot, count):
    rows = ids_t.shape[1]
    row = [ids_t[j : j + 1, :] for j in range(2)]
    tall = jnp.concatenate([r.astype(F32) for r in row] + [jnp.zeros((6, rows), F32)], axis=0)
    ids[...] = tall.T[:, 0:2].astype(I32)
    col = [ids[:, j : j + 1] for j in range(2)]
    lane = iota((rows, LANES), 1)
    hot = [(lane == c).astype(BF) for c in col]
    either = hot[0] + hot[1]
    below = (iota((rows, rows), 0) > iota((rows, rows), 1)).astype(BF)
    before = mm(below, either)
    wide = max(experts, 16)
    deep = iota((wide, rows), 0)
    hot_t = [(deep == r).astype(BF) for r in row]
    above = (iota((rows, rows), 0) < iota((rows, rows), 1)).astype(BF)
    before_t = mm(hot_t[0] + hot_t[1], above)
    count[...] = jnp.sum(either.astype(F32), axis=0, keepdims=True)
    flat_t = []
    for j in range(2):
        at = jnp.sum(hot[j].astype(F32) * before, axis=1, keepdims=True).astype(I32)
        pos[:, j : j + 1] = col[j] * capacity + at
        slot[:, j : j + 1] = at
        at_t = jnp.sum(hot_t[j].astype(F32) * before_t, axis=0, keepdims=True).astype(I32)
        flat_t.append(row[j] * capacity + at_t)
    return flat_t


def fill_slots(flat_t, source, out):
    total, rows = out.shape[0], source.shape[0]
    half = total // 2
    for n in range(2):
        place = iota((half, rows), 0) + n * half
        pick = ((place == flat_t[0]) | (place == flat_t[1])).astype(BF)
        out[pl.ds(n * half, half), :] = mm(pick, source).astype(BF)


def attend_block(heads, ends, i, span, first, qkv, keys, scores, kept, inverse):
    width = heads * HEAD_DIM
    base = i * BLOCK
    rows = aligned(base, BLOCK)
    q_pos = base + iota((1, BLOCK), 1)
    begin = start_of(q_pos, ends)
    queries = [
        qkv[n * HEAD_DIM : (n + 1) * HEAD_DIM, rows] * jnp.asarray(SCALE, BF) for n in range(heads)
    ]
    tops = [jnp.full((1, BLOCK), MASKED, F32)] * heads
    for k in range(span):
        part = aligned((first + k) * BLOCK, BLOCK)
        k_pos = (first + k) * BLOCK + iota((BLOCK, BLOCK), 0)
        allowed = (k_pos <= q_pos) & (k_pos >= begin)
        for n in range(heads):
            score = jnp.where(allowed, mm(keys[n, part, :], queries[n]), MASKED)
            scores[n, k] = score
            tops[n] = jnp.maximum(tops[n], jnp.max(score, axis=0, keepdims=True))
    result = []
    for n in range(heads):
        total = jnp.zeros((1, BLOCK), F32)
        acc = jnp.zeros((HEAD_DIM, BLOCK), F32)
        lo = 2 * width + n * HEAD_DIM
        for k in range(span):
            weight = jnp.exp(scores[n, k] - tops[n])
            total = total + jnp.sum(weight, axis=0, keepdims=True)
            value = qkv[lo : lo + HEAD_DIM, aligned((first + k) * BLOCK, BLOCK)]
            low = weight.astype(BF)
            kept[n, k] = low
            acc = acc + mm(value, low)
        whole = 1.0 / total
        inverse[n : n + 1, rows] = whole
        result.append((acc * whole).astype(BF))
    return result


def spans(i, body):
    @pl.when(i < 2)
    def _short():
        body(2, 0)

    @pl.when(i >= 2)
    def _long():
        body(REACH, (i - (REACH - 1)) * (i // (REACH - 1)))


def front_body(
    n_e,
    n_h,
    experts,
    capacity,
    padded,
    heads,
    chunks,
    docs,
    ids_t,
    g1,
    s1,
    g2,
    s2,
    w_router,
    tokens,
    out_grad,
    w_query,
    w_key,
    w_value,
    w_out,
    w_up,
    all_tokens,
    qkv_out,
    att_out,
    att_t_out,
    w_t_out,
    g_in,
    x_slots,
    ups,
    weights,
    ids,
    pos,
    slot,
    count,
    inverse,
    residual,
    gates,
    gate_rows,
    tv,
    gv,
    wv,
    wo,
    w_t,
    qkv,
    keys,
    scores,
    kept,
    att_v,
    att_in,
    g_slots,
    xs_v,
    own_sem,
    w_sem,
    save_sem,
    kept_sem,
    ty_s,
    ty_r,
    tc_s,
    tc_r,
    tf_s,
    tf_r,
    gs_s,
    gs_r,
    at_s,
    at_r,
    wy_s,
    wy_r,
    wc_s,
    wc_r,
    wf_s,
    wf_r,
):
    e, h = lax.axis_index("expert"), lax.axis_index("hidden")
    far = n_h // 2
    pair, core = h // 2, lax.rem(h, 2)
    mate = pair * 2 + 1 - core
    rows, model = tokens.shape
    width = heads * HEAD_DIM
    per_device = rows // BLOCK
    ends = doc_bounds(docs)

    def across(t):
        return lax.rem(pair + t, far) * 2 + core

    def origin(t):
        return lax.rem(pair + far - t, far) * 2 + core

    own_tokens = pltpu.make_async_copy(tokens, tv.at[h], own_sem.at[0])
    own_grad = pltpu.make_async_copy(out_grad, gv, own_sem.at[1])
    own_grad.start()
    own_tokens.start()
    w_loads = [
        pltpu.make_async_copy(w, wv.at[n], w_sem.at[n])
        for n, w in enumerate((w_query, w_key, w_value))
    ]
    w_loads.append(pltpu.make_async_copy(w_out, wo, w_sem.at[3]))
    for load in w_loads:
        load.start()
    greet(
        [{"hidden": lax.rem(h + step, n_h)} for step in range(1, n_h)]
        + [{"expert": lax.rem(e + step, n_e)} for step in range(1, n_e)]
    )

    piece = rows // chunks
    sends = []
    for k in range(chunks):
        part = pl.ds(k * piece, piece)
        for t in range(1, far):
            copy = remote(
                tokens.at[part],
                tv.at[h, part],
                ty_s.at[t, k],
                ty_r.at[t, k],
                {"hidden": across(t)},
            )
            copy.start()
            sends.append(copy)
    beside = remote(tokens, tv.at[h], tc_s, tc_r, {"hidden": mate})
    beside.start()
    sends.append(beside)

    flat_t = find_slots(experts, capacity, ids, ids_t, pos, slot, count)
    own_grad.wait()
    fill_slots(flat_t, gv[...], g_slots)
    for step in range(1, n_e):
        peer = lax.rem(e + step, n_e)
        copy = remote(
            g_slots.at[aligned(peer * capacity, capacity)],
            g_in.at[e],
            gs_s.at[step],
            gs_r.at[step],
            {"expert": peer},
        )
        copy.start()
        sends.append(copy)
    own_slots = pltpu.make_async_copy(
        g_slots.at[aligned(e * capacity, capacity)], g_in.at[e], own_sem.at[1]
    )
    own_slots.start()

    def pass_on(t, k):
        part = pl.ds(k * piece, piece)
        place = tv.at[origin(t), part]
        remote(place, place, ty_s.at[t, k], ty_r.at[t, k], {"hidden": across(t)}).wait_recv()
        copy = remote(place, place, tf_s.at[t, k], tf_r.at[t, k], {"hidden": mate})
        copy.start()
        sends.append(copy)

    todo = [(t, k) for k in range(chunks) for t in range(1, far)]
    third = -(-len(todo) // 4)

    def pass_some():
        for _ in range(min(third, len(todo))):
            pass_on(*todo.pop(0))

    pick = (iota((width, model), 1) == iota((width, model), 0) + h * width).astype(BF)
    for n in range(3):
        w_loads[n].wait()
        w_t[n * width : (n + 1) * width, :] = mm_nt(pick, wv[n]).astype(BF)
        if n == 1:
            pass_some()
    save_w = pltpu.make_async_copy(w_t, w_t_out, save_sem.at[0])
    save_w.start()

    def project(source):
        def one(b, _):
            normed, _unused = norm_parts(tv[source, aligned(b * BLOCK, BLOCK), :].astype(F32))
            hidden = (normed * lying(g1) + lying(s1)).astype(BF)
            block = mm_nt(w_t[...], hidden)
            cols = aligned(source * rows + b * BLOCK, BLOCK)
            qkv[:, cols] = block.astype(BF)
            for n in range(heads):
                lo = width + n * HEAD_DIM
                keys[n, cols, :] = block[lo : lo + HEAD_DIM].T.astype(BF)
            return 0

        lax.fori_loop(0, per_device, one, 0)

    pass_some()
    own_tokens.wait()
    project(h)
    pass_some()
    remote(tokens, tv.at[mate], tc_s, tc_r, {"hidden": mate}).wait_recv()
    project(mate)
    while todo:
        pass_some()

    deep = w_up.shape[1] // 2

    def up_part(k):
        return pl.ds(k * deep, deep)

    def up_across(k):
        for t in range(1, far):
            copy = remote(
                w_up.at[0, up_part(k)],
                ups.at[h, up_part(k)],
                wy_s.at[t, k],
                wy_r.at[t, k],
                {"hidden": across(t)},
            )
            copy.start()
            sends.append(copy)

    def up_onward(k):
        for t in range(1, far):
            place = ups.at[origin(t), up_part(k)]
            remote(place, place, wy_s.at[t, k], wy_r.at[t, k], {"hidden": mate}).wait_recv()
            copy = remote(place, place, wf_s.at[t, k], wf_r.at[t, k], {"hidden": mate})
            copy.start()
            sends.append(copy)

    own_up = pltpu.make_async_copy(w_up.at[0], ups.at[h], own_sem.at[2])
    own_up.start()
    up_beside = remote(w_up.at[0], ups.at[h], wc_s, wc_r, {"hidden": mate})
    up_beside.start()
    sends.append(up_beside)
    up_across(0)
    for t in range(1, far):
        project(origin(t))
    for t in range(1, far):
        there = lax.rem(pair + far - t, far) * 2 + 1 - core
        for k in range(chunks):
            place = tv.at[there, pl.ds(k * piece, piece)]
            remote(place, place, tf_s.at[t, k], tf_r.at[t, k], {"hidden": mate}).wait_recv()
        project(there)
    save_tokens = pltpu.make_async_copy(tv, all_tokens, save_sem.at[1])
    save_qkv = pltpu.make_async_copy(qkv, qkv_out, save_sem.at[2])
    save_tokens.start()
    save_qkv.start()

    inverse[...] = jnp.zeros_like(inverse)

    def device_at(n, sign):
        t, other = n // 2, lax.rem(n, 2)
        return lax.rem(pair + far + sign * t, far) * 2 + lax.rem(core + other, 2)

    def give_att(n):
        owner = device_at(n, 1)
        return remote(
            att_v.at[owner], att_in.at[h], at_s.at[n], at_r.at[n], {"hidden": owner}
        )

    def save_kept(i, turn):
        return pltpu.make_async_copy(kept.at[turn], weights.at[i], kept_sem.at[turn])

    def attend(at, _):
        n = n_h - 1 - at // per_device
        b = lax.rem(at, per_device)
        owner = device_at(n, 1)
        i = owner * per_device + b
        turn = lax.rem(at, 2)

        @pl.when(at >= 2)
        def _free():
            save_kept(i, turn).wait()

        def block(span, first):
            done = attend_block(
                heads, ends, i, span, first, qkv, keys, scores, kept.at[turn], inverse
            )
            for m in range(heads):
                lo = m * HEAD_DIM
                att_v[owner, lo : lo + HEAD_DIM, aligned(b * BLOCK, BLOCK)] = done[m]

        spans(i, block)
        save_kept(i, turn).start()

        @pl.when((b == per_device - 1) & (n > 0))
        def _give():
            give_att(n).start()

        return 0

    lax.fori_loop(0, n_h * per_device, attend, 0)
    up_onward(0)
    att_in[h] = att_v[h]
    save_att = pltpu.make_async_copy(att_v, att_out, save_sem.at[3])
    save_att.start()
    for n in range(n_h - 1, 0, -1):
        give_att(n).wait_recv()
    save_att_t = pltpu.make_async_copy(att_in, att_t_out, save_sem.at[4])
    save_att_t.start()

    up_across(1)

    w_loads[3].wait()
    res = tv[h].astype(F32) + mm_tn(att_in[...].reshape(model, rows), wo[...])
    residual[...] = res
    normed, _unused = norm_parts(res)
    hidden = (normed * lying(g2) + lying(s2)).astype(BF)
    fill_slots(flat_t, hidden, xs_v)
    save_x = [
        pltpu.make_async_copy(
            xs_v.at[pl.ds(n * capacity, capacity)], x_slots.at[n], save_sem.at[5 + n]
        )
        for n in range(experts)
    ]
    for save in save_x:
        save.start()
    logits = mm_nt(hidden, w_router[...])
    lane = iota((rows, experts), 1)
    chosen = [
        jnp.sum(jnp.where(lane == ids[:, j : j + 1], logits, 0.0), axis=1, keepdims=True)
        for j in range(2)
    ]
    top = jnp.maximum(chosen[0], chosen[1])
    raised = [jnp.exp(c - top) for c in chosen]
    both = raised[0] + raised[1]
    gate = [r / both for r in raised]
    for j in range(2):
        gates[:, j : j + 1] = gate[j]
    column = iota((rows, padded), 1)
    for n in range(experts):
        mix = jnp.zeros((rows, padded), F32)
        for j in range(2):
            here = jnp.where(ids[:, j : j + 1] == n, slot[:, j : j + 1], -1) == column
            mix = jnp.where(here, gate[j], mix)
        line = jnp.sum(mix, axis=0, keepdims=True)
        gate_rows[n] = jnp.broadcast_to(line, (8, padded))

    up_onward(1)
    place = ups.at[mate]
    remote(place, place, wc_s, wc_r, {"hidden": mate}).wait_recv()
    for k in range(2):
        for t in range(1, far):
            there = lax.rem(pair + far - t, far) * 2 + 1 - core
            place = ups.at[there, up_part(k)]
            remote(place, place, wf_s.at[t, k], wf_r.at[t, k], {"hidden": mate}).wait_recv()
    own_up.wait()
    for step in range(1, n_e):
        source = lax.rem(e + n_e - step, n_e)
        place = g_in.at[source]
        remote(place, place, gs_s.at[step], gs_r.at[step], {"expert": e}).wait_recv()
    own_slots.wait()
    for n in range(1, n_h):
        give_att(n).wait_send()
    for turn in range(2):
        save_kept(0, turn).wait()
    for copy in sends:
        copy.wait_send()
    for save in [save_w, save_tokens, save_qkv, save_att, save_att_t, *save_x]:
        save.wait()


def run_front(
    docs, ids_t, g1, s1, g2, s2, w_router, tokens, out_grad, ws, w_up, capacity, heads, cid
):
    n_e, n_h = lax.axis_size("expert"), lax.axis_size("hidden")
    experts = n_e * w_up.shape[0]
    rows, model = tokens.shape
    padded = -(-capacity // LANES) * LANES
    width, group, total = heads * HEAD_DIM, rows * n_h, experts * capacity
    far, chunks = n_h // 2, 8

    def pairs(*shape):
        return [DMA(shape), DMA(shape)]

    return pl.pallas_call(
        partial(front_body, n_e, n_h, experts, capacity, padded, heads, chunks),
        name="front",
        out_shape=[
            shape_of((n_h, rows, model), BF),
            shape_of((3 * width, group), BF),
            shape_of((n_h, width, rows), BF),
            shape_of((n_h, width, rows), BF),
            shape_of((3 * width, model), BF),
            shape_of((experts, capacity, model), BF),
            shape_of((experts, capacity, model), BF),
            shape_of((n_h, *w_up.shape[1:]), BF),
            shape_of((group // BLOCK, heads, REACH, BLOCK, BLOCK), BF),
            shape_of((rows, 2), I32),
            shape_of((rows, 2), I32),
            shape_of((rows, 2), I32),
            shape_of((1, LANES), F32),
            shape_of((8, group), F32),
            shape_of((rows, model), F32),
            shape_of((rows, 2), F32),
            shape_of((experts, 8, padded), F32),
        ],
        in_specs=[SMEM] + [VMEM] * 6 + [ANY] * 7,
        out_specs=[ANY] * 9 + [VMEM] * 8,
        scratch_shapes=[
            pltpu.VMEM((n_h, rows, model), BF),
            pltpu.VMEM((rows, model), BF),
            pltpu.VMEM((3, model, model), BF),
            pltpu.VMEM((model, model), BF),
            pltpu.VMEM((3 * width, model), BF),
            pltpu.VMEM((3 * width, group), BF),
            pltpu.VMEM((heads, group, HEAD_DIM), BF),
            pltpu.VMEM((heads, REACH, BLOCK, BLOCK), F32),
            pltpu.VMEM((2, heads, REACH, BLOCK, BLOCK), BF),
            pltpu.VMEM((n_h, width, rows), BF),
            pltpu.VMEM((n_h, width, rows), BF),
            pltpu.VMEM((total, model), BF),
            pltpu.VMEM((total, model), BF),
            DMA((4,)),
            DMA((4,)),
            DMA((5 + experts,)),
            DMA((2,)),
            *pairs(far, chunks),
            DMA,
            DMA,
            *pairs(far, chunks),
            *pairs(n_e),
            *pairs(n_h),
            *pairs(far, 2),
            DMA,
            DMA,
            *pairs(far, 2),
        ],
        compiler_params=pltpu.CompilerParams(
            collective_id=cid, has_side_effects=True, vmem_limit_bytes=58 << 20
        ),
    )(docs, ids_t, g1, s1, g2, s2, w_router, tokens, out_grad, *ws, w_up)


def moe_body(
    size,
    capacity,
    padded,
    per,
    x_slots,
    gate_rows,
    g_in,
    ups,
    w_down,
    dx_back,
    dg_back,
    y_out,
    dw_sum,
    dw_far,
    xv,
    gv,
    gates_v,
    up_v,
    down_v,
    act,
    dz,
    xg,
    dy,
    xg_t,
    dy_t,
    dxv,
    yv,
    dgv,
    y_acc,
    dx_acc,
    dw_box,
    load_sem,
    save_sem,
    wy_s,
    wy_r,
    wc_s,
    wc_r,
    wf_s,
    wf_r,
    dc_s,
    dc_r,
    df_s,
    df_r,
    g_sem,
    own_sem,
    xs_sem,
    xr_sem,
    gs_sem,
    gr_sem,
    ds_sem,
    dr_sem,
    ts_sem,
    tr_sem,
    out_sem,
):
    me, h = lax.axis_index("expert"), lax.axis_index("hidden")
    shards_n = ups.shape[0]
    far = shards_n // 2
    pair, core = h // 2, lax.rem(h, 2)
    mate = pair * 2 + 1 - core
    deep = w_down.shape[1] // 2
    tall = per * capacity
    steps = size // per

    middle = size // 2

    def peer_at(p):
        mask = jnp.where(p < 2, p, jnp.where(p < 2 + middle, p - 2 + middle, p - middle))
        peer, bit = 0, 1
        while bit < size:
            peer = peer + lax.rem(me // bit + mask // bit, 2) * bit
            bit *= 2
        return peer

    def rows_of(p):
        return pl.ds(pl.multiple_of(p * capacity, capacity), capacity)

    def send_x(p):
        peer = peer_at(p)
        return remote(
            x_slots.at[peer], xv.at[rows_of(p)], xs_sem.at[p], xr_sem.at[p], {"expert": peer}
        )

    def send_gate(p):
        peer = peer_at(p)
        return remote(
            gate_rows.at[peer], gates_v.at[p], gs_sem.at[p], gr_sem.at[p], {"expert": peer}
        )

    def send_dx(p):
        peer = peer_at(p)
        return remote(
            dxv.at[rows_of(p)], dx_back.at[me], ds_sem.at[p], dr_sem.at[p], {"expert": peer}
        )

    def send_dg(p):
        peer = peer_at(p)
        return remote(dgv.at[p], dg_back.at[me], ts_sem.at[p], tr_sem.at[p], {"expert": peer})

    def load_g(p):
        return pltpu.make_async_copy(g_in.at[peer_at(p)], gv.at[rows_of(p)], g_sem.at[p])

    def save_y(p):
        return pltpu.make_async_copy(yv.at[rows_of(p)], y_out.at[peer_at(p)], out_sem.at[p])

    own_x = pltpu.make_async_copy(x_slots.at[me], xv.at[rows_of(0)], own_sem.at[0])
    own_gate = pltpu.make_async_copy(gate_rows.at[me], gates_v.at[0], own_sem.at[1])
    own_dx = pltpu.make_async_copy(dxv.at[rows_of(0)], dx_back.at[me], own_sem.at[2])
    own_dg = pltpu.make_async_copy(dgv.at[0], dg_back.at[me], own_sem.at[3])
    load_up = pltpu.make_async_copy(ups, up_v, load_sem.at[0])
    load_down = pltpu.make_async_copy(w_down.at[0], down_v.at[h], load_sem.at[1])

    def half(k):
        return aligned(k * deep, deep)

    def down_across(t, k):
        there = {"hidden": lax.rem(pair + t, far) * 2 + core}
        return remote(
            w_down.at[0, half(k)], down_v.at[h, half(k)], wy_s.at[t, k], wy_r.at[t, k], there
        )

    def down_onward(t, k):
        place = down_v.at[lax.rem(pair + far - t, far) * 2 + core, half(k)]
        return remote(place, place, wf_s.at[t, k], wf_r.at[t, k], {"hidden": mate})

    down_beside = remote(w_down.at[0], down_v.at[h], wc_s, wc_r, {"hidden": mate})
    own_x.start()
    own_gate.start()
    for p in range(size):
        load_g(p).start()
    load_up.start()
    load_down.start()
    greet(
        [{"expert": lax.rem(me + step, size)} for step in range(1, size)]
        + [{"hidden": lax.rem(h + step, shards_n)} for step in range(1, shards_n)]
    )
    for p in range(1, middle):
        send_x(p).start()
        send_gate(p).start()
    for k in range(2):
        for t in range(1, far):
            down_across(t, k).start()
    down_beside.start()
    own_x.wait()
    own_gate.wait()
    load_up.wait()
    load_down.wait()

    def step_body(step, _):
        base = step * per
        for s in range(per):

            @pl.when(base + s > 0)
            def _arrive(s=s):
                send_x(base + s).wait_recv()
                send_gate(base + s).wait_recv()

            load_g(base + s).wait()
        rows = pl.ds(pl.multiple_of(step * tall, tall), tall)
        x, g = xv[rows, :], gv[rows, :]
        y_acc[...] = jnp.zeros_like(y_acc)
        dx_acc[...] = jnp.zeros_like(dx_acc)

        def shard_body(n, _):
            t = n // 2
            beside = lax.rem(n, 2)
            c = lax.rem(pair + far - t, far) * 2 + lax.rem(core + beside, 2)

            @pl.when((step == 0) & (n == 1))
            def _beside():
                down_beside.wait_recv()

            @pl.when((step == 0) & (n == 2))
            def _second_half():
                for p in range(1, middle):
                    send_x(p).wait_send()
                    send_gate(p).wait_send()
                for p in range(middle, size):
                    send_x(p).start()
                    send_gate(p).start()

            @pl.when((step == 0) & (n >= 2) & (beside == 0))
            def _across():
                for k in range(2):
                    down_across(t, k).wait_recv()
                    down_onward(t, k).start()

            @pl.when((step == 0) & (n >= 2) & (beside == 1))
            def _onward():
                for k in range(2):
                    down_onward(t, k).wait_recv()

            z = mm(x, up_v[c])
            du = mm_nt(g, down_v[c])
            square = z * z
            curve = jnp.tanh(z * (GELU_A + GELU_A * GELU_B * square))
            plus = 0.5 + 0.5 * curve
            hidden = (z * plus).astype(BF)
            rise = GELU_A + 3.0 * GELU_A * GELU_B * square
            slope = plus + 0.5 * z * (1.0 - curve * curve) * rise
            back = (slope * du).astype(BF)
            act[c, rows, :] = hidden
            dz[c, rows, :] = back
            y_acc[...] += mm(hidden, down_v[c])
            dx_acc[...] += mm_nt(back, up_v[c])
            return 0

        lax.fori_loop(0, shards_n, shard_body, 0)
        dxv[rows, :] = dx_acc[...].astype(BF)
        y_low = y_acc[...].astype(BF)
        yv[rows, :] = y_low
        dots = jnp.sum(y_low.astype(F32) * g.astype(F32), axis=1, keepdims=True)
        for s in range(per):
            p = base + s
            part = slice(s * capacity, (s + 1) * capacity)
            tall_dots = jnp.broadcast_to(dots[part], (capacity, LANES))
            if padded > capacity:
                blank = jnp.zeros((padded - capacity, LANES), F32)
                tall_dots = jnp.concatenate([tall_dots, blank], axis=0)
            dgv[p] = tall_dots.T[0:8]

            @pl.when(p > 0)
            def _give(p=p):
                send_dx(p).start()
                send_dg(p).start()

            @pl.when(p == 0)
            def _keep():
                own_dx.start()
                own_dg.start()

            save_y(p).start()
        for s in range(per):
            p = base + s
            part = slice(s * capacity, (s + 1) * capacity)
            gate = gates_v[p].T[0:capacity, 0:1]
            xg[rows_of(p), :] = (x[part].astype(F32) * gate).astype(BF)
            dy[rows_of(p), :] = (g[part].astype(F32) * gate).astype(BF)
        return 0

    lax.fori_loop(0, steps, step_body, 0)

    total = size * capacity
    turn = 256
    for k in range(total // turn):
        rows = slice(k * turn, (k + 1) * turn)
        xg_t[:, rows] = xg[rows, :].astype(F32).T.astype(BF)
        dy_t[:, rows] = dy[rows, :].astype(F32).T.astype(BF)
    model = xg_t.shape[0]
    bands = model // turn

    for t in range(1, far):
        for k in range(2):
            down_across(t, k).wait_send()
            down_onward(t, k).wait_send()
    down_beside.wait_send()

    def give(which, step):
        source = (up_v, down_v)[which].at[lax.rem(pair + step, far) * 2 + 1 - core]
        return remote(
            source,
            dw_box.at[which, step],
            dc_s.at[which, step],
            dc_r.at[which, step],
            {"hidden": mate},
        )

    def keep(which, step):
        source = (up_v, down_v)[which].at[lax.rem(pair + step, far) * 2 + core]
        return pltpu.make_async_copy(source, dw_sum.at[which, step], save_sem.at[which, step])

    def cross(step):
        source = up_v.at[lax.rem(pair + step, far) * 2 + core, half(0)]
        there = {"hidden": lax.rem(pair + step, far) * 2 + core}
        return remote(source, dw_far.at[step - 1], df_s.at[step], df_r.at[step], there)

    def other_body(n, _):
        band, step = lax.rem(n, bands), lax.rem(n // bands + 1, far)
        c = lax.rem(pair + step, far) * 2 + 1 - core
        lines = aligned(band * turn, turn)
        up_v[c, lines, :] = mm(xg_t[lines, :], dz[c]).astype(BF)
        down_v[c, lines, :] = mm(dy_t[lines, :], act[c]).astype(BF)

        @pl.when(band == bands - 1)
        def _give():
            for which in range(2):
                give(which, step).start()

        return 0

    lax.fori_loop(0, far * bands, other_body, 0)

    def own_body(n, _):
        band, step = lax.rem(n, bands), lax.rem(n // bands + 1, far)
        c = lax.rem(pair + step, far) * 2 + core

        @pl.when(band == 0)
        def _take():
            for which in range(2):
                give(which, step).wait_recv()

        lines = aligned(band * turn, turn)
        up = mm(xg_t[lines, :], dz[c]) + dw_box[0, step, lines, :].astype(F32)
        down = mm(dy_t[lines, :], act[c]) + dw_box[1, step, lines, :].astype(F32)
        up_v[c, lines, :] = up.astype(BF)
        down_v[c, lines, :] = down.astype(BF)

        @pl.when(band == bands - 1)
        def _keep():
            for which in range(2):
                keep(which, step).start()

        @pl.when((band == bands - 1) & (step > 0))
        def _cross():
            cross(step).start()

        return 0

    lax.fori_loop(0, far * bands, own_body, 0)
    for p in range(middle, size):
        send_x(p).wait_send()
        send_gate(p).wait_send()
    for p in range(1, size):
        send_dx(p).wait()
        send_dg(p).wait()
    for p in range(size):
        save_y(p).wait()
    own_dx.wait()
    own_dg.wait()
    for step in range(far):
        for which in range(2):
            give(which, step).wait_send()
            keep(which, step).wait()
    for step in range(1, far):
        cross(step).wait()


def run_experts(x_slots, gate_rows, g_in, ups, w_down, cid):
    size = lax.axis_size("expert")
    experts, capacity, model = x_slots.shape
    padded = gate_rows.shape[2]
    shards_n, _unused, width = ups.shape
    total = experts * capacity
    per = 1
    while per * 2 * capacity <= 320 and size % (per * 2) == 0:
        per *= 2
    tall = per * capacity
    rows2 = (total, model)
    return pl.pallas_call(
        partial(moe_body, size, capacity, padded, per),
        name="experts",
        out_shape=[
            shape_of(x_slots.shape, BF),
            shape_of(gate_rows.shape, F32),
            shape_of(x_slots.shape, BF),
            shape_of((2, shards_n // 2, model, width), BF),
            shape_of((shards_n // 2 - 1, model // 2, width), BF),
        ],
        in_specs=[ANY] * 5,
        out_specs=[ANY] * 5,
        scratch_shapes=[
            pltpu.VMEM(rows2, BF),
            pltpu.VMEM(rows2, BF),
            pltpu.VMEM(gate_rows.shape, F32),
            pltpu.VMEM((shards_n, model, width), BF),
            pltpu.VMEM((shards_n, width, model), BF),
            pltpu.VMEM((shards_n, total, width), BF),
            pltpu.VMEM((shards_n, total, width), BF),
            pltpu.VMEM(rows2, BF),
            pltpu.VMEM(rows2, BF),
            pltpu.VMEM((model, total), BF),
            pltpu.VMEM((model, total), BF),
            pltpu.VMEM(rows2, BF),
            pltpu.VMEM(rows2, BF),
            pltpu.VMEM(gate_rows.shape, F32),
            pltpu.VMEM((tall, model), F32),
            pltpu.VMEM((tall, model), F32),
            pltpu.VMEM((2, shards_n // 2, model, width), BF),
            DMA((2,)),
            DMA((2, shards_n // 2)),
            DMA((shards_n // 2, 2)),
            DMA((shards_n // 2, 2)),
            DMA,
            DMA,
            DMA((shards_n // 2, 2)),
            DMA((shards_n // 2, 2)),
            DMA((2, shards_n // 2)),
            DMA((2, shards_n // 2)),
            DMA((shards_n // 2,)),
            DMA((shards_n // 2,)),
            DMA((size,)),
            DMA((4,)),
        ]
        + [DMA((size,))] * 9,
        compiler_params=pltpu.CompilerParams(
            collective_id=cid, has_side_effects=True, vmem_limit_bytes=60 << 20
        ),
        cost_estimate=pl.CostEstimate(
            flops=12 * total * model * width * shards_n, bytes_accessed=40 << 20, transcendentals=0
        ),
    )(x_slots, gate_rows, g_in, ups, w_down)


def tail_body(
    n_e,
    n_h,
    chunks,
    dh,
    w_all,
    small,
    tokens,
    gain,
    d_res,
    residual,
    gates,
    pos,
    y_back,
    input_grad,
    output,
    full,
    total,
    mine,
    beside,
    across,
    passing,
    x_box,
    z_box,
    w_mid,
    piece,
    small_mid,
    small_h,
    small_e,
    mine_sem,
    cs_sem,
    cr_sem,
    as_sem,
    ar_sem,
    ws_sem,
    wr_sem,
    vs_sem,
    vr_sem,
    hs_sem,
    hr_sem,
    es_sem,
    er_sem,
    keep_sem,
    zs_sem,
    zr_sem,
    xs_sem,
    xr_sem,
    ys_sem,
    yr_sem,
    ms_sem,
    mr_sem,
):
    e, h = lax.axis_index("expert"), lax.axis_index("hidden")
    far, high = n_h // 2, n_e // 2
    pair, core = h // 2, lax.rem(h, 2)
    eh, el = e // 2, lax.rem(e, 2)
    mate = pair * 2 + 1 - core
    greet(
        [{"expert": lax.rem(e + step, n_e)} for step in range(1, n_e)]
        + [{"hidden": lax.rem(h + step, n_h)} for step in range(1, n_h)]
    )
    w_sends, w_order = [], list(range(1, high)) + [0]
    for step in w_order:
        there = lax.rem(eh + step, high)
        copy = remote(
            w_all.at[there * 2 + 1 - el],
            x_box.at[step],
            ws_sem.at[step],
            wr_sem.at[step],
            {"expert": eh * 2 + 1 - el},
        )
        copy.start()
        w_sends.append(copy)
    rows = dh.shape[1] // chunks
    core_sends = {}
    for step in list(range(1, far)) + [0]:
        there = lax.rem(pair + step, far)
        for k in range(chunks):
            part = pl.ds(k * rows, rows)
            copy = remote(
                dh.at[there * 2 + 1 - core, part],
                beside.at[step, part],
                cs_sem.at[step, k],
                cr_sem.at[step, k],
                {"hidden": mate},
            )
            copy.start()
            core_sends[step, k] = copy
    loads = []
    for step in range(far):
        there = lax.rem(pair + step, far)
        load = pltpu.make_async_copy(dh.at[there * 2 + core], mine.at[step], mine_sem.at[step])
        load.start()
        loads.append(load)
    small_sends = []
    for at in range(n_h - 1):
        peer = lax.rem(h + 1 + at, n_h)
        copy = remote(small, small_h.at[at], hs_sem.at[at], hr_sem.at[at], {"hidden": peer})
        copy.start()
        small_sends.append(copy)
    v_sends = []
    for at, step in enumerate(w_order[:-1]):
        there = lax.rem(eh + step, high) * 2 + el
        w_sends[at].wait_recv()
        w_mid[step - 1] = (w_all[there].astype(F32) + x_box[step].astype(F32)).astype(BF)
        copy = remote(
            w_mid.at[step - 1],
            z_box.at[step - 1],
            vs_sem.at[step],
            vr_sem.at[step],
            {"expert": there},
        )
        copy.start()
        v_sends.append(copy)
    for load in loads:
        load.wait()
    far_sends = []
    for step in range(1, far):
        there = lax.rem(pair + step, far)
        for k in range(chunks):
            part = pl.ds(k * rows, rows)
            core_sends[step, k].wait_recv()
            both = mine[step, part, :].astype(F32) + beside[step, part, :].astype(F32)
            passing[step - 1, part, :] = both.astype(BF)
            copy = remote(
                passing.at[step - 1, part],
                across.at[step - 1, part],
                as_sem.at[step - 1, k],
                ar_sem.at[step - 1, k],
                {"hidden": there * 2 + core},
            )
            copy.start()
            far_sends.append(copy)
    for copy in small_sends:
        copy.wait_recv()
    summed = small[...]
    for at in range(n_h - 1):
        summed = summed + small_h[at]
    small_mid[...] = summed
    small_out = []
    for at in range(n_e - 1):
        peer = lax.rem(e + 1 + at, n_e)
        copy = remote(small_mid, small_e.at[at], es_sem.at[at], er_sem.at[at], {"expert": peer})
        copy.start()
        small_out.append(copy)
    w_sends[-1].wait_recv()
    acc = w_all[e].astype(F32) + x_box[0].astype(F32)
    for at, copy in enumerate(v_sends):
        copy.wait_recv()
        acc = acc + z_box[at].astype(F32)
    piece[...] = acc.astype(BF)
    keep = pltpu.make_async_copy(piece, full.at[h, e], keep_sem)
    keep.start()
    started = []

    def slot(eh_of, el_of, pair_of, core_of):
        return full.at[pair_of * 2 + core_of, eh_of * 2 + el_of]

    def back(step, size, place):
        return lax.rem(place + size - step, size)

    def give_z(source):
        for s in range(1, high):
            there = lax.rem(eh + s, high) * 2 + el
            copy = remote(
                source, slot(eh, el, pair, core), zs_sem.at[s], zr_sem.at[s], {"expert": there}
            )
            copy.start()
            started.append(copy)

    def z_arrival(s):
        place = slot(back(s, high, eh), el, pair, core)
        return place, remote(place, place, zs_sem.at[s], zr_sem.at[s], {"expert": e})

    def give_x(source, s):
        target = slot(back(s, high, eh), el, pair, core)
        copy = remote(
            source, target, xs_sem.at[s], xr_sem.at[s], {"expert": eh * 2 + 1 - el}
        )
        copy.start()
        started.append(copy)

    def x_arrival(s):
        place = slot(back(s, high, eh), 1 - el, pair, core)
        return place, remote(place, place, xs_sem.at[s], xr_sem.at[s], {"expert": e})

    def give_y(source, s, flag):
        target = slot(back(s, high, eh), el if flag == 0 else 1 - el, pair, core)
        for t in range(1, far):
            there = lax.rem(pair + t, far) * 2 + core
            at = 2 * s + flag
            copy = remote(
                source, target, ys_sem.at[t, at], yr_sem.at[t, at], {"hidden": there}
            )
            copy.start()
            started.append(copy)

    def y_arrival(t, s, flag):
        other = el if flag == 0 else 1 - el
        place = slot(back(s, high, eh), other, back(t, far, pair), core)
        at = 2 * s + flag
        return place, remote(place, place, ys_sem.at[t, at], yr_sem.at[t, at], {"hidden": h})

    def give_mate(source, t, s, flag):
        other = el if flag == 0 else 1 - el
        target = slot(back(s, high, eh), other, back(t, far, pair), core)
        at = 2 * s + flag
        copy = remote(source, target, ms_sem.at[t, at], mr_sem.at[t, at], {"hidden": mate})
        copy.start()
        started.append(copy)

    def mate_arrival(t, s, flag):
        other = el if flag == 0 else 1 - el
        place = slot(back(s, high, eh), other, back(t, far, pair), 1 - core)
        at = 2 * s + flag
        return place, remote(place, place, ms_sem.at[t, at], mr_sem.at[t, at], {"hidden": h})

    give_z(piece)
    give_x(piece, 0)
    give_y(piece, 0, 0)
    give_mate(piece, 0, 0, 0)
    for s in range(1, high):
        place, arrival = z_arrival(s)
        arrival.wait_recv()
        give_x(place, s)
        give_y(place, s, 0)
        give_mate(place, 0, s, 0)
    for s in range(high):
        place, arrival = x_arrival(s)
        arrival.wait_recv()
        give_y(place, s, 1)
        give_mate(place, 0, s, 1)
    place_of = iota((residual.shape[0], y_back.shape[0]), 1)
    result = residual[...]
    for j in range(2):
        pick = (place_of == pos[:, j : j + 1]).astype(BF)
        result = result + gates[:, j : j + 1] * mm(pick, y_back[...])
    output[...] = result.astype(BF)
    for copy in small_out:
        copy.wait_recv()
    summed = small_mid[...]
    for at in range(n_e - 1):
        summed = summed + small_e[at]
    total[...] = summed
    for k in range(chunks):
        part = pl.ds(k * rows, rows)
        core_sends[0, k].wait_recv()
    for copy in far_sends:
        copy.wait_recv()
    grad = mine[0].astype(F32) + beside[0].astype(F32)
    for step in range(far - 1):
        grad = grad + across[step].astype(F32)
    normed, inverse = norm_parts(tokens[...].astype(F32))
    input_grad[...] = (d_res[...] + norm_back(grad, normed, inverse, lying(gain))).astype(BF)
    for t in range(1, far):
        for s in range(high):
            for flag in range(2):
                place, arrival = y_arrival(t, s, flag)
                arrival.wait_recv()
                give_mate(place, t, s, flag)
    for t in range(far):
        for s in range(high):
            for flag in range(2):
                _place, arrival = mate_arrival(t, s, flag)
                arrival.wait_recv()
    keep.wait()
    for copy in started + w_sends + v_sends + small_sends + small_out + far_sends:
        copy.wait_send()
    for copy in core_sends.values():
        copy.wait_send()


def run_tail(dh, w_all, small, tokens, gain, d_res, residual, gates, pos, y_back, cid):
    n_e, n_h = lax.axis_size("expert"), lax.axis_size("hidden")
    far, high = n_h // 2, n_e // 2
    chunks = 4
    _unused, rows, model = dh.shape
    piece = w_all.shape[1:]
    return pl.pallas_call(
        partial(tail_body, n_e, n_h, chunks),
        name="tail",
        out_shape=[
            shape_of((rows, model), BF),
            shape_of((rows, model), BF),
            shape_of((n_h, n_e, *piece), BF),
            shape_of(small.shape, F32),
        ],
        in_specs=[ANY] + [VMEM] * 9,
        out_specs=[VMEM, VMEM, ANY, VMEM],
        scratch_shapes=[
            pltpu.VMEM((far, rows, model), BF),
            pltpu.VMEM((far, rows, model), BF),
            pltpu.VMEM((far - 1, rows, model), BF),
            pltpu.VMEM((far - 1, rows, model), BF),
            pltpu.VMEM((high, *piece), BF),
            pltpu.VMEM((high - 1, *piece), BF),
            pltpu.VMEM((high - 1, *piece), BF),
            pltpu.VMEM(piece, BF),
            pltpu.VMEM(small.shape, F32),
            pltpu.VMEM((n_h - 1, *small.shape), F32),
            pltpu.VMEM((n_e - 1, *small.shape), F32),
            DMA((far,)),
            DMA((far, chunks)),
            DMA((far, chunks)),
            DMA((far - 1, chunks)),
            DMA((far - 1, chunks)),
            DMA((high,)),
            DMA((high,)),
            DMA((high,)),
            DMA((high,)),
            DMA((n_h - 1,)),
            DMA((n_h - 1,)),
            DMA((n_e - 1,)),
            DMA((n_e - 1,)),
            DMA,
            DMA((high,)),
            DMA((high,)),
            DMA((high,)),
            DMA((high,)),
            DMA((far, n_e)),
            DMA((far, n_e)),
            DMA((far, n_e)),
            DMA((far, n_e)),
        ],
        compiler_params=pltpu.CompilerParams(
            collective_id=cid, has_side_effects=True, vmem_limit_bytes=56 << 20
        ),
    )(dh, w_all, small, tokens, gain, d_res, residual, gates, pos, y_back)


def turn_body(
    width,
    experts,
    scale,
    full,
    dw,
    small,
    input_grad,
    output,
    q_out,
    k_out,
    v_out,
    o_out,
    up_out,
    down_out,
    g1_out,
    s1_out,
    g2_out,
    s2_out,
    router_out,
    input_out,
    output_out,
    load_out,
):
    @pl.when(pl.program_id(0) == 0)
    def _begin():
        input_out[...] = input_grad[...]
        output_out[...] = output[...]
        for n, out in enumerate((g1_out, s1_out, g2_out, s2_out)):
            out[...] = small[n : n + 1, :].reshape(out.shape)
        router_out[...] = small[8 : 8 + experts, :]
        load_out[...] = small[4:5, 0:experts].reshape(experts) * scale

    for n, out in enumerate((q_out, k_out, v_out)):
        part = full[:, n * width : (n + 1) * width, :].astype(F32)
        out[...] = part.reshape(-1, part.shape[2]).T
    part = full[:, 3 * width :, :].astype(F32)
    o_out[...] = part.reshape(-1, part.shape[2])
    trained = jnp.where(lax.axis_index("expert") >= experts // 2, 1.0, 0.0)
    up_out[...] = dw[0].astype(F32) * trained
    down_out[...] = dw[1].astype(F32).T * trained


def turn_weights(full, dw, small, input_grad, output, width, experts, scale):
    n_h, deep, model = full.shape
    cols = 128
    across = pl.BlockSpec((cols, model), lambda i: (i, 0))
    down = pl.BlockSpec((model, cols), lambda i: (0, i))
    flat = pl.BlockSpec((model,), lambda i: (0,))
    whole = pl.BlockSpec(output.shape, lambda i: (0, 0))
    square = shape_of((model, model), F32)
    return pl.pallas_call(
        partial(turn_body, width, experts, scale),
        name="turn_weights",
        grid=(model // cols,),
        out_shape=[square] * 6
        + [shape_of((model,), F32)] * 4
        + [
            shape_of((experts, model), F32),
            shape_of(input_grad.shape, BF),
            shape_of(output.shape, BF),
            shape_of((experts,), F32),
        ],
        in_specs=[
            pl.BlockSpec((n_h, deep, cols), lambda i: (0, 0, i)),
            pl.BlockSpec((2, model, cols), lambda i: (0, 0, i)),
            pl.BlockSpec(small.shape, lambda i: (0, 0)),
            whole,
            whole,
        ],
        out_specs=[across, across, across, down, down, across]
        + [flat] * 4
        + [pl.BlockSpec((experts, model), lambda i: (0, 0)), whole, whole]
        + [pl.BlockSpec((experts,), lambda i: (0,))],
        compiler_params=pltpu.CompilerParams(
            dimension_semantics=("arbitrary",), vmem_limit_bytes=60 << 20
        ),
        cost_estimate=pl.CostEstimate(flops=0, bytes_accessed=24 << 20, transcendentals=0),
    )(full, dw, small, input_grad, output)


def attend_back(
    heads, i, span, first, qkv, given, centre, kept, values, dq_acc, dk_acc, dv_acc
):
    width = heads * HEAD_DIM
    rows = aligned(i * BLOCK, BLOCK)
    dq_acc[...] = jnp.zeros_like(dq_acc)
    queries = [
        qkv[n * HEAD_DIM : (n + 1) * HEAD_DIM, rows] * jnp.asarray(SCALE, BF) for n in range(heads)
    ]
    for k in range(span):
        part = aligned((first + k) * BLOCK, BLOCK)
        for n in range(heads):
            here = slice(n * HEAD_DIM, (n + 1) * HEAD_DIM)
            weight = kept[n, k]
            d_weight = mm(values[n, part, :], given[n])
            d_score = (weight.astype(F32) * (d_weight - centre[n])).astype(BF)
            dv_acc[here, part] += mm_nt(given[n], weight)
            dk_acc[here, part] += mm_nt(queries[n], d_score)
            lo = width + n * HEAD_DIM
            dq_acc[here, :] += mm(qkv[lo : lo + HEAD_DIM, part], d_score)


def back_body(
    n_e,
    n_h,
    experts,
    capacity,
    padded,
    heads,
    ids,
    slot,
    pos,
    gates,
    count,
    g1,
    s1,
    g2,
    s2,
    w_router,
    inverse,
    dg_rows,
    dx_back,
    y_out,
    dw_sum,
    dw_far,
    out_grad,
    residual,
    all_tokens,
    qkv_in,
    att_in,
    att_t_in,
    w_out,
    w_t_in,
    weights,
    y_back,
    d_hidden,
    d_res,
    w_all,
    small,
    dw_own,
    dxv,
    gv,
    res_v,
    tv,
    qkv,
    att_v,
    att_t,
    wo,
    w_t,
    d_att_v,
    d_att,
    wo_box,
    wo_far,
    kept,
    values,
    dq_acc,
    dk_acc,
    dv_acc,
    d_qkv,
    w_acc,
    dw_mine,
    dw_across,
    load_sem,
    save_sem,
    dw_sem,
    kept_sem,
    y_own,
    y_s,
    y_r,
    at_s,
    at_r,
    wo_s,
    wo_r,
    wf_s,
    wf_r,
    da_s,
    da_r,
):
    e, h = lax.axis_index("expert"), lax.axis_index("hidden")
    far = n_h // 2
    pair, core = h // 2, lax.rem(h, 2)
    mate = pair * 2 + 1 - core
    rows, model = out_grad.shape
    width = heads * HEAD_DIM
    group = rows * n_h
    per_device = rows // BLOCK
    blocks = group // BLOCK
    sends = []

    loads = [
        pltpu.make_async_copy(source, target, load_sem.at[n])
        for n, (source, target) in enumerate(
            (
                (residual, res_v),
                (dx_back, dxv),
                (out_grad, gv),
                (w_out, wo),
                (att_t_in, att_t),
                (qkv_in, qkv),
                (att_in, att_v),
                (all_tokens, tv),
                (w_t_in, w_t),
            )
        )
    ]
    for load in loads:
        load.start()
    greet(
        [{"hidden": lax.rem(h + step, n_h)} for step in range(1, n_h)]
        + [{"expert": lax.rem(e + step, n_e)} for step in range(1, n_e)]
    )
    load_dw = pltpu.make_async_copy(dw_sum.at[:, 0], dw_mine, dw_sem.at[0])
    load_dw.start()
    deep = dw_mine.shape[1] // 2
    load_far = pltpu.make_async_copy(
        dw_far, dw_across.at[0, :, pl.ds(0, deep)], dw_sem.at[1]
    )
    load_far.start()

    def dw_across_copy(which, step, k):
        part = pl.ds(k * deep, deep)
        return remote(
            dw_sum.at[which, step, part],
            dw_across.at[which, step - 1, part],
            da_s.at[which, step, k],
            da_r.at[which, step, k],
            {"hidden": lax.rem(pair + step, far) * 2 + core},
        )

    def dw_send(which, k):
        for step in range(1, far):
            dw_across_copy(which, step, k).start()

    dw_send(0, 1)
    for step in range(1, n_e):
        peer = lax.rem(e + step, n_e)
        copy = remote(y_out.at[peer], y_back.at[e], y_s.at[step], y_r.at[step], {"expert": peer})
        copy.start()
        sends.append(copy)
    own_y = pltpu.make_async_copy(y_out.at[e], y_back.at[e], y_own)
    own_y.start()

    for load in loads[:3]:
        load.wait()
    normed, spread = norm_parts(res_v[...])
    hidden = (normed * lying(g2) + lying(s2)).astype(BF)
    gate = [gates[:, j : j + 1] for j in range(2)]
    column = iota((rows, padded), 1)
    dot_of = []
    for j in range(2):
        mix = jnp.zeros((rows, padded), F32)
        for n in range(experts):
            here = jnp.where(ids[:, j : j + 1] == n, slot[:, j : j + 1], -1) == column
            mix = jnp.where(here, dg_rows[n, 0:1, :], mix)
        dot_of.append(jnp.sum(mix, axis=1, keepdims=True))
    mean = gate[0] * dot_of[0] + gate[1] * dot_of[1]
    lane = iota((rows, experts), 1)
    d_logits = jnp.zeros((rows, experts), F32)
    for j in range(2):
        d_logits = jnp.where(lane == ids[:, j : j + 1], gate[j] * (dot_of[j] - mean), d_logits)
    high, low = split_two(d_logits)
    grad = mm(high, w_router[...]) + mm(low, w_router[...])
    small[...] = jnp.zeros_like(small)
    small[8 : 8 + experts, :] = mm_tn(high, hidden) + mm_tn(low, hidden)
    small[4:5, 0:LANES] = count[...]
    place = iota((rows, experts * capacity), 1)
    for j in range(2):
        pick = (place == pos[:, j : j + 1]).astype(BF)
        grad = grad + gate[j] * mm(pick, dxv[...])
    small[2:3, :] = jnp.sum(grad * normed, axis=0, keepdims=True)
    small[3:4, :] = jnp.sum(grad, axis=0, keepdims=True)
    d_resid = gv[...].astype(F32) + norm_back(grad, normed, spread, lying(g2))
    d_res[...] = d_resid
    branch = d_resid.astype(BF)
    loads[3].wait()

    def device_at(n, sign):
        t, other = n // 2, lax.rem(n, 2)
        return lax.rem(pair + far + sign * t, far) * 2 + lax.rem(core + other, 2)

    def give_att(n):
        owner = device_at(n, 1)
        return remote(
            d_att_v.at[owner], d_att.at[h], at_s.at[n], at_r.at[n], {"hidden": owner}
        )

    for n in range(n_h - 1, -1, -1):
        owner = device_at(n, 1)
        block = mm_nt(wo[owner], branch).astype(BF)
        if n == 0:
            d_att[h] = block
        else:
            d_att_v[owner] = block
            give_att(n).start()
    loads[4].wait()
    for t in range(n_h):
        owner = lax.rem(h + t, n_h)
        wo[owner] = mm(att_t[owner], branch).astype(BF)
    for step in list(range(1, far)) + [0]:
        copy = remote(
            wo.at[lax.rem(pair + step, far) * 2 + 1 - core],
            wo_box.at[step],
            wo_s.at[step],
            wo_r.at[step],
            {"hidden": mate},
        )
        copy.start()
        sends.append(copy)
    def give_wo(step):
        target = lax.rem(pair + step, far) * 2 + core
        return remote(
            wo.at[target],
            wo_far.at[step - 1],
            wf_s.at[step],
            wf_r.at[step],
            {"hidden": target},
        )

    for load in loads[5:]:
        load.wait()

    def load_kept(i, turn):
        return pltpu.make_async_copy(weights.at[i], kept.at[turn], kept_sem.at[turn])

    def block_at(at):
        owner = device_at(at // per_device, 1)
        return owner, owner * per_device + lax.rem(at, per_device)

    load_kept(block_at(0)[1], 0).start()
    dk_acc[...] = jnp.zeros_like(dk_acc)
    dv_acc[...] = jnp.zeros_like(dv_acc)

    def turn_values(i, _):
        cols = aligned(i * BLOCK, BLOCK)
        for n in range(heads):
            lo = 2 * width + n * HEAD_DIM
            values[n, cols, :] = qkv[lo : lo + HEAD_DIM, cols].astype(F32).T.astype(BF)
        return 0

    lax.fori_loop(0, blocks, turn_values, 0)

    def over_queries(at, _):
        owner, i = block_at(at)
        turn = lax.rem(at, 2)

        @pl.when(at + 1 < blocks)
        def _next():
            load_kept(block_at(at + 1)[1], 1 - turn).start()

        @pl.when((at >= per_device) & (lax.rem(at, per_device) == 0))
        def _arrive():
            n = at // per_device
            source = lax.rem(far - n // 2, far) * 2 + lax.rem(n, 2)
            give_att(source).wait_recv()

        @pl.when(at == per_device)
        def _weights():
            for step in range(1, far):
                there = wo_box.at[step]
                target = lax.rem(pair + step, far) * 2 + core
                remote(there, there, wo_s.at[step], wo_r.at[step], {"hidden": mate}).wait_recv()
                both = wo[target].astype(F32) + wo_box[step].astype(F32)
                wo[target] = both.astype(BF)
                give_wo(step).start()
            dw_send(1, 0)
            dw_send(1, 1)

        load_kept(i, turn).wait()
        cols = aligned(lax.rem(at, per_device) * BLOCK, BLOCK)
        rows_i = aligned(i * BLOCK, BLOCK)
        given, centre = [], []
        for n in range(heads):
            here = slice(n * HEAD_DIM, (n + 1) * HEAD_DIM)
            scaled = d_att[owner, here, cols].astype(F32) * inverse[n : n + 1, rows_i]
            given.append(scaled.astype(BF))
            product = att_v[owner, here, cols].astype(F32) * scaled
            centre.append(jnp.sum(product, axis=0, keepdims=True))

        def block(span, first):
            attend_back(
                heads,
                i,
                span,
                first,
                qkv,
                given,
                centre,
                kept.at[turn],
                values,
                dq_acc,
                dk_acc,
                dv_acc,
            )

        spans(i, block)
        d_qkv[0:width, rows_i] = (dq_acc[...] * SCALE).astype(BF)
        return 0

    lax.fori_loop(0, blocks, over_queries, 0)
    w_acc[...] = jnp.zeros_like(w_acc)

    def finish(i, _):
        cols = aligned(i * BLOCK, BLOCK)
        d_qkv[width : 2 * width, cols] = dk_acc[:, cols].astype(BF)
        d_qkv[2 * width :, cols] = dv_acc[:, cols].astype(BF)
        block = d_qkv[:, cols]
        grad = mm_tn(block, w_t[...])
        inner = aligned(lax.rem(i, per_device) * BLOCK, BLOCK)
        normed, _unused = norm_parts(tv[i // per_device, inner, :].astype(F32))
        tv[i // per_device, inner, :] = grad.astype(BF)
        small[0:1, :] += jnp.sum(grad * normed, axis=0, keepdims=True)
        small[1:2, :] += jnp.sum(grad, axis=0, keepdims=True)
        hidden = (normed * lying(g1) + lying(s1)).astype(BF)
        w_acc[...] += mm(block, hidden)
        return 0

    lax.fori_loop(0, blocks, finish, 0)
    save_dh = pltpu.make_async_copy(tv, d_hidden, save_sem)
    save_dh.start()
    w_all[0 : 3 * width, :] = w_acc[...].astype(BF)
    there = wo_box.at[0]
    remote(there, there, wo_s.at[0], wo_r.at[0], {"hidden": mate}).wait_recv()
    total = wo[h].astype(F32) + wo_box[0].astype(F32)
    for step in range(1, far):
        give_wo(step).wait_recv()
        total = total + wo_far[step - 1].astype(F32)
    w_all[3 * width :, :] = total.astype(BF)
    load_dw.wait()
    load_far.wait()
    for which in range(2):
        for step in range(1, far):
            for k in range(1 - which, 2):
                dw_across_copy(which, step, k).wait()

        def add_all(n, _, which=which):
            band = aligned(n * 96, 96)
            both = dw_mine[which, band, :].astype(F32)
            for step in range(1, far):
                both = both + dw_across[which, step - 1, band, :].astype(F32)
            dw_own[which, band, :] = both.astype(BF)
            return 0

        lax.fori_loop(0, dw_mine.shape[1] // 96, add_all, 0)
    for step in range(1, n_e):
        there = y_back.at[lax.rem(e + n_e - step, n_e)]
        remote(there, there, y_s.at[step], y_r.at[step], {"expert": e}).wait_recv()
    own_y.wait()
    save_dh.wait()
    for n in range(1, n_h):
        give_att(n).wait_send()
    for step in range(1, far):
        give_wo(step).wait_send()
    for copy in sends:
        copy.wait_send()


def run_back(
    ids,
    slot,
    pos,
    gates,
    count,
    g1,
    s1,
    g2,
    s2,
    w_router,
    inverse,
    dg_rows,
    dx_back,
    y_out,
    dw_sum,
    dw_far,
    out_grad,
    residual,
    all_tokens,
    qkv,
    att,
    att_t,
    w_out,
    w_t,
    weights,
    cid,
):
    n_e, n_h = lax.axis_size("expert"), lax.axis_size("hidden")
    experts, capacity, model = y_out.shape
    padded = dg_rows.shape[2]
    rows = out_grad.shape[0]
    width = w_t.shape[0] // 3
    heads = width // HEAD_DIM
    group, far = rows * n_h, n_h // 2
    shard = dw_sum.shape[2:]
    tall = 8 + experts

    def pairs(*shape):
        return [DMA(shape), DMA(shape)]

    return pl.pallas_call(
        partial(back_body, n_e, n_h, experts, capacity, padded, heads),
        name="back",
        out_shape=[
            shape_of(y_out.shape, BF),
            shape_of((n_h, rows, model), BF),
            shape_of((rows, model), F32),
            shape_of((4 * width, model), BF),
            shape_of((tall, model), F32),
            shape_of((2, *shard), BF),
        ],
        in_specs=[VMEM] * 12 + [ANY] * 13,
        out_specs=[ANY] * 2 + [VMEM] * 4,
        scratch_shapes=[
            pltpu.VMEM((experts * capacity, model), BF),
            pltpu.VMEM((rows, model), BF),
            pltpu.VMEM((rows, model), F32),
            pltpu.VMEM((n_h, rows, model), BF),
            pltpu.VMEM((3 * width, group), BF),
            pltpu.VMEM((n_h, width, rows), BF),
            pltpu.VMEM((n_h, width, rows), BF),
            pltpu.VMEM((n_h, width, model), BF),
            pltpu.VMEM((3 * width, model), BF),
            pltpu.VMEM((n_h, width, rows), BF),
            pltpu.VMEM((n_h, width, rows), BF),
            pltpu.VMEM((far, width, model), BF),
            pltpu.VMEM((far - 1, width, model), BF),
            pltpu.VMEM((2, heads, REACH, BLOCK, BLOCK), BF),
            pltpu.VMEM((heads, group, HEAD_DIM), BF),
            pltpu.VMEM((width, BLOCK), F32),
            pltpu.VMEM((width, group), F32),
            pltpu.VMEM((width, group), F32),
            pltpu.VMEM((3 * width, group), BF),
            pltpu.VMEM((3 * width, model), F32),
            pltpu.VMEM((2, *shard), BF),
            pltpu.VMEM((2, far - 1, *shard), BF),
            DMA((9,)),
            DMA,
            DMA((2,)),
            DMA((2,)),
            DMA,
            *pairs(n_e),
            *pairs(n_h),
            *pairs(far),
            *pairs(far),
            *pairs(2, far, 2),
        ],
        compiler_params=pltpu.CompilerParams(
            collective_id=cid, has_side_effects=True, vmem_limit_bytes=60 << 20
        ),
    )(
        ids,
        slot,
        pos,
        gates,
        count,
        g1,
        s1,
        g2,
        s2,
        w_router,
        inverse,
        dg_rows,
        dx_back.reshape(experts * capacity, model),
        y_out,
        dw_sum,
        dw_far,
        out_grad,
        residual,
        all_tokens,
        qkv,
        att,
        att_t,
        w_out.reshape(n_h, width, model),
        w_t,
        weights,
    )


def shards(
    tokens,
    doc_lengths,
    expert_ids,
    gain_one,
    shift_one,
    w_query,
    w_key,
    w_value,
    w_out,
    gain_two,
    shift_two,
    w_router,
    w_up,
    w_down,
    out_grad,
):
    rows, model = tokens.shape
    n_expert, n_hidden = lax.axis_size("expert"), lax.axis_size("hidden")
    experts = n_expert * w_up.shape[0]
    capacity = max(2, rows * 2 * 5 // (4 * experts))
    capacity = -(-capacity // 16) * 16
    total = experts * capacity
    heads = HEADS // n_hidden
    width = heads * HEAD_DIM
    g1, s1, g2, s2 = gain_one, shift_one, gain_two, shift_two
    router_t = w_router.T

    (
        all_tokens,
        qkv,
        att,
        att_t,
        w_t,
        g_in,
        x_slots,
        ups,
        weights,
        ids,
        pos,
        slot,
        count,
        inverse,
        residual,
        gates,
        gate_rows,
    ) = run_front(
        doc_lengths,
        expert_ids.T,
        g1,
        s1,
        g2,
        s2,
        router_t,
        tokens,
        out_grad,
        (w_query, w_key, w_value, w_out),
        w_up,
        capacity,
        heads,
        1,
    )
    dx_back, dg_back, y_out, dw_sum, dw_far = run_experts(
        x_slots, gate_rows, g_in, ups, w_down, 2
    )
    y_back, d_hidden, d_res, w_all, small, dw_own = run_back(
        ids,
        slot,
        pos,
        gates,
        count,
        g1,
        s1,
        g2,
        s2,
        router_t,
        inverse,
        dg_back,
        dx_back,
        y_out,
        dw_sum,
        dw_far,
        out_grad,
        residual,
        all_tokens,
        qkv,
        att,
        att_t,
        w_out,
        w_t,
        weights,
        3,
    )
    input_grad, output, full, small = run_tail(
        d_hidden,
        w_all.reshape(n_expert, 4 * width // n_expert, model),
        small,
        tokens,
        g1,
        d_res,
        residual,
        gates,
        pos,
        y_back.reshape(total, model),
        4,
    )
    scale = experts / (rows * n_expert * n_hidden * 2)
    turned = turn_weights(
        full.reshape(n_hidden, 4 * width, model),
        dw_own,
        small,
        input_grad,
        output,
        width,
        experts,
        scale,
    )
    w_grads, (up_grad, down_grad) = turned[:4], turned[4:6]
    gain_one_grad, shift_one_grad, gain_two_grad, shift_two_grad = turned[6:10]
    router_grad, input_grad, output, load = turned[10:]
    return (
        output,
        input_grad,
        gain_one_grad,
        shift_one_grad,
        *w_grads,
        gain_two_grad,
        shift_two_grad,
        router_grad.T,
        up_grad[None],
        down_grad[None],
        load,
    )


def solution(mesh):
    in_specs = (
        P(("expert", "hidden"), None),
        P("expert", None),
        P(("expert", "hidden"), None),
        P(),
        P(),
        P(),
        P(),
        P(),
        P(),
        P(),
        P(),
        P(),
        P("expert", None, "hidden"),
        P("expert", "hidden", None),
        P(("expert", "hidden"), None),
    )
    out_specs = (
        P(("expert", "hidden"), None),
        P(("expert", "hidden"), None),
        P(),
        P(),
        P(),
        P(),
        P(),
        P(),
        P(),
        P(),
        P(),
        P("expert", None, "hidden"),
        P("expert", "hidden", None),
        P(),
    )
    return jax.shard_map(shards, mesh=mesh, in_specs=in_specs, out_specs=out_specs, check_vma=False)
```

```python
from functools import partial

import jax
import jax.numpy as jnp
from jax import lax
from jax.experimental import pallas as pl
from jax.experimental.pallas import tpu as pltpu
from jax.sharding import PartitionSpec as P

HEAD_DIM = 64
HEADS = 12
EPSILON = 1e-05
SCALE = 0.125
MASKED = -1e30
BLOCK = 256
LONGEST = 1024
REACH = LONGEST // BLOCK + 1
LANES = 128
BF = jnp.bfloat16
F32 = jnp.float32
I32 = jnp.int32
MESH = pl.DeviceIdType.MESH
ANY = pl.BlockSpec(memory_space=pl.ANY)
SMEM = pl.BlockSpec(memory_space=pltpu.SMEM)
VMEM = pl.BlockSpec(memory_space=pltpu.VMEM)
DMA = pltpu.SemaphoreType.DMA
GELU_A = 0.7978845608028654
GELU_B = 0.044715


def mm(left, right):
    return jnp.dot(left, right, preferred_element_type=F32)


def mm_nt(left, right):
    return lax.dot_general(left, right, (((1,), (1,)), ((), ())), preferred_element_type=F32)


def mm_tn(left, right):
    return lax.dot_general(left, right, (((0,), (0,)), ((), ())), preferred_element_type=F32)


def iota(shape, axis):
    return lax.broadcasted_iota(I32, shape, axis)


def norm_parts(values):
    centred = values - jnp.mean(values, axis=-1, keepdims=True)
    inverse = lax.rsqrt(jnp.mean(centred * centred, axis=-1, keepdims=True) + EPSILON)
    return centred * inverse, inverse


def norm_back(grad_out, normed, inverse, gain):
    grad_normed = grad_out * gain
    first = jnp.mean(grad_normed, axis=-1, keepdims=True)
    second = jnp.mean(grad_normed * normed, axis=-1, keepdims=True)
    return inverse * (grad_normed - first - normed * second)


def split_two(value):
    high = value.astype(BF)
    return high, (value - high.astype(F32)).astype(BF)


def shape_of(shape, dtype):
    return jax.ShapeDtypeStruct(shape, dtype)


def greet(peers):
    barrier = pltpu.get_barrier_semaphore()
    for peer in peers:
        pl.semaphore_signal(barrier, inc=1, device_id=peer, device_id_type=MESH)
    pl.semaphore_wait(barrier, len(peers))


def remote(src, dst, send, recv, peer):
    return pltpu.make_async_remote_copy(
        src_ref=src, dst_ref=dst, send_sem=send, recv_sem=recv, device_id=peer, device_id_type=MESH
    )


def doc_bounds(docs):
    ends, at = [], 0
    for n in range(docs.shape[1] - 1):
        at = at + docs[0, n]
        ends.append(at)
    return ends


def start_of(place, ends):
    begin = jnp.zeros_like(place)
    for end in ends:
        begin = jnp.where(place >= end, end, begin)
    return begin


def lying(ref):
    return ref[...].reshape(1, ref.shape[0])


def aligned(at, size):
    return pl.ds(pl.multiple_of(at, size), size)


def find_slots(experts, capacity, ids, ids_t, pos, slot, count):
    rows = ids_t.shape[1]
    row = [ids_t[j : j + 1, :] for j in range(2)]
    tall = jnp.concatenate([r.astype(F32) for r in row] + [jnp.zeros((6, rows), F32)], axis=0)
    ids[...] = tall.T[:, 0:2].astype(I32)
    col = [ids[:, j : j + 1] for j in range(2)]
    lane = iota((rows, LANES), 1)
    hot = [(lane == c).astype(BF) for c in col]
    either = hot[0] + hot[1]
    below = (iota((rows, rows), 0) > iota((rows, rows), 1)).astype(BF)
    before = mm(below, either)
    wide = max(experts, 16)
    deep = iota((wide, rows), 0)
    hot_t = [(deep == r).astype(BF) for r in row]
    above = (iota((rows, rows), 0) < iota((rows, rows), 1)).astype(BF)
    before_t = mm(hot_t[0] + hot_t[1], above)
    count[...] = jnp.sum(either.astype(F32), axis=0, keepdims=True)
    flat_t = []
    for j in range(2):
        at = jnp.sum(hot[j].astype(F32) * before, axis=1, keepdims=True).astype(I32)
        pos[:, j : j + 1] = col[j] * capacity + at
        slot[:, j : j + 1] = at
        at_t = jnp.sum(hot_t[j].astype(F32) * before_t, axis=0, keepdims=True).astype(I32)
        flat_t.append(row[j] * capacity + at_t)
    return flat_t


def fill_slots(flat_t, source, out):
    total, rows = out.shape[0], source.shape[0]
    half = total // 2
    for n in range(2):
        place = iota((half, rows), 0) + n * half
        pick = ((place == flat_t[0]) | (place == flat_t[1])).astype(BF)
        out[pl.ds(n * half, half), :] = mm(pick, source).astype(BF)


def attend_block(heads, ends, i, span, first, qkv, keys, scores, kept, inverse):
    width = heads * HEAD_DIM
    base = i * BLOCK
    rows = aligned(base, BLOCK)
    q_pos = base + iota((1, BLOCK), 1)
    begin = start_of(q_pos, ends)
    queries = [
        qkv[n * HEAD_DIM : (n + 1) * HEAD_DIM, rows] * jnp.asarray(SCALE, BF) for n in range(heads)
    ]
    tops = [jnp.full((1, BLOCK), MASKED, F32)] * heads
    for k in range(span):
        part = aligned((first + k) * BLOCK, BLOCK)
        k_pos = (first + k) * BLOCK + iota((BLOCK, BLOCK), 0)
        allowed = (k_pos <= q_pos) & (k_pos >= begin)
        for n in range(heads):
            score = jnp.where(allowed, mm(keys[n, part, :], queries[n]), MASKED)
            scores[n, k] = score
            tops[n] = jnp.maximum(tops[n], jnp.max(score, axis=0, keepdims=True))
    result = []
    for n in range(heads):
        total = jnp.zeros((1, BLOCK), F32)
        acc = jnp.zeros((HEAD_DIM, BLOCK), F32)
        lo = 2 * width + n * HEAD_DIM
        for k in range(span):
            weight = jnp.exp(scores[n, k] - tops[n])
            total = total + jnp.sum(weight, axis=0, keepdims=True)
            value = qkv[lo : lo + HEAD_DIM, aligned((first + k) * BLOCK, BLOCK)]
            low = weight.astype(BF)
            kept[n, k] = low
            acc = acc + mm(value, low)
        whole = 1.0 / total
        inverse[n : n + 1, rows] = whole
        result.append((acc * whole).astype(BF))
    return result


def spans(i, body):
    @pl.when(i < 2)
    def _short():
        body(2, 0)

    @pl.when(i >= 2)
    def _long():
        body(REACH, (i - (REACH - 1)) * (i // (REACH - 1)))


def front_body(
    n_e,
    n_h,
    experts,
    capacity,
    padded,
    heads,
    chunks,
    docs,
    ids_t,
    g1,
    s1,
    g2,
    s2,
    w_router,
    tokens,
    out_grad,
    w_query,
    w_key,
    w_value,
    w_out,
    w_up,
    all_tokens,
    qkv_out,
    att_out,
    att_t_out,
    w_t_out,
    g_in,
    x_slots,
    ups,
    weights,
    ids,
    pos,
    slot,
    count,
    inverse,
    residual,
    gates,
    gate_rows,
    tv,
    gv,
    wv,
    wo,
    w_t,
    qkv,
    keys,
    scores,
    kept,
    att_v,
    att_in,
    g_slots,
    xs_v,
    own_sem,
    w_sem,
    save_sem,
    kept_sem,
    ty_s,
    ty_r,
    tc_s,
    tc_r,
    tf_s,
    tf_r,
    gs_s,
    gs_r,
    at_s,
    at_r,
    wy_s,
    wy_r,
    wc_s,
    wc_r,
    wf_s,
    wf_r,
):
    e, h = lax.axis_index("expert"), lax.axis_index("hidden")
    far = n_h // 2
    pair, core = h // 2, lax.rem(h, 2)
    mate = pair * 2 + 1 - core
    rows, model = tokens.shape
    width = heads * HEAD_DIM
    per_device = rows // BLOCK
    ends = doc_bounds(docs)

    def across(t):
        return lax.rem(pair + t, far) * 2 + core

    def origin(t):
        return lax.rem(pair + far - t, far) * 2 + core

    own_tokens = pltpu.make_async_copy(tokens, tv.at[h], own_sem.at[0])
    own_grad = pltpu.make_async_copy(out_grad, gv, own_sem.at[1])
    own_grad.start()
    own_tokens.start()
    w_loads = [
        pltpu.make_async_copy(w, wv.at[n], w_sem.at[n])
        for n, w in enumerate((w_query, w_key, w_value))
    ]
    w_loads.append(pltpu.make_async_copy(w_out, wo, w_sem.at[3]))
    for load in w_loads:
        load.start()
    greet(
        [{"hidden": lax.rem(h + step, n_h)} for step in range(1, n_h)]
        + [{"expert": lax.rem(e + step, n_e)} for step in range(1, n_e)]
    )

    piece = rows // chunks
    sends = []
    for k in range(chunks):
        part = pl.ds(k * piece, piece)
        for t in range(1, far):
            copy = remote(
                tokens.at[part],
                tv.at[h, part],
                ty_s.at[t, k],
                ty_r.at[t, k],
                {"hidden": across(t)},
            )
            copy.start()
            sends.append(copy)
    beside = remote(tokens, tv.at[h], tc_s, tc_r, {"hidden": mate})
    beside.start()
    sends.append(beside)

    flat_t = find_slots(experts, capacity, ids, ids_t, pos, slot, count)
    own_grad.wait()
    fill_slots(flat_t, gv[...], g_slots)
    for step in range(1, n_e):
        peer = lax.rem(e + step, n_e)
        copy = remote(
            g_slots.at[aligned(peer * capacity, capacity)],
            g_in.at[e],
            gs_s.at[step],
            gs_r.at[step],
            {"expert": peer},
        )
        copy.start()
        sends.append(copy)
    own_slots = pltpu.make_async_copy(
        g_slots.at[aligned(e * capacity, capacity)], g_in.at[e], own_sem.at[1]
    )
    own_slots.start()

    def pass_on(t, k):
        part = pl.ds(k * piece, piece)
        place = tv.at[origin(t), part]
        remote(place, place, ty_s.at[t, k], ty_r.at[t, k], {"hidden": across(t)}).wait_recv()
        copy = remote(place, place, tf_s.at[t, k], tf_r.at[t, k], {"hidden": mate})
        copy.start()
        sends.append(copy)

    todo = [(t, k) for k in range(chunks) for t in range(1, far)]
    third = -(-len(todo) // 4)

    def pass_some():
        for _ in range(min(third, len(todo))):
            pass_on(*todo.pop(0))

    pick = (iota((width, model), 1) == iota((width, model), 0) + h * width).astype(BF)
    for n in range(3):
        w_loads[n].wait()
        w_t[n * width : (n + 1) * width, :] = mm_nt(pick, wv[n]).astype(BF)
        if n == 1:
            pass_some()
    save_w = pltpu.make_async_copy(w_t, w_t_out, save_sem.at[0])
    save_w.start()

    def project(source):
        def one(b, _):
            normed, _unused = norm_parts(tv[source, aligned(b * BLOCK, BLOCK), :].astype(F32))
            hidden = (normed * lying(g1) + lying(s1)).astype(BF)
            block = mm_nt(w_t[...], hidden)
            cols = aligned(source * rows + b * BLOCK, BLOCK)
            qkv[:, cols] = block.astype(BF)
            for n in range(heads):
                lo = width + n * HEAD_DIM
                keys[n, cols, :] = block[lo : lo + HEAD_DIM].T.astype(BF)
            return 0

        lax.fori_loop(0, per_device, one, 0)

    pass_some()
    own_tokens.wait()
    project(h)
    pass_some()
    remote(tokens, tv.at[mate], tc_s, tc_r, {"hidden": mate}).wait_recv()
    project(mate)
    while todo:
        pass_some()

    deep = w_up.shape[1] // 2

    def up_part(k):
        return pl.ds(k * deep, deep)

    def up_across(k):
        for t in range(1, far):
            copy = remote(
                w_up.at[0, up_part(k)],
                ups.at[h, up_part(k)],
                wy_s.at[t, k],
                wy_r.at[t, k],
                {"hidden": across(t)},
            )
            copy.start()
            sends.append(copy)

    def up_onward(k):
        for t in range(1, far):
            place = ups.at[origin(t), up_part(k)]
            remote(place, place, wy_s.at[t, k], wy_r.at[t, k], {"hidden": mate}).wait_recv()
            copy = remote(place, place, wf_s.at[t, k], wf_r.at[t, k], {"hidden": mate})
            copy.start()
            sends.append(copy)

    own_up = pltpu.make_async_copy(w_up.at[0], ups.at[h], own_sem.at[2])
    own_up.start()
    up_beside = remote(w_up.at[0], ups.at[h], wc_s, wc_r, {"hidden": mate})
    up_beside.start()
    sends.append(up_beside)
    up_across(0)
    for t in range(1, far):
        project(origin(t))
    for t in range(1, far):
        there = lax.rem(pair + far - t, far) * 2 + 1 - core
        for k in range(chunks):
            place = tv.at[there, pl.ds(k * piece, piece)]
            remote(place, place, tf_s.at[t, k], tf_r.at[t, k], {"hidden": mate}).wait_recv()
        project(there)
    save_tokens = pltpu.make_async_copy(tv, all_tokens, save_sem.at[1])
    save_qkv = pltpu.make_async_copy(qkv, qkv_out, save_sem.at[2])
    save_tokens.start()
    save_qkv.start()

    inverse[...] = jnp.zeros_like(inverse)

    def device_at(n, sign):
        t, other = n // 2, lax.rem(n, 2)
        return lax.rem(pair + far + sign * t, far) * 2 + lax.rem(core + other, 2)

    def give_att(n):
        owner = device_at(n, 1)
        return remote(
            att_v.at[owner], att_in.at[h], at_s.at[n], at_r.at[n], {"hidden": owner}
        )

    def save_kept(i, turn):
        return pltpu.make_async_copy(kept.at[turn], weights.at[i], kept_sem.at[turn])

    def attend(at, _):
        n = n_h - 1 - at // per_device
        b = lax.rem(at, per_device)
        owner = device_at(n, 1)
        i = owner * per_device + b
        turn = lax.rem(at, 2)

        @pl.when(at >= 2)
        def _free():
            save_kept(i, turn).wait()

        def block(span, first):
            done = attend_block(
                heads, ends, i, span, first, qkv, keys, scores, kept.at[turn], inverse
            )
            for m in range(heads):
                lo = m * HEAD_DIM
                att_v[owner, lo : lo + HEAD_DIM, aligned(b * BLOCK, BLOCK)] = done[m]

        spans(i, block)
        save_kept(i, turn).start()

        @pl.when((b == per_device - 1) & (n > 0))
        def _give():
            give_att(n).start()

        return 0

    lax.fori_loop(0, n_h * per_device, attend, 0)
    up_onward(0)
    att_in[h] = att_v[h]
    save_att = pltpu.make_async_copy(att_v, att_out, save_sem.at[3])
    save_att.start()
    for n in range(n_h - 1, 0, -1):
        give_att(n).wait_recv()
    save_att_t = pltpu.make_async_copy(att_in, att_t_out, save_sem.at[4])
    save_att_t.start()

    up_across(1)

    w_loads[3].wait()
    res = tv[h].astype(F32) + mm_tn(att_in[...].reshape(model, rows), wo[...])
    residual[...] = res
    normed, _unused = norm_parts(res)
    hidden = (normed * lying(g2) + lying(s2)).astype(BF)
    fill_slots(flat_t, hidden, xs_v)
    save_x = [
        pltpu.make_async_copy(
            xs_v.at[pl.ds(n * capacity, capacity)], x_slots.at[n], save_sem.at[5 + n]
        )
        for n in range(experts)
    ]
    for save in save_x:
        save.start()
    logits = mm_nt(hidden, w_router[...])
    lane = iota((rows, experts), 1)
    chosen = [
        jnp.sum(jnp.where(lane == ids[:, j : j + 1], logits, 0.0), axis=1, keepdims=True)
        for j in range(2)
    ]
    top = jnp.maximum(chosen[0], chosen[1])
    raised = [jnp.exp(c - top) for c in chosen]
    both = raised[0] + raised[1]
    gate = [r / both for r in raised]
    for j in range(2):
        gates[:, j : j + 1] = gate[j]
    column = iota((rows, padded), 1)
    for n in range(experts):
        mix = jnp.zeros((rows, padded), F32)
        for j in range(2):
            here = jnp.where(ids[:, j : j + 1] == n, slot[:, j : j + 1], -1) == column
            mix = jnp.where(here, gate[j], mix)
        line = jnp.sum(mix, axis=0, keepdims=True)
        gate_rows[n] = jnp.broadcast_to(line, (8, padded))

    up_onward(1)
    place = ups.at[mate]
    remote(place, place, wc_s, wc_r, {"hidden": mate}).wait_recv()
    for k in range(2):
        for t in range(1, far):
            there = lax.rem(pair + far - t, far) * 2 + 1 - core
            place = ups.at[there, up_part(k)]
            remote(place, place, wf_s.at[t, k], wf_r.at[t, k], {"hidden": mate}).wait_recv()
    own_up.wait()
    for step in range(1, n_e):
        source = lax.rem(e + n_e - step, n_e)
        place = g_in.at[source]
        remote(place, place, gs_s.at[step], gs_r.at[step], {"expert": e}).wait_recv()
    own_slots.wait()
    for n in range(1, n_h):
        give_att(n).wait_send()
    for turn in range(2):
        save_kept(0, turn).wait()
    for copy in sends:
        copy.wait_send()
    for save in [save_w, save_tokens, save_qkv, save_att, save_att_t, *save_x]:
        save.wait()


def run_front(
    docs, ids_t, g1, s1, g2, s2, w_router, tokens, out_grad, ws, w_up, capacity, heads, cid
):
    n_e, n_h = lax.axis_size("expert"), lax.axis_size("hidden")
    experts = n_e * w_up.shape[0]
    rows, model = tokens.shape
    padded = -(-capacity // LANES) * LANES
    width, group, total = heads * HEAD_DIM, rows * n_h, experts * capacity
    far, chunks = n_h // 2, 8

    def pairs(*shape):
        return [DMA(shape), DMA(shape)]

    return pl.pallas_call(
        partial(front_body, n_e, n_h, experts, capacity, padded, heads, chunks),
        name="front",
        out_shape=[
            shape_of((n_h, rows, model), BF),
            shape_of((3 * width, group), BF),
            shape_of((n_h, width, rows), BF),
            shape_of((n_h, width, rows), BF),
            shape_of((3 * width, model), BF),
            shape_of((experts, capacity, model), BF),
            shape_of((experts, capacity, model), BF),
            shape_of((n_h, *w_up.shape[1:]), BF),
            shape_of((group // BLOCK, heads, REACH, BLOCK, BLOCK), BF),
            shape_of((rows, 2), I32),
            shape_of((rows, 2), I32),
            shape_of((rows, 2), I32),
            shape_of((1, LANES), F32),
            shape_of((8, group), F32),
            shape_of((rows, model), F32),
            shape_of((rows, 2), F32),
            shape_of((experts, 8, padded), F32),
        ],
        in_specs=[SMEM] + [VMEM] * 6 + [ANY] * 7,
        out_specs=[ANY] * 9 + [VMEM] * 8,
        scratch_shapes=[
            pltpu.VMEM((n_h, rows, model), BF),
            pltpu.VMEM((rows, model), BF),
            pltpu.VMEM((3, model, model), BF),
            pltpu.VMEM((model, model), BF),
            pltpu.VMEM((3 * width, model), BF),
            pltpu.VMEM((3 * width, group), BF),
            pltpu.VMEM((heads, group, HEAD_DIM), BF),
            pltpu.VMEM((heads, REACH, BLOCK, BLOCK), F32),
            pltpu.VMEM((2, heads, REACH, BLOCK, BLOCK), BF),
            pltpu.VMEM((n_h, width, rows), BF),
            pltpu.VMEM((n_h, width, rows), BF),
            pltpu.VMEM((total, model), BF),
            pltpu.VMEM((total, model), BF),
            DMA((4,)),
            DMA((4,)),
            DMA((5 + experts,)),
            DMA((2,)),
            *pairs(far, chunks),
            DMA,
            DMA,
            *pairs(far, chunks),
            *pairs(n_e),
            *pairs(n_h),
            *pairs(far, 2),
            DMA,
            DMA,
            *pairs(far, 2),
        ],
        compiler_params=pltpu.CompilerParams(
            collective_id=cid, has_side_effects=True, vmem_limit_bytes=58 << 20
        ),
    )(docs, ids_t, g1, s1, g2, s2, w_router, tokens, out_grad, *ws, w_up)


def moe_body(
    size,
    capacity,
    padded,
    per,
    x_slots,
    gate_rows,
    g_in,
    ups,
    w_down,
    dx_back,
    dg_back,
    y_out,
    dw_sum,
    dw_far,
    xv,
    gv,
    gates_v,
    up_v,
    down_v,
    act,
    dz,
    xg,
    dy,
    xg_t,
    dy_t,
    dxv,
    yv,
    dgv,
    y_acc,
    dx_acc,
    dw_box,
    load_sem,
    save_sem,
    wy_s,
    wy_r,
    wc_s,
    wc_r,
    wf_s,
    wf_r,
    dc_s,
    dc_r,
    df_s,
    df_r,
    g_sem,
    own_sem,
    xs_sem,
    xr_sem,
    gs_sem,
    gr_sem,
    ds_sem,
    dr_sem,
    ts_sem,
    tr_sem,
    out_sem,
):
    me, h = lax.axis_index("expert"), lax.axis_index("hidden")
    shards_n = ups.shape[0]
    far = shards_n // 2
    pair, core = h // 2, lax.rem(h, 2)
    mate = pair * 2 + 1 - core
    deep = w_down.shape[1] // 2
    tall = per * capacity
    steps = size // per

    middle = size // 2
    inner = lax.rem((me // 2 * 8 // size + 1) // 2, 2)

    def group_at(step):
        late = jnp.where(step <= steps // 2, step - 1 + steps // 2, step - steps // 2)
        return jnp.where((inner == 1) & (step > 0), late, step)

    def peer_at(p):
        peer, bit = 0, 1
        while bit < size:
            peer = peer + lax.rem(me // bit + p // bit, 2) * bit
            bit *= 2
        return peer

    def rows_of(p):
        return pl.ds(pl.multiple_of(p * capacity, capacity), capacity)

    def send_x(p):
        peer = peer_at(p)
        return remote(
            x_slots.at[peer], xv.at[rows_of(p)], xs_sem.at[p], xr_sem.at[p], {"expert": peer}
        )

    def send_gate(p):
        peer = peer_at(p)
        return remote(
            gate_rows.at[peer], gates_v.at[p], gs_sem.at[p], gr_sem.at[p], {"expert": peer}
        )

    def send_dx(p):
        peer = peer_at(p)
        return remote(
            dxv.at[rows_of(p)], dx_back.at[me], ds_sem.at[p], dr_sem.at[p], {"expert": peer}
        )

    def send_dg(p):
        peer = peer_at(p)
        return remote(dgv.at[p], dg_back.at[me], ts_sem.at[p], tr_sem.at[p], {"expert": peer})

    def load_g(p):
        return pltpu.make_async_copy(g_in.at[peer_at(p)], gv.at[rows_of(p)], g_sem.at[p])

    def save_y(p):
        return pltpu.make_async_copy(yv.at[rows_of(p)], y_out.at[peer_at(p)], out_sem.at[p])

    own_x = pltpu.make_async_copy(x_slots.at[me], xv.at[rows_of(0)], own_sem.at[0])
    own_gate = pltpu.make_async_copy(gate_rows.at[me], gates_v.at[0], own_sem.at[1])
    own_dx = pltpu.make_async_copy(dxv.at[rows_of(0)], dx_back.at[me], own_sem.at[2])
    own_dg = pltpu.make_async_copy(dgv.at[0], dg_back.at[me], own_sem.at[3])
    load_up = pltpu.make_async_copy(ups, up_v, load_sem.at[0])
    load_down = pltpu.make_async_copy(w_down.at[0], down_v.at[h], load_sem.at[1])

    def half(k):
        return aligned(k * deep, deep)

    def down_across(t, k):
        there = {"hidden": lax.rem(pair + t, far) * 2 + core}
        return remote(
            w_down.at[0, half(k)], down_v.at[h, half(k)], wy_s.at[t, k], wy_r.at[t, k], there
        )

    def down_onward(t, k):
        place = down_v.at[lax.rem(pair + far - t, far) * 2 + core, half(k)]
        return remote(place, place, wf_s.at[t, k], wf_r.at[t, k], {"hidden": mate})

    down_beside = remote(w_down.at[0], down_v.at[h], wc_s, wc_r, {"hidden": mate})
    own_x.start()
    own_gate.start()
    for p in range(size):
        load_g(p).start()
    load_up.start()
    load_down.start()
    greet(
        [{"expert": lax.rem(me + step, size)} for step in range(1, size)]
        + [{"hidden": lax.rem(h + step, shards_n)} for step in range(1, shards_n)]
    )

    def send_all(order):
        for p in order:
            send_x(p).start()
            send_gate(p).start()

    @pl.when(inner == 1)
    def _far_first():
        send_all([1, *range(middle, size), *range(2, middle)])

    @pl.when(inner == 0)
    def _near_first():
        send_all(range(1, size))

    for k in range(2):
        for t in range(1, far):
            down_across(t, k).start()
    down_beside.start()
    own_x.wait()
    own_gate.wait()
    load_up.wait()
    load_down.wait()

    def step_body(step, _):
        group = group_at(step)
        base = group * per
        for s in range(per):

            @pl.when(base + s > 0)
            def _arrive(s=s):
                send_x(base + s).wait_recv()
                send_gate(base + s).wait_recv()

            load_g(base + s).wait()
        rows = pl.ds(pl.multiple_of(group * tall, tall), tall)
        x, g = xv[rows, :], gv[rows, :]
        y_acc[...] = jnp.zeros_like(y_acc)
        dx_acc[...] = jnp.zeros_like(dx_acc)

        def shard_body(n, _):
            t = n // 2
            beside = lax.rem(n, 2)
            c = lax.rem(pair + far - t, far) * 2 + lax.rem(core + beside, 2)

            @pl.when((step == 0) & (n == 1))
            def _beside():
                down_beside.wait_recv()

            @pl.when((step == 0) & (n >= 2) & (beside == 0))
            def _across():
                for k in range(2):
                    down_across(t, k).wait_recv()
                    down_onward(t, k).start()

            @pl.when((step == 0) & (n >= 2) & (beside == 1))
            def _onward():
                for k in range(2):
                    down_onward(t, k).wait_recv()

            z = mm(x, up_v[c])
            du = mm_nt(g, down_v[c])
            square = z * z
            curve = jnp.tanh(z * (GELU_A + GELU_A * GELU_B * square))
            plus = 0.5 + 0.5 * curve
            hidden = (z * plus).astype(BF)
            rise = GELU_A + 3.0 * GELU_A * GELU_B * square
            slope = plus + 0.5 * z * (1.0 - curve * curve) * rise
            back = (slope * du).astype(BF)
            act[c, rows, :] = hidden
            dz[c, rows, :] = back
            y_acc[...] += mm(hidden, down_v[c])
            dx_acc[...] += mm_nt(back, up_v[c])
            return 0

        lax.fori_loop(0, shards_n, shard_body, 0)
        dxv[rows, :] = dx_acc[...].astype(BF)
        y_low = y_acc[...].astype(BF)
        yv[rows, :] = y_low
        dots = jnp.sum(y_low.astype(F32) * g.astype(F32), axis=1, keepdims=True)
        for s in range(per):
            p = base + s
            part = slice(s * capacity, (s + 1) * capacity)
            tall_dots = jnp.broadcast_to(dots[part], (capacity, LANES))
            if padded > capacity:
                blank = jnp.zeros((padded - capacity, LANES), F32)
                tall_dots = jnp.concatenate([tall_dots, blank], axis=0)
            dgv[p] = tall_dots.T[0:8]

            @pl.when(p > 0)
            def _give(p=p):
                send_dx(p).start()
                send_dg(p).start()

            @pl.when(p == 0)
            def _keep():
                own_dx.start()
                own_dg.start()

            save_y(p).start()
        for s in range(per):
            p = base + s
            part = slice(s * capacity, (s + 1) * capacity)
            gate = gates_v[p].T[0:capacity, 0:1]
            xg[rows_of(p), :] = (x[part].astype(F32) * gate).astype(BF)
            dy[rows_of(p), :] = (g[part].astype(F32) * gate).astype(BF)
        return 0

    lax.fori_loop(0, steps, step_body, 0)

    total = size * capacity
    turn = 256
    for k in range(total // turn):
        rows = slice(k * turn, (k + 1) * turn)
        xg_t[:, rows] = xg[rows, :].astype(F32).T.astype(BF)
        dy_t[:, rows] = dy[rows, :].astype(F32).T.astype(BF)
    model = xg_t.shape[0]
    bands = model // turn

    for t in range(1, far):
        for k in range(2):
            down_across(t, k).wait_send()
            down_onward(t, k).wait_send()
    down_beside.wait_send()

    def give(which, step):
        source = (up_v, down_v)[which].at[lax.rem(pair + step, far) * 2 + 1 - core]
        return remote(
            source,
            dw_box.at[which, step],
            dc_s.at[which, step],
            dc_r.at[which, step],
            {"hidden": mate},
        )

    def keep(which, step):
        source = (up_v, down_v)[which].at[lax.rem(pair + step, far) * 2 + core]
        return pltpu.make_async_copy(source, dw_sum.at[which, step], save_sem.at[which, step])

    def cross(step, k):
        there = lax.rem(pair + step, far) * 2 + core
        return remote(
            up_v.at[there, half(k)],
            dw_far.at[step - 1, half(k)],
            df_s.at[step, k],
            df_r.at[step, k],
            {"hidden": there},
        )

    def gradients(n, _):
        band, kind = lax.rem(n, bands), lax.rem(n // bands, 2)
        step = lax.rem(n // (2 * bands) + 1, far)
        c = lax.rem(pair + step, far) * 2 + lax.rem(core + 1 + kind, 2)
        lines = aligned(band * turn, turn)
        up = mm(xg_t[lines, :], dz[c])
        down = mm(dy_t[lines, :], act[c])

        @pl.when(kind == 0)
        def _other():
            up_v[c, lines, :] = up.astype(BF)
            down_v[c, lines, :] = down.astype(BF)

        @pl.when((kind == 0) & (band == bands - 1))
        def _give():
            for which in range(2):
                give(which, step).start()

        @pl.when((kind == 1) & (band == 0))
        def _take():
            for which in range(2):
                give(which, step).wait_recv()

        @pl.when(kind == 1)
        def _own():
            up_v[c, lines, :] = (up + dw_box[0, step, lines, :].astype(F32)).astype(BF)
            down_v[c, lines, :] = (down + dw_box[1, step, lines, :].astype(F32)).astype(BF)

        @pl.when((kind == 1) & (band == bands - 1))
        def _keep():
            for which in range(2):
                keep(which, step).start()

        @pl.when((kind == 1) & (band == bands - 1) & (step > 0))
        def _cross():
            for k in range(2):
                cross(step, k).start()

        return 0

    lax.fori_loop(0, 2 * far * bands, gradients, 0)
    for p in range(1, size):
        send_x(p).wait_send()
        send_gate(p).wait_send()
        send_dx(p).wait()
        send_dg(p).wait()
    for p in range(size):
        save_y(p).wait()
    own_dx.wait()
    own_dg.wait()
    for step in range(far):
        for which in range(2):
            give(which, step).wait_send()
            keep(which, step).wait()
    for step in range(1, far):
        for k in range(2):
            cross(step, k).wait()


def run_experts(x_slots, gate_rows, g_in, ups, w_down, cid):
    size = lax.axis_size("expert")
    experts, capacity, model = x_slots.shape
    padded = gate_rows.shape[2]
    shards_n, _unused, width = ups.shape
    total = experts * capacity
    per = 1
    while per * 2 * capacity <= 320 and size % (per * 2) == 0:
        per *= 2
    tall = per * capacity
    rows2 = (total, model)
    return pl.pallas_call(
        partial(moe_body, size, capacity, padded, per),
        name="experts",
        out_shape=[
            shape_of(x_slots.shape, BF),
            shape_of(gate_rows.shape, F32),
            shape_of(x_slots.shape, BF),
            shape_of((2, shards_n // 2, model, width), BF),
            shape_of((shards_n // 2 - 1, model, width), BF),
        ],
        in_specs=[ANY] * 5,
        out_specs=[ANY] * 5,
        scratch_shapes=[
            pltpu.VMEM(rows2, BF),
            pltpu.VMEM(rows2, BF),
            pltpu.VMEM(gate_rows.shape, F32),
            pltpu.VMEM((shards_n, model, width), BF),
            pltpu.VMEM((shards_n, width, model), BF),
            pltpu.VMEM((shards_n, total, width), BF),
            pltpu.VMEM((shards_n, total, width), BF),
            pltpu.VMEM(rows2, BF),
            pltpu.VMEM(rows2, BF),
            pltpu.VMEM((model, total), BF),
            pltpu.VMEM((model, total), BF),
            pltpu.VMEM(rows2, BF),
            pltpu.VMEM(rows2, BF),
            pltpu.VMEM(gate_rows.shape, F32),
            pltpu.VMEM((tall, model), F32),
            pltpu.VMEM((tall, model), F32),
            pltpu.VMEM((2, shards_n // 2, model, width), BF),
            DMA((2,)),
            DMA((2, shards_n // 2)),
            DMA((shards_n // 2, 2)),
            DMA((shards_n // 2, 2)),
            DMA,
            DMA,
            DMA((shards_n // 2, 2)),
            DMA((shards_n // 2, 2)),
            DMA((2, shards_n // 2)),
            DMA((2, shards_n // 2)),
            DMA((shards_n // 2, 2)),
            DMA((shards_n // 2, 2)),
            DMA((size,)),
            DMA((4,)),
        ]
        + [DMA((size,))] * 9,
        compiler_params=pltpu.CompilerParams(
            collective_id=cid, has_side_effects=True, vmem_limit_bytes=60 << 20
        ),
        cost_estimate=pl.CostEstimate(
            flops=12 * total * model * width * shards_n, bytes_accessed=40 << 20, transcendentals=0
        ),
    )(x_slots, gate_rows, g_in, ups, w_down)


def tail_body(
    n_e,
    n_h,
    chunks,
    dh,
    w_all,
    small,
    tokens,
    gain,
    d_res,
    residual,
    gates,
    pos,
    y_back,
    input_grad,
    output,
    full,
    total,
    wv,
    tok_v,
    d_res_v,
    res_v,
    yv,
    mine,
    beside,
    across,
    passing,
    x_box,
    z_box,
    w_mid,
    piece,
    small_mid,
    small_h,
    small_e,
    load_sem,
    mine_sem,
    cs_sem,
    cr_sem,
    as_sem,
    ar_sem,
    ws_sem,
    wr_sem,
    vs_sem,
    vr_sem,
    hs_sem,
    hr_sem,
    es_sem,
    er_sem,
    keep_sem,
    zs_sem,
    zr_sem,
    xs_sem,
    xr_sem,
    ys_sem,
    yr_sem,
    ms_sem,
    mr_sem,
):
    e, h = lax.axis_index("expert"), lax.axis_index("hidden")
    far, high = n_h // 2, n_e // 2
    pair, core = h // 2, lax.rem(h, 2)
    eh, el = e // 2, lax.rem(e, 2)
    mate = pair * 2 + 1 - core
    greet(
        [{"expert": lax.rem(e + step, n_e)} for step in range(1, n_e)]
        + [{"hidden": lax.rem(h + step, n_h)} for step in range(1, n_h)]
    )
    w_sends, w_order = {}, list(range(1, high)) + [0]
    for step in w_order:
        there = lax.rem(eh + step, high)
        copy = remote(
            w_all.at[there * 2 + 1 - el],
            x_box.at[step],
            ws_sem.at[step],
            wr_sem.at[step],
            {"expert": eh * 2 + 1 - el},
        )
        copy.start()
        w_sends[step] = copy
    rows = dh.shape[1] // chunks
    core_sends = {}
    for step in list(range(1, far)) + [0]:
        there = lax.rem(pair + step, far)
        for k in range(chunks):
            part = pl.ds(k * rows, rows)
            copy = remote(
                dh.at[there * 2 + 1 - core, part],
                beside.at[step, part],
                cs_sem.at[step, k],
                cr_sem.at[step, k],
                {"hidden": mate},
            )
            copy.start()
            core_sends[step, k] = copy
    mine_loads = []
    for step in range(far):
        there = lax.rem(pair + step, far)
        load = pltpu.make_async_copy(dh.at[there * 2 + core], mine.at[step], mine_sem.at[step])
        load.start()
        mine_loads.append(load)
    loads = [
        pltpu.make_async_copy(source, target, load_sem.at[n])
        for n, (source, target) in enumerate(
            ((w_all, wv), (residual, res_v), (y_back, yv), (tokens, tok_v), (d_res, d_res_v))
        )
    ]
    for load in loads:
        load.start()
    for load in mine_loads:
        load.wait()
    far_sends = []
    for step in range(1, far):
        there = lax.rem(pair + step, far)
        for k in range(chunks):
            part = pl.ds(k * rows, rows)
            core_sends[step, k].wait_recv()
            both = mine[step, part, :].astype(F32) + beside[step, part, :].astype(F32)
            passing[step - 1, part, :] = both.astype(BF)
            copy = remote(
                passing.at[step - 1, part],
                across.at[step - 1, part],
                as_sem.at[step - 1, k],
                ar_sem.at[step - 1, k],
                {"hidden": there * 2 + core},
            )
            copy.start()
            far_sends.append(copy)
    loads[0].wait()
    v_sends = []
    for step in w_order[:-1]:
        there = lax.rem(eh + step, high) * 2 + el
        w_sends[step].wait_recv()
        w_mid[step - 1] = (wv[there].astype(F32) + x_box[step].astype(F32)).astype(BF)
        copy = remote(
            w_mid.at[step - 1],
            z_box.at[step - 1],
            vs_sem.at[step],
            vr_sem.at[step],
            {"expert": there},
        )
        copy.start()
        v_sends.append(copy)
    small_sends = []
    for at in range(n_h - 1):
        peer = lax.rem(h + 1 + at, n_h)
        copy = remote(small, small_h.at[at], hs_sem.at[at], hr_sem.at[at], {"hidden": peer})
        copy.start()
        small_sends.append(copy)
    w_sends[0].wait_recv()
    acc = wv[e].astype(F32) + x_box[0].astype(F32)
    for at, copy in enumerate(v_sends):
        copy.wait_recv()
        acc = acc + z_box[at].astype(F32)
    piece[...] = acc.astype(BF)
    keep = pltpu.make_async_copy(piece, full.at[h, e], keep_sem)
    keep.start()
    started = []

    def slot(eh_of, el_of, pair_of, core_of):
        return full.at[pair_of * 2 + core_of, eh_of * 2 + el_of]

    def back(step, size, place):
        return lax.rem(place + size - step, size)

    def give_z(source):
        for s in range(1, high):
            there = lax.rem(eh + s, high) * 2 + el
            copy = remote(
                source, slot(eh, el, pair, core), zs_sem.at[s], zr_sem.at[s], {"expert": there}
            )
            copy.start()
            started.append(copy)

    def z_arrival(s):
        place = slot(back(s, high, eh), el, pair, core)
        return place, remote(place, place, zs_sem.at[s], zr_sem.at[s], {"expert": e})

    def give_x(source, s):
        target = slot(back(s, high, eh), el, pair, core)
        copy = remote(
            source, target, xs_sem.at[s], xr_sem.at[s], {"expert": eh * 2 + 1 - el}
        )
        copy.start()
        started.append(copy)

    def x_arrival(s):
        place = slot(back(s, high, eh), 1 - el, pair, core)
        return place, remote(place, place, xs_sem.at[s], xr_sem.at[s], {"expert": e})

    def give_y(source, s, flag):
        target = slot(back(s, high, eh), el if flag == 0 else 1 - el, pair, core)
        for t in range(1, far):
            there = lax.rem(pair + t, far) * 2 + core
            at = 2 * s + flag
            copy = remote(
                source, target, ys_sem.at[t, at], yr_sem.at[t, at], {"hidden": there}
            )
            copy.start()
            started.append(copy)

    def y_arrival(t, s, flag):
        other = el if flag == 0 else 1 - el
        place = slot(back(s, high, eh), other, back(t, far, pair), core)
        at = 2 * s + flag
        return place, remote(place, place, ys_sem.at[t, at], yr_sem.at[t, at], {"hidden": h})

    def give_mate(source, t, s, flag):
        other = el if flag == 0 else 1 - el
        target = slot(back(s, high, eh), other, back(t, far, pair), core)
        at = 2 * s + flag
        copy = remote(source, target, ms_sem.at[t, at], mr_sem.at[t, at], {"hidden": mate})
        copy.start()
        started.append(copy)

    def mate_arrival(t, s, flag):
        other = el if flag == 0 else 1 - el
        place = slot(back(s, high, eh), other, back(t, far, pair), 1 - core)
        at = 2 * s + flag
        return place, remote(place, place, ms_sem.at[t, at], mr_sem.at[t, at], {"hidden": h})

    give_z(piece)
    give_x(piece, 0)
    give_y(piece, 0, 0)
    give_mate(piece, 0, 0, 0)
    arrived = [(0, 0)]

    def take_x(s):
        place, arrival = x_arrival(s)
        arrival.wait_recv()
        give_y(place, s, 1)
        give_mate(place, 0, s, 1)
        arrived.append((s, 1))

    for s in range(1, high):
        place, arrival = z_arrival(s)
        arrival.wait_recv()
        give_x(place, s)
        give_y(place, s, 0)
        give_mate(place, 0, s, 0)
        arrived.append((s, 0))
        take_x(s - 1)
    take_x(high - 1)
    for copy in small_sends:
        copy.wait_recv()
    summed = small[...]
    for at in range(n_h - 1):
        summed = summed + small_h[at]
    small_mid[...] = summed
    small_out = []
    for at in range(n_e - 1):
        peer = lax.rem(e + 1 + at, n_e)
        copy = remote(small_mid, small_e.at[at], es_sem.at[at], er_sem.at[at], {"expert": peer})
        copy.start()
        small_out.append(copy)
    for load in loads[1:]:
        load.wait()
    place_of = iota((residual.shape[0], y_back.shape[0]), 1)
    result = res_v[...]
    for j in range(2):
        pick = (place_of == pos[:, j : j + 1]).astype(BF)
        result = result + gates[:, j : j + 1] * mm(pick, yv[...])
    output[...] = result.astype(BF)
    for k in range(chunks):
        part = pl.ds(k * rows, rows)
        core_sends[0, k].wait_recv()
    for copy in far_sends:
        copy.wait_recv()
    grad = mine[0].astype(F32) + beside[0].astype(F32)
    for step in range(far - 1):
        grad = grad + across[step].astype(F32)
    normed, inverse = norm_parts(tok_v[...].astype(F32))
    input_grad[...] = (d_res_v[...] + norm_back(grad, normed, inverse, lying(gain))).astype(BF)
    for t in range(1, far):
        for s, flag in arrived:
            place, arrival = y_arrival(t, s, flag)
            arrival.wait_recv()
            give_mate(place, t, s, flag)
    for copy in small_out:
        copy.wait_recv()
    summed = small_mid[...]
    for at in range(n_e - 1):
        summed = summed + small_e[at]
    total[...] = summed
    for t in range(far):
        for s, flag in arrived:
            _place, arrival = mate_arrival(t, s, flag)
            arrival.wait_recv()
    keep.wait()
    for copy in [*started, *w_sends.values(), *v_sends, *small_sends, *small_out, *far_sends]:
        copy.wait_send()
    for copy in core_sends.values():
        copy.wait_send()


def run_tail(dh, w_all, small, tokens, gain, d_res, residual, gates, pos, y_back, cid):
    n_e, n_h = lax.axis_size("expert"), lax.axis_size("hidden")
    far, high = n_h // 2, n_e // 2
    chunks = 4
    _unused, rows, model = dh.shape
    piece = w_all.shape[1:]
    return pl.pallas_call(
        partial(tail_body, n_e, n_h, chunks),
        name="tail",
        out_shape=[
            shape_of((rows, model), BF),
            shape_of((rows, model), BF),
            shape_of((n_h, n_e, *piece), BF),
            shape_of(small.shape, F32),
        ],
        in_specs=[ANY, ANY, VMEM, ANY, VMEM, ANY, ANY, VMEM, VMEM, ANY],
        out_specs=[VMEM, VMEM, ANY, VMEM],
        scratch_shapes=[
            pltpu.VMEM(w_all.shape, BF),
            pltpu.VMEM(tokens.shape, BF),
            pltpu.VMEM(d_res.shape, F32),
            pltpu.VMEM(residual.shape, F32),
            pltpu.VMEM(y_back.shape, BF),
            pltpu.VMEM((far, rows, model), BF),
            pltpu.VMEM((far, rows, model), BF),
            pltpu.VMEM((far - 1, rows, model), BF),
            pltpu.VMEM((far - 1, rows, model), BF),
            pltpu.VMEM((high, *piece), BF),
            pltpu.VMEM((high - 1, *piece), BF),
            pltpu.VMEM((high - 1, *piece), BF),
            pltpu.VMEM(piece, BF),
            pltpu.VMEM(small.shape, F32),
            pltpu.VMEM((n_h - 1, *small.shape), F32),
            pltpu.VMEM((n_e - 1, *small.shape), F32),
            DMA((5,)),
            DMA((far,)),
            DMA((far, chunks)),
            DMA((far, chunks)),
            DMA((far - 1, chunks)),
            DMA((far - 1, chunks)),
            DMA((high,)),
            DMA((high,)),
            DMA((high,)),
            DMA((high,)),
            DMA((n_h - 1,)),
            DMA((n_h - 1,)),
            DMA((n_e - 1,)),
            DMA((n_e - 1,)),
            DMA,
            DMA((high,)),
            DMA((high,)),
            DMA((high,)),
            DMA((high,)),
            DMA((far, n_e)),
            DMA((far, n_e)),
            DMA((far, n_e)),
            DMA((far, n_e)),
        ],
        compiler_params=pltpu.CompilerParams(
            collective_id=cid, has_side_effects=True, vmem_limit_bytes=56 << 20
        ),
    )(dh, w_all, small, tokens, gain, d_res, residual, gates, pos, y_back)


def turn_body(
    width,
    experts,
    scale,
    full,
    dw,
    small,
    input_grad,
    output,
    q_out,
    k_out,
    v_out,
    o_out,
    up_out,
    down_out,
    g1_out,
    s1_out,
    g2_out,
    s2_out,
    router_out,
    input_out,
    output_out,
    load_out,
):
    @pl.when(pl.program_id(0) == 0)
    def _begin():
        input_out[...] = input_grad[...]
        output_out[...] = output[...]
        for n, out in enumerate((g1_out, s1_out, g2_out, s2_out)):
            out[...] = small[n : n + 1, :].reshape(out.shape)
        router_out[...] = small[8 : 8 + experts, :]
        load_out[...] = small[4:5, 0:experts].reshape(experts) * scale

    for n, out in enumerate((q_out, k_out, v_out)):
        part = full[:, n * width : (n + 1) * width, :].astype(F32)
        out[...] = part.reshape(-1, part.shape[2]).T
    part = full[:, 3 * width :, :].astype(F32)
    o_out[...] = part.reshape(-1, part.shape[2])
    trained = jnp.where(lax.axis_index("expert") >= experts // 2, 1.0, 0.0)
    up_out[...] = dw[0].astype(F32) * trained
    down_out[...] = dw[1].astype(F32).T * trained


def turn_weights(full, dw, small, input_grad, output, width, experts, scale):
    n_h, deep, model = full.shape
    cols = 128
    across = pl.BlockSpec((cols, model), lambda i: (i, 0))
    down = pl.BlockSpec((model, cols), lambda i: (0, i))
    flat = pl.BlockSpec((model,), lambda i: (0,))
    whole = pl.BlockSpec(output.shape, lambda i: (0, 0))
    square = shape_of((model, model), F32)
    return pl.pallas_call(
        partial(turn_body, width, experts, scale),
        name="turn_weights",
        grid=(model // cols,),
        out_shape=[square] * 6
        + [shape_of((model,), F32)] * 4
        + [
            shape_of((experts, model), F32),
            shape_of(input_grad.shape, BF),
            shape_of(output.shape, BF),
            shape_of((experts,), F32),
        ],
        in_specs=[
            pl.BlockSpec((n_h, deep, cols), lambda i: (0, 0, i)),
            pl.BlockSpec((2, model, cols), lambda i: (0, 0, i)),
            pl.BlockSpec(small.shape, lambda i: (0, 0)),
            whole,
            whole,
        ],
        out_specs=[across, across, across, down, down, across]
        + [flat] * 4
        + [pl.BlockSpec((experts, model), lambda i: (0, 0)), whole, whole]
        + [pl.BlockSpec((experts,), lambda i: (0,))],
        compiler_params=pltpu.CompilerParams(
            dimension_semantics=("arbitrary",), vmem_limit_bytes=60 << 20
        ),
        cost_estimate=pl.CostEstimate(flops=0, bytes_accessed=24 << 20, transcendentals=0),
    )(full, dw, small, input_grad, output)


def attend_back(
    heads, i, span, first, qkv, given, centre, kept, values, dq_acc, dk_acc, dv_acc
):
    width = heads * HEAD_DIM
    rows = aligned(i * BLOCK, BLOCK)
    dq_acc[...] = jnp.zeros_like(dq_acc)
    queries = [
        qkv[n * HEAD_DIM : (n + 1) * HEAD_DIM, rows] * jnp.asarray(SCALE, BF) for n in range(heads)
    ]
    for k in range(span):
        part = aligned((first + k) * BLOCK, BLOCK)
        for n in range(heads):
            here = slice(n * HEAD_DIM, (n + 1) * HEAD_DIM)
            weight = kept[n, k]
            d_weight = mm(values[n, part, :], given[n])
            d_score = (weight.astype(F32) * (d_weight - centre[n])).astype(BF)
            dv_acc[here, part] += mm_nt(given[n], weight)
            dk_acc[here, part] += mm_nt(queries[n], d_score)
            lo = width + n * HEAD_DIM
            dq_acc[here, :] += mm(qkv[lo : lo + HEAD_DIM, part], d_score)


def back_body(
    n_e,
    n_h,
    experts,
    capacity,
    padded,
    heads,
    ids,
    slot,
    pos,
    gates,
    count,
    g1,
    s1,
    g2,
    s2,
    w_router,
    inverse,
    dg_rows,
    dx_back,
    y_out,
    dw_sum,
    dw_far,
    out_grad,
    residual,
    all_tokens,
    qkv_in,
    att_in,
    att_t_in,
    w_out,
    w_t_in,
    weights,
    y_back,
    d_hidden,
    d_res,
    w_all,
    small,
    dw_own,
    dxv,
    gv,
    res_v,
    tv,
    qkv,
    att_v,
    att_t,
    wo,
    w_t,
    d_att_v,
    d_att,
    wo_box,
    wo_far,
    kept,
    values,
    dq_acc,
    dk_acc,
    dv_acc,
    d_qkv,
    w_acc,
    dw_mine,
    dw_across,
    load_sem,
    save_sem,
    dw_sem,
    kept_sem,
    y_own,
    y_s,
    y_r,
    at_s,
    at_r,
    wo_s,
    wo_r,
    wf_s,
    wf_r,
    da_s,
    da_r,
):
    e, h = lax.axis_index("expert"), lax.axis_index("hidden")
    far = n_h // 2
    pair, core = h // 2, lax.rem(h, 2)
    mate = pair * 2 + 1 - core
    rows, model = out_grad.shape
    width = heads * HEAD_DIM
    group = rows * n_h
    per_device = rows // BLOCK
    blocks = group // BLOCK
    sends = []

    loads = [
        pltpu.make_async_copy(source, target, load_sem.at[n])
        for n, (source, target) in enumerate(
            (
                (residual, res_v),
                (dx_back, dxv),
                (out_grad, gv),
                (w_out, wo),
                (att_t_in, att_t),
                (qkv_in, qkv),
                (att_in, att_v),
                (all_tokens, tv),
                (w_t_in, w_t),
            )
        )
    ]
    for load in loads:
        load.start()
    greet(
        [{"hidden": lax.rem(h + step, n_h)} for step in range(1, n_h)]
        + [{"expert": lax.rem(e + step, n_e)} for step in range(1, n_e)]
    )
    load_dw = pltpu.make_async_copy(dw_sum.at[:, 0], dw_mine, dw_sem.at[0])
    load_dw.start()
    deep = dw_mine.shape[1] // 2
    load_far = pltpu.make_async_copy(
        dw_far, dw_across.at[0], dw_sem.at[1]
    )
    load_far.start()

    def dw_across_copy(step, k):
        part = pl.ds(k * deep, deep)
        return remote(
            dw_sum.at[1, step, part],
            dw_across.at[1, step - 1, part],
            da_s.at[step, k],
            da_r.at[step, k],
            {"hidden": lax.rem(pair + step, far) * 2 + core},
        )

    def dw_send(k):
        for step in range(1, far):
            dw_across_copy(step, k).start()

    dw_send(0)
    for step in range(1, n_e):
        peer = lax.rem(e + step, n_e)
        copy = remote(y_out.at[peer], y_back.at[e], y_s.at[step], y_r.at[step], {"expert": peer})
        copy.start()
        sends.append(copy)
    own_y = pltpu.make_async_copy(y_out.at[e], y_back.at[e], y_own)
    own_y.start()

    for load in loads[:3]:
        load.wait()
    normed, spread = norm_parts(res_v[...])
    hidden = (normed * lying(g2) + lying(s2)).astype(BF)
    gate = [gates[:, j : j + 1] for j in range(2)]
    column = iota((rows, padded), 1)
    dot_of = []
    for j in range(2):
        mix = jnp.zeros((rows, padded), F32)
        for n in range(experts):
            here = jnp.where(ids[:, j : j + 1] == n, slot[:, j : j + 1], -1) == column
            mix = jnp.where(here, dg_rows[n, 0:1, :], mix)
        dot_of.append(jnp.sum(mix, axis=1, keepdims=True))
    mean = gate[0] * dot_of[0] + gate[1] * dot_of[1]
    lane = iota((rows, experts), 1)
    d_logits = jnp.zeros((rows, experts), F32)
    for j in range(2):
        d_logits = jnp.where(lane == ids[:, j : j + 1], gate[j] * (dot_of[j] - mean), d_logits)
    high, low = split_two(d_logits)
    grad = mm(high, w_router[...]) + mm(low, w_router[...])
    small[...] = jnp.zeros_like(small)
    small[8 : 8 + experts, :] = mm_tn(high, hidden) + mm_tn(low, hidden)
    small[4:5, 0:LANES] = count[...]
    place = iota((rows, experts * capacity), 1)
    for j in range(2):
        pick = (place == pos[:, j : j + 1]).astype(BF)
        grad = grad + gate[j] * mm(pick, dxv[...])
    small[2:3, :] = jnp.sum(grad * normed, axis=0, keepdims=True)
    small[3:4, :] = jnp.sum(grad, axis=0, keepdims=True)
    d_resid = gv[...].astype(F32) + norm_back(grad, normed, spread, lying(g2))
    d_res[...] = d_resid
    branch = d_resid.astype(BF)
    loads[3].wait()

    def device_at(n, sign):
        t, other = n // 2, lax.rem(n, 2)
        return lax.rem(pair + far + sign * t, far) * 2 + lax.rem(core + other, 2)

    def give_att(n):
        owner = device_at(n, 1)
        return remote(
            d_att_v.at[owner], d_att.at[h], at_s.at[n], at_r.at[n], {"hidden": owner}
        )

    for n in range(n_h - 1, -1, -1):
        owner = device_at(n, 1)
        block = mm_nt(wo[owner], branch).astype(BF)
        if n == 0:
            d_att[h] = block
        else:
            d_att_v[owner] = block
            give_att(n).start()
    loads[4].wait()
    for t in range(n_h):
        owner = lax.rem(h + t, n_h)
        wo[owner] = mm(att_t[owner], branch).astype(BF)
    for step in list(range(1, far)) + [0]:
        copy = remote(
            wo.at[lax.rem(pair + step, far) * 2 + 1 - core],
            wo_box.at[step],
            wo_s.at[step],
            wo_r.at[step],
            {"hidden": mate},
        )
        copy.start()
        sends.append(copy)
    def give_wo(step):
        target = lax.rem(pair + step, far) * 2 + core
        return remote(
            wo.at[target],
            wo_far.at[step - 1],
            wf_s.at[step],
            wf_r.at[step],
            {"hidden": target},
        )

    for load in loads[5:]:
        load.wait()

    def load_kept(i, turn):
        return pltpu.make_async_copy(weights.at[i], kept.at[turn], kept_sem.at[turn])

    def block_at(at):
        owner = device_at(at // per_device, 1)
        return owner, owner * per_device + lax.rem(at, per_device)

    load_kept(block_at(0)[1], 0).start()
    dk_acc[...] = jnp.zeros_like(dk_acc)
    dv_acc[...] = jnp.zeros_like(dv_acc)

    def turn_values(i, _):
        cols = aligned(i * BLOCK, BLOCK)
        for n in range(heads):
            lo = 2 * width + n * HEAD_DIM
            values[n, cols, :] = qkv[lo : lo + HEAD_DIM, cols].astype(F32).T.astype(BF)
        return 0

    lax.fori_loop(0, blocks, turn_values, 0)

    def over_queries(at, _):
        owner, i = block_at(at)
        turn = lax.rem(at, 2)

        @pl.when(at + 1 < blocks)
        def _next():
            load_kept(block_at(at + 1)[1], 1 - turn).start()

        @pl.when((at >= per_device) & (lax.rem(at, per_device) == 0))
        def _arrive():
            n = at // per_device
            source = lax.rem(far - n // 2, far) * 2 + lax.rem(n, 2)
            give_att(source).wait_recv()

        @pl.when(at == per_device)
        def _weights():
            for step in range(1, far):
                there = wo_box.at[step]
                target = lax.rem(pair + step, far) * 2 + core
                remote(there, there, wo_s.at[step], wo_r.at[step], {"hidden": mate}).wait_recv()
                both = wo[target].astype(F32) + wo_box[step].astype(F32)
                wo[target] = both.astype(BF)
                give_wo(step).start()
            dw_send(1)

        load_kept(i, turn).wait()
        cols = aligned(lax.rem(at, per_device) * BLOCK, BLOCK)
        rows_i = aligned(i * BLOCK, BLOCK)
        given, centre = [], []
        for n in range(heads):
            here = slice(n * HEAD_DIM, (n + 1) * HEAD_DIM)
            scaled = d_att[owner, here, cols].astype(F32) * inverse[n : n + 1, rows_i]
            given.append(scaled.astype(BF))
            product = att_v[owner, here, cols].astype(F32) * scaled
            centre.append(jnp.sum(product, axis=0, keepdims=True))

        def block(span, first):
            attend_back(
                heads,
                i,
                span,
                first,
                qkv,
                given,
                centre,
                kept.at[turn],
                values,
                dq_acc,
                dk_acc,
                dv_acc,
            )

        spans(i, block)
        d_qkv[0:width, rows_i] = (dq_acc[...] * SCALE).astype(BF)
        return 0

    lax.fori_loop(0, blocks, over_queries, 0)
    w_acc[...] = jnp.zeros_like(w_acc)

    def finish(i, _):
        cols = aligned(i * BLOCK, BLOCK)
        d_qkv[width : 2 * width, cols] = dk_acc[:, cols].astype(BF)
        d_qkv[2 * width :, cols] = dv_acc[:, cols].astype(BF)
        block = d_qkv[:, cols]
        grad = mm_tn(block, w_t[...])
        inner = aligned(lax.rem(i, per_device) * BLOCK, BLOCK)
        normed, _unused = norm_parts(tv[i // per_device, inner, :].astype(F32))
        tv[i // per_device, inner, :] = grad.astype(BF)
        small[0:1, :] += jnp.sum(grad * normed, axis=0, keepdims=True)
        small[1:2, :] += jnp.sum(grad, axis=0, keepdims=True)
        hidden = (normed * lying(g1) + lying(s1)).astype(BF)
        w_acc[...] += mm(block, hidden)
        return 0

    lax.fori_loop(0, blocks, finish, 0)
    save_dh = pltpu.make_async_copy(tv, d_hidden, save_sem)
    save_dh.start()
    w_all[0 : 3 * width, :] = w_acc[...].astype(BF)
    there = wo_box.at[0]
    remote(there, there, wo_s.at[0], wo_r.at[0], {"hidden": mate}).wait_recv()
    total = wo[h].astype(F32) + wo_box[0].astype(F32)
    for step in range(1, far):
        give_wo(step).wait_recv()
        total = total + wo_far[step - 1].astype(F32)
    w_all[3 * width :, :] = total.astype(BF)
    load_dw.wait()
    load_far.wait()
    for which in range(2):
        for step in range(1, far if which == 1 else 1):
            for k in range(2):
                dw_across_copy(step, k).wait()

        def add_all(n, _, which=which):
            band = aligned(n * 96, 96)
            both = dw_mine[which, band, :].astype(F32)
            for step in range(1, far):
                both = both + dw_across[which, step - 1, band, :].astype(F32)
            dw_own[which, band, :] = both.astype(BF)
            return 0

        lax.fori_loop(0, dw_mine.shape[1] // 96, add_all, 0)
    for step in range(1, n_e):
        there = y_back.at[lax.rem(e + n_e - step, n_e)]
        remote(there, there, y_s.at[step], y_r.at[step], {"expert": e}).wait_recv()
    own_y.wait()
    save_dh.wait()
    for n in range(1, n_h):
        give_att(n).wait_send()
    for step in range(1, far):
        give_wo(step).wait_send()
    for copy in sends:
        copy.wait_send()


def run_back(
    ids,
    slot,
    pos,
    gates,
    count,
    g1,
    s1,
    g2,
    s2,
    w_router,
    inverse,
    dg_rows,
    dx_back,
    y_out,
    dw_sum,
    dw_far,
    out_grad,
    residual,
    all_tokens,
    qkv,
    att,
    att_t,
    w_out,
    w_t,
    weights,
    cid,
):
    n_e, n_h = lax.axis_size("expert"), lax.axis_size("hidden")
    experts, capacity, model = y_out.shape
    padded = dg_rows.shape[2]
    rows = out_grad.shape[0]
    width = w_t.shape[0] // 3
    heads = width // HEAD_DIM
    group, far = rows * n_h, n_h // 2
    shard = dw_sum.shape[2:]
    tall = 8 + experts

    def pairs(*shape):
        return [DMA(shape), DMA(shape)]

    return pl.pallas_call(
        partial(back_body, n_e, n_h, experts, capacity, padded, heads),
        name="back",
        out_shape=[
            shape_of(y_out.shape, BF),
            shape_of((n_h, rows, model), BF),
            shape_of((rows, model), F32),
            shape_of((4 * width, model), BF),
            shape_of((tall, model), F32),
            shape_of((2, *shard), BF),
        ],
        in_specs=[VMEM] * 12 + [ANY] * 13,
        out_specs=[ANY] * 2 + [VMEM] * 4,
        scratch_shapes=[
            pltpu.VMEM((experts * capacity, model), BF),
            pltpu.VMEM((rows, model), BF),
            pltpu.VMEM((rows, model), F32),
            pltpu.VMEM((n_h, rows, model), BF),
            pltpu.VMEM((3 * width, group), BF),
            pltpu.VMEM((n_h, width, rows), BF),
            pltpu.VMEM((n_h, width, rows), BF),
            pltpu.VMEM((n_h, width, model), BF),
            pltpu.VMEM((3 * width, model), BF),
            pltpu.VMEM((n_h, width, rows), BF),
            pltpu.VMEM((n_h, width, rows), BF),
            pltpu.VMEM((far, width, model), BF),
            pltpu.VMEM((far - 1, width, model), BF),
            pltpu.VMEM((2, heads, REACH, BLOCK, BLOCK), BF),
            pltpu.VMEM((heads, group, HEAD_DIM), BF),
            pltpu.VMEM((width, BLOCK), F32),
            pltpu.VMEM((width, group), F32),
            pltpu.VMEM((width, group), F32),
            pltpu.VMEM((3 * width, group), BF),
            pltpu.VMEM((3 * width, model), F32),
            pltpu.VMEM((2, *shard), BF),
            pltpu.VMEM((2, far - 1, *shard), BF),
            DMA((9,)),
            DMA,
            DMA((2,)),
            DMA((2,)),
            DMA,
            *pairs(n_e),
            *pairs(n_h),
            *pairs(far),
            *pairs(far),
            *pairs(far, 2),
        ],
        compiler_params=pltpu.CompilerParams(
            collective_id=cid, has_side_effects=True, vmem_limit_bytes=60 << 20
        ),
    )(
        ids,
        slot,
        pos,
        gates,
        count,
        g1,
        s1,
        g2,
        s2,
        w_router,
        inverse,
        dg_rows,
        dx_back.reshape(experts * capacity, model),
        y_out,
        dw_sum,
        dw_far,
        out_grad,
        residual,
        all_tokens,
        qkv,
        att,
        att_t,
        w_out.reshape(n_h, width, model),
        w_t,
        weights,
    )


def shards(
    tokens,
    doc_lengths,
    expert_ids,
    gain_one,
    shift_one,
    w_query,
    w_key,
    w_value,
    w_out,
    gain_two,
    shift_two,
    w_router,
    w_up,
    w_down,
    out_grad,
):
    rows, model = tokens.shape
    n_expert, n_hidden = lax.axis_size("expert"), lax.axis_size("hidden")
    experts = n_expert * w_up.shape[0]
    capacity = max(2, rows * 2 * 5 // (4 * experts))
    capacity = -(-capacity // 16) * 16
    total = experts * capacity
    heads = HEADS // n_hidden
    width = heads * HEAD_DIM
    g1, s1, g2, s2 = gain_one, shift_one, gain_two, shift_two
    router_t = w_router.T

    (
        all_tokens,
        qkv,
        att,
        att_t,
        w_t,
        g_in,
        x_slots,
        ups,
        weights,
        ids,
        pos,
        slot,
        count,
        inverse,
        residual,
        gates,
        gate_rows,
    ) = run_front(
        doc_lengths,
        expert_ids.T,
        g1,
        s1,
        g2,
        s2,
        router_t,
        tokens,
        out_grad,
        (w_query, w_key, w_value, w_out),
        w_up,
        capacity,
        heads,
        1,
    )
    dx_back, dg_back, y_out, dw_sum, dw_far = run_experts(
        x_slots, gate_rows, g_in, ups, w_down, 2
    )
    y_back, d_hidden, d_res, w_all, small, dw_own = run_back(
        ids,
        slot,
        pos,
        gates,
        count,
        g1,
        s1,
        g2,
        s2,
        router_t,
        inverse,
        dg_back,
        dx_back,
        y_out,
        dw_sum,
        dw_far,
        out_grad,
        residual,
        all_tokens,
        qkv,
        att,
        att_t,
        w_out,
        w_t,
        weights,
        3,
    )
    input_grad, output, full, small = run_tail(
        d_hidden,
        w_all.reshape(n_expert, 4 * width // n_expert, model),
        small,
        tokens,
        g1,
        d_res,
        residual,
        gates,
        pos,
        y_back.reshape(total, model),
        4,
    )
    scale = experts / (rows * n_expert * n_hidden * 2)
    turned = turn_weights(
        full.reshape(n_hidden, 4 * width, model),
        dw_own,
        small,
        input_grad,
        output,
        width,
        experts,
        scale,
    )
    w_grads, (up_grad, down_grad) = turned[:4], turned[4:6]
    gain_one_grad, shift_one_grad, gain_two_grad, shift_two_grad = turned[6:10]
    router_grad, input_grad, output, load = turned[10:]
    return (
        output,
        input_grad,
        gain_one_grad,
        shift_one_grad,
        *w_grads,
        gain_two_grad,
        shift_two_grad,
        router_grad.T,
        up_grad[None],
        down_grad[None],
        load,
    )


def solution(mesh):
    in_specs = (
        P(("expert", "hidden"), None),
        P("expert", None),
        P(("expert", "hidden"), None),
        P(),
        P(),
        P(),
        P(),
        P(),
        P(),
        P(),
        P(),
        P(),
        P("expert", None, "hidden"),
        P("expert", "hidden", None),
        P(("expert", "hidden"), None),
    )
    out_specs = (
        P(("expert", "hidden"), None),
        P(("expert", "hidden"), None),
        P(),
        P(),
        P(),
        P(),
        P(),
        P(),
        P(),
        P(),
        P(),
        P("expert", None, "hidden"),
        P("expert", "hidden", None),
        P(),
    )
    return jax.shard_map(shards, mesh=mesh, in_specs=in_specs, out_specs=out_specs, check_vma=False)
```

```python
from functools import partial

import jax
import jax.numpy as jnp
from jax import lax
from jax.experimental import pallas as pl
from jax.experimental.pallas import tpu as pltpu
from jax.sharding import PartitionSpec as P

HEAD_DIM = 64
HEADS = 12
EPSILON = 1e-05
SCALE = 0.125
MASKED = -1e30
BLOCK = 256
LONGEST = 1024
REACH = LONGEST // BLOCK + 1
LANES = 128
BF = jnp.bfloat16
F32 = jnp.float32
I32 = jnp.int32
MESH = pl.DeviceIdType.MESH
ANY = pl.BlockSpec(memory_space=pl.ANY)
SMEM = pl.BlockSpec(memory_space=pltpu.SMEM)
VMEM = pl.BlockSpec(memory_space=pltpu.VMEM)
DMA = pltpu.SemaphoreType.DMA
GELU_A = 0.7978845608028654
GELU_B = 0.044715


def mm(left, right):
    return jnp.dot(left, right, preferred_element_type=F32)


def mm_nt(left, right):
    return lax.dot_general(left, right, (((1,), (1,)), ((), ())), preferred_element_type=F32)


def mm_tn(left, right):
    return lax.dot_general(left, right, (((0,), (0,)), ((), ())), preferred_element_type=F32)


def iota(shape, axis):
    return lax.broadcasted_iota(I32, shape, axis)


def norm_parts(values):
    centred = values - jnp.mean(values, axis=-1, keepdims=True)
    inverse = lax.rsqrt(jnp.mean(centred * centred, axis=-1, keepdims=True) + EPSILON)
    return centred * inverse, inverse


def norm_back(grad_out, normed, inverse, gain):
    grad_normed = grad_out * gain
    first = jnp.mean(grad_normed, axis=-1, keepdims=True)
    second = jnp.mean(grad_normed * normed, axis=-1, keepdims=True)
    return inverse * (grad_normed - first - normed * second)


def split_two(value):
    high = value.astype(BF)
    return high, (value - high.astype(F32)).astype(BF)


def shape_of(shape, dtype):
    return jax.ShapeDtypeStruct(shape, dtype)


def greet(peers):
    barrier = pltpu.get_barrier_semaphore()
    for peer in peers:
        pl.semaphore_signal(barrier, inc=1, device_id=peer, device_id_type=MESH)
    pl.semaphore_wait(barrier, len(peers))


def remote(src, dst, send, recv, peer):
    return pltpu.make_async_remote_copy(
        src_ref=src, dst_ref=dst, send_sem=send, recv_sem=recv, device_id=peer, device_id_type=MESH
    )


def doc_bounds(docs):
    ends, at = [], 0
    for n in range(docs.shape[1] - 1):
        at = at + docs[0, n]
        ends.append(at)
    return ends


def start_of(place, ends):
    begin = jnp.zeros_like(place)
    for end in ends:
        begin = jnp.where(place >= end, end, begin)
    return begin


def lying(ref):
    return ref[...].reshape(1, ref.shape[0])


def aligned(at, size):
    return pl.ds(pl.multiple_of(at, size), size)


def find_slots(experts, capacity, ids, ids_t, pos, slot, count):
    rows = ids_t.shape[1]
    row = [ids_t[j : j + 1, :] for j in range(2)]
    tall = jnp.concatenate([r.astype(F32) for r in row] + [jnp.zeros((6, rows), F32)], axis=0)
    ids[...] = tall.T[:, 0:2].astype(I32)
    col = [ids[:, j : j + 1] for j in range(2)]
    lane = iota((rows, LANES), 1)
    hot = [(lane == c).astype(BF) for c in col]
    either = hot[0] + hot[1]
    below = (iota((rows, rows), 0) > iota((rows, rows), 1)).astype(BF)
    before = mm(below, either)
    wide = max(experts, 16)
    deep = iota((wide, rows), 0)
    hot_t = [(deep == r).astype(BF) for r in row]
    above = (iota((rows, rows), 0) < iota((rows, rows), 1)).astype(BF)
    before_t = mm(hot_t[0] + hot_t[1], above)
    count[...] = jnp.sum(either.astype(F32), axis=0, keepdims=True)
    flat_t = []
    for j in range(2):
        at = jnp.sum(hot[j].astype(F32) * before, axis=1, keepdims=True).astype(I32)
        pos[:, j : j + 1] = col[j] * capacity + at
        slot[:, j : j + 1] = at
        at_t = jnp.sum(hot_t[j].astype(F32) * before_t, axis=0, keepdims=True).astype(I32)
        flat_t.append(row[j] * capacity + at_t)
    return flat_t


def fill_slots(flat_t, source, out):
    total, rows = out.shape[0], source.shape[0]
    half = total // 2
    for n in range(2):
        place = iota((half, rows), 0) + n * half
        pick = ((place == flat_t[0]) | (place == flat_t[1])).astype(BF)
        out[pl.ds(n * half, half), :] = mm(pick, source).astype(BF)


def attend_block(heads, ends, i, span, first, qkv, keys, scores, kept, inverse):
    width = heads * HEAD_DIM
    base = i * BLOCK
    rows = aligned(base, BLOCK)
    q_pos = base + iota((1, BLOCK), 1)
    begin = start_of(q_pos, ends)
    queries = [
        qkv[n * HEAD_DIM : (n + 1) * HEAD_DIM, rows] * jnp.asarray(SCALE, BF) for n in range(heads)
    ]
    tops = [jnp.full((1, BLOCK), MASKED, F32)] * heads
    for k in range(span):
        part = aligned((first + k) * BLOCK, BLOCK)
        k_pos = (first + k) * BLOCK + iota((BLOCK, BLOCK), 0)
        allowed = (k_pos <= q_pos) & (k_pos >= begin)
        for n in range(heads):
            score = jnp.where(allowed, mm(keys[n, part, :], queries[n]), MASKED)
            scores[n, k] = score
            tops[n] = jnp.maximum(tops[n], jnp.max(score, axis=0, keepdims=True))
    result = []
    for n in range(heads):
        total = jnp.zeros((1, BLOCK), F32)
        acc = jnp.zeros((HEAD_DIM, BLOCK), F32)
        lo = 2 * width + n * HEAD_DIM
        for k in range(span):
            weight = jnp.exp(scores[n, k] - tops[n])
            total = total + jnp.sum(weight, axis=0, keepdims=True)
            value = qkv[lo : lo + HEAD_DIM, aligned((first + k) * BLOCK, BLOCK)]
            low = weight.astype(BF)
            kept[n, k] = low
            acc = acc + mm(value, low)
        whole = 1.0 / total
        inverse[n : n + 1, rows] = whole
        result.append((acc * whole).astype(BF))
    return result


def spans(i, body):
    @pl.when(i < 2)
    def _short():
        body(2, 0)

    @pl.when(i >= 2)
    def _long():
        body(REACH, (i - (REACH - 1)) * (i // (REACH - 1)))


def front_body(
    n_e,
    n_h,
    experts,
    capacity,
    padded,
    heads,
    chunks,
    docs,
    ids_t,
    g1,
    s1,
    g2,
    s2,
    w_router,
    tokens,
    out_grad,
    w_query,
    w_key,
    w_value,
    w_out,
    w_up,
    all_tokens,
    qkv_out,
    att_out,
    att_t_out,
    w_t_out,
    g_in,
    x_slots,
    ups,
    weights,
    ids,
    pos,
    slot,
    count,
    inverse,
    residual,
    gates,
    gate_rows,
    tv,
    gv,
    wv,
    wo,
    w_t,
    qkv,
    keys,
    scores,
    kept,
    att_v,
    att_in,
    g_slots,
    xs_v,
    own_sem,
    w_sem,
    save_sem,
    kept_sem,
    ty_s,
    ty_r,
    tc_s,
    tc_r,
    tf_s,
    tf_r,
    gs_s,
    gs_r,
    at_s,
    at_r,
    wy_s,
    wy_r,
    wc_s,
    wc_r,
    wf_s,
    wf_r,
):
    e, h = lax.axis_index("expert"), lax.axis_index("hidden")
    far = n_h // 2
    pair, core = h // 2, lax.rem(h, 2)
    mate = pair * 2 + 1 - core
    rows, model = tokens.shape
    width = heads * HEAD_DIM
    per_device = rows // BLOCK
    ends = doc_bounds(docs)

    def across(t):
        return lax.rem(pair + t, far) * 2 + core

    def origin(t):
        return lax.rem(pair + far - t, far) * 2 + core

    own_tokens = pltpu.make_async_copy(tokens, tv.at[h], own_sem.at[0])
    own_grad = pltpu.make_async_copy(out_grad, gv, own_sem.at[1])
    own_grad.start()
    own_tokens.start()
    w_loads = [
        pltpu.make_async_copy(w, wv.at[n], w_sem.at[n])
        for n, w in enumerate((w_query, w_key, w_value))
    ]
    w_loads.append(pltpu.make_async_copy(w_out, wo, w_sem.at[3]))
    for load in w_loads:
        load.start()
    greet(
        [{"hidden": lax.rem(h + step, n_h)} for step in range(1, n_h)]
        + [{"expert": lax.rem(e + step, n_e)} for step in range(1, n_e)]
    )

    piece = rows // chunks
    sends = []
    for k in range(chunks):
        part = pl.ds(k * piece, piece)
        for t in range(1, far):
            copy = remote(
                tokens.at[part],
                tv.at[h, part],
                ty_s.at[t, k],
                ty_r.at[t, k],
                {"hidden": across(t)},
            )
            copy.start()
            sends.append(copy)
    beside = remote(tokens, tv.at[h], tc_s, tc_r, {"hidden": mate})
    beside.start()
    sends.append(beside)

    flat_t = find_slots(experts, capacity, ids, ids_t, pos, slot, count)
    own_grad.wait()
    fill_slots(flat_t, gv[...], g_slots)
    for step in range(1, n_e):
        peer = lax.rem(e + step, n_e)
        copy = remote(
            g_slots.at[aligned(peer * capacity, capacity)],
            g_in.at[e],
            gs_s.at[step],
            gs_r.at[step],
            {"expert": peer},
        )
        copy.start()
        sends.append(copy)
    own_slots = pltpu.make_async_copy(
        g_slots.at[aligned(e * capacity, capacity)], g_in.at[e], own_sem.at[1]
    )
    own_slots.start()

    def pass_on(t, k):
        part = pl.ds(k * piece, piece)
        place = tv.at[origin(t), part]
        remote(place, place, ty_s.at[t, k], ty_r.at[t, k], {"hidden": across(t)}).wait_recv()
        copy = remote(place, place, tf_s.at[t, k], tf_r.at[t, k], {"hidden": mate})
        copy.start()
        sends.append(copy)

    todo = [(t, k) for k in range(chunks) for t in range(1, far)]
    third = -(-len(todo) // 4)

    def pass_some():
        for _ in range(min(third, len(todo))):
            pass_on(*todo.pop(0))

    pick = (iota((width, model), 1) == iota((width, model), 0) + h * width).astype(BF)
    for n in range(3):
        w_loads[n].wait()
        w_t[n * width : (n + 1) * width, :] = mm_nt(pick, wv[n]).astype(BF)
        if n == 1:
            pass_some()
    save_w = pltpu.make_async_copy(w_t, w_t_out, save_sem.at[0])
    save_w.start()

    def project(source):
        def one(b, _):
            normed, _unused = norm_parts(tv[source, aligned(b * BLOCK, BLOCK), :].astype(F32))
            hidden = (normed * lying(g1) + lying(s1)).astype(BF)
            block = mm_nt(w_t[...], hidden)
            cols = aligned(source * rows + b * BLOCK, BLOCK)
            qkv[:, cols] = block.astype(BF)
            for n in range(heads):
                lo = width + n * HEAD_DIM
                keys[n, cols, :] = block[lo : lo + HEAD_DIM].T.astype(BF)
            return 0

        lax.fori_loop(0, per_device, one, 0)

    pass_some()
    own_tokens.wait()
    project(h)
    pass_some()
    remote(tokens, tv.at[mate], tc_s, tc_r, {"hidden": mate}).wait_recv()
    project(mate)
    while todo:
        pass_some()

    deep = w_up.shape[1] // 2

    def up_copy(t, source):
        place = pl.ds(0, deep)
        return remote(
            w_up.at[0, place], ups.at[source, place], wy_s.at[t], wy_r.at[t], {"hidden": across(t)}
        )

    def up_onward(t):
        place = ups.at[origin(t), pl.ds(0, deep)]
        return remote(place, place, wf_s.at[t], wf_r.at[t], {"hidden": mate})

    up_beside = remote(w_up.at[0], ups.at[h], wc_s, wc_r, {"hidden": mate})
    up_beside.start()
    sends.append(up_beside)
    for t in range(1, far):
        up_copy(t, h).start()
    for t in range(1, far):
        project(origin(t))
    for t in range(1, far):
        there = lax.rem(pair + far - t, far) * 2 + 1 - core
        for k in range(chunks):
            place = tv.at[there, pl.ds(k * piece, piece)]
            remote(place, place, tf_s.at[t, k], tf_r.at[t, k], {"hidden": mate}).wait_recv()
        project(there)
    save_tokens = pltpu.make_async_copy(tv, all_tokens, save_sem.at[1])
    save_qkv = pltpu.make_async_copy(qkv, qkv_out, save_sem.at[2])
    save_tokens.start()
    save_qkv.start()

    inverse[...] = jnp.zeros_like(inverse)

    def device_at(n, sign):
        t, other = n // 2, lax.rem(n, 2)
        return lax.rem(pair + far + sign * t, far) * 2 + lax.rem(core + other, 2)

    def give_att(n):
        owner = device_at(n, 1)
        return remote(
            att_v.at[owner], att_in.at[h], at_s.at[n], at_r.at[n], {"hidden": owner}
        )

    def save_kept(i, turn):
        return pltpu.make_async_copy(kept.at[turn], weights.at[i], kept_sem.at[turn])

    def attend(at, _):
        n = n_h - 1 - at // per_device
        b = lax.rem(at, per_device)
        owner = device_at(n, 1)
        i = owner * per_device + b
        turn = lax.rem(at, 2)

        @pl.when(at >= 2)
        def _free():
            save_kept(i, turn).wait()

        def block(span, first):
            done = attend_block(
                heads, ends, i, span, first, qkv, keys, scores, kept.at[turn], inverse
            )
            for m in range(heads):
                lo = m * HEAD_DIM
                att_v[owner, lo : lo + HEAD_DIM, aligned(b * BLOCK, BLOCK)] = done[m]

        spans(i, block)
        save_kept(i, turn).start()

        @pl.when((b == per_device - 1) & (n > 0))
        def _give():
            give_att(n).start()

        return 0

    lax.fori_loop(0, n_h * per_device, attend, 0)
    for t in range(1, far):
        up_copy(t, origin(t)).wait_recv()
        up_onward(t).start()
    att_in[h] = att_v[h]
    save_att = pltpu.make_async_copy(att_v, att_out, save_sem.at[3])
    save_att.start()
    for n in range(n_h - 1, 0, -1):
        give_att(n).wait_recv()
    save_att_t = pltpu.make_async_copy(att_in, att_t_out, save_sem.at[4])
    save_att_t.start()

    w_loads[3].wait()
    res = tv[h].astype(F32) + mm_tn(att_in[...].reshape(model, rows), wo[...])
    residual[...] = res
    normed, _unused = norm_parts(res)
    hidden = (normed * lying(g2) + lying(s2)).astype(BF)
    fill_slots(flat_t, hidden, xs_v)
    save_x = [
        pltpu.make_async_copy(
            xs_v.at[pl.ds(n * capacity, capacity)], x_slots.at[n], save_sem.at[5 + n]
        )
        for n in range(experts)
    ]
    for save in save_x:
        save.start()
    logits = mm_nt(hidden, w_router[...])
    lane = iota((rows, experts), 1)
    chosen = [
        jnp.sum(jnp.where(lane == ids[:, j : j + 1], logits, 0.0), axis=1, keepdims=True)
        for j in range(2)
    ]
    top = jnp.maximum(chosen[0], chosen[1])
    raised = [jnp.exp(c - top) for c in chosen]
    both = raised[0] + raised[1]
    gate = [r / both for r in raised]
    for j in range(2):
        gates[:, j : j + 1] = gate[j]
    column = iota((rows, padded), 1)
    for n in range(experts):
        mix = jnp.zeros((rows, padded), F32)
        for j in range(2):
            here = jnp.where(ids[:, j : j + 1] == n, slot[:, j : j + 1], -1) == column
            mix = jnp.where(here, gate[j], mix)
        line = jnp.sum(mix, axis=0, keepdims=True)
        gate_rows[n] = jnp.broadcast_to(line, (8, padded))

    place = ups.at[mate]
    remote(place, place, wc_s, wc_r, {"hidden": mate}).wait_recv()
    for t in range(1, far):
        up_onward(t).wait()
    for step in range(1, n_e):
        source = lax.rem(e + n_e - step, n_e)
        place = g_in.at[source]
        remote(place, place, gs_s.at[step], gs_r.at[step], {"expert": e}).wait_recv()
    own_slots.wait()
    for n in range(1, n_h):
        give_att(n).wait_send()
    for turn in range(2):
        save_kept(0, turn).wait()
    for t in range(1, far):
        up_copy(t, h).wait_send()
    for copy in sends:
        copy.wait_send()
    for save in [save_w, save_tokens, save_qkv, save_att, save_att_t, *save_x]:
        save.wait()


def run_front(
    docs, ids_t, g1, s1, g2, s2, w_router, tokens, out_grad, ws, w_up, capacity, heads, cid
):
    n_e, n_h = lax.axis_size("expert"), lax.axis_size("hidden")
    experts = n_e * w_up.shape[0]
    rows, model = tokens.shape
    padded = -(-capacity // LANES) * LANES
    width, group, total = heads * HEAD_DIM, rows * n_h, experts * capacity
    far, chunks = n_h // 2, 8

    def pairs(*shape):
        return [DMA(shape), DMA(shape)]

    return pl.pallas_call(
        partial(front_body, n_e, n_h, experts, capacity, padded, heads, chunks),
        name="front",
        out_shape=[
            shape_of((n_h, rows, model), BF),
            shape_of((3 * width, group), BF),
            shape_of((n_h, width, rows), BF),
            shape_of((n_h, width, rows), BF),
            shape_of((3 * width, model), BF),
            shape_of((experts, capacity, model), BF),
            shape_of((experts, capacity, model), BF),
            shape_of((n_h, *w_up.shape[1:]), BF),
            shape_of((group // BLOCK, heads, REACH, BLOCK, BLOCK), BF),
            shape_of((rows, 2), I32),
            shape_of((rows, 2), I32),
            shape_of((rows, 2), I32),
            shape_of((1, LANES), F32),
            shape_of((8, group), F32),
            shape_of((rows, model), F32),
            shape_of((rows, 2), F32),
            shape_of((experts, 8, padded), F32),
        ],
        in_specs=[SMEM] + [VMEM] * 6 + [ANY] * 7,
        out_specs=[ANY] * 9 + [VMEM] * 8,
        scratch_shapes=[
            pltpu.VMEM((n_h, rows, model), BF),
            pltpu.VMEM((rows, model), BF),
            pltpu.VMEM((3, model, model), BF),
            pltpu.VMEM((model, model), BF),
            pltpu.VMEM((3 * width, model), BF),
            pltpu.VMEM((3 * width, group), BF),
            pltpu.VMEM((heads, group, HEAD_DIM), BF),
            pltpu.VMEM((heads, REACH, BLOCK, BLOCK), F32),
            pltpu.VMEM((2, heads, REACH, BLOCK, BLOCK), BF),
            pltpu.VMEM((n_h, width, rows), BF),
            pltpu.VMEM((n_h, width, rows), BF),
            pltpu.VMEM((total, model), BF),
            pltpu.VMEM((total, model), BF),
            DMA((2,)),
            DMA((4,)),
            DMA((5 + experts,)),
            DMA((2,)),
            *pairs(far, chunks),
            DMA,
            DMA,
            *pairs(far, chunks),
            *pairs(n_e),
            *pairs(n_h),
            *pairs(far),
            DMA,
            DMA,
            *pairs(far),
        ],
        compiler_params=pltpu.CompilerParams(
            collective_id=cid, has_side_effects=True, vmem_limit_bytes=58 << 20
        ),
    )(docs, ids_t, g1, s1, g2, s2, w_router, tokens, out_grad, *ws, w_up)


def moe_body(
    size,
    capacity,
    padded,
    per,
    x_slots,
    gate_rows,
    g_in,
    ups,
    w_up,
    w_down,
    dx_back,
    dg_back,
    y_out,
    dw_sum,
    dw_far,
    xv,
    gv,
    gates_v,
    up_v,
    down_v,
    act,
    dz,
    xg,
    dy,
    xg_t,
    dy_t,
    dxv,
    yv,
    dgv,
    y_acc,
    dx_acc,
    dw_box,
    load_sem,
    save_sem,
    wy_s,
    wy_r,
    wc_s,
    wc_r,
    wf_s,
    wf_r,
    dc_s,
    dc_r,
    df_s,
    df_r,
    g_sem,
    own_sem,
    xs_sem,
    xr_sem,
    gs_sem,
    gr_sem,
    ds_sem,
    dr_sem,
    ts_sem,
    tr_sem,
    out_sem,
):
    me, h = lax.axis_index("expert"), lax.axis_index("hidden")
    shards_n = ups.shape[0]
    far = shards_n // 2
    pair, core = h // 2, lax.rem(h, 2)
    mate = pair * 2 + 1 - core
    deep = w_down.shape[1] // 2
    tall = per * capacity
    steps = size // per

    middle = size // 2
    inner = lax.rem((me // 2 * 8 // size + 1) // 2, 2)

    def group_at(step):
        some = steps // 4
        early = jnp.where(step <= some, step - 1 + steps // 2, step - some)
        early = jnp.where((step > 0) & (step < steps - some), early, step)
        return jnp.where(inner == 1, early, step)

    def peer_at(p):
        peer, bit = 0, 1
        while bit < size:
            peer = peer + lax.rem(me // bit + p // bit, 2) * bit
            bit *= 2
        return peer

    def rows_of(p):
        return pl.ds(pl.multiple_of(p * capacity, capacity), capacity)

    def send_x(p):
        peer = peer_at(p)
        return remote(
            x_slots.at[peer], xv.at[rows_of(p)], xs_sem.at[p], xr_sem.at[p], {"expert": peer}
        )

    def send_gate(p):
        peer = peer_at(p)
        return remote(
            gate_rows.at[peer], gates_v.at[p], gs_sem.at[p], gr_sem.at[p], {"expert": peer}
        )

    def send_dx(p):
        peer = peer_at(p)
        return remote(
            dxv.at[rows_of(p)], dx_back.at[me], ds_sem.at[p], dr_sem.at[p], {"expert": peer}
        )

    def send_dg(p):
        peer = peer_at(p)
        return remote(dgv.at[p], dg_back.at[me], ts_sem.at[p], tr_sem.at[p], {"expert": peer})

    def load_g(p):
        return pltpu.make_async_copy(g_in.at[peer_at(p)], gv.at[rows_of(p)], g_sem.at[p])

    def save_y(p):
        return pltpu.make_async_copy(yv.at[rows_of(p)], y_out.at[peer_at(p)], out_sem.at[p])

    own_x = pltpu.make_async_copy(x_slots.at[me], xv.at[rows_of(0)], own_sem.at[0])
    own_gate = pltpu.make_async_copy(gate_rows.at[me], gates_v.at[0], own_sem.at[1])
    own_dx = pltpu.make_async_copy(dxv.at[rows_of(0)], dx_back.at[me], own_sem.at[2])
    own_dg = pltpu.make_async_copy(dgv.at[0], dg_back.at[me], own_sem.at[3])
    loads = [
        pltpu.make_async_copy(w_up.at[0], up_v.at[h], load_sem.at[0]),
        pltpu.make_async_copy(w_down.at[0], down_v.at[h], load_sem.at[1]),
    ]
    loads.append(pltpu.make_async_copy(ups.at[mate], up_v.at[mate], load_sem.at[2]))

    def half(k):
        return aligned(k * deep, deep)

    for t in range(1, far):
        for other in range(2):
            c = lax.rem(pair + t, far) * 2 + other
            place = (c, half(0))
            loads.append(
                pltpu.make_async_copy(
                    ups.at[place], up_v.at[place], load_sem.at[1 + 2 * t + other]
                )
            )
    parts = ((w_up, up_v, 1), (w_down, down_v, 0), (w_down, down_v, 1))

    def part_across(t, n):
        source, target, k = parts[n]
        there = {"hidden": lax.rem(pair + t, far) * 2 + core}
        return remote(
            source.at[0, half(k)], target.at[h, half(k)], wy_s.at[t, n], wy_r.at[t, n], there
        )

    def part_onward(t, n):
        _source, target, k = parts[n]
        place = target.at[lax.rem(pair + far - t, far) * 2 + core, half(k)]
        return remote(place, place, wf_s.at[t, n], wf_r.at[t, n], {"hidden": mate})

    down_beside = remote(w_down.at[0], down_v.at[h], wc_s, wc_r, {"hidden": mate})
    own_x.start()
    own_gate.start()
    for p in range(size):
        load_g(p).start()
    for load in loads:
        load.start()
    greet(
        [{"expert": lax.rem(me + step, size)} for step in range(1, size)]
        + [{"hidden": lax.rem(h + step, shards_n)} for step in range(1, shards_n)]
    )

    def send_all(order):
        for p in order:
            send_x(p).start()
            send_gate(p).start()

    @pl.when(inner == 1)
    def _far_first():
        send_all([1, *range(middle, size), *range(2, middle)])

    @pl.when(inner == 0)
    def _near_first():
        send_all(range(1, size))

    for n in range(3):
        for t in range(1, far):
            part_across(t, n).start()
    down_beside.start()
    own_x.wait()
    own_gate.wait()
    for load in loads:
        load.wait()

    def step_body(step, _):
        group = group_at(step)
        base = group * per
        for s in range(per):

            @pl.when(base + s > 0)
            def _arrive(s=s):
                send_x(base + s).wait_recv()
                send_gate(base + s).wait_recv()

            load_g(base + s).wait()
        rows = pl.ds(pl.multiple_of(group * tall, tall), tall)
        x, g = xv[rows, :], gv[rows, :]
        y_acc[...] = jnp.zeros_like(y_acc)
        dx_acc[...] = jnp.zeros_like(dx_acc)

        def shard_body(n, _):
            t = n // 2
            beside = lax.rem(n, 2)
            c = lax.rem(pair + far - t, far) * 2 + lax.rem(core + beside, 2)

            @pl.when((step == 0) & (n == 1))
            def _beside():
                down_beside.wait_recv()

            @pl.when((step == 0) & (n >= 2) & (beside == 0))
            def _across():
                for k in range(3):
                    part_across(t, k).wait_recv()
                    part_onward(t, k).start()

            @pl.when((step == 0) & (n >= 2) & (beside == 1))
            def _onward():
                for k in range(3):
                    part_onward(t, k).wait_recv()

            z = mm(x, up_v[c])
            du = mm_nt(g, down_v[c])
            square = z * z
            curve = jnp.tanh(z * (GELU_A + GELU_A * GELU_B * square))
            plus = 0.5 + 0.5 * curve
            hidden = (z * plus).astype(BF)
            rise = GELU_A + 3.0 * GELU_A * GELU_B * square
            slope = plus + 0.5 * z * (1.0 - curve * curve) * rise
            back = (slope * du).astype(BF)
            act[c, rows, :] = hidden
            dz[c, rows, :] = back
            y_acc[...] += mm(hidden, down_v[c])
            dx_acc[...] += mm_nt(back, up_v[c])
            return 0

        lax.fori_loop(0, shards_n, shard_body, 0)
        dxv[rows, :] = dx_acc[...].astype(BF)
        y_low = y_acc[...].astype(BF)
        yv[rows, :] = y_low
        dots = jnp.sum(y_low.astype(F32) * g.astype(F32), axis=1, keepdims=True)
        for s in range(per):
            p = base + s
            part = slice(s * capacity, (s + 1) * capacity)
            tall_dots = jnp.broadcast_to(dots[part], (capacity, LANES))
            if padded > capacity:
                blank = jnp.zeros((padded - capacity, LANES), F32)
                tall_dots = jnp.concatenate([tall_dots, blank], axis=0)
            dgv[p] = tall_dots.T[0:8]

            @pl.when(p > 0)
            def _give(p=p):
                send_dx(p).start()
                send_dg(p).start()

            @pl.when(p == 0)
            def _keep():
                own_dx.start()
                own_dg.start()

            save_y(p).start()
        for s in range(per):
            p = base + s
            part = slice(s * capacity, (s + 1) * capacity)
            gate = gates_v[p].T[0:capacity, 0:1]
            xg[rows_of(p), :] = (x[part].astype(F32) * gate).astype(BF)
            dy[rows_of(p), :] = (g[part].astype(F32) * gate).astype(BF)
        return 0

    lax.fori_loop(0, steps, step_body, 0)

    total = size * capacity
    turn = 256
    for k in range(total // turn):
        rows = slice(k * turn, (k + 1) * turn)
        xg_t[:, rows] = xg[rows, :].astype(F32).T.astype(BF)
        dy_t[:, rows] = dy[rows, :].astype(F32).T.astype(BF)
    for t in range(1, far):
        for k in range(3):
            part_across(t, k).wait_send()
            part_onward(t, k).wait_send()
    down_beside.wait_send()

    def give(which, step):
        source = (up_v, down_v)[which].at[lax.rem(pair + step, far) * 2 + 1 - core]
        return remote(
            source,
            dw_box.at[which, step],
            dc_s.at[which, step],
            dc_r.at[which, step],
            {"hidden": mate},
        )

    def keep(which, step):
        source = (up_v, down_v)[which].at[lax.rem(pair + step, far) * 2 + core]
        return pltpu.make_async_copy(source, dw_sum.at[which, step], save_sem.at[which, step])

    def cross(step, k):
        there = lax.rem(pair + step, far) * 2 + core
        return remote(
            up_v.at[there, half(k)],
            dw_far.at[step - 1, half(k)],
            df_s.at[step, k],
            df_r.at[step, k],
            {"hidden": there},
        )

    def gradients(which, left, right, held):
        def other(n, _):
            step = lax.rem(n + 1, far)
            c = lax.rem(pair + step, far) * 2 + 1 - core
            held[c] = mm(left[...], right[c]).astype(BF)
            give(which, step).start()
            return 0

        def own(n, _):
            step = lax.rem(n + 1, far)
            c = lax.rem(pair + step, far) * 2 + core
            total_of = mm(left[...], right[c])
            give(which, step).wait_recv()
            held[c] = (total_of + dw_box[which, step].astype(F32)).astype(BF)
            keep(which, step).start()

            if which == 0:

                @pl.when(step > 0)
                def _cross():
                    for k in range(2):
                        cross(step, k).start()

            return 0

        lax.fori_loop(0, far, other, 0)
        lax.fori_loop(0, far, own, 0)

    gradients(0, xg_t, dz, up_v)
    gradients(1, dy_t, act, down_v)
    for p in range(1, size):
        send_x(p).wait_send()
        send_gate(p).wait_send()
        send_dx(p).wait()
        send_dg(p).wait()
    for p in range(size):
        save_y(p).wait()
    own_dx.wait()
    own_dg.wait()
    for step in range(far):
        for which in range(2):
            give(which, step).wait_send()
            keep(which, step).wait()
    for step in range(1, far):
        for k in range(2):
            cross(step, k).wait()


def run_experts(x_slots, gate_rows, g_in, ups, w_up, w_down, cid):
    size = lax.axis_size("expert")
    experts, capacity, model = x_slots.shape
    padded = gate_rows.shape[2]
    shards_n, _unused, width = ups.shape
    total = experts * capacity
    per = 1
    while per * 2 * capacity <= 320 and size % (per * 2) == 0:
        per *= 2
    tall = per * capacity
    rows2 = (total, model)
    return pl.pallas_call(
        partial(moe_body, size, capacity, padded, per),
        name="experts",
        out_shape=[
            shape_of(x_slots.shape, BF),
            shape_of(gate_rows.shape, F32),
            shape_of(x_slots.shape, BF),
            shape_of((2, shards_n // 2, model, width), BF),
            shape_of((shards_n // 2 - 1, model, width), BF),
        ],
        in_specs=[ANY] * 6,
        out_specs=[ANY] * 5,
        scratch_shapes=[
            pltpu.VMEM(rows2, BF),
            pltpu.VMEM(rows2, BF),
            pltpu.VMEM(gate_rows.shape, F32),
            pltpu.VMEM((shards_n, model, width), BF),
            pltpu.VMEM((shards_n, width, model), BF),
            pltpu.VMEM((shards_n, total, width), BF),
            pltpu.VMEM((shards_n, total, width), BF),
            pltpu.VMEM(rows2, BF),
            pltpu.VMEM(rows2, BF),
            pltpu.VMEM((model, total), BF),
            pltpu.VMEM((model, total), BF),
            pltpu.VMEM(rows2, BF),
            pltpu.VMEM(rows2, BF),
            pltpu.VMEM(gate_rows.shape, F32),
            pltpu.VMEM((tall, model), F32),
            pltpu.VMEM((tall, model), F32),
            pltpu.VMEM((2, shards_n // 2, model, width), BF),
            DMA((shards_n + 1,)),
            DMA((2, shards_n // 2)),
            DMA((shards_n // 2, 3)),
            DMA((shards_n // 2, 3)),
            DMA,
            DMA,
            DMA((shards_n // 2, 3)),
            DMA((shards_n // 2, 3)),
            DMA((2, shards_n // 2)),
            DMA((2, shards_n // 2)),
            DMA((shards_n // 2, 2)),
            DMA((shards_n // 2, 2)),
            DMA((size,)),
            DMA((4,)),
        ]
        + [DMA((size,))] * 9,
        compiler_params=pltpu.CompilerParams(
            collective_id=cid, has_side_effects=True, vmem_limit_bytes=60 << 20
        ),
        cost_estimate=pl.CostEstimate(
            flops=12 * total * model * width * shards_n, bytes_accessed=40 << 20, transcendentals=0
        ),
    )(x_slots, gate_rows, g_in, ups, w_up, w_down)


def tail_body(
    n_e,
    n_h,
    chunks,
    dh,
    w_all,
    small,
    tokens,
    gain,
    d_res,
    residual,
    gates,
    pos,
    y_back,
    input_grad,
    output,
    full,
    total,
    wv,
    tok_v,
    d_res_v,
    res_v,
    yv,
    mine,
    beside,
    across,
    passing,
    x_box,
    z_box,
    w_mid,
    piece,
    small_mid,
    small_h,
    small_e,
    load_sem,
    mine_sem,
    cs_sem,
    cr_sem,
    as_sem,
    ar_sem,
    ws_sem,
    wr_sem,
    vs_sem,
    vr_sem,
    hs_sem,
    hr_sem,
    es_sem,
    er_sem,
    keep_sem,
    zs_sem,
    zr_sem,
    xs_sem,
    xr_sem,
    ys_sem,
    yr_sem,
    ms_sem,
    mr_sem,
):
    e, h = lax.axis_index("expert"), lax.axis_index("hidden")
    far, high = n_h // 2, n_e // 2
    pair, core = h // 2, lax.rem(h, 2)
    eh, el = e // 2, lax.rem(e, 2)
    mate = pair * 2 + 1 - core
    greet(
        [{"expert": lax.rem(e + step, n_e)} for step in range(1, n_e)]
        + [{"hidden": lax.rem(h + step, n_h)} for step in range(1, n_h)]
    )
    w_sends, w_order = {}, list(range(1, high)) + [0]
    for step in w_order:
        there = lax.rem(eh + step, high)
        copy = remote(
            w_all.at[there * 2 + 1 - el],
            x_box.at[step],
            ws_sem.at[step],
            wr_sem.at[step],
            {"expert": eh * 2 + 1 - el},
        )
        copy.start()
        w_sends[step] = copy
    rows = dh.shape[1] // chunks
    core_sends = {}
    for step in list(range(1, far)) + [0]:
        there = lax.rem(pair + step, far)
        for k in range(chunks):
            part = pl.ds(k * rows, rows)
            copy = remote(
                dh.at[there * 2 + 1 - core, part],
                beside.at[step, part],
                cs_sem.at[step, k],
                cr_sem.at[step, k],
                {"hidden": mate},
            )
            copy.start()
            core_sends[step, k] = copy
    mine_loads = []
    for step in range(far):
        there = lax.rem(pair + step, far)
        load = pltpu.make_async_copy(dh.at[there * 2 + core], mine.at[step], mine_sem.at[step])
        load.start()
        mine_loads.append(load)
    loads = [
        pltpu.make_async_copy(source, target, load_sem.at[n])
        for n, (source, target) in enumerate(
            ((w_all, wv), (residual, res_v), (y_back, yv), (tokens, tok_v), (d_res, d_res_v))
        )
    ]
    for load in loads:
        load.start()
    for load in mine_loads:
        load.wait()
    far_sends = []
    for step in range(1, far):
        there = lax.rem(pair + step, far)
        for k in range(chunks):
            part = pl.ds(k * rows, rows)
            core_sends[step, k].wait_recv()
            both = mine[step, part, :].astype(F32) + beside[step, part, :].astype(F32)
            passing[step - 1, part, :] = both.astype(BF)
            copy = remote(
                passing.at[step - 1, part],
                across.at[step - 1, part],
                as_sem.at[step - 1, k],
                ar_sem.at[step - 1, k],
                {"hidden": there * 2 + core},
            )
            copy.start()
            far_sends.append(copy)
    loads[0].wait()
    v_sends = []
    for step in w_order[:-1]:
        there = lax.rem(eh + step, high) * 2 + el
        w_sends[step].wait_recv()
        w_mid[step - 1] = (wv[there].astype(F32) + x_box[step].astype(F32)).astype(BF)
        copy = remote(
            w_mid.at[step - 1],
            z_box.at[step - 1],
            vs_sem.at[step],
            vr_sem.at[step],
            {"expert": there},
        )
        copy.start()
        v_sends.append(copy)
    small_sends = []
    for at in range(n_h - 1):
        peer = lax.rem(h + 1 + at, n_h)
        copy = remote(small, small_h.at[at], hs_sem.at[at], hr_sem.at[at], {"hidden": peer})
        copy.start()
        small_sends.append(copy)
    w_sends[0].wait_recv()
    acc = wv[e].astype(F32) + x_box[0].astype(F32)
    for at, copy in enumerate(v_sends):
        copy.wait_recv()
        acc = acc + z_box[at].astype(F32)
    piece[...] = acc.astype(BF)
    keep = pltpu.make_async_copy(piece, full.at[h, e], keep_sem)
    keep.start()
    started = []

    def slot(eh_of, el_of, pair_of, core_of):
        return full.at[pair_of * 2 + core_of, eh_of * 2 + el_of]

    def back(step, size, place):
        return lax.rem(place + size - step, size)

    def give_z(source):
        for s in range(1, high):
            there = lax.rem(eh + s, high) * 2 + el
            copy = remote(
                source, slot(eh, el, pair, core), zs_sem.at[s], zr_sem.at[s], {"expert": there}
            )
            copy.start()
            started.append(copy)

    def z_arrival(s):
        place = slot(back(s, high, eh), el, pair, core)
        return place, remote(place, place, zs_sem.at[s], zr_sem.at[s], {"expert": e})

    def give_x(source, s):
        target = slot(back(s, high, eh), el, pair, core)
        copy = remote(
            source, target, xs_sem.at[s], xr_sem.at[s], {"expert": eh * 2 + 1 - el}
        )
        copy.start()
        started.append(copy)

    def x_arrival(s):
        place = slot(back(s, high, eh), 1 - el, pair, core)
        return place, remote(place, place, xs_sem.at[s], xr_sem.at[s], {"expert": e})

    def give_y(source, s, flag):
        target = slot(back(s, high, eh), el if flag == 0 else 1 - el, pair, core)
        for t in range(1, far):
            there = lax.rem(pair + t, far) * 2 + core
            at = 2 * s + flag
            copy = remote(
                source, target, ys_sem.at[t, at], yr_sem.at[t, at], {"hidden": there}
            )
            copy.start()
            started.append(copy)

    def y_arrival(t, s, flag):
        other = el if flag == 0 else 1 - el
        place = slot(back(s, high, eh), other, back(t, far, pair), core)
        at = 2 * s + flag
        return place, remote(place, place, ys_sem.at[t, at], yr_sem.at[t, at], {"hidden": h})

    def give_mate(source, t, s, flag):
        other = el if flag == 0 else 1 - el
        target = slot(back(s, high, eh), other, back(t, far, pair), core)
        at = 2 * s + flag
        copy = remote(source, target, ms_sem.at[t, at], mr_sem.at[t, at], {"hidden": mate})
        copy.start()
        started.append(copy)

    def mate_arrival(t, s, flag):
        other = el if flag == 0 else 1 - el
        place = slot(back(s, high, eh), other, back(t, far, pair), 1 - core)
        at = 2 * s + flag
        return place, remote(place, place, ms_sem.at[t, at], mr_sem.at[t, at], {"hidden": h})

    give_z(piece)
    give_x(piece, 0)
    give_y(piece, 0, 0)
    give_mate(piece, 0, 0, 0)
    arrived = [(0, 0)]

    def take_x(s):
        place, arrival = x_arrival(s)
        arrival.wait_recv()
        give_y(place, s, 1)
        give_mate(place, 0, s, 1)
        arrived.append((s, 1))

    for s in range(1, high):
        place, arrival = z_arrival(s)
        arrival.wait_recv()
        give_x(place, s)
        give_y(place, s, 0)
        give_mate(place, 0, s, 0)
        arrived.append((s, 0))
        take_x(s - 1)
    take_x(high - 1)
    for copy in small_sends:
        copy.wait_recv()
    summed = small[...]
    for at in range(n_h - 1):
        summed = summed + small_h[at]
    small_mid[...] = summed
    small_out = []
    for at in range(n_e - 1):
        peer = lax.rem(e + 1 + at, n_e)
        copy = remote(small_mid, small_e.at[at], es_sem.at[at], er_sem.at[at], {"expert": peer})
        copy.start()
        small_out.append(copy)
    for load in loads[1:]:
        load.wait()
    place_of = iota((residual.shape[0], y_back.shape[0]), 1)
    result = res_v[...]
    for j in range(2):
        pick = (place_of == pos[:, j : j + 1]).astype(BF)
        result = result + gates[:, j : j + 1] * mm(pick, yv[...])
    output[...] = result.astype(BF)
    for k in range(chunks):
        part = pl.ds(k * rows, rows)
        core_sends[0, k].wait_recv()
    for copy in far_sends:
        copy.wait_recv()
    grad = mine[0].astype(F32) + beside[0].astype(F32)
    for step in range(far - 1):
        grad = grad + across[step].astype(F32)
    normed, inverse = norm_parts(tok_v[...].astype(F32))
    input_grad[...] = (d_res_v[...] + norm_back(grad, normed, inverse, lying(gain))).astype(BF)
    for t in range(1, far):
        for s, flag in arrived:
            place, arrival = y_arrival(t, s, flag)
            arrival.wait_recv()
            give_mate(place, t, s, flag)
    for copy in small_out:
        copy.wait_recv()
    summed = small_mid[...]
    for at in range(n_e - 1):
        summed = summed + small_e[at]
    total[...] = summed
    for t in range(far):
        for s, flag in arrived:
            _place, arrival = mate_arrival(t, s, flag)
            arrival.wait_recv()
    keep.wait()
    for copy in [*started, *w_sends.values(), *v_sends, *small_sends, *small_out, *far_sends]:
        copy.wait_send()
    for copy in core_sends.values():
        copy.wait_send()


def run_tail(dh, w_all, small, tokens, gain, d_res, residual, gates, pos, y_back, cid):
    n_e, n_h = lax.axis_size("expert"), lax.axis_size("hidden")
    far, high = n_h // 2, n_e // 2
    chunks = 4
    _unused, rows, model = dh.shape
    piece = w_all.shape[1:]
    return pl.pallas_call(
        partial(tail_body, n_e, n_h, chunks),
        name="tail",
        out_shape=[
            shape_of((rows, model), BF),
            shape_of((rows, model), BF),
            shape_of((n_h, n_e, *piece), BF),
            shape_of(small.shape, F32),
        ],
        in_specs=[ANY, ANY, VMEM, ANY, VMEM, ANY, ANY, VMEM, VMEM, ANY],
        out_specs=[VMEM, VMEM, ANY, VMEM],
        scratch_shapes=[
            pltpu.VMEM(w_all.shape, BF),
            pltpu.VMEM(tokens.shape, BF),
            pltpu.VMEM(d_res.shape, F32),
            pltpu.VMEM(residual.shape, F32),
            pltpu.VMEM(y_back.shape, BF),
            pltpu.VMEM((far, rows, model), BF),
            pltpu.VMEM((far, rows, model), BF),
            pltpu.VMEM((far - 1, rows, model), BF),
            pltpu.VMEM((far - 1, rows, model), BF),
            pltpu.VMEM((high, *piece), BF),
            pltpu.VMEM((high - 1, *piece), BF),
            pltpu.VMEM((high - 1, *piece), BF),
            pltpu.VMEM(piece, BF),
            pltpu.VMEM(small.shape, F32),
            pltpu.VMEM((n_h - 1, *small.shape), F32),
            pltpu.VMEM((n_e - 1, *small.shape), F32),
            DMA((5,)),
            DMA((far,)),
            DMA((far, chunks)),
            DMA((far, chunks)),
            DMA((far - 1, chunks)),
            DMA((far - 1, chunks)),
            DMA((high,)),
            DMA((high,)),
            DMA((high,)),
            DMA((high,)),
            DMA((n_h - 1,)),
            DMA((n_h - 1,)),
            DMA((n_e - 1,)),
            DMA((n_e - 1,)),
            DMA,
            DMA((high,)),
            DMA((high,)),
            DMA((high,)),
            DMA((high,)),
            DMA((far, n_e)),
            DMA((far, n_e)),
            DMA((far, n_e)),
            DMA((far, n_e)),
        ],
        compiler_params=pltpu.CompilerParams(
            collective_id=cid, has_side_effects=True, vmem_limit_bytes=56 << 20
        ),
    )(dh, w_all, small, tokens, gain, d_res, residual, gates, pos, y_back)


def turn_body(
    width,
    experts,
    scale,
    full,
    dw,
    small,
    input_grad,
    output,
    q_out,
    k_out,
    v_out,
    o_out,
    up_out,
    down_out,
    g1_out,
    s1_out,
    g2_out,
    s2_out,
    router_out,
    input_out,
    output_out,
    load_out,
):
    @pl.when(pl.program_id(0) == 0)
    def _begin():
        input_out[...] = input_grad[...]
        output_out[...] = output[...]
        for n, out in enumerate((g1_out, s1_out, g2_out, s2_out)):
            out[...] = small[n : n + 1, :].reshape(out.shape)
        router_out[...] = small[8 : 8 + experts, :]
        load_out[...] = small[4:5, 0:experts].reshape(experts) * scale

    for n, out in enumerate((q_out, k_out, v_out)):
        part = full[:, n * width : (n + 1) * width, :].astype(F32)
        out[...] = part.reshape(-1, part.shape[2]).T
    part = full[:, 3 * width :, :].astype(F32)
    o_out[...] = part.reshape(-1, part.shape[2])
    trained = jnp.where(lax.axis_index("expert") >= experts // 2, 1.0, 0.0)
    up_out[...] = dw[0].astype(F32) * trained
    down_out[...] = dw[1].astype(F32).T * trained


def turn_weights(full, dw, small, input_grad, output, width, experts, scale):
    n_h, deep, model = full.shape
    cols = 128
    across = pl.BlockSpec((cols, model), lambda i: (i, 0))
    down = pl.BlockSpec((model, cols), lambda i: (0, i))
    flat = pl.BlockSpec((model,), lambda i: (0,))
    whole = pl.BlockSpec(output.shape, lambda i: (0, 0))
    square = shape_of((model, model), F32)
    return pl.pallas_call(
        partial(turn_body, width, experts, scale),
        name="turn_weights",
        grid=(model // cols,),
        out_shape=[square] * 6
        + [shape_of((model,), F32)] * 4
        + [
            shape_of((experts, model), F32),
            shape_of(input_grad.shape, BF),
            shape_of(output.shape, BF),
            shape_of((experts,), F32),
        ],
        in_specs=[
            pl.BlockSpec((n_h, deep, cols), lambda i: (0, 0, i)),
            pl.BlockSpec((2, model, cols), lambda i: (0, 0, i)),
            pl.BlockSpec(small.shape, lambda i: (0, 0)),
            whole,
            whole,
        ],
        out_specs=[across, across, across, down, down, across]
        + [flat] * 4
        + [pl.BlockSpec((experts, model), lambda i: (0, 0)), whole, whole]
        + [pl.BlockSpec((experts,), lambda i: (0,))],
        compiler_params=pltpu.CompilerParams(
            dimension_semantics=("arbitrary",), vmem_limit_bytes=60 << 20
        ),
        cost_estimate=pl.CostEstimate(flops=0, bytes_accessed=24 << 20, transcendentals=0),
    )(full, dw, small, input_grad, output)


def attend_back(
    heads, i, span, first, qkv, given, centre, kept, values, dq_acc, dk_acc, dv_acc
):
    width = heads * HEAD_DIM
    rows = aligned(i * BLOCK, BLOCK)
    dq_acc[...] = jnp.zeros_like(dq_acc)
    queries = [
        qkv[n * HEAD_DIM : (n + 1) * HEAD_DIM, rows] * jnp.asarray(SCALE, BF) for n in range(heads)
    ]
    for k in range(span):
        part = aligned((first + k) * BLOCK, BLOCK)
        for n in range(heads):
            here = slice(n * HEAD_DIM, (n + 1) * HEAD_DIM)
            weight = kept[n, k]
            d_weight = mm(values[n, part, :], given[n])
            d_score = (weight.astype(F32) * (d_weight - centre[n])).astype(BF)
            dv_acc[here, part] += mm_nt(given[n], weight)
            dk_acc[here, part] += mm_nt(queries[n], d_score)
            lo = width + n * HEAD_DIM
            dq_acc[here, :] += mm(qkv[lo : lo + HEAD_DIM, part], d_score)


def back_body(
    n_e,
    n_h,
    experts,
    capacity,
    padded,
    heads,
    ids,
    slot,
    pos,
    gates,
    count,
    g1,
    s1,
    g2,
    s2,
    w_router,
    inverse,
    dg_rows,
    dx_back,
    y_out,
    dw_sum,
    dw_far,
    out_grad,
    residual,
    all_tokens,
    qkv_in,
    att_in,
    att_t_in,
    w_out,
    w_t_in,
    weights,
    y_back,
    d_hidden,
    d_res,
    w_all,
    small,
    dw_own,
    dxv,
    gv,
    res_v,
    tv,
    qkv,
    att_v,
    att_t,
    wo,
    w_t,
    d_att_v,
    d_att,
    wo_box,
    wo_far,
    kept,
    values,
    dq_acc,
    dk_acc,
    dv_acc,
    d_qkv,
    w_acc,
    dw_mine,
    dw_across,
    load_sem,
    save_sem,
    dw_sem,
    kept_sem,
    y_own,
    y_s,
    y_r,
    at_s,
    at_r,
    wo_s,
    wo_r,
    wf_s,
    wf_r,
    da_s,
    da_r,
):
    e, h = lax.axis_index("expert"), lax.axis_index("hidden")
    far = n_h // 2
    pair, core = h // 2, lax.rem(h, 2)
    mate = pair * 2 + 1 - core
    rows, model = out_grad.shape
    width = heads * HEAD_DIM
    group = rows * n_h
    per_device = rows // BLOCK
    blocks = group // BLOCK
    sends = []

    loads = [
        pltpu.make_async_copy(source, target, load_sem.at[n])
        for n, (source, target) in enumerate(
            (
                (residual, res_v),
                (dx_back, dxv),
                (out_grad, gv),
                (w_out, wo),
                (att_t_in, att_t),
                (qkv_in, qkv),
                (att_in, att_v),
                (all_tokens, tv),
                (w_t_in, w_t),
            )
        )
    ]
    for load in loads:
        load.start()
    greet(
        [{"hidden": lax.rem(h + step, n_h)} for step in range(1, n_h)]
        + [{"expert": lax.rem(e + step, n_e)} for step in range(1, n_e)]
    )
    load_dw = pltpu.make_async_copy(dw_sum.at[:, 0], dw_mine, dw_sem.at[0])
    load_dw.start()
    deep = dw_mine.shape[1] // 2
    load_far = pltpu.make_async_copy(
        dw_far, dw_across.at[0], dw_sem.at[1]
    )
    load_far.start()

    def dw_across_copy(step, k):
        part = pl.ds(k * deep, deep)
        return remote(
            dw_sum.at[1, step, part],
            dw_across.at[1, step - 1, part],
            da_s.at[step, k],
            da_r.at[step, k],
            {"hidden": lax.rem(pair + step, far) * 2 + core},
        )

    def dw_send(k):
        for step in range(1, far):
            dw_across_copy(step, k).start()

    dw_send(0)
    for step in range(1, n_e):
        peer = lax.rem(e + step, n_e)
        copy = remote(y_out.at[peer], y_back.at[e], y_s.at[step], y_r.at[step], {"expert": peer})
        copy.start()
        sends.append(copy)
    own_y = pltpu.make_async_copy(y_out.at[e], y_back.at[e], y_own)
    own_y.start()

    for load in loads[:3]:
        load.wait()
    normed, spread = norm_parts(res_v[...])
    hidden = (normed * lying(g2) + lying(s2)).astype(BF)
    gate = [gates[:, j : j + 1] for j in range(2)]
    column = iota((rows, padded), 1)
    dot_of = []
    for j in range(2):
        mix = jnp.zeros((rows, padded), F32)
        for n in range(experts):
            here = jnp.where(ids[:, j : j + 1] == n, slot[:, j : j + 1], -1) == column
            mix = jnp.where(here, dg_rows[n, 0:1, :], mix)
        dot_of.append(jnp.sum(mix, axis=1, keepdims=True))
    mean = gate[0] * dot_of[0] + gate[1] * dot_of[1]
    lane = iota((rows, experts), 1)
    d_logits = jnp.zeros((rows, experts), F32)
    for j in range(2):
        d_logits = jnp.where(lane == ids[:, j : j + 1], gate[j] * (dot_of[j] - mean), d_logits)
    high, low = split_two(d_logits)
    grad = mm(high, w_router[...]) + mm(low, w_router[...])
    small[...] = jnp.zeros_like(small)
    small[8 : 8 + experts, :] = mm_tn(high, hidden) + mm_tn(low, hidden)
    small[4:5, 0:LANES] = count[...]
    place = iota((rows, experts * capacity), 1)
    for j in range(2):
        pick = (place == pos[:, j : j + 1]).astype(BF)
        grad = grad + gate[j] * mm(pick, dxv[...])
    small[2:3, :] = jnp.sum(grad * normed, axis=0, keepdims=True)
    small[3:4, :] = jnp.sum(grad, axis=0, keepdims=True)
    d_resid = gv[...].astype(F32) + norm_back(grad, normed, spread, lying(g2))
    d_res[...] = d_resid
    branch = d_resid.astype(BF)
    loads[3].wait()

    def device_at(n, sign):
        t, other = n // 2, lax.rem(n, 2)
        return lax.rem(pair + far + sign * t, far) * 2 + lax.rem(core + other, 2)

    def give_att(n):
        owner = device_at(n, 1)
        return remote(
            d_att_v.at[owner], d_att.at[h], at_s.at[n], at_r.at[n], {"hidden": owner}
        )

    for n in range(n_h - 1, -1, -1):
        owner = device_at(n, 1)
        block = mm_nt(wo[owner], branch).astype(BF)
        if n == 0:
            d_att[h] = block
        else:
            d_att_v[owner] = block
            give_att(n).start()
    loads[4].wait()
    for t in range(n_h):
        owner = lax.rem(h + t, n_h)
        wo[owner] = mm(att_t[owner], branch).astype(BF)
    for step in list(range(1, far)) + [0]:
        copy = remote(
            wo.at[lax.rem(pair + step, far) * 2 + 1 - core],
            wo_box.at[step],
            wo_s.at[step],
            wo_r.at[step],
            {"hidden": mate},
        )
        copy.start()
        sends.append(copy)
    def give_wo(step):
        target = lax.rem(pair + step, far) * 2 + core
        return remote(
            wo.at[target],
            wo_far.at[step - 1],
            wf_s.at[step],
            wf_r.at[step],
            {"hidden": target},
        )

    for load in loads[5:]:
        load.wait()

    def load_kept(i, turn):
        return pltpu.make_async_copy(weights.at[i], kept.at[turn], kept_sem.at[turn])

    def block_at(at):
        owner = device_at(at // per_device, 1)
        return owner, owner * per_device + lax.rem(at, per_device)

    load_kept(block_at(0)[1], 0).start()
    dk_acc[...] = jnp.zeros_like(dk_acc)
    dv_acc[...] = jnp.zeros_like(dv_acc)

    def turn_values(i, _):
        cols = aligned(i * BLOCK, BLOCK)
        for n in range(heads):
            lo = 2 * width + n * HEAD_DIM
            values[n, cols, :] = qkv[lo : lo + HEAD_DIM, cols].astype(F32).T.astype(BF)
        return 0

    lax.fori_loop(0, blocks, turn_values, 0)

    def over_queries(at, _):
        owner, i = block_at(at)
        turn = lax.rem(at, 2)

        @pl.when(at + 1 < blocks)
        def _next():
            load_kept(block_at(at + 1)[1], 1 - turn).start()

        @pl.when((at >= per_device) & (lax.rem(at, per_device) == 0))
        def _arrive():
            n = at // per_device
            source = lax.rem(far - n // 2, far) * 2 + lax.rem(n, 2)
            give_att(source).wait_recv()

        @pl.when(at == per_device)
        def _weights():
            for step in range(1, far):
                there = wo_box.at[step]
                target = lax.rem(pair + step, far) * 2 + core
                remote(there, there, wo_s.at[step], wo_r.at[step], {"hidden": mate}).wait_recv()
                both = wo[target].astype(F32) + wo_box[step].astype(F32)
                wo[target] = both.astype(BF)
                give_wo(step).start()
            dw_send(1)

        load_kept(i, turn).wait()
        cols = aligned(lax.rem(at, per_device) * BLOCK, BLOCK)
        rows_i = aligned(i * BLOCK, BLOCK)
        given, centre = [], []
        for n in range(heads):
            here = slice(n * HEAD_DIM, (n + 1) * HEAD_DIM)
            scaled = d_att[owner, here, cols].astype(F32) * inverse[n : n + 1, rows_i]
            given.append(scaled.astype(BF))
            product = att_v[owner, here, cols].astype(F32) * scaled
            centre.append(jnp.sum(product, axis=0, keepdims=True))

        def block(span, first):
            attend_back(
                heads,
                i,
                span,
                first,
                qkv,
                given,
                centre,
                kept.at[turn],
                values,
                dq_acc,
                dk_acc,
                dv_acc,
            )

        spans(i, block)
        d_qkv[0:width, rows_i] = (dq_acc[...] * SCALE).astype(BF)
        return 0

    lax.fori_loop(0, blocks, over_queries, 0)
    w_acc[...] = jnp.zeros_like(w_acc)

    def finish(i, _):
        cols = aligned(i * BLOCK, BLOCK)
        d_qkv[width : 2 * width, cols] = dk_acc[:, cols].astype(BF)
        d_qkv[2 * width :, cols] = dv_acc[:, cols].astype(BF)
        block = d_qkv[:, cols]
        grad = mm_tn(block, w_t[...])
        inner = aligned(lax.rem(i, per_device) * BLOCK, BLOCK)
        normed, _unused = norm_parts(tv[i // per_device, inner, :].astype(F32))
        tv[i // per_device, inner, :] = grad.astype(BF)
        small[0:1, :] += jnp.sum(grad * normed, axis=0, keepdims=True)
        small[1:2, :] += jnp.sum(grad, axis=0, keepdims=True)
        hidden = (normed * lying(g1) + lying(s1)).astype(BF)
        w_acc[...] += mm(block, hidden)
        return 0

    lax.fori_loop(0, blocks, finish, 0)
    save_dh = pltpu.make_async_copy(tv, d_hidden, save_sem)
    save_dh.start()
    w_all[0 : 3 * width, :] = w_acc[...].astype(BF)
    there = wo_box.at[0]
    remote(there, there, wo_s.at[0], wo_r.at[0], {"hidden": mate}).wait_recv()
    total = wo[h].astype(F32) + wo_box[0].astype(F32)
    for step in range(1, far):
        give_wo(step).wait_recv()
        total = total + wo_far[step - 1].astype(F32)
    w_all[3 * width :, :] = total.astype(BF)
    load_dw.wait()
    load_far.wait()
    for which in range(2):
        for step in range(1, far if which == 1 else 1):
            for k in range(2):
                dw_across_copy(step, k).wait()

        def add_all(n, _, which=which):
            band = aligned(n * 96, 96)
            both = dw_mine[which, band, :].astype(F32)
            for step in range(1, far):
                both = both + dw_across[which, step - 1, band, :].astype(F32)
            dw_own[which, band, :] = both.astype(BF)
            return 0

        lax.fori_loop(0, dw_mine.shape[1] // 96, add_all, 0)
    for step in range(1, n_e):
        there = y_back.at[lax.rem(e + n_e - step, n_e)]
        remote(there, there, y_s.at[step], y_r.at[step], {"expert": e}).wait_recv()
    own_y.wait()
    save_dh.wait()
    for n in range(1, n_h):
        give_att(n).wait_send()
    for step in range(1, far):
        give_wo(step).wait_send()
    for copy in sends:
        copy.wait_send()


def run_back(
    ids,
    slot,
    pos,
    gates,
    count,
    g1,
    s1,
    g2,
    s2,
    w_router,
    inverse,
    dg_rows,
    dx_back,
    y_out,
    dw_sum,
    dw_far,
    out_grad,
    residual,
    all_tokens,
    qkv,
    att,
    att_t,
    w_out,
    w_t,
    weights,
    cid,
):
    n_e, n_h = lax.axis_size("expert"), lax.axis_size("hidden")
    experts, capacity, model = y_out.shape
    padded = dg_rows.shape[2]
    rows = out_grad.shape[0]
    width = w_t.shape[0] // 3
    heads = width // HEAD_DIM
    group, far = rows * n_h, n_h // 2
    shard = dw_sum.shape[2:]
    tall = 8 + experts

    def pairs(*shape):
        return [DMA(shape), DMA(shape)]

    return pl.pallas_call(
        partial(back_body, n_e, n_h, experts, capacity, padded, heads),
        name="back",
        out_shape=[
            shape_of(y_out.shape, BF),
            shape_of((n_h, rows, model), BF),
            shape_of((rows, model), F32),
            shape_of((4 * width, model), BF),
            shape_of((tall, model), F32),
            shape_of((2, *shard), BF),
        ],
        in_specs=[VMEM] * 12 + [ANY] * 13,
        out_specs=[ANY] * 2 + [VMEM] * 4,
        scratch_shapes=[
            pltpu.VMEM((experts * capacity, model), BF),
            pltpu.VMEM((rows, model), BF),
            pltpu.VMEM((rows, model), F32),
            pltpu.VMEM((n_h, rows, model), BF),
            pltpu.VMEM((3 * width, group), BF),
            pltpu.VMEM((n_h, width, rows), BF),
            pltpu.VMEM((n_h, width, rows), BF),
            pltpu.VMEM((n_h, width, model), BF),
            pltpu.VMEM((3 * width, model), BF),
            pltpu.VMEM((n_h, width, rows), BF),
            pltpu.VMEM((n_h, width, rows), BF),
            pltpu.VMEM((far, width, model), BF),
            pltpu.VMEM((far - 1, width, model), BF),
            pltpu.VMEM((2, heads, REACH, BLOCK, BLOCK), BF),
            pltpu.VMEM((heads, group, HEAD_DIM), BF),
            pltpu.VMEM((width, BLOCK), F32),
            pltpu.VMEM((width, group), F32),
            pltpu.VMEM((width, group), F32),
            pltpu.VMEM((3 * width, group), BF),
            pltpu.VMEM((3 * width, model), F32),
            pltpu.VMEM((2, *shard), BF),
            pltpu.VMEM((2, far - 1, *shard), BF),
            DMA((9,)),
            DMA,
            DMA((2,)),
            DMA((2,)),
            DMA,
            *pairs(n_e),
            *pairs(n_h),
            *pairs(far),
            *pairs(far),
            *pairs(far, 2),
        ],
        compiler_params=pltpu.CompilerParams(
            collective_id=cid, has_side_effects=True, vmem_limit_bytes=60 << 20
        ),
    )(
        ids,
        slot,
        pos,
        gates,
        count,
        g1,
        s1,
        g2,
        s2,
        w_router,
        inverse,
        dg_rows,
        dx_back.reshape(experts * capacity, model),
        y_out,
        dw_sum,
        dw_far,
        out_grad,
        residual,
        all_tokens,
        qkv,
        att,
        att_t,
        w_out.reshape(n_h, width, model),
        w_t,
        weights,
    )


def shards(
    tokens,
    doc_lengths,
    expert_ids,
    gain_one,
    shift_one,
    w_query,
    w_key,
    w_value,
    w_out,
    gain_two,
    shift_two,
    w_router,
    w_up,
    w_down,
    out_grad,
):
    rows, model = tokens.shape
    n_expert, n_hidden = lax.axis_size("expert"), lax.axis_size("hidden")
    experts = n_expert * w_up.shape[0]
    capacity = max(2, rows * 2 * 5 // (4 * experts))
    capacity = -(-capacity // 16) * 16
    total = experts * capacity
    heads = HEADS // n_hidden
    width = heads * HEAD_DIM
    g1, s1, g2, s2 = gain_one, shift_one, gain_two, shift_two
    router_t = w_router.T

    (
        all_tokens,
        qkv,
        att,
        att_t,
        w_t,
        g_in,
        x_slots,
        ups,
        weights,
        ids,
        pos,
        slot,
        count,
        inverse,
        residual,
        gates,
        gate_rows,
    ) = run_front(
        doc_lengths,
        expert_ids.T,
        g1,
        s1,
        g2,
        s2,
        router_t,
        tokens,
        out_grad,
        (w_query, w_key, w_value, w_out),
        w_up,
        capacity,
        heads,
        1,
    )
    dx_back, dg_back, y_out, dw_sum, dw_far = run_experts(
        x_slots, gate_rows, g_in, ups, w_up, w_down, 2
    )
    y_back, d_hidden, d_res, w_all, small, dw_own = run_back(
        ids,
        slot,
        pos,
        gates,
        count,
        g1,
        s1,
        g2,
        s2,
        router_t,
        inverse,
        dg_back,
        dx_back,
        y_out,
        dw_sum,
        dw_far,
        out_grad,
        residual,
        all_tokens,
        qkv,
        att,
        att_t,
        w_out,
        w_t,
        weights,
        3,
    )
    input_grad, output, full, small = run_tail(
        d_hidden,
        w_all.reshape(n_expert, 4 * width // n_expert, model),
        small,
        tokens,
        g1,
        d_res,
        residual,
        gates,
        pos,
        y_back.reshape(total, model),
        4,
    )
    scale = experts / (rows * n_expert * n_hidden * 2)
    turned = turn_weights(
        full.reshape(n_hidden, 4 * width, model),
        dw_own,
        small,
        input_grad,
        output,
        width,
        experts,
        scale,
    )
    w_grads, (up_grad, down_grad) = turned[:4], turned[4:6]
    gain_one_grad, shift_one_grad, gain_two_grad, shift_two_grad = turned[6:10]
    router_grad, input_grad, output, load = turned[10:]
    return (
        output,
        input_grad,
        gain_one_grad,
        shift_one_grad,
        *w_grads,
        gain_two_grad,
        shift_two_grad,
        router_grad.T,
        up_grad[None],
        down_grad[None],
        load,
    )


def solution(mesh):
    in_specs = (
        P(("expert", "hidden"), None),
        P("expert", None),
        P(("expert", "hidden"), None),
        P(),
        P(),
        P(),
        P(),
        P(),
        P(),
        P(),
        P(),
        P(),
        P("expert", None, "hidden"),
        P("expert", "hidden", None),
        P(("expert", "hidden"), None),
    )
    out_specs = (
        P(("expert", "hidden"), None),
        P(("expert", "hidden"), None),
        P(),
        P(),
        P(),
        P(),
        P(),
        P(),
        P(),
        P(),
        P(),
        P("expert", None, "hidden"),
        P("expert", "hidden", None),
        P(),
    )
    return jax.shard_map(shards, mesh=mesh, in_specs=in_specs, out_specs=out_specs, check_vma=False)
```

```python
from functools import partial

import jax
import jax.numpy as jnp
from jax import lax
from jax.experimental import pallas as pl
from jax.experimental.pallas import tpu as pltpu
from jax.sharding import PartitionSpec as P

HEAD_DIM = 64
HEADS = 12
EPSILON = 1e-05
SCALE = 0.125
MASKED = -1e30
BLOCK = 256
LONGEST = 1024
REACH = LONGEST // BLOCK + 1
UP_EARLY = 6
LANES = 128
BF = jnp.bfloat16
F32 = jnp.float32
I32 = jnp.int32
MESH = pl.DeviceIdType.MESH
ANY = pl.BlockSpec(memory_space=pl.ANY)
SMEM = pl.BlockSpec(memory_space=pltpu.SMEM)
VMEM = pl.BlockSpec(memory_space=pltpu.VMEM)
DMA = pltpu.SemaphoreType.DMA
GELU_A = 0.7978845608028654
GELU_B = 0.044715


def mm(left, right):
    return jnp.dot(left, right, preferred_element_type=F32)


def mm_nt(left, right):
    return lax.dot_general(left, right, (((1,), (1,)), ((), ())), preferred_element_type=F32)


def mm_tn(left, right):
    return lax.dot_general(left, right, (((0,), (0,)), ((), ())), preferred_element_type=F32)


def iota(shape, axis):
    return lax.broadcasted_iota(I32, shape, axis)


def norm_parts(values):
    centred = values - jnp.mean(values, axis=-1, keepdims=True)
    inverse = lax.rsqrt(jnp.mean(centred * centred, axis=-1, keepdims=True) + EPSILON)
    return centred * inverse, inverse


def norm_back(grad_out, normed, inverse, gain):
    grad_normed = grad_out * gain
    first = jnp.mean(grad_normed, axis=-1, keepdims=True)
    second = jnp.mean(grad_normed * normed, axis=-1, keepdims=True)
    return inverse * (grad_normed - first - normed * second)


def split_two(value):
    high = value.astype(BF)
    return high, (value - high.astype(F32)).astype(BF)


def shape_of(shape, dtype):
    return jax.ShapeDtypeStruct(shape, dtype)


def greet(peers):
    barrier = pltpu.get_barrier_semaphore()
    for peer in peers:
        pl.semaphore_signal(barrier, inc=1, device_id=peer, device_id_type=MESH)
    pl.semaphore_wait(barrier, len(peers))


def remote(src, dst, send, recv, peer):
    return pltpu.make_async_remote_copy(
        src_ref=src, dst_ref=dst, send_sem=send, recv_sem=recv, device_id=peer, device_id_type=MESH
    )


def doc_bounds(docs):
    ends, at = [], 0
    for n in range(docs.shape[1] - 1):
        at = at + docs[0, n]
        ends.append(at)
    return ends


def start_of(place, ends):
    begin = jnp.zeros_like(place)
    for end in ends:
        begin = jnp.where(place >= end, end, begin)
    return begin


def lying(ref):
    return ref[...].reshape(1, ref.shape[0])


def aligned(at, size):
    return pl.ds(pl.multiple_of(at, size), size)


def find_slots(experts, capacity, ids, ids_t, pos, slot, count):
    rows = ids_t.shape[1]
    row = [ids_t[j : j + 1, :] for j in range(2)]
    tall = jnp.concatenate([r.astype(F32) for r in row] + [jnp.zeros((6, rows), F32)], axis=0)
    ids[...] = tall.T[:, 0:2].astype(I32)
    col = [ids[:, j : j + 1] for j in range(2)]
    lane = iota((rows, LANES), 1)
    hot = [(lane == c).astype(BF) for c in col]
    either = hot[0] + hot[1]
    below = (iota((rows, rows), 0) > iota((rows, rows), 1)).astype(BF)
    before = mm(below, either)
    wide = max(experts, 16)
    deep = iota((wide, rows), 0)
    hot_t = [(deep == r).astype(BF) for r in row]
    above = (iota((rows, rows), 0) < iota((rows, rows), 1)).astype(BF)
    before_t = mm(hot_t[0] + hot_t[1], above)
    count[...] = jnp.sum(either.astype(F32), axis=0, keepdims=True)
    flat_t = []
    for j in range(2):
        at = jnp.sum(hot[j].astype(F32) * before, axis=1, keepdims=True).astype(I32)
        pos[:, j : j + 1] = col[j] * capacity + at
        slot[:, j : j + 1] = at
        at_t = jnp.sum(hot_t[j].astype(F32) * before_t, axis=0, keepdims=True).astype(I32)
        flat_t.append(row[j] * capacity + at_t)
    return flat_t


def fill_slots(flat_t, source, out):
    total, rows = out.shape[0], source.shape[0]
    half = total // 2
    for n in range(2):
        place = iota((half, rows), 0) + n * half
        pick = ((place == flat_t[0]) | (place == flat_t[1])).astype(BF)
        out[pl.ds(n * half, half), :] = mm(pick, source).astype(BF)


def attend_block(heads, ends, i, span, first, qkv, keys, scores, kept, inverse):
    width = heads * HEAD_DIM
    base = i * BLOCK
    rows = aligned(base, BLOCK)
    q_pos = base + iota((1, BLOCK), 1)
    begin = start_of(q_pos, ends)
    queries = [
        qkv[n * HEAD_DIM : (n + 1) * HEAD_DIM, rows] * jnp.asarray(SCALE, BF) for n in range(heads)
    ]
    tops = [jnp.full((1, BLOCK), MASKED, F32)] * heads
    for k in range(span):
        part = aligned((first + k) * BLOCK, BLOCK)
        k_pos = (first + k) * BLOCK + iota((BLOCK, BLOCK), 0)
        allowed = (k_pos <= q_pos) & (k_pos >= begin)
        for n in range(heads):
            score = jnp.where(allowed, mm(keys[n, part, :], queries[n]), MASKED)
            scores[n, k] = score
            tops[n] = jnp.maximum(tops[n], jnp.max(score, axis=0, keepdims=True))
    result = []
    for n in range(heads):
        total = jnp.zeros((1, BLOCK), F32)
        acc = jnp.zeros((HEAD_DIM, BLOCK), F32)
        lo = 2 * width + n * HEAD_DIM
        for k in range(span):
            weight = jnp.exp(scores[n, k] - tops[n])
            total = total + jnp.sum(weight, axis=0, keepdims=True)
            value = qkv[lo : lo + HEAD_DIM, aligned((first + k) * BLOCK, BLOCK)]
            low = weight.astype(BF)
            kept[n, k] = low
            acc = acc + mm(value, low)
        whole = 1.0 / total
        inverse[n : n + 1, rows] = whole
        result.append((acc * whole).astype(BF))
    return result


def spans(i, body):
    @pl.when(i < 2)
    def _short():
        body(2, 0)

    @pl.when(i >= 2)
    def _long():
        body(REACH, (i - (REACH - 1)) * (i // (REACH - 1)))


def front_body(
    n_e,
    n_h,
    experts,
    capacity,
    padded,
    heads,
    chunks,
    docs,
    ids_t,
    g1,
    s1,
    g2,
    s2,
    w_router,
    tokens,
    out_grad,
    w_query,
    w_key,
    w_value,
    w_out,
    w_up,
    all_tokens,
    qkv_out,
    att_out,
    att_t_out,
    w_t_out,
    g_in,
    x_slots,
    ups,
    weights,
    ids,
    pos,
    slot,
    count,
    inverse,
    residual,
    gates,
    gate_rows,
    tv,
    gv,
    wv,
    wo,
    w_t,
    qkv,
    keys,
    scores,
    kept,
    att_v,
    att_in,
    g_slots,
    xs_v,
    own_sem,
    w_sem,
    save_sem,
    kept_sem,
    ty_s,
    ty_r,
    tc_s,
    tc_r,
    tf_s,
    tf_r,
    gs_s,
    gs_r,
    at_s,
    at_r,
    wy_s,
    wy_r,
    wc_s,
    wc_r,
    wf_s,
    wf_r,
):
    e, h = lax.axis_index("expert"), lax.axis_index("hidden")
    far = n_h // 2
    pair, core = h // 2, lax.rem(h, 2)
    mate = pair * 2 + 1 - core
    rows, model = tokens.shape
    width = heads * HEAD_DIM
    per_device = rows // BLOCK
    ends = doc_bounds(docs)

    def across(t):
        return lax.rem(pair + t, far) * 2 + core

    def origin(t):
        return lax.rem(pair + far - t, far) * 2 + core

    own_tokens = pltpu.make_async_copy(tokens, tv.at[h], own_sem.at[0])
    own_grad = pltpu.make_async_copy(out_grad, gv, own_sem.at[1])
    own_grad.start()
    own_tokens.start()
    w_loads = [
        pltpu.make_async_copy(w, wv.at[n], w_sem.at[n])
        for n, w in enumerate((w_query, w_key, w_value))
    ]
    w_loads.append(pltpu.make_async_copy(w_out, wo, w_sem.at[3]))
    for load in w_loads:
        load.start()
    greet(
        [{"hidden": lax.rem(h + step, n_h)} for step in range(1, n_h)]
        + [{"expert": lax.rem(e + step, n_e)} for step in range(1, n_e)]
    )

    piece = rows // chunks
    sends = []
    for k in range(chunks):
        part = pl.ds(k * piece, piece)
        for t in range(1, far):
            copy = remote(
                tokens.at[part],
                tv.at[h, part],
                ty_s.at[t, k],
                ty_r.at[t, k],
                {"hidden": across(t)},
            )
            copy.start()
            sends.append(copy)
    beside = remote(tokens, tv.at[h], tc_s, tc_r, {"hidden": mate})
    beside.start()
    sends.append(beside)

    flat_t = find_slots(experts, capacity, ids, ids_t, pos, slot, count)
    own_grad.wait()
    fill_slots(flat_t, gv[...], g_slots)
    for step in range(1, n_e):
        peer = lax.rem(e + step, n_e)
        copy = remote(
            g_slots.at[aligned(peer * capacity, capacity)],
            g_in.at[e],
            gs_s.at[step],
            gs_r.at[step],
            {"expert": peer},
        )
        copy.start()
        sends.append(copy)
    own_slots = pltpu.make_async_copy(
        g_slots.at[aligned(e * capacity, capacity)], g_in.at[e], own_sem.at[1]
    )
    own_slots.start()

    def pass_on(t, k):
        part = pl.ds(k * piece, piece)
        place = tv.at[origin(t), part]
        remote(place, place, ty_s.at[t, k], ty_r.at[t, k], {"hidden": across(t)}).wait_recv()
        copy = remote(place, place, tf_s.at[t, k], tf_r.at[t, k], {"hidden": mate})
        copy.start()
        sends.append(copy)

    todo = [(t, k) for k in range(chunks) for t in range(1, far)]
    third = -(-len(todo) // 4)

    def pass_some():
        for _ in range(min(third, len(todo))):
            pass_on(*todo.pop(0))

    pick = (iota((width, model), 1) == iota((width, model), 0) + h * width).astype(BF)
    for n in range(3):
        w_loads[n].wait()
        w_t[n * width : (n + 1) * width, :] = mm_nt(pick, wv[n]).astype(BF)
        if n == 1:
            pass_some()
    save_w = pltpu.make_async_copy(w_t, w_t_out, save_sem.at[0])
    save_w.start()

    def project(source):
        def one(b, _):
            normed, _unused = norm_parts(tv[source, aligned(b * BLOCK, BLOCK), :].astype(F32))
            hidden = (normed * lying(g1) + lying(s1)).astype(BF)
            block = mm_nt(w_t[...], hidden)
            cols = aligned(source * rows + b * BLOCK, BLOCK)
            qkv[:, cols] = block.astype(BF)
            for n in range(heads):
                lo = width + n * HEAD_DIM
                keys[n, cols, :] = block[lo : lo + HEAD_DIM].T.astype(BF)
            return 0

        lax.fori_loop(0, per_device, one, 0)

    pass_some()
    own_tokens.wait()
    project(h)
    pass_some()
    remote(tokens, tv.at[mate], tc_s, tc_r, {"hidden": mate}).wait_recv()
    project(mate)
    while todo:
        pass_some()

    early = w_up.shape[1] * UP_EARLY // 8

    def up_copy(t, source):
        place = pl.ds(0, early)
        return remote(
            w_up.at[0, place], ups.at[source, place], wy_s.at[t], wy_r.at[t], {"hidden": across(t)}
        )

    def up_onward(t):
        place = ups.at[origin(t), pl.ds(0, early)]
        return remote(place, place, wf_s.at[t], wf_r.at[t], {"hidden": mate})

    up_beside = remote(w_up.at[0], ups.at[h], wc_s, wc_r, {"hidden": mate})
    up_beside.start()
    sends.append(up_beside)
    for t in range(1, far):
        up_copy(t, h).start()
    for t in range(1, far):
        project(origin(t))
    for t in range(1, far):
        there = lax.rem(pair + far - t, far) * 2 + 1 - core
        for k in range(chunks):
            place = tv.at[there, pl.ds(k * piece, piece)]
            remote(place, place, tf_s.at[t, k], tf_r.at[t, k], {"hidden": mate}).wait_recv()
        project(there)
    save_tokens = pltpu.make_async_copy(tv, all_tokens, save_sem.at[1])
    save_qkv = pltpu.make_async_copy(qkv, qkv_out, save_sem.at[2])
    save_tokens.start()
    save_qkv.start()

    inverse[...] = jnp.zeros_like(inverse)

    def device_at(n, sign):
        t, other = n // 2, lax.rem(n, 2)
        return lax.rem(pair + far + sign * t, far) * 2 + lax.rem(core + other, 2)

    def give_att(n):
        owner = device_at(n, 1)
        return remote(
            att_v.at[owner], att_in.at[h], at_s.at[n], at_r.at[n], {"hidden": owner}
        )

    def save_kept(i, turn):
        return pltpu.make_async_copy(kept.at[turn], weights.at[i], kept_sem.at[turn])

    def attend(at, _):
        n = n_h - 1 - at // per_device
        b = lax.rem(at, per_device)
        owner = device_at(n, 1)
        i = owner * per_device + b
        turn = lax.rem(at, 2)

        @pl.when(at >= 2)
        def _free():
            save_kept(i, turn).wait()

        def block(span, first):
            done = attend_block(
                heads, ends, i, span, first, qkv, keys, scores, kept.at[turn], inverse
            )
            for m in range(heads):
                lo = m * HEAD_DIM
                att_v[owner, lo : lo + HEAD_DIM, aligned(b * BLOCK, BLOCK)] = done[m]

        spans(i, block)
        save_kept(i, turn).start()

        @pl.when((b == per_device - 1) & (n > 0))
        def _give():
            give_att(n).start()

        return 0

    lax.fori_loop(0, n_h * per_device, attend, 0)
    for t in range(1, far):
        up_copy(t, origin(t)).wait_recv()
        up_onward(t).start()
    att_in[h] = att_v[h]
    save_att = pltpu.make_async_copy(att_v, att_out, save_sem.at[3])
    save_att.start()
    for n in range(n_h - 1, 0, -1):
        give_att(n).wait_recv()
    save_att_t = pltpu.make_async_copy(att_in, att_t_out, save_sem.at[4])
    save_att_t.start()

    w_loads[3].wait()
    res = tv[h].astype(F32) + mm_tn(att_in[...].reshape(model, rows), wo[...])
    residual[...] = res
    normed, _unused = norm_parts(res)
    hidden = (normed * lying(g2) + lying(s2)).astype(BF)
    fill_slots(flat_t, hidden, xs_v)
    save_x = [
        pltpu.make_async_copy(
            xs_v.at[pl.ds(n * capacity, capacity)], x_slots.at[n], save_sem.at[5 + n]
        )
        for n in range(experts)
    ]
    for save in save_x:
        save.start()
    logits = mm_nt(hidden, w_router[...])
    lane = iota((rows, experts), 1)
    chosen = [
        jnp.sum(jnp.where(lane == ids[:, j : j + 1], logits, 0.0), axis=1, keepdims=True)
        for j in range(2)
    ]
    top = jnp.maximum(chosen[0], chosen[1])
    raised = [jnp.exp(c - top) for c in chosen]
    both = raised[0] + raised[1]
    gate = [r / both for r in raised]
    for j in range(2):
        gates[:, j : j + 1] = gate[j]
    column = iota((rows, padded), 1)
    for n in range(experts):
        mix = jnp.zeros((rows, padded), F32)
        for j in range(2):
            here = jnp.where(ids[:, j : j + 1] == n, slot[:, j : j + 1], -1) == column
            mix = jnp.where(here, gate[j], mix)
        line = jnp.sum(mix, axis=0, keepdims=True)
        gate_rows[n] = jnp.broadcast_to(line, (8, padded))

    place = ups.at[mate]
    remote(place, place, wc_s, wc_r, {"hidden": mate}).wait_recv()
    for t in range(1, far):
        up_onward(t).wait()
    for step in range(1, n_e):
        source = lax.rem(e + n_e - step, n_e)
        place = g_in.at[source]
        remote(place, place, gs_s.at[step], gs_r.at[step], {"expert": e}).wait_recv()
    own_slots.wait()
    for n in range(1, n_h):
        give_att(n).wait_send()
    for turn in range(2):
        save_kept(0, turn).wait()
    for t in range(1, far):
        up_copy(t, h).wait_send()
    for copy in sends:
        copy.wait_send()
    for save in [save_w, save_tokens, save_qkv, save_att, save_att_t, *save_x]:
        save.wait()


def run_front(
    docs, ids_t, g1, s1, g2, s2, w_router, tokens, out_grad, ws, w_up, capacity, heads, cid
):
    n_e, n_h = lax.axis_size("expert"), lax.axis_size("hidden")
    experts = n_e * w_up.shape[0]
    rows, model = tokens.shape
    padded = -(-capacity // LANES) * LANES
    width, group, total = heads * HEAD_DIM, rows * n_h, experts * capacity
    far, chunks = n_h // 2, 8

    def pairs(*shape):
        return [DMA(shape), DMA(shape)]

    return pl.pallas_call(
        partial(front_body, n_e, n_h, experts, capacity, padded, heads, chunks),
        name="front",
        out_shape=[
            shape_of((n_h, rows, model), BF),
            shape_of((3 * width, group), BF),
            shape_of((n_h, width, rows), BF),
            shape_of((n_h, width, rows), BF),
            shape_of((3 * width, model), BF),
            shape_of((experts, capacity, model), BF),
            shape_of((experts, capacity, model), BF),
            shape_of((n_h, *w_up.shape[1:]), BF),
            shape_of((group // BLOCK, heads, REACH, BLOCK, BLOCK), BF),
            shape_of((rows, 2), I32),
            shape_of((rows, 2), I32),
            shape_of((rows, 2), I32),
            shape_of((1, LANES), F32),
            shape_of((8, group), F32),
            shape_of((rows, model), F32),
            shape_of((rows, 2), F32),
            shape_of((experts, 8, padded), F32),
        ],
        in_specs=[SMEM] + [VMEM] * 6 + [ANY] * 7,
        out_specs=[ANY] * 9 + [VMEM] * 8,
        scratch_shapes=[
            pltpu.VMEM((n_h, rows, model), BF),
            pltpu.VMEM((rows, model), BF),
            pltpu.VMEM((3, model, model), BF),
            pltpu.VMEM((model, model), BF),
            pltpu.VMEM((3 * width, model), BF),
            pltpu.VMEM((3 * width, group), BF),
            pltpu.VMEM((heads, group, HEAD_DIM), BF),
            pltpu.VMEM((heads, REACH, BLOCK, BLOCK), F32),
            pltpu.VMEM((2, heads, REACH, BLOCK, BLOCK), BF),
            pltpu.VMEM((n_h, width, rows), BF),
            pltpu.VMEM((n_h, width, rows), BF),
            pltpu.VMEM((total, model), BF),
            pltpu.VMEM((total, model), BF),
            DMA((2,)),
            DMA((4,)),
            DMA((5 + experts,)),
            DMA((2,)),
            *pairs(far, chunks),
            DMA,
            DMA,
            *pairs(far, chunks),
            *pairs(n_e),
            *pairs(n_h),
            *pairs(far),
            DMA,
            DMA,
            *pairs(far),
        ],
        compiler_params=pltpu.CompilerParams(
            collective_id=cid, has_side_effects=True, vmem_limit_bytes=58 << 20
        ),
    )(docs, ids_t, g1, s1, g2, s2, w_router, tokens, out_grad, *ws, w_up)


def moe_body(
    size,
    capacity,
    padded,
    per,
    x_slots,
    gate_rows,
    g_in,
    ups,
    w_up,
    w_down,
    dx_back,
    dg_back,
    y_out,
    dw_sum,
    dw_far,
    xv,
    gv,
    gates_v,
    up_v,
    down_v,
    act,
    dz,
    xg,
    dy,
    xg_t,
    dy_t,
    dxv,
    yv,
    dgv,
    y_acc,
    dx_acc,
    dw_box,
    load_sem,
    save_sem,
    wy_s,
    wy_r,
    wc_s,
    wc_r,
    wf_s,
    wf_r,
    dc_s,
    dc_r,
    df_s,
    df_r,
    g_sem,
    own_sem,
    xs_sem,
    xr_sem,
    gs_sem,
    gr_sem,
    ds_sem,
    dr_sem,
    ts_sem,
    tr_sem,
    out_sem,
):
    me, h = lax.axis_index("expert"), lax.axis_index("hidden")
    shards_n = ups.shape[0]
    far = shards_n // 2
    pair, core = h // 2, lax.rem(h, 2)
    mate = pair * 2 + 1 - core
    deep = w_down.shape[1] // 2
    tall = per * capacity
    steps = size // per

    middle = size // 2
    inner = lax.rem((me // 2 * 8 // size + 1) // 2, 2)

    def group_at(step):
        some = steps // 4
        early = jnp.where(step <= some, step - 1 + steps // 2, step - some)
        early = jnp.where((step > 0) & (step < steps - some), early, step)
        return jnp.where(inner == 1, early, step)

    def peer_at(p):
        peer, bit = 0, 1
        while bit < size:
            peer = peer + lax.rem(me // bit + p // bit, 2) * bit
            bit *= 2
        return peer

    def rows_of(p):
        return pl.ds(pl.multiple_of(p * capacity, capacity), capacity)

    def send_x(p):
        peer = peer_at(p)
        return remote(
            x_slots.at[peer], xv.at[rows_of(p)], xs_sem.at[p], xr_sem.at[p], {"expert": peer}
        )

    def send_gate(p):
        peer = peer_at(p)
        return remote(
            gate_rows.at[peer], gates_v.at[p], gs_sem.at[p], gr_sem.at[p], {"expert": peer}
        )

    def send_dx(p):
        peer = peer_at(p)
        return remote(
            dxv.at[rows_of(p)], dx_back.at[me], ds_sem.at[p], dr_sem.at[p], {"expert": peer}
        )

    def send_dg(p):
        peer = peer_at(p)
        return remote(dgv.at[p], dg_back.at[me], ts_sem.at[p], tr_sem.at[p], {"expert": peer})

    def load_g(p):
        return pltpu.make_async_copy(g_in.at[peer_at(p)], gv.at[rows_of(p)], g_sem.at[p])

    def save_y(p):
        return pltpu.make_async_copy(yv.at[rows_of(p)], y_out.at[peer_at(p)], out_sem.at[p])

    own_x = pltpu.make_async_copy(x_slots.at[me], xv.at[rows_of(0)], own_sem.at[0])
    own_gate = pltpu.make_async_copy(gate_rows.at[me], gates_v.at[0], own_sem.at[1])
    own_dx = pltpu.make_async_copy(dxv.at[rows_of(0)], dx_back.at[me], own_sem.at[2])
    own_dg = pltpu.make_async_copy(dgv.at[0], dg_back.at[me], own_sem.at[3])
    loads = [
        pltpu.make_async_copy(w_up.at[0], up_v.at[h], load_sem.at[0]),
        pltpu.make_async_copy(w_down.at[0], down_v.at[h], load_sem.at[1]),
    ]
    loads.append(pltpu.make_async_copy(ups.at[mate], up_v.at[mate], load_sem.at[2]))

    early = w_up.shape[1] * UP_EARLY // 8

    def half(k):
        return aligned(k * deep, deep)

    for t in range(1, far):
        for other in range(2):
            c = lax.rem(pair + t, far) * 2 + other
            place = (c, pl.ds(0, early))
            loads.append(
                pltpu.make_async_copy(
                    ups.at[place], up_v.at[place], load_sem.at[1 + 2 * t + other]
                )
            )
    rest = pl.ds(early, w_up.shape[1] - early)
    parts = ((w_up, up_v, rest), (w_down, down_v, half(0)), (w_down, down_v, half(1)))

    def part_across(t, n):
        source, target, k = parts[n]
        there = {"hidden": lax.rem(pair + t, far) * 2 + core}
        return remote(
            source.at[0, k], target.at[h, k], wy_s.at[t, n], wy_r.at[t, n], there
        )

    def part_onward(t, n):
        _source, target, k = parts[n]
        place = target.at[lax.rem(pair + far - t, far) * 2 + core, k]
        return remote(place, place, wf_s.at[t, n], wf_r.at[t, n], {"hidden": mate})

    down_beside = remote(w_down.at[0], down_v.at[h], wc_s, wc_r, {"hidden": mate})
    own_x.start()
    own_gate.start()
    for p in range(size):
        load_g(p).start()
    for load in loads:
        load.start()
    greet(
        [{"expert": lax.rem(me + step, size)} for step in range(1, size)]
        + [{"hidden": lax.rem(h + step, shards_n)} for step in range(1, shards_n)]
    )

    def send_all(order):
        for p in order:
            send_x(p).start()
            send_gate(p).start()

    @pl.when(inner == 1)
    def _far_first():
        send_all([1, *range(middle, size), *range(2, middle)])

    @pl.when(inner == 0)
    def _near_first():
        send_all(range(1, size))

    for n in range(3):
        for t in range(1, far):
            part_across(t, n).start()
    down_beside.start()
    own_x.wait()
    own_gate.wait()
    for load in loads:
        load.wait()

    def finish(base, rows, held):
        dxv[rows, :] = dx_acc[held, :].astype(BF)
        y_low = y_acc[held, :].astype(BF)
        yv[rows, :] = y_low
        x, g = xv[rows, :], gv[rows, :]
        dots = jnp.sum(y_low.astype(F32) * g.astype(F32), axis=1, keepdims=True)
        for s in range(per):
            p = base + s
            part = slice(s * capacity, (s + 1) * capacity)
            tall_dots = jnp.broadcast_to(dots[part], (capacity, LANES))
            if padded > capacity:
                blank = jnp.zeros((padded - capacity, LANES), F32)
                tall_dots = jnp.concatenate([tall_dots, blank], axis=0)
            dgv[p] = tall_dots.T[0:8]

            @pl.when(p > 0)
            def _give(p=p):
                send_dx(p).start()
                send_dg(p).start()

            @pl.when(p == 0)
            def _keep():
                own_dx.start()
                own_dg.start()

            save_y(p).start()
        for s in range(per):
            p = base + s
            part = slice(s * capacity, (s + 1) * capacity)
            gate = gates_v[p].T[0:capacity, 0:1]
            xg[rows_of(p), :] = (x[part].astype(F32) * gate).astype(BF)
            dy[rows_of(p), :] = (g[part].astype(F32) * gate).astype(BF)

    first = shards_n // 2

    def unit(m):
        step = jnp.where(m < 2 * shards_n, lax.rem(m // first, 2), m // shards_n)
        n = m // shards_n * first + lax.rem(m, first)
        n = jnp.where(m < 2 * shards_n, n, lax.rem(m, shards_n))
        return step, n

    def unit_body(m, _):
        step, n = unit(m)
        base = group_at(step) * per
        rows = pl.ds(pl.multiple_of(base * capacity, tall), tall)
        held = aligned(jnp.where(step == 1, tall, 0), tall)

        @pl.when(n == 0)
        def _begin():
            for s in range(per):

                @pl.when(base + s > 0)
                def _arrive(s=s):
                    send_x(base + s).wait_recv()
                    send_gate(base + s).wait_recv()

                load_g(base + s).wait()
            y_acc[held, :] = jnp.zeros((tall, y_acc.shape[1]), F32)
            dx_acc[held, :] = jnp.zeros((tall, y_acc.shape[1]), F32)

        t = n // 2
        beside = lax.rem(n, 2)
        c = lax.rem(pair + far - t, far) * 2 + lax.rem(core + beside, 2)

        @pl.when(m == 1)
        def _beside():
            down_beside.wait_recv()

        @pl.when((step == 0) & (n >= 2) & (beside == 0))
        def _across():
            for k in range(3):
                part_across(t, k).wait_recv()
                part_onward(t, k).start()

        @pl.when((step == 0) & (n >= 2) & (beside == 1))
        def _onward():
            for k in range(3):
                part_onward(t, k).wait_recv()

        x, g = xv[rows, :], gv[rows, :]
        z = mm(x, up_v[c])
        du = mm_nt(g, down_v[c])
        square = z * z
        curve = jnp.tanh(z * (GELU_A + GELU_A * GELU_B * square))
        plus = 0.5 + 0.5 * curve
        hidden = (z * plus).astype(BF)
        rise = GELU_A + 3.0 * GELU_A * GELU_B * square
        slope = plus + 0.5 * z * (1.0 - curve * curve) * rise
        back = (slope * du).astype(BF)
        act[c, rows, :] = hidden
        dz[c, rows, :] = back
        y_acc[held, :] += mm(hidden, down_v[c])
        dx_acc[held, :] += mm_nt(back, up_v[c])

        @pl.when(n == shards_n - 1)
        def _end():
            finish(base, rows, held)

        return 0

    lax.fori_loop(0, steps * shards_n, unit_body, 0)

    total = size * capacity
    turn = 256
    for k in range(total // turn):
        rows = slice(k * turn, (k + 1) * turn)
        xg_t[:, rows] = xg[rows, :].astype(F32).T.astype(BF)
    for t in range(1, far):
        for k in range(3):
            part_across(t, k).wait_send()
            part_onward(t, k).wait_send()
    down_beside.wait_send()

    def give(which, step):
        source = (up_v, down_v)[which].at[lax.rem(pair + step, far) * 2 + 1 - core]
        return remote(
            source,
            dw_box.at[which, step],
            dc_s.at[which, step],
            dc_r.at[which, step],
            {"hidden": mate},
        )

    def keep(which, step):
        source = (up_v, down_v)[which].at[lax.rem(pair + step, far) * 2 + core]
        return pltpu.make_async_copy(source, dw_sum.at[which, step], save_sem.at[which, step])

    def cross(step, k):
        there = lax.rem(pair + step, far) * 2 + core
        return remote(
            up_v.at[there, half(k)],
            dw_far.at[step - 1, half(k)],
            df_s.at[step, k],
            df_r.at[step, k],
            {"hidden": there},
        )

    def gradients(which, left, right, held):
        def other(n, _):
            step = lax.rem(n + 1, far)
            c = lax.rem(pair + step, far) * 2 + 1 - core
            held[c] = mm(left[...], right[c]).astype(BF)
            give(which, step).start()
            return 0

        def own(n, _):
            step = lax.rem(n + 1, far)
            c = lax.rem(pair + step, far) * 2 + core
            total_of = mm(left[...], right[c])
            give(which, step).wait_recv()
            held[c] = (total_of + dw_box[which, step].astype(F32)).astype(BF)
            keep(which, step).start()

            if which == 0:

                @pl.when(step > 0)
                def _cross():
                    for k in range(2):
                        cross(step, k).start()

            return 0

        lax.fori_loop(0, far, other, 0)
        lax.fori_loop(0, far, own, 0)

    gradients(0, xg_t, dz, up_v)
    for k in range(total // turn):
        rows = slice(k * turn, (k + 1) * turn)
        dy_t[:, rows] = dy[rows, :].astype(F32).T.astype(BF)
    gradients(1, dy_t, act, down_v)
    for p in range(1, size):
        send_x(p).wait_send()
        send_gate(p).wait_send()
        send_dx(p).wait()
        send_dg(p).wait()
    for p in range(size):
        save_y(p).wait()
    own_dx.wait()
    own_dg.wait()
    for step in range(far):
        for which in range(2):
            give(which, step).wait_send()
            keep(which, step).wait()
    for step in range(1, far):
        for k in range(2):
            cross(step, k).wait()


def run_experts(x_slots, gate_rows, g_in, ups, w_up, w_down, cid):
    size = lax.axis_size("expert")
    experts, capacity, model = x_slots.shape
    padded = gate_rows.shape[2]
    shards_n, _unused, width = ups.shape
    total = experts * capacity
    per = 1
    while per * 2 * capacity <= 320 and size % (per * 2) == 0:
        per *= 2
    tall = per * capacity
    rows2 = (total, model)
    return pl.pallas_call(
        partial(moe_body, size, capacity, padded, per),
        name="experts",
        out_shape=[
            shape_of(x_slots.shape, BF),
            shape_of(gate_rows.shape, F32),
            shape_of(x_slots.shape, BF),
            shape_of((2, shards_n // 2, model, width), BF),
            shape_of((shards_n // 2 - 1, model, width), BF),
        ],
        in_specs=[ANY] * 6,
        out_specs=[ANY] * 5,
        scratch_shapes=[
            pltpu.VMEM(rows2, BF),
            pltpu.VMEM(rows2, BF),
            pltpu.VMEM(gate_rows.shape, F32),
            pltpu.VMEM((shards_n, model, width), BF),
            pltpu.VMEM((shards_n, width, model), BF),
            pltpu.VMEM((shards_n, total, width), BF),
            pltpu.VMEM((shards_n, total, width), BF),
            pltpu.VMEM(rows2, BF),
            pltpu.VMEM(rows2, BF),
            pltpu.VMEM((model, total), BF),
            pltpu.VMEM((model, total), BF),
            pltpu.VMEM(rows2, BF),
            pltpu.VMEM(rows2, BF),
            pltpu.VMEM(gate_rows.shape, F32),
            pltpu.VMEM((2 * tall, model), F32),
            pltpu.VMEM((2 * tall, model), F32),
            pltpu.VMEM((2, shards_n // 2, model, width), BF),
            DMA((shards_n + 1,)),
            DMA((2, shards_n // 2)),
            DMA((shards_n // 2, 3)),
            DMA((shards_n // 2, 3)),
            DMA,
            DMA,
            DMA((shards_n // 2, 3)),
            DMA((shards_n // 2, 3)),
            DMA((2, shards_n // 2)),
            DMA((2, shards_n // 2)),
            DMA((shards_n // 2, 2)),
            DMA((shards_n // 2, 2)),
            DMA((size,)),
            DMA((4,)),
        ]
        + [DMA((size,))] * 9,
        compiler_params=pltpu.CompilerParams(
            collective_id=cid, has_side_effects=True, vmem_limit_bytes=60 << 20
        ),
        cost_estimate=pl.CostEstimate(
            flops=12 * total * model * width * shards_n, bytes_accessed=40 << 20, transcendentals=0
        ),
    )(x_slots, gate_rows, g_in, ups, w_up, w_down)


def tail_body(
    n_e,
    n_h,
    chunks,
    dh,
    w_all,
    small,
    tokens,
    gain,
    d_res,
    residual,
    gates,
    pos,
    y_back,
    input_grad,
    output,
    full,
    total,
    wv,
    tok_v,
    d_res_v,
    res_v,
    yv,
    mine,
    beside,
    across,
    passing,
    x_box,
    z_box,
    w_mid,
    piece,
    small_mid,
    small_h,
    small_e,
    load_sem,
    mine_sem,
    cs_sem,
    cr_sem,
    as_sem,
    ar_sem,
    ws_sem,
    wr_sem,
    vs_sem,
    vr_sem,
    hs_sem,
    hr_sem,
    es_sem,
    er_sem,
    keep_sem,
    zs_sem,
    zr_sem,
    xs_sem,
    xr_sem,
    ys_sem,
    yr_sem,
    ms_sem,
    mr_sem,
):
    e, h = lax.axis_index("expert"), lax.axis_index("hidden")
    far, high = n_h // 2, n_e // 2
    pair, core = h // 2, lax.rem(h, 2)
    eh, el = e // 2, lax.rem(e, 2)
    mate = pair * 2 + 1 - core
    greet(
        [{"expert": lax.rem(e + step, n_e)} for step in range(1, n_e)]
        + [{"hidden": lax.rem(h + step, n_h)} for step in range(1, n_h)]
    )
    w_sends, w_order = {}, list(range(1, high)) + [0]
    for step in w_order:
        there = lax.rem(eh + step, high)
        copy = remote(
            w_all.at[there * 2 + 1 - el],
            x_box.at[step],
            ws_sem.at[step],
            wr_sem.at[step],
            {"expert": eh * 2 + 1 - el},
        )
        copy.start()
        w_sends[step] = copy
    rows = dh.shape[1] // chunks
    core_sends = {}
    for step in list(range(1, far)) + [0]:
        there = lax.rem(pair + step, far)
        for k in range(chunks):
            part = pl.ds(k * rows, rows)
            copy = remote(
                dh.at[there * 2 + 1 - core, part],
                beside.at[step, part],
                cs_sem.at[step, k],
                cr_sem.at[step, k],
                {"hidden": mate},
            )
            copy.start()
            core_sends[step, k] = copy
    mine_loads = []
    for step in range(far):
        there = lax.rem(pair + step, far)
        load = pltpu.make_async_copy(dh.at[there * 2 + core], mine.at[step], mine_sem.at[step])
        load.start()
        mine_loads.append(load)
    loads = [
        pltpu.make_async_copy(source, target, load_sem.at[n])
        for n, (source, target) in enumerate(
            ((w_all, wv), (residual, res_v), (y_back, yv), (tokens, tok_v), (d_res, d_res_v))
        )
    ]
    for load in loads:
        load.start()
    for load in mine_loads:
        load.wait()
    far_sends = []
    for step in range(1, far):
        there = lax.rem(pair + step, far)
        for k in range(chunks):
            part = pl.ds(k * rows, rows)
            core_sends[step, k].wait_recv()
            both = mine[step, part, :].astype(F32) + beside[step, part, :].astype(F32)
            passing[step - 1, part, :] = both.astype(BF)
            copy = remote(
                passing.at[step - 1, part],
                across.at[step - 1, part],
                as_sem.at[step - 1, k],
                ar_sem.at[step - 1, k],
                {"hidden": there * 2 + core},
            )
            copy.start()
            far_sends.append(copy)
    loads[0].wait()
    v_sends = []
    for step in w_order[:-1]:
        there = lax.rem(eh + step, high) * 2 + el
        w_sends[step].wait_recv()
        w_mid[step - 1] = (wv[there].astype(F32) + x_box[step].astype(F32)).astype(BF)
        copy = remote(
            w_mid.at[step - 1],
            z_box.at[step - 1],
            vs_sem.at[step],
            vr_sem.at[step],
            {"expert": there},
        )
        copy.start()
        v_sends.append(copy)
    small_sends = []
    for at in range(n_h - 1):
        peer = lax.rem(h + 1 + at, n_h)
        copy = remote(small, small_h.at[at], hs_sem.at[at], hr_sem.at[at], {"hidden": peer})
        copy.start()
        small_sends.append(copy)
    w_sends[0].wait_recv()
    acc = wv[e].astype(F32) + x_box[0].astype(F32)
    for at, copy in enumerate(v_sends):
        copy.wait_recv()
        acc = acc + z_box[at].astype(F32)
    piece[...] = acc.astype(BF)
    keep = pltpu.make_async_copy(piece, full.at[h, e], keep_sem)
    keep.start()
    started = []

    def slot(eh_of, el_of, pair_of, core_of):
        return full.at[pair_of * 2 + core_of, eh_of * 2 + el_of]

    def back(step, size, place):
        return lax.rem(place + size - step, size)

    def give_z(source):
        for s in range(1, high):
            there = lax.rem(eh + s, high) * 2 + el
            copy = remote(
                source, slot(eh, el, pair, core), zs_sem.at[s], zr_sem.at[s], {"expert": there}
            )
            copy.start()
            started.append(copy)

    def z_arrival(s):
        place = slot(back(s, high, eh), el, pair, core)
        return place, remote(place, place, zs_sem.at[s], zr_sem.at[s], {"expert": e})

    def give_x(source, s):
        target = slot(back(s, high, eh), el, pair, core)
        copy = remote(
            source, target, xs_sem.at[s], xr_sem.at[s], {"expert": eh * 2 + 1 - el}
        )
        copy.start()
        started.append(copy)

    def x_arrival(s):
        place = slot(back(s, high, eh), 1 - el, pair, core)
        return place, remote(place, place, xs_sem.at[s], xr_sem.at[s], {"expert": e})

    def give_y(source, s, flag):
        target = slot(back(s, high, eh), el if flag == 0 else 1 - el, pair, core)
        for t in range(1, far):
            there = lax.rem(pair + t, far) * 2 + core
            at = 2 * s + flag
            copy = remote(
                source, target, ys_sem.at[t, at], yr_sem.at[t, at], {"hidden": there}
            )
            copy.start()
            started.append(copy)

    def y_arrival(t, s, flag):
        other = el if flag == 0 else 1 - el
        place = slot(back(s, high, eh), other, back(t, far, pair), core)
        at = 2 * s + flag
        return place, remote(place, place, ys_sem.at[t, at], yr_sem.at[t, at], {"hidden": h})

    def give_mate(source, t, s, flag):
        other = el if flag == 0 else 1 - el
        target = slot(back(s, high, eh), other, back(t, far, pair), core)
        at = 2 * s + flag
        copy = remote(source, target, ms_sem.at[t, at], mr_sem.at[t, at], {"hidden": mate})
        copy.start()
        started.append(copy)

    def mate_arrival(t, s, flag):
        other = el if flag == 0 else 1 - el
        place = slot(back(s, high, eh), other, back(t, far, pair), 1 - core)
        at = 2 * s + flag
        return place, remote(place, place, ms_sem.at[t, at], mr_sem.at[t, at], {"hidden": h})

    give_z(piece)
    give_x(piece, 0)
    give_y(piece, 0, 0)
    give_mate(piece, 0, 0, 0)
    arrived = [(0, 0)]

    def take_x(s):
        place, arrival = x_arrival(s)
        arrival.wait_recv()
        give_y(place, s, 1)
        give_mate(place, 0, s, 1)
        arrived.append((s, 1))

    for s in range(1, high):
        place, arrival = z_arrival(s)
        arrival.wait_recv()
        give_x(place, s)
        give_y(place, s, 0)
        give_mate(place, 0, s, 0)
        arrived.append((s, 0))
        take_x(s - 1)
    take_x(high - 1)
    for copy in small_sends:
        copy.wait_recv()
    summed = small[...]
    for at in range(n_h - 1):
        summed = summed + small_h[at]
    small_mid[...] = summed
    small_out = []
    for at in range(n_e - 1):
        peer = lax.rem(e + 1 + at, n_e)
        copy = remote(small_mid, small_e.at[at], es_sem.at[at], er_sem.at[at], {"expert": peer})
        copy.start()
        small_out.append(copy)
    for load in loads[1:]:
        load.wait()
    place_of = iota((residual.shape[0], y_back.shape[0]), 1)
    result = res_v[...]
    for j in range(2):
        pick = (place_of == pos[:, j : j + 1]).astype(BF)
        result = result + gates[:, j : j + 1] * mm(pick, yv[...])
    output[...] = result.astype(BF)
    for k in range(chunks):
        part = pl.ds(k * rows, rows)
        core_sends[0, k].wait_recv()
    for copy in far_sends:
        copy.wait_recv()
    grad = mine[0].astype(F32) + beside[0].astype(F32)
    for step in range(far - 1):
        grad = grad + across[step].astype(F32)
    normed, inverse = norm_parts(tok_v[...].astype(F32))
    input_grad[...] = (d_res_v[...] + norm_back(grad, normed, inverse, lying(gain))).astype(BF)
    for t in range(1, far):
        for s, flag in arrived:
            place, arrival = y_arrival(t, s, flag)
            arrival.wait_recv()
            give_mate(place, t, s, flag)
    for copy in small_out:
        copy.wait_recv()
    summed = small_mid[...]
    for at in range(n_e - 1):
        summed = summed + small_e[at]
    total[...] = summed
    for t in range(far):
        for s, flag in arrived:
            _place, arrival = mate_arrival(t, s, flag)
            arrival.wait_recv()
    keep.wait()
    for copy in [*started, *w_sends.values(), *v_sends, *small_sends, *small_out, *far_sends]:
        copy.wait_send()
    for copy in core_sends.values():
        copy.wait_send()


def run_tail(dh, w_all, small, tokens, gain, d_res, residual, gates, pos, y_back, cid):
    n_e, n_h = lax.axis_size("expert"), lax.axis_size("hidden")
    far, high = n_h // 2, n_e // 2
    chunks = 4
    _unused, rows, model = dh.shape
    piece = w_all.shape[1:]
    return pl.pallas_call(
        partial(tail_body, n_e, n_h, chunks),
        name="tail",
        out_shape=[
            shape_of((rows, model), BF),
            shape_of((rows, model), BF),
            shape_of((n_h, n_e, *piece), BF),
            shape_of(small.shape, F32),
        ],
        in_specs=[ANY, ANY, VMEM, ANY, VMEM, ANY, ANY, VMEM, VMEM, ANY],
        out_specs=[VMEM, VMEM, ANY, VMEM],
        scratch_shapes=[
            pltpu.VMEM(w_all.shape, BF),
            pltpu.VMEM(tokens.shape, BF),
            pltpu.VMEM(d_res.shape, F32),
            pltpu.VMEM(residual.shape, F32),
            pltpu.VMEM(y_back.shape, BF),
            pltpu.VMEM((far, rows, model), BF),
            pltpu.VMEM((far, rows, model), BF),
            pltpu.VMEM((far - 1, rows, model), BF),
            pltpu.VMEM((far - 1, rows, model), BF),
            pltpu.VMEM((high, *piece), BF),
            pltpu.VMEM((high - 1, *piece), BF),
            pltpu.VMEM((high - 1, *piece), BF),
            pltpu.VMEM(piece, BF),
            pltpu.VMEM(small.shape, F32),
            pltpu.VMEM((n_h - 1, *small.shape), F32),
            pltpu.VMEM((n_e - 1, *small.shape), F32),
            DMA((5,)),
            DMA((far,)),
            DMA((far, chunks)),
            DMA((far, chunks)),
            DMA((far - 1, chunks)),
            DMA((far - 1, chunks)),
            DMA((high,)),
            DMA((high,)),
            DMA((high,)),
            DMA((high,)),
            DMA((n_h - 1,)),
            DMA((n_h - 1,)),
            DMA((n_e - 1,)),
            DMA((n_e - 1,)),
            DMA,
            DMA((high,)),
            DMA((high,)),
            DMA((high,)),
            DMA((high,)),
            DMA((far, n_e)),
            DMA((far, n_e)),
            DMA((far, n_e)),
            DMA((far, n_e)),
        ],
        compiler_params=pltpu.CompilerParams(
            collective_id=cid, has_side_effects=True, vmem_limit_bytes=56 << 20
        ),
    )(dh, w_all, small, tokens, gain, d_res, residual, gates, pos, y_back)


def turn_body(
    width,
    experts,
    scale,
    full,
    dw,
    small,
    input_grad,
    output,
    q_out,
    k_out,
    v_out,
    o_out,
    up_out,
    down_out,
    g1_out,
    s1_out,
    g2_out,
    s2_out,
    router_out,
    input_out,
    output_out,
    load_out,
):
    @pl.when(pl.program_id(0) == 0)
    def _begin():
        input_out[...] = input_grad[...]
        output_out[...] = output[...]
        for n, out in enumerate((g1_out, s1_out, g2_out, s2_out)):
            out[...] = small[n : n + 1, :].reshape(out.shape)
        router_out[...] = small[8 : 8 + experts, :]
        load_out[...] = small[4:5, 0:experts].reshape(experts) * scale

    for n, out in enumerate((q_out, k_out, v_out)):
        part = full[:, n * width : (n + 1) * width, :].astype(F32)
        out[...] = part.reshape(-1, part.shape[2]).T
    part = full[:, 3 * width :, :].astype(F32)
    o_out[...] = part.reshape(-1, part.shape[2])
    trained = jnp.where(lax.axis_index("expert") >= experts // 2, 1.0, 0.0)
    up_out[...] = dw[0].astype(F32) * trained
    down_out[...] = dw[1].astype(F32).T * trained


def turn_weights(full, dw, small, input_grad, output, width, experts, scale):
    n_h, deep, model = full.shape
    cols = 128
    across = pl.BlockSpec((cols, model), lambda i: (i, 0))
    down = pl.BlockSpec((model, cols), lambda i: (0, i))
    flat = pl.BlockSpec((model,), lambda i: (0,))
    whole = pl.BlockSpec(output.shape, lambda i: (0, 0))
    square = shape_of((model, model), F32)
    return pl.pallas_call(
        partial(turn_body, width, experts, scale),
        name="turn_weights",
        grid=(model // cols,),
        out_shape=[square] * 6
        + [shape_of((model,), F32)] * 4
        + [
            shape_of((experts, model), F32),
            shape_of(input_grad.shape, BF),
            shape_of(output.shape, BF),
            shape_of((experts,), F32),
        ],
        in_specs=[
            pl.BlockSpec((n_h, deep, cols), lambda i: (0, 0, i)),
            pl.BlockSpec((2, model, cols), lambda i: (0, 0, i)),
            pl.BlockSpec(small.shape, lambda i: (0, 0)),
            whole,
            whole,
        ],
        out_specs=[across, across, across, down, down, across]
        + [flat] * 4
        + [pl.BlockSpec((experts, model), lambda i: (0, 0)), whole, whole]
        + [pl.BlockSpec((experts,), lambda i: (0,))],
        compiler_params=pltpu.CompilerParams(
            dimension_semantics=("arbitrary",), vmem_limit_bytes=60 << 20
        ),
        cost_estimate=pl.CostEstimate(flops=0, bytes_accessed=24 << 20, transcendentals=0),
    )(full, dw, small, input_grad, output)


def attend_back(
    heads, i, span, first, qkv, given, centre, kept, values, dq_acc, dk_acc, dv_acc
):
    width = heads * HEAD_DIM
    rows = aligned(i * BLOCK, BLOCK)
    dq_acc[...] = jnp.zeros_like(dq_acc)
    queries = [
        qkv[n * HEAD_DIM : (n + 1) * HEAD_DIM, rows] * jnp.asarray(SCALE, BF) for n in range(heads)
    ]
    for k in range(span):
        part = aligned((first + k) * BLOCK, BLOCK)
        for n in range(heads):
            here = slice(n * HEAD_DIM, (n + 1) * HEAD_DIM)
            weight = kept[n, k]
            d_weight = mm(values[n, part, :], given[n])
            d_score = (weight.astype(F32) * (d_weight - centre[n])).astype(BF)
            dv_acc[here, part] += mm_nt(given[n], weight)
            dk_acc[here, part] += mm_nt(queries[n], d_score)
            lo = width + n * HEAD_DIM
            dq_acc[here, :] += mm(qkv[lo : lo + HEAD_DIM, part], d_score)


def back_body(
    n_e,
    n_h,
    experts,
    capacity,
    padded,
    heads,
    ids,
    slot,
    pos,
    gates,
    count,
    g1,
    s1,
    g2,
    s2,
    w_router,
    inverse,
    dg_rows,
    dx_back,
    y_out,
    dw_sum,
    dw_far,
    out_grad,
    residual,
    all_tokens,
    qkv_in,
    att_in,
    att_t_in,
    w_out,
    w_t_in,
    weights,
    y_back,
    d_hidden,
    d_res,
    w_all,
    small,
    dw_own,
    dxv,
    gv,
    res_v,
    tv,
    qkv,
    att_v,
    att_t,
    wo,
    w_t,
    d_att_v,
    d_att,
    wo_box,
    wo_far,
    kept,
    values,
    dq_acc,
    dk_acc,
    dv_acc,
    d_qkv,
    w_acc,
    dw_mine,
    dw_across,
    load_sem,
    save_sem,
    dw_sem,
    kept_sem,
    y_own,
    y_s,
    y_r,
    at_s,
    at_r,
    wo_s,
    wo_r,
    wf_s,
    wf_r,
    da_s,
    da_r,
):
    e, h = lax.axis_index("expert"), lax.axis_index("hidden")
    far = n_h // 2
    pair, core = h // 2, lax.rem(h, 2)
    mate = pair * 2 + 1 - core
    rows, model = out_grad.shape
    width = heads * HEAD_DIM
    group = rows * n_h
    per_device = rows // BLOCK
    blocks = group // BLOCK
    sends = []

    loads = [
        pltpu.make_async_copy(source, target, load_sem.at[n])
        for n, (source, target) in enumerate(
            (
                (residual, res_v),
                (dx_back, dxv),
                (out_grad, gv),
                (w_out, wo),
                (att_t_in, att_t),
                (qkv_in, qkv),
                (att_in, att_v),
                (all_tokens, tv),
                (w_t_in, w_t),
            )
        )
    ]
    for load in loads:
        load.start()
    greet(
        [{"hidden": lax.rem(h + step, n_h)} for step in range(1, n_h)]
        + [{"expert": lax.rem(e + step, n_e)} for step in range(1, n_e)]
    )
    load_dw = pltpu.make_async_copy(dw_sum.at[:, 0], dw_mine, dw_sem.at[0])
    load_dw.start()
    deep = dw_mine.shape[1] // 2
    load_far = pltpu.make_async_copy(
        dw_far, dw_across.at[0], dw_sem.at[1]
    )
    load_far.start()

    def dw_across_copy(step, k):
        part = pl.ds(k * deep, deep)
        return remote(
            dw_sum.at[1, step, part],
            dw_across.at[1, step - 1, part],
            da_s.at[step, k],
            da_r.at[step, k],
            {"hidden": lax.rem(pair + step, far) * 2 + core},
        )

    def dw_send(k):
        for step in range(1, far):
            dw_across_copy(step, k).start()

    dw_send(0)
    for step in range(1, n_e):
        peer = lax.rem(e + step, n_e)
        copy = remote(y_out.at[peer], y_back.at[e], y_s.at[step], y_r.at[step], {"expert": peer})
        copy.start()
        sends.append(copy)
    own_y = pltpu.make_async_copy(y_out.at[e], y_back.at[e], y_own)
    own_y.start()

    for load in loads[:3]:
        load.wait()
    normed, spread = norm_parts(res_v[...])
    hidden = (normed * lying(g2) + lying(s2)).astype(BF)
    gate = [gates[:, j : j + 1] for j in range(2)]
    column = iota((rows, padded), 1)
    dot_of = []
    for j in range(2):
        mix = jnp.zeros((rows, padded), F32)
        for n in range(experts):
            here = jnp.where(ids[:, j : j + 1] == n, slot[:, j : j + 1], -1) == column
            mix = jnp.where(here, dg_rows[n, 0:1, :], mix)
        dot_of.append(jnp.sum(mix, axis=1, keepdims=True))
    mean = gate[0] * dot_of[0] + gate[1] * dot_of[1]
    lane = iota((rows, experts), 1)
    d_logits = jnp.zeros((rows, experts), F32)
    for j in range(2):
        d_logits = jnp.where(lane == ids[:, j : j + 1], gate[j] * (dot_of[j] - mean), d_logits)
    high, low = split_two(d_logits)
    grad = mm(high, w_router[...]) + mm(low, w_router[...])
    small[...] = jnp.zeros_like(small)
    small[8 : 8 + experts, :] = mm_tn(high, hidden) + mm_tn(low, hidden)
    small[4:5, 0:LANES] = count[...]
    place = iota((rows, experts * capacity), 1)
    for j in range(2):
        pick = (place == pos[:, j : j + 1]).astype(BF)
        grad = grad + gate[j] * mm(pick, dxv[...])
    small[2:3, :] = jnp.sum(grad * normed, axis=0, keepdims=True)
    small[3:4, :] = jnp.sum(grad, axis=0, keepdims=True)
    d_resid = gv[...].astype(F32) + norm_back(grad, normed, spread, lying(g2))
    d_res[...] = d_resid
    branch = d_resid.astype(BF)
    loads[3].wait()

    def device_at(n, sign):
        t, other = n // 2, lax.rem(n, 2)
        return lax.rem(pair + far + sign * t, far) * 2 + lax.rem(core + other, 2)

    def give_att(n):
        owner = device_at(n, 1)
        return remote(
            d_att_v.at[owner], d_att.at[h], at_s.at[n], at_r.at[n], {"hidden": owner}
        )

    for n in range(n_h - 1, -1, -1):
        owner = device_at(n, 1)
        block = mm_nt(wo[owner], branch).astype(BF)
        if n == 0:
            d_att[h] = block
        else:
            d_att_v[owner] = block
            give_att(n).start()
    loads[4].wait()
    for t in range(n_h):
        owner = lax.rem(h + t, n_h)
        wo[owner] = mm(att_t[owner], branch).astype(BF)
    for step in list(range(1, far)) + [0]:
        copy = remote(
            wo.at[lax.rem(pair + step, far) * 2 + 1 - core],
            wo_box.at[step],
            wo_s.at[step],
            wo_r.at[step],
            {"hidden": mate},
        )
        copy.start()
        sends.append(copy)
    def give_wo(step):
        target = lax.rem(pair + step, far) * 2 + core
        return remote(
            wo.at[target],
            wo_far.at[step - 1],
            wf_s.at[step],
            wf_r.at[step],
            {"hidden": target},
        )

    for load in loads[5:]:
        load.wait()

    def load_kept(i, turn):
        return pltpu.make_async_copy(weights.at[i], kept.at[turn], kept_sem.at[turn])

    def block_at(at):
        owner = device_at(at // per_device, 1)
        return owner, owner * per_device + lax.rem(at, per_device)

    load_kept(block_at(0)[1], 0).start()
    dk_acc[...] = jnp.zeros_like(dk_acc)
    dv_acc[...] = jnp.zeros_like(dv_acc)

    def turn_values(i, _):
        cols = aligned(i * BLOCK, BLOCK)
        for n in range(heads):
            lo = 2 * width + n * HEAD_DIM
            values[n, cols, :] = qkv[lo : lo + HEAD_DIM, cols].astype(F32).T.astype(BF)
        return 0

    lax.fori_loop(0, blocks, turn_values, 0)

    def over_queries(at, _):
        owner, i = block_at(at)
        turn = lax.rem(at, 2)

        @pl.when(at + 1 < blocks)
        def _next():
            load_kept(block_at(at + 1)[1], 1 - turn).start()

        @pl.when((at >= per_device) & (lax.rem(at, per_device) == 0))
        def _arrive():
            n = at // per_device
            source = lax.rem(far - n // 2, far) * 2 + lax.rem(n, 2)
            give_att(source).wait_recv()

        @pl.when(at == per_device)
        def _weights():
            for step in range(1, far):
                there = wo_box.at[step]
                target = lax.rem(pair + step, far) * 2 + core
                remote(there, there, wo_s.at[step], wo_r.at[step], {"hidden": mate}).wait_recv()
                both = wo[target].astype(F32) + wo_box[step].astype(F32)
                wo[target] = both.astype(BF)
                give_wo(step).start()
            dw_send(1)

        load_kept(i, turn).wait()
        cols = aligned(lax.rem(at, per_device) * BLOCK, BLOCK)
        rows_i = aligned(i * BLOCK, BLOCK)
        given, centre = [], []
        for n in range(heads):
            here = slice(n * HEAD_DIM, (n + 1) * HEAD_DIM)
            scaled = d_att[owner, here, cols].astype(F32) * inverse[n : n + 1, rows_i]
            given.append(scaled.astype(BF))
            product = att_v[owner, here, cols].astype(F32) * scaled
            centre.append(jnp.sum(product, axis=0, keepdims=True))

        def block(span, first):
            attend_back(
                heads,
                i,
                span,
                first,
                qkv,
                given,
                centre,
                kept.at[turn],
                values,
                dq_acc,
                dk_acc,
                dv_acc,
            )

        spans(i, block)
        d_qkv[0:width, rows_i] = (dq_acc[...] * SCALE).astype(BF)
        return 0

    lax.fori_loop(0, blocks, over_queries, 0)
    w_acc[...] = jnp.zeros_like(w_acc)

    def finish(i, _):
        cols = aligned(i * BLOCK, BLOCK)
        d_qkv[width : 2 * width, cols] = dk_acc[:, cols].astype(BF)
        d_qkv[2 * width :, cols] = dv_acc[:, cols].astype(BF)
        block = d_qkv[:, cols]
        grad = mm_tn(block, w_t[...])
        inner = aligned(lax.rem(i, per_device) * BLOCK, BLOCK)
        normed, _unused = norm_parts(tv[i // per_device, inner, :].astype(F32))
        tv[i // per_device, inner, :] = grad.astype(BF)
        small[0:1, :] += jnp.sum(grad * normed, axis=0, keepdims=True)
        small[1:2, :] += jnp.sum(grad, axis=0, keepdims=True)
        hidden = (normed * lying(g1) + lying(s1)).astype(BF)
        w_acc[...] += mm(block, hidden)
        return 0

    lax.fori_loop(0, blocks, finish, 0)
    save_dh = pltpu.make_async_copy(tv, d_hidden, save_sem)
    save_dh.start()
    w_all[0 : 3 * width, :] = w_acc[...].astype(BF)
    there = wo_box.at[0]
    remote(there, there, wo_s.at[0], wo_r.at[0], {"hidden": mate}).wait_recv()
    total = wo[h].astype(F32) + wo_box[0].astype(F32)
    for step in range(1, far):
        give_wo(step).wait_recv()
        total = total + wo_far[step - 1].astype(F32)
    w_all[3 * width :, :] = total.astype(BF)
    load_dw.wait()
    load_far.wait()
    for which in range(2):
        for step in range(1, far if which == 1 else 1):
            for k in range(2):
                dw_across_copy(step, k).wait()

        def add_all(n, _, which=which):
            band = aligned(n * 96, 96)
            both = dw_mine[which, band, :].astype(F32)
            for step in range(1, far):
                both = both + dw_across[which, step - 1, band, :].astype(F32)
            dw_own[which, band, :] = both.astype(BF)
            return 0

        lax.fori_loop(0, dw_mine.shape[1] // 96, add_all, 0)
    for step in range(1, n_e):
        there = y_back.at[lax.rem(e + n_e - step, n_e)]
        remote(there, there, y_s.at[step], y_r.at[step], {"expert": e}).wait_recv()
    own_y.wait()
    save_dh.wait()
    for n in range(1, n_h):
        give_att(n).wait_send()
    for step in range(1, far):
        give_wo(step).wait_send()
    for copy in sends:
        copy.wait_send()


def run_back(
    ids,
    slot,
    pos,
    gates,
    count,
    g1,
    s1,
    g2,
    s2,
    w_router,
    inverse,
    dg_rows,
    dx_back,
    y_out,
    dw_sum,
    dw_far,
    out_grad,
    residual,
    all_tokens,
    qkv,
    att,
    att_t,
    w_out,
    w_t,
    weights,
    cid,
):
    n_e, n_h = lax.axis_size("expert"), lax.axis_size("hidden")
    experts, capacity, model = y_out.shape
    padded = dg_rows.shape[2]
    rows = out_grad.shape[0]
    width = w_t.shape[0] // 3
    heads = width // HEAD_DIM
    group, far = rows * n_h, n_h // 2
    shard = dw_sum.shape[2:]
    tall = 8 + experts

    def pairs(*shape):
        return [DMA(shape), DMA(shape)]

    return pl.pallas_call(
        partial(back_body, n_e, n_h, experts, capacity, padded, heads),
        name="back",
        out_shape=[
            shape_of(y_out.shape, BF),
            shape_of((n_h, rows, model), BF),
            shape_of((rows, model), F32),
            shape_of((4 * width, model), BF),
            shape_of((tall, model), F32),
            shape_of((2, *shard), BF),
        ],
        in_specs=[VMEM] * 12 + [ANY] * 13,
        out_specs=[ANY] * 2 + [VMEM] * 4,
        scratch_shapes=[
            pltpu.VMEM((experts * capacity, model), BF),
            pltpu.VMEM((rows, model), BF),
            pltpu.VMEM((rows, model), F32),
            pltpu.VMEM((n_h, rows, model), BF),
            pltpu.VMEM((3 * width, group), BF),
            pltpu.VMEM((n_h, width, rows), BF),
            pltpu.VMEM((n_h, width, rows), BF),
            pltpu.VMEM((n_h, width, model), BF),
            pltpu.VMEM((3 * width, model), BF),
            pltpu.VMEM((n_h, width, rows), BF),
            pltpu.VMEM((n_h, width, rows), BF),
            pltpu.VMEM((far, width, model), BF),
            pltpu.VMEM((far - 1, width, model), BF),
            pltpu.VMEM((2, heads, REACH, BLOCK, BLOCK), BF),
            pltpu.VMEM((heads, group, HEAD_DIM), BF),
            pltpu.VMEM((width, BLOCK), F32),
            pltpu.VMEM((width, group), F32),
            pltpu.VMEM((width, group), F32),
            pltpu.VMEM((3 * width, group), BF),
            pltpu.VMEM((3 * width, model), F32),
            pltpu.VMEM((2, *shard), BF),
            pltpu.VMEM((2, far - 1, *shard), BF),
            DMA((9,)),
            DMA,
            DMA((2,)),
            DMA((2,)),
            DMA,
            *pairs(n_e),
            *pairs(n_h),
            *pairs(far),
            *pairs(far),
            *pairs(far, 2),
        ],
        compiler_params=pltpu.CompilerParams(
            collective_id=cid, has_side_effects=True, vmem_limit_bytes=60 << 20
        ),
    )(
        ids,
        slot,
        pos,
        gates,
        count,
        g1,
        s1,
        g2,
        s2,
        w_router,
        inverse,
        dg_rows,
        dx_back.reshape(experts * capacity, model),
        y_out,
        dw_sum,
        dw_far,
        out_grad,
        residual,
        all_tokens,
        qkv,
        att,
        att_t,
        w_out.reshape(n_h, width, model),
        w_t,
        weights,
    )


def shards(
    tokens,
    doc_lengths,
    expert_ids,
    gain_one,
    shift_one,
    w_query,
    w_key,
    w_value,
    w_out,
    gain_two,
    shift_two,
    w_router,
    w_up,
    w_down,
    out_grad,
):
    rows, model = tokens.shape
    n_expert, n_hidden = lax.axis_size("expert"), lax.axis_size("hidden")
    experts = n_expert * w_up.shape[0]
    capacity = max(2, rows * 2 * 5 // (4 * experts))
    capacity = -(-capacity // 16) * 16
    total = experts * capacity
    heads = HEADS // n_hidden
    width = heads * HEAD_DIM
    g1, s1, g2, s2 = gain_one, shift_one, gain_two, shift_two
    router_t = w_router.T

    (
        all_tokens,
        qkv,
        att,
        att_t,
        w_t,
        g_in,
        x_slots,
        ups,
        weights,
        ids,
        pos,
        slot,
        count,
        inverse,
        residual,
        gates,
        gate_rows,
    ) = run_front(
        doc_lengths,
        expert_ids.T,
        g1,
        s1,
        g2,
        s2,
        router_t,
        tokens,
        out_grad,
        (w_query, w_key, w_value, w_out),
        w_up,
        capacity,
        heads,
        1,
    )
    dx_back, dg_back, y_out, dw_sum, dw_far = run_experts(
        x_slots, gate_rows, g_in, ups, w_up, w_down, 2
    )
    y_back, d_hidden, d_res, w_all, small, dw_own = run_back(
        ids,
        slot,
        pos,
        gates,
        count,
        g1,
        s1,
        g2,
        s2,
        router_t,
        inverse,
        dg_back,
        dx_back,
        y_out,
        dw_sum,
        dw_far,
        out_grad,
        residual,
        all_tokens,
        qkv,
        att,
        att_t,
        w_out,
        w_t,
        weights,
        3,
    )
    input_grad, output, full, small = run_tail(
        d_hidden,
        w_all.reshape(n_expert, 4 * width // n_expert, model),
        small,
        tokens,
        g1,
        d_res,
        residual,
        gates,
        pos,
        y_back.reshape(total, model),
        4,
    )
    scale = experts / (rows * n_expert * n_hidden * 2)
    turned = turn_weights(
        full.reshape(n_hidden, 4 * width, model),
        dw_own,
        small,
        input_grad,
        output,
        width,
        experts,
        scale,
    )
    w_grads, (up_grad, down_grad) = turned[:4], turned[4:6]
    gain_one_grad, shift_one_grad, gain_two_grad, shift_two_grad = turned[6:10]
    router_grad, input_grad, output, load = turned[10:]
    return (
        output,
        input_grad,
        gain_one_grad,
        shift_one_grad,
        *w_grads,
        gain_two_grad,
        shift_two_grad,
        router_grad.T,
        up_grad[None],
        down_grad[None],
        load,
    )


def solution(mesh):
    in_specs = (
        P(("expert", "hidden"), None),
        P("expert", None),
        P(("expert", "hidden"), None),
        P(),
        P(),
        P(),
        P(),
        P(),
        P(),
        P(),
        P(),
        P(),
        P("expert", None, "hidden"),
        P("expert", "hidden", None),
        P(("expert", "hidden"), None),
    )
    out_specs = (
        P(("expert", "hidden"), None),
        P(("expert", "hidden"), None),
        P(),
        P(),
        P(),
        P(),
        P(),
        P(),
        P(),
        P(),
        P(),
        P("expert", None, "hidden"),
        P("expert", "hidden", None),
        P(),
    )
    return jax.shard_map(shards, mesh=mesh, in_specs=in_specs, out_specs=out_specs, check_vma=False)
```

```python
from functools import partial

import jax
import jax.numpy as jnp
from jax import lax
from jax.experimental import pallas as pl
from jax.experimental.pallas import tpu as pltpu
from jax.sharding import PartitionSpec as P

HEAD_DIM = 64
HEADS = 12
EPSILON = 1e-05
SCALE = 0.125
MASKED = -1e30
BLOCK = 256
LONGEST = 1024
REACH = LONGEST // BLOCK + 1
UP_EARLY = 6
LANES = 128
BF = jnp.bfloat16
F32 = jnp.float32
I32 = jnp.int32
MESH = pl.DeviceIdType.MESH
ANY = pl.BlockSpec(memory_space=pl.ANY)
SMEM = pl.BlockSpec(memory_space=pltpu.SMEM)
VMEM = pl.BlockSpec(memory_space=pltpu.VMEM)
DMA = pltpu.SemaphoreType.DMA
GELU_A = 0.7978845608028654
GELU_B = 0.044715


def mm(left, right):
    return jnp.dot(left, right, preferred_element_type=F32)


def mm_nt(left, right):
    return lax.dot_general(left, right, (((1,), (1,)), ((), ())), preferred_element_type=F32)


def mm_tn(left, right):
    return lax.dot_general(left, right, (((0,), (0,)), ((), ())), preferred_element_type=F32)


def iota(shape, axis):
    return lax.broadcasted_iota(I32, shape, axis)


def norm_parts(values):
    centred = values - jnp.mean(values, axis=-1, keepdims=True)
    inverse = lax.rsqrt(jnp.mean(centred * centred, axis=-1, keepdims=True) + EPSILON)
    return centred * inverse, inverse


def norm_back(grad_out, normed, inverse, gain):
    grad_normed = grad_out * gain
    first = jnp.mean(grad_normed, axis=-1, keepdims=True)
    second = jnp.mean(grad_normed * normed, axis=-1, keepdims=True)
    return inverse * (grad_normed - first - normed * second)


def split_two(value):
    high = value.astype(BF)
    return high, (value - high.astype(F32)).astype(BF)


def row_at(ref, row):
    share = ref.shape[1]
    return row // share, slice(row % share, row % share + 1)


def shape_of(shape, dtype):
    return jax.ShapeDtypeStruct(shape, dtype)


def greet(peers):
    barrier = pltpu.get_barrier_semaphore()
    for peer in peers:
        pl.semaphore_signal(barrier, inc=1, device_id=peer, device_id_type=MESH)
    pl.semaphore_wait(barrier, len(peers))


def remote(src, dst, send, recv, peer):
    return pltpu.make_async_remote_copy(
        src_ref=src, dst_ref=dst, send_sem=send, recv_sem=recv, device_id=peer, device_id_type=MESH
    )


def doc_bounds(docs):
    ends, at = [], 0
    for n in range(docs.shape[1] - 1):
        at = at + docs[0, n]
        ends.append(at)
    return ends


def start_of(place, ends):
    begin = jnp.zeros_like(place)
    for end in ends:
        begin = jnp.where(place >= end, end, begin)
    return begin


def lying(ref):
    return ref[...].reshape(1, ref.shape[0])


def aligned(at, size):
    return pl.ds(pl.multiple_of(at, size), size)


def find_slots(experts, capacity, ids, ids_t, pos, slot, count):
    rows = ids_t.shape[1]
    row = [ids_t[j : j + 1, :] for j in range(2)]
    tall = jnp.concatenate([r.astype(F32) for r in row] + [jnp.zeros((6, rows), F32)], axis=0)
    ids[...] = tall.T[:, 0:2].astype(I32)
    col = [ids[:, j : j + 1] for j in range(2)]
    lane = iota((rows, LANES), 1)
    hot = [(lane == c).astype(BF) for c in col]
    either = hot[0] + hot[1]
    below = (iota((rows, rows), 0) > iota((rows, rows), 1)).astype(BF)
    before = mm(below, either)
    wide = max(experts, 16)
    deep = iota((wide, rows), 0)
    hot_t = [(deep == r).astype(BF) for r in row]
    above = (iota((rows, rows), 0) < iota((rows, rows), 1)).astype(BF)
    before_t = mm(hot_t[0] + hot_t[1], above)
    count[...] = jnp.sum(either.astype(F32), axis=0, keepdims=True)
    flat_t = []
    for j in range(2):
        at = jnp.sum(hot[j].astype(F32) * before, axis=1, keepdims=True).astype(I32)
        pos[:, j : j + 1] = col[j] * capacity + at
        slot[:, j : j + 1] = at
        at_t = jnp.sum(hot_t[j].astype(F32) * before_t, axis=0, keepdims=True).astype(I32)
        flat_t.append(row[j] * capacity + at_t)
    return flat_t


def fill_slots(flat_t, source, out):
    total, rows = out.shape[0], source.shape[0]
    half = total // 2
    for n in range(2):
        place = iota((half, rows), 0) + n * half
        pick = ((place == flat_t[0]) | (place == flat_t[1])).astype(BF)
        out[pl.ds(n * half, half), :] = mm(pick, source).astype(BF)


def attend_block(heads, ends, i, span, first, qkv, keys, scores, kept, inverse):
    width = heads * HEAD_DIM
    base = i * BLOCK
    rows = aligned(base, BLOCK)
    q_pos = base + iota((1, BLOCK), 1)
    begin = start_of(q_pos, ends)
    queries = [
        qkv[n * HEAD_DIM : (n + 1) * HEAD_DIM, rows] * jnp.asarray(SCALE, BF) for n in range(heads)
    ]
    tops = [jnp.full((1, BLOCK), MASKED, F32)] * heads
    for k in range(span):
        part = aligned((first + k) * BLOCK, BLOCK)
        k_pos = (first + k) * BLOCK + iota((BLOCK, BLOCK), 0)
        allowed = (k_pos <= q_pos) & (k_pos >= begin)
        for n in range(heads):
            score = jnp.where(allowed, mm(keys[n, part, :], queries[n]), MASKED)
            scores[n, k] = score
            tops[n] = jnp.maximum(tops[n], jnp.max(score, axis=0, keepdims=True))
    result = []
    for n in range(heads):
        total = jnp.zeros((1, BLOCK), F32)
        acc = jnp.zeros((HEAD_DIM, BLOCK), F32)
        lo = 2 * width + n * HEAD_DIM
        for k in range(span):
            weight = jnp.exp(scores[n, k] - tops[n])
            total = total + jnp.sum(weight, axis=0, keepdims=True)
            value = qkv[lo : lo + HEAD_DIM, aligned((first + k) * BLOCK, BLOCK)]
            low = weight.astype(BF)
            kept[n, k] = low
            acc = acc + mm(value, low)
        whole = 1.0 / total
        inverse[n : n + 1, rows] = whole
        result.append((acc * whole).astype(BF))
    return result


def spans(i, body):
    @pl.when(i < 2)
    def _short():
        body(2, 0)

    @pl.when(i >= 2)
    def _long():
        body(REACH, (i - (REACH - 1)) * (i // (REACH - 1)))


def front_body(
    n_e,
    n_h,
    experts,
    capacity,
    padded,
    heads,
    chunks,
    docs,
    ids_t,
    g1,
    s1,
    g2,
    s2,
    w_router,
    tokens,
    out_grad,
    w_query,
    w_key,
    w_value,
    w_out,
    w_up,
    all_tokens,
    qkv_out,
    att_out,
    att_t_out,
    w_t_out,
    g_in,
    x_slots,
    ups,
    weights,
    ids,
    pos,
    slot,
    count,
    inverse,
    residual,
    gates,
    gate_rows,
    tv,
    gv,
    wv,
    wo,
    w_t,
    qkv,
    keys,
    scores,
    kept,
    att_v,
    att_in,
    g_slots,
    xs_v,
    own_sem,
    w_sem,
    save_sem,
    kept_sem,
    ty_s,
    ty_r,
    tc_s,
    tc_r,
    tf_s,
    tf_r,
    gs_s,
    gs_r,
    at_s,
    at_r,
    wy_s,
    wy_r,
    wc_s,
    wc_r,
    wf_s,
    wf_r,
):
    e, h = lax.axis_index("expert"), lax.axis_index("hidden")
    far = n_h // 2
    pair, core = h // 2, lax.rem(h, 2)
    mate = pair * 2 + 1 - core
    rows, model = tokens.shape
    width = heads * HEAD_DIM
    per_device = rows // BLOCK
    ends = doc_bounds(docs)

    def across(t):
        return lax.rem(pair + t, far) * 2 + core

    def origin(t):
        return lax.rem(pair + far - t, far) * 2 + core

    own_tokens = pltpu.make_async_copy(tokens, tv.at[h], own_sem.at[0])
    own_grad = pltpu.make_async_copy(out_grad, gv, own_sem.at[1])
    own_grad.start()
    own_tokens.start()
    w_loads = [
        pltpu.make_async_copy(w, wv.at[n], w_sem.at[n])
        for n, w in enumerate((w_query, w_key, w_value))
    ]
    w_loads.append(pltpu.make_async_copy(w_out, wo, w_sem.at[3]))
    for load in w_loads:
        load.start()
    greet(
        [{"hidden": lax.rem(h + step, n_h)} for step in range(1, n_h)]
        + [{"expert": lax.rem(e + step, n_e)} for step in range(1, n_e)]
    )

    piece = rows // chunks
    sends = []
    for k in range(chunks):
        part = pl.ds(k * piece, piece)
        for t in range(1, far):
            copy = remote(
                tokens.at[part],
                tv.at[h, part],
                ty_s.at[t, k],
                ty_r.at[t, k],
                {"hidden": across(t)},
            )
            copy.start()
            sends.append(copy)
    beside = remote(tokens, tv.at[h], tc_s, tc_r, {"hidden": mate})
    beside.start()
    sends.append(beside)

    flat_t = find_slots(experts, capacity, ids, ids_t, pos, slot, count)
    own_grad.wait()
    fill_slots(flat_t, gv[...], g_slots)
    for step in range(1, n_e):
        peer = lax.rem(e + step, n_e)
        copy = remote(
            g_slots.at[aligned(peer * capacity, capacity)],
            g_in.at[e],
            gs_s.at[step],
            gs_r.at[step],
            {"expert": peer},
        )
        copy.start()
        sends.append(copy)
    own_slots = pltpu.make_async_copy(
        g_slots.at[aligned(e * capacity, capacity)], g_in.at[e], own_sem.at[1]
    )
    own_slots.start()

    def pass_on(t, k):
        part = pl.ds(k * piece, piece)
        place = tv.at[origin(t), part]
        remote(place, place, ty_s.at[t, k], ty_r.at[t, k], {"hidden": across(t)}).wait_recv()
        copy = remote(place, place, tf_s.at[t, k], tf_r.at[t, k], {"hidden": mate})
        copy.start()
        sends.append(copy)

    todo = [(t, k) for k in range(chunks) for t in range(1, far)]
    third = -(-len(todo) // 4)

    def pass_some():
        for _ in range(min(third, len(todo))):
            pass_on(*todo.pop(0))

    pick = (iota((width, model), 1) == iota((width, model), 0) + h * width).astype(BF)
    for n in range(3):
        w_loads[n].wait()
        w_t[n * width : (n + 1) * width, :] = mm_nt(pick, wv[n]).astype(BF)
        if n == 1:
            pass_some()
    save_w = pltpu.make_async_copy(w_t, w_t_out, save_sem.at[0])
    save_w.start()

    def project(source):
        def one(b, _):
            normed, _unused = norm_parts(tv[source, aligned(b * BLOCK, BLOCK), :].astype(F32))
            hidden = (normed * lying(g1) + lying(s1)).astype(BF)
            block = mm_nt(w_t[...], hidden)
            cols = aligned(source * rows + b * BLOCK, BLOCK)
            qkv[:, cols] = block.astype(BF)
            for n in range(heads):
                lo = width + n * HEAD_DIM
                keys[n, cols, :] = block[lo : lo + HEAD_DIM].T.astype(BF)
            return 0

        lax.fori_loop(0, per_device, one, 0)

    pass_some()
    own_tokens.wait()
    project(h)
    pass_some()
    remote(tokens, tv.at[mate], tc_s, tc_r, {"hidden": mate}).wait_recv()
    project(mate)
    while todo:
        pass_some()

    early = w_up.shape[1] * UP_EARLY // 8

    def up_copy(t, source):
        place = pl.ds(0, early)
        return remote(
            w_up.at[0, place], ups.at[source, place], wy_s.at[t], wy_r.at[t], {"hidden": across(t)}
        )

    def up_onward(t):
        place = ups.at[origin(t), pl.ds(0, early)]
        return remote(place, place, wf_s.at[t], wf_r.at[t], {"hidden": mate})

    up_beside = remote(w_up.at[0], ups.at[h], wc_s, wc_r, {"hidden": mate})
    up_beside.start()
    sends.append(up_beside)
    for t in range(1, far):
        up_copy(t, h).start()
    for t in range(1, far):
        project(origin(t))
    for t in range(1, far):
        there = lax.rem(pair + far - t, far) * 2 + 1 - core
        for k in range(chunks):
            place = tv.at[there, pl.ds(k * piece, piece)]
            remote(place, place, tf_s.at[t, k], tf_r.at[t, k], {"hidden": mate}).wait_recv()
        project(there)
    save_tokens = pltpu.make_async_copy(tv, all_tokens, save_sem.at[1])
    save_qkv = pltpu.make_async_copy(qkv, qkv_out, save_sem.at[2])
    save_tokens.start()
    save_qkv.start()

    inverse[...] = jnp.zeros_like(inverse)

    def device_at(n, sign):
        t, other = n // 2, lax.rem(n, 2)
        return lax.rem(pair + far + sign * t, far) * 2 + lax.rem(core + other, 2)

    def give_att(n):
        owner = device_at(n, 1)
        return remote(
            att_v.at[owner], att_in.at[h], at_s.at[n], at_r.at[n], {"hidden": owner}
        )

    def save_kept(i, turn):
        return pltpu.make_async_copy(kept.at[turn], weights.at[i], kept_sem.at[turn])

    def attend(at, _):
        n = n_h - 1 - at // per_device
        b = lax.rem(at, per_device)
        owner = device_at(n, 1)
        i = owner * per_device + b
        turn = lax.rem(at, 2)

        @pl.when(at >= 2)
        def _free():
            save_kept(i, turn).wait()

        def block(span, first):
            done = attend_block(
                heads, ends, i, span, first, qkv, keys, scores, kept.at[turn], inverse
            )
            for m in range(heads):
                lo = m * HEAD_DIM
                att_v[owner, lo : lo + HEAD_DIM, aligned(b * BLOCK, BLOCK)] = done[m]

        spans(i, block)
        save_kept(i, turn).start()

        @pl.when((b == per_device - 1) & (n > 0))
        def _give():
            give_att(n).start()

        return 0

    lax.fori_loop(0, n_h * per_device, attend, 0)
    for t in range(1, far):
        up_copy(t, origin(t)).wait_recv()
        up_onward(t).start()
    att_in[h] = att_v[h]
    save_att = pltpu.make_async_copy(att_v, att_out, save_sem.at[3])
    save_att.start()
    for n in range(n_h - 1, 0, -1):
        give_att(n).wait_recv()
    save_att_t = pltpu.make_async_copy(att_in, att_t_out, save_sem.at[4])
    save_att_t.start()

    w_loads[3].wait()
    res = tv[h].astype(F32) + mm_tn(att_in[...].reshape(model, rows), wo[...])
    residual[...] = res
    normed, _unused = norm_parts(res)
    hidden = (normed * lying(g2) + lying(s2)).astype(BF)
    fill_slots(flat_t, hidden, xs_v)
    save_x = [
        pltpu.make_async_copy(
            xs_v.at[pl.ds(n * capacity, capacity)], x_slots.at[n], save_sem.at[5 + n]
        )
        for n in range(experts)
    ]
    for save in save_x:
        save.start()
    logits = mm_nt(hidden, w_router[...])
    lane = iota((rows, experts), 1)
    chosen = [
        jnp.sum(jnp.where(lane == ids[:, j : j + 1], logits, 0.0), axis=1, keepdims=True)
        for j in range(2)
    ]
    top = jnp.maximum(chosen[0], chosen[1])
    raised = [jnp.exp(c - top) for c in chosen]
    both = raised[0] + raised[1]
    gate = [r / both for r in raised]
    for j in range(2):
        gates[:, j : j + 1] = gate[j]
    column = iota((rows, padded), 1)
    for n in range(experts):
        mix = jnp.zeros((rows, padded), F32)
        for j in range(2):
            here = jnp.where(ids[:, j : j + 1] == n, slot[:, j : j + 1], -1) == column
            mix = jnp.where(here, gate[j], mix)
        line = jnp.sum(mix, axis=0, keepdims=True)
        gate_rows[n] = jnp.broadcast_to(line, (8, padded))

    place = ups.at[mate]
    remote(place, place, wc_s, wc_r, {"hidden": mate}).wait_recv()
    for t in range(1, far):
        up_onward(t).wait()
    for step in range(1, n_e):
        source = lax.rem(e + n_e - step, n_e)
        place = g_in.at[source]
        remote(place, place, gs_s.at[step], gs_r.at[step], {"expert": e}).wait_recv()
    own_slots.wait()
    for n in range(1, n_h):
        give_att(n).wait_send()
    for turn in range(2):
        save_kept(0, turn).wait()
    for t in range(1, far):
        up_copy(t, h).wait_send()
    for copy in sends:
        copy.wait_send()
    for save in [save_w, save_tokens, save_qkv, save_att, save_att_t, *save_x]:
        save.wait()


def run_front(
    docs, ids_t, g1, s1, g2, s2, w_router, tokens, out_grad, ws, w_up, capacity, heads, cid
):
    n_e, n_h = lax.axis_size("expert"), lax.axis_size("hidden")
    experts = n_e * w_up.shape[0]
    rows, model = tokens.shape
    padded = -(-capacity // LANES) * LANES
    width, group, total = heads * HEAD_DIM, rows * n_h, experts * capacity
    far, chunks = n_h // 2, 8

    def pairs(*shape):
        return [DMA(shape), DMA(shape)]

    return pl.pallas_call(
        partial(front_body, n_e, n_h, experts, capacity, padded, heads, chunks),
        name="front",
        out_shape=[
            shape_of((n_h, rows, model), BF),
            shape_of((3 * width, group), BF),
            shape_of((n_h, width, rows), BF),
            shape_of((n_h, width, rows), BF),
            shape_of((3 * width, model), BF),
            shape_of((experts, capacity, model), BF),
            shape_of((experts, capacity, model), BF),
            shape_of((n_h, *w_up.shape[1:]), BF),
            shape_of((group // BLOCK, heads, REACH, BLOCK, BLOCK), BF),
            shape_of((rows, 2), I32),
            shape_of((rows, 2), I32),
            shape_of((rows, 2), I32),
            shape_of((1, LANES), F32),
            shape_of((8, group), F32),
            shape_of((rows, model), F32),
            shape_of((rows, 2), F32),
            shape_of((experts, 8, padded), F32),
        ],
        in_specs=[SMEM] + [VMEM] * 6 + [ANY] * 7,
        out_specs=[ANY] * 9 + [VMEM] * 8,
        scratch_shapes=[
            pltpu.VMEM((n_h, rows, model), BF),
            pltpu.VMEM((rows, model), BF),
            pltpu.VMEM((3, model, model), BF),
            pltpu.VMEM((model, model), BF),
            pltpu.VMEM((3 * width, model), BF),
            pltpu.VMEM((3 * width, group), BF),
            pltpu.VMEM((heads, group, HEAD_DIM), BF),
            pltpu.VMEM((heads, REACH, BLOCK, BLOCK), F32),
            pltpu.VMEM((2, heads, REACH, BLOCK, BLOCK), BF),
            pltpu.VMEM((n_h, width, rows), BF),
            pltpu.VMEM((n_h, width, rows), BF),
            pltpu.VMEM((total, model), BF),
            pltpu.VMEM((total, model), BF),
            DMA((2,)),
            DMA((4,)),
            DMA((5 + experts,)),
            DMA((2,)),
            *pairs(far, chunks),
            DMA,
            DMA,
            *pairs(far, chunks),
            *pairs(n_e),
            *pairs(n_h),
            *pairs(far),
            DMA,
            DMA,
            *pairs(far),
        ],
        compiler_params=pltpu.CompilerParams(
            collective_id=cid, has_side_effects=True, vmem_limit_bytes=58 << 20
        ),
    )(docs, ids_t, g1, s1, g2, s2, w_router, tokens, out_grad, *ws, w_up)


def moe_body(
    size,
    capacity,
    padded,
    per,
    x_slots,
    gate_rows,
    g_in,
    ups,
    w_up,
    w_down,
    dx_back,
    dg_back,
    y_out,
    dw_sum,
    dw_far,
    xv,
    gv,
    gates_v,
    up_v,
    down_v,
    act,
    dz,
    xg,
    dy,
    xg_t,
    dy_t,
    dxv,
    yv,
    dgv,
    y_acc,
    dx_acc,
    dw_box,
    load_sem,
    save_sem,
    wy_s,
    wy_r,
    wc_s,
    wc_r,
    wf_s,
    wf_r,
    dc_s,
    dc_r,
    df_s,
    df_r,
    g_sem,
    own_sem,
    xs_sem,
    xr_sem,
    gs_sem,
    gr_sem,
    ds_sem,
    dr_sem,
    ts_sem,
    tr_sem,
    out_sem,
):
    me, h = lax.axis_index("expert"), lax.axis_index("hidden")
    shards_n = ups.shape[0]
    far = shards_n // 2
    pair, core = h // 2, lax.rem(h, 2)
    mate = pair * 2 + 1 - core
    deep = w_down.shape[1] // 2
    tall = per * capacity
    steps = size // per

    middle = size // 2
    inner = lax.rem((me // 2 * 8 // size + 1) // 2, 2)

    def group_at(step):
        some = steps // 4
        early = jnp.where(step <= some, step - 1 + steps // 2, step - some)
        early = jnp.where((step > 0) & (step < steps - some), early, step)
        return jnp.where(inner == 1, early, step)

    def peer_at(p):
        peer, bit = 0, 1
        while bit < size:
            peer = peer + lax.rem(me // bit + p // bit, 2) * bit
            bit *= 2
        return peer

    def rows_of(p):
        return pl.ds(pl.multiple_of(p * capacity, capacity), capacity)

    def send_x(p):
        peer = peer_at(p)
        return remote(
            x_slots.at[peer], xv.at[rows_of(p)], xs_sem.at[p], xr_sem.at[p], {"expert": peer}
        )

    def send_gate(p):
        peer = peer_at(p)
        return remote(
            gate_rows.at[peer], gates_v.at[p], gs_sem.at[p], gr_sem.at[p], {"expert": peer}
        )

    def send_dx(p):
        peer = peer_at(p)
        return remote(
            dxv.at[rows_of(p)], dx_back.at[me], ds_sem.at[p], dr_sem.at[p], {"expert": peer}
        )

    def send_dg(p):
        peer = peer_at(p)
        return remote(dgv.at[p], dg_back.at[me], ts_sem.at[p], tr_sem.at[p], {"expert": peer})

    def load_g(p):
        return pltpu.make_async_copy(g_in.at[peer_at(p)], gv.at[rows_of(p)], g_sem.at[p])

    def save_y(p):
        return pltpu.make_async_copy(yv.at[rows_of(p)], y_out.at[peer_at(p)], out_sem.at[p])

    own_x = pltpu.make_async_copy(x_slots.at[me], xv.at[rows_of(0)], own_sem.at[0])
    own_gate = pltpu.make_async_copy(gate_rows.at[me], gates_v.at[0], own_sem.at[1])
    own_dx = pltpu.make_async_copy(dxv.at[rows_of(0)], dx_back.at[me], own_sem.at[2])
    own_dg = pltpu.make_async_copy(dgv.at[0], dg_back.at[me], own_sem.at[3])
    loads = [
        pltpu.make_async_copy(w_up.at[0], up_v.at[h], load_sem.at[0]),
        pltpu.make_async_copy(w_down.at[0], down_v.at[h], load_sem.at[1]),
    ]
    loads.append(pltpu.make_async_copy(ups.at[mate], up_v.at[mate], load_sem.at[2]))

    early = w_up.shape[1] * UP_EARLY // 8

    def half(k):
        return aligned(k * deep, deep)

    for t in range(1, far):
        for other in range(2):
            c = lax.rem(pair + t, far) * 2 + other
            place = (c, pl.ds(0, early))
            loads.append(
                pltpu.make_async_copy(
                    ups.at[place], up_v.at[place], load_sem.at[1 + 2 * t + other]
                )
            )
    rest = pl.ds(early, w_up.shape[1] - early)
    parts = ((w_up, up_v, rest), (w_down, down_v, half(0)), (w_down, down_v, half(1)))

    def part_across(t, n):
        source, target, k = parts[n]
        there = {"hidden": lax.rem(pair + t, far) * 2 + core}
        return remote(
            source.at[0, k], target.at[h, k], wy_s.at[t, n], wy_r.at[t, n], there
        )

    def part_onward(t, n):
        _source, target, k = parts[n]
        place = target.at[lax.rem(pair + far - t, far) * 2 + core, k]
        return remote(place, place, wf_s.at[t, n], wf_r.at[t, n], {"hidden": mate})

    down_beside = remote(w_down.at[0], down_v.at[h], wc_s, wc_r, {"hidden": mate})
    own_x.start()
    own_gate.start()
    for p in range(size):
        load_g(p).start()
    for load in loads:
        load.start()
    greet(
        [{"expert": lax.rem(me + step, size)} for step in range(1, size)]
        + [{"hidden": lax.rem(h + step, shards_n)} for step in range(1, shards_n)]
    )

    def send_all(order):
        for p in order:
            send_x(p).start()
            send_gate(p).start()

    @pl.when(inner == 1)
    def _far_first():
        send_all([1, *range(middle, size), *range(2, middle)])

    @pl.when(inner == 0)
    def _near_first():
        send_all(range(1, size))

    for n in range(3):
        for t in range(1, far):
            part_across(t, n).start()
    down_beside.start()
    own_x.wait()
    own_gate.wait()
    for load in loads:
        load.wait()

    def finish(base, rows, held):
        dxv[rows, :] = dx_acc[held, :].astype(BF)
        y_low = y_acc[held, :].astype(BF)
        yv[rows, :] = y_low
        x, g = xv[rows, :], gv[rows, :]
        dots = jnp.sum(y_low.astype(F32) * g.astype(F32), axis=1, keepdims=True)
        for s in range(per):
            p = base + s
            part = slice(s * capacity, (s + 1) * capacity)
            tall_dots = jnp.broadcast_to(dots[part], (capacity, LANES))
            if padded > capacity:
                blank = jnp.zeros((padded - capacity, LANES), F32)
                tall_dots = jnp.concatenate([tall_dots, blank], axis=0)
            dgv[p] = tall_dots.T[0:8]

            @pl.when(p > 0)
            def _give(p=p):
                send_dx(p).start()
                send_dg(p).start()

            @pl.when(p == 0)
            def _keep():
                own_dx.start()
                own_dg.start()

            save_y(p).start()
        for s in range(per):
            p = base + s
            part = slice(s * capacity, (s + 1) * capacity)
            gate = gates_v[p].T[0:capacity, 0:1]
            xg[rows_of(p), :] = (x[part].astype(F32) * gate).astype(BF)
            dy[rows_of(p), :] = (g[part].astype(F32) * gate).astype(BF)

    first = shards_n // 2

    def unit(m):
        step = jnp.where(m < 2 * shards_n, lax.rem(m // first, 2), m // shards_n)
        n = m // shards_n * first + lax.rem(m, first)
        n = jnp.where(m < 2 * shards_n, n, lax.rem(m, shards_n))
        return step, n

    def unit_body(m, _):
        step, n = unit(m)
        base = group_at(step) * per
        rows = pl.ds(pl.multiple_of(base * capacity, tall), tall)
        held = aligned(jnp.where(step == 1, tall, 0), tall)

        @pl.when(n == 0)
        def _begin():
            for s in range(per):

                @pl.when(base + s > 0)
                def _arrive(s=s):
                    send_x(base + s).wait_recv()
                    send_gate(base + s).wait_recv()

                load_g(base + s).wait()
            y_acc[held, :] = jnp.zeros((tall, y_acc.shape[1]), F32)
            dx_acc[held, :] = jnp.zeros((tall, y_acc.shape[1]), F32)

        t = n // 2
        beside = lax.rem(n, 2)
        c = lax.rem(pair + far - t, far) * 2 + lax.rem(core + beside, 2)

        @pl.when(m == 1)
        def _beside():
            down_beside.wait_recv()

        @pl.when((step == 0) & (n >= 2) & (beside == 0))
        def _across():
            for k in range(3):
                part_across(t, k).wait_recv()
                part_onward(t, k).start()

        @pl.when((step == 0) & (n >= 2) & (beside == 1))
        def _onward():
            for k in range(3):
                part_onward(t, k).wait_recv()

        x, g = xv[rows, :], gv[rows, :]
        z = mm(x, up_v[c])
        du = mm_nt(g, down_v[c])
        square = z * z
        curve = jnp.tanh(z * (GELU_A + GELU_A * GELU_B * square))
        plus = 0.5 + 0.5 * curve
        hidden = (z * plus).astype(BF)
        rise = GELU_A + 3.0 * GELU_A * GELU_B * square
        slope = plus + 0.5 * z * (1.0 - curve * curve) * rise
        back = (slope * du).astype(BF)
        act[c, rows, :] = hidden
        dz[c, rows, :] = back
        y_acc[held, :] += mm(hidden, down_v[c])
        dx_acc[held, :] += mm_nt(back, up_v[c])

        @pl.when(n == shards_n - 1)
        def _end():
            finish(base, rows, held)

        return 0

    lax.fori_loop(0, steps * shards_n, unit_body, 0)

    total = size * capacity
    turn = 256
    for k in range(total // turn):
        rows = slice(k * turn, (k + 1) * turn)
        xg_t[:, rows] = xg[rows, :].astype(F32).T.astype(BF)
    for t in range(1, far):
        for k in range(3):
            part_across(t, k).wait_send()
            part_onward(t, k).wait_send()
    down_beside.wait_send()

    def give(which, step):
        source = (up_v, down_v)[which].at[lax.rem(pair + step, far) * 2 + 1 - core]
        return remote(
            source,
            dw_box.at[which, step],
            dc_s.at[which, step],
            dc_r.at[which, step],
            {"hidden": mate},
        )

    def keep(which, step):
        source = (up_v, down_v)[which].at[lax.rem(pair + step, far) * 2 + core]
        return pltpu.make_async_copy(source, dw_sum.at[which, step], save_sem.at[which, step])

    def cross(step, k):
        there = lax.rem(pair + step, far) * 2 + core
        return remote(
            up_v.at[there, half(k)],
            dw_far.at[step - 1, half(k)],
            df_s.at[step, k],
            df_r.at[step, k],
            {"hidden": there},
        )

    def gradients(which, left, right, held):
        def other(n, _):
            step = lax.rem(n + 1, far)
            c = lax.rem(pair + step, far) * 2 + 1 - core
            held[c] = mm(left[...], right[c]).astype(BF)
            give(which, step).start()
            return 0

        def own(n, _):
            step = lax.rem(n + 1, far)
            c = lax.rem(pair + step, far) * 2 + core
            total_of = mm(left[...], right[c])
            give(which, step).wait_recv()
            held[c] = (total_of + dw_box[which, step].astype(F32)).astype(BF)
            keep(which, step).start()

            if which == 0:

                @pl.when(step > 0)
                def _cross():
                    for k in range(2):
                        cross(step, k).start()

            return 0

        lax.fori_loop(0, far, other, 0)
        lax.fori_loop(0, far, own, 0)

    gradients(0, xg_t, dz, up_v)
    for k in range(total // turn):
        rows = slice(k * turn, (k + 1) * turn)
        dy_t[:, rows] = dy[rows, :].astype(F32).T.astype(BF)
    gradients(1, dy_t, act, down_v)
    for p in range(1, size):
        send_x(p).wait_send()
        send_gate(p).wait_send()
        send_dx(p).wait()
        send_dg(p).wait()
    for p in range(size):
        save_y(p).wait()
    own_dx.wait()
    own_dg.wait()
    for step in range(far):
        for which in range(2):
            give(which, step).wait_send()
            keep(which, step).wait()
    for step in range(1, far):
        for k in range(2):
            cross(step, k).wait()


def run_experts(x_slots, gate_rows, g_in, ups, w_up, w_down, cid):
    size = lax.axis_size("expert")
    experts, capacity, model = x_slots.shape
    padded = gate_rows.shape[2]
    shards_n, _unused, width = ups.shape
    total = experts * capacity
    per = 1
    while per * 2 * capacity <= 320 and size % (per * 2) == 0:
        per *= 2
    tall = per * capacity
    rows2 = (total, model)
    return pl.pallas_call(
        partial(moe_body, size, capacity, padded, per),
        name="experts",
        out_shape=[
            shape_of(x_slots.shape, BF),
            shape_of(gate_rows.shape, F32),
            shape_of(x_slots.shape, BF),
            shape_of((2, shards_n // 2, model, width), BF),
            shape_of((shards_n // 2 - 1, model, width), BF),
        ],
        in_specs=[ANY] * 6,
        out_specs=[ANY] * 5,
        scratch_shapes=[
            pltpu.VMEM(rows2, BF),
            pltpu.VMEM(rows2, BF),
            pltpu.VMEM(gate_rows.shape, F32),
            pltpu.VMEM((shards_n, model, width), BF),
            pltpu.VMEM((shards_n, width, model), BF),
            pltpu.VMEM((shards_n, total, width), BF),
            pltpu.VMEM((shards_n, total, width), BF),
            pltpu.VMEM(rows2, BF),
            pltpu.VMEM(rows2, BF),
            pltpu.VMEM((model, total), BF),
            pltpu.VMEM((model, total), BF),
            pltpu.VMEM(rows2, BF),
            pltpu.VMEM(rows2, BF),
            pltpu.VMEM(gate_rows.shape, F32),
            pltpu.VMEM((2 * tall, model), F32),
            pltpu.VMEM((2 * tall, model), F32),
            pltpu.VMEM((2, shards_n // 2, model, width), BF),
            DMA((shards_n + 1,)),
            DMA((2, shards_n // 2)),
            DMA((shards_n // 2, 3)),
            DMA((shards_n // 2, 3)),
            DMA,
            DMA,
            DMA((shards_n // 2, 3)),
            DMA((shards_n // 2, 3)),
            DMA((2, shards_n // 2)),
            DMA((2, shards_n // 2)),
            DMA((shards_n // 2, 2)),
            DMA((shards_n // 2, 2)),
            DMA((size,)),
            DMA((4,)),
        ]
        + [DMA((size,))] * 9,
        compiler_params=pltpu.CompilerParams(
            collective_id=cid, has_side_effects=True, vmem_limit_bytes=60 << 20
        ),
        cost_estimate=pl.CostEstimate(
            flops=12 * total * model * width * shards_n, bytes_accessed=40 << 20, transcendentals=0
        ),
    )(x_slots, gate_rows, g_in, ups, w_up, w_down)


def tail_body(
    n_e,
    n_h,
    chunks,
    dh,
    w_all,
    small,
    tokens,
    gain,
    d_res,
    residual,
    gates,
    pos,
    y_back,
    input_grad,
    output,
    full,
    total,
    wv,
    tok_v,
    d_res_v,
    res_v,
    yv,
    mine,
    beside,
    across,
    passing,
    x_box,
    z_box,
    w_mid,
    piece,
    small_mid,
    small_h,
    small_e,
    small_all,
    load_sem,
    mine_sem,
    cs_sem,
    cr_sem,
    as_sem,
    ar_sem,
    ws_sem,
    wr_sem,
    vs_sem,
    vr_sem,
    hs_sem,
    hr_sem,
    es_sem,
    er_sem,
    bs_sem,
    br_sem,
    keep_sem,
    zs_sem,
    zr_sem,
    xs_sem,
    xr_sem,
    ys_sem,
    yr_sem,
    ms_sem,
    mr_sem,
):
    e, h = lax.axis_index("expert"), lax.axis_index("hidden")
    far, high = n_h // 2, n_e // 2
    pair, core = h // 2, lax.rem(h, 2)
    eh, el = e // 2, lax.rem(e, 2)
    mate = pair * 2 + 1 - core
    greet(
        [{"expert": lax.rem(e + step, n_e)} for step in range(1, n_e)]
        + [{"hidden": lax.rem(h + step, n_h)} for step in range(1, n_h)]
    )
    w_sends, w_order = {}, list(range(1, high)) + [0]
    for step in w_order:
        there = lax.rem(eh + step, high)
        copy = remote(
            w_all.at[there * 2 + 1 - el],
            x_box.at[step],
            ws_sem.at[step],
            wr_sem.at[step],
            {"expert": eh * 2 + 1 - el},
        )
        copy.start()
        w_sends[step] = copy
    small_sends = []
    for at in range(n_h - 1):
        peer = lax.rem(h + 1 + at, n_h)
        copy = remote(
            small.at[peer], small_h.at[at], hs_sem.at[at], hr_sem.at[at], {"hidden": peer}
        )
        copy.start()
        small_sends.append(copy)
    rows = dh.shape[1] // chunks
    core_sends = {}
    for step in list(range(1, far)) + [0]:
        there = lax.rem(pair + step, far)
        for k in range(chunks):
            part = pl.ds(k * rows, rows)
            copy = remote(
                dh.at[there * 2 + 1 - core, part],
                beside.at[step, part],
                cs_sem.at[step, k],
                cr_sem.at[step, k],
                {"hidden": mate},
            )
            copy.start()
            core_sends[step, k] = copy
    mine_loads = []
    for step in range(far):
        there = lax.rem(pair + step, far)
        load = pltpu.make_async_copy(dh.at[there * 2 + core], mine.at[step], mine_sem.at[step])
        load.start()
        mine_loads.append(load)
    loads = [
        pltpu.make_async_copy(source, target, load_sem.at[n])
        for n, (source, target) in enumerate(
            ((w_all, wv), (residual, res_v), (y_back, yv), (tokens, tok_v), (d_res, d_res_v))
        )
    ]
    for load in loads:
        load.start()
    for load in mine_loads:
        load.wait()
    far_sends = []
    for step in range(1, far):
        there = lax.rem(pair + step, far)
        for k in range(chunks):
            part = pl.ds(k * rows, rows)
            core_sends[step, k].wait_recv()
            both = mine[step, part, :].astype(F32) + beside[step, part, :].astype(F32)
            passing[step - 1, part, :] = both.astype(BF)
            copy = remote(
                passing.at[step - 1, part],
                across.at[step - 1, part],
                as_sem.at[step - 1, k],
                ar_sem.at[step - 1, k],
                {"hidden": there * 2 + core},
            )
            copy.start()
            far_sends.append(copy)
    loads[0].wait()
    v_sends = []
    for step in w_order[:-1]:
        there = lax.rem(eh + step, high) * 2 + el
        w_sends[step].wait_recv()
        w_mid[step - 1] = (wv[there].astype(F32) + x_box[step].astype(F32)).astype(BF)
        copy = remote(
            w_mid.at[step - 1],
            z_box.at[step - 1],
            vs_sem.at[step],
            vr_sem.at[step],
            {"expert": there},
        )
        copy.start()
        v_sends.append(copy)
    summed = small[h]
    for at, copy in enumerate(small_sends):
        copy.wait_recv()
        summed = summed + small_h[at]
    small_mid[...] = summed
    small_out = []
    for at in range(n_e - 1):
        peer = lax.rem(e + 1 + at, n_e)
        copy = remote(small_mid, small_e.at[at], es_sem.at[at], er_sem.at[at], {"expert": peer})
        copy.start()
        small_out.append(copy)
    w_sends[0].wait_recv()
    acc = wv[e].astype(F32) + x_box[0].astype(F32)
    for at, copy in enumerate(v_sends):
        copy.wait_recv()
        acc = acc + z_box[at].astype(F32)
    piece[...] = acc.astype(BF)
    keep = pltpu.make_async_copy(piece, full.at[h, e], keep_sem)
    keep.start()

    def spot(t, s, flag, core_of):
        eh_of = lax.rem(eh + high - s, high)
        el_of = el if flag == 0 else 1 - el
        return full.at[lax.rem(pair + far - t, far) * 2 + core_of, eh_of * 2 + el_of]

    def held(t, s, flag):
        return piece if (t, s, flag) == (0, 0, 0) else spot(t, s, flag, core)

    def along(t, s):
        there = {"expert": lax.rem(eh + s, high) * 2 + el}
        return remote(held(t, 0, 0), spot(t, 0, 0, core), zs_sem.at[t, s], zr_sem.at[t, s], there)

    def aside(t, s):
        there = {"expert": eh * 2 + 1 - el}
        return remote(held(t, s, 0), spot(t, s, 0, core), xs_sem.at[t, s], xr_sem.at[t, s], there)

    def over(t, s, flag):
        there = {"hidden": lax.rem(pair + t, far) * 2 + core}
        at = 2 * s + flag
        return remote(
            held(0, s, flag), spot(0, s, flag, core), ys_sem.at[t, at], yr_sem.at[t, at], there
        )

    def to_mate(t, s, flag):
        at = 2 * s + flag
        return remote(
            held(t, s, flag),
            spot(t, s, flag, core),
            ms_sem.at[t, at],
            mr_sem.at[t, at],
            {"hidden": mate},
        )

    line_order = list(range(1, high))
    pieces = [(s, flag) for s in range(high) for flag in range(2)]
    first, second = core == 0, core == 1

    @pl.when(first)
    def _spread_first():
        for s in line_order:
            along(0, s).start()
        aside(0, 0).start()
        for t in range(1, far):
            over(t, 0, 0).start()
        to_mate(0, 0, 0).start()

        def take_aside(s):
            aside(0, s).wait_recv()
            for t in range(1, far):
                over(t, s, 1).start()
            to_mate(0, s, 1).start()

        for s in line_order:
            along(0, s).wait_recv()
            aside(0, s).start()
            for t in range(1, far):
                over(t, s, 0).start()
            to_mate(0, s, 0).start()
            take_aside(s - 1)
        take_aside(high - 1)

    @pl.when(second)
    def _spread_second():
        for t in range(1, far):
            over(t, 0, 0).start()
        for s in line_order:
            along(0, s).start()
        aside(0, 0).start()
        to_mate(0, 0, 0).start()
        for t in range(1, far):
            over(t, 0, 0).wait_recv()
            for s in line_order:
                along(t, s).start()
            aside(t, 0).start()
            to_mate(t, 0, 0).start()
        for s in line_order:
            for t in range(far):
                along(t, s).wait_recv()
                aside(t, s).start()
                to_mate(t, s, 0).start()

    summed = small_mid[...]
    for at, copy in enumerate(small_out):
        copy.wait_recv()
        summed = summed + small_e[at]
    small_all[h] = summed
    small_back = []
    for at in range(n_h - 1):
        peer = lax.rem(h + 1 + at, n_h)
        copy = remote(
            small_all.at[h], small_all.at[h], bs_sem.at[at], br_sem.at[at], {"hidden": peer}
        )
        copy.start()
        small_back.append(copy)
    for load in loads[1:]:
        load.wait()
    place_of = iota((residual.shape[0], y_back.shape[0]), 1)
    result = res_v[...]
    for j in range(2):
        pick = (place_of == pos[:, j : j + 1]).astype(BF)
        result = result + gates[:, j : j + 1] * mm(pick, yv[...])
    output[...] = result.astype(BF)
    for k in range(chunks):
        part = pl.ds(k * rows, rows)
        core_sends[0, k].wait_recv()
    for copy in far_sends:
        copy.wait_recv()
    grad = mine[0].astype(F32) + beside[0].astype(F32)
    for step in range(far - 1):
        grad = grad + across[step].astype(F32)
    normed, inverse = norm_parts(tok_v[...].astype(F32))
    input_grad[...] = (d_res_v[...] + norm_back(grad, normed, inverse, lying(gain))).astype(BF)
    @pl.when(first)
    def _finish_first():
        for t in range(1, far):
            for s, flag in pieces:
                over(t, s, flag).wait_recv()
                to_mate(t, s, flag).start()

    @pl.when(second)
    def _finish_second():
        for s in range(high):
            for t in range(far):
                aside(t, s).wait_recv()
                to_mate(t, s, 1).start()

    for copy in small_back:
        copy.wait_recv()
    total[...] = small_all[...]
    for t in range(far):
        for s, flag in pieces:
            to_mate(t, s, flag).wait()
    keep.wait()

    @pl.when(first)
    def _sent_first():
        for s in line_order:
            along(0, s).wait_send()
        for s in range(high):
            aside(0, s).wait_send()
        for t in range(1, far):
            for s, flag in pieces:
                over(t, s, flag).wait_send()

    @pl.when(second)
    def _sent_second():
        for t in range(1, far):
            over(t, 0, 0).wait_send()
        for t in range(far):
            for s in line_order:
                along(t, s).wait_send()
            for s in range(high):
                aside(t, s).wait_send()

    for copy in [*w_sends.values(), *v_sends, *small_sends, *small_out, *small_back, *far_sends]:
        copy.wait_send()
    for copy in core_sends.values():
        copy.wait_send()


def run_tail(dh, w_all, small, tokens, gain, d_res, residual, gates, pos, y_back, cid):
    n_e, n_h = lax.axis_size("expert"), lax.axis_size("hidden")
    far, high = n_h // 2, n_e // 2
    chunks = 4
    _unused, rows, model = dh.shape
    piece = w_all.shape[1:]
    return pl.pallas_call(
        partial(tail_body, n_e, n_h, chunks),
        name="tail",
        out_shape=[
            shape_of((rows, model), BF),
            shape_of((rows, model), BF),
            shape_of((n_h, n_e, *piece), BF),
            shape_of(small.shape, F32),
        ],
        in_specs=[ANY, ANY, VMEM, ANY, VMEM, ANY, ANY, VMEM, VMEM, ANY],
        out_specs=[VMEM, VMEM, ANY, VMEM],
        scratch_shapes=[
            pltpu.VMEM(w_all.shape, BF),
            pltpu.VMEM(tokens.shape, BF),
            pltpu.VMEM(d_res.shape, F32),
            pltpu.VMEM(residual.shape, F32),
            pltpu.VMEM(y_back.shape, BF),
            pltpu.VMEM((far, rows, model), BF),
            pltpu.VMEM((far, rows, model), BF),
            pltpu.VMEM((far - 1, rows, model), BF),
            pltpu.VMEM((far - 1, rows, model), BF),
            pltpu.VMEM((high, *piece), BF),
            pltpu.VMEM((high - 1, *piece), BF),
            pltpu.VMEM((high - 1, *piece), BF),
            pltpu.VMEM(piece, BF),
            pltpu.VMEM(small.shape[1:], F32),
            pltpu.VMEM((n_h - 1, *small.shape[1:]), F32),
            pltpu.VMEM((n_e - 1, *small.shape[1:]), F32),
            pltpu.VMEM(small.shape, F32),
            DMA((5,)),
            DMA((far,)),
            DMA((far, chunks)),
            DMA((far, chunks)),
            DMA((far - 1, chunks)),
            DMA((far - 1, chunks)),
            DMA((high,)),
            DMA((high,)),
            DMA((high,)),
            DMA((high,)),
            DMA((n_h - 1,)),
            DMA((n_h - 1,)),
            DMA((n_e - 1,)),
            DMA((n_e - 1,)),
            DMA((n_h - 1,)),
            DMA((n_h - 1,)),
            DMA,
            DMA((far, high)),
            DMA((far, high)),
            DMA((far, high)),
            DMA((far, high)),
            DMA((far, n_e)),
            DMA((far, n_e)),
            DMA((far, n_e)),
            DMA((far, n_e)),
        ],
        compiler_params=pltpu.CompilerParams(
            collective_id=cid, has_side_effects=True, vmem_limit_bytes=56 << 20
        ),
    )(dh, w_all, small, tokens, gain, d_res, residual, gates, pos, y_back)


def turn_body(
    width,
    experts,
    scale,
    full,
    dw,
    small,
    input_grad,
    output,
    q_out,
    k_out,
    v_out,
    o_out,
    up_out,
    down_out,
    g1_out,
    s1_out,
    g2_out,
    s2_out,
    router_out,
    input_out,
    output_out,
    load_out,
):
    @pl.when(pl.program_id(0) == 0)
    def _begin():
        input_out[...] = input_grad[...]
        output_out[...] = output[...]
        for n, out in enumerate((g1_out, s1_out, g2_out, s2_out)):
            out[...] = small[row_at(small, n)].reshape(out.shape)
        for n in range(experts):
            router_out[n : n + 1, :] = small[row_at(small, 8 + n)]
        load_out[...] = small[row_at(small, 4)][:, 0:experts].reshape(experts) * scale

    for n, out in enumerate((q_out, k_out, v_out)):
        part = full[:, n * width : (n + 1) * width, :].astype(F32)
        out[...] = part.reshape(-1, part.shape[2]).T
    part = full[:, 3 * width :, :].astype(F32)
    o_out[...] = part.reshape(-1, part.shape[2])
    trained = jnp.where(lax.axis_index("expert") >= experts // 2, 1.0, 0.0)
    up_out[...] = dw[0].astype(F32) * trained
    down_out[...] = dw[1].astype(F32).T * trained


def turn_weights(full, dw, small, input_grad, output, width, experts, scale):
    n_h, deep, model = full.shape
    cols = 384
    across = pl.BlockSpec((cols, model), lambda i: (i, 0))
    down = pl.BlockSpec((model, cols), lambda i: (0, i))
    flat = pl.BlockSpec((model,), lambda i: (0,))
    whole = pl.BlockSpec(output.shape, lambda i: (0, 0))
    square = shape_of((model, model), F32)
    return pl.pallas_call(
        partial(turn_body, width, experts, scale),
        name="turn_weights",
        grid=(model // cols,),
        out_shape=[square] * 6
        + [shape_of((model,), F32)] * 4
        + [
            shape_of((experts, model), F32),
            shape_of(input_grad.shape, BF),
            shape_of(output.shape, BF),
            shape_of((experts,), F32),
        ],
        in_specs=[
            pl.BlockSpec((n_h, deep, cols), lambda i: (0, 0, i)),
            pl.BlockSpec((2, model, cols), lambda i: (0, 0, i)),
            pl.BlockSpec(small.shape, lambda i: (0, 0, 0)),
            whole,
            whole,
        ],
        out_specs=[across, across, across, down, down, across]
        + [flat] * 4
        + [pl.BlockSpec((experts, model), lambda i: (0, 0)), whole, whole]
        + [pl.BlockSpec((experts,), lambda i: (0,))],
        compiler_params=pltpu.CompilerParams(
            dimension_semantics=("arbitrary",), vmem_limit_bytes=60 << 20
        ),
        cost_estimate=pl.CostEstimate(flops=0, bytes_accessed=24 << 20, transcendentals=0),
    )(full, dw, small, input_grad, output)


def attend_back(
    heads, i, span, first, qkv, given, centre, kept, values, dq_acc, dk_acc, dv_acc
):
    width = heads * HEAD_DIM
    rows = aligned(i * BLOCK, BLOCK)
    dq_acc[...] = jnp.zeros_like(dq_acc)
    queries = [
        qkv[n * HEAD_DIM : (n + 1) * HEAD_DIM, rows] * jnp.asarray(SCALE, BF) for n in range(heads)
    ]
    for k in range(span):
        part = aligned((first + k) * BLOCK, BLOCK)
        for n in range(heads):
            here = slice(n * HEAD_DIM, (n + 1) * HEAD_DIM)
            weight = kept[n, k]
            d_weight = mm(values[n, part, :], given[n])
            d_score = (weight.astype(F32) * (d_weight - centre[n])).astype(BF)
            dv_acc[here, part] += mm_nt(given[n], weight)
            dk_acc[here, part] += mm_nt(queries[n], d_score)
            lo = width + n * HEAD_DIM
            dq_acc[here, :] += mm(qkv[lo : lo + HEAD_DIM, part], d_score)


def back_body(
    n_e,
    n_h,
    experts,
    capacity,
    padded,
    heads,
    ids,
    slot,
    pos,
    gates,
    count,
    g1,
    s1,
    g2,
    s2,
    w_router,
    inverse,
    dg_rows,
    dx_back,
    y_out,
    dw_sum,
    dw_far,
    out_grad,
    residual,
    all_tokens,
    qkv_in,
    att_in,
    att_t_in,
    w_out,
    w_t_in,
    weights,
    y_back,
    d_hidden,
    d_res,
    w_all,
    small,
    dw_own,
    dxv,
    gv,
    res_v,
    tv,
    qkv,
    att_v,
    att_t,
    wo,
    w_t,
    d_att_v,
    d_att,
    wo_box,
    wo_far,
    kept,
    values,
    dq_acc,
    dk_acc,
    dv_acc,
    d_qkv,
    w_acc,
    dw_mine,
    dw_across,
    load_sem,
    save_sem,
    dw_sem,
    kept_sem,
    y_own,
    y_s,
    y_r,
    at_s,
    at_r,
    wo_s,
    wo_r,
    wf_s,
    wf_r,
    da_s,
    da_r,
):
    e, h = lax.axis_index("expert"), lax.axis_index("hidden")
    far = n_h // 2
    pair, core = h // 2, lax.rem(h, 2)
    mate = pair * 2 + 1 - core
    rows, model = out_grad.shape
    width = heads * HEAD_DIM
    group = rows * n_h
    per_device = rows // BLOCK
    blocks = group // BLOCK
    sends = []

    loads = [
        pltpu.make_async_copy(source, target, load_sem.at[n])
        for n, (source, target) in enumerate(
            (
                (residual, res_v),
                (dx_back, dxv),
                (out_grad, gv),
                (w_out, wo),
                (att_t_in, att_t),
                (qkv_in, qkv),
                (att_in, att_v),
                (all_tokens, tv),
                (w_t_in, w_t),
            )
        )
    ]
    for load in loads:
        load.start()
    greet(
        [{"hidden": lax.rem(h + step, n_h)} for step in range(1, n_h)]
        + [{"expert": lax.rem(e + step, n_e)} for step in range(1, n_e)]
    )
    load_dw = pltpu.make_async_copy(dw_sum.at[:, 0], dw_mine, dw_sem.at[0])
    load_dw.start()
    deep = dw_mine.shape[1] // 2
    load_far = pltpu.make_async_copy(
        dw_far, dw_across.at[0], dw_sem.at[1]
    )
    load_far.start()

    def dw_across_copy(step, k):
        part = pl.ds(k * deep, deep)
        return remote(
            dw_sum.at[1, step, part],
            dw_across.at[1, step - 1, part],
            da_s.at[step, k],
            da_r.at[step, k],
            {"hidden": lax.rem(pair + step, far) * 2 + core},
        )

    def dw_send(k):
        for step in range(1, far):
            dw_across_copy(step, k).start()

    dw_send(0)
    for step in range(1, n_e):
        peer = lax.rem(e + step, n_e)
        copy = remote(y_out.at[peer], y_back.at[e], y_s.at[step], y_r.at[step], {"expert": peer})
        copy.start()
        sends.append(copy)
    own_y = pltpu.make_async_copy(y_out.at[e], y_back.at[e], y_own)
    own_y.start()

    for load in loads[:3]:
        load.wait()
    normed, spread = norm_parts(res_v[...])
    hidden = (normed * lying(g2) + lying(s2)).astype(BF)
    gate = [gates[:, j : j + 1] for j in range(2)]
    column = iota((rows, padded), 1)
    dot_of = []
    for j in range(2):
        mix = jnp.zeros((rows, padded), F32)
        for n in range(experts):
            here = jnp.where(ids[:, j : j + 1] == n, slot[:, j : j + 1], -1) == column
            mix = jnp.where(here, dg_rows[n, 0:1, :], mix)
        dot_of.append(jnp.sum(mix, axis=1, keepdims=True))
    mean = gate[0] * dot_of[0] + gate[1] * dot_of[1]
    lane = iota((rows, experts), 1)
    d_logits = jnp.zeros((rows, experts), F32)
    for j in range(2):
        d_logits = jnp.where(lane == ids[:, j : j + 1], gate[j] * (dot_of[j] - mean), d_logits)
    high, low = split_two(d_logits)
    grad = mm(high, w_router[...]) + mm(low, w_router[...])
    small[...] = jnp.zeros_like(small)
    for_router = mm_tn(high, hidden) + mm_tn(low, hidden)
    for n in range(experts):
        small[row_at(small, 8 + n)] = for_router[n : n + 1]
    place, line = row_at(small, 4)
    small[place, line, 0:LANES] = count[...]
    place = iota((rows, experts * capacity), 1)
    for j in range(2):
        pick = (place == pos[:, j : j + 1]).astype(BF)
        grad = grad + gate[j] * mm(pick, dxv[...])
    small[row_at(small, 2)] = jnp.sum(grad * normed, axis=0, keepdims=True)
    small[row_at(small, 3)] = jnp.sum(grad, axis=0, keepdims=True)
    d_resid = gv[...].astype(F32) + norm_back(grad, normed, spread, lying(g2))
    d_res[...] = d_resid
    branch = d_resid.astype(BF)
    loads[3].wait()

    def device_at(n, sign):
        t, other = n // 2, lax.rem(n, 2)
        return lax.rem(pair + far + sign * t, far) * 2 + lax.rem(core + other, 2)

    def give_att(n):
        owner = device_at(n, 1)
        return remote(
            d_att_v.at[owner], d_att.at[h], at_s.at[n], at_r.at[n], {"hidden": owner}
        )

    for n in range(n_h - 1, -1, -1):
        owner = device_at(n, 1)
        block = mm_nt(wo[owner], branch).astype(BF)
        if n == 0:
            d_att[h] = block
        else:
            d_att_v[owner] = block
            give_att(n).start()
    loads[4].wait()
    for t in range(n_h):
        owner = lax.rem(h + t, n_h)
        wo[owner] = mm(att_t[owner], branch).astype(BF)
    for step in list(range(1, far)) + [0]:
        copy = remote(
            wo.at[lax.rem(pair + step, far) * 2 + 1 - core],
            wo_box.at[step],
            wo_s.at[step],
            wo_r.at[step],
            {"hidden": mate},
        )
        copy.start()
        sends.append(copy)
    def give_wo(step):
        target = lax.rem(pair + step, far) * 2 + core
        return remote(
            wo.at[target],
            wo_far.at[step - 1],
            wf_s.at[step],
            wf_r.at[step],
            {"hidden": target},
        )

    for load in loads[5:]:
        load.wait()

    def load_kept(i, turn):
        return pltpu.make_async_copy(weights.at[i], kept.at[turn], kept_sem.at[turn])

    def block_at(at):
        owner = device_at(at // per_device, 1)
        return owner, owner * per_device + lax.rem(at, per_device)

    load_kept(block_at(0)[1], 0).start()
    dk_acc[...] = jnp.zeros_like(dk_acc)
    dv_acc[...] = jnp.zeros_like(dv_acc)

    def turn_values(i, _):
        cols = aligned(i * BLOCK, BLOCK)
        for n in range(heads):
            lo = 2 * width + n * HEAD_DIM
            values[n, cols, :] = qkv[lo : lo + HEAD_DIM, cols].astype(F32).T.astype(BF)
        return 0

    lax.fori_loop(0, blocks, turn_values, 0)

    def over_queries(at, _):
        owner, i = block_at(at)
        turn = lax.rem(at, 2)

        @pl.when(at + 1 < blocks)
        def _next():
            load_kept(block_at(at + 1)[1], 1 - turn).start()

        @pl.when((at >= per_device) & (lax.rem(at, per_device) == 0))
        def _arrive():
            n = at // per_device
            source = lax.rem(far - n // 2, far) * 2 + lax.rem(n, 2)
            give_att(source).wait_recv()

        @pl.when(at == per_device)
        def _weights():
            for step in range(1, far):
                there = wo_box.at[step]
                target = lax.rem(pair + step, far) * 2 + core
                remote(there, there, wo_s.at[step], wo_r.at[step], {"hidden": mate}).wait_recv()
                both = wo[target].astype(F32) + wo_box[step].astype(F32)
                wo[target] = both.astype(BF)
                give_wo(step).start()
            dw_send(1)

        load_kept(i, turn).wait()
        cols = aligned(lax.rem(at, per_device) * BLOCK, BLOCK)
        rows_i = aligned(i * BLOCK, BLOCK)
        given, centre = [], []
        for n in range(heads):
            here = slice(n * HEAD_DIM, (n + 1) * HEAD_DIM)
            scaled = d_att[owner, here, cols].astype(F32) * inverse[n : n + 1, rows_i]
            given.append(scaled.astype(BF))
            product = att_v[owner, here, cols].astype(F32) * scaled
            centre.append(jnp.sum(product, axis=0, keepdims=True))

        def block(span, first):
            attend_back(
                heads,
                i,
                span,
                first,
                qkv,
                given,
                centre,
                kept.at[turn],
                values,
                dq_acc,
                dk_acc,
                dv_acc,
            )

        spans(i, block)
        d_qkv[0:width, rows_i] = (dq_acc[...] * SCALE).astype(BF)
        return 0

    lax.fori_loop(0, blocks, over_queries, 0)
    w_acc[...] = jnp.zeros_like(w_acc)

    def finish(i, _):
        cols = aligned(i * BLOCK, BLOCK)
        d_qkv[width : 2 * width, cols] = dk_acc[:, cols].astype(BF)
        d_qkv[2 * width :, cols] = dv_acc[:, cols].astype(BF)
        block = d_qkv[:, cols]
        grad = mm_tn(block, w_t[...])
        inner = aligned(lax.rem(i, per_device) * BLOCK, BLOCK)
        normed, _unused = norm_parts(tv[i // per_device, inner, :].astype(F32))
        tv[i // per_device, inner, :] = grad.astype(BF)
        small[row_at(small, 0)] += jnp.sum(grad * normed, axis=0, keepdims=True)
        small[row_at(small, 1)] += jnp.sum(grad, axis=0, keepdims=True)
        hidden = (normed * lying(g1) + lying(s1)).astype(BF)
        w_acc[...] += mm(block, hidden)
        return 0

    lax.fori_loop(0, blocks, finish, 0)
    save_dh = pltpu.make_async_copy(tv, d_hidden, save_sem)
    save_dh.start()
    w_all[0 : 3 * width, :] = w_acc[...].astype(BF)
    there = wo_box.at[0]
    remote(there, there, wo_s.at[0], wo_r.at[0], {"hidden": mate}).wait_recv()
    total = wo[h].astype(F32) + wo_box[0].astype(F32)
    for step in range(1, far):
        give_wo(step).wait_recv()
        total = total + wo_far[step - 1].astype(F32)
    w_all[3 * width :, :] = total.astype(BF)
    load_dw.wait()
    load_far.wait()
    for which in range(2):
        for step in range(1, far if which == 1 else 1):
            for k in range(2):
                dw_across_copy(step, k).wait()

        def add_all(n, _, which=which):
            band = aligned(n * 96, 96)
            both = dw_mine[which, band, :].astype(F32)
            for step in range(1, far):
                both = both + dw_across[which, step - 1, band, :].astype(F32)
            dw_own[which, band, :] = both.astype(BF)
            return 0

        lax.fori_loop(0, dw_mine.shape[1] // 96, add_all, 0)
    for step in range(1, n_e):
        there = y_back.at[lax.rem(e + n_e - step, n_e)]
        remote(there, there, y_s.at[step], y_r.at[step], {"expert": e}).wait_recv()
    own_y.wait()
    save_dh.wait()
    for n in range(1, n_h):
        give_att(n).wait_send()
    for step in range(1, far):
        give_wo(step).wait_send()
    for copy in sends:
        copy.wait_send()


def run_back(
    ids,
    slot,
    pos,
    gates,
    count,
    g1,
    s1,
    g2,
    s2,
    w_router,
    inverse,
    dg_rows,
    dx_back,
    y_out,
    dw_sum,
    dw_far,
    out_grad,
    residual,
    all_tokens,
    qkv,
    att,
    att_t,
    w_out,
    w_t,
    weights,
    cid,
):
    n_e, n_h = lax.axis_size("expert"), lax.axis_size("hidden")
    experts, capacity, model = y_out.shape
    padded = dg_rows.shape[2]
    rows = out_grad.shape[0]
    width = w_t.shape[0] // 3
    heads = width // HEAD_DIM
    group, far = rows * n_h, n_h // 2
    shard = dw_sum.shape[2:]
    tall = 8 + experts

    def pairs(*shape):
        return [DMA(shape), DMA(shape)]

    return pl.pallas_call(
        partial(back_body, n_e, n_h, experts, capacity, padded, heads),
        name="back",
        out_shape=[
            shape_of(y_out.shape, BF),
            shape_of((n_h, rows, model), BF),
            shape_of((rows, model), F32),
            shape_of((4 * width, model), BF),
            shape_of((n_h, tall // n_h, model), F32),
            shape_of((2, *shard), BF),
        ],
        in_specs=[VMEM] * 12 + [ANY] * 13,
        out_specs=[ANY] * 2 + [VMEM] * 4,
        scratch_shapes=[
            pltpu.VMEM((experts * capacity, model), BF),
            pltpu.VMEM((rows, model), BF),
            pltpu.VMEM((rows, model), F32),
            pltpu.VMEM((n_h, rows, model), BF),
            pltpu.VMEM((3 * width, group), BF),
            pltpu.VMEM((n_h, width, rows), BF),
            pltpu.VMEM((n_h, width, rows), BF),
            pltpu.VMEM((n_h, width, model), BF),
            pltpu.VMEM((3 * width, model), BF),
            pltpu.VMEM((n_h, width, rows), BF),
            pltpu.VMEM((n_h, width, rows), BF),
            pltpu.VMEM((far, width, model), BF),
            pltpu.VMEM((far - 1, width, model), BF),
            pltpu.VMEM((2, heads, REACH, BLOCK, BLOCK), BF),
            pltpu.VMEM((heads, group, HEAD_DIM), BF),
            pltpu.VMEM((width, BLOCK), F32),
            pltpu.VMEM((width, group), F32),
            pltpu.VMEM((width, group), F32),
            pltpu.VMEM((3 * width, group), BF),
            pltpu.VMEM((3 * width, model), F32),
            pltpu.VMEM((2, *shard), BF),
            pltpu.VMEM((2, far - 1, *shard), BF),
            DMA((9,)),
            DMA,
            DMA((2,)),
            DMA((2,)),
            DMA,
            *pairs(n_e),
            *pairs(n_h),
            *pairs(far),
            *pairs(far),
            *pairs(far, 2),
        ],
        compiler_params=pltpu.CompilerParams(
            collective_id=cid, has_side_effects=True, vmem_limit_bytes=60 << 20
        ),
    )(
        ids,
        slot,
        pos,
        gates,
        count,
        g1,
        s1,
        g2,
        s2,
        w_router,
        inverse,
        dg_rows,
        dx_back.reshape(experts * capacity, model),
        y_out,
        dw_sum,
        dw_far,
        out_grad,
        residual,
        all_tokens,
        qkv,
        att,
        att_t,
        w_out.reshape(n_h, width, model),
        w_t,
        weights,
    )


def shards(
    tokens,
    doc_lengths,
    expert_ids,
    gain_one,
    shift_one,
    w_query,
    w_key,
    w_value,
    w_out,
    gain_two,
    shift_two,
    w_router,
    w_up,
    w_down,
    out_grad,
):
    rows, model = tokens.shape
    n_expert, n_hidden = lax.axis_size("expert"), lax.axis_size("hidden")
    experts = n_expert * w_up.shape[0]
    capacity = max(2, rows * 2 * 5 // (4 * experts))
    capacity = -(-capacity // 16) * 16
    total = experts * capacity
    heads = HEADS // n_hidden
    width = heads * HEAD_DIM
    g1, s1, g2, s2 = gain_one, shift_one, gain_two, shift_two
    router_t = w_router.T

    (
        all_tokens,
        qkv,
        att,
        att_t,
        w_t,
        g_in,
        x_slots,
        ups,
        weights,
        ids,
        pos,
        slot,
        count,
        inverse,
        residual,
        gates,
        gate_rows,
    ) = run_front(
        doc_lengths,
        expert_ids.T,
        g1,
        s1,
        g2,
        s2,
        router_t,
        tokens,
        out_grad,
        (w_query, w_key, w_value, w_out),
        w_up,
        capacity,
        heads,
        1,
    )
    dx_back, dg_back, y_out, dw_sum, dw_far = run_experts(
        x_slots, gate_rows, g_in, ups, w_up, w_down, 2
    )
    y_back, d_hidden, d_res, w_all, small, dw_own = run_back(
        ids,
        slot,
        pos,
        gates,
        count,
        g1,
        s1,
        g2,
        s2,
        router_t,
        inverse,
        dg_back,
        dx_back,
        y_out,
        dw_sum,
        dw_far,
        out_grad,
        residual,
        all_tokens,
        qkv,
        att,
        att_t,
        w_out,
        w_t,
        weights,
        3,
    )
    input_grad, output, full, small = run_tail(
        d_hidden,
        w_all.reshape(n_expert, 4 * width // n_expert, model),
        small,
        tokens,
        g1,
        d_res,
        residual,
        gates,
        pos,
        y_back.reshape(total, model),
        4,
    )
    scale = experts / (rows * n_expert * n_hidden * 2)
    turned = turn_weights(
        full.reshape(n_hidden, 4 * width, model),
        dw_own,
        small,
        input_grad,
        output,
        width,
        experts,
        scale,
    )
    w_grads, (up_grad, down_grad) = turned[:4], turned[4:6]
    gain_one_grad, shift_one_grad, gain_two_grad, shift_two_grad = turned[6:10]
    router_grad, input_grad, output, load = turned[10:]
    return (
        output,
        input_grad,
        gain_one_grad,
        shift_one_grad,
        *w_grads,
        gain_two_grad,
        shift_two_grad,
        router_grad.T,
        up_grad[None],
        down_grad[None],
        load,
    )


def solution(mesh):
    in_specs = (
        P(("expert", "hidden"), None),
        P("expert", None),
        P(("expert", "hidden"), None),
        P(),
        P(),
        P(),
        P(),
        P(),
        P(),
        P(),
        P(),
        P(),
        P("expert", None, "hidden"),
        P("expert", "hidden", None),
        P(("expert", "hidden"), None),
    )
    out_specs = (
        P(("expert", "hidden"), None),
        P(("expert", "hidden"), None),
        P(),
        P(),
        P(),
        P(),
        P(),
        P(),
        P(),
        P(),
        P(),
        P("expert", None, "hidden"),
        P("expert", "hidden", None),
        P(),
    )
    return jax.shard_map(shards, mesh=mesh, in_specs=in_specs, out_specs=out_specs, check_vma=False)
```

```python
from functools import partial

import jax
import jax.numpy as jnp
from jax import lax
from jax.experimental import pallas as pl
from jax.experimental.pallas import tpu as pltpu
from jax.sharding import PartitionSpec as P

HEAD_DIM = 64
HEADS = 12
EPSILON = 1e-05
SCALE = 0.125
MASKED = -1e30
BLOCK = 256
LONGEST = 1024
REACH = LONGEST // BLOCK + 1
UP_FIRST = 4
UP_EARLY = 6
LANES = 128
BF = jnp.bfloat16
F32 = jnp.float32
I32 = jnp.int32
MESH = pl.DeviceIdType.MESH
ANY = pl.BlockSpec(memory_space=pl.ANY)
SMEM = pl.BlockSpec(memory_space=pltpu.SMEM)
VMEM = pl.BlockSpec(memory_space=pltpu.VMEM)
DMA = pltpu.SemaphoreType.DMA
GELU_A = 0.7978845608028654
GELU_B = 0.044715


def mm(left, right):
    return jnp.dot(left, right, preferred_element_type=F32)


def mm_nt(left, right):
    return lax.dot_general(left, right, (((1,), (1,)), ((), ())), preferred_element_type=F32)


def mm_tn(left, right):
    return lax.dot_general(left, right, (((0,), (0,)), ((), ())), preferred_element_type=F32)


def iota(shape, axis):
    return lax.broadcasted_iota(I32, shape, axis)


def norm_parts(values):
    centred = values - jnp.mean(values, axis=-1, keepdims=True)
    inverse = lax.rsqrt(jnp.mean(centred * centred, axis=-1, keepdims=True) + EPSILON)
    return centred * inverse, inverse


def norm_back(grad_out, normed, inverse, gain):
    grad_normed = grad_out * gain
    first = jnp.mean(grad_normed, axis=-1, keepdims=True)
    second = jnp.mean(grad_normed * normed, axis=-1, keepdims=True)
    return inverse * (grad_normed - first - normed * second)


def split_two(value):
    high = value.astype(BF)
    return high, (value - high.astype(F32)).astype(BF)


def row_at(ref, row):
    share = ref.shape[1]
    return row // share, slice(row % share, row % share + 1)


def shape_of(shape, dtype):
    return jax.ShapeDtypeStruct(shape, dtype)


def greet(peers):
    barrier = pltpu.get_barrier_semaphore()
    for peer in peers:
        pl.semaphore_signal(barrier, inc=1, device_id=peer, device_id_type=MESH)
    pl.semaphore_wait(barrier, len(peers))


def remote(src, dst, send, recv, peer):
    return pltpu.make_async_remote_copy(
        src_ref=src, dst_ref=dst, send_sem=send, recv_sem=recv, device_id=peer, device_id_type=MESH
    )


def doc_bounds(docs):
    ends, at = [], 0
    for n in range(docs.shape[1] - 1):
        at = at + docs[0, n]
        ends.append(at)
    return ends


def start_of(place, ends):
    begin = jnp.zeros_like(place)
    for end in ends:
        begin = jnp.where(place >= end, end, begin)
    return begin


def lying(ref):
    return ref[...].reshape(1, ref.shape[0])


def aligned(at, size):
    return pl.ds(pl.multiple_of(at, size), size)


def find_slots(experts, capacity, ids, ids_t, pos, slot, count):
    rows = ids_t.shape[1]
    row = [ids_t[j : j + 1, :] for j in range(2)]
    tall = jnp.concatenate([r.astype(F32) for r in row] + [jnp.zeros((6, rows), F32)], axis=0)
    ids[...] = tall.T[:, 0:2].astype(I32)
    col = [ids[:, j : j + 1] for j in range(2)]
    lane = iota((rows, LANES), 1)
    hot = [(lane == c).astype(BF) for c in col]
    either = hot[0] + hot[1]
    below = (iota((rows, rows), 0) > iota((rows, rows), 1)).astype(BF)
    before = mm(below, either)
    wide = max(experts, 16)
    deep = iota((wide, rows), 0)
    hot_t = [(deep == r).astype(BF) for r in row]
    above = (iota((rows, rows), 0) < iota((rows, rows), 1)).astype(BF)
    before_t = mm(hot_t[0] + hot_t[1], above)
    count[...] = jnp.sum(either.astype(F32), axis=0, keepdims=True)
    flat_t = []
    for j in range(2):
        at = jnp.sum(hot[j].astype(F32) * before, axis=1, keepdims=True).astype(I32)
        pos[:, j : j + 1] = col[j] * capacity + at
        slot[:, j : j + 1] = at
        at_t = jnp.sum(hot_t[j].astype(F32) * before_t, axis=0, keepdims=True).astype(I32)
        flat_t.append(row[j] * capacity + at_t)
    return flat_t


def fill_slots(flat_t, source, out):
    total, rows = out.shape[0], source.shape[0]
    half = total // 2
    for n in range(2):
        place = iota((half, rows), 0) + n * half
        pick = ((place == flat_t[0]) | (place == flat_t[1])).astype(BF)
        out[pl.ds(n * half, half), :] = mm(pick, source).astype(BF)


def attend_block(heads, ends, i, span, first, qkv, keys, scores, kept, inverse):
    width = heads * HEAD_DIM
    base = i * BLOCK
    rows = aligned(base, BLOCK)
    q_pos = base + iota((1, BLOCK), 1)
    begin = start_of(q_pos, ends)
    queries = [
        qkv[n * HEAD_DIM : (n + 1) * HEAD_DIM, rows] * jnp.asarray(SCALE, BF) for n in range(heads)
    ]
    tops = [jnp.full((1, BLOCK), MASKED, F32)] * heads
    for k in range(span):
        part = aligned((first + k) * BLOCK, BLOCK)
        k_pos = (first + k) * BLOCK + iota((BLOCK, BLOCK), 0)
        allowed = (k_pos <= q_pos) & (k_pos >= begin)
        for n in range(heads):
            score = jnp.where(allowed, mm(keys[n, part, :], queries[n]), MASKED)
            scores[n, k] = score
            tops[n] = jnp.maximum(tops[n], jnp.max(score, axis=0, keepdims=True))
    result = []
    for n in range(heads):
        total = jnp.zeros((1, BLOCK), F32)
        acc = jnp.zeros((HEAD_DIM, BLOCK), F32)
        lo = 2 * width + n * HEAD_DIM
        for k in range(span):
            weight = jnp.exp(scores[n, k] - tops[n])
            total = total + jnp.sum(weight, axis=0, keepdims=True)
            value = qkv[lo : lo + HEAD_DIM, aligned((first + k) * BLOCK, BLOCK)]
            low = weight.astype(BF)
            kept[n, k] = low
            acc = acc + mm(value, low)
        whole = 1.0 / total
        inverse[n : n + 1, rows] = whole
        result.append((acc * whole).astype(BF))
    return result


def spans(i, body):
    @pl.when(i < 2)
    def _short():
        body(2, 0)

    @pl.when(i >= 2)
    def _long():
        body(REACH, (i - (REACH - 1)) * (i // (REACH - 1)))


def front_body(
    n_e,
    n_h,
    experts,
    capacity,
    padded,
    heads,
    chunks,
    docs,
    ids_t,
    g1,
    s1,
    g2,
    s2,
    w_router,
    tokens,
    out_grad,
    w_query,
    w_key,
    w_value,
    w_out,
    w_up,
    all_tokens,
    qkv_out,
    att_out,
    att_t_out,
    w_t_out,
    g_in,
    x_slots,
    ups,
    weights,
    ids,
    pos,
    slot,
    count,
    inverse,
    residual,
    gates,
    gate_rows,
    tv,
    gv,
    wv,
    wo,
    w_t,
    qkv,
    keys,
    scores,
    kept,
    att_v,
    att_in,
    g_slots,
    xs_v,
    own_sem,
    w_sem,
    save_sem,
    kept_sem,
    ty_s,
    ty_r,
    tc_s,
    tc_r,
    tf_s,
    tf_r,
    gs_s,
    gs_r,
    at_s,
    at_r,
    wy_s,
    wy_r,
    wc_s,
    wc_r,
    wf_s,
    wf_r,
):
    e, h = lax.axis_index("expert"), lax.axis_index("hidden")
    far = n_h // 2
    pair, core = h // 2, lax.rem(h, 2)
    mate = pair * 2 + 1 - core
    rows, model = tokens.shape
    width = heads * HEAD_DIM
    per_device = rows // BLOCK
    ends = doc_bounds(docs)

    def across(t):
        return lax.rem(pair + t, far) * 2 + core

    def origin(t):
        return lax.rem(pair + far - t, far) * 2 + core

    own_tokens = pltpu.make_async_copy(tokens, tv.at[h], own_sem.at[0])
    own_grad = pltpu.make_async_copy(out_grad, gv, own_sem.at[1])
    own_grad.start()
    own_tokens.start()
    w_loads = [
        pltpu.make_async_copy(w, wv.at[n], w_sem.at[n])
        for n, w in enumerate((w_query, w_key, w_value))
    ]
    w_loads.append(pltpu.make_async_copy(w_out, wo, w_sem.at[3]))
    for load in w_loads:
        load.start()
    greet(
        [{"hidden": lax.rem(h + step, n_h)} for step in range(1, n_h)]
        + [{"expert": lax.rem(e + step, n_e)} for step in range(1, n_e)]
    )

    piece = rows // chunks
    sends = []
    for k in range(chunks):
        part = pl.ds(k * piece, piece)
        for t in range(1, far):
            copy = remote(
                tokens.at[part],
                tv.at[h, part],
                ty_s.at[t, k],
                ty_r.at[t, k],
                {"hidden": across(t)},
            )
            copy.start()
            sends.append(copy)
    beside = remote(tokens, tv.at[h], tc_s, tc_r, {"hidden": mate})
    beside.start()
    sends.append(beside)

    flat_t = find_slots(experts, capacity, ids, ids_t, pos, slot, count)
    own_grad.wait()
    fill_slots(flat_t, gv[...], g_slots)
    for step in range(1, n_e):
        peer = lax.rem(e + step, n_e)
        copy = remote(
            g_slots.at[aligned(peer * capacity, capacity)],
            g_in.at[e],
            gs_s.at[step],
            gs_r.at[step],
            {"expert": peer},
        )
        copy.start()
        sends.append(copy)
    own_slots = pltpu.make_async_copy(
        g_slots.at[aligned(e * capacity, capacity)], g_in.at[e], own_sem.at[1]
    )
    own_slots.start()

    def pass_on(t, k):
        part = pl.ds(k * piece, piece)
        place = tv.at[origin(t), part]
        remote(place, place, ty_s.at[t, k], ty_r.at[t, k], {"hidden": across(t)}).wait_recv()
        copy = remote(place, place, tf_s.at[t, k], tf_r.at[t, k], {"hidden": mate})
        copy.start()
        sends.append(copy)

    todo = [(t, k) for k in range(chunks) for t in range(1, far)]
    third = -(-len(todo) // 4)

    def pass_some():
        for _ in range(min(third, len(todo))):
            pass_on(*todo.pop(0))

    pick = (iota((width, model), 1) == iota((width, model), 0) + h * width).astype(BF)
    for n in range(3):
        w_loads[n].wait()
        w_t[n * width : (n + 1) * width, :] = mm_nt(pick, wv[n]).astype(BF)
        if n == 1:
            pass_some()
    save_w = pltpu.make_async_copy(w_t, w_t_out, save_sem.at[0])
    save_w.start()

    def project(source):
        def one(b, _):
            normed, _unused = norm_parts(tv[source, aligned(b * BLOCK, BLOCK), :].astype(F32))
            hidden = (normed * lying(g1) + lying(s1)).astype(BF)
            block = mm_nt(w_t[...], hidden)
            cols = aligned(source * rows + b * BLOCK, BLOCK)
            qkv[:, cols] = block.astype(BF)
            for n in range(heads):
                lo = width + n * HEAD_DIM
                keys[n, cols, :] = block[lo : lo + HEAD_DIM].T.astype(BF)
            return 0

        lax.fori_loop(0, per_device, one, 0)

    pass_some()
    own_tokens.wait()
    project(h)
    pass_some()
    remote(tokens, tv.at[mate], tc_s, tc_r, {"hidden": mate}).wait_recv()
    project(mate)
    while todo:
        pass_some()

    eighth = w_up.shape[1] // 8
    up_parts = (
        pl.ds(0, UP_FIRST * eighth),
        pl.ds(UP_FIRST * eighth, (UP_EARLY - UP_FIRST) * eighth),
    )

    def up_copy(t, k, source):
        return remote(
            w_up.at[0, up_parts[k]],
            ups.at[source, up_parts[k]],
            wy_s.at[t, k],
            wy_r.at[t, k],
            {"hidden": across(t)},
        )

    def up_onward(t, k):
        place = ups.at[origin(t), up_parts[k]]
        return remote(place, place, wf_s.at[t, k], wf_r.at[t, k], {"hidden": mate})

    def up_arrived(k):
        for t in range(1, far):
            up_copy(t, k, origin(t)).wait_recv()
            up_onward(t, k).start()

    up_beside = remote(w_up.at[0], ups.at[h], wc_s, wc_r, {"hidden": mate})
    up_beside.start()
    sends.append(up_beside)
    for t in range(1, far):
        up_copy(t, 0, h).start()
    for t in range(1, far):
        project(origin(t))
    for t in range(1, far):
        there = lax.rem(pair + far - t, far) * 2 + 1 - core
        for k in range(chunks):
            place = tv.at[there, pl.ds(k * piece, piece)]
            remote(place, place, tf_s.at[t, k], tf_r.at[t, k], {"hidden": mate}).wait_recv()
        project(there)
    save_tokens = pltpu.make_async_copy(tv, all_tokens, save_sem.at[1])
    save_qkv = pltpu.make_async_copy(qkv, qkv_out, save_sem.at[2])
    save_tokens.start()
    save_qkv.start()

    inverse[...] = jnp.zeros_like(inverse)

    def device_at(n, sign):
        t, other = n // 2, lax.rem(n, 2)
        return lax.rem(pair + far + sign * t, far) * 2 + lax.rem(core + other, 2)

    def give_att(n):
        owner = device_at(n, 1)
        return remote(
            att_v.at[owner], att_in.at[h], at_s.at[n], at_r.at[n], {"hidden": owner}
        )

    def save_kept(i, turn):
        return pltpu.make_async_copy(kept.at[turn], weights.at[i], kept_sem.at[turn])

    def attend(at, _):
        n = n_h - 1 - at // per_device
        b = lax.rem(at, per_device)
        owner = device_at(n, 1)
        i = owner * per_device + b
        turn = lax.rem(at, 2)

        @pl.when(at >= 2)
        def _free():
            save_kept(i, turn).wait()

        def block(span, first):
            done = attend_block(
                heads, ends, i, span, first, qkv, keys, scores, kept.at[turn], inverse
            )
            for m in range(heads):
                lo = m * HEAD_DIM
                att_v[owner, lo : lo + HEAD_DIM, aligned(b * BLOCK, BLOCK)] = done[m]

        spans(i, block)
        save_kept(i, turn).start()

        @pl.when((b == per_device - 1) & (n > 0))
        def _give():
            give_att(n).start()

        @pl.when(at == (n_h - 2) * per_device - 1)
        def _more():
            for t in range(1, far):
                up_copy(t, 1, h).start()

        return 0

    lax.fori_loop(0, n_h * per_device, attend, 0)
    up_arrived(0)
    att_in[h] = att_v[h]
    save_att = pltpu.make_async_copy(att_v, att_out, save_sem.at[3])
    save_att.start()
    for n in range(n_h - 1, 0, -1):
        give_att(n).wait_recv()
    save_att_t = pltpu.make_async_copy(att_in, att_t_out, save_sem.at[4])
    save_att_t.start()

    w_loads[3].wait()
    res = tv[h].astype(F32) + mm_tn(att_in[...].reshape(model, rows), wo[...])
    residual[...] = res
    normed, _unused = norm_parts(res)
    hidden = (normed * lying(g2) + lying(s2)).astype(BF)
    fill_slots(flat_t, hidden, xs_v)
    save_x = [
        pltpu.make_async_copy(
            xs_v.at[pl.ds(n * capacity, capacity)], x_slots.at[n], save_sem.at[5 + n]
        )
        for n in range(experts)
    ]
    for save in save_x:
        save.start()
    logits = mm_nt(hidden, w_router[...])
    lane = iota((rows, experts), 1)
    chosen = [
        jnp.sum(jnp.where(lane == ids[:, j : j + 1], logits, 0.0), axis=1, keepdims=True)
        for j in range(2)
    ]
    top = jnp.maximum(chosen[0], chosen[1])
    raised = [jnp.exp(c - top) for c in chosen]
    both = raised[0] + raised[1]
    gate = [r / both for r in raised]
    for j in range(2):
        gates[:, j : j + 1] = gate[j]
    column = iota((rows, padded), 1)
    for n in range(experts):
        mix = jnp.zeros((rows, padded), F32)
        for j in range(2):
            here = jnp.where(ids[:, j : j + 1] == n, slot[:, j : j + 1], -1) == column
            mix = jnp.where(here, gate[j], mix)
        line = jnp.sum(mix, axis=0, keepdims=True)
        gate_rows[n] = jnp.broadcast_to(line, (8, padded))

    place = ups.at[mate]
    remote(place, place, wc_s, wc_r, {"hidden": mate}).wait_recv()
    up_arrived(1)
    for t in range(1, far):
        for k in range(2):
            up_onward(t, k).wait()
    for step in range(1, n_e):
        source = lax.rem(e + n_e - step, n_e)
        place = g_in.at[source]
        remote(place, place, gs_s.at[step], gs_r.at[step], {"expert": e}).wait_recv()
    own_slots.wait()
    for n in range(1, n_h):
        give_att(n).wait_send()
    for turn in range(2):
        save_kept(0, turn).wait()
    for t in range(1, far):
        for k in range(2):
            up_copy(t, k, h).wait_send()
    for copy in sends:
        copy.wait_send()
    for save in [save_w, save_tokens, save_qkv, save_att, save_att_t, *save_x]:
        save.wait()


def run_front(
    docs, ids_t, g1, s1, g2, s2, w_router, tokens, out_grad, ws, w_up, capacity, heads, cid
):
    n_e, n_h = lax.axis_size("expert"), lax.axis_size("hidden")
    experts = n_e * w_up.shape[0]
    rows, model = tokens.shape
    padded = -(-capacity // LANES) * LANES
    width, group, total = heads * HEAD_DIM, rows * n_h, experts * capacity
    far, chunks = n_h // 2, 8

    def pairs(*shape):
        return [DMA(shape), DMA(shape)]

    return pl.pallas_call(
        partial(front_body, n_e, n_h, experts, capacity, padded, heads, chunks),
        name="front",
        out_shape=[
            shape_of((n_h, rows, model), BF),
            shape_of((3 * width, group), BF),
            shape_of((n_h, width, rows), BF),
            shape_of((n_h, width, rows), BF),
            shape_of((3 * width, model), BF),
            shape_of((experts, capacity, model), BF),
            shape_of((experts, capacity, model), BF),
            shape_of((n_h, *w_up.shape[1:]), BF),
            shape_of((group // BLOCK, heads, REACH, BLOCK, BLOCK), BF),
            shape_of((rows, 2), I32),
            shape_of((rows, 2), I32),
            shape_of((rows, 2), I32),
            shape_of((1, LANES), F32),
            shape_of((8, group), F32),
            shape_of((rows, model), F32),
            shape_of((rows, 2), F32),
            shape_of((experts, 8, padded), F32),
        ],
        in_specs=[SMEM] + [VMEM] * 6 + [ANY] * 7,
        out_specs=[ANY] * 9 + [VMEM] * 8,
        scratch_shapes=[
            pltpu.VMEM((n_h, rows, model), BF),
            pltpu.VMEM((rows, model), BF),
            pltpu.VMEM((3, model, model), BF),
            pltpu.VMEM((model, model), BF),
            pltpu.VMEM((3 * width, model), BF),
            pltpu.VMEM((3 * width, group), BF),
            pltpu.VMEM((heads, group, HEAD_DIM), BF),
            pltpu.VMEM((heads, REACH, BLOCK, BLOCK), F32),
            pltpu.VMEM((2, heads, REACH, BLOCK, BLOCK), BF),
            pltpu.VMEM((n_h, width, rows), BF),
            pltpu.VMEM((n_h, width, rows), BF),
            pltpu.VMEM((total, model), BF),
            pltpu.VMEM((total, model), BF),
            DMA((2,)),
            DMA((4,)),
            DMA((5 + experts,)),
            DMA((2,)),
            *pairs(far, chunks),
            DMA,
            DMA,
            *pairs(far, chunks),
            *pairs(n_e),
            *pairs(n_h),
            *pairs(far, 2),
            DMA,
            DMA,
            *pairs(far, 2),
        ],
        compiler_params=pltpu.CompilerParams(
            collective_id=cid, has_side_effects=True, vmem_limit_bytes=58 << 20
        ),
    )(docs, ids_t, g1, s1, g2, s2, w_router, tokens, out_grad, *ws, w_up)


def moe_body(
    size,
    capacity,
    padded,
    per,
    x_slots,
    gate_rows,
    g_in,
    ups,
    w_up,
    w_down,
    dx_back,
    dg_back,
    y_out,
    dw_sum,
    dw_far,
    xv,
    gv,
    gates_v,
    up_v,
    down_v,
    act,
    dz,
    xg,
    dy,
    xg_t,
    dy_t,
    dxv,
    yv,
    dgv,
    y_acc,
    dx_acc,
    dw_box,
    load_sem,
    save_sem,
    wy_s,
    wy_r,
    wc_s,
    wc_r,
    wf_s,
    wf_r,
    dc_s,
    dc_r,
    df_s,
    df_r,
    g_sem,
    own_sem,
    xs_sem,
    xr_sem,
    gs_sem,
    gr_sem,
    ds_sem,
    dr_sem,
    ts_sem,
    tr_sem,
    out_sem,
):
    me, h = lax.axis_index("expert"), lax.axis_index("hidden")
    shards_n = ups.shape[0]
    far = shards_n // 2
    pair, core = h // 2, lax.rem(h, 2)
    mate = pair * 2 + 1 - core
    deep = w_down.shape[1] // 2
    tall = per * capacity
    steps = size // per

    middle = size // 2
    inner = lax.rem((me // 2 * 8 // size + 1) // 2, 2)

    def group_at(step):
        some = steps // 4
        early = jnp.where(step <= some, step - 1 + steps // 2, step - some)
        early = jnp.where((step > 0) & (step < steps - some), early, step)
        return jnp.where(inner == 1, early, step)

    def peer_at(p):
        peer, bit = 0, 1
        while bit < size:
            peer = peer + lax.rem(me // bit + p // bit, 2) * bit
            bit *= 2
        return peer

    def rows_of(p):
        return pl.ds(pl.multiple_of(p * capacity, capacity), capacity)

    def send_x(p):
        peer = peer_at(p)
        return remote(
            x_slots.at[peer], xv.at[rows_of(p)], xs_sem.at[p], xr_sem.at[p], {"expert": peer}
        )

    def send_gate(p):
        peer = peer_at(p)
        return remote(
            gate_rows.at[peer], gates_v.at[p], gs_sem.at[p], gr_sem.at[p], {"expert": peer}
        )

    def send_dx(p):
        peer = peer_at(p)
        return remote(
            dxv.at[rows_of(p)], dx_back.at[me], ds_sem.at[p], dr_sem.at[p], {"expert": peer}
        )

    def send_dg(p):
        peer = peer_at(p)
        return remote(dgv.at[p], dg_back.at[me], ts_sem.at[p], tr_sem.at[p], {"expert": peer})

    def load_g(p):
        return pltpu.make_async_copy(g_in.at[peer_at(p)], gv.at[rows_of(p)], g_sem.at[p])

    def save_y(p):
        return pltpu.make_async_copy(yv.at[rows_of(p)], y_out.at[peer_at(p)], out_sem.at[p])

    own_x = pltpu.make_async_copy(x_slots.at[me], xv.at[rows_of(0)], own_sem.at[0])
    own_gate = pltpu.make_async_copy(gate_rows.at[me], gates_v.at[0], own_sem.at[1])
    own_dx = pltpu.make_async_copy(dxv.at[rows_of(0)], dx_back.at[me], own_sem.at[2])
    own_dg = pltpu.make_async_copy(dgv.at[0], dg_back.at[me], own_sem.at[3])
    loads = [
        pltpu.make_async_copy(w_up.at[0], up_v.at[h], load_sem.at[0]),
        pltpu.make_async_copy(w_down.at[0], down_v.at[h], load_sem.at[1]),
    ]
    loads.append(pltpu.make_async_copy(ups.at[mate], up_v.at[mate], load_sem.at[2]))

    early = w_up.shape[1] * UP_EARLY // 8

    def half(k):
        return aligned(k * deep, deep)

    for t in range(1, far):
        for other in range(2):
            c = lax.rem(pair + t, far) * 2 + other
            place = (c, pl.ds(0, early))
            loads.append(
                pltpu.make_async_copy(
                    ups.at[place], up_v.at[place], load_sem.at[1 + 2 * t + other]
                )
            )
    rest = pl.ds(early, w_up.shape[1] - early)
    parts = ((w_up, up_v, rest), (w_down, down_v, half(0)), (w_down, down_v, half(1)))

    def part_across(t, n):
        source, target, k = parts[n]
        there = {"hidden": lax.rem(pair + t, far) * 2 + core}
        return remote(
            source.at[0, k], target.at[h, k], wy_s.at[t, n], wy_r.at[t, n], there
        )

    def part_onward(t, n):
        _source, target, k = parts[n]
        place = target.at[lax.rem(pair + far - t, far) * 2 + core, k]
        return remote(place, place, wf_s.at[t, n], wf_r.at[t, n], {"hidden": mate})

    down_beside = remote(w_down.at[0], down_v.at[h], wc_s, wc_r, {"hidden": mate})
    own_x.start()
    own_gate.start()
    for p in range(size):
        load_g(p).start()
    for load in loads:
        load.start()
    greet(
        [{"expert": lax.rem(me + step, size)} for step in range(1, size)]
        + [{"hidden": lax.rem(h + step, shards_n)} for step in range(1, shards_n)]
    )

    def send_all(order):
        for p in order:
            send_x(p).start()
            send_gate(p).start()

    @pl.when(inner == 1)
    def _far_first():
        send_all([1, *range(middle, size), *range(2, middle)])

    @pl.when(inner == 0)
    def _near_first():
        send_all(range(1, size))

    for n in range(3):
        for t in range(1, far):
            part_across(t, n).start()
    down_beside.start()
    own_x.wait()
    own_gate.wait()
    for load in loads:
        load.wait()

    def finish(base, rows, held):
        dxv[rows, :] = dx_acc[held, :].astype(BF)
        y_low = y_acc[held, :].astype(BF)
        yv[rows, :] = y_low
        x, g = xv[rows, :], gv[rows, :]
        dots = jnp.sum(y_low.astype(F32) * g.astype(F32), axis=1, keepdims=True)
        for s in range(per):
            p = base + s
            part = slice(s * capacity, (s + 1) * capacity)
            tall_dots = jnp.broadcast_to(dots[part], (capacity, LANES))
            if padded > capacity:
                blank = jnp.zeros((padded - capacity, LANES), F32)
                tall_dots = jnp.concatenate([tall_dots, blank], axis=0)
            dgv[p] = tall_dots.T[0:8]

            @pl.when(p > 0)
            def _give(p=p):
                send_dx(p).start()
                send_dg(p).start()

            @pl.when(p == 0)
            def _keep():
                own_dx.start()
                own_dg.start()

            save_y(p).start()
        for s in range(per):
            p = base + s
            part = slice(s * capacity, (s + 1) * capacity)
            gate = gates_v[p].T[0:capacity, 0:1]
            xg[rows_of(p), :] = (x[part].astype(F32) * gate).astype(BF)
            dy[rows_of(p), :] = (g[part].astype(F32) * gate).astype(BF)

    first = shards_n // 2

    def unit(m):
        step = jnp.where(m < 2 * shards_n, lax.rem(m // first, 2), m // shards_n)
        n = m // shards_n * first + lax.rem(m, first)
        n = jnp.where(m < 2 * shards_n, n, lax.rem(m, shards_n))
        return step, n

    def unit_body(m, _):
        step, n = unit(m)
        base = group_at(step) * per
        rows = pl.ds(pl.multiple_of(base * capacity, tall), tall)
        held = aligned(jnp.where(step == 1, tall, 0), tall)

        @pl.when(n == 0)
        def _begin():
            for s in range(per):

                @pl.when(base + s > 0)
                def _arrive(s=s):
                    send_x(base + s).wait_recv()
                    send_gate(base + s).wait_recv()

                load_g(base + s).wait()
            y_acc[held, :] = jnp.zeros((tall, y_acc.shape[1]), F32)
            dx_acc[held, :] = jnp.zeros((tall, y_acc.shape[1]), F32)

        t = n // 2
        beside = lax.rem(n, 2)
        c = lax.rem(pair + far - t, far) * 2 + lax.rem(core + beside, 2)

        @pl.when(m == 1)
        def _beside():
            down_beside.wait_recv()

        @pl.when((step == 0) & (n >= 2) & (beside == 0))
        def _across():
            for k in range(3):
                part_across(t, k).wait_recv()
                part_onward(t, k).start()

        @pl.when((step == 0) & (n >= 2) & (beside == 1))
        def _onward():
            for k in range(3):
                part_onward(t, k).wait_recv()

        x, g = xv[rows, :], gv[rows, :]
        z = mm(x, up_v[c])
        du = mm_nt(g, down_v[c])
        square = z * z
        curve = jnp.tanh(z * (GELU_A + GELU_A * GELU_B * square))
        plus = 0.5 + 0.5 * curve
        hidden = (z * plus).astype(BF)
        rise = GELU_A + 3.0 * GELU_A * GELU_B * square
        slope = plus + 0.5 * z * (1.0 - curve * curve) * rise
        back = (slope * du).astype(BF)
        act[c, rows, :] = hidden
        dz[c, rows, :] = back
        y_acc[held, :] += mm(hidden, down_v[c])
        dx_acc[held, :] += mm_nt(back, up_v[c])

        @pl.when(n == shards_n - 1)
        def _end():
            finish(base, rows, held)

        return 0

    lax.fori_loop(0, steps * shards_n, unit_body, 0)

    total = size * capacity
    turn = 256
    for k in range(total // turn):
        rows = slice(k * turn, (k + 1) * turn)
        xg_t[:, rows] = xg[rows, :].astype(F32).T.astype(BF)
    for t in range(1, far):
        for k in range(3):
            part_across(t, k).wait_send()
            part_onward(t, k).wait_send()
    down_beside.wait_send()

    def give(which, step):
        source = (up_v, down_v)[which].at[lax.rem(pair + step, far) * 2 + 1 - core]
        return remote(
            source,
            dw_box.at[which, step],
            dc_s.at[which, step],
            dc_r.at[which, step],
            {"hidden": mate},
        )

    def keep(which, step):
        source = (up_v, down_v)[which].at[lax.rem(pair + step, far) * 2 + core]
        return pltpu.make_async_copy(source, dw_sum.at[which, step], save_sem.at[which, step])

    def cross(step, k):
        there = lax.rem(pair + step, far) * 2 + core
        return remote(
            up_v.at[there, half(k)],
            dw_far.at[step - 1, half(k)],
            df_s.at[step, k],
            df_r.at[step, k],
            {"hidden": there},
        )

    def gradients(which, left, right, held):
        def other(n, _):
            step = lax.rem(n + 1, far)
            c = lax.rem(pair + step, far) * 2 + 1 - core
            held[c] = mm(left[...], right[c]).astype(BF)
            give(which, step).start()
            return 0

        def own(n, _):
            step = lax.rem(n + 1, far)
            c = lax.rem(pair + step, far) * 2 + core
            total_of = mm(left[...], right[c])
            give(which, step).wait_recv()
            held[c] = (total_of + dw_box[which, step].astype(F32)).astype(BF)
            keep(which, step).start()

            if which == 0:

                @pl.when(step > 0)
                def _cross():
                    for k in range(2):
                        cross(step, k).start()

            return 0

        lax.fori_loop(0, far, other, 0)
        lax.fori_loop(0, far, own, 0)

    gradients(0, xg_t, dz, up_v)
    for k in range(total // turn):
        rows = slice(k * turn, (k + 1) * turn)
        dy_t[:, rows] = dy[rows, :].astype(F32).T.astype(BF)
    gradients(1, dy_t, act, down_v)
    for p in range(1, size):
        send_x(p).wait_send()
        send_gate(p).wait_send()
        send_dx(p).wait()
        send_dg(p).wait()
    for p in range(size):
        save_y(p).wait()
    own_dx.wait()
    own_dg.wait()
    for step in range(far):
        for which in range(2):
            give(which, step).wait_send()
            keep(which, step).wait()
    for step in range(1, far):
        for k in range(2):
            cross(step, k).wait()


def run_experts(x_slots, gate_rows, g_in, ups, w_up, w_down, cid):
    size = lax.axis_size("expert")
    experts, capacity, model = x_slots.shape
    padded = gate_rows.shape[2]
    shards_n, _unused, width = ups.shape
    total = experts * capacity
    per = 1
    while per * 2 * capacity <= 320 and size % (per * 2) == 0:
        per *= 2
    tall = per * capacity
    rows2 = (total, model)
    return pl.pallas_call(
        partial(moe_body, size, capacity, padded, per),
        name="experts",
        out_shape=[
            shape_of(x_slots.shape, BF),
            shape_of(gate_rows.shape, F32),
            shape_of(x_slots.shape, BF),
            shape_of((2, shards_n // 2, model, width), BF),
            shape_of((shards_n // 2 - 1, model, width), BF),
        ],
        in_specs=[ANY] * 6,
        out_specs=[ANY] * 5,
        scratch_shapes=[
            pltpu.VMEM(rows2, BF),
            pltpu.VMEM(rows2, BF),
            pltpu.VMEM(gate_rows.shape, F32),
            pltpu.VMEM((shards_n, model, width), BF),
            pltpu.VMEM((shards_n, width, model), BF),
            pltpu.VMEM((shards_n, total, width), BF),
            pltpu.VMEM((shards_n, total, width), BF),
            pltpu.VMEM(rows2, BF),
            pltpu.VMEM(rows2, BF),
            pltpu.VMEM((model, total), BF),
            pltpu.VMEM((model, total), BF),
            pltpu.VMEM(rows2, BF),
            pltpu.VMEM(rows2, BF),
            pltpu.VMEM(gate_rows.shape, F32),
            pltpu.VMEM((2 * tall, model), F32),
            pltpu.VMEM((2 * tall, model), F32),
            pltpu.VMEM((2, shards_n // 2, model, width), BF),
            DMA((shards_n + 1,)),
            DMA((2, shards_n // 2)),
            DMA((shards_n // 2, 3)),
            DMA((shards_n // 2, 3)),
            DMA,
            DMA,
            DMA((shards_n // 2, 3)),
            DMA((shards_n // 2, 3)),
            DMA((2, shards_n // 2)),
            DMA((2, shards_n // 2)),
            DMA((shards_n // 2, 2)),
            DMA((shards_n // 2, 2)),
            DMA((size,)),
            DMA((4,)),
        ]
        + [DMA((size,))] * 9,
        compiler_params=pltpu.CompilerParams(
            collective_id=cid, has_side_effects=True, vmem_limit_bytes=60 << 20
        ),
        cost_estimate=pl.CostEstimate(
            flops=12 * total * model * width * shards_n, bytes_accessed=40 << 20, transcendentals=0
        ),
    )(x_slots, gate_rows, g_in, ups, w_up, w_down)


def tail_body(
    n_e,
    n_h,
    chunks,
    dh,
    w_all,
    small,
    tokens,
    gain,
    d_res,
    residual,
    gates,
    pos,
    y_back,
    input_grad,
    output,
    full,
    total,
    wv,
    tok_v,
    d_res_v,
    res_v,
    yv,
    mine,
    beside,
    across,
    passing,
    x_box,
    z_box,
    w_mid,
    piece,
    small_mid,
    small_h,
    small_e,
    small_all,
    load_sem,
    mine_sem,
    cs_sem,
    cr_sem,
    as_sem,
    ar_sem,
    ws_sem,
    wr_sem,
    vs_sem,
    vr_sem,
    hs_sem,
    hr_sem,
    es_sem,
    er_sem,
    bs_sem,
    br_sem,
    keep_sem,
    zs_sem,
    zr_sem,
    xs_sem,
    xr_sem,
    ys_sem,
    yr_sem,
    ms_sem,
    mr_sem,
):
    e, h = lax.axis_index("expert"), lax.axis_index("hidden")
    far, high = n_h // 2, n_e // 2
    pair, core = h // 2, lax.rem(h, 2)
    eh, el = e // 2, lax.rem(e, 2)
    mate = pair * 2 + 1 - core
    greet(
        [{"expert": lax.rem(e + step, n_e)} for step in range(1, n_e)]
        + [{"hidden": lax.rem(h + step, n_h)} for step in range(1, n_h)]
    )
    w_sends, w_order = {}, list(range(1, high)) + [0]
    for step in w_order:
        there = lax.rem(eh + step, high)
        copy = remote(
            w_all.at[there * 2 + 1 - el],
            x_box.at[step],
            ws_sem.at[step],
            wr_sem.at[step],
            {"expert": eh * 2 + 1 - el},
        )
        copy.start()
        w_sends[step] = copy
    small_sends = []
    for at in range(n_h - 1):
        peer = lax.rem(h + 1 + at, n_h)
        copy = remote(
            small.at[peer], small_h.at[at], hs_sem.at[at], hr_sem.at[at], {"hidden": peer}
        )
        copy.start()
        small_sends.append(copy)
    rows = dh.shape[1] // chunks
    core_sends = {}
    for step in list(range(1, far)) + [0]:
        there = lax.rem(pair + step, far)
        for k in range(chunks):
            part = pl.ds(k * rows, rows)
            copy = remote(
                dh.at[there * 2 + 1 - core, part],
                beside.at[step, part],
                cs_sem.at[step, k],
                cr_sem.at[step, k],
                {"hidden": mate},
            )
            copy.start()
            core_sends[step, k] = copy
    mine_loads = []
    for step in range(far):
        there = lax.rem(pair + step, far)
        load = pltpu.make_async_copy(dh.at[there * 2 + core], mine.at[step], mine_sem.at[step])
        load.start()
        mine_loads.append(load)
    loads = [
        pltpu.make_async_copy(source, target, load_sem.at[n])
        for n, (source, target) in enumerate(
            ((w_all, wv), (residual, res_v), (y_back, yv), (tokens, tok_v), (d_res, d_res_v))
        )
    ]
    for load in loads:
        load.start()
    for load in mine_loads:
        load.wait()
    far_sends = []
    for step in range(1, far):
        there = lax.rem(pair + step, far)
        for k in range(chunks):
            part = pl.ds(k * rows, rows)
            core_sends[step, k].wait_recv()
            both = mine[step, part, :].astype(F32) + beside[step, part, :].astype(F32)
            passing[step - 1, part, :] = both.astype(BF)
            copy = remote(
                passing.at[step - 1, part],
                across.at[step - 1, part],
                as_sem.at[step - 1, k],
                ar_sem.at[step - 1, k],
                {"hidden": there * 2 + core},
            )
            copy.start()
            far_sends.append(copy)
    loads[0].wait()
    v_sends = []
    for step in w_order[:-1]:
        there = lax.rem(eh + step, high) * 2 + el
        w_sends[step].wait_recv()
        w_mid[step - 1] = (wv[there].astype(F32) + x_box[step].astype(F32)).astype(BF)
        copy = remote(
            w_mid.at[step - 1],
            z_box.at[step - 1],
            vs_sem.at[step],
            vr_sem.at[step],
            {"expert": there},
        )
        copy.start()
        v_sends.append(copy)
    summed = small[h]
    for at, copy in enumerate(small_sends):
        copy.wait_recv()
        summed = summed + small_h[at]
    small_mid[...] = summed
    small_out = []
    for at in range(n_e - 1):
        peer = lax.rem(e + 1 + at, n_e)
        copy = remote(small_mid, small_e.at[at], es_sem.at[at], er_sem.at[at], {"expert": peer})
        copy.start()
        small_out.append(copy)
    w_sends[0].wait_recv()
    acc = wv[e].astype(F32) + x_box[0].astype(F32)
    for at, copy in enumerate(v_sends):
        copy.wait_recv()
        acc = acc + z_box[at].astype(F32)
    piece[...] = acc.astype(BF)
    keep = pltpu.make_async_copy(piece, full.at[h, e], keep_sem)
    keep.start()

    def spot(t, s, flag, core_of):
        eh_of = lax.rem(eh + high - s, high)
        el_of = el if flag == 0 else 1 - el
        return full.at[lax.rem(pair + far - t, far) * 2 + core_of, eh_of * 2 + el_of]

    def held(t, s, flag):
        return piece if (t, s, flag) == (0, 0, 0) else spot(t, s, flag, core)

    def along(t, s):
        there = {"expert": lax.rem(eh + s, high) * 2 + el}
        return remote(held(t, 0, 0), spot(t, 0, 0, core), zs_sem.at[t, s], zr_sem.at[t, s], there)

    def aside(t, s):
        there = {"expert": eh * 2 + 1 - el}
        return remote(held(t, s, 0), spot(t, s, 0, core), xs_sem.at[t, s], xr_sem.at[t, s], there)

    def over(t, s, flag):
        there = {"hidden": lax.rem(pair + t, far) * 2 + core}
        at = 2 * s + flag
        return remote(
            held(0, s, flag), spot(0, s, flag, core), ys_sem.at[t, at], yr_sem.at[t, at], there
        )

    def to_mate(t, s, flag):
        at = 2 * s + flag
        return remote(
            held(t, s, flag),
            spot(t, s, flag, core),
            ms_sem.at[t, at],
            mr_sem.at[t, at],
            {"hidden": mate},
        )

    line_order = list(range(1, high))
    pieces = [(s, flag) for s in range(high) for flag in range(2)]
    first, second = core == 0, core == 1

    @pl.when(first)
    def _spread_first():
        for s in line_order:
            along(0, s).start()
        aside(0, 0).start()
        for t in range(1, far):
            over(t, 0, 0).start()
        to_mate(0, 0, 0).start()

        def take_aside(s):
            aside(0, s).wait_recv()
            for t in range(1, far):
                over(t, s, 1).start()
            to_mate(0, s, 1).start()

        for s in line_order:
            along(0, s).wait_recv()
            aside(0, s).start()
            for t in range(1, far):
                over(t, s, 0).start()
            to_mate(0, s, 0).start()
            take_aside(s - 1)
        take_aside(high - 1)

    @pl.when(second)
    def _spread_second():
        for t in range(1, far):
            over(t, 0, 0).start()
        for s in line_order:
            along(0, s).start()
        aside(0, 0).start()
        to_mate(0, 0, 0).start()
        for t in range(1, far):
            over(t, 0, 0).wait_recv()
            for s in line_order:
                along(t, s).start()
            aside(t, 0).start()
            to_mate(t, 0, 0).start()
        for s in line_order:
            for t in range(far):
                along(t, s).wait_recv()
                aside(t, s).start()
                to_mate(t, s, 0).start()

    summed = small_mid[...]
    for at, copy in enumerate(small_out):
        copy.wait_recv()
        summed = summed + small_e[at]
    small_all[h] = summed
    small_back = []
    for at in range(n_h - 1):
        peer = lax.rem(h + 1 + at, n_h)
        copy = remote(
            small_all.at[h], small_all.at[h], bs_sem.at[at], br_sem.at[at], {"hidden": peer}
        )
        copy.start()
        small_back.append(copy)
    for load in loads[1:]:
        load.wait()
    place_of = iota((residual.shape[0], y_back.shape[0]), 1)
    result = res_v[...]
    for j in range(2):
        pick = (place_of == pos[:, j : j + 1]).astype(BF)
        result = result + gates[:, j : j + 1] * mm(pick, yv[...])
    output[...] = result.astype(BF)
    for k in range(chunks):
        part = pl.ds(k * rows, rows)
        core_sends[0, k].wait_recv()
    for copy in far_sends:
        copy.wait_recv()
    grad = mine[0].astype(F32) + beside[0].astype(F32)
    for step in range(far - 1):
        grad = grad + across[step].astype(F32)
    normed, inverse = norm_parts(tok_v[...].astype(F32))
    input_grad[...] = (d_res_v[...] + norm_back(grad, normed, inverse, lying(gain))).astype(BF)
    @pl.when(first)
    def _finish_first():
        for t in range(1, far):
            for s, flag in pieces:
                over(t, s, flag).wait_recv()
                to_mate(t, s, flag).start()

    @pl.when(second)
    def _finish_second():
        for s in range(high):
            for t in range(far):
                aside(t, s).wait_recv()
                to_mate(t, s, 1).start()

    for copy in small_back:
        copy.wait_recv()
    total[...] = small_all[...]
    for t in range(far):
        for s, flag in pieces:
            to_mate(t, s, flag).wait()
    keep.wait()

    @pl.when(first)
    def _sent_first():
        for s in line_order:
            along(0, s).wait_send()
        for s in range(high):
            aside(0, s).wait_send()
        for t in range(1, far):
            for s, flag in pieces:
                over(t, s, flag).wait_send()

    @pl.when(second)
    def _sent_second():
        for t in range(1, far):
            over(t, 0, 0).wait_send()
        for t in range(far):
            for s in line_order:
                along(t, s).wait_send()
            for s in range(high):
                aside(t, s).wait_send()

    for copy in [*w_sends.values(), *v_sends, *small_sends, *small_out, *small_back, *far_sends]:
        copy.wait_send()
    for copy in core_sends.values():
        copy.wait_send()


def run_tail(dh, w_all, small, tokens, gain, d_res, residual, gates, pos, y_back, cid):
    n_e, n_h = lax.axis_size("expert"), lax.axis_size("hidden")
    far, high = n_h // 2, n_e // 2
    chunks = 4
    _unused, rows, model = dh.shape
    piece = w_all.shape[1:]
    return pl.pallas_call(
        partial(tail_body, n_e, n_h, chunks),
        name="tail",
        out_shape=[
            shape_of((rows, model), BF),
            shape_of((rows, model), BF),
            shape_of((n_h, n_e, *piece), BF),
            shape_of(small.shape, F32),
        ],
        in_specs=[ANY, ANY, VMEM, ANY, VMEM, ANY, ANY, VMEM, VMEM, ANY],
        out_specs=[VMEM, VMEM, ANY, VMEM],
        scratch_shapes=[
            pltpu.VMEM(w_all.shape, BF),
            pltpu.VMEM(tokens.shape, BF),
            pltpu.VMEM(d_res.shape, F32),
            pltpu.VMEM(residual.shape, F32),
            pltpu.VMEM(y_back.shape, BF),
            pltpu.VMEM((far, rows, model), BF),
            pltpu.VMEM((far, rows, model), BF),
            pltpu.VMEM((far - 1, rows, model), BF),
            pltpu.VMEM((far - 1, rows, model), BF),
            pltpu.VMEM((high, *piece), BF),
            pltpu.VMEM((high - 1, *piece), BF),
            pltpu.VMEM((high - 1, *piece), BF),
            pltpu.VMEM(piece, BF),
            pltpu.VMEM(small.shape[1:], F32),
            pltpu.VMEM((n_h - 1, *small.shape[1:]), F32),
            pltpu.VMEM((n_e - 1, *small.shape[1:]), F32),
            pltpu.VMEM(small.shape, F32),
            DMA((5,)),
            DMA((far,)),
            DMA((far, chunks)),
            DMA((far, chunks)),
            DMA((far - 1, chunks)),
            DMA((far - 1, chunks)),
            DMA((high,)),
            DMA((high,)),
            DMA((high,)),
            DMA((high,)),
            DMA((n_h - 1,)),
            DMA((n_h - 1,)),
            DMA((n_e - 1,)),
            DMA((n_e - 1,)),
            DMA((n_h - 1,)),
            DMA((n_h - 1,)),
            DMA,
            DMA((far, high)),
            DMA((far, high)),
            DMA((far, high)),
            DMA((far, high)),
            DMA((far, n_e)),
            DMA((far, n_e)),
            DMA((far, n_e)),
            DMA((far, n_e)),
        ],
        compiler_params=pltpu.CompilerParams(
            collective_id=cid, has_side_effects=True, vmem_limit_bytes=56 << 20
        ),
    )(dh, w_all, small, tokens, gain, d_res, residual, gates, pos, y_back)


def turn_body(
    width,
    experts,
    scale,
    full,
    dw,
    small,
    input_grad,
    output,
    q_out,
    k_out,
    v_out,
    o_out,
    up_out,
    down_out,
    g1_out,
    s1_out,
    g2_out,
    s2_out,
    router_out,
    input_out,
    output_out,
    load_out,
):
    @pl.when(pl.program_id(0) == 0)
    def _begin():
        input_out[...] = input_grad[...]
        output_out[...] = output[...]
        for n, out in enumerate((g1_out, s1_out, g2_out, s2_out)):
            out[...] = small[row_at(small, n)].reshape(out.shape)
        for n in range(experts):
            router_out[n : n + 1, :] = small[row_at(small, 8 + n)]
        load_out[...] = small[row_at(small, 4)][:, 0:experts].reshape(experts) * scale

    for n, out in enumerate((q_out, k_out, v_out)):
        part = full[:, n * width : (n + 1) * width, :].astype(F32)
        out[...] = part.reshape(-1, part.shape[2]).T
    part = full[:, 3 * width :, :].astype(F32)
    o_out[...] = part.reshape(-1, part.shape[2])
    trained = jnp.where(lax.axis_index("expert") >= experts // 2, 1.0, 0.0)
    up_out[...] = dw[0].astype(F32) * trained
    down_out[...] = dw[1].astype(F32).T * trained


def turn_weights(full, dw, small, input_grad, output, width, experts, scale):
    n_h, deep, model = full.shape
    cols = 384
    across = pl.BlockSpec((cols, model), lambda i: (i, 0))
    down = pl.BlockSpec((model, cols), lambda i: (0, i))
    flat = pl.BlockSpec((model,), lambda i: (0,))
    whole = pl.BlockSpec(output.shape, lambda i: (0, 0))
    square = shape_of((model, model), F32)
    return pl.pallas_call(
        partial(turn_body, width, experts, scale),
        name="turn_weights",
        grid=(model // cols,),
        out_shape=[square] * 6
        + [shape_of((model,), F32)] * 4
        + [
            shape_of((experts, model), F32),
            shape_of(input_grad.shape, BF),
            shape_of(output.shape, BF),
            shape_of((experts,), F32),
        ],
        in_specs=[
            pl.BlockSpec((n_h, deep, cols), lambda i: (0, 0, i)),
            pl.BlockSpec((2, model, cols), lambda i: (0, 0, i)),
            pl.BlockSpec(small.shape, lambda i: (0, 0, 0)),
            whole,
            whole,
        ],
        out_specs=[across, across, across, down, down, across]
        + [flat] * 4
        + [pl.BlockSpec((experts, model), lambda i: (0, 0)), whole, whole]
        + [pl.BlockSpec((experts,), lambda i: (0,))],
        compiler_params=pltpu.CompilerParams(
            dimension_semantics=("arbitrary",), vmem_limit_bytes=60 << 20
        ),
        cost_estimate=pl.CostEstimate(flops=0, bytes_accessed=24 << 20, transcendentals=0),
    )(full, dw, small, input_grad, output)


def attend_back(
    heads, i, span, first, qkv, given, centre, kept, values, dq_acc, dk_acc, dv_acc
):
    width = heads * HEAD_DIM
    rows = aligned(i * BLOCK, BLOCK)
    dq_acc[...] = jnp.zeros_like(dq_acc)
    queries = [
        qkv[n * HEAD_DIM : (n + 1) * HEAD_DIM, rows] * jnp.asarray(SCALE, BF) for n in range(heads)
    ]
    for k in range(span):
        part = aligned((first + k) * BLOCK, BLOCK)
        for n in range(heads):
            here = slice(n * HEAD_DIM, (n + 1) * HEAD_DIM)
            weight = kept[n, k]
            d_weight = mm(values[n, part, :], given[n])
            d_score = (weight.astype(F32) * (d_weight - centre[n])).astype(BF)
            dv_acc[here, part] += mm_nt(given[n], weight)
            dk_acc[here, part] += mm_nt(queries[n], d_score)
            lo = width + n * HEAD_DIM
            dq_acc[here, :] += mm(qkv[lo : lo + HEAD_DIM, part], d_score)


def back_body(
    n_e,
    n_h,
    experts,
    capacity,
    padded,
    heads,
    ids,
    slot,
    pos,
    gates,
    count,
    g1,
    s1,
    g2,
    s2,
    w_router,
    inverse,
    dg_rows,
    dx_back,
    y_out,
    dw_sum,
    dw_far,
    out_grad,
    residual,
    all_tokens,
    qkv_in,
    att_in,
    att_t_in,
    w_out,
    w_t_in,
    weights,
    y_back,
    d_hidden,
    d_res,
    w_all,
    small,
    dw_own,
    dxv,
    gv,
    res_v,
    tv,
    qkv,
    att_v,
    att_t,
    wo,
    w_t,
    d_att_v,
    d_att,
    wo_box,
    wo_far,
    kept,
    values,
    dq_acc,
    dk_acc,
    dv_acc,
    d_qkv,
    w_acc,
    dw_mine,
    dw_across,
    load_sem,
    save_sem,
    dw_sem,
    kept_sem,
    y_own,
    y_s,
    y_r,
    at_s,
    at_r,
    wo_s,
    wo_r,
    wf_s,
    wf_r,
    da_s,
    da_r,
):
    e, h = lax.axis_index("expert"), lax.axis_index("hidden")
    far = n_h // 2
    pair, core = h // 2, lax.rem(h, 2)
    mate = pair * 2 + 1 - core
    rows, model = out_grad.shape
    width = heads * HEAD_DIM
    group = rows * n_h
    per_device = rows // BLOCK
    blocks = group // BLOCK
    sends = []

    loads = [
        pltpu.make_async_copy(source, target, load_sem.at[n])
        for n, (source, target) in enumerate(
            (
                (residual, res_v),
                (dx_back, dxv),
                (out_grad, gv),
                (w_out, wo),
                (att_t_in, att_t),
                (qkv_in, qkv),
                (att_in, att_v),
                (all_tokens, tv),
                (w_t_in, w_t),
            )
        )
    ]
    for load in loads:
        load.start()
    greet(
        [{"hidden": lax.rem(h + step, n_h)} for step in range(1, n_h)]
        + [{"expert": lax.rem(e + step, n_e)} for step in range(1, n_e)]
    )
    load_dw = pltpu.make_async_copy(dw_sum.at[:, 0], dw_mine, dw_sem.at[0])
    load_dw.start()
    deep = dw_mine.shape[1] // 2
    load_far = pltpu.make_async_copy(
        dw_far, dw_across.at[0], dw_sem.at[1]
    )
    load_far.start()

    def dw_across_copy(step, k):
        part = pl.ds(k * deep, deep)
        return remote(
            dw_sum.at[1, step, part],
            dw_across.at[1, step - 1, part],
            da_s.at[step, k],
            da_r.at[step, k],
            {"hidden": lax.rem(pair + step, far) * 2 + core},
        )

    def dw_send(k):
        for step in range(1, far):
            dw_across_copy(step, k).start()

    dw_send(0)
    for step in range(1, n_e):
        peer = lax.rem(e + step, n_e)
        copy = remote(y_out.at[peer], y_back.at[e], y_s.at[step], y_r.at[step], {"expert": peer})
        copy.start()
        sends.append(copy)
    own_y = pltpu.make_async_copy(y_out.at[e], y_back.at[e], y_own)
    own_y.start()

    for load in loads[:3]:
        load.wait()
    normed, spread = norm_parts(res_v[...])
    hidden = (normed * lying(g2) + lying(s2)).astype(BF)
    gate = [gates[:, j : j + 1] for j in range(2)]
    column = iota((rows, padded), 1)
    dot_of = []
    for j in range(2):
        mix = jnp.zeros((rows, padded), F32)
        for n in range(experts):
            here = jnp.where(ids[:, j : j + 1] == n, slot[:, j : j + 1], -1) == column
            mix = jnp.where(here, dg_rows[n, 0:1, :], mix)
        dot_of.append(jnp.sum(mix, axis=1, keepdims=True))
    mean = gate[0] * dot_of[0] + gate[1] * dot_of[1]
    lane = iota((rows, experts), 1)
    d_logits = jnp.zeros((rows, experts), F32)
    for j in range(2):
        d_logits = jnp.where(lane == ids[:, j : j + 1], gate[j] * (dot_of[j] - mean), d_logits)
    high, low = split_two(d_logits)
    grad = mm(high, w_router[...]) + mm(low, w_router[...])
    small[...] = jnp.zeros_like(small)
    for_router = mm_tn(high, hidden) + mm_tn(low, hidden)
    for n in range(experts):
        small[row_at(small, 8 + n)] = for_router[n : n + 1]
    place, line = row_at(small, 4)
    small[place, line, 0:LANES] = count[...]
    place = iota((rows, experts * capacity), 1)
    for j in range(2):
        pick = (place == pos[:, j : j + 1]).astype(BF)
        grad = grad + gate[j] * mm(pick, dxv[...])
    small[row_at(small, 2)] = jnp.sum(grad * normed, axis=0, keepdims=True)
    small[row_at(small, 3)] = jnp.sum(grad, axis=0, keepdims=True)
    d_resid = gv[...].astype(F32) + norm_back(grad, normed, spread, lying(g2))
    d_res[...] = d_resid
    branch = d_resid.astype(BF)
    loads[3].wait()

    def device_at(n, sign):
        t, other = n // 2, lax.rem(n, 2)
        return lax.rem(pair + far + sign * t, far) * 2 + lax.rem(core + other, 2)

    def give_att(n):
        owner = device_at(n, 1)
        return remote(
            d_att_v.at[owner], d_att.at[h], at_s.at[n], at_r.at[n], {"hidden": owner}
        )

    for n in range(n_h - 1, -1, -1):
        owner = device_at(n, 1)
        block = mm_nt(wo[owner], branch).astype(BF)
        if n == 0:
            d_att[h] = block
        else:
            d_att_v[owner] = block
            give_att(n).start()
    loads[4].wait()
    for t in range(n_h):
        owner = lax.rem(h + t, n_h)
        wo[owner] = mm(att_t[owner], branch).astype(BF)
    for step in list(range(1, far)) + [0]:
        copy = remote(
            wo.at[lax.rem(pair + step, far) * 2 + 1 - core],
            wo_box.at[step],
            wo_s.at[step],
            wo_r.at[step],
            {"hidden": mate},
        )
        copy.start()
        sends.append(copy)
    def give_wo(step):
        target = lax.rem(pair + step, far) * 2 + core
        return remote(
            wo.at[target],
            wo_far.at[step - 1],
            wf_s.at[step],
            wf_r.at[step],
            {"hidden": target},
        )

    for load in loads[5:]:
        load.wait()

    def load_kept(i, turn):
        return pltpu.make_async_copy(weights.at[i], kept.at[turn], kept_sem.at[turn])

    def block_at(at):
        owner = device_at(at // per_device, 1)
        return owner, owner * per_device + lax.rem(at, per_device)

    load_kept(block_at(0)[1], 0).start()
    dk_acc[...] = jnp.zeros_like(dk_acc)
    dv_acc[...] = jnp.zeros_like(dv_acc)

    def turn_values(i, _):
        cols = aligned(i * BLOCK, BLOCK)
        for n in range(heads):
            lo = 2 * width + n * HEAD_DIM
            values[n, cols, :] = qkv[lo : lo + HEAD_DIM, cols].astype(F32).T.astype(BF)
        return 0

    lax.fori_loop(0, blocks, turn_values, 0)

    def over_queries(at, _):
        owner, i = block_at(at)
        turn = lax.rem(at, 2)

        @pl.when(at + 1 < blocks)
        def _next():
            load_kept(block_at(at + 1)[1], 1 - turn).start()

        @pl.when((at >= per_device) & (lax.rem(at, per_device) == 0))
        def _arrive():
            n = at // per_device
            source = lax.rem(far - n // 2, far) * 2 + lax.rem(n, 2)
            give_att(source).wait_recv()

        @pl.when(at == per_device)
        def _weights():
            for step in range(1, far):
                there = wo_box.at[step]
                target = lax.rem(pair + step, far) * 2 + core
                remote(there, there, wo_s.at[step], wo_r.at[step], {"hidden": mate}).wait_recv()
                both = wo[target].astype(F32) + wo_box[step].astype(F32)
                wo[target] = both.astype(BF)
                give_wo(step).start()
            dw_send(1)

        load_kept(i, turn).wait()
        cols = aligned(lax.rem(at, per_device) * BLOCK, BLOCK)
        rows_i = aligned(i * BLOCK, BLOCK)
        given, centre = [], []
        for n in range(heads):
            here = slice(n * HEAD_DIM, (n + 1) * HEAD_DIM)
            scaled = d_att[owner, here, cols].astype(F32) * inverse[n : n + 1, rows_i]
            given.append(scaled.astype(BF))
            product = att_v[owner, here, cols].astype(F32) * scaled
            centre.append(jnp.sum(product, axis=0, keepdims=True))

        def block(span, first):
            attend_back(
                heads,
                i,
                span,
                first,
                qkv,
                given,
                centre,
                kept.at[turn],
                values,
                dq_acc,
                dk_acc,
                dv_acc,
            )

        spans(i, block)
        d_qkv[0:width, rows_i] = (dq_acc[...] * SCALE).astype(BF)
        return 0

    lax.fori_loop(0, blocks, over_queries, 0)
    w_acc[...] = jnp.zeros_like(w_acc)

    def finish(i, _):
        cols = aligned(i * BLOCK, BLOCK)
        d_qkv[width : 2 * width, cols] = dk_acc[:, cols].astype(BF)
        d_qkv[2 * width :, cols] = dv_acc[:, cols].astype(BF)
        block = d_qkv[:, cols]
        grad = mm_tn(block, w_t[...])
        inner = aligned(lax.rem(i, per_device) * BLOCK, BLOCK)
        normed, _unused = norm_parts(tv[i // per_device, inner, :].astype(F32))
        tv[i // per_device, inner, :] = grad.astype(BF)
        small[row_at(small, 0)] += jnp.sum(grad * normed, axis=0, keepdims=True)
        small[row_at(small, 1)] += jnp.sum(grad, axis=0, keepdims=True)
        hidden = (normed * lying(g1) + lying(s1)).astype(BF)
        w_acc[...] += mm(block, hidden)
        return 0

    lax.fori_loop(0, blocks, finish, 0)
    save_dh = pltpu.make_async_copy(tv, d_hidden, save_sem)
    save_dh.start()
    w_all[0 : 3 * width, :] = w_acc[...].astype(BF)
    there = wo_box.at[0]
    remote(there, there, wo_s.at[0], wo_r.at[0], {"hidden": mate}).wait_recv()
    total = wo[h].astype(F32) + wo_box[0].astype(F32)
    for step in range(1, far):
        give_wo(step).wait_recv()
        total = total + wo_far[step - 1].astype(F32)
    w_all[3 * width :, :] = total.astype(BF)
    load_dw.wait()
    load_far.wait()
    for which in range(2):
        for step in range(1, far if which == 1 else 1):
            for k in range(2):
                dw_across_copy(step, k).wait()

        def add_all(n, _, which=which):
            band = aligned(n * 96, 96)
            both = dw_mine[which, band, :].astype(F32)
            for step in range(1, far):
                both = both + dw_across[which, step - 1, band, :].astype(F32)
            dw_own[which, band, :] = both.astype(BF)
            return 0

        lax.fori_loop(0, dw_mine.shape[1] // 96, add_all, 0)
    for step in range(1, n_e):
        there = y_back.at[lax.rem(e + n_e - step, n_e)]
        remote(there, there, y_s.at[step], y_r.at[step], {"expert": e}).wait_recv()
    own_y.wait()
    save_dh.wait()
    for n in range(1, n_h):
        give_att(n).wait_send()
    for step in range(1, far):
        give_wo(step).wait_send()
    for copy in sends:
        copy.wait_send()


def run_back(
    ids,
    slot,
    pos,
    gates,
    count,
    g1,
    s1,
    g2,
    s2,
    w_router,
    inverse,
    dg_rows,
    dx_back,
    y_out,
    dw_sum,
    dw_far,
    out_grad,
    residual,
    all_tokens,
    qkv,
    att,
    att_t,
    w_out,
    w_t,
    weights,
    cid,
):
    n_e, n_h = lax.axis_size("expert"), lax.axis_size("hidden")
    experts, capacity, model = y_out.shape
    padded = dg_rows.shape[2]
    rows = out_grad.shape[0]
    width = w_t.shape[0] // 3
    heads = width // HEAD_DIM
    group, far = rows * n_h, n_h // 2
    shard = dw_sum.shape[2:]
    tall = 8 + experts

    def pairs(*shape):
        return [DMA(shape), DMA(shape)]

    return pl.pallas_call(
        partial(back_body, n_e, n_h, experts, capacity, padded, heads),
        name="back",
        out_shape=[
            shape_of(y_out.shape, BF),
            shape_of((n_h, rows, model), BF),
            shape_of((rows, model), F32),
            shape_of((4 * width, model), BF),
            shape_of((n_h, tall // n_h, model), F32),
            shape_of((2, *shard), BF),
        ],
        in_specs=[VMEM] * 12 + [ANY] * 13,
        out_specs=[ANY] * 2 + [VMEM] * 4,
        scratch_shapes=[
            pltpu.VMEM((experts * capacity, model), BF),
            pltpu.VMEM((rows, model), BF),
            pltpu.VMEM((rows, model), F32),
            pltpu.VMEM((n_h, rows, model), BF),
            pltpu.VMEM((3 * width, group), BF),
            pltpu.VMEM((n_h, width, rows), BF),
            pltpu.VMEM((n_h, width, rows), BF),
            pltpu.VMEM((n_h, width, model), BF),
            pltpu.VMEM((3 * width, model), BF),
            pltpu.VMEM((n_h, width, rows), BF),
            pltpu.VMEM((n_h, width, rows), BF),
            pltpu.VMEM((far, width, model), BF),
            pltpu.VMEM((far - 1, width, model), BF),
            pltpu.VMEM((2, heads, REACH, BLOCK, BLOCK), BF),
            pltpu.VMEM((heads, group, HEAD_DIM), BF),
            pltpu.VMEM((width, BLOCK), F32),
            pltpu.VMEM((width, group), F32),
            pltpu.VMEM((width, group), F32),
            pltpu.VMEM((3 * width, group), BF),
            pltpu.VMEM((3 * width, model), F32),
            pltpu.VMEM((2, *shard), BF),
            pltpu.VMEM((2, far - 1, *shard), BF),
            DMA((9,)),
            DMA,
            DMA((2,)),
            DMA((2,)),
            DMA,
            *pairs(n_e),
            *pairs(n_h),
            *pairs(far),
            *pairs(far),
            *pairs(far, 2),
        ],
        compiler_params=pltpu.CompilerParams(
            collective_id=cid, has_side_effects=True, vmem_limit_bytes=60 << 20
        ),
    )(
        ids,
        slot,
        pos,
        gates,
        count,
        g1,
        s1,
        g2,
        s2,
        w_router,
        inverse,
        dg_rows,
        dx_back.reshape(experts * capacity, model),
        y_out,
        dw_sum,
        dw_far,
        out_grad,
        residual,
        all_tokens,
        qkv,
        att,
        att_t,
        w_out.reshape(n_h, width, model),
        w_t,
        weights,
    )


def shards(
    tokens,
    doc_lengths,
    expert_ids,
    gain_one,
    shift_one,
    w_query,
    w_key,
    w_value,
    w_out,
    gain_two,
    shift_two,
    w_router,
    w_up,
    w_down,
    out_grad,
):
    rows, model = tokens.shape
    n_expert, n_hidden = lax.axis_size("expert"), lax.axis_size("hidden")
    experts = n_expert * w_up.shape[0]
    capacity = max(2, rows * 2 * 5 // (4 * experts))
    capacity = -(-capacity // 16) * 16
    total = experts * capacity
    heads = HEADS // n_hidden
    width = heads * HEAD_DIM
    g1, s1, g2, s2 = gain_one, shift_one, gain_two, shift_two
    router_t = w_router.T

    (
        all_tokens,
        qkv,
        att,
        att_t,
        w_t,
        g_in,
        x_slots,
        ups,
        weights,
        ids,
        pos,
        slot,
        count,
        inverse,
        residual,
        gates,
        gate_rows,
    ) = run_front(
        doc_lengths,
        expert_ids.T,
        g1,
        s1,
        g2,
        s2,
        router_t,
        tokens,
        out_grad,
        (w_query, w_key, w_value, w_out),
        w_up,
        capacity,
        heads,
        1,
    )
    dx_back, dg_back, y_out, dw_sum, dw_far = run_experts(
        x_slots, gate_rows, g_in, ups, w_up, w_down, 2
    )
    y_back, d_hidden, d_res, w_all, small, dw_own = run_back(
        ids,
        slot,
        pos,
        gates,
        count,
        g1,
        s1,
        g2,
        s2,
        router_t,
        inverse,
        dg_back,
        dx_back,
        y_out,
        dw_sum,
        dw_far,
        out_grad,
        residual,
        all_tokens,
        qkv,
        att,
        att_t,
        w_out,
        w_t,
        weights,
        3,
    )
    input_grad, output, full, small = run_tail(
        d_hidden,
        w_all.reshape(n_expert, 4 * width // n_expert, model),
        small,
        tokens,
        g1,
        d_res,
        residual,
        gates,
        pos,
        y_back.reshape(total, model),
        4,
    )
    scale = experts / (rows * n_expert * n_hidden * 2)
    turned = turn_weights(
        full.reshape(n_hidden, 4 * width, model),
        dw_own,
        small,
        input_grad,
        output,
        width,
        experts,
        scale,
    )
    w_grads, (up_grad, down_grad) = turned[:4], turned[4:6]
    gain_one_grad, shift_one_grad, gain_two_grad, shift_two_grad = turned[6:10]
    router_grad, input_grad, output, load = turned[10:]
    return (
        output,
        input_grad,
        gain_one_grad,
        shift_one_grad,
        *w_grads,
        gain_two_grad,
        shift_two_grad,
        router_grad.T,
        up_grad[None],
        down_grad[None],
        load,
    )


def solution(mesh):
    in_specs = (
        P(("expert", "hidden"), None),
        P("expert", None),
        P(("expert", "hidden"), None),
        P(),
        P(),
        P(),
        P(),
        P(),
        P(),
        P(),
        P(),
        P(),
        P("expert", None, "hidden"),
        P("expert", "hidden", None),
        P(("expert", "hidden"), None),
    )
    out_specs = (
        P(("expert", "hidden"), None),
        P(("expert", "hidden"), None),
        P(),
        P(),
        P(),
        P(),
        P(),
        P(),
        P(),
        P(),
        P(),
        P("expert", None, "hidden"),
        P("expert", "hidden", None),
        P(),
    )
    return jax.shard_map(shards, mesh=mesh, in_specs=in_specs, out_specs=out_specs, check_vma=False)
```

```python
from functools import partial

import jax
import jax.numpy as jnp
from jax import lax
from jax.experimental import pallas as pl
from jax.experimental.pallas import tpu as pltpu
from jax.sharding import PartitionSpec as P

HEAD_DIM = 64
HEADS = 12
EPSILON = 1e-05
SCALE = 0.125
MASKED = -1e30
BLOCK = 256
LONGEST = 1024
REACH = LONGEST // BLOCK + 1
UP_FIRST = 4
UP_EARLY = 6
UP_CROSS = 7
LANES = 128
BF = jnp.bfloat16
F32 = jnp.float32
I32 = jnp.int32
MESH = pl.DeviceIdType.MESH
ANY = pl.BlockSpec(memory_space=pl.ANY)
SMEM = pl.BlockSpec(memory_space=pltpu.SMEM)
VMEM = pl.BlockSpec(memory_space=pltpu.VMEM)
DMA = pltpu.SemaphoreType.DMA
GELU_A = 0.7978845608028654
GELU_B = 0.044715


def mm(left, right):
    return jnp.dot(left, right, preferred_element_type=F32)


def mm_nt(left, right):
    return lax.dot_general(left, right, (((1,), (1,)), ((), ())), preferred_element_type=F32)


def mm_tn(left, right):
    return lax.dot_general(left, right, (((0,), (0,)), ((), ())), preferred_element_type=F32)


def iota(shape, axis):
    return lax.broadcasted_iota(I32, shape, axis)


def norm_parts(values):
    centred = values - jnp.mean(values, axis=-1, keepdims=True)
    inverse = lax.rsqrt(jnp.mean(centred * centred, axis=-1, keepdims=True) + EPSILON)
    return centred * inverse, inverse


def norm_back(grad_out, normed, inverse, gain):
    grad_normed = grad_out * gain
    first = jnp.mean(grad_normed, axis=-1, keepdims=True)
    second = jnp.mean(grad_normed * normed, axis=-1, keepdims=True)
    return inverse * (grad_normed - first - normed * second)


def split_two(value):
    high = value.astype(BF)
    return high, (value - high.astype(F32)).astype(BF)


def row_at(ref, row):
    share = ref.shape[1]
    return row // share, slice(row % share, row % share + 1)


def shape_of(shape, dtype):
    return jax.ShapeDtypeStruct(shape, dtype)


def greet(peers):
    barrier = pltpu.get_barrier_semaphore()
    for peer in peers:
        pl.semaphore_signal(barrier, inc=1, device_id=peer, device_id_type=MESH)
    pl.semaphore_wait(barrier, len(peers))


def remote(src, dst, send, recv, peer):
    return pltpu.make_async_remote_copy(
        src_ref=src, dst_ref=dst, send_sem=send, recv_sem=recv, device_id=peer, device_id_type=MESH
    )


def doc_bounds(docs):
    ends, at = [], 0
    for n in range(docs.shape[1] - 1):
        at = at + docs[0, n]
        ends.append(at)
    return ends


def start_of(place, ends):
    begin = jnp.zeros_like(place)
    for end in ends:
        begin = jnp.where(place >= end, end, begin)
    return begin


def lying(ref):
    return ref[...].reshape(1, ref.shape[0])


def aligned(at, size):
    return pl.ds(pl.multiple_of(at, size), size)


def find_slots(experts, capacity, ids, ids_t, pos, slot, count):
    rows = ids_t.shape[1]
    row = [ids_t[j : j + 1, :] for j in range(2)]
    tall = jnp.concatenate([r.astype(F32) for r in row] + [jnp.zeros((6, rows), F32)], axis=0)
    ids[...] = tall.T[:, 0:2].astype(I32)
    col = [ids[:, j : j + 1] for j in range(2)]
    lane = iota((rows, LANES), 1)
    hot = [(lane == c).astype(BF) for c in col]
    either = hot[0] + hot[1]
    below = (iota((rows, rows), 0) > iota((rows, rows), 1)).astype(BF)
    before = mm(below, either)
    wide = max(experts, 16)
    deep = iota((wide, rows), 0)
    hot_t = [(deep == r).astype(BF) for r in row]
    above = (iota((rows, rows), 0) < iota((rows, rows), 1)).astype(BF)
    before_t = mm(hot_t[0] + hot_t[1], above)
    count[...] = jnp.sum(either.astype(F32), axis=0, keepdims=True)
    flat_t = []
    for j in range(2):
        at = jnp.sum(hot[j].astype(F32) * before, axis=1, keepdims=True).astype(I32)
        pos[:, j : j + 1] = col[j] * capacity + at
        slot[:, j : j + 1] = at
        at_t = jnp.sum(hot_t[j].astype(F32) * before_t, axis=0, keepdims=True).astype(I32)
        flat_t.append(row[j] * capacity + at_t)
    return flat_t


def fill_slots(flat_t, source, out):
    total, rows = out.shape[0], source.shape[0]
    half = total // 2
    for n in range(2):
        place = iota((half, rows), 0) + n * half
        pick = ((place == flat_t[0]) | (place == flat_t[1])).astype(BF)
        out[pl.ds(n * half, half), :] = mm(pick, source).astype(BF)


def attend_block(heads, ends, i, span, first, qkv, keys, scores, kept, inverse):
    width = heads * HEAD_DIM
    base = i * BLOCK
    rows = aligned(base, BLOCK)
    q_pos = base + iota((1, BLOCK), 1)
    begin = start_of(q_pos, ends)
    queries = [
        qkv[n * HEAD_DIM : (n + 1) * HEAD_DIM, rows] * jnp.asarray(SCALE, BF) for n in range(heads)
    ]
    tops = [jnp.full((1, BLOCK), MASKED, F32)] * heads
    for k in range(span):
        part = aligned((first + k) * BLOCK, BLOCK)
        k_pos = (first + k) * BLOCK + iota((BLOCK, BLOCK), 0)
        allowed = (k_pos <= q_pos) & (k_pos >= begin)
        for n in range(heads):
            score = jnp.where(allowed, mm(keys[n, part, :], queries[n]), MASKED)
            scores[n, k] = score
            tops[n] = jnp.maximum(tops[n], jnp.max(score, axis=0, keepdims=True))
    result = []
    for n in range(heads):
        total = jnp.zeros((1, BLOCK), F32)
        acc = jnp.zeros((HEAD_DIM, BLOCK), F32)
        lo = 2 * width + n * HEAD_DIM
        for k in range(span):
            weight = jnp.exp(scores[n, k] - tops[n])
            total = total + jnp.sum(weight, axis=0, keepdims=True)
            value = qkv[lo : lo + HEAD_DIM, aligned((first + k) * BLOCK, BLOCK)]
            low = weight.astype(BF)
            kept[n, k] = low
            acc = acc + mm(value, low)
        whole = 1.0 / total
        inverse[n : n + 1, rows] = whole
        result.append((acc * whole).astype(BF))
    return result


def spans(i, body):
    @pl.when(i < 2)
    def _short():
        body(2, 0)

    @pl.when(i >= 2)
    def _long():
        body(REACH, (i - (REACH - 1)) * (i // (REACH - 1)))


def front_body(
    n_e,
    n_h,
    experts,
    capacity,
    padded,
    heads,
    chunks,
    docs,
    ids_t,
    g1,
    s1,
    g2,
    s2,
    w_router,
    tokens,
    out_grad,
    w_query,
    w_key,
    w_value,
    w_out,
    w_up,
    all_tokens,
    qkv_out,
    att_out,
    att_t_out,
    w_t_out,
    g_in,
    x_slots,
    ups,
    weights,
    ids,
    pos,
    slot,
    count,
    inverse,
    residual,
    gates,
    gate_rows,
    tv,
    gv,
    wv,
    wo,
    w_t,
    qkv,
    keys,
    scores,
    kept,
    att_v,
    att_in,
    g_slots,
    xs_v,
    own_sem,
    w_sem,
    save_sem,
    kept_sem,
    ty_s,
    ty_r,
    tc_s,
    tc_r,
    tf_s,
    tf_r,
    gs_s,
    gs_r,
    at_s,
    at_r,
    wy_s,
    wy_r,
    wc_s,
    wc_r,
    wf_s,
    wf_r,
):
    e, h = lax.axis_index("expert"), lax.axis_index("hidden")
    far = n_h // 2
    pair, core = h // 2, lax.rem(h, 2)
    mate = pair * 2 + 1 - core
    rows, model = tokens.shape
    width = heads * HEAD_DIM
    per_device = rows // BLOCK
    ends = doc_bounds(docs)

    def across(t):
        return lax.rem(pair + t, far) * 2 + core

    def origin(t):
        return lax.rem(pair + far - t, far) * 2 + core

    own_tokens = pltpu.make_async_copy(tokens, tv.at[h], own_sem.at[0])
    own_grad = pltpu.make_async_copy(out_grad, gv, own_sem.at[1])
    own_grad.start()
    own_tokens.start()
    w_loads = [
        pltpu.make_async_copy(w, wv.at[n], w_sem.at[n])
        for n, w in enumerate((w_query, w_key, w_value))
    ]
    w_loads.append(pltpu.make_async_copy(w_out, wo, w_sem.at[3]))
    for load in w_loads:
        load.start()
    greet(
        [{"hidden": lax.rem(h + step, n_h)} for step in range(1, n_h)]
        + [{"expert": lax.rem(e + step, n_e)} for step in range(1, n_e)]
    )

    piece = rows // chunks
    sends = []
    for k in range(chunks):
        part = pl.ds(k * piece, piece)
        for t in range(1, far):
            copy = remote(
                tokens.at[part],
                tv.at[h, part],
                ty_s.at[t, k],
                ty_r.at[t, k],
                {"hidden": across(t)},
            )
            copy.start()
            sends.append(copy)
    beside = remote(tokens, tv.at[h], tc_s, tc_r, {"hidden": mate})
    beside.start()
    sends.append(beside)

    flat_t = find_slots(experts, capacity, ids, ids_t, pos, slot, count)
    own_grad.wait()
    fill_slots(flat_t, gv[...], g_slots)
    for step in range(1, n_e):
        peer = lax.rem(e + step, n_e)
        copy = remote(
            g_slots.at[aligned(peer * capacity, capacity)],
            g_in.at[e],
            gs_s.at[step],
            gs_r.at[step],
            {"expert": peer},
        )
        copy.start()
        sends.append(copy)
    own_slots = pltpu.make_async_copy(
        g_slots.at[aligned(e * capacity, capacity)], g_in.at[e], own_sem.at[1]
    )
    own_slots.start()

    def pass_on(t, k):
        part = pl.ds(k * piece, piece)
        place = tv.at[origin(t), part]
        remote(place, place, ty_s.at[t, k], ty_r.at[t, k], {"hidden": across(t)}).wait_recv()
        copy = remote(place, place, tf_s.at[t, k], tf_r.at[t, k], {"hidden": mate})
        copy.start()
        sends.append(copy)

    todo = [(t, k) for k in range(chunks) for t in range(1, far)]
    third = -(-len(todo) // 4)

    def pass_some():
        for _ in range(min(third, len(todo))):
            pass_on(*todo.pop(0))

    pick = (iota((width, model), 1) == iota((width, model), 0) + h * width).astype(BF)
    for n in range(3):
        w_loads[n].wait()
        w_t[n * width : (n + 1) * width, :] = mm_nt(pick, wv[n]).astype(BF)
        if n == 1:
            pass_some()
    save_w = pltpu.make_async_copy(w_t, w_t_out, save_sem.at[0])
    save_w.start()

    def project(source):
        def one(b, _):
            normed, _unused = norm_parts(tv[source, aligned(b * BLOCK, BLOCK), :].astype(F32))
            hidden = (normed * lying(g1) + lying(s1)).astype(BF)
            block = mm_nt(w_t[...], hidden)
            cols = aligned(source * rows + b * BLOCK, BLOCK)
            qkv[:, cols] = block.astype(BF)
            for n in range(heads):
                lo = width + n * HEAD_DIM
                keys[n, cols, :] = block[lo : lo + HEAD_DIM].T.astype(BF)
            return 0

        lax.fori_loop(0, per_device, one, 0)

    pass_some()
    own_tokens.wait()
    project(h)
    pass_some()
    remote(tokens, tv.at[mate], tc_s, tc_r, {"hidden": mate}).wait_recv()
    project(mate)
    while todo:
        pass_some()

    eighth = w_up.shape[1] // 8
    up_parts = (
        pl.ds(0, UP_FIRST * eighth),
        pl.ds(UP_FIRST * eighth, (UP_EARLY - UP_FIRST) * eighth),
    )

    def up_copy(t, k, source):
        return remote(
            w_up.at[0, up_parts[k]],
            ups.at[source, up_parts[k]],
            wy_s.at[t, k],
            wy_r.at[t, k],
            {"hidden": across(t)},
        )

    def up_onward(t, k):
        place = ups.at[origin(t), up_parts[k]]
        return remote(place, place, wf_s.at[t, k], wf_r.at[t, k], {"hidden": mate})

    def up_arrived(k):
        for t in range(1, far):
            up_copy(t, k, origin(t)).wait_recv()
            up_onward(t, k).start()

    up_beside = remote(w_up.at[0], ups.at[h], wc_s, wc_r, {"hidden": mate})
    up_beside.start()
    sends.append(up_beside)
    for t in range(1, far):
        up_copy(t, 0, h).start()
    for t in range(1, far):
        project(origin(t))
    for t in range(1, far):
        there = lax.rem(pair + far - t, far) * 2 + 1 - core
        for k in range(chunks):
            place = tv.at[there, pl.ds(k * piece, piece)]
            remote(place, place, tf_s.at[t, k], tf_r.at[t, k], {"hidden": mate}).wait_recv()
        project(there)
    save_tokens = pltpu.make_async_copy(tv, all_tokens, save_sem.at[1])
    save_qkv = pltpu.make_async_copy(qkv, qkv_out, save_sem.at[2])
    save_tokens.start()
    save_qkv.start()

    inverse[...] = jnp.zeros_like(inverse)

    def device_at(n, sign):
        t, other = n // 2, lax.rem(n, 2)
        return lax.rem(pair + far + sign * t, far) * 2 + lax.rem(core + other, 2)

    def give_att(n):
        owner = device_at(n, 1)
        return remote(
            att_v.at[owner], att_in.at[h], at_s.at[n], at_r.at[n], {"hidden": owner}
        )

    def save_kept(i, turn):
        return pltpu.make_async_copy(kept.at[turn], weights.at[i], kept_sem.at[turn])

    def attend(at, _):
        n = n_h - 1 - at // per_device
        b = lax.rem(at, per_device)
        owner = device_at(n, 1)
        i = owner * per_device + b
        turn = lax.rem(at, 2)

        @pl.when(at >= 2)
        def _free():
            save_kept(i, turn).wait()

        def block(span, first):
            done = attend_block(
                heads, ends, i, span, first, qkv, keys, scores, kept.at[turn], inverse
            )
            for m in range(heads):
                lo = m * HEAD_DIM
                att_v[owner, lo : lo + HEAD_DIM, aligned(b * BLOCK, BLOCK)] = done[m]

        spans(i, block)
        save_kept(i, turn).start()

        @pl.when((b == per_device - 1) & (n > 0))
        def _give():
            give_att(n).start()

        @pl.when(at == (n_h - 2) * per_device - 1)
        def _more():
            for t in range(1, far):
                up_copy(t, 1, h).start()

        return 0

    lax.fori_loop(0, n_h * per_device, attend, 0)
    up_arrived(0)
    att_in[h] = att_v[h]
    save_att = pltpu.make_async_copy(att_v, att_out, save_sem.at[3])
    save_att.start()
    for n in range(n_h - 1, 0, -1):
        give_att(n).wait_recv()
    save_att_t = pltpu.make_async_copy(att_in, att_t_out, save_sem.at[4])
    save_att_t.start()

    w_loads[3].wait()
    res = tv[h].astype(F32) + mm_tn(att_in[...].reshape(model, rows), wo[...])
    residual[...] = res
    normed, _unused = norm_parts(res)
    hidden = (normed * lying(g2) + lying(s2)).astype(BF)
    fill_slots(flat_t, hidden, xs_v)
    save_x = [
        pltpu.make_async_copy(
            xs_v.at[pl.ds(n * capacity, capacity)], x_slots.at[n], save_sem.at[5 + n]
        )
        for n in range(experts)
    ]
    for save in save_x:
        save.start()
    logits = mm_nt(hidden, w_router[...])
    lane = iota((rows, experts), 1)
    chosen = [
        jnp.sum(jnp.where(lane == ids[:, j : j + 1], logits, 0.0), axis=1, keepdims=True)
        for j in range(2)
    ]
    top = jnp.maximum(chosen[0], chosen[1])
    raised = [jnp.exp(c - top) for c in chosen]
    both = raised[0] + raised[1]
    gate = [r / both for r in raised]
    for j in range(2):
        gates[:, j : j + 1] = gate[j]
    column = iota((rows, padded), 1)
    for n in range(experts):
        mix = jnp.zeros((rows, padded), F32)
        for j in range(2):
            here = jnp.where(ids[:, j : j + 1] == n, slot[:, j : j + 1], -1) == column
            mix = jnp.where(here, gate[j], mix)
        line = jnp.sum(mix, axis=0, keepdims=True)
        gate_rows[n] = jnp.broadcast_to(line, (8, padded))

    place = ups.at[mate]
    remote(place, place, wc_s, wc_r, {"hidden": mate}).wait_recv()
    up_arrived(1)
    for t in range(1, far):
        for k in range(2):
            up_onward(t, k).wait()
    for step in range(1, n_e):
        source = lax.rem(e + n_e - step, n_e)
        place = g_in.at[source]
        remote(place, place, gs_s.at[step], gs_r.at[step], {"expert": e}).wait_recv()
    own_slots.wait()
    for n in range(1, n_h):
        give_att(n).wait_send()
    for turn in range(2):
        save_kept(0, turn).wait()
    for t in range(1, far):
        for k in range(2):
            up_copy(t, k, h).wait_send()
    for copy in sends:
        copy.wait_send()
    for save in [save_w, save_tokens, save_qkv, save_att, save_att_t, *save_x]:
        save.wait()


def run_front(
    docs, ids_t, g1, s1, g2, s2, w_router, tokens, out_grad, ws, w_up, capacity, heads, cid
):
    n_e, n_h = lax.axis_size("expert"), lax.axis_size("hidden")
    experts = n_e * w_up.shape[0]
    rows, model = tokens.shape
    padded = -(-capacity // LANES) * LANES
    width, group, total = heads * HEAD_DIM, rows * n_h, experts * capacity
    far, chunks = n_h // 2, 8

    def pairs(*shape):
        return [DMA(shape), DMA(shape)]

    return pl.pallas_call(
        partial(front_body, n_e, n_h, experts, capacity, padded, heads, chunks),
        name="front",
        out_shape=[
            shape_of((n_h, rows, model), BF),
            shape_of((3 * width, group), BF),
            shape_of((n_h, width, rows), BF),
            shape_of((n_h, width, rows), BF),
            shape_of((3 * width, model), BF),
            shape_of((experts, capacity, model), BF),
            shape_of((experts, capacity, model), BF),
            shape_of((n_h, *w_up.shape[1:]), BF),
            shape_of((group // BLOCK, heads, REACH, BLOCK, BLOCK), BF),
            shape_of((rows, 2), I32),
            shape_of((rows, 2), I32),
            shape_of((rows, 2), I32),
            shape_of((1, LANES), F32),
            shape_of((8, group), F32),
            shape_of((rows, model), F32),
            shape_of((rows, 2), F32),
            shape_of((experts, 8, padded), F32),
        ],
        in_specs=[SMEM] + [VMEM] * 6 + [ANY] * 7,
        out_specs=[ANY] * 9 + [VMEM] * 8,
        scratch_shapes=[
            pltpu.VMEM((n_h, rows, model), BF),
            pltpu.VMEM((rows, model), BF),
            pltpu.VMEM((3, model, model), BF),
            pltpu.VMEM((model, model), BF),
            pltpu.VMEM((3 * width, model), BF),
            pltpu.VMEM((3 * width, group), BF),
            pltpu.VMEM((heads, group, HEAD_DIM), BF),
            pltpu.VMEM((heads, REACH, BLOCK, BLOCK), F32),
            pltpu.VMEM((2, heads, REACH, BLOCK, BLOCK), BF),
            pltpu.VMEM((n_h, width, rows), BF),
            pltpu.VMEM((n_h, width, rows), BF),
            pltpu.VMEM((total, model), BF),
            pltpu.VMEM((total, model), BF),
            DMA((2,)),
            DMA((4,)),
            DMA((5 + experts,)),
            DMA((2,)),
            *pairs(far, chunks),
            DMA,
            DMA,
            *pairs(far, chunks),
            *pairs(n_e),
            *pairs(n_h),
            *pairs(far, 2),
            DMA,
            DMA,
            *pairs(far, 2),
        ],
        compiler_params=pltpu.CompilerParams(
            collective_id=cid, has_side_effects=True, vmem_limit_bytes=58 << 20
        ),
    )(docs, ids_t, g1, s1, g2, s2, w_router, tokens, out_grad, *ws, w_up)


def moe_body(
    size,
    capacity,
    padded,
    per,
    x_slots,
    gate_rows,
    g_in,
    ups,
    w_up,
    w_down,
    dx_back,
    dg_back,
    y_out,
    dw_sum,
    dw_far,
    xv,
    gv,
    gates_v,
    up_v,
    down_v,
    act,
    dz,
    xg,
    dy,
    xg_t,
    dy_t,
    dxv,
    yv,
    dgv,
    y_acc,
    dx_acc,
    dw_box,
    load_sem,
    save_sem,
    wy_s,
    wy_r,
    wc_s,
    wc_r,
    wf_s,
    wf_r,
    dc_s,
    dc_r,
    df_s,
    df_r,
    g_sem,
    own_sem,
    xs_sem,
    xr_sem,
    gs_sem,
    gr_sem,
    ds_sem,
    dr_sem,
    ts_sem,
    tr_sem,
    out_sem,
):
    me, h = lax.axis_index("expert"), lax.axis_index("hidden")
    shards_n = ups.shape[0]
    far = shards_n // 2
    pair, core = h // 2, lax.rem(h, 2)
    mate = pair * 2 + 1 - core
    deep = w_down.shape[1] // 2
    tall = per * capacity
    steps = size // per

    middle = size // 2
    inner = lax.rem((me // 2 * 8 // size + 1) // 2, 2)

    def group_at(step):
        some = steps // 4
        early = jnp.where(step <= some, step - 1 + steps // 2, step - some)
        early = jnp.where((step > 0) & (step < steps - some), early, step)
        return jnp.where(inner == 1, early, step)

    def peer_at(p):
        peer, bit = 0, 1
        while bit < size:
            peer = peer + lax.rem(me // bit + p // bit, 2) * bit
            bit *= 2
        return peer

    def rows_of(p):
        return pl.ds(pl.multiple_of(p * capacity, capacity), capacity)

    def send_x(p):
        peer = peer_at(p)
        return remote(
            x_slots.at[peer], xv.at[rows_of(p)], xs_sem.at[p], xr_sem.at[p], {"expert": peer}
        )

    def send_gate(p):
        peer = peer_at(p)
        return remote(
            gate_rows.at[peer], gates_v.at[p], gs_sem.at[p], gr_sem.at[p], {"expert": peer}
        )

    def send_dx(p):
        peer = peer_at(p)
        return remote(
            dxv.at[rows_of(p)], dx_back.at[me], ds_sem.at[p], dr_sem.at[p], {"expert": peer}
        )

    def send_dg(p):
        peer = peer_at(p)
        return remote(dgv.at[p], dg_back.at[me], ts_sem.at[p], tr_sem.at[p], {"expert": peer})

    def load_g(p):
        return pltpu.make_async_copy(g_in.at[peer_at(p)], gv.at[rows_of(p)], g_sem.at[p])

    def save_y(p):
        return pltpu.make_async_copy(yv.at[rows_of(p)], y_out.at[peer_at(p)], out_sem.at[p])

    own_x = pltpu.make_async_copy(x_slots.at[me], xv.at[rows_of(0)], own_sem.at[0])
    own_gate = pltpu.make_async_copy(gate_rows.at[me], gates_v.at[0], own_sem.at[1])
    own_dx = pltpu.make_async_copy(dxv.at[rows_of(0)], dx_back.at[me], own_sem.at[2])
    own_dg = pltpu.make_async_copy(dgv.at[0], dg_back.at[me], own_sem.at[3])
    loads = [
        pltpu.make_async_copy(w_up.at[0], up_v.at[h], load_sem.at[0]),
        pltpu.make_async_copy(w_down.at[0], down_v.at[h], load_sem.at[1]),
    ]
    loads.append(pltpu.make_async_copy(ups.at[mate], up_v.at[mate], load_sem.at[2]))

    early = w_up.shape[1] * UP_EARLY // 8

    def half(k):
        return aligned(k * deep, deep)

    for t in range(1, far):
        for other in range(2):
            c = lax.rem(pair + t, far) * 2 + other
            place = (c, pl.ds(0, early))
            loads.append(
                pltpu.make_async_copy(
                    ups.at[place], up_v.at[place], load_sem.at[1 + 2 * t + other]
                )
            )
    rest = pl.ds(early, w_up.shape[1] - early)
    parts = ((w_up, up_v, rest), (w_down, down_v, half(0)), (w_down, down_v, half(1)))

    def part_across(t, n):
        source, target, k = parts[n]
        there = {"hidden": lax.rem(pair + t, far) * 2 + core}
        return remote(
            source.at[0, k], target.at[h, k], wy_s.at[t, n], wy_r.at[t, n], there
        )

    def part_onward(t, n):
        _source, target, k = parts[n]
        place = target.at[lax.rem(pair + far - t, far) * 2 + core, k]
        return remote(place, place, wf_s.at[t, n], wf_r.at[t, n], {"hidden": mate})

    down_beside = remote(w_down.at[0], down_v.at[h], wc_s, wc_r, {"hidden": mate})
    own_x.start()
    own_gate.start()
    for p in range(size):
        load_g(p).start()
    for load in loads:
        load.start()
    greet(
        [{"expert": lax.rem(me + step, size)} for step in range(1, size)]
        + [{"hidden": lax.rem(h + step, shards_n)} for step in range(1, shards_n)]
    )

    def send_all(order):
        for p in order:
            send_x(p).start()
            send_gate(p).start()

    @pl.when(inner == 1)
    def _far_first():
        send_all([1, *range(middle, size), *range(2, middle)])

    @pl.when(inner == 0)
    def _near_first():
        send_all(range(1, size))

    for n in range(3):
        for t in range(1, far):
            part_across(t, n).start()
    down_beside.start()
    own_x.wait()
    own_gate.wait()
    for load in loads:
        load.wait()

    def finish(base, rows, held):
        dxv[rows, :] = dx_acc[held, :].astype(BF)
        y_low = y_acc[held, :].astype(BF)
        yv[rows, :] = y_low
        x, g = xv[rows, :], gv[rows, :]
        dots = jnp.sum(y_low.astype(F32) * g.astype(F32), axis=1, keepdims=True)
        for s in range(per):
            p = base + s
            part = slice(s * capacity, (s + 1) * capacity)
            tall_dots = jnp.broadcast_to(dots[part], (capacity, LANES))
            if padded > capacity:
                blank = jnp.zeros((padded - capacity, LANES), F32)
                tall_dots = jnp.concatenate([tall_dots, blank], axis=0)
            dgv[p] = tall_dots.T[0:8]

            @pl.when(p > 0)
            def _give(p=p):
                send_dx(p).start()
                send_dg(p).start()

            @pl.when(p == 0)
            def _keep():
                own_dx.start()
                own_dg.start()

            save_y(p).start()
        for s in range(per):
            p = base + s
            part = slice(s * capacity, (s + 1) * capacity)
            gate = gates_v[p].T[0:capacity, 0:1]
            xg[rows_of(p), :] = (x[part].astype(F32) * gate).astype(BF)
            dy[rows_of(p), :] = (g[part].astype(F32) * gate).astype(BF)

    first = shards_n // 2

    def unit(m):
        step = jnp.where(m < 2 * shards_n, lax.rem(m // first, 2), m // shards_n)
        n = m // shards_n * first + lax.rem(m, first)
        n = jnp.where(m < 2 * shards_n, n, lax.rem(m, shards_n))
        return step, n

    def unit_body(m, _):
        step, n = unit(m)
        base = group_at(step) * per
        rows = pl.ds(pl.multiple_of(base * capacity, tall), tall)
        held = aligned(jnp.where(step == 1, tall, 0), tall)

        @pl.when(n == 0)
        def _begin():
            for s in range(per):

                @pl.when(base + s > 0)
                def _arrive(s=s):
                    send_x(base + s).wait_recv()
                    send_gate(base + s).wait_recv()

                load_g(base + s).wait()
            y_acc[held, :] = jnp.zeros((tall, y_acc.shape[1]), F32)
            dx_acc[held, :] = jnp.zeros((tall, y_acc.shape[1]), F32)

        t = n // 2
        beside = lax.rem(n, 2)
        c = lax.rem(pair + far - t, far) * 2 + lax.rem(core + beside, 2)

        @pl.when(m == 1)
        def _beside():
            down_beside.wait_recv()

        @pl.when((step == 0) & (n >= 2) & (beside == 0))
        def _across():
            for k in range(3):
                part_across(t, k).wait_recv()
                part_onward(t, k).start()

        @pl.when((step == 0) & (n >= 2) & (beside == 1))
        def _onward():
            for k in range(3):
                part_onward(t, k).wait_recv()

        x, g = xv[rows, :], gv[rows, :]
        z = mm(x, up_v[c])
        du = mm_nt(g, down_v[c])
        square = z * z
        curve = jnp.tanh(z * (GELU_A + GELU_A * GELU_B * square))
        plus = 0.5 + 0.5 * curve
        hidden = (z * plus).astype(BF)
        rise = GELU_A + 3.0 * GELU_A * GELU_B * square
        slope = plus + 0.5 * z * (1.0 - curve * curve) * rise
        back = (slope * du).astype(BF)
        act[c, rows, :] = hidden
        dz[c, rows, :] = back
        y_acc[held, :] += mm(hidden, down_v[c])
        dx_acc[held, :] += mm_nt(back, up_v[c])

        @pl.when(n == shards_n - 1)
        def _end():
            finish(base, rows, held)

        return 0

    lax.fori_loop(0, steps * shards_n, unit_body, 0)

    total = size * capacity
    turn = 256
    for k in range(total // turn):
        rows = slice(k * turn, (k + 1) * turn)
        xg_t[:, rows] = xg[rows, :].astype(F32).T.astype(BF)
    for t in range(1, far):
        for k in range(3):
            part_across(t, k).wait_send()
            part_onward(t, k).wait_send()
    down_beside.wait_send()

    def give(which, step):
        source = (up_v, down_v)[which].at[lax.rem(pair + step, far) * 2 + 1 - core]
        return remote(
            source,
            dw_box.at[which, step],
            dc_s.at[which, step],
            dc_r.at[which, step],
            {"hidden": mate},
        )

    def keep(which, step):
        source = (up_v, down_v)[which].at[lax.rem(pair + step, far) * 2 + core]
        return pltpu.make_async_copy(source, dw_sum.at[which, step], save_sem.at[which, step])

    middle_row = up_v.shape[1] // 2
    cross_parts = (pl.ds(0, middle_row), pl.ds(middle_row, dw_far.shape[1] - middle_row))

    def cross(step, k):
        there = lax.rem(pair + step, far) * 2 + core
        return remote(
            up_v.at[there, cross_parts[k]],
            dw_far.at[step - 1, cross_parts[k]],
            df_s.at[step, k],
            df_r.at[step, k],
            {"hidden": there},
        )

    def gradients(which, left, right, held):
        def other(n, _):
            step = lax.rem(n + 1, far)
            c = lax.rem(pair + step, far) * 2 + 1 - core
            held[c] = mm(left[...], right[c]).astype(BF)
            give(which, step).start()
            return 0

        def own(n, _):
            step = lax.rem(n + 1, far)
            c = lax.rem(pair + step, far) * 2 + core
            total_of = mm(left[...], right[c])
            give(which, step).wait_recv()
            held[c] = (total_of + dw_box[which, step].astype(F32)).astype(BF)
            keep(which, step).start()

            if which == 0:

                @pl.when(step > 0)
                def _cross():
                    for k in range(2):
                        cross(step, k).start()

            return 0

        lax.fori_loop(0, far, other, 0)
        lax.fori_loop(0, far, own, 0)

    gradients(0, xg_t, dz, up_v)
    for k in range(total // turn):
        rows = slice(k * turn, (k + 1) * turn)
        dy_t[:, rows] = dy[rows, :].astype(F32).T.astype(BF)
    gradients(1, dy_t, act, down_v)
    for p in range(1, size):
        send_x(p).wait_send()
        send_gate(p).wait_send()
        send_dx(p).wait()
        send_dg(p).wait()
    for p in range(size):
        save_y(p).wait()
    own_dx.wait()
    own_dg.wait()
    for step in range(far):
        for which in range(2):
            give(which, step).wait_send()
            keep(which, step).wait()
    for step in range(1, far):
        for k in range(2):
            cross(step, k).wait()


def run_experts(x_slots, gate_rows, g_in, ups, w_up, w_down, cid):
    size = lax.axis_size("expert")
    experts, capacity, model = x_slots.shape
    padded = gate_rows.shape[2]
    shards_n, _unused, width = ups.shape
    total = experts * capacity
    per = 1
    while per * 2 * capacity <= 320 and size % (per * 2) == 0:
        per *= 2
    tall = per * capacity
    rows2 = (total, model)
    return pl.pallas_call(
        partial(moe_body, size, capacity, padded, per),
        name="experts",
        out_shape=[
            shape_of(x_slots.shape, BF),
            shape_of(gate_rows.shape, F32),
            shape_of(x_slots.shape, BF),
            shape_of((2, shards_n // 2, model, width), BF),
            shape_of((shards_n // 2 - 1, model * UP_CROSS // 8, width), BF),
        ],
        in_specs=[ANY] * 6,
        out_specs=[ANY] * 5,
        scratch_shapes=[
            pltpu.VMEM(rows2, BF),
            pltpu.VMEM(rows2, BF),
            pltpu.VMEM(gate_rows.shape, F32),
            pltpu.VMEM((shards_n, model, width), BF),
            pltpu.VMEM((shards_n, width, model), BF),
            pltpu.VMEM((shards_n, total, width), BF),
            pltpu.VMEM((shards_n, total, width), BF),
            pltpu.VMEM(rows2, BF),
            pltpu.VMEM(rows2, BF),
            pltpu.VMEM((model, total), BF),
            pltpu.VMEM((model, total), BF),
            pltpu.VMEM(rows2, BF),
            pltpu.VMEM(rows2, BF),
            pltpu.VMEM(gate_rows.shape, F32),
            pltpu.VMEM((2 * tall, model), F32),
            pltpu.VMEM((2 * tall, model), F32),
            pltpu.VMEM((2, shards_n // 2, model, width), BF),
            DMA((shards_n + 1,)),
            DMA((2, shards_n // 2)),
            DMA((shards_n // 2, 3)),
            DMA((shards_n // 2, 3)),
            DMA,
            DMA,
            DMA((shards_n // 2, 3)),
            DMA((shards_n // 2, 3)),
            DMA((2, shards_n // 2)),
            DMA((2, shards_n // 2)),
            DMA((shards_n // 2, 2)),
            DMA((shards_n // 2, 2)),
            DMA((size,)),
            DMA((4,)),
        ]
        + [DMA((size,))] * 9,
        compiler_params=pltpu.CompilerParams(
            collective_id=cid, has_side_effects=True, vmem_limit_bytes=60 << 20
        ),
        cost_estimate=pl.CostEstimate(
            flops=12 * total * model * width * shards_n, bytes_accessed=40 << 20, transcendentals=0
        ),
    )(x_slots, gate_rows, g_in, ups, w_up, w_down)


def tail_body(
    n_e,
    n_h,
    chunks,
    dh,
    w_all,
    small,
    tokens,
    gain,
    d_res,
    residual,
    gates,
    pos,
    y_back,
    input_grad,
    output,
    full,
    total,
    wv,
    tok_v,
    d_res_v,
    res_v,
    yv,
    mine,
    beside,
    across,
    passing,
    x_box,
    z_box,
    w_mid,
    piece,
    small_mid,
    small_h,
    small_e,
    small_all,
    load_sem,
    mine_sem,
    cs_sem,
    cr_sem,
    as_sem,
    ar_sem,
    ws_sem,
    wr_sem,
    vs_sem,
    vr_sem,
    hs_sem,
    hr_sem,
    es_sem,
    er_sem,
    bs_sem,
    br_sem,
    keep_sem,
    zs_sem,
    zr_sem,
    xs_sem,
    xr_sem,
    ys_sem,
    yr_sem,
    ms_sem,
    mr_sem,
):
    e, h = lax.axis_index("expert"), lax.axis_index("hidden")
    far, high = n_h // 2, n_e // 2
    pair, core = h // 2, lax.rem(h, 2)
    eh, el = e // 2, lax.rem(e, 2)
    mate = pair * 2 + 1 - core
    greet(
        [{"expert": lax.rem(e + step, n_e)} for step in range(1, n_e)]
        + [{"hidden": lax.rem(h + step, n_h)} for step in range(1, n_h)]
    )
    w_sends, w_order = {}, list(range(1, high)) + [0]
    for step in w_order:
        there = lax.rem(eh + step, high)
        copy = remote(
            w_all.at[there * 2 + 1 - el],
            x_box.at[step],
            ws_sem.at[step],
            wr_sem.at[step],
            {"expert": eh * 2 + 1 - el},
        )
        copy.start()
        w_sends[step] = copy
    small_sends = []
    for at in range(n_h - 1):
        peer = lax.rem(h + 1 + at, n_h)
        copy = remote(
            small.at[peer], small_h.at[at], hs_sem.at[at], hr_sem.at[at], {"hidden": peer}
        )
        copy.start()
        small_sends.append(copy)
    rows = dh.shape[1] // chunks
    core_sends = {}
    for step in list(range(1, far)) + [0]:
        there = lax.rem(pair + step, far)
        for k in range(chunks):
            part = pl.ds(k * rows, rows)
            copy = remote(
                dh.at[there * 2 + 1 - core, part],
                beside.at[step, part],
                cs_sem.at[step, k],
                cr_sem.at[step, k],
                {"hidden": mate},
            )
            copy.start()
            core_sends[step, k] = copy
    mine_loads = []
    for step in range(far):
        there = lax.rem(pair + step, far)
        load = pltpu.make_async_copy(dh.at[there * 2 + core], mine.at[step], mine_sem.at[step])
        load.start()
        mine_loads.append(load)
    loads = [
        pltpu.make_async_copy(source, target, load_sem.at[n])
        for n, (source, target) in enumerate(
            ((w_all, wv), (residual, res_v), (y_back, yv), (tokens, tok_v), (d_res, d_res_v))
        )
    ]
    for load in loads:
        load.start()
    for load in mine_loads:
        load.wait()
    far_sends = []
    for step in range(1, far):
        there = lax.rem(pair + step, far)
        for k in range(chunks):
            part = pl.ds(k * rows, rows)
            core_sends[step, k].wait_recv()
            both = mine[step, part, :].astype(F32) + beside[step, part, :].astype(F32)
            passing[step - 1, part, :] = both.astype(BF)
            copy = remote(
                passing.at[step - 1, part],
                across.at[step - 1, part],
                as_sem.at[step - 1, k],
                ar_sem.at[step - 1, k],
                {"hidden": there * 2 + core},
            )
            copy.start()
            far_sends.append(copy)
    loads[0].wait()
    v_sends = []
    for step in w_order[:-1]:
        there = lax.rem(eh + step, high) * 2 + el
        w_sends[step].wait_recv()
        w_mid[step - 1] = (wv[there].astype(F32) + x_box[step].astype(F32)).astype(BF)
        copy = remote(
            w_mid.at[step - 1],
            z_box.at[step - 1],
            vs_sem.at[step],
            vr_sem.at[step],
            {"expert": there},
        )
        copy.start()
        v_sends.append(copy)
    summed = small[h]
    for at, copy in enumerate(small_sends):
        copy.wait_recv()
        summed = summed + small_h[at]
    small_mid[...] = summed
    small_out = []
    for at in range(n_e - 1):
        peer = lax.rem(e + 1 + at, n_e)
        copy = remote(small_mid, small_e.at[at], es_sem.at[at], er_sem.at[at], {"expert": peer})
        copy.start()
        small_out.append(copy)
    w_sends[0].wait_recv()
    acc = wv[e].astype(F32) + x_box[0].astype(F32)
    for at, copy in enumerate(v_sends):
        copy.wait_recv()
        acc = acc + z_box[at].astype(F32)
    piece[...] = acc.astype(BF)
    keep = pltpu.make_async_copy(piece, full.at[h, e], keep_sem)
    keep.start()

    def spot(t, s, flag, core_of):
        eh_of = lax.rem(eh + high - s, high)
        el_of = el if flag == 0 else 1 - el
        return full.at[lax.rem(pair + far - t, far) * 2 + core_of, eh_of * 2 + el_of]

    def held(t, s, flag):
        return piece if (t, s, flag) == (0, 0, 0) else spot(t, s, flag, core)

    def along(t, s):
        there = {"expert": lax.rem(eh + s, high) * 2 + el}
        return remote(held(t, 0, 0), spot(t, 0, 0, core), zs_sem.at[t, s], zr_sem.at[t, s], there)

    def aside(t, s):
        there = {"expert": eh * 2 + 1 - el}
        return remote(held(t, s, 0), spot(t, s, 0, core), xs_sem.at[t, s], xr_sem.at[t, s], there)

    def over(t, s, flag):
        there = {"hidden": lax.rem(pair + t, far) * 2 + core}
        at = 2 * s + flag
        return remote(
            held(0, s, flag), spot(0, s, flag, core), ys_sem.at[t, at], yr_sem.at[t, at], there
        )

    def to_mate(t, s, flag):
        at = 2 * s + flag
        return remote(
            held(t, s, flag),
            spot(t, s, flag, core),
            ms_sem.at[t, at],
            mr_sem.at[t, at],
            {"hidden": mate},
        )

    line_order = list(range(1, high))
    pieces = [(s, flag) for s in range(high) for flag in range(2)]
    first, second = core == 0, core == 1

    @pl.when(first)
    def _spread_first():
        for s in line_order:
            along(0, s).start()
        aside(0, 0).start()
        for t in range(1, far):
            over(t, 0, 0).start()
        to_mate(0, 0, 0).start()

        def take_aside(s):
            aside(0, s).wait_recv()
            for t in range(1, far):
                over(t, s, 1).start()
            to_mate(0, s, 1).start()

        for s in line_order:
            along(0, s).wait_recv()
            aside(0, s).start()
            for t in range(1, far):
                over(t, s, 0).start()
            to_mate(0, s, 0).start()
            take_aside(s - 1)
        take_aside(high - 1)

    @pl.when(second)
    def _spread_second():
        for t in range(1, far):
            over(t, 0, 0).start()
        for s in line_order:
            along(0, s).start()
        aside(0, 0).start()
        to_mate(0, 0, 0).start()
        for t in range(1, far):
            over(t, 0, 0).wait_recv()
            for s in line_order:
                along(t, s).start()
            aside(t, 0).start()
            to_mate(t, 0, 0).start()
        for s in line_order:
            for t in range(far):
                along(t, s).wait_recv()
                aside(t, s).start()
                to_mate(t, s, 0).start()

    summed = small_mid[...]
    for at, copy in enumerate(small_out):
        copy.wait_recv()
        summed = summed + small_e[at]
    small_all[h] = summed
    small_back = []
    for at in range(n_h - 1):
        peer = lax.rem(h + 1 + at, n_h)
        copy = remote(
            small_all.at[h], small_all.at[h], bs_sem.at[at], br_sem.at[at], {"hidden": peer}
        )
        copy.start()
        small_back.append(copy)
    for load in loads[1:]:
        load.wait()
    place_of = iota((residual.shape[0], y_back.shape[0]), 1)
    result = res_v[...]
    for j in range(2):
        pick = (place_of == pos[:, j : j + 1]).astype(BF)
        result = result + gates[:, j : j + 1] * mm(pick, yv[...])
    output[...] = result.astype(BF)
    for k in range(chunks):
        part = pl.ds(k * rows, rows)
        core_sends[0, k].wait_recv()
    for copy in far_sends:
        copy.wait_recv()
    grad = mine[0].astype(F32) + beside[0].astype(F32)
    for step in range(far - 1):
        grad = grad + across[step].astype(F32)
    normed, inverse = norm_parts(tok_v[...].astype(F32))
    input_grad[...] = (d_res_v[...] + norm_back(grad, normed, inverse, lying(gain))).astype(BF)
    @pl.when(first)
    def _finish_first():
        for t in range(1, far):
            for s, flag in pieces:
                over(t, s, flag).wait_recv()
                to_mate(t, s, flag).start()

    @pl.when(second)
    def _finish_second():
        for s in range(high):
            for t in range(far):
                aside(t, s).wait_recv()
                to_mate(t, s, 1).start()

    for copy in small_back:
        copy.wait_recv()
    total[...] = small_all[...]
    for t in range(far):
        for s, flag in pieces:
            to_mate(t, s, flag).wait()
    keep.wait()

    @pl.when(first)
    def _sent_first():
        for s in line_order:
            along(0, s).wait_send()
        for s in range(high):
            aside(0, s).wait_send()
        for t in range(1, far):
            for s, flag in pieces:
                over(t, s, flag).wait_send()

    @pl.when(second)
    def _sent_second():
        for t in range(1, far):
            over(t, 0, 0).wait_send()
        for t in range(far):
            for s in line_order:
                along(t, s).wait_send()
            for s in range(high):
                aside(t, s).wait_send()

    for copy in [*w_sends.values(), *v_sends, *small_sends, *small_out, *small_back, *far_sends]:
        copy.wait_send()
    for copy in core_sends.values():
        copy.wait_send()


def run_tail(dh, w_all, small, tokens, gain, d_res, residual, gates, pos, y_back, cid):
    n_e, n_h = lax.axis_size("expert"), lax.axis_size("hidden")
    far, high = n_h // 2, n_e // 2
    chunks = 4
    _unused, rows, model = dh.shape
    piece = w_all.shape[1:]
    return pl.pallas_call(
        partial(tail_body, n_e, n_h, chunks),
        name="tail",
        out_shape=[
            shape_of((rows, model), BF),
            shape_of((rows, model), BF),
            shape_of((n_h, n_e, *piece), BF),
            shape_of(small.shape, F32),
        ],
        in_specs=[ANY, ANY, VMEM, ANY, VMEM, ANY, ANY, VMEM, VMEM, ANY],
        out_specs=[VMEM, VMEM, ANY, VMEM],
        scratch_shapes=[
            pltpu.VMEM(w_all.shape, BF),
            pltpu.VMEM(tokens.shape, BF),
            pltpu.VMEM(d_res.shape, F32),
            pltpu.VMEM(residual.shape, F32),
            pltpu.VMEM(y_back.shape, BF),
            pltpu.VMEM((far, rows, model), BF),
            pltpu.VMEM((far, rows, model), BF),
            pltpu.VMEM((far - 1, rows, model), BF),
            pltpu.VMEM((far - 1, rows, model), BF),
            pltpu.VMEM((high, *piece), BF),
            pltpu.VMEM((high - 1, *piece), BF),
            pltpu.VMEM((high - 1, *piece), BF),
            pltpu.VMEM(piece, BF),
            pltpu.VMEM(small.shape[1:], F32),
            pltpu.VMEM((n_h - 1, *small.shape[1:]), F32),
            pltpu.VMEM((n_e - 1, *small.shape[1:]), F32),
            pltpu.VMEM(small.shape, F32),
            DMA((5,)),
            DMA((far,)),
            DMA((far, chunks)),
            DMA((far, chunks)),
            DMA((far - 1, chunks)),
            DMA((far - 1, chunks)),
            DMA((high,)),
            DMA((high,)),
            DMA((high,)),
            DMA((high,)),
            DMA((n_h - 1,)),
            DMA((n_h - 1,)),
            DMA((n_e - 1,)),
            DMA((n_e - 1,)),
            DMA((n_h - 1,)),
            DMA((n_h - 1,)),
            DMA,
            DMA((far, high)),
            DMA((far, high)),
            DMA((far, high)),
            DMA((far, high)),
            DMA((far, n_e)),
            DMA((far, n_e)),
            DMA((far, n_e)),
            DMA((far, n_e)),
        ],
        compiler_params=pltpu.CompilerParams(
            collective_id=cid, has_side_effects=True, vmem_limit_bytes=56 << 20
        ),
    )(dh, w_all, small, tokens, gain, d_res, residual, gates, pos, y_back)


def turn_body(
    width,
    experts,
    scale,
    full,
    dw,
    small,
    input_grad,
    output,
    q_out,
    k_out,
    v_out,
    o_out,
    up_out,
    down_out,
    g1_out,
    s1_out,
    g2_out,
    s2_out,
    router_out,
    input_out,
    output_out,
    load_out,
):
    @pl.when(pl.program_id(0) == 0)
    def _begin():
        input_out[...] = input_grad[...]
        output_out[...] = output[...]
        for n, out in enumerate((g1_out, s1_out, g2_out, s2_out)):
            out[...] = small[row_at(small, n)].reshape(out.shape)
        for n in range(experts):
            router_out[n : n + 1, :] = small[row_at(small, 8 + n)]
        load_out[...] = small[row_at(small, 4)][:, 0:experts].reshape(experts) * scale

    for n, out in enumerate((q_out, k_out, v_out)):
        part = full[:, n * width : (n + 1) * width, :].astype(F32)
        out[...] = part.reshape(-1, part.shape[2]).T
    part = full[:, 3 * width :, :].astype(F32)
    o_out[...] = part.reshape(-1, part.shape[2])
    trained = jnp.where(lax.axis_index("expert") >= experts // 2, 1.0, 0.0)
    up_out[...] = dw[0].astype(F32) * trained
    down_out[...] = dw[1].astype(F32).T * trained


def turn_weights(full, dw, small, input_grad, output, width, experts, scale):
    n_h, deep, model = full.shape
    cols = 384
    across = pl.BlockSpec((cols, model), lambda i: (i, 0))
    down = pl.BlockSpec((model, cols), lambda i: (0, i))
    flat = pl.BlockSpec((model,), lambda i: (0,))
    whole = pl.BlockSpec(output.shape, lambda i: (0, 0))
    square = shape_of((model, model), F32)
    return pl.pallas_call(
        partial(turn_body, width, experts, scale),
        name="turn_weights",
        grid=(model // cols,),
        out_shape=[square] * 6
        + [shape_of((model,), F32)] * 4
        + [
            shape_of((experts, model), F32),
            shape_of(input_grad.shape, BF),
            shape_of(output.shape, BF),
            shape_of((experts,), F32),
        ],
        in_specs=[
            pl.BlockSpec((n_h, deep, cols), lambda i: (0, 0, i)),
            pl.BlockSpec((2, model, cols), lambda i: (0, 0, i)),
            pl.BlockSpec(small.shape, lambda i: (0, 0, 0)),
            whole,
            whole,
        ],
        out_specs=[across, across, across, down, down, across]
        + [flat] * 4
        + [pl.BlockSpec((experts, model), lambda i: (0, 0)), whole, whole]
        + [pl.BlockSpec((experts,), lambda i: (0,))],
        compiler_params=pltpu.CompilerParams(
            dimension_semantics=("arbitrary",), vmem_limit_bytes=60 << 20
        ),
        cost_estimate=pl.CostEstimate(flops=0, bytes_accessed=24 << 20, transcendentals=0),
    )(full, dw, small, input_grad, output)


def attend_back(
    heads, i, span, first, qkv, given, centre, kept, values, dq_acc, dk_acc, dv_acc
):
    width = heads * HEAD_DIM
    rows = aligned(i * BLOCK, BLOCK)
    dq_acc[...] = jnp.zeros_like(dq_acc)
    queries = [
        qkv[n * HEAD_DIM : (n + 1) * HEAD_DIM, rows] * jnp.asarray(SCALE, BF) for n in range(heads)
    ]
    for k in range(span):
        part = aligned((first + k) * BLOCK, BLOCK)
        for n in range(heads):
            here = slice(n * HEAD_DIM, (n + 1) * HEAD_DIM)
            weight = kept[n, k]
            d_weight = mm(values[n, part, :], given[n])
            d_score = (weight.astype(F32) * (d_weight - centre[n])).astype(BF)
            dv_acc[here, part] += mm_nt(given[n], weight)
            dk_acc[here, part] += mm_nt(queries[n], d_score)
            lo = width + n * HEAD_DIM
            dq_acc[here, :] += mm(qkv[lo : lo + HEAD_DIM, part], d_score)


def back_body(
    n_e,
    n_h,
    experts,
    capacity,
    padded,
    heads,
    ids,
    slot,
    pos,
    gates,
    count,
    g1,
    s1,
    g2,
    s2,
    w_router,
    inverse,
    dg_rows,
    dx_back,
    y_out,
    dw_sum,
    dw_far,
    out_grad,
    residual,
    all_tokens,
    qkv_in,
    att_in,
    att_t_in,
    w_out,
    w_t_in,
    weights,
    y_back,
    d_hidden,
    d_res,
    w_all,
    small,
    dw_own,
    dxv,
    gv,
    res_v,
    tv,
    qkv,
    att_v,
    att_t,
    wo,
    w_t,
    d_att_v,
    d_att,
    wo_box,
    wo_far,
    kept,
    values,
    dq_acc,
    dk_acc,
    dv_acc,
    d_qkv,
    w_acc,
    dw_mine,
    dw_across,
    load_sem,
    save_sem,
    dw_sem,
    kept_sem,
    y_own,
    y_s,
    y_r,
    at_s,
    at_r,
    wo_s,
    wo_r,
    wf_s,
    wf_r,
    da_s,
    da_r,
):
    e, h = lax.axis_index("expert"), lax.axis_index("hidden")
    far = n_h // 2
    pair, core = h // 2, lax.rem(h, 2)
    mate = pair * 2 + 1 - core
    rows, model = out_grad.shape
    width = heads * HEAD_DIM
    group = rows * n_h
    per_device = rows // BLOCK
    blocks = group // BLOCK
    sends = []

    loads = [
        pltpu.make_async_copy(source, target, load_sem.at[n])
        for n, (source, target) in enumerate(
            (
                (residual, res_v),
                (dx_back, dxv),
                (out_grad, gv),
                (w_out, wo),
                (att_t_in, att_t),
                (qkv_in, qkv),
                (att_in, att_v),
                (all_tokens, tv),
                (w_t_in, w_t),
            )
        )
    ]
    for load in loads:
        load.start()
    greet(
        [{"hidden": lax.rem(h + step, n_h)} for step in range(1, n_h)]
        + [{"expert": lax.rem(e + step, n_e)} for step in range(1, n_e)]
    )
    load_dw = pltpu.make_async_copy(dw_sum.at[:, 0], dw_mine, dw_sem.at[0])
    load_dw.start()
    deep = dw_mine.shape[1] // 2
    crossed = dw_far.shape[1]
    load_far = pltpu.make_async_copy(
        dw_far, dw_across.at[0, :, pl.ds(0, crossed)], dw_sem.at[1]
    )
    load_far.start()

    def dw_across_copy(step, k):
        part = pl.ds(k * deep, deep)
        return remote(
            dw_sum.at[1, step, part],
            dw_across.at[1, step - 1, part],
            da_s.at[step, k],
            da_r.at[step, k],
            {"hidden": lax.rem(pair + step, far) * 2 + core},
        )

    def dw_send(k):
        for step in range(1, far):
            dw_across_copy(step, k).start()

    def up_rest_copy(step):
        part = pl.ds(crossed, dw_mine.shape[1] - crossed)
        return remote(
            dw_sum.at[0, step, part],
            dw_across.at[0, step - 1, part],
            da_s.at[step, 2],
            da_r.at[step, 2],
            {"hidden": lax.rem(pair + step, far) * 2 + core},
        )

    for step in range(1, far):
        up_rest_copy(step).start()
    dw_send(0)
    for step in range(1, n_e):
        peer = lax.rem(e + step, n_e)
        copy = remote(y_out.at[peer], y_back.at[e], y_s.at[step], y_r.at[step], {"expert": peer})
        copy.start()
        sends.append(copy)
    own_y = pltpu.make_async_copy(y_out.at[e], y_back.at[e], y_own)
    own_y.start()

    for load in loads[:3]:
        load.wait()
    normed, spread = norm_parts(res_v[...])
    hidden = (normed * lying(g2) + lying(s2)).astype(BF)
    gate = [gates[:, j : j + 1] for j in range(2)]
    column = iota((rows, padded), 1)
    dot_of = []
    for j in range(2):
        mix = jnp.zeros((rows, padded), F32)
        for n in range(experts):
            here = jnp.where(ids[:, j : j + 1] == n, slot[:, j : j + 1], -1) == column
            mix = jnp.where(here, dg_rows[n, 0:1, :], mix)
        dot_of.append(jnp.sum(mix, axis=1, keepdims=True))
    mean = gate[0] * dot_of[0] + gate[1] * dot_of[1]
    lane = iota((rows, experts), 1)
    d_logits = jnp.zeros((rows, experts), F32)
    for j in range(2):
        d_logits = jnp.where(lane == ids[:, j : j + 1], gate[j] * (dot_of[j] - mean), d_logits)
    high, low = split_two(d_logits)
    grad = mm(high, w_router[...]) + mm(low, w_router[...])
    small[...] = jnp.zeros_like(small)
    for_router = mm_tn(high, hidden) + mm_tn(low, hidden)
    for n in range(experts):
        small[row_at(small, 8 + n)] = for_router[n : n + 1]
    place, line = row_at(small, 4)
    small[place, line, 0:LANES] = count[...]
    place = iota((rows, experts * capacity), 1)
    for j in range(2):
        pick = (place == pos[:, j : j + 1]).astype(BF)
        grad = grad + gate[j] * mm(pick, dxv[...])
    small[row_at(small, 2)] = jnp.sum(grad * normed, axis=0, keepdims=True)
    small[row_at(small, 3)] = jnp.sum(grad, axis=0, keepdims=True)
    d_resid = gv[...].astype(F32) + norm_back(grad, normed, spread, lying(g2))
    d_res[...] = d_resid
    branch = d_resid.astype(BF)
    loads[3].wait()

    def device_at(n, sign):
        t, other = n // 2, lax.rem(n, 2)
        return lax.rem(pair + far + sign * t, far) * 2 + lax.rem(core + other, 2)

    def give_att(n):
        owner = device_at(n, 1)
        return remote(
            d_att_v.at[owner], d_att.at[h], at_s.at[n], at_r.at[n], {"hidden": owner}
        )

    for n in range(n_h - 1, -1, -1):
        owner = device_at(n, 1)
        block = mm_nt(wo[owner], branch).astype(BF)
        if n == 0:
            d_att[h] = block
        else:
            d_att_v[owner] = block
            give_att(n).start()
    loads[4].wait()
    for t in range(n_h):
        owner = lax.rem(h + t, n_h)
        wo[owner] = mm(att_t[owner], branch).astype(BF)
    for step in list(range(1, far)) + [0]:
        copy = remote(
            wo.at[lax.rem(pair + step, far) * 2 + 1 - core],
            wo_box.at[step],
            wo_s.at[step],
            wo_r.at[step],
            {"hidden": mate},
        )
        copy.start()
        sends.append(copy)
    def give_wo(step):
        target = lax.rem(pair + step, far) * 2 + core
        return remote(
            wo.at[target],
            wo_far.at[step - 1],
            wf_s.at[step],
            wf_r.at[step],
            {"hidden": target},
        )

    for load in loads[5:]:
        load.wait()

    def load_kept(i, turn):
        return pltpu.make_async_copy(weights.at[i], kept.at[turn], kept_sem.at[turn])

    def block_at(at):
        owner = device_at(at // per_device, 1)
        return owner, owner * per_device + lax.rem(at, per_device)

    load_kept(block_at(0)[1], 0).start()
    dk_acc[...] = jnp.zeros_like(dk_acc)
    dv_acc[...] = jnp.zeros_like(dv_acc)

    def turn_values(i, _):
        cols = aligned(i * BLOCK, BLOCK)
        for n in range(heads):
            lo = 2 * width + n * HEAD_DIM
            values[n, cols, :] = qkv[lo : lo + HEAD_DIM, cols].astype(F32).T.astype(BF)
        return 0

    lax.fori_loop(0, blocks, turn_values, 0)

    def over_queries(at, _):
        owner, i = block_at(at)
        turn = lax.rem(at, 2)

        @pl.when(at + 1 < blocks)
        def _next():
            load_kept(block_at(at + 1)[1], 1 - turn).start()

        @pl.when((at >= per_device) & (lax.rem(at, per_device) == 0))
        def _arrive():
            n = at // per_device
            source = lax.rem(far - n // 2, far) * 2 + lax.rem(n, 2)
            give_att(source).wait_recv()

        @pl.when(at == per_device)
        def _weights():
            for step in range(1, far):
                there = wo_box.at[step]
                target = lax.rem(pair + step, far) * 2 + core
                remote(there, there, wo_s.at[step], wo_r.at[step], {"hidden": mate}).wait_recv()
                both = wo[target].astype(F32) + wo_box[step].astype(F32)
                wo[target] = both.astype(BF)
                give_wo(step).start()
            dw_send(1)

        load_kept(i, turn).wait()
        cols = aligned(lax.rem(at, per_device) * BLOCK, BLOCK)
        rows_i = aligned(i * BLOCK, BLOCK)
        given, centre = [], []
        for n in range(heads):
            here = slice(n * HEAD_DIM, (n + 1) * HEAD_DIM)
            scaled = d_att[owner, here, cols].astype(F32) * inverse[n : n + 1, rows_i]
            given.append(scaled.astype(BF))
            product = att_v[owner, here, cols].astype(F32) * scaled
            centre.append(jnp.sum(product, axis=0, keepdims=True))

        def block(span, first):
            attend_back(
                heads,
                i,
                span,
                first,
                qkv,
                given,
                centre,
                kept.at[turn],
                values,
                dq_acc,
                dk_acc,
                dv_acc,
            )

        spans(i, block)
        d_qkv[0:width, rows_i] = (dq_acc[...] * SCALE).astype(BF)
        return 0

    lax.fori_loop(0, blocks, over_queries, 0)
    w_acc[...] = jnp.zeros_like(w_acc)

    def finish(i, _):
        cols = aligned(i * BLOCK, BLOCK)
        d_qkv[width : 2 * width, cols] = dk_acc[:, cols].astype(BF)
        d_qkv[2 * width :, cols] = dv_acc[:, cols].astype(BF)
        block = d_qkv[:, cols]
        grad = mm_tn(block, w_t[...])
        inner = aligned(lax.rem(i, per_device) * BLOCK, BLOCK)
        normed, _unused = norm_parts(tv[i // per_device, inner, :].astype(F32))
        tv[i // per_device, inner, :] = grad.astype(BF)
        small[row_at(small, 0)] += jnp.sum(grad * normed, axis=0, keepdims=True)
        small[row_at(small, 1)] += jnp.sum(grad, axis=0, keepdims=True)
        hidden = (normed * lying(g1) + lying(s1)).astype(BF)
        w_acc[...] += mm(block, hidden)
        return 0

    lax.fori_loop(0, blocks, finish, 0)
    save_dh = pltpu.make_async_copy(tv, d_hidden, save_sem)
    save_dh.start()
    w_all[0 : 3 * width, :] = w_acc[...].astype(BF)
    there = wo_box.at[0]
    remote(there, there, wo_s.at[0], wo_r.at[0], {"hidden": mate}).wait_recv()
    total = wo[h].astype(F32) + wo_box[0].astype(F32)
    for step in range(1, far):
        give_wo(step).wait_recv()
        total = total + wo_far[step - 1].astype(F32)
    w_all[3 * width :, :] = total.astype(BF)
    load_dw.wait()
    load_far.wait()
    for which in range(2):
        for step in range(1, far):
            if which == 0:
                up_rest_copy(step).wait()
            else:
                for k in range(2):
                    dw_across_copy(step, k).wait()

        def add_all(n, _, which=which):
            band = aligned(n * 96, 96)
            both = dw_mine[which, band, :].astype(F32)
            for step in range(1, far):
                both = both + dw_across[which, step - 1, band, :].astype(F32)
            dw_own[which, band, :] = both.astype(BF)
            return 0

        lax.fori_loop(0, dw_mine.shape[1] // 96, add_all, 0)
    for step in range(1, n_e):
        there = y_back.at[lax.rem(e + n_e - step, n_e)]
        remote(there, there, y_s.at[step], y_r.at[step], {"expert": e}).wait_recv()
    own_y.wait()
    save_dh.wait()
    for n in range(1, n_h):
        give_att(n).wait_send()
    for step in range(1, far):
        give_wo(step).wait_send()
    for copy in sends:
        copy.wait_send()


def run_back(
    ids,
    slot,
    pos,
    gates,
    count,
    g1,
    s1,
    g2,
    s2,
    w_router,
    inverse,
    dg_rows,
    dx_back,
    y_out,
    dw_sum,
    dw_far,
    out_grad,
    residual,
    all_tokens,
    qkv,
    att,
    att_t,
    w_out,
    w_t,
    weights,
    cid,
):
    n_e, n_h = lax.axis_size("expert"), lax.axis_size("hidden")
    experts, capacity, model = y_out.shape
    padded = dg_rows.shape[2]
    rows = out_grad.shape[0]
    width = w_t.shape[0] // 3
    heads = width // HEAD_DIM
    group, far = rows * n_h, n_h // 2
    shard = dw_sum.shape[2:]
    tall = 8 + experts

    def pairs(*shape):
        return [DMA(shape), DMA(shape)]

    return pl.pallas_call(
        partial(back_body, n_e, n_h, experts, capacity, padded, heads),
        name="back",
        out_shape=[
            shape_of(y_out.shape, BF),
            shape_of((n_h, rows, model), BF),
            shape_of((rows, model), F32),
            shape_of((4 * width, model), BF),
            shape_of((n_h, tall // n_h, model), F32),
            shape_of((2, *shard), BF),
        ],
        in_specs=[VMEM] * 12 + [ANY] * 13,
        out_specs=[ANY] * 2 + [VMEM] * 4,
        scratch_shapes=[
            pltpu.VMEM((experts * capacity, model), BF),
            pltpu.VMEM((rows, model), BF),
            pltpu.VMEM((rows, model), F32),
            pltpu.VMEM((n_h, rows, model), BF),
            pltpu.VMEM((3 * width, group), BF),
            pltpu.VMEM((n_h, width, rows), BF),
            pltpu.VMEM((n_h, width, rows), BF),
            pltpu.VMEM((n_h, width, model), BF),
            pltpu.VMEM((3 * width, model), BF),
            pltpu.VMEM((n_h, width, rows), BF),
            pltpu.VMEM((n_h, width, rows), BF),
            pltpu.VMEM((far, width, model), BF),
            pltpu.VMEM((far - 1, width, model), BF),
            pltpu.VMEM((2, heads, REACH, BLOCK, BLOCK), BF),
            pltpu.VMEM((heads, group, HEAD_DIM), BF),
            pltpu.VMEM((width, BLOCK), F32),
            pltpu.VMEM((width, group), F32),
            pltpu.VMEM((width, group), F32),
            pltpu.VMEM((3 * width, group), BF),
            pltpu.VMEM((3 * width, model), F32),
            pltpu.VMEM((2, *shard), BF),
            pltpu.VMEM((2, far - 1, *shard), BF),
            DMA((9,)),
            DMA,
            DMA((2,)),
            DMA((2,)),
            DMA,
            *pairs(n_e),
            *pairs(n_h),
            *pairs(far),
            *pairs(far),
            *pairs(far, 3),
        ],
        compiler_params=pltpu.CompilerParams(
            collective_id=cid, has_side_effects=True, vmem_limit_bytes=60 << 20
        ),
    )(
        ids,
        slot,
        pos,
        gates,
        count,
        g1,
        s1,
        g2,
        s2,
        w_router,
        inverse,
        dg_rows,
        dx_back.reshape(experts * capacity, model),
        y_out,
        dw_sum,
        dw_far,
        out_grad,
        residual,
        all_tokens,
        qkv,
        att,
        att_t,
        w_out.reshape(n_h, width, model),
        w_t,
        weights,
    )


def shards(
    tokens,
    doc_lengths,
    expert_ids,
    gain_one,
    shift_one,
    w_query,
    w_key,
    w_value,
    w_out,
    gain_two,
    shift_two,
    w_router,
    w_up,
    w_down,
    out_grad,
):
    rows, model = tokens.shape
    n_expert, n_hidden = lax.axis_size("expert"), lax.axis_size("hidden")
    experts = n_expert * w_up.shape[0]
    capacity = max(2, rows * 2 * 5 // (4 * experts))
    capacity = -(-capacity // 16) * 16
    total = experts * capacity
    heads = HEADS // n_hidden
    width = heads * HEAD_DIM
    g1, s1, g2, s2 = gain_one, shift_one, gain_two, shift_two
    router_t = w_router.T

    (
        all_tokens,
        qkv,
        att,
        att_t,
        w_t,
        g_in,
        x_slots,
        ups,
        weights,
        ids,
        pos,
        slot,
        count,
        inverse,
        residual,
        gates,
        gate_rows,
    ) = run_front(
        doc_lengths,
        expert_ids.T,
        g1,
        s1,
        g2,
        s2,
        router_t,
        tokens,
        out_grad,
        (w_query, w_key, w_value, w_out),
        w_up,
        capacity,
        heads,
        1,
    )
    dx_back, dg_back, y_out, dw_sum, dw_far = run_experts(
        x_slots, gate_rows, g_in, ups, w_up, w_down, 2
    )
    y_back, d_hidden, d_res, w_all, small, dw_own = run_back(
        ids,
        slot,
        pos,
        gates,
        count,
        g1,
        s1,
        g2,
        s2,
        router_t,
        inverse,
        dg_back,
        dx_back,
        y_out,
        dw_sum,
        dw_far,
        out_grad,
        residual,
        all_tokens,
        qkv,
        att,
        att_t,
        w_out,
        w_t,
        weights,
        3,
    )
    input_grad, output, full, small = run_tail(
        d_hidden,
        w_all.reshape(n_expert, 4 * width // n_expert, model),
        small,
        tokens,
        g1,
        d_res,
        residual,
        gates,
        pos,
        y_back.reshape(total, model),
        4,
    )
    scale = experts / (rows * n_expert * n_hidden * 2)
    turned = turn_weights(
        full.reshape(n_hidden, 4 * width, model),
        dw_own,
        small,
        input_grad,
        output,
        width,
        experts,
        scale,
    )
    w_grads, (up_grad, down_grad) = turned[:4], turned[4:6]
    gain_one_grad, shift_one_grad, gain_two_grad, shift_two_grad = turned[6:10]
    router_grad, input_grad, output, load = turned[10:]
    return (
        output,
        input_grad,
        gain_one_grad,
        shift_one_grad,
        *w_grads,
        gain_two_grad,
        shift_two_grad,
        router_grad.T,
        up_grad[None],
        down_grad[None],
        load,
    )


def solution(mesh):
    in_specs = (
        P(("expert", "hidden"), None),
        P("expert", None),
        P(("expert", "hidden"), None),
        P(),
        P(),
        P(),
        P(),
        P(),
        P(),
        P(),
        P(),
        P(),
        P("expert", None, "hidden"),
        P("expert", "hidden", None),
        P(("expert", "hidden"), None),
    )
    out_specs = (
        P(("expert", "hidden"), None),
        P(("expert", "hidden"), None),
        P(),
        P(),
        P(),
        P(),
        P(),
        P(),
        P(),
        P(),
        P(),
        P("expert", None, "hidden"),
        P("expert", "hidden", None),
        P(),
    )
    return jax.shard_map(shards, mesh=mesh, in_specs=in_specs, out_specs=out_specs, check_vma=False)
```

```python
from functools import partial

import jax
import jax.numpy as jnp
from jax import lax
from jax.experimental import pallas as pl
from jax.experimental.pallas import tpu as pltpu
from jax.sharding import PartitionSpec as P

HEAD_DIM = 64
HEADS = 12
EPSILON = 1e-05
SCALE = 0.125
MASKED = -1e30
BLOCK = 256
LONGEST = 1024
REACH = LONGEST // BLOCK + 1
UP_FIRST = 4
UP_EARLY = 6
UP_CROSS = 7
LANES = 128
BF = jnp.bfloat16
F32 = jnp.float32
I32 = jnp.int32
MESH = pl.DeviceIdType.MESH
ANY = pl.BlockSpec(memory_space=pl.ANY)
SMEM = pl.BlockSpec(memory_space=pltpu.SMEM)
VMEM = pl.BlockSpec(memory_space=pltpu.VMEM)
DMA = pltpu.SemaphoreType.DMA
GELU_A = 0.7978845608028654
GELU_B = 0.044715


def mm(left, right):
    return jnp.dot(left, right, preferred_element_type=F32)


def mm_nt(left, right):
    return lax.dot_general(left, right, (((1,), (1,)), ((), ())), preferred_element_type=F32)


def mm_tn(left, right):
    return lax.dot_general(left, right, (((0,), (0,)), ((), ())), preferred_element_type=F32)


def iota(shape, axis):
    return lax.broadcasted_iota(I32, shape, axis)


def norm_parts(values):
    centred = values - jnp.mean(values, axis=-1, keepdims=True)
    inverse = lax.rsqrt(jnp.mean(centred * centred, axis=-1, keepdims=True) + EPSILON)
    return centred * inverse, inverse


def norm_back(grad_out, normed, inverse, gain):
    grad_normed = grad_out * gain
    first = jnp.mean(grad_normed, axis=-1, keepdims=True)
    second = jnp.mean(grad_normed * normed, axis=-1, keepdims=True)
    return inverse * (grad_normed - first - normed * second)


def split_two(value):
    high = value.astype(BF)
    return high, (value - high.astype(F32)).astype(BF)


def row_at(ref, row):
    share = ref.shape[1]
    return row // share, slice(row % share, row % share + 1)


def shape_of(shape, dtype):
    return jax.ShapeDtypeStruct(shape, dtype)


def greet(peers):
    barrier = pltpu.get_barrier_semaphore()
    for peer in peers:
        pl.semaphore_signal(barrier, inc=1, device_id=peer, device_id_type=MESH)
    pl.semaphore_wait(barrier, len(peers))


def remote(src, dst, send, recv, peer):
    return pltpu.make_async_remote_copy(
        src_ref=src, dst_ref=dst, send_sem=send, recv_sem=recv, device_id=peer, device_id_type=MESH
    )


def doc_bounds(docs):
    ends, at = [], 0
    for n in range(docs.shape[1] - 1):
        at = at + docs[0, n]
        ends.append(at)
    return ends


def start_of(place, ends):
    begin = jnp.zeros_like(place)
    for end in ends:
        begin = jnp.where(place >= end, end, begin)
    return begin


def lying(ref):
    return ref[...].reshape(1, ref.shape[0])


def aligned(at, size):
    return pl.ds(pl.multiple_of(at, size), size)


def find_slots(experts, capacity, ids, ids_t, pos, slot, count):
    rows = ids_t.shape[1]
    row = [ids_t[j : j + 1, :] for j in range(2)]
    tall = jnp.concatenate([r.astype(F32) for r in row] + [jnp.zeros((6, rows), F32)], axis=0)
    ids[...] = tall.T[:, 0:2].astype(I32)
    col = [ids[:, j : j + 1] for j in range(2)]
    lane = iota((rows, LANES), 1)
    hot = [(lane == c).astype(BF) for c in col]
    either = hot[0] + hot[1]
    below = (iota((rows, rows), 0) > iota((rows, rows), 1)).astype(BF)
    before = mm(below, either)
    wide = max(experts, 16)
    deep = iota((wide, rows), 0)
    hot_t = [(deep == r).astype(BF) for r in row]
    above = (iota((rows, rows), 0) < iota((rows, rows), 1)).astype(BF)
    before_t = mm(hot_t[0] + hot_t[1], above)
    count[...] = jnp.sum(either.astype(F32), axis=0, keepdims=True)
    flat_t = []
    for j in range(2):
        at = jnp.sum(hot[j].astype(F32) * before, axis=1, keepdims=True).astype(I32)
        pos[:, j : j + 1] = col[j] * capacity + at
        slot[:, j : j + 1] = at
        at_t = jnp.sum(hot_t[j].astype(F32) * before_t, axis=0, keepdims=True).astype(I32)
        flat_t.append(row[j] * capacity + at_t)
    return flat_t


def fill_slots(flat_t, source, out):
    total, rows = out.shape[0], source.shape[0]
    half = total // 2
    for n in range(2):
        place = iota((half, rows), 0) + n * half
        pick = ((place == flat_t[0]) | (place == flat_t[1])).astype(BF)
        out[pl.ds(n * half, half), :] = mm(pick, source).astype(BF)


def attend_block(heads, ends, i, span, first, qkv, keys, scores, kept, inverse):
    width = heads * HEAD_DIM
    base = i * BLOCK
    rows = aligned(base, BLOCK)
    q_pos = base + iota((1, BLOCK), 1)
    begin = start_of(q_pos, ends)
    queries = [
        qkv[n * HEAD_DIM : (n + 1) * HEAD_DIM, rows] * jnp.asarray(SCALE, BF) for n in range(heads)
    ]
    tops = [jnp.full((1, BLOCK), MASKED, F32)] * heads
    for k in range(span):
        part = aligned((first + k) * BLOCK, BLOCK)
        k_pos = (first + k) * BLOCK + iota((BLOCK, BLOCK), 0)
        allowed = (k_pos <= q_pos) & (k_pos >= begin)
        for n in range(heads):
            score = jnp.where(allowed, mm(keys[n, part, :], queries[n]), MASKED)
            scores[n, k] = score
            tops[n] = jnp.maximum(tops[n], jnp.max(score, axis=0, keepdims=True))
    result = []
    for n in range(heads):
        total = jnp.zeros((1, BLOCK), F32)
        acc = jnp.zeros((HEAD_DIM, BLOCK), F32)
        lo = 2 * width + n * HEAD_DIM
        for k in range(span):
            weight = jnp.exp(scores[n, k] - tops[n])
            total = total + jnp.sum(weight, axis=0, keepdims=True)
            value = qkv[lo : lo + HEAD_DIM, aligned((first + k) * BLOCK, BLOCK)]
            low = weight.astype(BF)
            kept[n, k] = low
            acc = acc + mm(value, low)
        whole = 1.0 / total
        inverse[n : n + 1, rows] = whole
        result.append((acc * whole).astype(BF))
    return result


def spans(i, body):
    @pl.when(i < 2)
    def _short():
        body(2, 0)

    @pl.when(i >= 2)
    def _long():
        body(REACH, (i - (REACH - 1)) * (i // (REACH - 1)))


def front_body(
    n_e,
    n_h,
    experts,
    capacity,
    padded,
    heads,
    chunks,
    docs,
    ids_t,
    g1,
    s1,
    g2,
    s2,
    w_router,
    tokens,
    out_grad,
    w_query,
    w_key,
    w_value,
    w_out,
    w_up,
    all_tokens,
    qkv_out,
    att_out,
    att_t_out,
    w_t_out,
    g_in,
    x_slots,
    ups,
    weights,
    ids,
    pos,
    slot,
    count,
    inverse,
    residual,
    gates,
    gate_rows,
    tv,
    gv,
    wv,
    wo,
    w_t,
    qkv,
    keys,
    scores,
    kept,
    att_v,
    att_in,
    g_slots,
    xs_v,
    own_sem,
    w_sem,
    save_sem,
    kept_sem,
    ty_s,
    ty_r,
    tc_s,
    tc_r,
    tf_s,
    tf_r,
    gs_s,
    gs_r,
    at_s,
    at_r,
    wy_s,
    wy_r,
    wc_s,
    wc_r,
    wf_s,
    wf_r,
):
    e, h = lax.axis_index("expert"), lax.axis_index("hidden")
    far = n_h // 2
    pair, core = h // 2, lax.rem(h, 2)
    mate = pair * 2 + 1 - core
    rows, model = tokens.shape
    width = heads * HEAD_DIM
    per_device = rows // BLOCK
    ends = doc_bounds(docs)

    def across(t):
        return lax.rem(pair + t, far) * 2 + core

    def origin(t):
        return lax.rem(pair + far - t, far) * 2 + core

    own_tokens = pltpu.make_async_copy(tokens, tv.at[h], own_sem.at[0])
    own_grad = pltpu.make_async_copy(out_grad, gv, own_sem.at[1])
    own_grad.start()
    own_tokens.start()
    w_loads = [
        pltpu.make_async_copy(w, wv.at[n], w_sem.at[n])
        for n, w in enumerate((w_query, w_key, w_value))
    ]
    w_loads.append(pltpu.make_async_copy(w_out, wo, w_sem.at[3]))
    for load in w_loads:
        load.start()
    greet(
        [{"hidden": lax.rem(h + step, n_h)} for step in range(1, n_h)]
        + [{"expert": lax.rem(e + step, n_e)} for step in range(1, n_e)]
    )

    piece = rows // chunks
    sends = []
    for k in range(chunks):
        part = pl.ds(k * piece, piece)
        for t in range(1, far):
            copy = remote(
                tokens.at[part],
                tv.at[h, part],
                ty_s.at[t, k],
                ty_r.at[t, k],
                {"hidden": across(t)},
            )
            copy.start()
            sends.append(copy)
    beside = remote(tokens, tv.at[h], tc_s, tc_r, {"hidden": mate})
    beside.start()
    sends.append(beside)

    flat_t = find_slots(experts, capacity, ids, ids_t, pos, slot, count)
    own_grad.wait()
    fill_slots(flat_t, gv[...], g_slots)
    for step in range(1, n_e):
        peer = lax.rem(e + step, n_e)
        copy = remote(
            g_slots.at[aligned(peer * capacity, capacity)],
            g_in.at[e],
            gs_s.at[step],
            gs_r.at[step],
            {"expert": peer},
        )
        copy.start()
        sends.append(copy)
    own_slots = pltpu.make_async_copy(
        g_slots.at[aligned(e * capacity, capacity)], g_in.at[e], own_sem.at[1]
    )
    own_slots.start()

    def pass_on(t, k):
        part = pl.ds(k * piece, piece)
        place = tv.at[origin(t), part]
        remote(place, place, ty_s.at[t, k], ty_r.at[t, k], {"hidden": across(t)}).wait_recv()
        copy = remote(place, place, tf_s.at[t, k], tf_r.at[t, k], {"hidden": mate})
        copy.start()
        sends.append(copy)

    todo = [(t, k) for k in range(chunks) for t in range(1, far)]
    third = -(-len(todo) // 4)

    def pass_some():
        for _ in range(min(third, len(todo))):
            pass_on(*todo.pop(0))

    pick = (iota((width, model), 1) == iota((width, model), 0) + h * width).astype(BF)
    for n in range(3):
        w_loads[n].wait()
        w_t[n * width : (n + 1) * width, :] = mm_nt(pick, wv[n]).astype(BF)
        if n == 1:
            pass_some()
    save_w = pltpu.make_async_copy(w_t, w_t_out, save_sem.at[0])
    save_w.start()

    def project(source):
        def one(b, _):
            normed, _unused = norm_parts(tv[source, aligned(b * BLOCK, BLOCK), :].astype(F32))
            hidden = (normed * lying(g1) + lying(s1)).astype(BF)
            block = mm_nt(w_t[...], hidden)
            cols = aligned(source * rows + b * BLOCK, BLOCK)
            qkv[:, cols] = block.astype(BF)
            for n in range(heads):
                lo = width + n * HEAD_DIM
                keys[n, cols, :] = block[lo : lo + HEAD_DIM].T.astype(BF)
            return 0

        lax.fori_loop(0, per_device, one, 0)

    pass_some()
    own_tokens.wait()
    project(h)
    pass_some()
    remote(tokens, tv.at[mate], tc_s, tc_r, {"hidden": mate}).wait_recv()
    project(mate)
    while todo:
        pass_some()

    eighth = w_up.shape[1] // 8
    up_parts = (
        pl.ds(0, UP_FIRST * eighth),
        pl.ds(UP_FIRST * eighth, (UP_EARLY - UP_FIRST) * eighth),
    )

    def up_copy(t, k, source):
        return remote(
            w_up.at[0, up_parts[k]],
            ups.at[source, up_parts[k]],
            wy_s.at[t, k],
            wy_r.at[t, k],
            {"hidden": across(t)},
        )

    def up_onward(t, k):
        place = ups.at[origin(t), up_parts[k]]
        return remote(place, place, wf_s.at[t, k], wf_r.at[t, k], {"hidden": mate})

    def up_arrived(k):
        for t in range(1, far):
            up_copy(t, k, origin(t)).wait_recv()
            up_onward(t, k).start()

    up_beside = remote(w_up.at[0], ups.at[h], wc_s, wc_r, {"hidden": mate})
    up_beside.start()
    sends.append(up_beside)
    for t in range(1, far):
        up_copy(t, 0, h).start()
    for t in range(1, far):
        project(origin(t))
    for t in range(1, far):
        there = lax.rem(pair + far - t, far) * 2 + 1 - core
        for k in range(chunks):
            place = tv.at[there, pl.ds(k * piece, piece)]
            remote(place, place, tf_s.at[t, k], tf_r.at[t, k], {"hidden": mate}).wait_recv()
        project(there)
    save_tokens = pltpu.make_async_copy(tv, all_tokens, save_sem.at[1])
    save_qkv = pltpu.make_async_copy(qkv, qkv_out, save_sem.at[2])
    save_tokens.start()
    save_qkv.start()

    inverse[...] = jnp.zeros_like(inverse)

    def device_at(n, sign):
        t, other = n // 2, lax.rem(n, 2)
        return lax.rem(pair + far + sign * t, far) * 2 + lax.rem(core + other, 2)

    def give_att(n):
        owner = device_at(n, 1)
        return remote(
            att_v.at[owner], att_in.at[h], at_s.at[n], at_r.at[n], {"hidden": owner}
        )

    def save_kept(i, turn):
        return pltpu.make_async_copy(kept.at[turn], weights.at[i], kept_sem.at[turn])

    def attend(at, _):
        n = n_h - 1 - at // per_device
        b = lax.rem(at, per_device)
        owner = device_at(n, 1)
        i = owner * per_device + b
        turn = lax.rem(at, 2)

        @pl.when(at >= 2)
        def _free():
            save_kept(i, turn).wait()

        def block(span, first):
            done = attend_block(
                heads, ends, i, span, first, qkv, keys, scores, kept.at[turn], inverse
            )
            for m in range(heads):
                lo = m * HEAD_DIM
                att_v[owner, lo : lo + HEAD_DIM, aligned(b * BLOCK, BLOCK)] = done[m]

        spans(i, block)
        save_kept(i, turn).start()

        @pl.when((b == per_device - 1) & (n > 0))
        def _give():
            give_att(n).start()

        @pl.when(at == (n_h - 2) * per_device - 1)
        def _more():
            for t in range(1, far):
                up_copy(t, 1, h).start()

        return 0

    lax.fori_loop(0, n_h * per_device, attend, 0)
    up_arrived(0)
    att_in[h] = att_v[h]
    save_att = pltpu.make_async_copy(att_v, att_out, save_sem.at[3])
    save_att.start()
    for n in range(n_h - 1, 0, -1):
        give_att(n).wait_recv()
    save_att_t = pltpu.make_async_copy(att_in, att_t_out, save_sem.at[4])
    save_att_t.start()

    w_loads[3].wait()
    res = tv[h].astype(F32) + mm_tn(att_in[...].reshape(model, rows), wo[...])
    residual[...] = res
    normed, _unused = norm_parts(res)
    hidden = (normed * lying(g2) + lying(s2)).astype(BF)
    fill_slots(flat_t, hidden, xs_v)
    save_x = [
        pltpu.make_async_copy(
            xs_v.at[pl.ds(n * capacity, capacity)], x_slots.at[n], save_sem.at[5 + n]
        )
        for n in range(experts)
    ]
    for save in save_x:
        save.start()
    logits = mm_nt(hidden, w_router[...])
    lane = iota((rows, experts), 1)
    chosen = [
        jnp.sum(jnp.where(lane == ids[:, j : j + 1], logits, 0.0), axis=1, keepdims=True)
        for j in range(2)
    ]
    top = jnp.maximum(chosen[0], chosen[1])
    raised = [jnp.exp(c - top) for c in chosen]
    both = raised[0] + raised[1]
    gate = [r / both for r in raised]
    for j in range(2):
        gates[:, j : j + 1] = gate[j]
    column = iota((rows, padded), 1)
    for n in range(experts):
        mix = jnp.zeros((rows, padded), F32)
        for j in range(2):
            here = jnp.where(ids[:, j : j + 1] == n, slot[:, j : j + 1], -1) == column
            mix = jnp.where(here, gate[j], mix)
        line = jnp.sum(mix, axis=0, keepdims=True)
        gate_rows[n] = jnp.broadcast_to(line, (8, padded))

    place = ups.at[mate]
    remote(place, place, wc_s, wc_r, {"hidden": mate}).wait_recv()
    up_arrived(1)
    for t in range(1, far):
        for k in range(2):
            up_onward(t, k).wait()
    for step in range(1, n_e):
        source = lax.rem(e + n_e - step, n_e)
        place = g_in.at[source]
        remote(place, place, gs_s.at[step], gs_r.at[step], {"expert": e}).wait_recv()
    own_slots.wait()
    for n in range(1, n_h):
        give_att(n).wait_send()
    for turn in range(2):
        save_kept(0, turn).wait()
    for t in range(1, far):
        for k in range(2):
            up_copy(t, k, h).wait_send()
    for copy in sends:
        copy.wait_send()
    for save in [save_w, save_tokens, save_qkv, save_att, save_att_t, *save_x]:
        save.wait()


def run_front(
    docs, ids_t, g1, s1, g2, s2, w_router, tokens, out_grad, ws, w_up, capacity, heads, cid
):
    n_e, n_h = lax.axis_size("expert"), lax.axis_size("hidden")
    experts = n_e * w_up.shape[0]
    rows, model = tokens.shape
    padded = -(-capacity // LANES) * LANES
    width, group, total = heads * HEAD_DIM, rows * n_h, experts * capacity
    far, chunks = n_h // 2, 8

    def pairs(*shape):
        return [DMA(shape), DMA(shape)]

    return pl.pallas_call(
        partial(front_body, n_e, n_h, experts, capacity, padded, heads, chunks),
        name="front",
        out_shape=[
            shape_of((n_h, rows, model), BF),
            shape_of((3 * width, group), BF),
            shape_of((n_h, width, rows), BF),
            shape_of((n_h, width, rows), BF),
            shape_of((3 * width, model), BF),
            shape_of((experts, capacity, model), BF),
            shape_of((experts, capacity, model), BF),
            shape_of((n_h, *w_up.shape[1:]), BF),
            shape_of((group // BLOCK, heads, REACH, BLOCK, BLOCK), BF),
            shape_of((rows, 2), I32),
            shape_of((rows, 2), I32),
            shape_of((rows, 2), I32),
            shape_of((1, LANES), F32),
            shape_of((8, group), F32),
            shape_of((rows, model), F32),
            shape_of((rows, 2), F32),
            shape_of((experts, 8, padded), F32),
        ],
        in_specs=[SMEM] + [VMEM] * 6 + [ANY] * 7,
        out_specs=[ANY] * 9 + [VMEM] * 8,
        scratch_shapes=[
            pltpu.VMEM((n_h, rows, model), BF),
            pltpu.VMEM((rows, model), BF),
            pltpu.VMEM((3, model, model), BF),
            pltpu.VMEM((model, model), BF),
            pltpu.VMEM((3 * width, model), BF),
            pltpu.VMEM((3 * width, group), BF),
            pltpu.VMEM((heads, group, HEAD_DIM), BF),
            pltpu.VMEM((heads, REACH, BLOCK, BLOCK), F32),
            pltpu.VMEM((2, heads, REACH, BLOCK, BLOCK), BF),
            pltpu.VMEM((n_h, width, rows), BF),
            pltpu.VMEM((n_h, width, rows), BF),
            pltpu.VMEM((total, model), BF),
            pltpu.VMEM((total, model), BF),
            DMA((2,)),
            DMA((4,)),
            DMA((5 + experts,)),
            DMA((2,)),
            *pairs(far, chunks),
            DMA,
            DMA,
            *pairs(far, chunks),
            *pairs(n_e),
            *pairs(n_h),
            *pairs(far, 2),
            DMA,
            DMA,
            *pairs(far, 2),
        ],
        compiler_params=pltpu.CompilerParams(
            collective_id=cid, has_side_effects=True, vmem_limit_bytes=58 << 20
        ),
    )(docs, ids_t, g1, s1, g2, s2, w_router, tokens, out_grad, *ws, w_up)


def moe_body(
    size,
    capacity,
    padded,
    per,
    x_slots,
    gate_rows,
    g_in,
    ups,
    w_up,
    w_down,
    dx_back,
    dg_back,
    y_out,
    dw_sum,
    dw_far,
    xv,
    gv,
    gates_v,
    up_v,
    down_v,
    act,
    dz,
    xg,
    dy,
    xg_t,
    dy_t,
    dxv,
    yv,
    dgv,
    y_acc,
    dx_acc,
    dw_box,
    load_sem,
    save_sem,
    wy_s,
    wy_r,
    wc_s,
    wc_r,
    wf_s,
    wf_r,
    dc_s,
    dc_r,
    df_s,
    df_r,
    g_sem,
    own_sem,
    xs_sem,
    xr_sem,
    gs_sem,
    gr_sem,
    ds_sem,
    dr_sem,
    ts_sem,
    tr_sem,
    out_sem,
):
    me, h = lax.axis_index("expert"), lax.axis_index("hidden")
    shards_n = ups.shape[0]
    far = shards_n // 2
    pair, core = h // 2, lax.rem(h, 2)
    mate = pair * 2 + 1 - core
    deep = w_down.shape[1] // 2
    tall = per * capacity
    steps = size // per

    middle = size // 2
    inner = lax.rem((me // 2 * 8 // size + 1) // 2, 2)

    def group_at(step):
        some = steps // 4
        early = jnp.where(step <= some, step - 1 + steps // 2, step - some)
        early = jnp.where((step > 0) & (step < steps - some), early, step)
        return jnp.where(inner == 1, early, step)

    def peer_at(p):
        peer, bit = 0, 1
        while bit < size:
            peer = peer + lax.rem(me // bit + p // bit, 2) * bit
            bit *= 2
        return peer

    def rows_of(p):
        return pl.ds(pl.multiple_of(p * capacity, capacity), capacity)

    def send_x(p):
        peer = peer_at(p)
        return remote(
            x_slots.at[peer], xv.at[rows_of(p)], xs_sem.at[p], xr_sem.at[p], {"expert": peer}
        )

    def send_gate(p):
        peer = peer_at(p)
        return remote(
            gate_rows.at[peer], gates_v.at[p], gs_sem.at[p], gr_sem.at[p], {"expert": peer}
        )

    def send_dx(p):
        peer = peer_at(p)
        return remote(
            dxv.at[rows_of(p)], dx_back.at[me], ds_sem.at[p], dr_sem.at[p], {"expert": peer}
        )

    def send_dg(p):
        peer = peer_at(p)
        return remote(dgv.at[p], dg_back.at[me], ts_sem.at[p], tr_sem.at[p], {"expert": peer})

    def load_g(p):
        return pltpu.make_async_copy(g_in.at[peer_at(p)], gv.at[rows_of(p)], g_sem.at[p])

    def save_y(p):
        return pltpu.make_async_copy(yv.at[rows_of(p)], y_out.at[peer_at(p)], out_sem.at[p])

    own_x = pltpu.make_async_copy(x_slots.at[me], xv.at[rows_of(0)], own_sem.at[0])
    own_gate = pltpu.make_async_copy(gate_rows.at[me], gates_v.at[0], own_sem.at[1])
    own_dx = pltpu.make_async_copy(dxv.at[rows_of(0)], dx_back.at[me], own_sem.at[2])
    own_dg = pltpu.make_async_copy(dgv.at[0], dg_back.at[me], own_sem.at[3])
    loads = [
        pltpu.make_async_copy(w_up.at[0], up_v.at[h], load_sem.at[0]),
        pltpu.make_async_copy(w_down.at[0], down_v.at[h], load_sem.at[1]),
    ]
    loads.append(pltpu.make_async_copy(ups.at[mate], up_v.at[mate], load_sem.at[2]))

    early = w_up.shape[1] * UP_EARLY // 8

    def half(k):
        return aligned(k * deep, deep)

    for t in range(1, far):
        for other in range(2):
            c = lax.rem(pair + t, far) * 2 + other
            place = (c, pl.ds(0, early))
            loads.append(
                pltpu.make_async_copy(
                    ups.at[place], up_v.at[place], load_sem.at[1 + 2 * t + other]
                )
            )
    rest = pl.ds(early, w_up.shape[1] - early)
    parts = ((w_up, up_v, rest), (w_down, down_v, half(0)), (w_down, down_v, half(1)))

    def part_across(t, n):
        source, target, k = parts[n]
        there = {"hidden": lax.rem(pair + t, far) * 2 + core}
        return remote(
            source.at[0, k], target.at[h, k], wy_s.at[t, n], wy_r.at[t, n], there
        )

    def part_onward(t, n):
        _source, target, k = parts[n]
        place = target.at[lax.rem(pair + far - t, far) * 2 + core, k]
        return remote(place, place, wf_s.at[t, n], wf_r.at[t, n], {"hidden": mate})

    down_beside = remote(w_down.at[0], down_v.at[h], wc_s, wc_r, {"hidden": mate})
    own_x.start()
    own_gate.start()
    for p in range(size):
        load_g(p).start()
    for load in loads:
        load.start()
    greet(
        [{"expert": lax.rem(me + step, size)} for step in range(1, size)]
        + [{"hidden": lax.rem(h + step, shards_n)} for step in range(1, shards_n)]
    )

    def send_all(order):
        for p in order:
            send_x(p).start()
            send_gate(p).start()

    @pl.when(inner == 1)
    def _far_first():
        send_all([1, *range(middle, size), *range(2, middle)])

    @pl.when(inner == 0)
    def _near_first():
        send_all(range(1, size))

    for n in range(3):
        for t in range(1, far):
            part_across(t, n).start()
    down_beside.start()
    own_x.wait()
    own_gate.wait()
    for load in loads:
        load.wait()

    def finish(base, rows, held):
        dxv[rows, :] = dx_acc[held, :].astype(BF)
        y_low = y_acc[held, :].astype(BF)
        yv[rows, :] = y_low
        x, g = xv[rows, :], gv[rows, :]
        dots = jnp.sum(y_low.astype(F32) * g.astype(F32), axis=1, keepdims=True)
        for s in range(per):
            p = base + s
            part = slice(s * capacity, (s + 1) * capacity)
            tall_dots = jnp.broadcast_to(dots[part], (capacity, LANES))
            if padded > capacity:
                blank = jnp.zeros((padded - capacity, LANES), F32)
                tall_dots = jnp.concatenate([tall_dots, blank], axis=0)
            dgv[p] = tall_dots.T[0:8]

            @pl.when(p > 0)
            def _give(p=p):
                send_dx(p).start()
                send_dg(p).start()

            @pl.when(p == 0)
            def _keep():
                own_dx.start()
                own_dg.start()

            save_y(p).start()
        for s in range(per):
            p = base + s
            part = slice(s * capacity, (s + 1) * capacity)
            gate = gates_v[p].T[0:capacity, 0:1]
            xg[rows_of(p), :] = (x[part].astype(F32) * gate).astype(BF)
            dy[rows_of(p), :] = (g[part].astype(F32) * gate).astype(BF)

    first = shards_n // 2

    def unit(m):
        step = jnp.where(m < 2 * shards_n, lax.rem(m // first, 2), m // shards_n)
        n = m // shards_n * first + lax.rem(m, first)
        n = jnp.where(m < 2 * shards_n, n, lax.rem(m, shards_n))
        return step, n

    def unit_body(m, _):
        step, n = unit(m)
        base = group_at(step) * per
        rows = pl.ds(pl.multiple_of(base * capacity, tall), tall)
        held = aligned(jnp.where(step == 1, tall, 0), tall)

        @pl.when(n == 0)
        def _begin():
            for s in range(per):

                @pl.when(base + s > 0)
                def _arrive(s=s):
                    send_x(base + s).wait_recv()
                    send_gate(base + s).wait_recv()

                load_g(base + s).wait()
            y_acc[held, :] = jnp.zeros((tall, y_acc.shape[1]), F32)
            dx_acc[held, :] = jnp.zeros((tall, y_acc.shape[1]), F32)

        t = n // 2
        beside = lax.rem(n, 2)
        c = lax.rem(pair + far - t, far) * 2 + lax.rem(core + beside, 2)

        @pl.when(m == 1)
        def _beside():
            down_beside.wait_recv()

        @pl.when((step == 0) & (n >= 2) & (beside == 0))
        def _across():
            for k in range(3):
                part_across(t, k).wait_recv()
                part_onward(t, k).start()

        @pl.when((step == 0) & (n >= 2) & (beside == 1))
        def _onward():
            for k in range(3):
                part_onward(t, k).wait_recv()

        x, g = xv[rows, :], gv[rows, :]
        z = mm(x, up_v[c])
        du = mm_nt(g, down_v[c])
        square = z * z
        curve = jnp.tanh(z * (GELU_A + GELU_A * GELU_B * square))
        plus = 0.5 + 0.5 * curve
        hidden = (z * plus).astype(BF)
        rise = GELU_A + 3.0 * GELU_A * GELU_B * square
        slope = plus + 0.5 * z * (1.0 - curve * curve) * rise
        back = (slope * du).astype(BF)
        act[c, rows, :] = hidden
        dz[c, rows, :] = back
        y_acc[held, :] += mm(hidden, down_v[c])
        dx_acc[held, :] += mm_nt(back, up_v[c])

        @pl.when(n == shards_n - 1)
        def _end():
            finish(base, rows, held)

        return 0

    lax.fori_loop(0, steps * shards_n, unit_body, 0)

    total = size * capacity
    turn = 256
    for k in range(total // turn):
        rows = slice(k * turn, (k + 1) * turn)
        xg_t[:, rows] = xg[rows, :].astype(F32).T.astype(BF)
    for t in range(1, far):
        for k in range(3):
            part_across(t, k).wait_send()
            part_onward(t, k).wait_send()
    down_beside.wait_send()

    def give(which, step):
        source = (up_v, down_v)[which].at[lax.rem(pair + step, far) * 2 + 1 - core]
        return remote(
            source,
            dw_box.at[which, step],
            dc_s.at[which, step],
            dc_r.at[which, step],
            {"hidden": mate},
        )

    def keep(which, step):
        source = (up_v, down_v)[which].at[lax.rem(pair + step, far) * 2 + core]
        return pltpu.make_async_copy(source, dw_sum.at[which, step], save_sem.at[which, step])

    middle_row = up_v.shape[1] // 2
    cross_parts = (pl.ds(0, middle_row), pl.ds(middle_row, dw_far.shape[1] - middle_row))

    def cross(step, k):
        there = lax.rem(pair + step, far) * 2 + core
        return remote(
            up_v.at[there, cross_parts[k]],
            dw_far.at[step - 1, cross_parts[k]],
            df_s.at[step, k],
            df_r.at[step, k],
            {"hidden": there},
        )

    def gradients(which, left, right, held):
        def other(n, _):
            step = lax.rem(n + 1, far)
            c = lax.rem(pair + step, far) * 2 + 1 - core
            held[c] = mm(left[...], right[c]).astype(BF)
            give(which, step).start()
            return 0

        def own(n, _):
            step = lax.rem(n + 1, far)
            c = lax.rem(pair + step, far) * 2 + core
            total_of = mm(left[...], right[c])
            give(which, step).wait_recv()
            held[c] = (total_of + dw_box[which, step].astype(F32)).astype(BF)
            keep(which, step).start()

            if which == 0:

                @pl.when(step > 0)
                def _cross():
                    for k in range(2):
                        cross(step, k).start()

            return 0

        lax.fori_loop(0, far, other, 0)
        lax.fori_loop(0, far, own, 0)

    gradients(0, xg_t, dz, up_v)
    for k in range(total // turn):
        rows = slice(k * turn, (k + 1) * turn)
        dy_t[:, rows] = dy[rows, :].astype(F32).T.astype(BF)
    gradients(1, dy_t, act, down_v)
    for p in range(1, size):
        send_x(p).wait_send()
        send_gate(p).wait_send()
        send_dx(p).wait()
        send_dg(p).wait()
    for p in range(size):
        save_y(p).wait()
    own_dx.wait()
    own_dg.wait()
    for step in range(far):
        for which in range(2):
            give(which, step).wait_send()
            keep(which, step).wait()
    for step in range(1, far):
        for k in range(2):
            cross(step, k).wait()


def run_experts(x_slots, gate_rows, g_in, ups, w_up, w_down, cid):
    size = lax.axis_size("expert")
    experts, capacity, model = x_slots.shape
    padded = gate_rows.shape[2]
    shards_n, _unused, width = ups.shape
    total = experts * capacity
    per = 1
    while per * 2 * capacity <= 320 and size % (per * 2) == 0:
        per *= 2
    tall = per * capacity
    rows2 = (total, model)
    return pl.pallas_call(
        partial(moe_body, size, capacity, padded, per),
        name="experts",
        out_shape=[
            shape_of(x_slots.shape, BF),
            shape_of(gate_rows.shape, F32),
            shape_of(x_slots.shape, BF),
            shape_of((2, shards_n // 2, model, width), BF),
            shape_of((shards_n // 2 - 1, model * UP_CROSS // 8, width), BF),
        ],
        in_specs=[ANY] * 6,
        out_specs=[ANY] * 5,
        scratch_shapes=[
            pltpu.VMEM(rows2, BF),
            pltpu.VMEM(rows2, BF),
            pltpu.VMEM(gate_rows.shape, F32),
            pltpu.VMEM((shards_n, model, width), BF),
            pltpu.VMEM((shards_n, width, model), BF),
            pltpu.VMEM((shards_n, total, width), BF),
            pltpu.VMEM((shards_n, total, width), BF),
            pltpu.VMEM(rows2, BF),
            pltpu.VMEM(rows2, BF),
            pltpu.VMEM((model, total), BF),
            pltpu.VMEM((model, total), BF),
            pltpu.VMEM(rows2, BF),
            pltpu.VMEM(rows2, BF),
            pltpu.VMEM(gate_rows.shape, F32),
            pltpu.VMEM((2 * tall, model), F32),
            pltpu.VMEM((2 * tall, model), F32),
            pltpu.VMEM((2, shards_n // 2, model, width), BF),
            DMA((shards_n + 1,)),
            DMA((2, shards_n // 2)),
            DMA((shards_n // 2, 3)),
            DMA((shards_n // 2, 3)),
            DMA,
            DMA,
            DMA((shards_n // 2, 3)),
            DMA((shards_n // 2, 3)),
            DMA((2, shards_n // 2)),
            DMA((2, shards_n // 2)),
            DMA((shards_n // 2, 2)),
            DMA((shards_n // 2, 2)),
            DMA((size,)),
            DMA((4,)),
        ]
        + [DMA((size,))] * 9,
        compiler_params=pltpu.CompilerParams(
            collective_id=cid, has_side_effects=True, vmem_limit_bytes=60 << 20
        ),
        cost_estimate=pl.CostEstimate(
            flops=12 * total * model * width * shards_n, bytes_accessed=40 << 20, transcendentals=0
        ),
    )(x_slots, gate_rows, g_in, ups, w_up, w_down)


def tail_body(
    n_e,
    n_h,
    chunks,
    dh,
    w_all,
    small,
    tokens,
    gain,
    d_res,
    residual,
    gates,
    pos,
    y_back,
    input_grad,
    output,
    full,
    total,
    wv,
    tok_v,
    d_res_v,
    res_v,
    yv,
    mine,
    beside,
    across,
    passing,
    x_box,
    z_box,
    w_mid,
    piece,
    small_mid,
    small_h,
    small_e,
    small_all,
    load_sem,
    mine_sem,
    cs_sem,
    cr_sem,
    as_sem,
    ar_sem,
    ws_sem,
    wr_sem,
    vs_sem,
    vr_sem,
    hs_sem,
    hr_sem,
    es_sem,
    er_sem,
    bs_sem,
    br_sem,
    keep_sem,
    zs_sem,
    zr_sem,
    xs_sem,
    xr_sem,
    ys_sem,
    yr_sem,
    ms_sem,
    mr_sem,
):
    e, h = lax.axis_index("expert"), lax.axis_index("hidden")
    far, high = n_h // 2, n_e // 2
    pair, core = h // 2, lax.rem(h, 2)
    eh, el = e // 2, lax.rem(e, 2)
    mate = pair * 2 + 1 - core
    greet(
        [{"expert": lax.rem(e + step, n_e)} for step in range(1, n_e)]
        + [{"hidden": lax.rem(h + step, n_h)} for step in range(1, n_h)]
    )
    w_sends, w_order = {}, list(range(1, high)) + [0]
    for step in w_order:
        there = lax.rem(eh + step, high)
        copy = remote(
            w_all.at[there * 2 + 1 - el],
            x_box.at[step],
            ws_sem.at[step],
            wr_sem.at[step],
            {"expert": eh * 2 + 1 - el},
        )
        copy.start()
        w_sends[step] = copy
    small_sends = []
    for at in range(n_h - 1):
        peer = lax.rem(h + 1 + at, n_h)
        copy = remote(
            small.at[peer], small_h.at[at], hs_sem.at[at], hr_sem.at[at], {"hidden": peer}
        )
        copy.start()
        small_sends.append(copy)
    rows = dh.shape[1] // chunks
    core_sends = {}
    for step in list(range(1, far)) + [0]:
        there = lax.rem(pair + step, far)
        for k in range(chunks):
            part = pl.ds(k * rows, rows)
            copy = remote(
                dh.at[there * 2 + 1 - core, part],
                beside.at[step, part],
                cs_sem.at[step, k],
                cr_sem.at[step, k],
                {"hidden": mate},
            )
            copy.start()
            core_sends[step, k] = copy
    mine_loads = []
    for step in range(far):
        there = lax.rem(pair + step, far)
        load = pltpu.make_async_copy(dh.at[there * 2 + core], mine.at[step], mine_sem.at[step])
        load.start()
        mine_loads.append(load)
    loads = [
        pltpu.make_async_copy(source, target, load_sem.at[n])
        for n, (source, target) in enumerate(
            ((w_all, wv), (residual, res_v), (y_back, yv), (tokens, tok_v), (d_res, d_res_v))
        )
    ]
    for load in loads:
        load.start()
    for load in mine_loads:
        load.wait()
    far_sends = []
    for step in range(1, far):
        there = lax.rem(pair + step, far)
        for k in range(chunks):
            part = pl.ds(k * rows, rows)
            core_sends[step, k].wait_recv()
            both = mine[step, part, :].astype(F32) + beside[step, part, :].astype(F32)
            passing[step - 1, part, :] = both.astype(BF)
            copy = remote(
                passing.at[step - 1, part],
                across.at[step - 1, part],
                as_sem.at[step - 1, k],
                ar_sem.at[step - 1, k],
                {"hidden": there * 2 + core},
            )
            copy.start()
            far_sends.append(copy)
    loads[0].wait()
    v_sends = []
    for step in w_order[:-1]:
        there = lax.rem(eh + step, high) * 2 + el
        w_sends[step].wait_recv()
        w_mid[step - 1] = (wv[there].astype(F32) + x_box[step].astype(F32)).astype(BF)
        copy = remote(
            w_mid.at[step - 1],
            z_box.at[step - 1],
            vs_sem.at[step],
            vr_sem.at[step],
            {"expert": there},
        )
        copy.start()
        v_sends.append(copy)
    summed = small[h]
    for at, copy in enumerate(small_sends):
        copy.wait_recv()
        summed = summed + small_h[at]
    small_mid[...] = summed
    small_out = []
    for at in range(n_e - 1):
        peer = lax.rem(e + 1 + at, n_e)
        copy = remote(small_mid, small_e.at[at], es_sem.at[at], er_sem.at[at], {"expert": peer})
        copy.start()
        small_out.append(copy)
    w_sends[0].wait_recv()
    acc = wv[e].astype(F32) + x_box[0].astype(F32)
    for at, copy in enumerate(v_sends):
        copy.wait_recv()
        acc = acc + z_box[at].astype(F32)
    piece[...] = acc.astype(BF)
    keep = pltpu.make_async_copy(piece, full.at[h, e], keep_sem)
    keep.start()

    def spot(t, s, flag, core_of):
        eh_of = lax.rem(eh + high - s, high)
        el_of = el if flag == 0 else 1 - el
        return full.at[lax.rem(pair + far - t, far) * 2 + core_of, eh_of * 2 + el_of]

    def held(t, s, flag):
        return piece if (t, s, flag) == (0, 0, 0) else spot(t, s, flag, core)

    def along(t, s):
        there = {"expert": lax.rem(eh + s, high) * 2 + el}
        return remote(held(t, 0, 0), spot(t, 0, 0, core), zs_sem.at[t, s], zr_sem.at[t, s], there)

    def aside(t, s):
        there = {"expert": eh * 2 + 1 - el}
        return remote(held(t, s, 0), spot(t, s, 0, core), xs_sem.at[t, s], xr_sem.at[t, s], there)

    def over(t, s, flag):
        there = {"hidden": lax.rem(pair + t, far) * 2 + core}
        at = 2 * s + flag
        return remote(
            held(0, s, flag), spot(0, s, flag, core), ys_sem.at[t, at], yr_sem.at[t, at], there
        )

    def to_mate(t, s, flag):
        at = 2 * s + flag
        return remote(
            held(t, s, flag),
            spot(t, s, flag, core),
            ms_sem.at[t, at],
            mr_sem.at[t, at],
            {"hidden": mate},
        )

    line_order = list(range(1, high))
    pieces = [(s, flag) for s in range(high) for flag in range(2)]
    first, second = core == 0, core == 1

    @pl.when(first)
    def _spread_first():
        for s in line_order:
            along(0, s).start()
        aside(0, 0).start()
        for t in range(1, far):
            over(t, 0, 0).start()
        to_mate(0, 0, 0).start()

        def take_aside(s):
            aside(0, s).wait_recv()
            for t in range(1, far):
                over(t, s, 1).start()
            to_mate(0, s, 1).start()

        for s in line_order:
            along(0, s).wait_recv()
            aside(0, s).start()
            for t in range(1, far):
                over(t, s, 0).start()
            to_mate(0, s, 0).start()
            take_aside(s - 1)
        take_aside(high - 1)

    @pl.when(second)
    def _spread_second():
        for t in range(1, far):
            over(t, 0, 0).start()
        for s in line_order:
            along(0, s).start()
        aside(0, 0).start()
        to_mate(0, 0, 0).start()
        for t in range(1, far):
            over(t, 0, 0).wait_recv()
            for s in line_order:
                along(t, s).start()
            aside(t, 0).start()
            to_mate(t, 0, 0).start()
        for s in line_order:
            for t in range(far):
                along(t, s).wait_recv()
                aside(t, s).start()
                to_mate(t, s, 0).start()

    summed = small_mid[...]
    for at, copy in enumerate(small_out):
        copy.wait_recv()
        summed = summed + small_e[at]
    small_all[h] = summed
    small_back = []
    for at in range(n_h - 1):
        peer = lax.rem(h + 1 + at, n_h)
        copy = remote(
            small_all.at[h], small_all.at[h], bs_sem.at[at], br_sem.at[at], {"hidden": peer}
        )
        copy.start()
        small_back.append(copy)
    for load in loads[1:]:
        load.wait()
    place_of = iota((residual.shape[0], y_back.shape[0]), 1)
    result = res_v[...]
    for j in range(2):
        pick = (place_of == pos[:, j : j + 1]).astype(BF)
        result = result + gates[:, j : j + 1] * mm(pick, yv[...])
    output[...] = result.astype(BF)
    for k in range(chunks):
        part = pl.ds(k * rows, rows)
        core_sends[0, k].wait_recv()
    for copy in far_sends:
        copy.wait_recv()
    grad = mine[0].astype(F32) + beside[0].astype(F32)
    for step in range(far - 1):
        grad = grad + across[step].astype(F32)
    normed, inverse = norm_parts(tok_v[...].astype(F32))
    input_grad[...] = (d_res_v[...] + norm_back(grad, normed, inverse, lying(gain))).astype(BF)
    @pl.when(first)
    def _finish_first():
        for t in range(1, far):
            for s, flag in pieces:
                over(t, s, flag).wait_recv()
                to_mate(t, s, flag).start()

    @pl.when(second)
    def _finish_second():
        for s in range(high):
            for t in range(far):
                aside(t, s).wait_recv()
                to_mate(t, s, 1).start()

    for copy in small_back:
        copy.wait_recv()
    total[...] = small_all[...]
    for t in range(far):
        for s, flag in pieces:
            to_mate(t, s, flag).wait()
    keep.wait()

    @pl.when(first)
    def _sent_first():
        for s in line_order:
            along(0, s).wait_send()
        for s in range(high):
            aside(0, s).wait_send()
        for t in range(1, far):
            for s, flag in pieces:
                over(t, s, flag).wait_send()

    @pl.when(second)
    def _sent_second():
        for t in range(1, far):
            over(t, 0, 0).wait_send()
        for t in range(far):
            for s in line_order:
                along(t, s).wait_send()
            for s in range(high):
                aside(t, s).wait_send()

    for copy in [*w_sends.values(), *v_sends, *small_sends, *small_out, *small_back, *far_sends]:
        copy.wait_send()
    for copy in core_sends.values():
        copy.wait_send()


def run_tail(dh, w_all, small, tokens, gain, d_res, residual, gates, pos, y_back, cid):
    n_e, n_h = lax.axis_size("expert"), lax.axis_size("hidden")
    far, high = n_h // 2, n_e // 2
    chunks = 4
    _unused, rows, model = dh.shape
    piece = w_all.shape[1:]
    return pl.pallas_call(
        partial(tail_body, n_e, n_h, chunks),
        name="tail",
        out_shape=[
            shape_of((rows, model), BF),
            shape_of((rows, model), BF),
            shape_of((n_h, n_e, *piece), BF),
            shape_of(small.shape, F32),
        ],
        in_specs=[ANY, ANY, VMEM, ANY, VMEM, ANY, ANY, VMEM, VMEM, ANY],
        out_specs=[VMEM, VMEM, ANY, VMEM],
        scratch_shapes=[
            pltpu.VMEM(w_all.shape, BF),
            pltpu.VMEM(tokens.shape, BF),
            pltpu.VMEM(d_res.shape, F32),
            pltpu.VMEM(residual.shape, F32),
            pltpu.VMEM(y_back.shape, BF),
            pltpu.VMEM((far, rows, model), BF),
            pltpu.VMEM((far, rows, model), BF),
            pltpu.VMEM((far - 1, rows, model), BF),
            pltpu.VMEM((far - 1, rows, model), BF),
            pltpu.VMEM((high, *piece), BF),
            pltpu.VMEM((high - 1, *piece), BF),
            pltpu.VMEM((high - 1, *piece), BF),
            pltpu.VMEM(piece, BF),
            pltpu.VMEM(small.shape[1:], F32),
            pltpu.VMEM((n_h - 1, *small.shape[1:]), F32),
            pltpu.VMEM((n_e - 1, *small.shape[1:]), F32),
            pltpu.VMEM(small.shape, F32),
            DMA((5,)),
            DMA((far,)),
            DMA((far, chunks)),
            DMA((far, chunks)),
            DMA((far - 1, chunks)),
            DMA((far - 1, chunks)),
            DMA((high,)),
            DMA((high,)),
            DMA((high,)),
            DMA((high,)),
            DMA((n_h - 1,)),
            DMA((n_h - 1,)),
            DMA((n_e - 1,)),
            DMA((n_e - 1,)),
            DMA((n_h - 1,)),
            DMA((n_h - 1,)),
            DMA,
            DMA((far, high)),
            DMA((far, high)),
            DMA((far, high)),
            DMA((far, high)),
            DMA((far, n_e)),
            DMA((far, n_e)),
            DMA((far, n_e)),
            DMA((far, n_e)),
        ],
        compiler_params=pltpu.CompilerParams(
            collective_id=cid, has_side_effects=True, vmem_limit_bytes=56 << 20
        ),
    )(dh, w_all, small, tokens, gain, d_res, residual, gates, pos, y_back)


def turn_body(
    width,
    experts,
    scale,
    full,
    dw,
    small,
    input_grad,
    output,
    q_out,
    k_out,
    v_out,
    o_out,
    up_out,
    down_out,
    g1_out,
    s1_out,
    g2_out,
    s2_out,
    router_out,
    input_out,
    output_out,
    load_out,
):
    @pl.when(pl.program_id(0) == 0)
    def _begin():
        input_out[...] = input_grad[...]
        output_out[...] = output[...]
        for n, out in enumerate((g1_out, s1_out, g2_out, s2_out)):
            out[...] = small[row_at(small, n)].reshape(out.shape)
        for n in range(experts):
            router_out[n : n + 1, :] = small[row_at(small, 8 + n)]
        load_out[...] = small[row_at(small, 4)][:, 0:experts].reshape(experts) * scale

    for n, out in enumerate((q_out, k_out, v_out)):
        part = full[:, n * width : (n + 1) * width, :].astype(F32)
        out[...] = part.reshape(-1, part.shape[2]).T
    part = full[:, 3 * width :, :].astype(F32)
    o_out[...] = part.reshape(-1, part.shape[2])
    trained = jnp.where(lax.axis_index("expert") >= experts // 2, 1.0, 0.0)
    up_out[...] = dw[0].astype(F32) * trained
    down_out[...] = dw[1].astype(F32).T * trained


def turn_weights(full, dw, small, input_grad, output, width, experts, scale):
    n_h, deep, model = full.shape
    cols = model
    across = pl.BlockSpec((cols, model), lambda i: (i, 0))
    down = pl.BlockSpec((model, cols), lambda i: (0, i))
    flat = pl.BlockSpec((model,), lambda i: (0,))
    whole = pl.BlockSpec(output.shape, lambda i: (0, 0))
    square = shape_of((model, model), F32)
    return pl.pallas_call(
        partial(turn_body, width, experts, scale),
        name="turn_weights",
        grid=(model // cols,),
        out_shape=[square] * 6
        + [shape_of((model,), F32)] * 4
        + [
            shape_of((experts, model), F32),
            shape_of(input_grad.shape, BF),
            shape_of(output.shape, BF),
            shape_of((experts,), F32),
        ],
        in_specs=[
            pl.BlockSpec((n_h, deep, cols), lambda i: (0, 0, i)),
            pl.BlockSpec((2, model, cols), lambda i: (0, 0, i)),
            pl.BlockSpec(small.shape, lambda i: (0, 0, 0)),
            whole,
            whole,
        ],
        out_specs=[across, across, across, down, down, across]
        + [flat] * 4
        + [pl.BlockSpec((experts, model), lambda i: (0, 0)), whole, whole]
        + [pl.BlockSpec((experts,), lambda i: (0,))],
        compiler_params=pltpu.CompilerParams(
            dimension_semantics=("arbitrary",), vmem_limit_bytes=60 << 20
        ),
        cost_estimate=pl.CostEstimate(flops=0, bytes_accessed=24 << 20, transcendentals=0),
    )(full, dw, small, input_grad, output)


def attend_back(
    heads, i, span, first, qkv, given, centre, kept, values, dq_acc, dk_acc, dv_acc
):
    width = heads * HEAD_DIM
    rows = aligned(i * BLOCK, BLOCK)
    dq_acc[...] = jnp.zeros_like(dq_acc)
    queries = [
        qkv[n * HEAD_DIM : (n + 1) * HEAD_DIM, rows] * jnp.asarray(SCALE, BF) for n in range(heads)
    ]
    for k in range(span):
        part = aligned((first + k) * BLOCK, BLOCK)
        for n in range(heads):
            here = slice(n * HEAD_DIM, (n + 1) * HEAD_DIM)
            weight = kept[n, k]
            d_weight = mm(values[n, part, :], given[n])
            d_score = (weight.astype(F32) * (d_weight - centre[n])).astype(BF)
            dv_acc[here, part] += mm_nt(given[n], weight)
            dk_acc[here, part] += mm_nt(queries[n], d_score)
            lo = width + n * HEAD_DIM
            dq_acc[here, :] += mm(qkv[lo : lo + HEAD_DIM, part], d_score)


def back_body(
    n_e,
    n_h,
    experts,
    capacity,
    padded,
    heads,
    ids,
    slot,
    pos,
    gates,
    count,
    g1,
    s1,
    g2,
    s2,
    w_router,
    inverse,
    dg_rows,
    dx_back,
    y_out,
    dw_sum,
    dw_far,
    out_grad,
    residual,
    all_tokens,
    qkv_in,
    att_in,
    att_t_in,
    w_out,
    w_t_in,
    weights,
    y_back,
    d_hidden,
    d_res,
    w_all,
    small,
    dw_own,
    dxv,
    gv,
    res_v,
    tv,
    qkv,
    att_v,
    att_t,
    wo,
    w_t,
    d_att_v,
    d_att,
    wo_box,
    wo_far,
    kept,
    values,
    dq_acc,
    dk_acc,
    dv_acc,
    d_qkv,
    w_acc,
    dw_mine,
    dw_across,
    load_sem,
    save_sem,
    dw_sem,
    kept_sem,
    y_own,
    y_s,
    y_r,
    at_s,
    at_r,
    wo_s,
    wo_r,
    wf_s,
    wf_r,
    da_s,
    da_r,
):
    e, h = lax.axis_index("expert"), lax.axis_index("hidden")
    far = n_h // 2
    pair, core = h // 2, lax.rem(h, 2)
    mate = pair * 2 + 1 - core
    rows, model = out_grad.shape
    width = heads * HEAD_DIM
    group = rows * n_h
    per_device = rows // BLOCK
    blocks = group // BLOCK
    sends = []

    loads = [
        pltpu.make_async_copy(source, target, load_sem.at[n])
        for n, (source, target) in enumerate(
            (
                (residual, res_v),
                (dx_back, dxv),
                (out_grad, gv),
                (w_out, wo),
                (att_t_in, att_t),
                (qkv_in, qkv),
                (att_in, att_v),
                (all_tokens, tv),
                (w_t_in, w_t),
            )
        )
    ]
    for load in loads:
        load.start()
    greet(
        [{"hidden": lax.rem(h + step, n_h)} for step in range(1, n_h)]
        + [{"expert": lax.rem(e + step, n_e)} for step in range(1, n_e)]
    )
    load_dw = pltpu.make_async_copy(dw_sum.at[:, 0], dw_mine, dw_sem.at[0])
    load_dw.start()
    deep = dw_mine.shape[1] // 2
    crossed = dw_far.shape[1]
    load_far = pltpu.make_async_copy(
        dw_far, dw_across.at[0, :, pl.ds(0, crossed)], dw_sem.at[1]
    )
    load_far.start()

    def dw_across_copy(step, k):
        part = pl.ds(k * deep, deep)
        return remote(
            dw_sum.at[1, step, part],
            dw_across.at[1, step - 1, part],
            da_s.at[step, k],
            da_r.at[step, k],
            {"hidden": lax.rem(pair + step, far) * 2 + core},
        )

    def dw_send(k):
        for step in range(1, far):
            dw_across_copy(step, k).start()

    def up_rest_copy(step):
        part = pl.ds(crossed, dw_mine.shape[1] - crossed)
        return remote(
            dw_sum.at[0, step, part],
            dw_across.at[0, step - 1, part],
            da_s.at[step, 2],
            da_r.at[step, 2],
            {"hidden": lax.rem(pair + step, far) * 2 + core},
        )

    for step in range(1, far):
        up_rest_copy(step).start()
    dw_send(0)
    for step in range(1, n_e):
        peer = lax.rem(e + step, n_e)
        copy = remote(y_out.at[peer], y_back.at[e], y_s.at[step], y_r.at[step], {"expert": peer})
        copy.start()
        sends.append(copy)
    own_y = pltpu.make_async_copy(y_out.at[e], y_back.at[e], y_own)
    own_y.start()

    for load in loads[:3]:
        load.wait()
    normed, spread = norm_parts(res_v[...])
    hidden = (normed * lying(g2) + lying(s2)).astype(BF)
    gate = [gates[:, j : j + 1] for j in range(2)]
    column = iota((rows, padded), 1)
    dot_of = []
    for j in range(2):
        mix = jnp.zeros((rows, padded), F32)
        for n in range(experts):
            here = jnp.where(ids[:, j : j + 1] == n, slot[:, j : j + 1], -1) == column
            mix = jnp.where(here, dg_rows[n, 0:1, :], mix)
        dot_of.append(jnp.sum(mix, axis=1, keepdims=True))
    mean = gate[0] * dot_of[0] + gate[1] * dot_of[1]
    lane = iota((rows, experts), 1)
    d_logits = jnp.zeros((rows, experts), F32)
    for j in range(2):
        d_logits = jnp.where(lane == ids[:, j : j + 1], gate[j] * (dot_of[j] - mean), d_logits)
    high, low = split_two(d_logits)
    grad = mm(high, w_router[...]) + mm(low, w_router[...])
    small[...] = jnp.zeros_like(small)
    for_router = mm_tn(high, hidden) + mm_tn(low, hidden)
    for n in range(experts):
        small[row_at(small, 8 + n)] = for_router[n : n + 1]
    place, line = row_at(small, 4)
    small[place, line, 0:LANES] = count[...]
    place = iota((rows, experts * capacity), 1)
    for j in range(2):
        pick = (place == pos[:, j : j + 1]).astype(BF)
        grad = grad + gate[j] * mm(pick, dxv[...])
    small[row_at(small, 2)] = jnp.sum(grad * normed, axis=0, keepdims=True)
    small[row_at(small, 3)] = jnp.sum(grad, axis=0, keepdims=True)
    d_resid = gv[...].astype(F32) + norm_back(grad, normed, spread, lying(g2))
    d_res[...] = d_resid
    branch = d_resid.astype(BF)
    loads[3].wait()

    def device_at(n, sign):
        t, other = n // 2, lax.rem(n, 2)
        return lax.rem(pair + far + sign * t, far) * 2 + lax.rem(core + other, 2)

    def give_att(n):
        owner = device_at(n, 1)
        return remote(
            d_att_v.at[owner], d_att.at[h], at_s.at[n], at_r.at[n], {"hidden": owner}
        )

    for n in range(n_h - 1, -1, -1):
        owner = device_at(n, 1)
        block = mm_nt(wo[owner], branch).astype(BF)
        if n == 0:
            d_att[h] = block
        else:
            d_att_v[owner] = block
            give_att(n).start()
    loads[4].wait()
    for t in range(n_h):
        owner = lax.rem(h + t, n_h)
        wo[owner] = mm(att_t[owner], branch).astype(BF)
    for step in list(range(1, far)) + [0]:
        copy = remote(
            wo.at[lax.rem(pair + step, far) * 2 + 1 - core],
            wo_box.at[step],
            wo_s.at[step],
            wo_r.at[step],
            {"hidden": mate},
        )
        copy.start()
        sends.append(copy)
    def give_wo(step):
        target = lax.rem(pair + step, far) * 2 + core
        return remote(
            wo.at[target],
            wo_far.at[step - 1],
            wf_s.at[step],
            wf_r.at[step],
            {"hidden": target},
        )

    for load in loads[5:]:
        load.wait()

    def load_kept(i, turn):
        return pltpu.make_async_copy(weights.at[i], kept.at[turn], kept_sem.at[turn])

    def block_at(at):
        owner = device_at(at // per_device, 1)
        return owner, owner * per_device + lax.rem(at, per_device)

    load_kept(block_at(0)[1], 0).start()
    dk_acc[...] = jnp.zeros_like(dk_acc)
    dv_acc[...] = jnp.zeros_like(dv_acc)

    def turn_values(i, _):
        cols = aligned(i * BLOCK, BLOCK)
        for n in range(heads):
            lo = 2 * width + n * HEAD_DIM
            values[n, cols, :] = qkv[lo : lo + HEAD_DIM, cols].astype(F32).T.astype(BF)
        return 0

    lax.fori_loop(0, blocks, turn_values, 0)

    def over_queries(at, _):
        owner, i = block_at(at)
        turn = lax.rem(at, 2)

        @pl.when(at + 1 < blocks)
        def _next():
            load_kept(block_at(at + 1)[1], 1 - turn).start()

        @pl.when((at >= per_device) & (lax.rem(at, per_device) == 0))
        def _arrive():
            n = at // per_device
            source = lax.rem(far - n // 2, far) * 2 + lax.rem(n, 2)
            give_att(source).wait_recv()

        @pl.when(at == per_device)
        def _weights():
            for step in range(1, far):
                there = wo_box.at[step]
                target = lax.rem(pair + step, far) * 2 + core
                remote(there, there, wo_s.at[step], wo_r.at[step], {"hidden": mate}).wait_recv()
                both = wo[target].astype(F32) + wo_box[step].astype(F32)
                wo[target] = both.astype(BF)
                give_wo(step).start()
            dw_send(1)

        load_kept(i, turn).wait()
        cols = aligned(lax.rem(at, per_device) * BLOCK, BLOCK)
        rows_i = aligned(i * BLOCK, BLOCK)
        given, centre = [], []
        for n in range(heads):
            here = slice(n * HEAD_DIM, (n + 1) * HEAD_DIM)
            scaled = d_att[owner, here, cols].astype(F32) * inverse[n : n + 1, rows_i]
            given.append(scaled.astype(BF))
            product = att_v[owner, here, cols].astype(F32) * scaled
            centre.append(jnp.sum(product, axis=0, keepdims=True))

        def block(span, first):
            attend_back(
                heads,
                i,
                span,
                first,
                qkv,
                given,
                centre,
                kept.at[turn],
                values,
                dq_acc,
                dk_acc,
                dv_acc,
            )

        spans(i, block)
        d_qkv[0:width, rows_i] = (dq_acc[...] * SCALE).astype(BF)
        return 0

    lax.fori_loop(0, blocks, over_queries, 0)
    w_acc[...] = jnp.zeros_like(w_acc)

    def finish(i, _):
        cols = aligned(i * BLOCK, BLOCK)
        d_qkv[width : 2 * width, cols] = dk_acc[:, cols].astype(BF)
        d_qkv[2 * width :, cols] = dv_acc[:, cols].astype(BF)
        block = d_qkv[:, cols]
        grad = mm_tn(block, w_t[...])
        inner = aligned(lax.rem(i, per_device) * BLOCK, BLOCK)
        normed, _unused = norm_parts(tv[i // per_device, inner, :].astype(F32))
        tv[i // per_device, inner, :] = grad.astype(BF)
        small[row_at(small, 0)] += jnp.sum(grad * normed, axis=0, keepdims=True)
        small[row_at(small, 1)] += jnp.sum(grad, axis=0, keepdims=True)
        hidden = (normed * lying(g1) + lying(s1)).astype(BF)
        w_acc[...] += mm(block, hidden)
        return 0

    lax.fori_loop(0, blocks, finish, 0)
    save_dh = pltpu.make_async_copy(tv, d_hidden, save_sem)
    save_dh.start()
    w_all[0 : 3 * width, :] = w_acc[...].astype(BF)
    there = wo_box.at[0]
    remote(there, there, wo_s.at[0], wo_r.at[0], {"hidden": mate}).wait_recv()
    total = wo[h].astype(F32) + wo_box[0].astype(F32)
    for step in range(1, far):
        give_wo(step).wait_recv()
        total = total + wo_far[step - 1].astype(F32)
    w_all[3 * width :, :] = total.astype(BF)
    load_dw.wait()
    load_far.wait()
    for which in range(2):
        for step in range(1, far):
            if which == 0:
                up_rest_copy(step).wait()
            else:
                for k in range(2):
                    dw_across_copy(step, k).wait()

        def add_all(n, _, which=which):
            band = aligned(n * 96, 96)
            both = dw_mine[which, band, :].astype(F32)
            for step in range(1, far):
                both = both + dw_across[which, step - 1, band, :].astype(F32)
            dw_own[which, band, :] = both.astype(BF)
            return 0

        lax.fori_loop(0, dw_mine.shape[1] // 96, add_all, 0)
    for step in range(1, n_e):
        there = y_back.at[lax.rem(e + n_e - step, n_e)]
        remote(there, there, y_s.at[step], y_r.at[step], {"expert": e}).wait_recv()
    own_y.wait()
    save_dh.wait()
    for n in range(1, n_h):
        give_att(n).wait_send()
    for step in range(1, far):
        give_wo(step).wait_send()
    for copy in sends:
        copy.wait_send()


def run_back(
    ids,
    slot,
    pos,
    gates,
    count,
    g1,
    s1,
    g2,
    s2,
    w_router,
    inverse,
    dg_rows,
    dx_back,
    y_out,
    dw_sum,
    dw_far,
    out_grad,
    residual,
    all_tokens,
    qkv,
    att,
    att_t,
    w_out,
    w_t,
    weights,
    cid,
):
    n_e, n_h = lax.axis_size("expert"), lax.axis_size("hidden")
    experts, capacity, model = y_out.shape
    padded = dg_rows.shape[2]
    rows = out_grad.shape[0]
    width = w_t.shape[0] // 3
    heads = width // HEAD_DIM
    group, far = rows * n_h, n_h // 2
    shard = dw_sum.shape[2:]
    tall = 8 + experts

    def pairs(*shape):
        return [DMA(shape), DMA(shape)]

    return pl.pallas_call(
        partial(back_body, n_e, n_h, experts, capacity, padded, heads),
        name="back",
        out_shape=[
            shape_of(y_out.shape, BF),
            shape_of((n_h, rows, model), BF),
            shape_of((rows, model), F32),
            shape_of((4 * width, model), BF),
            shape_of((n_h, tall // n_h, model), F32),
            shape_of((2, *shard), BF),
        ],
        in_specs=[VMEM] * 12 + [ANY] * 13,
        out_specs=[ANY] * 2 + [VMEM] * 4,
        scratch_shapes=[
            pltpu.VMEM((experts * capacity, model), BF),
            pltpu.VMEM((rows, model), BF),
            pltpu.VMEM((rows, model), F32),
            pltpu.VMEM((n_h, rows, model), BF),
            pltpu.VMEM((3 * width, group), BF),
            pltpu.VMEM((n_h, width, rows), BF),
            pltpu.VMEM((n_h, width, rows), BF),
            pltpu.VMEM((n_h, width, model), BF),
            pltpu.VMEM((3 * width, model), BF),
            pltpu.VMEM((n_h, width, rows), BF),
            pltpu.VMEM((n_h, width, rows), BF),
            pltpu.VMEM((far, width, model), BF),
            pltpu.VMEM((far - 1, width, model), BF),
            pltpu.VMEM((2, heads, REACH, BLOCK, BLOCK), BF),
            pltpu.VMEM((heads, group, HEAD_DIM), BF),
            pltpu.VMEM((width, BLOCK), F32),
            pltpu.VMEM((width, group), F32),
            pltpu.VMEM((width, group), F32),
            pltpu.VMEM((3 * width, group), BF),
            pltpu.VMEM((3 * width, model), F32),
            pltpu.VMEM((2, *shard), BF),
            pltpu.VMEM((2, far - 1, *shard), BF),
            DMA((9,)),
            DMA,
            DMA((2,)),
            DMA((2,)),
            DMA,
            *pairs(n_e),
            *pairs(n_h),
            *pairs(far),
            *pairs(far),
            *pairs(far, 3),
        ],
        compiler_params=pltpu.CompilerParams(
            collective_id=cid, has_side_effects=True, vmem_limit_bytes=60 << 20
        ),
    )(
        ids,
        slot,
        pos,
        gates,
        count,
        g1,
        s1,
        g2,
        s2,
        w_router,
        inverse,
        dg_rows,
        dx_back.reshape(experts * capacity, model),
        y_out,
        dw_sum,
        dw_far,
        out_grad,
        residual,
        all_tokens,
        qkv,
        att,
        att_t,
        w_out.reshape(n_h, width, model),
        w_t,
        weights,
    )


def shards(
    tokens,
    doc_lengths,
    expert_ids,
    gain_one,
    shift_one,
    w_query,
    w_key,
    w_value,
    w_out,
    gain_two,
    shift_two,
    w_router,
    w_up,
    w_down,
    out_grad,
):
    rows, model = tokens.shape
    n_expert, n_hidden = lax.axis_size("expert"), lax.axis_size("hidden")
    experts = n_expert * w_up.shape[0]
    capacity = max(2, rows * 2 * 5 // (4 * experts))
    capacity = -(-capacity // 16) * 16
    total = experts * capacity
    heads = HEADS // n_hidden
    width = heads * HEAD_DIM
    g1, s1, g2, s2 = gain_one, shift_one, gain_two, shift_two
    router_t = w_router.T

    (
        all_tokens,
        qkv,
        att,
        att_t,
        w_t,
        g_in,
        x_slots,
        ups,
        weights,
        ids,
        pos,
        slot,
        count,
        inverse,
        residual,
        gates,
        gate_rows,
    ) = run_front(
        doc_lengths,
        expert_ids.T,
        g1,
        s1,
        g2,
        s2,
        router_t,
        tokens,
        out_grad,
        (w_query, w_key, w_value, w_out),
        w_up,
        capacity,
        heads,
        1,
    )
    dx_back, dg_back, y_out, dw_sum, dw_far = run_experts(
        x_slots, gate_rows, g_in, ups, w_up, w_down, 2
    )
    y_back, d_hidden, d_res, w_all, small, dw_own = run_back(
        ids,
        slot,
        pos,
        gates,
        count,
        g1,
        s1,
        g2,
        s2,
        router_t,
        inverse,
        dg_back,
        dx_back,
        y_out,
        dw_sum,
        dw_far,
        out_grad,
        residual,
        all_tokens,
        qkv,
        att,
        att_t,
        w_out,
        w_t,
        weights,
        3,
    )
    input_grad, output, full, small = run_tail(
        d_hidden,
        w_all.reshape(n_expert, 4 * width // n_expert, model),
        small,
        tokens,
        g1,
        d_res,
        residual,
        gates,
        pos,
        y_back.reshape(total, model),
        4,
    )
    scale = experts / (rows * n_expert * n_hidden * 2)
    turned = turn_weights(
        full.reshape(n_hidden, 4 * width, model),
        dw_own,
        small,
        input_grad,
        output,
        width,
        experts,
        scale,
    )
    w_grads, (up_grad, down_grad) = turned[:4], turned[4:6]
    gain_one_grad, shift_one_grad, gain_two_grad, shift_two_grad = turned[6:10]
    router_grad, input_grad, output, load = turned[10:]
    return (
        output,
        input_grad,
        gain_one_grad,
        shift_one_grad,
        *w_grads,
        gain_two_grad,
        shift_two_grad,
        router_grad.T,
        up_grad[None],
        down_grad[None],
        load,
    )


def solution(mesh):
    in_specs = (
        P(("expert", "hidden"), None),
        P("expert", None),
        P(("expert", "hidden"), None),
        P(),
        P(),
        P(),
        P(),
        P(),
        P(),
        P(),
        P(),
        P(),
        P("expert", None, "hidden"),
        P("expert", "hidden", None),
        P(("expert", "hidden"), None),
    )
    out_specs = (
        P(("expert", "hidden"), None),
        P(("expert", "hidden"), None),
        P(),
        P(),
        P(),
        P(),
        P(),
        P(),
        P(),
        P(),
        P(),
        P("expert", None, "hidden"),
        P("expert", "hidden", None),
        P(),
    )
    return jax.shard_map(shards, mesh=mesh, in_specs=in_specs, out_specs=out_specs, check_vma=False)
```
